32 devices in a mesh: fsdp: 8 (over z, y), seq: 4 (over x, core).
Axes of the slice: x: 2, y: 2, z: 4, core: 2. Of those that a mesh axis runs over, the one named last changes fastest.
Arguments:
- inputs: bfloat16 [16, 2048, 1024], P('fsdp', 'seq'), may hold values from -6 to 6
- first_values: bfloat16 [16, 2048, 1024], P('fsdp', 'seq'), may hold values from -6 to 6
- out_grad: bfloat16 [16, 2048, 1024], P('fsdp', 'seq'), may hold values from -6 to 6
- attn_gain: bfloat16 [1024], P('fsdp'), may hold values from 0.099609375 to 1.8984375
- query_weight: bfloat16 [1024, 1024], P('fsdp'), may hold values from -0.25 to 0.25
- key_weight: bfloat16 [1024, 1024], P('fsdp'), may hold values from -0.25 to 0.25
- value_weight: bfloat16 [1024, 1024], P('fsdp'), may hold values from -0.1875 to 0.1875
- output_weight: bfloat16 [1024, 1024], P('fsdp'), may hold values from -1 to 1
- mlp_gain: bfloat16 [1024], P('fsdp'), may hold values from 0.099609375 to 1.8984375
- gate_weight: bfloat16 [1024, 2816], P('fsdp'), may hold values from -0.1875 to 0.1875
- up_weight: bfloat16 [1024, 2816], P('fsdp'), may hold values from -0.1875 to 0.1875
- down_weight: bfloat16 [2816, 1024], P('fsdp'), may hold values from -0.21875 to 0.21875
Outputs:
- outputs: float32 [16, 2048, 1024], P('fsdp', 'seq')
- input_grad: float32 [16, 2048, 1024], P('fsdp', 'seq')
- first_values_grad: float32 [16, 2048, 1024], P('fsdp', 'seq')
- attn_gain_grad: float32 [1024], P('fsdp')
- mlp_gain_grad: float32 [1024], P('fsdp')
- query_weight_grad: float32 [1024, 1024], P('fsdp')
- key_weight_grad: float32 [1024, 1024], P('fsdp')
- value_weight_grad: float32 [1024, 1024], P('fsdp')
- output_weight_grad: float32 [1024, 1024], P('fsdp')
- gate_weight_grad: float32 [1024, 2816], P('fsdp')
- up_weight_grad: float32 [1024, 2816], P('fsdp')
- down_weight_grad: float32 [2816, 1024], P('fsdp')
The draws below stay inside these ranges and needn't reach their ends.
All inputs are finite; a program needn't handle non-finite values.
Results may differ from the reference program's by a relative error of at most 0.023.
Values may be sent and summed in bfloat16 or wider, within the bound.
A program may use at most 384 MiB of HBM per device.

```python
import jax
import jax.numpy as jnp
from jax import lax

D = 1024
HEADS = 16
HEAD_DIM = 64
FF = 2816
LEN = 2048
SEQS = 16


def levels(own_key, extent, shards, low, largest):
    def one(position, parts):
        draws = jax.random.uniform(jax.random.fold_in(jax.random.fold_in(own_key, 6), position), (parts,), jnp.float32, low / len(shards), largest / len(shards))
        return jnp.repeat(jnp.exp(draws), extent[position] // parts).reshape((-1,) + (1,) * (len(extent) - position - 1))

    loudness = one(*shards[0])
    for cut in shards[1:]:
        loudness = loudness * one(*cut)
    return loudness


def bell_draw(rng, dims, deviation, most, pieces=(), kind=jnp.bfloat16):
    entries = deviation * jax.random.normal(rng, dims, jnp.float32)
    if pieces:
        entries = entries * levels(rng, dims, pieces, -0.22, 0.18)
    return jnp.clip(entries, -most, most).astype(kind)


def setup_inputs(seed: int = 0) -> dict:
    splits = jax.random.split(jax.random.key(seed), 13)
    return {
        "inputs": bell_draw(splits[0], (SEQS, LEN, D), 1.0, 6.0, ((0, 8), (1, 4))),
        "first_values": bell_draw(splits[1], (SEQS, LEN, D), 1.0, 6.0, ((0, 8), (1, 4))),
        "out_grad": bell_draw(splits[2], (SEQS, LEN, D), 1.0, 6.0, ((0, 8), (1, 4))),
        "attn_gain": jnp.clip(1.0 + 0.18 * jax.random.normal(splits[3], (D,), jnp.float32), 0.099609375, 1.8984375).astype(jnp.bfloat16),
        "query_weight": bell_draw(splits[4], (D, D), (D // 2) ** -0.5, 0.25, ((0, 8),)),
        "key_weight": bell_draw(splits[5], (D, D), (D // 2) ** -0.5, 0.25, ((0, 8),)),
        "value_weight": bell_draw(splits[6], (D, D), D ** -0.5, 0.1875, ((0, 8),)),
        "output_weight": bell_draw(splits[7], (D, D), (D // 32) ** -0.5, 1.0, ((0, 8),)),
        "mlp_gain": jnp.clip(1.0 + 0.18 * jax.random.normal(splits[8], (D,), jnp.float32), 0.099609375, 1.8984375).astype(jnp.bfloat16),
        "gate_weight": bell_draw(splits[9], (D, FF), D ** -0.5, 0.1875, ((0, 8),)),
        "up_weight": bell_draw(splits[10], (D, FF), D ** -0.5, 0.1875, ((0, 8),)),
        "down_weight": bell_draw(splits[11], (FF, D), (FF // 4) ** -0.5, 0.21875, ((0, 8),)),
    }


@jax.custom_vjp
def low(v):
    return lax.optimization_barrier(v.astype(jnp.bfloat16)).astype(jnp.float32)

@jax.custom_vjp
def low_back(v):
    return v

def low_keep(v):
    return (low(v), None)

def low_pass(kept, grad):
    return (grad,)

def back_keep(v):
    return (v, None)

def back_low(kept, grad):
    return (low(grad),)
low.defvjp(low_keep, low_pass)
low_back.defvjp(back_keep, back_low)
epsilon = 1e-06
rope_base = 10000.0

def rope_tables(positions, head_dim):
    half = head_dim // 2
    freqs = rope_base ** (-(jnp.arange(half, dtype=jnp.float32) * 2.0 / head_dim))
    angles = positions.astype(jnp.float32)[:, None] * freqs[None, :]
    return (jnp.cos(angles), jnp.sin(angles))

def rotate(values, cosine, sine):
    half = values.shape[-1] // 2
    first = values[..., :half]
    second = values[..., half:]
    return jnp.concatenate([first * cosine - second * sine, first * sine + second * cosine], axis=-1)

def to_heads(values):
    return values.reshape(LEN, HEADS, HEAD_DIM).transpose(1, 0, 2)

def sequence_forward(seq_in, seq_first, params):
    attn_gain, query_weight, key_weight, value_weight, output_weight, mlp_gain, gate_weight, up_weight, down_weight = params
    highest = lax.Precision.HIGHEST
    attn_scale = lax.rsqrt(lax.optimization_barrier(jnp.mean(seq_in * seq_in, axis=-1, keepdims=True)) + epsilon)
    normed = low(seq_in * attn_scale * attn_gain)
    raw_queries = low_back(jnp.dot(normed, query_weight, precision=highest))
    raw_keys = low_back(jnp.dot(normed, key_weight, precision=highest))
    raw_values = jnp.dot(normed, value_weight, precision=highest)
    cosine, sine = rope_tables(jnp.arange(LEN, dtype=jnp.int32), HEAD_DIM)
    queries = low(rotate(to_heads(raw_queries), cosine, sine))
    keys = low(rotate(to_heads(raw_keys), cosine, sine))
    mixed_values = low_back(low(0.5 * to_heads(raw_values) + 0.5 * to_heads(seq_first)))
    block = min(512, LEN)
    scale = HEAD_DIM ** (-0.5)
    key_pos = jnp.arange(LEN, dtype=jnp.int32)

    def one_block(start):
        rows = lax.dynamic_slice_in_dim(queries, start, block, 1)
        scores = low_back(jnp.einsum('hqe,hke->hqk', rows, keys, precision=highest) * scale)
        query_pos = start + jnp.arange(block, dtype=jnp.int32)
        allowed = key_pos[None, :] <= query_pos[:, None]
        probs = jax.nn.softmax(jnp.where(allowed[None], scores, -1e+30), axis=-1)
        probs = low(probs)
        return jnp.einsum('hqk,hke->hqe', probs, mixed_values, precision=highest)
    starts = jnp.arange(LEN // block, dtype=jnp.int32) * block
    blocks = lax.map(jax.checkpoint(one_block), starts)
    attended = jnp.moveaxis(blocks, 0, 1).reshape(HEADS, LEN, HEAD_DIM)
    attended = low_back(low(attended))
    joined = attended.transpose(1, 0, 2).reshape(LEN, D)
    middle = seq_in + low_back(jnp.dot(joined, output_weight, precision=highest))
    mlp_scale = lax.rsqrt(lax.optimization_barrier(jnp.mean(middle * middle, axis=-1, keepdims=True)) + epsilon)
    normed2 = low(middle * mlp_scale * mlp_gain)
    gate = low_back(jnp.dot(normed2, gate_weight, precision=highest))
    up = low_back(jnp.dot(normed2, up_weight, precision=highest))
    active = low(jax.nn.silu(gate) * up)
    return middle + jnp.dot(active, down_weight, precision=highest)

def reference(inputs, first_values, out_grad, attn_gain, query_weight, key_weight, value_weight, output_weight, mlp_gain, gate_weight, up_weight, down_weight):
    params = tuple((weight.astype(jnp.float32) for weight in (attn_gain, query_weight, key_weight, value_weight, output_weight, mlp_gain, gate_weight, up_weight, down_weight)))

    def step(totals, batch):
        seq_in, seq_first, seq_grad = batch
        result, pullback = jax.vjp(sequence_forward, seq_in.astype(jnp.float32), seq_first.astype(jnp.float32), params)
        grad_in, grad_first, grad_params = pullback(seq_grad.astype(jnp.float32))
        updated = tuple((total + grad for total, grad in zip(totals, grad_params)))
        return (updated, (result, grad_in, grad_first))
    initial = tuple((jnp.zeros_like(weight) for weight in params))
    totals, stacked = lax.scan(step, initial, (inputs, first_values, out_grad))
    outputs, input_grad, first_grad = stacked
    return (outputs, input_grad, first_grad, totals[0], totals[5], totals[1], totals[2], totals[3], totals[4], totals[6], totals[7], totals[8])
```

```python
import functools

import jax
import jax.numpy as jnp
from jax import lax
from jax.experimental import pallas as pl
from jax.experimental.pallas import tpu as pltpu
from jax.sharding import PartitionSpec as P

D = 1024
HEADS = 16
HEAD_DIM = 64
HALF = HEAD_DIM // 2
PAIR = 2 * HEAD_DIM
F32 = jnp.float32
BF16 = jnp.bfloat16
NEG = -1e30
MIB = 1024 * 1024
epsilon = 1e-06
rope_base = 10000.0


def dot(a, b):
    return lax.dot_general(a, b, (((1,), (0,)), ((), ())), preferred_element_type=F32)


def head_rows(value, head):
    row = lax.broadcasted_iota(jnp.int32, value.shape, 0)
    return jnp.where((row // HEAD_DIM) == head, value, jnp.zeros_like(value))


def head_lanes(value, head):
    lane = lax.broadcasted_iota(jnp.int32, value.shape, 1)
    return jnp.where((lane // HEAD_DIM) == head, value, jnp.zeros_like(value))


def causal(scores):
    side = scores.shape[0]
    square = scores[:, :side]
    key = lax.broadcasted_iota(jnp.int32, square.shape, 0)
    query = lax.broadcasted_iota(jnp.int32, square.shape, 1)
    square = jnp.where(key <= query, square, NEG)
    if scores.shape[1] == side:
        return square
    return jnp.concatenate([square, scores[:, side:]], axis=1)


def attend_kernel(count, slots, tok, tile_k, order, *refs):
    pieces = refs[:count]
    outs = refs[count : 2 * count]
    lse_ref = refs[2 * count]
    qz, kn, vt, ot = refs[2 * count + 1 :]
    for source in range(count):
        for slot in range(slots):
            cols = pl.ds(pl.multiple_of(order[source * slots + slot] * tok, tok), tok)
            take = slice(slot * tok, (slot + 1) * tok)
            query = pieces[source][0, :, take] * jnp.asarray(HEAD_DIM**-0.5, BF16)
            for head in range(2):
                qz[head, :, cols] = head_rows(query, head)
            kn[cols, :] = pieces[source][1, :, take].T
            vt[:, cols] = pieces[source][2, :, take]
    length = count * slots * tok


    def score(sub, head):
        start = sub * tile_k
        return causal(dot(kn[start : start + tile_k, :], qz[head, :, start:]))

    def absorb(sub, head, carry, scores):
        peak, total, mixed = carry
        start = sub * tile_k
        new_peak = jnp.maximum(peak, jnp.max(scores, axis=0, keepdims=True))
        weights = jnp.exp(scores - new_peak)
        fade = jnp.exp(peak - new_peak)
        total = total * fade + jnp.sum(weights, axis=0, keepdims=True)
        values = vt[head * HEAD_DIM : (head + 1) * HEAD_DIM, start : start + tile_k]
        mixed = mixed * fade + dot(values, weights.astype(BF16))
        return (new_peak, total, mixed)

    tiles = [(sub, head) for sub in range(length // tile_k) for head in range(2)]
    carries = [
        (
            jnp.full((1, length), NEG, F32),
            jnp.zeros((1, length), F32),
            jnp.zeros((HEAD_DIM, length), F32),
        )
        for _ in range(2)
    ]
    ahead = score(*tiles[0])
    for number, (sub, head) in enumerate(tiles):
        scores = ahead
        if number + 1 < len(tiles):
            ahead = score(*tiles[number + 1])
        peak, total, mixed = absorb(sub, head, carries[head], scores)
        done = slice(sub * tile_k, (sub + 1) * tile_k)
        rows = slice(head * HEAD_DIM, (head + 1) * HEAD_DIM)
        ot[rows, done] = (mixed[:, :tile_k] / total[:, :tile_k]).astype(BF16)
        lse_ref[0, head : head + 1, done] = peak[:, :tile_k] + jnp.log(total[:, :tile_k])
        carries[head] = (peak[:, tile_k:], total[:, tile_k:], mixed[:, tile_k:])
    for source in range(count):
        for slot in range(slots):
            cols = pl.ds(pl.multiple_of(order[source * slots + slot] * tok, tok), tok)
            outs[source][:, slot * tok : (slot + 1) * tok] = ot[:, cols]


def attend(pieces, order, slots):
    count = len(pieces)
    width, span = pieces[0].shape[1:]
    tok = span // slots
    length = count * span
    pairs = width // PAIR
    tile_k = min(256, length)
    grid_spec = pltpu.PrefetchScalarGridSpec(
        num_scalar_prefetch=1,
        grid=(pairs,),
        in_specs=[pl.BlockSpec((3, PAIR, span), lambda p, o: (0, p, 0))] * count,
        out_specs=[pl.BlockSpec((PAIR, span), lambda p, o: (p, 0))] * count
        + [pl.BlockSpec((1, 8, length), lambda p, o: (p, 0, 0))],
        scratch_shapes=[
            pltpu.VMEM((2, PAIR, length), BF16),
            pltpu.VMEM((length, PAIR), BF16),
            pltpu.VMEM((PAIR, length), BF16),
            pltpu.VMEM((PAIR, length), BF16),
        ],
    )
    area = pairs * 2 * length * length // 2
    results = pl.pallas_call(
        functools.partial(attend_kernel, count, slots, tok, tile_k),
        out_shape=[jax.ShapeDtypeStruct((width, span), BF16)] * count
        + [jax.ShapeDtypeStruct((pairs, 8, length), F32)],
        grid_spec=grid_spec,
        compiler_params=pltpu.CompilerParams(
            dimension_semantics=("arbitrary",), vmem_limit_bytes=48 * MIB
        ),
        cost_estimate=pl.CostEstimate(
            flops=area * 1024, bytes_accessed=8 * width * length, transcendentals=area
        ),
        name="attend",
    )(order, *pieces)
    return (results[:count], results[count])


def attend_back_kernel(count, slots, tok, tile_q, tile_k, order, *refs):
    pieces = refs[:count]
    mixes = refs[count : 2 * count]
    grads = refs[2 * count : 3 * count]
    lse_ref, cos_ref, sin_ref = refs[3 * count : 3 * count + 3]
    outs = refs[3 * count + 3 : 4 * count + 3]
    qz, gz, qn, gn, kn, vn, kt, inner, dq, dk, dv = refs[4 * count + 3 :]
    length = count * slots * tok
    for source in range(count):
        for slot in range(slots):
            cols = pl.ds(pl.multiple_of(order[source * slots + slot] * tok, tok), tok)
            take = slice(slot * tok, (slot + 1) * tok)
            query = pieces[source][0, :, take] * jnp.asarray(HEAD_DIM**-0.5, BF16)
            grad = grads[source][:, take]
            query_rows = query.T
            grad_rows = grad.T
            for head in range(2):
                qz[head, :, cols] = head_rows(query, head)
                gz[head, :, cols] = head_rows(grad, head)
                qn[head, cols, :] = head_lanes(query_rows, head)
                gn[head, cols, :] = head_lanes(grad_rows, head)
            key = pieces[source][1, :, take]
            kt[:, cols] = key
            kn[cols, :] = key.T
            vn[cols, :] = pieces[source][2, :, take].T
            both = grad.astype(F32) * mixes[source][:, take].astype(F32)
            for head in range(2):
                inner[head : head + 1, cols] = jnp.sum(
                    both[head * HEAD_DIM : (head + 1) * HEAD_DIM], axis=0, keepdims=True
                )
    dq[...] = jnp.zeros_like(dq)
    steps = tile_q // tile_k

    def tile(key_start, query_start, width, masked, carry):
        grad_keys, grad_values = carry
        keys = kn[pl.ds(key_start, tile_k), :]
        values = vn[pl.ds(key_start, tile_k), :]
        cols = pl.ds(query_start, width)
        for head in range(2):
            rows = slice(head * HEAD_DIM, (head + 1) * HEAD_DIM)
            scores = dot(keys, qz[head, :, cols])
            if masked:
                scores = causal(scores)
            probs = jnp.exp(scores - lse_ref[0, head : head + 1, cols])
            grad_probs = dot(values, gz[head, :, cols])
            grad_scores = (probs * (grad_probs - inner[head : head + 1, cols])).astype(BF16)
            grad_values = grad_values + dot(probs.astype(BF16), gn[head, cols, :])
            grad_keys = grad_keys + dot(grad_scores, qn[head, cols, :])
            dq[rows, cols] += dot(kt[rows, pl.ds(key_start, tile_k)], grad_scores)
        return (grad_keys, grad_values)

    def one(number, _):
        base = pl.multiple_of(number * tile_q, tile_q)
        for sub in range(steps):
            skip = sub * tile_k
            key_start = pl.multiple_of(base + skip, tile_k)
            carry = (jnp.zeros((tile_k, PAIR), F32), jnp.zeros((tile_k, PAIR), F32))
            carry = tile(key_start, key_start, tile_q - skip, True, carry)

            def body(step, carry):
                return tile(
                    key_start, pl.multiple_of(step * tile_q, tile_q), tile_q, False, carry
                )

            carry = lax.fori_loop(number + 1, length // tile_q, body, carry)
            dk[pl.ds(key_start, tile_k), :] = carry[0]
            dv[pl.ds(key_start, tile_k), :] = carry[1]
        return 0

    lax.fori_loop(0, length // tile_q, one, 0)
    half = HEAD_DIM // 2
    for source in range(count):
        for slot in range(slots):
            cols = pl.ds(pl.multiple_of(order[source * slots + slot] * tok, tok), tok)
            take = slice(slot * tok, (slot + 1) * tok)
            cosine = cos_ref[:, cols]
            sine = sin_ref[:, cols]
            for which, grad in enumerate((dq[:, cols] * (HEAD_DIM**-0.5), dk[cols, :].T)):
                for head in range(2):
                    low = head * HEAD_DIM
                    first = grad[low : low + half]
                    second = grad[low + half : low + 2 * half]
                    outs[source][which, low : low + half, take] = (
                        first * cosine + second * sine
                    ).astype(BF16)
                    outs[source][which, low + half : low + 2 * half, take] = (
                        second * cosine - first * sine
                    ).astype(BF16)
            outs[source][2, :, take] = dv[cols, :].T.astype(BF16)


def attend_back(pieces, mixes, grads, lse, cosine, sine, order, slots):
    count = len(pieces)
    width, span = pieces[0].shape[1:]
    tok = span // slots
    length = count * span
    pairs = width // PAIR
    tile_q = min(512, length)
    tile_k = min(256, length)
    triple = pl.BlockSpec((3, PAIR, span), lambda p, o: (0, p, 0))
    single = pl.BlockSpec((PAIR, span), lambda p, o: (p, 0))
    table = pl.BlockSpec((HEAD_DIM // 2, length), lambda p, o: (0, 0))
    grid_spec = pltpu.PrefetchScalarGridSpec(
        num_scalar_prefetch=1,
        grid=(pairs,),
        in_specs=[triple] * count
        + [single] * (2 * count)
        + [pl.BlockSpec((1, 8, length), lambda p, o: (p, 0, 0)), table, table],
        out_specs=[triple] * count,
        scratch_shapes=[
            pltpu.VMEM((2, PAIR, length), BF16),
            pltpu.VMEM((2, PAIR, length), BF16),
            pltpu.VMEM((2, length, PAIR), BF16),
            pltpu.VMEM((2, length, PAIR), BF16),
            pltpu.VMEM((length, PAIR), BF16),
            pltpu.VMEM((length, PAIR), BF16),
            pltpu.VMEM((PAIR, length), BF16),
            pltpu.VMEM((8, length), F32),
            pltpu.VMEM((PAIR, length), F32),
            pltpu.VMEM((length, PAIR), F32),
            pltpu.VMEM((length, PAIR), F32),
        ],
    )
    area = pairs * 2 * length * length // 2
    return pl.pallas_call(
        functools.partial(attend_back_kernel, count, slots, tok, tile_q, tile_k),
        out_shape=[jax.ShapeDtypeStruct((3, width, span), BF16)] * count,
        grid_spec=grid_spec,
        compiler_params=pltpu.CompilerParams(
            dimension_semantics=("arbitrary",), vmem_limit_bytes=56 * MIB
        ),
        cost_estimate=pl.CostEstimate(
            flops=area * 2560, bytes_accessed=16 * width * length, transcendentals=area
        ),
        name="attend_back",
    )(order, *pieces, *mixes, *grads, lse, cosine, sine)


def project_kernel(count, per, wide, place, x_ref, gain_ref, w_ref, first_ref, cos_ref, sin_ref, *refs):
    outs = refs[:count]
    normed_ref = refs[count]
    step = pl.program_id(0)
    kind = (step // per) % 3
    target = step // (3 * per)

    @pl.when(step == 0)
    def _():
        values = x_ref[...].astype(F32)
        scale = lax.rsqrt(jnp.mean(values * values, axis=1, keepdims=True) + epsilon)
        normed_ref[...] = (values * scale * gain_ref[...].astype(F32)).astype(BF16)

    raw = lax.dot_general(
        w_ref[...].T, normed_ref[...], (((1,), (1,)), ((), ())), preferred_element_type=F32
    )

    def store(value):
        for number in range(count):

            @pl.when(target == number)
            def _(number=number):
                outs[number][0] = value

    @pl.when(kind < 2)
    def _():
        parts = raw.reshape(wide // HEAD_DIM, 2, HALF, raw.shape[1])
        first, second = parts[:, 0], parts[:, 1]
        cosine, sine = cos_ref[...][None], sin_ref[...][None]
        turned = jnp.stack(
            [first * cosine - second * sine, first * sine + second * cosine], axis=1
        )
        store(turned.reshape(raw.shape).astype(BF16))

    @pl.when(kind == 2)
    def _():
        store((0.5 * raw + 0.5 * first_ref[...].T.astype(F32)).astype(BF16))


def project(x, gain, weight, first, cosine, sine, rank, count):
    span, depth = x.shape
    width = depth // count
    wide = min(width, 512)
    per = width // wide
    stride = depth // wide

    def column(step, place):
        return ((place[0] + 1 + step // (3 * per)) % count) * per + step % per

    def out_map(number):
        def index(step, place):
            local = jnp.clip(step - number * 3 * per, 0, 3 * per - 1)
            return (local // per, local % per, 0)

        return index

    grid_spec = pltpu.PrefetchScalarGridSpec(
        num_scalar_prefetch=1,
        grid=(count * 3 * per,),
        in_specs=[
            pl.BlockSpec((span, depth), lambda s, p: (0, 0)),
            pl.BlockSpec((1, depth), lambda s, p: (0, 0)),
            pl.BlockSpec((depth, wide), lambda s, p: (0, ((s // per) % 3) * stride + column(s, p))),
            pl.BlockSpec((span, wide), lambda s, p: (0, column(s, p))),
            pl.BlockSpec((HALF, span), lambda s, p: (0, 0)),
            pl.BlockSpec((HALF, span), lambda s, p: (0, 0)),
        ],
        out_specs=[pl.BlockSpec((1, wide, span), out_map(number)) for number in range(count)]
        + [pl.BlockSpec((span, depth), lambda s, p: (0, 0))],
    )
    results = pl.pallas_call(
        functools.partial(project_kernel, count, per, wide),
        out_shape=[jax.ShapeDtypeStruct((3, width, span), BF16)] * count
        + [jax.ShapeDtypeStruct((span, depth), BF16)],
        grid_spec=grid_spec,
        compiler_params=pltpu.CompilerParams(
            dimension_semantics=("arbitrary",), vmem_limit_bytes=48 * MIB
        ),
        cost_estimate=pl.CostEstimate(
            flops=6 * span * depth * depth,
            bytes_accessed=2 * (5 * span * depth + 3 * depth * depth),
            transcendentals=0,
        ),
        name="project",
    )(rank, x, gain, weight, first, cosine, sine)
    return (results[:count], results[count])


def norm_backward(values, scale, gain, grad_normed):
    weighted = grad_normed * gain
    inner = jnp.mean(weighted * values, axis=-1, keepdims=True)
    grad_values = scale * weighted - values * (scale * scale * scale) * inner
    grad_gain = jnp.sum(grad_normed * values * scale, axis=0)
    return (grad_values, grad_gain)


def inverse_rms(values):
    return lax.rsqrt(jnp.mean(values * values, axis=-1, keepdims=True) + epsilon)


def mm(subscripts, a, b):
    return jnp.einsum(subscripts, a, b, preferred_element_type=F32)


def shards(
    inputs,
    first_values,
    out_grad,
    attn_gain,
    query_weight,
    key_weight,
    value_weight,
    output_weight,
    mlp_gain,
    gate_weight,
    up_weight,
    down_weight,
):
    slots, tok, _ = inputs.shape
    groups = lax.axis_size("seq")
    count = groups // slots
    length = tok * groups
    span = slots * tok
    seat = lax.axis_index("seq")
    side = seat // count
    rank = seat % count
    width = D // count
    both = ("fsdp", "seq")

    def to_sequence(values):
        taken = [lax.dynamic_index_in_dim(values, side, 0, keepdims=False)]
        for jump in range(1, slots):
            sent = lax.dynamic_index_in_dim(values, (side + jump) % slots, 0, keepdims=False)
            pairs = [(i, (i + jump * count) % groups) for i in range(groups)]
            taken.append(lax.ppermute(sent, "seq", pairs))
        return jnp.concatenate(taken, axis=0)

    def to_home(values):
        rows = [values[:tok].astype(F32)]
        for jump in range(1, slots):
            sent = values[jump * tok : (jump + 1) * tok].astype(BF16)
            pairs = [((i + jump * count) % groups, i) for i in range(groups)]
            rows.append(lax.ppermute(sent, "seq", pairs).astype(F32))
        if slots == 2:
            swap = side == 1
            return jnp.stack([jnp.where(swap, rows[1], rows[0]), jnp.where(swap, rows[0], rows[1])])
        stacked = jnp.zeros((slots, tok, D), F32)
        for jump in range(slots):
            stacked = lax.dynamic_update_index_in_dim(
                stacked, rows[jump], (side + jump) % slots, 0
            )
        return stacked

    def exchange(pieces):
        received = []
        for jump in range(1, count):
            pairs = [
                (i, (i // count) * count + (i % count + jump) % count) for i in range(groups)
            ]
            received.append(lax.ppermute(pieces[jump - 1], "seq", pairs))
        return received + [pieces[count - 1]]

    def exchange_back(pieces):
        received = []
        for jump in range(1, count):
            pairs = [
                ((i // count) * count + (i % count + jump) % count, i) for i in range(groups)
            ]
            received.append(lax.ppermute(pieces[jump - 1], "seq", pairs))
        return received + [pieces[count - 1]]

    def join(pieces, axis):
        if count == 2:
            odd = rank == 1
            return jnp.concatenate(
                [
                    jnp.where(odd, pieces[0], pieces[1]),
                    jnp.where(odd, pieces[1], pieces[0]),
                ],
                axis=axis,
            )
        size = pieces[0].shape[axis]
        shape = list(pieces[0].shape)
        shape[axis] = size * count
        whole = jnp.zeros(shape, pieces[0].dtype)
        for number in range(count):
            whole = lax.dynamic_update_slice_in_dim(
                whole, pieces[number], ((rank + 1 + number) % count) * size, axis
            )
        return whole

    def gather(shard):
        part = shard.shape[0] // groups
        own = lax.dynamic_slice_in_dim(shard, seat * part, part, 0)
        return lax.all_gather(own, both, axis=0, tiled=True)

    def scatter(total):
        part = lax.psum_scatter(total.astype(BF16), both, scatter_dimension=0, tiled=True)
        return lax.all_gather(part, "seq", axis=0, tiled=True).astype(F32)

    steps = jnp.arange(slots, dtype=jnp.int32)
    starts = ((side - steps) % slots) * (count * tok) + rank * tok
    positions = (starts[:, None] + jnp.arange(tok, dtype=jnp.int32)[None]).reshape(span)
    freqs = rope_base ** (-(jnp.arange(HALF, dtype=F32) * 2.0 / HEAD_DIM))

    def tables(positions):
        angles = freqs[:, None] * positions.astype(F32)[None, :]
        return (jnp.cos(angles), jnp.sin(angles))

    cosine, sine = tables(positions)
    full_cos, full_sin = tables(jnp.arange(length, dtype=jnp.int32))
    sources = jnp.concatenate(
        [(rank - 1 - jnp.arange(count - 1, dtype=jnp.int32)) % count, rank[None]]
    ).astype(jnp.int32)
    order = (((side - steps) % slots)[None, :] * count + sources[:, None]).reshape(-1)
    order = order.astype(jnp.int32)

    qkv_weight = gather(jnp.concatenate([query_weight, key_weight, value_weight], axis=1))
    gains = lax.all_gather(
        jnp.stack([attn_gain, mlp_gain]), "fsdp", axis=1, tiled=True
    ).astype(F32)
    gain_attn, gain_mlp = gains[0:1], gains[1:2]
    tokens = to_sequence(inputs)
    firsts = to_sequence(first_values)
    grads = to_sequence(out_grad)
    output_full = gather(output_weight)
    gate_full = gather(gate_weight)
    up_full = gather(up_weight)
    down_full = gather(down_weight)

    resid = tokens.astype(F32)
    heads, normed_low = project(
        tokens, gain_attn.astype(BF16), qkv_weight, firsts, cosine, sine, rank[None], count
    )
    pieces = exchange(heads)
    mixes, lse = attend(pieces, order, slots)
    attended = join(exchange_back(mixes), 0)
    middle = resid + mm("ht,ho->to", attended, output_full)
    mlp_scale = inverse_rms(middle)
    normed2_low = (middle * mlp_scale * gain_mlp).astype(BF16)
    gate = mm("td,df->tf", normed2_low, gate_full)
    up_proj = mm("td,df->tf", normed2_low, up_full)
    sigma = jax.nn.sigmoid(gate)
    silu_gate = gate * sigma
    active = (silu_gate * up_proj).astype(BF16)
    outputs = middle + mm("tf,fd->td", active, down_full)
    grad_active = mm("td,fd->tf", grads, down_full)
    grad_gate = (grad_active * up_proj * sigma * (1.0 + gate * (1.0 - sigma))).astype(BF16)
    grad_up = (grad_active * silu_gate).astype(BF16)
    down_grad = mm("tf,td->fd", active, grads)
    gate_grad = mm("td,tf->df", normed2_low, grad_gate)
    up_grad = mm("td,tf->df", normed2_low, grad_up)
    grad_normed2 = mm("tf,df->td", grad_gate, gate_full) + mm("tf,df->td", grad_up, up_full)
    grad_middle, mlp_gain_grad = norm_backward(middle, mlp_scale, gain_mlp, grad_normed2)
    grad_middle = grad_middle + grads.astype(F32)
    low_grad_middle = grad_middle.astype(BF16)
    output_grad = mm("ht,to->ho", attended, low_grad_middle)
    grad_attended = mm("to,ho->ht", low_grad_middle, output_full).astype(BF16)
    grad_pieces = [
        lax.dynamic_slice_in_dim(grad_attended, ((rank + 1 + d) % count) * width, width, 0)
        for d in range(count)
    ]
    grad_heads = exchange(grad_pieces)
    back = attend_back(pieces, mixes, grad_heads, lse, full_cos, full_sin, order, slots)
    grad_qkv = join(exchange_back(back), 1)
    grad_query, grad_key, grad_mixed = grad_qkv[0], grad_qkv[1], grad_qkv[2]
    half_mixed = 0.5 * grad_mixed.astype(F32)
    half_low = half_mixed.astype(BF16)
    first_grad = half_mixed.T
    query_grad = mm("td,ct->dc", normed_low, grad_query)
    key_grad = mm("td,ct->dc", normed_low, grad_key)
    value_grad = mm("td,ct->dc", normed_low, half_low)
    grad_normed = mm("ct,dc->td", grad_query, qkv_weight[:, :D])
    grad_normed = grad_normed + mm("ct,dc->td", grad_key, qkv_weight[:, D : 2 * D])
    grad_normed = grad_normed + mm("ct,dc->td", half_low, qkv_weight[:, 2 * D :])
    grad_resid, attn_gain_grad = norm_backward(resid, inverse_rms(resid), gain_attn, grad_normed)
    input_grad = grad_resid + grad_middle
    gain_grads = lax.psum(jnp.stack([attn_gain_grad, mlp_gain_grad]), both)
    part = attn_gain.shape[0]
    gain_grads = lax.dynamic_slice_in_dim(gain_grads, lax.axis_index("fsdp") * part, part, 1)
    qkv_grad = scatter(jnp.concatenate([query_grad, key_grad, value_grad], axis=1))
    return (
        to_home(outputs),
        to_home(input_grad),
        to_home(first_grad),
        gain_grads[0],
        gain_grads[1],
        qkv_grad[:, :D],
        qkv_grad[:, D : 2 * D],
        qkv_grad[:, 2 * D :],
        scatter(output_grad),
        scatter(gate_grad),
        scatter(up_grad),
        scatter(down_grad),
    )


def solution(mesh):
    token_spec = P("fsdp", "seq", None)
    weight_spec = P("fsdp", None)
    gain_spec = P("fsdp")
    return jax.shard_map(
        shards,
        mesh=mesh,
        in_specs=(token_spec,) * 3
        + (gain_spec,)
        + (weight_spec,) * 4
        + (gain_spec,)
        + (weight_spec,) * 3,
        out_specs=(token_spec,) * 3 + (gain_spec,) * 2 + (weight_spec,) * 7,
        check_vma=False,
    )
```

```python
import functools

import jax
import jax.numpy as jnp
from jax import lax
from jax.experimental import pallas as pl
from jax.experimental.pallas import tpu as pltpu
from jax.sharding import PartitionSpec as P

D = 1024
HEADS = 16
HEAD_DIM = 64
HALF = HEAD_DIM // 2
PAIR = 2 * HEAD_DIM
F32 = jnp.float32
BF16 = jnp.bfloat16
NEG = -1e30
MIB = 1024 * 1024
epsilon = 1e-06
rope_base = 10000.0


def dot(a, b):
    return lax.dot_general(a, b, (((1,), (0,)), ((), ())), preferred_element_type=F32)


def head_rows(value, head):
    row = lax.broadcasted_iota(jnp.int32, value.shape, 0)
    return jnp.where((row // HEAD_DIM) == head, value, jnp.zeros_like(value))


def head_lanes(value, head):
    lane = lax.broadcasted_iota(jnp.int32, value.shape, 1)
    return jnp.where((lane // HEAD_DIM) == head, value, jnp.zeros_like(value))


def causal(scores):
    side = scores.shape[0]
    square = scores[:, :side]
    key = lax.broadcasted_iota(jnp.int32, square.shape, 0)
    query = lax.broadcasted_iota(jnp.int32, square.shape, 1)
    square = jnp.where(key <= query, square, NEG)
    if scores.shape[1] == side:
        return square
    return jnp.concatenate([square, scores[:, side:]], axis=1)


def attend_kernel(count, slots, tok, tile_k, order, *refs):
    pieces = refs[:count]
    outs = refs[count : 2 * count]
    lse_ref = refs[2 * count]
    qz, kn, vt, ot = refs[2 * count + 1 :]
    for source in range(count):
        for slot in range(slots):
            cols = pl.ds(pl.multiple_of(order[source * slots + slot] * tok, tok), tok)
            take = slice(slot * tok, (slot + 1) * tok)
            query = pieces[source][0, :, take] * jnp.asarray(HEAD_DIM**-0.5, BF16)
            for head in range(2):
                qz[head, :, cols] = head_rows(query, head)
            kn[cols, :] = pieces[source][1, :, take].T
            vt[:, cols] = pieces[source][2, :, take]
    length = count * slots * tok


    def score(sub, head):
        start = sub * tile_k
        return causal(dot(kn[start : start + tile_k, :], qz[head, :, start:]))

    def absorb(sub, head, carry, scores):
        peak, total, mixed = carry
        start = sub * tile_k
        new_peak = jnp.maximum(peak, jnp.max(scores, axis=0, keepdims=True))
        weights = jnp.exp(scores - new_peak)
        fade = jnp.exp(peak - new_peak)
        total = total * fade + jnp.sum(weights, axis=0, keepdims=True)
        values = vt[head * HEAD_DIM : (head + 1) * HEAD_DIM, start : start + tile_k]
        mixed = mixed * fade + dot(values, weights.astype(BF16))
        return (new_peak, total, mixed)

    tiles = [(sub, head) for sub in range(length // tile_k) for head in range(2)]
    carries = [
        (
            jnp.full((1, length), NEG, F32),
            jnp.zeros((1, length), F32),
            jnp.zeros((HEAD_DIM, length), F32),
        )
        for _ in range(2)
    ]
    ahead = score(*tiles[0])
    for number, (sub, head) in enumerate(tiles):
        scores = ahead
        if number + 1 < len(tiles):
            ahead = score(*tiles[number + 1])
        peak, total, mixed = absorb(sub, head, carries[head], scores)
        done = slice(sub * tile_k, (sub + 1) * tile_k)
        rows = slice(head * HEAD_DIM, (head + 1) * HEAD_DIM)
        ot[rows, done] = (mixed[:, :tile_k] / total[:, :tile_k]).astype(BF16)
        lse_ref[0, head : head + 1, done] = peak[:, :tile_k] + jnp.log(total[:, :tile_k])
        carries[head] = (peak[:, tile_k:], total[:, tile_k:], mixed[:, tile_k:])
    for source in range(count):
        for slot in range(slots):
            cols = pl.ds(pl.multiple_of(order[source * slots + slot] * tok, tok), tok)
            outs[source][:, slot * tok : (slot + 1) * tok] = ot[:, cols]


def attend(pieces, order, slots):
    count = len(pieces)
    width, span = pieces[0].shape[1:]
    tok = span // slots
    length = count * span
    pairs = width // PAIR
    tile_k = min(256, length)
    grid_spec = pltpu.PrefetchScalarGridSpec(
        num_scalar_prefetch=1,
        grid=(pairs,),
        in_specs=[pl.BlockSpec((3, PAIR, span), lambda p, o: (0, p, 0))] * count,
        out_specs=[pl.BlockSpec((PAIR, span), lambda p, o: (p, 0))] * count
        + [pl.BlockSpec((1, 8, length), lambda p, o: (p, 0, 0))],
        scratch_shapes=[
            pltpu.VMEM((2, PAIR, length), BF16),
            pltpu.VMEM((length, PAIR), BF16),
            pltpu.VMEM((PAIR, length), BF16),
            pltpu.VMEM((PAIR, length), BF16),
        ],
    )
    area = pairs * 2 * length * length // 2
    results = pl.pallas_call(
        functools.partial(attend_kernel, count, slots, tok, tile_k),
        out_shape=[jax.ShapeDtypeStruct((width, span), BF16)] * count
        + [jax.ShapeDtypeStruct((pairs, 8, length), F32)],
        grid_spec=grid_spec,
        compiler_params=pltpu.CompilerParams(
            dimension_semantics=("arbitrary",), vmem_limit_bytes=48 * MIB
        ),
        cost_estimate=pl.CostEstimate(
            flops=area * 1024, bytes_accessed=8 * width * length, transcendentals=area
        ),
        name="attend",
    )(order, *pieces)
    return (results[:count], results[count])


def attend_back_kernel(count, slots, tok, tile_q, tile_k, order, *refs):
    pieces = refs[:count]
    mixes = refs[count : 2 * count]
    grads = refs[2 * count : 3 * count]
    lse_ref, cos_ref, sin_ref = refs[3 * count : 3 * count + 3]
    outs = refs[3 * count + 3 : 4 * count + 3]
    qz, gz, qn, gn, kn, vn, kt, inner, dq, dk, dv = refs[4 * count + 3 :]
    length = count * slots * tok
    for source in range(count):
        for slot in range(slots):
            cols = pl.ds(pl.multiple_of(order[source * slots + slot] * tok, tok), tok)
            take = slice(slot * tok, (slot + 1) * tok)
            query = pieces[source][0, :, take] * jnp.asarray(HEAD_DIM**-0.5, BF16)
            grad = grads[source][:, take]
            query_rows = query.T
            grad_rows = grad.T
            for head in range(2):
                qz[head, :, cols] = head_rows(query, head)
                gz[head, :, cols] = head_rows(grad, head)
                qn[head, cols, :] = head_lanes(query_rows, head)
                gn[head, cols, :] = head_lanes(grad_rows, head)
            key = pieces[source][1, :, take]
            kt[:, cols] = key
            kn[cols, :] = key.T
            vn[cols, :] = pieces[source][2, :, take].T
            both = grad.astype(F32) * mixes[source][:, take].astype(F32)
            for head in range(2):
                inner[head : head + 1, cols] = jnp.sum(
                    both[head * HEAD_DIM : (head + 1) * HEAD_DIM], axis=0, keepdims=True
                )
    dq[...] = jnp.zeros_like(dq)
    steps = tile_q // tile_k

    def tile(key_start, query_start, width, masked, carry):
        grad_keys, grad_values = carry
        keys = kn[pl.ds(key_start, tile_k), :]
        values = vn[pl.ds(key_start, tile_k), :]
        cols = pl.ds(query_start, width)
        for head in range(2):
            rows = slice(head * HEAD_DIM, (head + 1) * HEAD_DIM)
            scores = dot(keys, qz[head, :, cols])
            if masked:
                scores = causal(scores)
            probs = jnp.exp(scores - lse_ref[0, head : head + 1, cols])
            grad_probs = dot(values, gz[head, :, cols])
            grad_scores = (probs * (grad_probs - inner[head : head + 1, cols])).astype(BF16)
            grad_values = grad_values + dot(probs.astype(BF16), gn[head, cols, :])
            grad_keys = grad_keys + dot(grad_scores, qn[head, cols, :])
            dq[rows, cols] += dot(kt[rows, pl.ds(key_start, tile_k)], grad_scores)
        return (grad_keys, grad_values)

    def one(number, _):
        base = pl.multiple_of(number * tile_q, tile_q)
        for sub in range(steps):
            skip = sub * tile_k
            key_start = pl.multiple_of(base + skip, tile_k)
            carry = (jnp.zeros((tile_k, PAIR), F32), jnp.zeros((tile_k, PAIR), F32))
            carry = tile(key_start, key_start, tile_q - skip, True, carry)

            def body(step, carry):
                return tile(
                    key_start, pl.multiple_of(step * tile_q, tile_q), tile_q, False, carry
                )

            carry = lax.fori_loop(number + 1, length // tile_q, body, carry)
            dk[pl.ds(key_start, tile_k), :] = carry[0]
            dv[pl.ds(key_start, tile_k), :] = carry[1]
        return 0

    lax.fori_loop(0, length // tile_q, one, 0)
    half = HEAD_DIM // 2
    for source in range(count):
        for slot in range(slots):
            cols = pl.ds(pl.multiple_of(order[source * slots + slot] * tok, tok), tok)
            take = slice(slot * tok, (slot + 1) * tok)
            cosine = cos_ref[:, cols]
            sine = sin_ref[:, cols]
            for which, grad in enumerate((dq[:, cols] * (HEAD_DIM**-0.5), dk[cols, :].T)):
                for head in range(2):
                    low = head * HEAD_DIM
                    first = grad[low : low + half]
                    second = grad[low + half : low + 2 * half]
                    outs[source][which, low : low + half, take] = (
                        first * cosine + second * sine
                    ).astype(BF16)
                    outs[source][which, low + half : low + 2 * half, take] = (
                        second * cosine - first * sine
                    ).astype(BF16)
            outs[source][2, :, take] = dv[cols, :].T.astype(BF16)


def attend_back(pieces, mixes, grads, lse, cosine, sine, order, slots):
    count = len(pieces)
    width, span = pieces[0].shape[1:]
    tok = span // slots
    length = count * span
    pairs = width // PAIR
    tile_q = min(512, length)
    tile_k = min(256, length)
    triple = pl.BlockSpec((3, PAIR, span), lambda p, o: (0, p, 0))
    single = pl.BlockSpec((PAIR, span), lambda p, o: (p, 0))
    table = pl.BlockSpec((HEAD_DIM // 2, length), lambda p, o: (0, 0))
    grid_spec = pltpu.PrefetchScalarGridSpec(
        num_scalar_prefetch=1,
        grid=(pairs,),
        in_specs=[triple] * count
        + [single] * (2 * count)
        + [pl.BlockSpec((1, 8, length), lambda p, o: (p, 0, 0)), table, table],
        out_specs=[triple] * count,
        scratch_shapes=[
            pltpu.VMEM((2, PAIR, length), BF16),
            pltpu.VMEM((2, PAIR, length), BF16),
            pltpu.VMEM((2, length, PAIR), BF16),
            pltpu.VMEM((2, length, PAIR), BF16),
            pltpu.VMEM((length, PAIR), BF16),
            pltpu.VMEM((length, PAIR), BF16),
            pltpu.VMEM((PAIR, length), BF16),
            pltpu.VMEM((8, length), F32),
            pltpu.VMEM((PAIR, length), F32),
            pltpu.VMEM((length, PAIR), F32),
            pltpu.VMEM((length, PAIR), F32),
        ],
    )
    area = pairs * 2 * length * length // 2
    return pl.pallas_call(
        functools.partial(attend_back_kernel, count, slots, tok, tile_q, tile_k),
        out_shape=[jax.ShapeDtypeStruct((3, width, span), BF16)] * count,
        grid_spec=grid_spec,
        compiler_params=pltpu.CompilerParams(
            dimension_semantics=("arbitrary",), vmem_limit_bytes=56 * MIB
        ),
        cost_estimate=pl.CostEstimate(
            flops=area * 2560, bytes_accessed=16 * width * length, transcendentals=area
        ),
        name="attend_back",
    )(order, *pieces, *mixes, *grads, lse, cosine, sine)


def nt(a, b):
    return lax.dot_general(a, b, (((1,), (1,)), ((), ())), preferred_element_type=F32)


def whole_block(shape):
    zeros = (0,) * len(shape)
    return pl.BlockSpec(shape, lambda *_: zeros)


def parameters(mib):
    return pltpu.CompilerParams(dimension_semantics=("arbitrary",), vmem_limit_bytes=mib * MIB)


def project_kernel(slots, tok, count, rows, place, *refs):
    xs, firsts = refs[:slots], refs[slots : 2 * slots]
    own = refs[2 * slots : 2 * slots + count]
    other = refs[2 * slots + count : 2 * slots + 2 * count]
    cos_ref, sin_ref = refs[2 * slots + 2 * count : 2 * slots + 2 * count + 2]
    other_ref, own_ref, normed_ref, full_ref, gains_ref, column = refs[2 * slots + 2 * count + 2 :]
    step = pl.program_id(0)
    target, kind = step // 3, step % 3
    core = place[1]
    half = jnp.where(target == 0, 1 - core, core)
    depth = normed_ref.shape[1]
    wide = own_ref.shape[1]

    @pl.when(step == 0)
    def _():
        for number in range(count):
            at = pl.ds(pl.multiple_of(place[2 + number] * rows, rows), rows)
            full_ref[core, at, :] = own[number][:, : 3 * wide]
            full_ref[1 - core, at, :] = other[number][:, : 3 * wide]
            column[at, :] = own[number][:, 3 * wide :]
        gains_ref[...] = column[...].T[:8].astype(F32)
        gain = gains_ref[0:1, :]
        for slot in range(slots):
            values = xs[slot][...].reshape(tok, depth).astype(F32)
            scale = lax.rsqrt(jnp.mean(values * values, axis=1, keepdims=True) + epsilon)
            normed_ref[slot * tok : (slot + 1) * tok, :] = (values * scale * gain).astype(BF16)

    weight = full_ref[half, :, pl.ds(pl.multiple_of(kind * wide, wide), wide)]
    raw = nt(weight.T, normed_ref[...])

    def store(value):
        @pl.when(target == 0)
        def _():
            other_ref[0] = value

        @pl.when(target == 1)
        def _():
            own_ref[0] = value

    @pl.when(kind < 2)
    def _():
        parts = raw.reshape(wide // HEAD_DIM, 2, HALF, raw.shape[1])
        first, second = parts[:, 0], parts[:, 1]
        cosine, sine = cos_ref[...][None], sin_ref[...][None]
        turned = jnp.stack(
            [first * cosine - second * sine, first * sine + second * cosine], axis=1
        )
        store(turned.reshape(raw.shape).astype(BF16))

    @pl.when(kind == 2)
    def _():
        first = jnp.concatenate(
            [ref[...].reshape(tok, wide).T.astype(F32) for ref in firsts], axis=1
        )
        store((0.5 * raw + 0.5 * first).astype(BF16))


def project(inputs, received, firsts, firsts_received, own, other, cosine, sine, place):
    slots, tok, depth = inputs.shape
    count, rows = len(own), own[0].shape[0]
    wide = depth // 2
    span = slots * tok

    def half(s, p):
        return jnp.where(s < 3, 1 - p[1], p[1])

    x_specs = [pl.BlockSpec((1, tok, depth), lambda s, p: (p[0], 0, 0))]
    x_specs += [whole_block((tok, depth))] * (slots - 1)
    first_specs = [pl.BlockSpec((1, tok, wide), lambda s, p: (p[0], 0, half(s, p)))]
    first_specs += [pl.BlockSpec((tok, wide), lambda s, p: (0, half(s, p)))] * (slots - 1)
    grid_spec = pltpu.PrefetchScalarGridSpec(
        num_scalar_prefetch=1,
        grid=(6,),
        in_specs=x_specs
        + first_specs
        + [whole_block(own[0].shape)] * (2 * count)
        + [whole_block((HALF, span))] * 2,
        out_specs=[
            pl.BlockSpec((1, wide, span), lambda s, p: (jnp.minimum(s, 2), 0, 0)),
            pl.BlockSpec((1, wide, span), lambda s, p: (jnp.maximum(s - 3, 0), 0, 0)),
            whole_block((span, depth)),
            whole_block((2, depth, 3 * wide)),
            whole_block((8, depth)),
        ],
        scratch_shapes=[pltpu.VMEM((depth, 128), BF16)],
    )
    return pl.pallas_call(
        functools.partial(project_kernel, slots, tok, count, rows),
        out_shape=[
            jax.ShapeDtypeStruct((3, wide, span), BF16),
            jax.ShapeDtypeStruct((3, wide, span), BF16),
            jax.ShapeDtypeStruct((span, depth), BF16),
            jax.ShapeDtypeStruct((2, depth, 3 * wide), BF16),
            jax.ShapeDtypeStruct((8, depth), F32),
        ],
        grid_spec=grid_spec,
        compiler_params=parameters(56),
        cost_estimate=pl.CostEstimate(
            flops=6 * span * depth * depth,
            bytes_accessed=2 * (8 * span * depth + 6 * depth * depth),
            transcendentals=0,
        ),
        name="project",
    )(place, inputs, *received, firsts, *firsts_received, *own, *other, cosine, sine)


def output_kernel(slots, tok, count, rows, place, *refs):
    xs = refs[:slots]
    own = refs[slots : slots + count]
    other = refs[slots + count : slots + 2 * count]
    att_other, att_own, gains_ref = refs[slots + 2 * count : slots + 2 * count + 3]
    middle_ref, normed_ref, full_ref = refs[slots + 2 * count + 3 :]
    step = pl.program_id(0)
    core = place[1]
    wide = att_own.shape[0]
    depth = 2 * wide
    mine = pl.ds(pl.multiple_of(core * wide, wide), wide)
    others = pl.ds(pl.multiple_of((1 - core) * wide, wide), wide)

    @pl.when(step == 0)
    def _():
        for number in range(count):
            at = pl.ds(pl.multiple_of(place[2 + number] * rows, rows), rows)
            full_ref[at, mine] = own[number][...]
            full_ref[at, others] = other[number][...]

    total = dot(att_own[...].T, full_ref[mine, :]) + dot(att_other[...].T, full_ref[others, :])
    for slot in range(slots):

        @pl.when(step == slot)
        def _(slot=slot):
            middle_ref[...] = xs[slot][...].reshape(tok, depth).astype(F32) + total

    middle = middle_ref[...]
    scale = lax.rsqrt(jnp.mean(middle * middle, axis=1, keepdims=True) + epsilon)
    normed_ref[...] = (middle * scale * gains_ref[1:2, :]).astype(BF16)


def output_projection(inputs, received, own, other, att_other, att_own, gains, place):
    slots, tok, depth = inputs.shape
    count, rows = len(own), own[0].shape[0]
    wide = depth // 2
    span = slots * tok
    x_specs = [pl.BlockSpec((1, tok, depth), lambda s, p: (p[0], 0, 0))]
    x_specs += [whole_block((tok, depth))] * (slots - 1)
    grid_spec = pltpu.PrefetchScalarGridSpec(
        num_scalar_prefetch=1,
        grid=(slots,),
        in_specs=x_specs
        + [whole_block(own[0].shape)] * (2 * count)
        + [pl.BlockSpec((wide, tok), lambda s, p: (0, s))] * 2
        + [whole_block((8, depth))],
        out_specs=[
            pl.BlockSpec((tok, depth), lambda s, p: (s, 0)),
            pl.BlockSpec((tok, depth), lambda s, p: (s, 0)),
            whole_block((depth, depth)),
        ],
    )
    return pl.pallas_call(
        functools.partial(output_kernel, slots, tok, count, rows),
        out_shape=[
            jax.ShapeDtypeStruct((span, depth), F32),
            jax.ShapeDtypeStruct((span, depth), BF16),
            jax.ShapeDtypeStruct((depth, depth), BF16),
        ],
        grid_spec=grid_spec,
        compiler_params=parameters(56),
        cost_estimate=pl.CostEstimate(
            flops=2 * span * depth * depth,
            bytes_accessed=12 * span * depth + 4 * depth * depth,
            transcendentals=0,
        ),
        name="output_projection",
    )(place, inputs, *received, *own, *other, att_other, att_own, gains)


def mlp_kernel(slots, tok, count, rows, down_rows, blocks, place, *refs):
    grads = refs[:slots]
    middle_ref, normed_ref, gains_ref = refs[slots : slots + 3]
    base = slots + 3
    own_gu, other_gu = refs[base : base + count], refs[base + count : base + 2 * count]
    own_d, other_d = refs[base + 2 * count : base + 3 * count], refs[base + 3 * count : base + 4 * count]
    (
        out_ref,
        send_ref,
        grad_ref,
        low_ref,
        gain_ref,
        gu_send,
        gu_keep,
        d_send,
        d_keep,
        wgu,
        wd,
        og,
        normed_t,
        acc,
        back,
        sems,
    ) = refs[base + 4 * count :]
    step = pl.program_id(0)
    core = place[1]
    depth = og.shape[1]
    wide = depth // 2
    strip = 128
    mine = pl.ds(pl.multiple_of(core * wide, wide), wide)
    others = pl.ds(pl.multiple_of((1 - core) * wide, wide), wide)

    def loads():
        copies = []
        for number in range(count):
            at = pl.ds(pl.multiple_of(place[2 + number] * rows, rows), rows)
            copies.append((own_gu[number], wgu.at[0, at, :], 0))
            copies.append((other_gu[number], wgu.at[1, at, :], 0))
        for number in range(count):
            at = pl.ds(pl.multiple_of(place[2 + number] * down_rows, down_rows), down_rows)
            copies.append((own_d[number], wd.at[at, mine], 1))
            copies.append((other_d[number], wd.at[at, others], 1))
        return [
            pltpu.make_async_copy(source, target, sems.at[number])
            for number, (source, target, _) in enumerate(copies)
        ]

    @pl.when(step == 0)
    def _():
        copies = loads()
        for copy in copies:
            copy.start()
        for slot in range(slots):
            og[slot * tok : (slot + 1) * tok, :] = grads[slot][...].reshape(tok, depth)
        normed_t[...] = normed_ref[...].T
        acc[...] = jnp.zeros_like(acc)
        back[...] = jnp.zeros_like(back)
        for copy in copies:
            copy.wait()

    half_width = blocks * strip
    at = pl.ds(pl.multiple_of(step * strip, strip), strip)
    up_at = pl.ds(pl.multiple_of(half_width + step * strip, strip), strip)
    gate_w = jnp.concatenate([wgu[0, :, at], wgu[1, :, at]], axis=1)
    up_w = jnp.concatenate([wgu[0, :, up_at], wgu[1, :, up_at]], axis=1)
    own_rows = pl.ds(pl.multiple_of(core * half_width + step * strip, strip), strip)
    other_rows = pl.ds(pl.multiple_of((1 - core) * half_width + step * strip, strip), strip)
    down_w = jnp.concatenate([wd[own_rows, :], wd[other_rows, :]], axis=0)
    normed = normed_ref[...]
    gate = dot(normed, gate_w)
    up = dot(normed, up_w)
    grad_active = nt(og[...], down_w)
    sigma = jax.nn.sigmoid(gate)
    silu = gate * sigma
    active = (silu * up).astype(BF16)
    grad_up = (grad_active * silu).astype(BF16)
    grad_gate = (grad_active * up * sigma * (1.0 + gate * (1.0 - sigma))).astype(BF16)
    acc[...] += dot(active, down_w)
    back[...] += nt(grad_gate, gate_w) + nt(grad_up, up_w)
    grad_gate_w = dot(normed_t[...], grad_gate).astype(BF16)
    gu_keep[0] = grad_gate_w[:, :strip]
    gu_send[0] = grad_gate_w[:, strip:]
    grad_up_w = dot(normed_t[...], grad_up).astype(BF16)
    gu_keep[1] = grad_up_w[:, :strip]
    gu_send[1] = grad_up_w[:, strip:]
    active_t = active.T
    kept = dot(active_t, og[:, mine]).astype(BF16)
    sent = dot(active_t, og[:, others]).astype(BF16)
    d_keep[core] = kept[:strip]
    d_keep[1 - core] = kept[strip:]
    d_send[core] = sent[:strip]
    d_send[1 - core] = sent[strip:]

    @pl.when(step == blocks - 1)
    def _():
        gain = gains_ref[1:2, :]
        chunk = min(128, tok)
        gain_ref[...] = jnp.zeros_like(gain_ref)
        for slot in range(slots):

            def finish(number, _, slot=slot):
                local = pl.ds(pl.multiple_of(number * chunk, chunk), chunk)
                some = pl.ds(pl.multiple_of(slot * tok + number * chunk, chunk), chunk)
                middle = middle_ref[some, :]
                scale = lax.rsqrt(jnp.mean(middle * middle, axis=1, keepdims=True) + epsilon)
                result = middle + acc[some, :]
                if slot == 0:
                    out_ref[0, local, :] = result
                else:
                    send_ref[pl.ds(pl.multiple_of((slot - 1) * tok + number * chunk, chunk), chunk), :] = (
                        result.astype(BF16)
                    )
                grad = back[some, :]
                gain_ref[0:1, :] += jnp.sum(grad * middle * scale, axis=0, keepdims=True)
                weighted = grad * gain
                inner = jnp.mean(weighted * middle, axis=1, keepdims=True)
                grad_middle = (
                    scale * weighted
                    - middle * (scale * scale * scale) * inner
                    + og[some, :].astype(F32)
                )
                grad_ref[some, :] = grad_middle
                low_ref[some, :] = grad_middle.astype(BF16)
                return 0

            lax.fori_loop(0, tok // chunk, finish, 0)


def mlp(grads, grads_received, middle, normed, gains, gate_up, down, place):
    slots, tok, depth = grads.shape
    own_gu, other_gu = gate_up
    own_d, other_d = down
    count, rows = len(own_gu), own_gu[0].shape[0]
    down_rows = own_d[0].shape[0]
    half_width = own_gu[0].shape[1] // 2
    wide = depth // 2
    span = slots * tok
    blocks = half_width // 128
    once = pl.Buffered(1)
    g_specs = [pl.BlockSpec((1, tok, depth), lambda s, p: (p[0], 0, 0), pipeline_mode=once)]
    g_specs += [pl.BlockSpec((tok, depth), lambda s, p: (0, 0), pipeline_mode=once)] * (slots - 1)
    gu_spec = pl.BlockSpec((2, depth, 128), lambda s, p: (0, 0, s))
    d_spec = pl.BlockSpec((2, 128, wide), lambda s, p: (0, s, 0))
    grid_spec = pltpu.PrefetchScalarGridSpec(
        num_scalar_prefetch=1,
        grid=(blocks,),
        in_specs=g_specs
        + [
            pl.BlockSpec((span, depth), lambda s, p: (0, 0), pipeline_mode=once),
            pl.BlockSpec((span, depth), lambda s, p: (0, 0), pipeline_mode=once),
            whole_block((8, depth)),
        ]
        + [pl.BlockSpec(memory_space=pl.ANY)] * (4 * count),
        out_specs=[
            pl.BlockSpec((1, tok, depth), lambda s, p: (p[0], 0, 0), pipeline_mode=once),
            pl.BlockSpec(((slots - 1) * tok, depth), lambda s, p: (0, 0), pipeline_mode=once),
            pl.BlockSpec((span, depth), lambda s, p: (0, 0), pipeline_mode=once),
            pl.BlockSpec((span, depth), lambda s, p: (0, 0), pipeline_mode=once),
            whole_block((8, depth)),
            gu_spec,
            gu_spec,
            d_spec,
            d_spec,
        ],
        scratch_shapes=[
            pltpu.VMEM((2, depth, 2 * half_width), BF16),
            pltpu.VMEM((2 * half_width, depth), BF16),
            pltpu.VMEM((span, depth), BF16),
            pltpu.VMEM((depth, span), BF16),
            pltpu.VMEM((span, depth), F32),
            pltpu.VMEM((span, depth), F32),
            pltpu.SemaphoreType.DMA((4 * count,)),
        ],
    )
    return pl.pallas_call(
        functools.partial(mlp_kernel, slots, tok, count, rows, down_rows, blocks),
        out_shape=[
            jax.ShapeDtypeStruct((slots, tok, depth), F32),
            jax.ShapeDtypeStruct(((slots - 1) * tok, depth), BF16),
            jax.ShapeDtypeStruct((span, depth), F32),
            jax.ShapeDtypeStruct((span, depth), BF16),
            jax.ShapeDtypeStruct((8, depth), F32),
            jax.ShapeDtypeStruct((2, depth, half_width), BF16),
            jax.ShapeDtypeStruct((2, depth, half_width), BF16),
            jax.ShapeDtypeStruct((2, half_width, wide), BF16),
            jax.ShapeDtypeStruct((2, half_width, wide), BF16),
        ],
        grid_spec=grid_spec,
        compiler_params=parameters(63),
        cost_estimate=pl.CostEstimate(
            flops=16 * span * depth * 2 * half_width,
            bytes_accessed=24 * depth * half_width + 20 * span * depth,
            transcendentals=2 * span * half_width,
        ),
        name="mlp",
    )(place, grads, *grads_received, middle, normed, gains, *own_gu, *other_gu, *own_d, *other_d)


def grad_attended_kernel(place, low_ref, full_ref, att_other, att_own, ga_other, ga_own, sent, kept):
    step = pl.program_id(0)
    core = place[1]
    wide = att_own.shape[0]
    mine = pl.ds(pl.multiple_of(core * wide, wide), wide)
    others = pl.ds(pl.multiple_of((1 - core) * wide, wide), wide)
    for number, (att, result) in enumerate(((att_other, ga_other), (att_own, ga_own))):

        @pl.when(step == number)
        def _(att=att, result=result):
            result[...] = nt(full_ref[...], low_ref[...]).astype(BF16)
            kept[...] = dot(att[...], low_ref[:, mine]).astype(BF16)
            sent[...] = dot(att[...], low_ref[:, others]).astype(BF16)


def grad_attended(low, full, att_other, att_own, place):
    span, depth = low.shape
    wide = depth // 2

    def half(s, p):
        return jnp.where(s == 0, 1 - p[1], p[1])

    row_spec = pl.BlockSpec((wide, wide), lambda s, p: (half(s, p), 0))
    grid_spec = pltpu.PrefetchScalarGridSpec(
        num_scalar_prefetch=1,
        grid=(2,),
        in_specs=[
            whole_block((span, depth)),
            pl.BlockSpec((wide, depth), lambda s, p: (half(s, p), 0)),
            whole_block((wide, span)),
            whole_block((wide, span)),
        ],
        out_specs=[whole_block((wide, span)), whole_block((wide, span)), row_spec, row_spec],
    )
    return pl.pallas_call(
        grad_attended_kernel,
        out_shape=[
            jax.ShapeDtypeStruct((wide, span), BF16),
            jax.ShapeDtypeStruct((wide, span), BF16),
            jax.ShapeDtypeStruct((depth, wide), BF16),
            jax.ShapeDtypeStruct((depth, wide), BF16),
        ],
        grid_spec=grid_spec,
        compiler_params=parameters(48),
        cost_estimate=pl.CostEstimate(
            flops=4 * span * depth * depth,
            bytes_accessed=6 * span * depth + 4 * depth * depth,
            transcendentals=0,
        ),
        name="grad_attended",
    )(place, low, full, att_other, att_own)


def tail_kernel(slots, tok, place, *refs):
    xs = refs[:slots]
    (
        back_other,
        back_own,
        full_ref,
        normed_ref,
        grad_ref,
        gains_ref,
        mlp_gain_ref,
        out_ref,
        send_ref,
        first_ref,
        first_send,
        gain_ref,
        sent,
        kept,
        normed_t,
        acc,
    ) = refs[slots:]
    step = pl.program_id(0)
    target, kind = step // 3, step % 3
    depth = acc.shape[1]

    @pl.when(step == 0)
    def _():
        normed_t[...] = normed_ref[...].T
        acc[...] = jnp.zeros_like(acc)

    def part(back, result):
        grad = back[0]

        @pl.when(kind == 2)
        def _():
            rows = 0.5 * grad.astype(F32).T
            first_ref[0] = rows[:tok]
            first_send[...] = rows[tok:].astype(BF16)

        grad = grad * jnp.where(kind == 2, 0.5, 1.0).astype(BF16)
        acc[...] += nt(grad.T, full_ref[0])
        result[0] = nt(normed_t[...], grad).astype(BF16)

    @pl.when(target == 0)
    def _():
        part(back_other, sent)

    @pl.when(target == 1)
    def _():
        part(back_own, kept)

    @pl.when(step == 5)
    def _():
        gain = gains_ref[0:1, :]
        chunk = min(128, tok)
        gain_ref[...] = jnp.zeros_like(gain_ref)
        gain_ref[1:2, :] = mlp_gain_ref[0:1, :]
        for slot in range(slots):

            def finish(number, _, slot=slot):
                local = pl.ds(pl.multiple_of(number * chunk, chunk), chunk)
                some = pl.ds(pl.multiple_of(slot * tok + number * chunk, chunk), chunk)
                if slot == 0:
                    values = xs[slot][0, local, :].astype(F32)
                else:
                    values = xs[slot][local, :].astype(F32)
                scale = lax.rsqrt(jnp.mean(values * values, axis=1, keepdims=True) + epsilon)
                grad = acc[some, :]
                gain_ref[0:1, :] += jnp.sum(grad * values * scale, axis=0, keepdims=True)
                weighted = grad * gain
                inner = jnp.mean(weighted * values, axis=1, keepdims=True)
                result = (
                    scale * weighted
                    - values * (scale * scale * scale) * inner
                    + grad_ref[some, :]
                )
                if slot == 0:
                    out_ref[0, local, :] = result
                else:
                    send_ref[pl.ds(pl.multiple_of((slot - 1) * tok + number * chunk, chunk), chunk), :] = (
                        result.astype(BF16)
                    )
                return 0

            lax.fori_loop(0, tok // chunk, finish, 0)


def tail(inputs, received, back_other, back_own, full, normed, grad_middle, gains, mlp_gain, place):
    slots, tok, depth = inputs.shape
    wide = depth // 2
    span = slots * tok
    rest = (slots - 1) * tok
    once = pl.Buffered(1)

    def half(s, p):
        return jnp.where(s < 3, 1 - p[1], p[1])

    x_specs = [pl.BlockSpec((1, tok, depth), lambda s, p: (p[0], 0, 0))]
    x_specs += [whole_block((tok, depth))] * (slots - 1)
    grid_spec = pltpu.PrefetchScalarGridSpec(
        num_scalar_prefetch=1,
        grid=(6,),
        in_specs=x_specs
        + [
            pl.BlockSpec((1, wide, span), lambda s, p: (jnp.minimum(s, 2), 0, 0)),
            pl.BlockSpec((1, wide, span), lambda s, p: (jnp.maximum(s - 3, 0), 0, 0)),
            pl.BlockSpec((1, depth, wide), lambda s, p: (half(s, p), 0, s % 3)),
            whole_block((span, depth)),
            pl.BlockSpec((span, depth), lambda s, p: (0, 0), pipeline_mode=once),
            whole_block((8, depth)),
            whole_block((8, depth)),
        ],
        out_specs=[
            pl.BlockSpec((1, tok, depth), lambda s, p: (p[0], 0, 0)),
            whole_block((rest, depth)),
            pl.BlockSpec((1, tok, wide), lambda s, p: (p[0], 0, half(s, p))),
            pl.BlockSpec((rest, wide), lambda s, p: (0, half(s, p))),
            whole_block((8, depth)),
            pl.BlockSpec((1, depth, wide), lambda s, p: (jnp.minimum(s, 2), 0, 0)),
            pl.BlockSpec((1, depth, wide), lambda s, p: (jnp.maximum(s - 3, 0), 0, 0)),
        ],
        scratch_shapes=[pltpu.VMEM((depth, span), BF16), pltpu.VMEM((span, depth), F32)],
    )
    return pl.pallas_call(
        functools.partial(tail_kernel, slots, tok),
        out_shape=[
            jax.ShapeDtypeStruct((slots, tok, depth), F32),
            jax.ShapeDtypeStruct((rest, depth), BF16),
            jax.ShapeDtypeStruct((slots, tok, depth), F32),
            jax.ShapeDtypeStruct((rest, depth), BF16),
            jax.ShapeDtypeStruct((8, depth), F32),
            jax.ShapeDtypeStruct((3, depth, wide), BF16),
            jax.ShapeDtypeStruct((3, depth, wide), BF16),
        ],
        grid_spec=grid_spec,
        compiler_params=parameters(60),
        cost_estimate=pl.CostEstimate(
            flops=12 * span * depth * depth,
            bytes_accessed=24 * span * depth + 12 * depth * depth,
            transcendentals=0,
        ),
        name="tail",
    )(
        place, inputs, *received, back_other, back_own, full, normed, grad_middle, gains, mlp_gain
    )


def land_kernel(place, whole_ref, part_ref, out_ref):
    out_ref[0] = part_ref[...].astype(F32)


def land(whole, part, slot):
    _, tok, depth = whole.shape
    tile = min(256, tok)
    grid_spec = pltpu.PrefetchScalarGridSpec(
        num_scalar_prefetch=1,
        grid=(tok // tile,),
        in_specs=[
            pl.BlockSpec(memory_space=pl.ANY),
            pl.BlockSpec((tile, depth), lambda s, p: (s, 0)),
        ],
        out_specs=pl.BlockSpec((1, tile, depth), lambda s, p: (p[0], s, 0)),
    )
    return pl.pallas_call(
        land_kernel,
        out_shape=jax.ShapeDtypeStruct(whole.shape, F32),
        grid_spec=grid_spec,
        input_output_aliases={1: 0},
        compiler_params=parameters(16),
        cost_estimate=pl.CostEstimate(
            flops=tok * depth, bytes_accessed=6 * tok * depth, transcendentals=0
        ),
        name="land",
    )(slot, whole, part)


def shards(
    inputs,
    first_values,
    out_grad,
    attn_gain,
    query_weight,
    key_weight,
    value_weight,
    output_weight,
    mlp_gain,
    gate_weight,
    up_weight,
    down_weight,
):
    slots, tok, _ = inputs.shape
    groups = lax.axis_size("seq")
    parts = lax.axis_size("fsdp")
    line = parts // 2
    count = groups // slots
    length = tok * groups
    span = slots * tok
    seat = lax.axis_index("seq")
    shard = lax.axis_index("fsdp")
    side = seat // count
    rank = seat % count
    core = seat % 2
    z, y = shard // 2, shard % 2
    wide = D // 2
    width = D // count

    def along_seq(value, partner):
        return lax.ppermute(value, "seq", [(i, partner(i)) for i in range(groups)])

    def along_fsdp(value, partner):
        return lax.ppermute(value, "fsdp", [(i, partner(i)) for i in range(parts)])

    def to_core(value):
        return along_seq(value, lambda i: i ^ 1)

    def to_y(value):
        return along_fsdp(value, lambda i: i ^ 1)

    def to_z(value, jump):
        return along_fsdp(value, lambda i: (i + 2 * jump) % parts)

    def after(value, *others):
        return lax.optimization_barrier((value,) + others)[0]

    def to_sequence(values):
        taken = []
        for jump in range(1, slots):
            sent = lax.dynamic_index_in_dim(values, (side + jump) % slots, 0, keepdims=False)
            taken.append(along_seq(sent, lambda i: (i + jump * count) % groups))
        return taken

    def to_home(whole, sent):
        for jump in range(1, slots):
            part = sent[(jump - 1) * tok : jump * tok]
            part = along_seq(part, lambda i: (i - jump * count) % groups)
            whole = land(whole, part, ((side + jump) % slots)[None])
        return whole

    def rank_up(i, jump):
        return (i // count) * count + (i % count + jump) % count

    def rank_down(i, jump):
        return (i // count) * count + (i % count - jump) % count

    def halves_to_ranks(other, own, axis):
        if count == 2:
            return [other, own]
        return [
            lax.dynamic_slice_in_dim(
                join(other, own, axis), ((rank + 1 + number) % count) * width, width, axis
            )
            for number in range(count)
        ]

    def join(other, own, axis):
        first = jnp.where(core == 0, own, other)
        second = jnp.where(core == 0, other, own)
        return jnp.concatenate([first, second], axis=axis)

    def ranks_to_halves(pieces, axis):
        if count == 2:
            return pieces
        shape = list(pieces[0].shape)
        shape[axis] = D
        whole = jnp.zeros(shape, pieces[0].dtype)
        for number in range(count):
            whole = lax.dynamic_update_slice_in_dim(
                whole, pieces[number], ((rank + 1 + number) % count) * width, axis
            )
        return [
            lax.dynamic_slice_in_dim(whole, which * wide, wide, axis)
            for which in (1 - core, core)
        ]

    def exchange(pieces):
        received = [
            along_seq(pieces[jump - 1], lambda i: rank_up(i, jump)) for jump in range(1, count)
        ]
        return received + [pieces[count - 1]]

    def exchange_back(pieces):
        received = [
            along_seq(pieces[jump - 1], lambda i: rank_down(i, jump)) for jump in range(1, count)
        ]
        return received + [pieces[count - 1]]

    def split(*weights):
        results = []
        for which in (core, 1 - core):
            columns = []
            for weight in weights:
                size = weight.shape[1] // 2
                columns.append(lax.dynamic_slice_in_dim(weight, which * size, size, 1))
            results.append(columns)
        return results

    def gather_z(half):
        return [half] + [to_z(half, jump) for jump in range(1, line)]

    def gather_rest(along_z, other):
        along_y = [to_y(piece) for piece in along_z]
        own = [piece for pair in zip(along_z, along_y) for piece in pair]
        return (own, [other] + [to_core(piece) for piece in own[1:]])

    numbers = []
    for jump in range(line):
        for flip in range(2):
            numbers.append(((z - jump) % line) * 2 + (y ^ flip))
    place = jnp.stack([side, core] + numbers).astype(jnp.int32)

    def low(value):
        return value.astype(BF16)

    def add(a, b):
        return low(a.astype(F32) + b.astype(F32))

    def pick(value, index, axis):
        return lax.dynamic_index_in_dim(value, index, axis, keepdims=False)

    def scatter(sent, kept, rows_axis):
        shape = kept.shape
        rows = shape[rows_axis] // parts
        cut = shape[:rows_axis] + (line, 2, rows) + shape[rows_axis + 1 :]
        received = to_core(sent).reshape(cut)
        kept = kept.reshape(cut)
        axis = rows_axis + 1
        received_y = to_y(add(pick(kept, 1 - y, axis), pick(received, 1 - y, axis)))
        kept_y = pick(kept, y, axis), pick(received, y, axis)

        def partial(index):
            total = pick(kept_y[0], index, rows_axis).astype(F32)
            total = total + pick(kept_y[1], index, rows_axis).astype(F32)
            return total + pick(received_y, index, rows_axis).astype(F32)

        total = partial(z)
        for jump in range(1, line):
            total = total + to_z(low(partial((z + jump) % line)), jump).astype(F32)
        mine = low(total)
        for jump in range(1, groups // 2):
            total = total + along_seq(mine, lambda i: (i + 2 * jump) % groups).astype(F32)
        mine = low(total)
        return (mine, to_core(mine))

    def columns(mine, others):
        first = jnp.where(core == 0, mine, others)
        second = jnp.where(core == 0, others, mine)
        return jnp.concatenate([first, second], axis=-1).astype(F32)

    def everywhere(value):
        value = value + to_core(value)
        value = value + to_y(value)
        total = value
        for jump in range(1, line):
            total = total + to_z(value, jump)
        value = total
        for jump in range(1, groups // 2):
            total = total + along_seq(value, lambda i: (i + 2 * jump) % groups)
        return total

    steps = jnp.arange(slots, dtype=jnp.int32)
    starts = ((side - steps) % slots) * (count * tok) + rank * tok
    positions = (starts[:, None] + jnp.arange(tok, dtype=jnp.int32)[None]).reshape(span)
    freqs = rope_base ** (-(jnp.arange(HALF, dtype=F32) * 2.0 / HEAD_DIM))

    def tables(positions):
        angles = freqs[:, None] * positions.astype(F32)[None, :]
        return (jnp.cos(angles), jnp.sin(angles))

    cosine, sine = tables(positions)
    full_cos, full_sin = tables(jnp.arange(length, dtype=jnp.int32))
    sources = jnp.concatenate(
        [(rank - 1 - jnp.arange(count - 1, dtype=jnp.int32)) % count, rank[None]]
    ).astype(jnp.int32)
    order = (((side - steps) % slots)[None, :] * count + sources[:, None]).reshape(-1)
    order = order.astype(jnp.int32)

    gains = jnp.pad(jnp.stack([attn_gain, mlp_gain], axis=1), ((0, 0), (0, 126)))
    qkv = [
        jnp.concatenate(half + [gains], axis=1)
        for half in split(query_weight, key_weight, value_weight)
    ]
    gate_up = [jnp.concatenate(half, axis=1) for half in split(gate_weight, up_weight)]
    out_halves = [half[0] for half in split(output_weight)]
    down_halves = [half[0] for half in split(down_weight)]

    tokens = to_sequence(inputs)
    qkv_z = gather_z(qkv[0])
    firsts = to_sequence(after(first_values, *tokens))
    qkv_own, qkv_other = gather_rest(qkv_z, qkv[1])
    out_z = gather_z(after(out_halves[0], *qkv_z))
    gate_up_z = gather_z(after(gate_up[0], *qkv_z))
    down_z = gather_z(after(down_halves[0], *qkv_z))
    grads = to_sequence(after(out_grad, *firsts))
    out_own, out_other = gather_rest(out_z, out_halves[1])
    gate_up_pieces = gather_rest(gate_up_z, gate_up[1])
    down_pieces = gather_rest(down_z, down_halves[1])

    heads_other, heads_own, normed, qkv_full, gains_full = project(
        inputs, tokens, first_values, firsts, qkv_own, qkv_other, cosine, sine, place
    )
    pieces = exchange(halves_to_ranks(heads_other, heads_own, 1))
    mixes, lse = attend(pieces, order, slots)
    att_other, att_own = ranks_to_halves(exchange_back(mixes), 0)
    middle, normed2, out_full = output_projection(
        inputs, tokens, out_own, out_other, att_other, att_own, gains_full, place
    )
    (
        outputs,
        outputs_sent,
        grad_middle,
        low_grad,
        mlp_gain_grad,
        gu_sent,
        gu_kept,
        down_sent,
        down_kept,
    ) = mlp(out_grad, grads, middle, normed2, gains_full, gate_up_pieces, down_pieces, place)
    ga_other, ga_own, out_sent, out_kept = grad_attended(
        low_grad, out_full, att_other, att_own, place
    )
    gate_up_grad = scatter(gu_sent, gu_kept, 1)
    down_grad = scatter(
        down_sent.reshape(-1, wide), down_kept.reshape(-1, wide), 0
    )
    output_grad = scatter(out_sent, out_kept, 0)
    grad_heads = exchange(halves_to_ranks(ga_other, ga_own, 0))
    back = attend_back(pieces, mixes, grad_heads, lse, full_cos, full_sin, order, slots)
    back_other, back_own = ranks_to_halves(exchange_back(back), 1)
    input_grad, input_sent, first_grad, first_sent, gain_grads, qkv_sent, qkv_kept = tail(
        inputs,
        tokens,
        back_other,
        back_own,
        qkv_full,
        normed,
        grad_middle,
        gains_full,
        mlp_gain_grad,
        place,
    )
    qkv_grad = columns(*scatter(qkv_sent, qkv_kept, 1))
    gate_up_grad = columns(*gate_up_grad)
    gain_grads = everywhere(gain_grads)
    gain_grads = lax.dynamic_slice_in_dim(gain_grads, shard * (D // parts), D // parts, 1)
    return (
        to_home(outputs, outputs_sent),
        to_home(input_grad, input_sent),
        to_home(first_grad, first_sent),
        gain_grads[0],
        gain_grads[1],
        qkv_grad[0],
        qkv_grad[1],
        qkv_grad[2],
        columns(*output_grad),
        gate_up_grad[0],
        gate_up_grad[1],
        columns(*down_grad),
    )


def solution(mesh):
    token_spec = P("fsdp", "seq", None)
    weight_spec = P("fsdp", None)
    gain_spec = P("fsdp")
    return jax.shard_map(
        shards,
        mesh=mesh,
        in_specs=(token_spec,) * 3
        + (gain_spec,)
        + (weight_spec,) * 4
        + (gain_spec,)
        + (weight_spec,) * 3,
        out_specs=(token_spec,) * 3 + (gain_spec,) * 2 + (weight_spec,) * 7,
        check_vma=False,
    )
```

```python
import functools

import jax
import jax.numpy as jnp
from jax import lax
from jax.experimental import pallas as pl
from jax.experimental.pallas import tpu as pltpu
from jax.sharding import PartitionSpec as P

D = 1024
HEADS = 16
HEAD_DIM = 64
HALF = HEAD_DIM // 2
PAIR = 2 * HEAD_DIM
F32 = jnp.float32
BF16 = jnp.bfloat16
NEG = -1e30
MIB = 1024 * 1024
epsilon = 1e-06
rope_base = 10000.0


def dot(a, b):
    return lax.dot_general(a, b, (((1,), (0,)), ((), ())), preferred_element_type=F32)


def head_rows(value, head):
    row = lax.broadcasted_iota(jnp.int32, value.shape, 0)
    return jnp.where((row // HEAD_DIM) == head, value, jnp.zeros_like(value))


def head_lanes(value, head):
    lane = lax.broadcasted_iota(jnp.int32, value.shape, 1)
    return jnp.where((lane // HEAD_DIM) == head, value, jnp.zeros_like(value))


def causal(scores):
    side = scores.shape[0]
    square = scores[:, :side]
    key = lax.broadcasted_iota(jnp.int32, square.shape, 0)
    query = lax.broadcasted_iota(jnp.int32, square.shape, 1)
    square = jnp.where(key <= query, square, NEG)
    if scores.shape[1] == side:
        return square
    return jnp.concatenate([square, scores[:, side:]], axis=1)


def attend_body(length, tile_k, qz, kn, vt, ot, lse_ref):
    def score(sub, head):
        start = sub * tile_k
        return causal(dot(kn[start : start + tile_k, :], qz[head, :, start:]))

    def absorb(sub, head, carry, scores):
        peak, total, mixed = carry
        start = sub * tile_k
        new_peak = jnp.maximum(peak, jnp.max(scores, axis=0, keepdims=True))
        weights = jnp.exp(scores - new_peak)
        fade = jnp.exp(peak - new_peak)
        total = total * fade + jnp.sum(weights, axis=0, keepdims=True)
        values = vt[head * HEAD_DIM : (head + 1) * HEAD_DIM, start : start + tile_k]
        mixed = mixed * fade + dot(values, weights.astype(BF16))
        return (new_peak, total, mixed)

    tiles = [(sub, head) for sub in range(length // tile_k) for head in range(2)]
    carries = [
        (
            jnp.full((1, length), NEG, F32),
            jnp.zeros((1, length), F32),
            jnp.zeros((HEAD_DIM, length), F32),
        )
        for _ in range(2)
    ]
    ahead = score(*tiles[0])
    for number, (sub, head) in enumerate(tiles):
        scores = ahead
        if number + 1 < len(tiles):
            ahead = score(*tiles[number + 1])
        peak, total, mixed = absorb(sub, head, carries[head], scores)
        done = slice(sub * tile_k, (sub + 1) * tile_k)
        rows = slice(head * HEAD_DIM, (head + 1) * HEAD_DIM)
        ot[rows, done] = (mixed[:, :tile_k] / total[:, :tile_k]).astype(BF16)
        lse_ref[0, head : head + 1, done] = peak[:, :tile_k] + jnp.log(total[:, :tile_k])
        carries[head] = (peak[:, tile_k:], total[:, tile_k:], mixed[:, tile_k:])


def attend_kernel(count, slots, tok, tile_k, order, *refs):
    pieces = refs[:count]
    outs = refs[count : 2 * count]
    lse_ref = refs[2 * count]
    qz, kn, vt, ot = refs[2 * count + 1 :]
    for source in range(count):
        for slot in range(slots):
            cols = pl.ds(pl.multiple_of(order[source * slots + slot] * tok, tok), tok)
            take = slice(slot * tok, (slot + 1) * tok)
            query = pieces[source][0, :, take] * jnp.asarray(HEAD_DIM**-0.5, BF16)
            for head in range(2):
                qz[head, :, cols] = head_rows(query, head)
            kn[cols, :] = pieces[source][1, :, take].T
            vt[:, cols] = pieces[source][2, :, take]
    length = count * slots * tok
    attend_body(length, tile_k, qz, kn, vt, ot, lse_ref)
    for source in range(count):
        for slot in range(slots):
            cols = pl.ds(pl.multiple_of(order[source * slots + slot] * tok, tok), tok)
            outs[source][:, slot * tok : (slot + 1) * tok] = ot[:, cols]


def attend(pieces, order, slots):
    count = len(pieces)
    width, span = pieces[0].shape[1:]
    tok = span // slots
    length = count * span
    pairs = width // PAIR
    tile_k = min(256, length)
    grid_spec = pltpu.PrefetchScalarGridSpec(
        num_scalar_prefetch=1,
        grid=(pairs,),
        in_specs=[pl.BlockSpec((3, PAIR, span), lambda p, o: (0, p, 0))] * count,
        out_specs=[pl.BlockSpec((PAIR, span), lambda p, o: (p, 0))] * count
        + [pl.BlockSpec((1, 8, length), lambda p, o: (p, 0, 0))],
        scratch_shapes=[
            pltpu.VMEM((2, PAIR, length), BF16),
            pltpu.VMEM((length, PAIR), BF16),
            pltpu.VMEM((PAIR, length), BF16),
            pltpu.VMEM((PAIR, length), BF16),
        ],
    )
    area = pairs * 2 * length * length // 2
    results = pl.pallas_call(
        functools.partial(attend_kernel, count, slots, tok, tile_k),
        out_shape=[jax.ShapeDtypeStruct((width, span), BF16)] * count
        + [jax.ShapeDtypeStruct((pairs, 8, length), F32)],
        grid_spec=grid_spec,
        compiler_params=pltpu.CompilerParams(
            dimension_semantics=("arbitrary",), vmem_limit_bytes=48 * MIB
        ),
        cost_estimate=pl.CostEstimate(
            flops=area * 1024, bytes_accessed=8 * width * length, transcendentals=area
        ),
        name="attend",
    )(order, *pieces)
    return (results[:count], results[count])


def attend_back_kernel(count, slots, tok, tile_q, tile_k, order, *refs):
    pieces = refs[:count]
    mixes = refs[count : 2 * count]
    grads = refs[2 * count : 3 * count]
    lse_ref, cos_ref, sin_ref = refs[3 * count : 3 * count + 3]
    outs = refs[3 * count + 3 : 4 * count + 3]
    qz, gz, qn, gn, kn, vn, kt, inner, dq, dk, dv = refs[4 * count + 3 :]
    length = count * slots * tok
    for source in range(count):
        for slot in range(slots):
            cols = pl.ds(pl.multiple_of(order[source * slots + slot] * tok, tok), tok)
            take = slice(slot * tok, (slot + 1) * tok)
            query = pieces[source][0, :, take] * jnp.asarray(HEAD_DIM**-0.5, BF16)
            grad = grads[source][:, take]
            query_rows = query.T
            grad_rows = grad.T
            for head in range(2):
                qz[head, :, cols] = head_rows(query, head)
                gz[head, :, cols] = head_rows(grad, head)
                qn[head, cols, :] = head_lanes(query_rows, head)
                gn[head, cols, :] = head_lanes(grad_rows, head)
            key = pieces[source][1, :, take]
            kt[:, cols] = key
            kn[cols, :] = key.T
            vn[cols, :] = pieces[source][2, :, take].T
            both = grad.astype(F32) * mixes[source][:, take].astype(F32)
            for head in range(2):
                inner[head : head + 1, cols] = jnp.sum(
                    both[head * HEAD_DIM : (head + 1) * HEAD_DIM], axis=0, keepdims=True
                )
    dq[...] = jnp.zeros_like(dq)
    steps = tile_q // tile_k

    def tile(key_start, query_start, width, masked, carry):
        grad_keys, grad_values = carry
        keys = kn[pl.ds(key_start, tile_k), :]
        values = vn[pl.ds(key_start, tile_k), :]
        cols = pl.ds(query_start, width)
        for head in range(2):
            rows = slice(head * HEAD_DIM, (head + 1) * HEAD_DIM)
            scores = dot(keys, qz[head, :, cols])
            if masked:
                scores = causal(scores)
            probs = jnp.exp(scores - lse_ref[0, head : head + 1, cols])
            grad_probs = dot(values, gz[head, :, cols])
            grad_scores = (probs * (grad_probs - inner[head : head + 1, cols])).astype(BF16)
            grad_values = grad_values + dot(probs.astype(BF16), gn[head, cols, :])
            grad_keys = grad_keys + dot(grad_scores, qn[head, cols, :])
            dq[rows, cols] += dot(kt[rows, pl.ds(key_start, tile_k)], grad_scores)
        return (grad_keys, grad_values)

    def one(number, _):
        base = pl.multiple_of(number * tile_q, tile_q)
        for sub in range(steps):
            skip = sub * tile_k
            key_start = pl.multiple_of(base + skip, tile_k)
            carry = (jnp.zeros((tile_k, PAIR), F32), jnp.zeros((tile_k, PAIR), F32))
            carry = tile(key_start, key_start, tile_q - skip, True, carry)

            def body(step, carry):
                return tile(
                    key_start, pl.multiple_of(step * tile_q, tile_q), tile_q, False, carry
                )

            carry = lax.fori_loop(number + 1, length // tile_q, body, carry)
            dk[pl.ds(key_start, tile_k), :] = carry[0]
            dv[pl.ds(key_start, tile_k), :] = carry[1]
        return 0

    lax.fori_loop(0, length // tile_q, one, 0)
    half = HEAD_DIM // 2
    for source in range(count):
        for slot in range(slots):
            cols = pl.ds(pl.multiple_of(order[source * slots + slot] * tok, tok), tok)
            take = slice(slot * tok, (slot + 1) * tok)
            cosine = cos_ref[:, cols]
            sine = sin_ref[:, cols]
            for which, grad in enumerate((dq[:, cols] * (HEAD_DIM**-0.5), dk[cols, :].T)):
                for head in range(2):
                    low = head * HEAD_DIM
                    first = grad[low : low + half]
                    second = grad[low + half : low + 2 * half]
                    outs[source][which, low : low + half, take] = (
                        first * cosine + second * sine
                    ).astype(BF16)
                    outs[source][which, low + half : low + 2 * half, take] = (
                        second * cosine - first * sine
                    ).astype(BF16)
            outs[source][2, :, take] = dv[cols, :].T.astype(BF16)


def attend_back(pieces, mixes, grads, lse, cosine, sine, order, slots):
    count = len(pieces)
    width, span = pieces[0].shape[1:]
    tok = span // slots
    length = count * span
    pairs = width // PAIR
    tile_q = min(512, length)
    tile_k = min(256, length)
    triple = pl.BlockSpec((3, PAIR, span), lambda p, o: (0, p, 0))
    single = pl.BlockSpec((PAIR, span), lambda p, o: (p, 0))
    table = pl.BlockSpec((HEAD_DIM // 2, length), lambda p, o: (0, 0))
    grid_spec = pltpu.PrefetchScalarGridSpec(
        num_scalar_prefetch=1,
        grid=(pairs,),
        in_specs=[triple] * count
        + [single] * (2 * count)
        + [pl.BlockSpec((1, 8, length), lambda p, o: (p, 0, 0)), table, table],
        out_specs=[triple] * count,
        scratch_shapes=[
            pltpu.VMEM((2, PAIR, length), BF16),
            pltpu.VMEM((2, PAIR, length), BF16),
            pltpu.VMEM((2, length, PAIR), BF16),
            pltpu.VMEM((2, length, PAIR), BF16),
            pltpu.VMEM((length, PAIR), BF16),
            pltpu.VMEM((length, PAIR), BF16),
            pltpu.VMEM((PAIR, length), BF16),
            pltpu.VMEM((8, length), F32),
            pltpu.VMEM((PAIR, length), F32),
            pltpu.VMEM((length, PAIR), F32),
            pltpu.VMEM((length, PAIR), F32),
        ],
    )
    area = pairs * 2 * length * length // 2
    return pl.pallas_call(
        functools.partial(attend_back_kernel, count, slots, tok, tile_q, tile_k),
        out_shape=[jax.ShapeDtypeStruct((3, width, span), BF16)] * count,
        grid_spec=grid_spec,
        compiler_params=pltpu.CompilerParams(
            dimension_semantics=("arbitrary",), vmem_limit_bytes=56 * MIB
        ),
        cost_estimate=pl.CostEstimate(
            flops=area * 2560, bytes_accessed=16 * width * length, transcendentals=area
        ),
        name="attend_back",
    )(order, *pieces, *mixes, *grads, lse, cosine, sine)


def nt(a, b):
    return lax.dot_general(a, b, (((1,), (1,)), ((), ())), preferred_element_type=F32)


def whole_block(shape):
    zeros = (0,) * len(shape)
    return pl.BlockSpec(shape, lambda *_: zeros)


def parameters(mib):
    return pltpu.CompilerParams(dimension_semantics=("arbitrary",), vmem_limit_bytes=mib * MIB)


def project_kernel(slots, tok, count, rows, place, *refs):
    xs, firsts = refs[:slots], refs[slots : 2 * slots]
    own = refs[2 * slots : 2 * slots + count]
    other = refs[2 * slots + count : 2 * slots + 2 * count]
    cos_ref, sin_ref = refs[2 * slots + 2 * count : 2 * slots + 2 * count + 2]
    other_ref, own_ref, normed_ref, full_ref, gains_ref, column = refs[2 * slots + 2 * count + 2 :]
    step = pl.program_id(0)
    target, kind = step // 3, step % 3
    core = place[1]
    half = jnp.where(target == 0, 1 - core, core)
    depth = normed_ref.shape[1]
    wide = own_ref.shape[1]

    @pl.when(step == 0)
    def _():
        for number in range(count):
            at = pl.ds(pl.multiple_of(place[2 + number] * rows, rows), rows)
            for which in range(3):
                columns = slice(which * wide, (which + 1) * wide)
                full_ref[core, which, at, :] = own[number][:, columns]
                full_ref[1 - core, which, at, :] = other[number][:, columns]
            column[at, :] = own[number][:, 3 * wide :]
        gains_ref[...] = column[...].T[:8].astype(F32)
        gain = gains_ref[0:1, :]
        for slot in range(slots):
            values = xs[slot][...].reshape(tok, depth).astype(F32)
            scale = lax.rsqrt(jnp.mean(values * values, axis=1, keepdims=True) + epsilon)
            normed_ref[slot * tok : (slot + 1) * tok, :] = (values * scale * gain).astype(BF16)

    weight = full_ref[half, kind]
    raw = nt(weight.T, normed_ref[...])

    def store(value):
        @pl.when(target == 0)
        def _():
            other_ref[0] = value

        @pl.when(target == 1)
        def _():
            own_ref[0] = value

    @pl.when(kind < 2)
    def _():
        parts = raw.reshape(wide // HEAD_DIM, 2, HALF, raw.shape[1])
        first, second = parts[:, 0], parts[:, 1]
        cosine, sine = cos_ref[...][None], sin_ref[...][None]
        turned = jnp.stack(
            [first * cosine - second * sine, first * sine + second * cosine], axis=1
        )
        store(turned.reshape(raw.shape).astype(BF16))

    @pl.when(kind == 2)
    def _():
        first = jnp.concatenate(
            [ref[...].reshape(tok, wide).T.astype(F32) for ref in firsts], axis=1
        )
        store((0.5 * raw + 0.5 * first).astype(BF16))


def project(inputs, received, firsts, firsts_received, own, other, cosine, sine, place):
    slots, tok, depth = inputs.shape
    count, rows = len(own), own[0].shape[0]
    wide = depth // 2
    span = slots * tok

    def half(s, p):
        return jnp.where(s < 3, 1 - p[1], p[1])

    x_specs = [pl.BlockSpec((1, tok, depth), lambda s, p: (p[0], 0, 0))]
    x_specs += [whole_block((tok, depth))] * (slots - 1)
    first_specs = [pl.BlockSpec((1, tok, wide), lambda s, p: (p[0], 0, half(s, p)))]
    first_specs += [pl.BlockSpec((tok, wide), lambda s, p: (0, half(s, p)))] * (slots - 1)
    grid_spec = pltpu.PrefetchScalarGridSpec(
        num_scalar_prefetch=1,
        grid=(6,),
        in_specs=x_specs
        + first_specs
        + [whole_block(own[0].shape)] * (2 * count)
        + [whole_block((HALF, span))] * 2,
        out_specs=[
            pl.BlockSpec((1, wide, span), lambda s, p: (jnp.minimum(s, 2), 0, 0)),
            pl.BlockSpec((1, wide, span), lambda s, p: (jnp.maximum(s - 3, 0), 0, 0)),
            whole_block((span, depth)),
            whole_block((2, 3, depth, wide)),
            whole_block((8, depth)),
        ],
        scratch_shapes=[pltpu.VMEM((depth, 128), BF16)],
    )
    return pl.pallas_call(
        functools.partial(project_kernel, slots, tok, count, rows),
        out_shape=[
            jax.ShapeDtypeStruct((3, wide, span), BF16),
            jax.ShapeDtypeStruct((3, wide, span), BF16),
            jax.ShapeDtypeStruct((span, depth), BF16),
            jax.ShapeDtypeStruct((2, 3, depth, wide), BF16),
            jax.ShapeDtypeStruct((8, depth), F32),
        ],
        grid_spec=grid_spec,
        compiler_params=parameters(56),
        cost_estimate=pl.CostEstimate(
            flops=6 * span * depth * depth,
            bytes_accessed=2 * (8 * span * depth + 6 * depth * depth),
            transcendentals=0,
        ),
        name="project",
    )(place, inputs, *received, firsts, *firsts_received, *own, *other, cosine, sine)


def output_kernel(slots, tok, count, rows, place, *refs):
    xs = refs[:slots]
    own = refs[slots : slots + count]
    other = refs[slots + count : slots + 2 * count]
    att_other, att_own, gains_ref = refs[slots + 2 * count : slots + 2 * count + 3]
    middle_ref, normed_ref, full_ref = refs[slots + 2 * count + 3 :]
    step = pl.program_id(0)
    core = place[1]
    wide = att_own.shape[0]
    depth = 2 * wide
    mine = pl.ds(pl.multiple_of(core * wide, wide), wide)
    others = pl.ds(pl.multiple_of((1 - core) * wide, wide), wide)

    @pl.when(step == 0)
    def _():
        for number in range(count):
            at = pl.ds(pl.multiple_of(place[2 + number] * rows, rows), rows)
            full_ref[at, mine] = own[number][...]
            full_ref[at, others] = other[number][...]

    total = dot(att_own[...].T, full_ref[mine, :]) + dot(att_other[...].T, full_ref[others, :])
    for slot in range(slots):

        @pl.when(step == slot)
        def _(slot=slot):
            middle_ref[...] = xs[slot][...].reshape(tok, depth).astype(F32) + total

    middle = middle_ref[...]
    scale = lax.rsqrt(jnp.mean(middle * middle, axis=1, keepdims=True) + epsilon)
    normed_ref[...] = (middle * scale * gains_ref[1:2, :]).astype(BF16)


def output_projection(inputs, received, own, other, att_other, att_own, gains, place):
    slots, tok, depth = inputs.shape
    count, rows = len(own), own[0].shape[0]
    wide = depth // 2
    span = slots * tok
    x_specs = [pl.BlockSpec((1, tok, depth), lambda s, p: (p[0], 0, 0))]
    x_specs += [whole_block((tok, depth))] * (slots - 1)
    grid_spec = pltpu.PrefetchScalarGridSpec(
        num_scalar_prefetch=1,
        grid=(slots,),
        in_specs=x_specs
        + [whole_block(own[0].shape)] * (2 * count)
        + [pl.BlockSpec((wide, tok), lambda s, p: (0, s))] * 2
        + [whole_block((8, depth))],
        out_specs=[
            pl.BlockSpec((tok, depth), lambda s, p: (s, 0)),
            pl.BlockSpec((tok, depth), lambda s, p: (s, 0)),
            whole_block((depth, depth)),
        ],
    )
    return pl.pallas_call(
        functools.partial(output_kernel, slots, tok, count, rows),
        out_shape=[
            jax.ShapeDtypeStruct((span, depth), F32),
            jax.ShapeDtypeStruct((span, depth), BF16),
            jax.ShapeDtypeStruct((depth, depth), BF16),
        ],
        grid_spec=grid_spec,
        compiler_params=parameters(56),
        cost_estimate=pl.CostEstimate(
            flops=2 * span * depth * depth,
            bytes_accessed=12 * span * depth + 4 * depth * depth,
            transcendentals=0,
        ),
        name="output_projection",
    )(place, inputs, *received, *own, *other, att_other, att_own, gains)


def mlp_kernel(slots, tok, count, rows, down_rows, blocks, place, *refs):
    grads = refs[:slots]
    middle_ref, normed_ref, gains_ref = refs[slots : slots + 3]
    base = slots + 3
    own_g, other_g, own_u, other_u, own_d, other_d = (
        refs[base + number * count : base + (number + 1) * count] for number in range(6)
    )
    (
        out_ref,
        send_ref,
        grad_ref,
        low_ref,
        gain_ref,
        gu_send,
        gu_keep,
        d_send,
        d_keep,
        wgu,
        wd,
        og,
        normed_t,
        acc,
        back,
        sems,
    ) = refs[base + 6 * count :]
    step = pl.program_id(0)
    core = place[1]
    depth = og.shape[1]
    wide = depth // 2
    strip = 128
    half_width = blocks * strip
    mine = pl.ds(pl.multiple_of(core * wide, wide), wide)
    others = pl.ds(pl.multiple_of((1 - core) * wide, wide), wide)

    def loads():
        copies = []
        for number in range(count):
            at = pl.ds(pl.multiple_of(place[2 + number] * rows, rows), rows)
            for which, (gate, up) in enumerate(((own_g, own_u), (other_g, other_u))):
                copies.append((gate[number], wgu.at[which, at, pl.ds(0, half_width)]))
                copies.append((up[number], wgu.at[which, at, pl.ds(half_width, half_width)]))
        for number in range(count):
            at = pl.ds(pl.multiple_of(place[2 + number] * down_rows, down_rows), down_rows)
            copies.append((own_d[number], wd.at[at, mine]))
            copies.append((other_d[number], wd.at[at, others]))
        return [
            pltpu.make_async_copy(source, target, sems.at[number])
            for number, (source, target) in enumerate(copies)
        ]

    @pl.when(step == 0)
    def _():
        copies = loads()
        for copy in copies:
            copy.start()
        for slot in range(slots):
            og[slot * tok : (slot + 1) * tok, :] = grads[slot][...].reshape(tok, depth)
        normed_t[...] = normed_ref[...].T
        acc[...] = jnp.zeros_like(acc)
        back[...] = jnp.zeros_like(back)
        for copy in copies:
            copy.wait()

    at = pl.ds(pl.multiple_of(step * strip, strip), strip)
    up_at = pl.ds(pl.multiple_of(half_width + step * strip, strip), strip)
    gate_w = jnp.concatenate([wgu[0, :, at], wgu[1, :, at]], axis=1)
    up_w = jnp.concatenate([wgu[0, :, up_at], wgu[1, :, up_at]], axis=1)
    own_rows = pl.ds(pl.multiple_of(core * half_width + step * strip, strip), strip)
    other_rows = pl.ds(pl.multiple_of((1 - core) * half_width + step * strip, strip), strip)
    down_w = jnp.concatenate([wd[own_rows, :], wd[other_rows, :]], axis=0)
    normed = normed_ref[...]
    gate = dot(normed, gate_w)
    up = dot(normed, up_w)
    grad_active = nt(og[...], down_w)
    sigma = jax.nn.sigmoid(gate)
    silu = gate * sigma
    active = (silu * up).astype(BF16)
    grad_up = (grad_active * silu).astype(BF16)
    grad_gate = (grad_active * up * sigma * (1.0 + gate * (1.0 - sigma))).astype(BF16)
    acc[...] += dot(active, down_w)
    back[...] += nt(grad_gate, gate_w) + nt(grad_up, up_w)
    grad_gate_w = dot(normed_t[...], grad_gate).astype(BF16)
    gu_keep[0] = grad_gate_w[:, :strip]
    gu_send[0] = grad_gate_w[:, strip:]
    grad_up_w = dot(normed_t[...], grad_up).astype(BF16)
    gu_keep[1] = grad_up_w[:, :strip]
    gu_send[1] = grad_up_w[:, strip:]
    active_t = active.T
    kept = dot(active_t, og[:, mine]).astype(BF16)
    sent = dot(active_t, og[:, others]).astype(BF16)
    d_keep[core] = kept[:strip]
    d_keep[1 - core] = kept[strip:]
    d_send[core] = sent[:strip]
    d_send[1 - core] = sent[strip:]

    @pl.when(step == blocks - 1)
    def _():
        gain = gains_ref[1:2, :]
        chunk = min(128, tok)
        gain_ref[...] = jnp.zeros_like(gain_ref)
        for slot in range(slots):

            def finish(number, _, slot=slot):
                local = pl.ds(pl.multiple_of(number * chunk, chunk), chunk)
                some = pl.ds(pl.multiple_of(slot * tok + number * chunk, chunk), chunk)
                middle = middle_ref[some, :]
                scale = lax.rsqrt(jnp.mean(middle * middle, axis=1, keepdims=True) + epsilon)
                result = middle + acc[some, :]
                if slot == 0:
                    out_ref[0, local, :] = result
                else:
                    send_ref[pl.ds(pl.multiple_of((slot - 1) * tok + number * chunk, chunk), chunk), :] = (
                        result.astype(BF16)
                    )
                grad = back[some, :]
                gain_ref[0:1, :] += jnp.sum(grad * middle * scale, axis=0, keepdims=True)
                weighted = grad * gain
                inner = jnp.mean(weighted * middle, axis=1, keepdims=True)
                grad_middle = (
                    scale * weighted
                    - middle * (scale * scale * scale) * inner
                    + og[some, :].astype(F32)
                )
                grad_ref[some, :] = grad_middle
                low_ref[some, :] = grad_middle.astype(BF16)
                return 0

            lax.fori_loop(0, tok // chunk, finish, 0)


def mlp(grads, grads_received, middle, normed, gains, gate, up, down, place):
    slots, tok, depth = grads.shape
    own_d, other_d = down
    count, rows = len(own_d), gate[0][0].shape[0]
    down_rows = own_d[0].shape[0]
    half_width = gate[0][0].shape[1]
    wide = depth // 2
    span = slots * tok
    blocks = half_width // 128
    once = pl.Buffered(1)
    g_specs = [pl.BlockSpec((1, tok, depth), lambda s, p: (p[0], 0, 0), pipeline_mode=once)]
    g_specs += [pl.BlockSpec((tok, depth), lambda s, p: (0, 0), pipeline_mode=once)] * (slots - 1)
    gu_spec = pl.BlockSpec((2, depth, 128), lambda s, p: (0, 0, s))
    d_spec = pl.BlockSpec((2, 128, wide), lambda s, p: (0, s, 0))
    grid_spec = pltpu.PrefetchScalarGridSpec(
        num_scalar_prefetch=1,
        grid=(blocks,),
        in_specs=g_specs
        + [
            pl.BlockSpec((span, depth), lambda s, p: (0, 0), pipeline_mode=once),
            pl.BlockSpec((span, depth), lambda s, p: (0, 0), pipeline_mode=once),
            whole_block((8, depth)),
        ]
        + [pl.BlockSpec(memory_space=pl.ANY)] * (6 * count),
        out_specs=[
            pl.BlockSpec((1, tok, depth), lambda s, p: (p[0], 0, 0), pipeline_mode=once),
            pl.BlockSpec(((slots - 1) * tok, depth), lambda s, p: (0, 0), pipeline_mode=once),
            pl.BlockSpec((span, depth), lambda s, p: (0, 0), pipeline_mode=once),
            pl.BlockSpec((span, depth), lambda s, p: (0, 0), pipeline_mode=once),
            whole_block((8, depth)),
            gu_spec,
            gu_spec,
            d_spec,
            d_spec,
        ],
        scratch_shapes=[
            pltpu.VMEM((2, depth, 2 * half_width), BF16),
            pltpu.VMEM((2 * half_width, depth), BF16),
            pltpu.VMEM((span, depth), BF16),
            pltpu.VMEM((depth, span), BF16),
            pltpu.VMEM((span, depth), F32),
            pltpu.VMEM((span, depth), F32),
            pltpu.SemaphoreType.DMA((6 * count,)),
        ],
    )
    return pl.pallas_call(
        functools.partial(mlp_kernel, slots, tok, count, rows, down_rows, blocks),
        out_shape=[
            jax.ShapeDtypeStruct((slots, tok, depth), F32),
            jax.ShapeDtypeStruct(((slots - 1) * tok, depth), BF16),
            jax.ShapeDtypeStruct((span, depth), F32),
            jax.ShapeDtypeStruct((span, depth), BF16),
            jax.ShapeDtypeStruct((8, depth), F32),
            jax.ShapeDtypeStruct((2, depth, half_width), BF16),
            jax.ShapeDtypeStruct((2, depth, half_width), BF16),
            jax.ShapeDtypeStruct((2, half_width, wide), BF16),
            jax.ShapeDtypeStruct((2, half_width, wide), BF16),
        ],
        grid_spec=grid_spec,
        compiler_params=parameters(63),
        cost_estimate=pl.CostEstimate(
            flops=16 * span * depth * 2 * half_width,
            bytes_accessed=24 * depth * half_width + 20 * span * depth,
            transcendentals=2 * span * half_width,
        ),
        name="mlp",
    )(
        place,
        grads,
        *grads_received,
        middle,
        normed,
        gains,
        *gate[0],
        *gate[1],
        *up[0],
        *up[1],
        *own_d,
        *other_d,
    )


def grad_attended_kernel(place, low_ref, full_ref, att_other, att_own, ga_other, ga_own, sent, kept):
    step = pl.program_id(0)
    core = place[1]
    wide = att_own.shape[0]
    mine = pl.ds(pl.multiple_of(core * wide, wide), wide)
    others = pl.ds(pl.multiple_of((1 - core) * wide, wide), wide)
    for number, (att, result) in enumerate(((att_other, ga_other), (att_own, ga_own))):

        @pl.when(step == number)
        def _(att=att, result=result):
            result[...] = nt(full_ref[...], low_ref[...]).astype(BF16)
            kept[...] = dot(att[...], low_ref[:, mine]).astype(BF16)
            sent[...] = dot(att[...], low_ref[:, others]).astype(BF16)


def grad_attended(low, full, att_other, att_own, place):
    span, depth = low.shape
    wide = depth // 2

    def half(s, p):
        return jnp.where(s == 0, 1 - p[1], p[1])

    row_spec = pl.BlockSpec((wide, wide), lambda s, p: (half(s, p), 0))
    grid_spec = pltpu.PrefetchScalarGridSpec(
        num_scalar_prefetch=1,
        grid=(2,),
        in_specs=[
            whole_block((span, depth)),
            pl.BlockSpec((wide, depth), lambda s, p: (half(s, p), 0)),
            whole_block((wide, span)),
            whole_block((wide, span)),
        ],
        out_specs=[whole_block((wide, span)), whole_block((wide, span)), row_spec, row_spec],
    )
    return pl.pallas_call(
        grad_attended_kernel,
        out_shape=[
            jax.ShapeDtypeStruct((wide, span), BF16),
            jax.ShapeDtypeStruct((wide, span), BF16),
            jax.ShapeDtypeStruct((depth, wide), BF16),
            jax.ShapeDtypeStruct((depth, wide), BF16),
        ],
        grid_spec=grid_spec,
        compiler_params=parameters(48),
        cost_estimate=pl.CostEstimate(
            flops=4 * span * depth * depth,
            bytes_accessed=6 * span * depth + 4 * depth * depth,
            transcendentals=0,
        ),
        name="grad_attended",
    )(place, low, full, att_other, att_own)


def tail_kernel(slots, tok, place, *refs):
    xs = refs[:slots]
    (
        back_other,
        back_own,
        full_ref,
        normed_ref,
        grad_ref,
        gains_ref,
        mlp_gain_ref,
        out_ref,
        send_ref,
        first_ref,
        first_send,
        gain_ref,
        sent,
        kept,
        normed_t,
        acc,
    ) = refs[slots:]
    step = pl.program_id(0)
    target, kind = step // 3, step % 3
    depth = acc.shape[1]

    @pl.when(step == 0)
    def _():
        normed_t[...] = normed_ref[...].T
        acc[...] = jnp.zeros_like(acc)

    def part(back, result):
        grad = back[0]

        @pl.when(kind == 2)
        def _():
            rows = 0.5 * grad.astype(F32).T
            first_ref[0] = rows[:tok]
            first_send[...] = rows[tok:].astype(BF16)

        grad = grad * jnp.where(kind == 2, 0.5, 1.0).astype(BF16)
        acc[...] += nt(grad.T, full_ref[0, 0])
        result[0] = nt(normed_t[...], grad).astype(BF16)

    @pl.when(target == 0)
    def _():
        part(back_other, sent)

    @pl.when(target == 1)
    def _():
        part(back_own, kept)

    @pl.when(step == 5)
    def _():
        gain = gains_ref[0:1, :]
        chunk = min(128, tok)
        gain_ref[...] = jnp.zeros_like(gain_ref)
        gain_ref[1:2, :] = mlp_gain_ref[0:1, :]
        for slot in range(slots):

            def finish(number, _, slot=slot):
                local = pl.ds(pl.multiple_of(number * chunk, chunk), chunk)
                some = pl.ds(pl.multiple_of(slot * tok + number * chunk, chunk), chunk)
                if slot == 0:
                    values = xs[slot][0, local, :].astype(F32)
                else:
                    values = xs[slot][local, :].astype(F32)
                scale = lax.rsqrt(jnp.mean(values * values, axis=1, keepdims=True) + epsilon)
                grad = acc[some, :]
                gain_ref[0:1, :] += jnp.sum(grad * values * scale, axis=0, keepdims=True)
                weighted = grad * gain
                inner = jnp.mean(weighted * values, axis=1, keepdims=True)
                result = (
                    scale * weighted
                    - values * (scale * scale * scale) * inner
                    + grad_ref[some, :]
                )
                if slot == 0:
                    out_ref[0, local, :] = result
                else:
                    send_ref[pl.ds(pl.multiple_of((slot - 1) * tok + number * chunk, chunk), chunk), :] = (
                        result.astype(BF16)
                    )
                return 0

            lax.fori_loop(0, tok // chunk, finish, 0)


def tail(inputs, received, back_other, back_own, full, normed, grad_middle, gains, mlp_gain, place):
    slots, tok, depth = inputs.shape
    wide = depth // 2
    span = slots * tok
    rest = (slots - 1) * tok
    once = pl.Buffered(1)

    def half(s, p):
        return jnp.where(s < 3, 1 - p[1], p[1])

    x_specs = [pl.BlockSpec((1, tok, depth), lambda s, p: (p[0], 0, 0))]
    x_specs += [whole_block((tok, depth))] * (slots - 1)
    grid_spec = pltpu.PrefetchScalarGridSpec(
        num_scalar_prefetch=1,
        grid=(6,),
        in_specs=x_specs
        + [
            pl.BlockSpec((1, wide, span), lambda s, p: (jnp.minimum(s, 2), 0, 0)),
            pl.BlockSpec((1, wide, span), lambda s, p: (jnp.maximum(s - 3, 0), 0, 0)),
            pl.BlockSpec((1, 1, depth, wide), lambda s, p: (half(s, p), s % 3, 0, 0)),
            whole_block((span, depth)),
            pl.BlockSpec((span, depth), lambda s, p: (0, 0), pipeline_mode=once),
            whole_block((8, depth)),
            whole_block((8, depth)),
        ],
        out_specs=[
            pl.BlockSpec((1, tok, depth), lambda s, p: (p[0], 0, 0)),
            whole_block((rest, depth)),
            pl.BlockSpec((1, tok, wide), lambda s, p: (p[0], 0, half(s, p))),
            pl.BlockSpec((rest, wide), lambda s, p: (0, half(s, p))),
            whole_block((8, depth)),
            pl.BlockSpec((1, depth, wide), lambda s, p: (jnp.minimum(s, 2), 0, 0)),
            pl.BlockSpec((1, depth, wide), lambda s, p: (jnp.maximum(s - 3, 0), 0, 0)),
        ],
        scratch_shapes=[pltpu.VMEM((depth, span), BF16), pltpu.VMEM((span, depth), F32)],
    )
    return pl.pallas_call(
        functools.partial(tail_kernel, slots, tok),
        out_shape=[
            jax.ShapeDtypeStruct((slots, tok, depth), F32),
            jax.ShapeDtypeStruct((rest, depth), BF16),
            jax.ShapeDtypeStruct((slots, tok, depth), F32),
            jax.ShapeDtypeStruct((rest, depth), BF16),
            jax.ShapeDtypeStruct((8, depth), F32),
            jax.ShapeDtypeStruct((3, depth, wide), BF16),
            jax.ShapeDtypeStruct((3, depth, wide), BF16),
        ],
        grid_spec=grid_spec,
        compiler_params=parameters(60),
        cost_estimate=pl.CostEstimate(
            flops=12 * span * depth * depth,
            bytes_accessed=24 * span * depth + 12 * depth * depth,
            transcendentals=0,
        ),
        name="tail",
    )(
        place, inputs, *received, back_other, back_own, full, normed, grad_middle, gains, mlp_gain
    )


def land_kernel(place, whole_ref, part_ref, out_ref):
    out_ref[0] = part_ref[...].astype(F32)


def land(whole, part, slot):
    _, tok, depth = whole.shape
    tile = min(256, tok)
    grid_spec = pltpu.PrefetchScalarGridSpec(
        num_scalar_prefetch=1,
        grid=(tok // tile,),
        in_specs=[
            pl.BlockSpec(memory_space=pl.ANY),
            pl.BlockSpec((tile, depth), lambda s, p: (s, 0)),
        ],
        out_specs=pl.BlockSpec((1, tile, depth), lambda s, p: (p[0], s, 0)),
    )
    return pl.pallas_call(
        land_kernel,
        out_shape=jax.ShapeDtypeStruct(whole.shape, F32),
        grid_spec=grid_spec,
        input_output_aliases={1: 0},
        compiler_params=parameters(16),
        cost_estimate=pl.CostEstimate(
            flops=tok * depth, bytes_accessed=6 * tok * depth, transcendentals=0
        ),
        name="land",
    )(slot, whole, part)


MESH = pl.DeviceIdType.MESH


def seats():
    shard = lax.axis_index("fsdp")
    seat = lax.axis_index("seq")
    return (shard // 2, shard % 2, seat // 2, seat % 2)


def meet(line, keys):
    shard = lax.axis_index("fsdp")
    seat = lax.axis_index("seq")
    partners = []
    if "z" in keys:
        partners += [{"fsdp": lax.rem(shard + 2 * jump, 2 * line)} for jump in range(1, line)]
    if "y" in keys:
        partners.append({"fsdp": shard + 1 - 2 * (shard % 2)})
    if "x" in keys:
        partners.append({"seq": lax.rem(seat + 2, 4)})
    if "core" in keys:
        partners.append({"seq": seat + 1 - 2 * (seat % 2)})
    barrier = pltpu.get_barrier_semaphore()
    for partner in partners:
        pl.semaphore_signal(barrier, inc=1, device_id=partner, device_id_type=MESH)
    pl.semaphore_wait(barrier, len(partners))


def send(source, target, sems, number, partner):
    return pltpu.make_async_remote_copy(
        src_ref=source,
        dst_ref=target,
        send_sem=sems.at[0, number],
        recv_sem=sems.at[1, number],
        device_id=partner,
        device_id_type=MESH,
    )


def to_core_partner():
    seat = lax.axis_index("seq")
    return {"seq": seat + 1 - 2 * (seat % 2)}


def to_x_partner():
    return {"seq": lax.rem(lax.axis_index("seq") + 2, 4)}


def to_y_partner():
    shard = lax.axis_index("fsdp")
    return {"fsdp": shard + 1 - 2 * (shard % 2)}


def to_z_partner(line, jump):
    return {"fsdp": lax.rem(lax.axis_index("fsdp") + 2 * jump, 2 * line)}


class Gather:
    def __init__(self, line, shard, own, other, sems, split=False):
        self.line, self.shard, self.own, self.other = line, shard, own, other
        self.sems = sems
        z, y, x, _ = seats()
        self.z, self.y = z, y
        rows = own.shape[2]
        if split:
            self.rows = pl.ds(pl.multiple_of(x * (rows // 2), rows // 2), rows // 2)
        else:
            self.rows = pl.ds(0, rows)

    def here(self):
        return pltpu.make_async_copy(
            self.shard.at[self.rows, :],
            self.own.at[self.z, self.y, self.rows, :],
            self.sems.at[0, self.line + 2],
        )

    def along_z(self):
        return [
            send(
                self.shard.at[self.rows, :],
                self.own.at[self.z, self.y, self.rows, :],
                self.sems,
                jump - 1,
                to_z_partner(self.line, jump),
            )
            for jump in range(1, self.line)
        ]

    def along_y(self):
        part = self.own.at[:, self.y, self.rows, :]
        return send(part, part, self.sems, self.line - 1, to_y_partner())

    def along_x(self):
        part = self.own.at[:, :, self.rows, :]
        return send(part, part, self.sems, self.line, to_x_partner())

    def along_core(self):
        return send(self.own, self.other, self.sems, self.line + 1, to_core_partner())

    def start_z(self):
        self.here().start()
        for copy in self.along_z():
            copy.start()

    def wait_z(self):
        self.here().wait()
        for copy in self.along_z():
            copy.wait()


def gather_sems(line):
    return pltpu.SemaphoreType.DMA((2, line + 3))


def front_kernel(line, tok, *refs):
    (
        inputs,
        firsts,
        q_shard,
        k_shard,
        v_shard,
        o_shard,
        d_shard,
        cos_ref,
        sin_ref,
        x_received,
        f_received,
        heads_own,
        heads_received,
        normed_ref,
        full_ref,
        gains_ref,
        o_own,
        o_other,
        d_own,
        xs,
        fs,
        q_own,
        q_other,
        k_own,
        k_other,
        v_own,
        v_other,
        outgoing,
        q_sems,
        k_sems,
        v_sems,
        o_sems,
        d_sems,
        swap_sems,
        head_sems,
        local_sems,
    ) = refs
    step = pl.program_id(0)
    _, _, side, core = seats()
    wide = outgoing.shape[1]
    depth = 2 * wide
    gathers = [
        Gather(line, q_shard, q_own, q_other, q_sems),
        Gather(line, k_shard, k_own, k_other, k_sems),
        Gather(line, v_shard, v_own, v_other, v_sems),
    ]
    query, key, value = gathers
    out = Gather(line, o_shard, o_own, o_other, o_sems)
    down = Gather(line, d_shard, d_own, d_own, d_sems, split=True)
    swap_x = send(inputs.at[1 - side], x_received, swap_sems, 0, to_x_partner())
    swap_f = send(firsts.at[1 - side], f_received, swap_sems, 1, to_x_partner())
    load_x = pltpu.make_async_copy(inputs.at[side], xs.at[pl.ds(0, tok), :], local_sems.at[0])
    load_f = pltpu.make_async_copy(firsts.at[side], fs.at[pl.ds(0, tok), :], local_sems.at[1])
    more_x = pltpu.make_async_copy(x_received, xs.at[pl.ds(tok, tok), :], local_sems.at[2])
    more_f = pltpu.make_async_copy(f_received, fs.at[pl.ds(tok, tok), :], local_sems.at[3])

    def weight(halves, columns):
        return halves[:, :, :, columns].reshape(depth, wide)

    def heads(number):
        return send(
            outgoing.at[number], heads_received.at[number], head_sems, number, to_core_partner()
        )

    saves = []
    for number, (mine, others) in enumerate(((q_own, q_other), (k_own, k_other), (v_own, v_other))):
        for which, ref in ((0, mine), (1, others)):
            half = core if which == 0 else 1 - core
            saves.append(
                pltpu.make_async_copy(
                    ref.at[:, :, :, pl.ds(0, wide)],
                    full_ref.at[half, number],
                    local_sems.at[4 + 2 * number + which],
                )
            )

    @pl.when(step == 0)
    def _():
        meet(line, ("z", "y", "x", "core"))
        swap_x.start()
        load_x.start()
        load_f.start()
        query.start_z()
        query.wait_z()
        query.along_y().start()
        key.start_z()
        key.wait_z()
        key.along_y().start()
        value.start_z()
        query.along_y().wait()
        query.along_core().start()
        swap_x.wait()
        more_x.start()
        swap_f.start()
        value.wait_z()
        value.along_y().start()
        out.start_z()
        key.along_y().wait()
        key.along_core().start()
        load_x.wait()
        more_x.wait()
        value.along_y().wait()
        value.along_core().start()
        columns = v_own[:, :, :, wide:].reshape(depth, 128)
        gains_ref[...] = columns.astype(F32).T[:8]
        gain = gains_ref[0:1, :]
        chunk = min(256, 2 * tok)

        def norm(number, _):
            at = pl.ds(pl.multiple_of(number * chunk, chunk), chunk)
            values = xs[at, :].astype(F32)
            scale = lax.rsqrt(jnp.mean(values * values, axis=1, keepdims=True) + epsilon)
            normed_ref[at, :] = (values * scale * gain).astype(BF16)
            return 0

        lax.fori_loop(0, 2 * tok // chunk, norm, 0)

    @pl.when(step == 2)
    def _():
        out.wait_z()
        out.along_y().start()
        down.start_z()
        swap_f.wait()
        more_f.start()
        load_f.wait()
        more_f.wait()

    @pl.when(step == 3)
    def _():
        query.along_core().wait()
        key.along_core().wait()
        value.along_core().wait()
        for save in saves:
            save.start()

    @pl.when(step == 5)
    def _():
        out.along_y().wait()
        out.along_core().start()

    def project_one(halves, kind, mine):
        raw = nt(weight(halves, slice(0, wide)).T, normed_ref[...])
        if kind < 2:
            parts = raw.reshape(wide // HEAD_DIM, 2, HALF, raw.shape[1])
            first, second = parts[:, 0], parts[:, 1]
            cosine, sine = cos_ref[...][None], sin_ref[...][None]
            turned = jnp.stack(
                [first * cosine - second * sine, first * sine + second * cosine], axis=1
            )
            result = turned.reshape(raw.shape).astype(BF16)
        else:
            half = core if mine else 1 - core
            first = fs[:, pl.ds(pl.multiple_of(half * wide, wide), wide)]
            result = (0.5 * raw + 0.5 * first.astype(F32).T).astype(BF16)
        if mine:
            heads_own[0] = result
        else:
            outgoing[kind] = result
            heads(kind).start()

    for number, (halves, kind, mine) in enumerate(
        (
            (q_own, 0, True),
            (k_own, 1, True),
            (v_own, 2, True),
            (q_other, 0, False),
            (k_other, 1, False),
            (v_other, 2, False),
        )
    ):

        @pl.when(step == number)
        def _(halves=halves, kind=kind, mine=mine):
            project_one(halves, kind, mine)

    @pl.when(step == 5)
    def _():
        for number in range(3):
            heads(number).wait()
        for save in saves:
            save.wait()
        out.along_core().wait()
        down.wait_z()


def front(inputs, firsts, q, k, v, o, d, cosine, sine, line):
    slots, tok, depth = inputs.shape
    span = slots * tok
    wide = depth // 2
    rows, down_rows = q.shape[0], d.shape[0]
    anywhere = pl.BlockSpec(memory_space=pl.ANY)
    weights = lambda columns: pltpu.VMEM((line, 2, rows, columns), BF16)
    return pl.pallas_call(
        functools.partial(front_kernel, line, tok),
        grid=(6,),
        in_specs=[anywhere] * 7 + [whole_block((HALF, span))] * 2,
        out_specs=[
            anywhere,
            anywhere,
            pl.BlockSpec((1, wide, span), lambda s: (jnp.minimum(s, 2), 0, 0)),
            anywhere,
            whole_block((span, depth)),
            anywhere,
            whole_block((8, depth)),
            anywhere,
            anywhere,
            anywhere,
        ],
        out_shape=[
            jax.ShapeDtypeStruct((tok, depth), BF16),
            jax.ShapeDtypeStruct((tok, depth), BF16),
            jax.ShapeDtypeStruct((3, wide, span), BF16),
            jax.ShapeDtypeStruct((3, wide, span), BF16),
            jax.ShapeDtypeStruct((span, depth), BF16),
            jax.ShapeDtypeStruct((2, 3, line, 2, rows, wide), BF16),
            jax.ShapeDtypeStruct((8, depth), F32),
            jax.ShapeDtypeStruct((line, 2, rows, wide), BF16),
            jax.ShapeDtypeStruct((line, 2, rows, wide), BF16),
            jax.ShapeDtypeStruct((line, 2, down_rows, wide), BF16),
        ],
        scratch_shapes=[
            pltpu.VMEM((span, depth), BF16),
            pltpu.VMEM((span, depth), BF16),
            weights(wide),
            weights(wide),
            weights(wide),
            weights(wide),
            weights(v.shape[1]),
            weights(v.shape[1]),
            pltpu.VMEM((3, wide, span), BF16),
        ]
        + [gather_sems(line)] * 5
        + [
            pltpu.SemaphoreType.DMA((2, 2)),
            pltpu.SemaphoreType.DMA((2, 3)),
            pltpu.SemaphoreType.DMA((10,)),
        ],
        compiler_params=pltpu.CompilerParams(
            dimension_semantics=("arbitrary",),
            vmem_limit_bytes=56 * MIB,
            collective_id=1,
            has_side_effects=True,
        ),
        cost_estimate=pl.CostEstimate(
            flops=6 * span * depth * depth,
            bytes_accessed=2 * (8 * span * depth + 6 * depth * depth),
            transcendentals=0,
        ),
        name="front",
    )(inputs, firsts, q, k, v, o, d, cosine, sine)


def block_of(source, slot, tok):
    _, _, side, core = seats()
    rank = 1 - core if source == 0 else core
    group = lax.rem(side + slot, 2)
    return pl.ds(pl.multiple_of((group * 2 + rank) * tok, tok), tok)


def attend_carry_kernel(line, tok, tile_k, *refs):
    (
        received,
        own,
        grad_in,
        d_in,
        g_shard,
        u_shard,
        mix_received,
        mix_own,
        lse_ref,
        att_other,
        grad_received,
        d_own,
        d_other,
        g_own,
        g_other,
        u_own,
        u_other,
        qz,
        kn,
        vt,
        ot,
        outgoing,
        d_sems,
        g_sems,
        u_sems,
        swap_sems,
        att_sems,
    ) = refs
    step = pl.program_id(0)
    pairs = pl.num_programs(0)
    _, _, side, _ = seats()
    down = Gather(line, d_in, d_own, d_other, d_sems, split=True)
    gate = Gather(line, g_shard, g_own, g_other, g_sems, split=True)
    up = Gather(line, u_shard, u_own, u_other, u_sems)
    swap = send(grad_in.at[1 - side], grad_received, swap_sems, 0, to_x_partner())
    pieces = (received, own)

    def hand_over(number):
        rows = pl.ds(number * PAIR, PAIR)
        return send(
            outgoing.at[rows, :], att_other.at[rows, :], att_sems, number, to_core_partner()
        )

    @pl.when(step == 0)
    def _():
        meet(line, ("z", "y", "x", "core"))
        down.along_y().start()
        gate.start_z()
        swap.start()

    @pl.when(step == 2)
    def _():
        gate.wait_z()
        gate.along_y().start()
        up.start_z()

    @pl.when(step == 3)
    def _():
        down.along_y().wait()
        down.along_x().start()

    for source in range(2):
        for slot in range(2):
            cols = block_of(source, slot, tok)
            take = slice(slot * tok, (slot + 1) * tok)
            query = pieces[source][0, :, take] * jnp.asarray(HEAD_DIM**-0.5, BF16)
            for head in range(2):
                qz[head, :, cols] = head_rows(query, head)
            kn[cols, :] = pieces[source][1, :, take].T
            vt[:, cols] = pieces[source][2, :, take]
    attend_body(4 * tok, tile_k, qz, kn, vt, ot, lse_ref)
    for slot in range(2):
        take = slice(slot * tok, (slot + 1) * tok)
        theirs = ot[:, block_of(0, slot, tok)]
        mix_received[:, take] = theirs
        for number in range(4):

            @pl.when(step == number)
            def _(number=number, theirs=theirs, take=take):
                outgoing[number * PAIR : (number + 1) * PAIR, take] = theirs

        mix_own[:, take] = ot[:, block_of(1, slot, tok)]
    for number in range(4):

        @pl.when(step == number)
        def _(number=number):
            hand_over(number).start()

    @pl.when(step == pairs - 1)
    def _():
        gate.along_y().wait()
        up.wait_z()
        up.along_y().start()
        down.along_x().wait()
        swap.wait()
        gate.along_x().start()
        down.along_core().start()
        up.along_y().wait()
        up.along_core().start()
        gate.along_x().wait()
        gate.along_core().start()
        for number in range(4):
            hand_over(number).wait()
        down.along_core().wait()
        up.along_core().wait()
        gate.along_core().wait()


def attend_carry(received, own, grads, d_own, gate, up, line):
    _, width, span = own.shape
    tok = span // 2
    length = 2 * span
    pairs = width // PAIR
    rows, down_rows = gate.shape[0], d_own.shape[2]
    depth = grads.shape[2]
    anywhere = pl.BlockSpec(memory_space=pl.ANY)
    triple = pl.BlockSpec((3, PAIR, span), lambda p: (0, p, 0))
    single = pl.BlockSpec((PAIR, span), lambda p: (p, 0))
    whole_gate = jax.ShapeDtypeStruct((line, 2, rows, gate.shape[1]), BF16)
    whole_down = jax.ShapeDtypeStruct((line, 2, down_rows, d_own.shape[3]), BF16)
    area = pairs * 2 * length * length // 2
    return pl.pallas_call(
        functools.partial(attend_carry_kernel, line, tok, min(256, length)),
        grid=(pairs,),
        in_specs=[triple, triple] + [anywhere] * 4,
        out_specs=[single, single, pl.BlockSpec((1, 8, length), lambda p: (p, 0, 0))]
        + [anywhere] * 8,
        out_shape=[
            jax.ShapeDtypeStruct((width, span), BF16),
            jax.ShapeDtypeStruct((width, span), BF16),
            jax.ShapeDtypeStruct((pairs, 8, length), F32),
            jax.ShapeDtypeStruct((width, span), BF16),
            jax.ShapeDtypeStruct((tok, depth), BF16),
            whole_down,
            whole_down,
            whole_gate,
            whole_gate,
            whole_gate,
            whole_gate,
        ],
        scratch_shapes=[
            pltpu.VMEM((2, PAIR, length), BF16),
            pltpu.VMEM((length, PAIR), BF16),
            pltpu.VMEM((PAIR, length), BF16),
            pltpu.VMEM((PAIR, length), BF16),
            pltpu.VMEM((width, span), BF16),
        ]
        + [gather_sems(line)] * 3
        + [pltpu.SemaphoreType.DMA((2, 1)), pltpu.SemaphoreType.DMA((2, 4))],
        input_output_aliases={3: 5},
        compiler_params=pltpu.CompilerParams(
            dimension_semantics=("arbitrary",),
            vmem_limit_bytes=48 * MIB,
            collective_id=2,
            has_side_effects=True,
        ),
        cost_estimate=pl.CostEstimate(
            flops=area * 1024, bytes_accessed=8 * width * length, transcendentals=area
        ),
        name="attend_carry",
    )(received, own, grads, d_own, gate, up)


def shards(
    inputs,
    first_values,
    out_grad,
    attn_gain,
    query_weight,
    key_weight,
    value_weight,
    output_weight,
    mlp_gain,
    gate_weight,
    up_weight,
    down_weight,
):
    slots, tok, _ = inputs.shape
    groups = lax.axis_size("seq")
    parts = lax.axis_size("fsdp")
    line = parts // 2
    count = groups // slots
    length = tok * groups
    span = slots * tok
    seat = lax.axis_index("seq")
    shard = lax.axis_index("fsdp")
    side = seat // count
    rank = seat % count
    core = seat % 2
    z, y = shard // 2, shard % 2
    wide = D // 2
    width = D // count

    def along_seq(value, partner):
        return lax.ppermute(value, "seq", [(i, partner(i)) for i in range(groups)])

    def along_fsdp(value, partner):
        return lax.ppermute(value, "fsdp", [(i, partner(i)) for i in range(parts)])

    def to_core(value):
        return along_seq(value, lambda i: i ^ 1)

    def to_y(value):
        return along_fsdp(value, lambda i: i ^ 1)

    def to_z(value, jump):
        return along_fsdp(value, lambda i: (i + 2 * jump) % parts)

    def after(value, *others):
        return lax.optimization_barrier((value,) + others)[0]

    def to_sequence(values):
        taken = []
        for jump in range(1, slots):
            sent = lax.dynamic_index_in_dim(values, (side + jump) % slots, 0, keepdims=False)
            taken.append(along_seq(sent, lambda i: (i + jump * count) % groups))
        return taken

    def to_home(whole, sent):
        for jump in range(1, slots):
            part = sent[(jump - 1) * tok : jump * tok]
            part = along_seq(part, lambda i: (i - jump * count) % groups)
            whole = land(whole, part, ((side + jump) % slots)[None])
        return whole

    def rank_up(i, jump):
        return (i // count) * count + (i % count + jump) % count

    def rank_down(i, jump):
        return (i // count) * count + (i % count - jump) % count

    def halves_to_ranks(other, own, axis):
        if count == 2:
            return [other, own]
        return [
            lax.dynamic_slice_in_dim(
                join(other, own, axis), ((rank + 1 + number) % count) * width, width, axis
            )
            for number in range(count)
        ]

    def join(other, own, axis):
        first = jnp.where(core == 0, own, other)
        second = jnp.where(core == 0, other, own)
        return jnp.concatenate([first, second], axis=axis)

    def ranks_to_halves(pieces, axis):
        if count == 2:
            return pieces
        shape = list(pieces[0].shape)
        shape[axis] = D
        whole = jnp.zeros(shape, pieces[0].dtype)
        for number in range(count):
            whole = lax.dynamic_update_slice_in_dim(
                whole, pieces[number], ((rank + 1 + number) % count) * width, axis
            )
        return [
            lax.dynamic_slice_in_dim(whole, which * wide, wide, axis)
            for which in (1 - core, core)
        ]

    def exchange(pieces):
        received = [
            along_seq(pieces[jump - 1], lambda i: rank_up(i, jump)) for jump in range(1, count)
        ]
        return received + [pieces[count - 1]]

    def exchange_back(pieces):
        received = [
            along_seq(pieces[jump - 1], lambda i: rank_down(i, jump)) for jump in range(1, count)
        ]
        return received + [pieces[count - 1]]

    def split(*weights):
        results = []
        for which in (core, 1 - core):
            columns = []
            for weight in weights:
                size = weight.shape[1] // 2
                columns.append(lax.dynamic_slice_in_dim(weight, which * size, size, 1))
            results.append(columns)
        return results

    def gather_z(half):
        return [half] + [to_z(half, jump) for jump in range(1, line)]

    def gather_rest(along_z, other):
        along_y = [to_y(piece) for piece in along_z]
        own = [piece for pair in zip(along_z, along_y) for piece in pair]
        return (own, [other] + [to_core(piece) for piece in own[1:]])

    numbers = []
    for jump in range(line):
        for flip in range(2):
            numbers.append(((z - jump) % line) * 2 + (y ^ flip))
    place = jnp.stack([side, core] + numbers).astype(jnp.int32)

    def low(value):
        return value.astype(BF16)

    def add(a, b):
        return low(a.astype(F32) + b.astype(F32))

    def pick(value, index, axis):
        return lax.dynamic_index_in_dim(value, index, axis, keepdims=False)

    def scatter(sent, kept, rows_axis):
        shape = kept.shape
        rows = shape[rows_axis] // parts
        cut = shape[:rows_axis] + (line, 2, rows) + shape[rows_axis + 1 :]
        received = to_core(sent).reshape(cut)
        kept = kept.reshape(cut)
        axis = rows_axis + 1
        received_y = to_y(add(pick(kept, 1 - y, axis), pick(received, 1 - y, axis)))
        kept_y = pick(kept, y, axis), pick(received, y, axis)

        def partial(index):
            total = pick(kept_y[0], index, rows_axis).astype(F32)
            total = total + pick(kept_y[1], index, rows_axis).astype(F32)
            return total + pick(received_y, index, rows_axis).astype(F32)

        total = partial(z)
        for jump in range(1, line):
            total = total + to_z(low(partial((z + jump) % line)), jump).astype(F32)
        mine = low(total)
        for jump in range(1, groups // 2):
            total = total + along_seq(mine, lambda i: (i + 2 * jump) % groups).astype(F32)
        mine = low(total)
        return (mine, to_core(mine))

    def columns(mine, others):
        first = jnp.where(core == 0, mine, others)
        second = jnp.where(core == 0, others, mine)
        return jnp.concatenate([first, second], axis=-1).astype(F32)

    def everywhere(value):
        value = value + to_core(value)
        value = value + to_y(value)
        total = value
        for jump in range(1, line):
            total = total + to_z(value, jump)
        value = total
        for jump in range(1, groups // 2):
            total = total + along_seq(value, lambda i: (i + 2 * jump) % groups)
        return total

    steps = jnp.arange(slots, dtype=jnp.int32)
    starts = ((side - steps) % slots) * (count * tok) + rank * tok
    positions = (starts[:, None] + jnp.arange(tok, dtype=jnp.int32)[None]).reshape(span)
    freqs = rope_base ** (-(jnp.arange(HALF, dtype=F32) * 2.0 / HEAD_DIM))

    def tables(positions):
        angles = freqs[:, None] * positions.astype(F32)[None, :]
        return (jnp.cos(angles), jnp.sin(angles))

    cosine, sine = tables(positions)
    full_cos, full_sin = tables(jnp.arange(length, dtype=jnp.int32))
    sources = jnp.concatenate(
        [(rank - 1 - jnp.arange(count - 1, dtype=jnp.int32)) % count, rank[None]]
    ).astype(jnp.int32)
    order = (((side - steps) % slots)[None, :] * count + sources[:, None]).reshape(-1)
    order = order.astype(jnp.int32)

    gains = jnp.pad(jnp.stack([attn_gain, mlp_gain], axis=1), ((0, 0), (0, 126)))
    gate_halves, up_halves, out_halves, down_halves = (
        [half[0] for half in split(weight)]
        for weight in (gate_weight, up_weight, output_weight, down_weight)
    )

    if (slots, count) == (2, 2):
        parts_of = lambda ref: [ref.reshape(-1, ref.shape[-1])]
        (q_half,), (k_half,), (v_half,) = (
            split(weight)[:1] for weight in (query_weight, key_weight, value_weight)
        )
        (
            tokens,
            firsts,
            heads_own,
            heads_received,
            normed,
            qkv_full,
            gains_full,
            out_own,
            out_other,
            down_own,
        ) = front(
            inputs,
            first_values,
            q_half[0],
            k_half[0],
            jnp.concatenate([v_half[0], gains], axis=1),
            out_halves[0],
            down_halves[0],
            cosine,
            sine,
            line,
        )
        qkv_full = qkv_full.reshape(2, 3, D, wide)
        tokens = [tokens]
        pieces = [heads_received, heads_own]
        (
            mix_received,
            att_own,
            lse,
            att_other,
            grads,
            down_own,
            down_other,
            gate_own,
            gate_other,
            up_own,
            up_other,
        ) = attend_carry(
            heads_received, heads_own, out_grad, down_own, gate_halves[0], up_halves[0], line
        )
        mixes = [mix_received, att_own]
        grads = [grads]
        layout = jnp.stack([side, core, 0 * core]).astype(jnp.int32)
        out_own, out_other = parts_of(out_own), parts_of(out_other)
        gate_pieces = parts_of(gate_own), parts_of(gate_other)
        up_pieces = parts_of(up_own), parts_of(up_other)
        down_pieces = parts_of(down_own), parts_of(down_other)
    else:
        qkv = [
            jnp.concatenate(half + [gains], axis=1)
            for half in split(query_weight, key_weight, value_weight)
        ]
        layout = place
        tokens = to_sequence(inputs)
        firsts = to_sequence(first_values)
        grads = to_sequence(out_grad)
        qkv_own, qkv_other = gather_rest(gather_z(qkv[0]), qkv[1])
        out_own, out_other = gather_rest(gather_z(out_halves[0]), out_halves[1])
        gate_pieces = gather_rest(gather_z(gate_halves[0]), gate_halves[1])
        up_pieces = gather_rest(gather_z(up_halves[0]), up_halves[1])
        down_pieces = gather_rest(gather_z(down_halves[0]), down_halves[1])
        heads_other, heads_own, normed, qkv_full, gains_full = project(
            inputs, tokens, first_values, firsts, qkv_own, qkv_other, cosine, sine, place
        )
        pieces = exchange(halves_to_ranks(heads_other, heads_own, 1))
        mixes, lse = attend(pieces, order, slots)
        att_other, att_own = ranks_to_halves(exchange_back(mixes), 0)

    middle, normed2, out_full = output_projection(
        inputs, tokens, out_own, out_other, att_other, att_own, gains_full, layout
    )
    (
        outputs,
        outputs_sent,
        grad_middle,
        low_grad,
        mlp_gain_grad,
        gu_sent,
        gu_kept,
        down_sent,
        down_kept,
    ) = mlp(out_grad, grads, middle, normed2, gains_full, gate_pieces, up_pieces, down_pieces, layout)
    ga_other, ga_own, out_sent, out_kept = grad_attended(
        low_grad, out_full, att_other, att_own, place
    )
    gate_up_grad = scatter(gu_sent, gu_kept, 1)
    down_grad = scatter(
        down_sent.reshape(-1, wide), down_kept.reshape(-1, wide), 0
    )
    output_grad = scatter(out_sent, out_kept, 0)
    grad_heads = exchange(halves_to_ranks(ga_other, ga_own, 0))
    back = attend_back(pieces, mixes, grad_heads, lse, full_cos, full_sin, order, slots)
    back_other, back_own = ranks_to_halves(exchange_back(back), 1)
    input_grad, input_sent, first_grad, first_sent, gain_grads, qkv_sent, qkv_kept = tail(
        inputs,
        tokens,
        back_other,
        back_own,
        qkv_full,
        normed,
        grad_middle,
        gains_full,
        mlp_gain_grad,
        place,
    )
    qkv_grad = columns(*scatter(qkv_sent, qkv_kept, 1))
    gate_up_grad = columns(*gate_up_grad)
    gain_grads = everywhere(gain_grads)
    gain_grads = lax.dynamic_slice_in_dim(gain_grads, shard * (D // parts), D // parts, 1)
    return (
        to_home(outputs, outputs_sent),
        to_home(input_grad, input_sent),
        to_home(first_grad, first_sent),
        gain_grads[0],
        gain_grads[1],
        qkv_grad[0],
        qkv_grad[1],
        qkv_grad[2],
        columns(*output_grad),
        gate_up_grad[0],
        gate_up_grad[1],
        columns(*down_grad),
    )


def solution(mesh):
    token_spec = P("fsdp", "seq", None)
    weight_spec = P("fsdp", None)
    gain_spec = P("fsdp")
    return jax.shard_map(
        shards,
        mesh=mesh,
        in_specs=(token_spec,) * 3
        + (gain_spec,)
        + (weight_spec,) * 4
        + (gain_spec,)
        + (weight_spec,) * 3,
        out_specs=(token_spec,) * 3 + (gain_spec,) * 2 + (weight_spec,) * 7,
        check_vma=False,
    )
```

```python
import functools

import jax
import jax.numpy as jnp
from jax import lax
from jax.experimental import pallas as pl
from jax.experimental.pallas import tpu as pltpu
from jax.sharding import PartitionSpec as P

D = 1024
HEADS = 16
HEAD_DIM = 64
HALF = HEAD_DIM // 2
PAIR = 2 * HEAD_DIM
F32 = jnp.float32
BF16 = jnp.bfloat16
NEG = -1e30
MIB = 1024 * 1024
epsilon = 1e-06
rope_base = 10000.0


def dot(a, b):
    return lax.dot_general(a, b, (((1,), (0,)), ((), ())), preferred_element_type=F32)


def head_rows(value, head):
    row = lax.broadcasted_iota(jnp.int32, value.shape, 0)
    return jnp.where((row // HEAD_DIM) == head, value, jnp.zeros_like(value))


def head_lanes(value, head):
    lane = lax.broadcasted_iota(jnp.int32, value.shape, 1)
    return jnp.where((lane // HEAD_DIM) == head, value, jnp.zeros_like(value))


def causal(scores):
    side = scores.shape[0]
    square = scores[:, :side]
    key = lax.broadcasted_iota(jnp.int32, square.shape, 0)
    query = lax.broadcasted_iota(jnp.int32, square.shape, 1)
    square = jnp.where(key <= query, square, NEG)
    if scores.shape[1] == side:
        return square
    return jnp.concatenate([square, scores[:, side:]], axis=1)


def attend_body(length, tile_k, qz, kn, vt, ot, lse_ref):
    def score(sub, head):
        start = sub * tile_k
        return causal(dot(kn[start : start + tile_k, :], qz[head, :, start:]))

    def absorb(sub, head, carry, scores):
        peak, total, mixed = carry
        start = sub * tile_k
        new_peak = jnp.maximum(peak, jnp.max(scores, axis=0, keepdims=True))
        weights = jnp.exp(scores - new_peak)
        fade = jnp.exp(peak - new_peak)
        total = total * fade + jnp.sum(weights, axis=0, keepdims=True)
        values = vt[head * HEAD_DIM : (head + 1) * HEAD_DIM, start : start + tile_k]
        mixed = mixed * fade + dot(values, weights.astype(BF16))
        return (new_peak, total, mixed)

    tiles = [(sub, head) for sub in range(length // tile_k) for head in range(2)]
    carries = [
        (
            jnp.full((1, length), NEG, F32),
            jnp.zeros((1, length), F32),
            jnp.zeros((HEAD_DIM, length), F32),
        )
        for _ in range(2)
    ]
    ahead = score(*tiles[0])
    for number, (sub, head) in enumerate(tiles):
        scores = ahead
        if number + 1 < len(tiles):
            ahead = score(*tiles[number + 1])
        peak, total, mixed = absorb(sub, head, carries[head], scores)
        done = slice(sub * tile_k, (sub + 1) * tile_k)
        rows = slice(head * HEAD_DIM, (head + 1) * HEAD_DIM)
        ot[rows, done] = (mixed[:, :tile_k] / total[:, :tile_k]).astype(BF16)
        lse_ref[0, head : head + 1, done] = peak[:, :tile_k] + jnp.log(total[:, :tile_k])
        carries[head] = (peak[:, tile_k:], total[:, tile_k:], mixed[:, tile_k:])


def attend_kernel(count, slots, tok, tile_k, order, *refs):
    pieces = refs[:count]
    outs = refs[count : 2 * count]
    lse_ref = refs[2 * count]
    qz, kn, vt, ot = refs[2 * count + 1 :]
    for source in range(count):
        for slot in range(slots):
            cols = pl.ds(pl.multiple_of(order[source * slots + slot] * tok, tok), tok)
            take = slice(slot * tok, (slot + 1) * tok)
            query = pieces[source][0, :, take] * jnp.asarray(HEAD_DIM**-0.5, BF16)
            for head in range(2):
                qz[head, :, cols] = head_rows(query, head)
            kn[cols, :] = pieces[source][1, :, take].T
            vt[:, cols] = pieces[source][2, :, take]
    length = count * slots * tok
    attend_body(length, tile_k, qz, kn, vt, ot, lse_ref)
    for source in range(count):
        for slot in range(slots):
            cols = pl.ds(pl.multiple_of(order[source * slots + slot] * tok, tok), tok)
            outs[source][:, slot * tok : (slot + 1) * tok] = ot[:, cols]


def attend(pieces, order, slots):
    count = len(pieces)
    width, span = pieces[0].shape[1:]
    tok = span // slots
    length = count * span
    pairs = width // PAIR
    tile_k = min(256, length)
    grid_spec = pltpu.PrefetchScalarGridSpec(
        num_scalar_prefetch=1,
        grid=(pairs,),
        in_specs=[pl.BlockSpec((3, PAIR, span), lambda p, o: (0, p, 0))] * count,
        out_specs=[pl.BlockSpec((PAIR, span), lambda p, o: (p, 0))] * count
        + [pl.BlockSpec((1, 8, length), lambda p, o: (p, 0, 0))],
        scratch_shapes=[
            pltpu.VMEM((2, PAIR, length), BF16),
            pltpu.VMEM((length, PAIR), BF16),
            pltpu.VMEM((PAIR, length), BF16),
            pltpu.VMEM((PAIR, length), BF16),
        ],
    )
    area = pairs * 2 * length * length // 2
    results = pl.pallas_call(
        functools.partial(attend_kernel, count, slots, tok, tile_k),
        out_shape=[jax.ShapeDtypeStruct((width, span), BF16)] * count
        + [jax.ShapeDtypeStruct((pairs, 8, length), F32)],
        grid_spec=grid_spec,
        compiler_params=pltpu.CompilerParams(
            dimension_semantics=("arbitrary",), vmem_limit_bytes=48 * MIB
        ),
        cost_estimate=pl.CostEstimate(
            flops=area * 1024, bytes_accessed=8 * width * length, transcendentals=area
        ),
        name="attend",
    )(order, *pieces)
    return (results[:count], results[count])


def attend_back_body(
    pieces,
    mixes,
    grads,
    columns,
    tok,
    length,
    tile_q,
    tile_k,
    lse_ref,
    qz,
    gz,
    qn,
    gn,
    kn,
    vn,
    kt,
    inner,
    dq,
    dk,
    dv,
):
    slots = pieces[0].shape[2] // tok
    for source in range(len(pieces)):
        for slot in range(slots):
            cols = columns(source, slot)
            take = slice(slot * tok, (slot + 1) * tok)
            query = pieces[source][0, :, take] * jnp.asarray(HEAD_DIM**-0.5, BF16)
            grad = grads[source][:, take]
            query_rows = query.T
            grad_rows = grad.T
            for head in range(2):
                qz[head, :, cols] = head_rows(query, head)
                gz[head, :, cols] = head_rows(grad, head)
                qn[head, cols, :] = head_lanes(query_rows, head)
                gn[head, cols, :] = head_lanes(grad_rows, head)
            key = pieces[source][1, :, take]
            kt[:, cols] = key
            kn[cols, :] = key.T
            vn[cols, :] = pieces[source][2, :, take].T
            both = grad.astype(F32) * mixes[source][:, take].astype(F32)
            for head in range(2):
                inner[head : head + 1, cols] = jnp.sum(
                    both[head * HEAD_DIM : (head + 1) * HEAD_DIM], axis=0, keepdims=True
                )
    dq[...] = jnp.zeros_like(dq)
    steps = tile_q // tile_k

    def tile(key_start, query_start, width, masked, carry):
        grad_keys, grad_values = carry
        keys = kn[pl.ds(key_start, tile_k), :]
        values = vn[pl.ds(key_start, tile_k), :]
        cols = pl.ds(query_start, width)
        for head in range(2):
            rows = slice(head * HEAD_DIM, (head + 1) * HEAD_DIM)
            scores = dot(keys, qz[head, :, cols])
            if masked:
                scores = causal(scores)
            probs = jnp.exp(scores - lse_ref[0, head : head + 1, cols])
            grad_probs = dot(values, gz[head, :, cols])
            grad_scores = (probs * (grad_probs - inner[head : head + 1, cols])).astype(BF16)
            grad_values = grad_values + dot(probs.astype(BF16), gn[head, cols, :])
            grad_keys = grad_keys + dot(grad_scores, qn[head, cols, :])
            dq[rows, cols] += dot(kt[rows, pl.ds(key_start, tile_k)], grad_scores)
        return (grad_keys, grad_values)

    def one(number, _):
        base = pl.multiple_of(number * tile_q, tile_q)
        for sub in range(steps):
            skip = sub * tile_k
            key_start = pl.multiple_of(base + skip, tile_k)
            carry = (jnp.zeros((tile_k, PAIR), F32), jnp.zeros((tile_k, PAIR), F32))
            carry = tile(key_start, key_start, tile_q - skip, True, carry)

            def body(step, carry):
                return tile(
                    key_start, pl.multiple_of(step * tile_q, tile_q), tile_q, False, carry
                )

            carry = lax.fori_loop(number + 1, length // tile_q, body, carry)
            dk[pl.ds(key_start, tile_k), :] = carry[0]
            dv[pl.ds(key_start, tile_k), :] = carry[1]
        return 0

    lax.fori_loop(0, length // tile_q, one, 0)


def turn_back(dq, dk, dv, cols, cosine, sine):
    half = HEAD_DIM // 2
    results = []
    for grad in (dq[:, cols] * (HEAD_DIM**-0.5), dk[cols, :].T):
        turned = []
        for head in range(2):
            low = head * HEAD_DIM
            first = grad[low : low + half]
            second = grad[low + half : low + 2 * half]
            turned += [first * cosine + second * sine, second * cosine - first * sine]
        results.append(jnp.concatenate(turned, axis=0).astype(BF16))
    results.append(dv[cols, :].T.astype(BF16))
    return results


def attend_back_kernel(count, slots, tok, tile_q, tile_k, order, *refs):
    pieces = refs[:count]
    mixes = refs[count : 2 * count]
    grads = refs[2 * count : 3 * count]
    lse_ref, cos_ref, sin_ref = refs[3 * count : 3 * count + 3]
    outs = refs[3 * count + 3 : 4 * count + 3]
    scratch = refs[4 * count + 3 :]
    dq, dk, dv = scratch[-3:]

    def columns(source, slot):
        return pl.ds(pl.multiple_of(order[source * slots + slot] * tok, tok), tok)

    attend_back_body(
        pieces,
        mixes,
        grads,
        columns,
        tok,
        count * slots * tok,
        tile_q,
        tile_k,
        lse_ref,
        *scratch,
    )
    for source in range(count):
        for slot in range(slots):
            cols = columns(source, slot)
            results = turn_back(dq, dk, dv, cols, cos_ref[:, cols], sin_ref[:, cols])
            for which, result in enumerate(results):
                outs[source][which, :, slot * tok : (slot + 1) * tok] = result


def attend_back(pieces, mixes, grads, lse, cosine, sine, order, slots):
    count = len(pieces)
    width, span = pieces[0].shape[1:]
    tok = span // slots
    length = count * span
    pairs = width // PAIR
    tile_q = min(512, length)
    tile_k = min(256, length)
    triple = pl.BlockSpec((3, PAIR, span), lambda p, o: (0, p, 0))
    single = pl.BlockSpec((PAIR, span), lambda p, o: (p, 0))
    table = pl.BlockSpec((HEAD_DIM // 2, length), lambda p, o: (0, 0))
    grid_spec = pltpu.PrefetchScalarGridSpec(
        num_scalar_prefetch=1,
        grid=(pairs,),
        in_specs=[triple] * count
        + [single] * (2 * count)
        + [pl.BlockSpec((1, 8, length), lambda p, o: (p, 0, 0)), table, table],
        out_specs=[triple] * count,
        scratch_shapes=[
            pltpu.VMEM((2, PAIR, length), BF16),
            pltpu.VMEM((2, PAIR, length), BF16),
            pltpu.VMEM((2, length, PAIR), BF16),
            pltpu.VMEM((2, length, PAIR), BF16),
            pltpu.VMEM((length, PAIR), BF16),
            pltpu.VMEM((length, PAIR), BF16),
            pltpu.VMEM((PAIR, length), BF16),
            pltpu.VMEM((8, length), F32),
            pltpu.VMEM((PAIR, length), F32),
            pltpu.VMEM((length, PAIR), F32),
            pltpu.VMEM((length, PAIR), F32),
        ],
    )
    area = pairs * 2 * length * length // 2
    return pl.pallas_call(
        functools.partial(attend_back_kernel, count, slots, tok, tile_q, tile_k),
        out_shape=[jax.ShapeDtypeStruct((3, width, span), BF16)] * count,
        grid_spec=grid_spec,
        compiler_params=pltpu.CompilerParams(
            dimension_semantics=("arbitrary",), vmem_limit_bytes=56 * MIB
        ),
        cost_estimate=pl.CostEstimate(
            flops=area * 2560, bytes_accessed=16 * width * length, transcendentals=area
        ),
        name="attend_back",
    )(order, *pieces, *mixes, *grads, lse, cosine, sine)


def nt(a, b):
    return lax.dot_general(a, b, (((1,), (1,)), ((), ())), preferred_element_type=F32)


def whole_block(shape):
    zeros = (0,) * len(shape)
    return pl.BlockSpec(shape, lambda *_: zeros)


def parameters(mib):
    return pltpu.CompilerParams(dimension_semantics=("arbitrary",), vmem_limit_bytes=mib * MIB)


def project_kernel(slots, tok, count, rows, place, *refs):
    xs, firsts = refs[:slots], refs[slots : 2 * slots]
    own = refs[2 * slots : 2 * slots + count]
    other = refs[2 * slots + count : 2 * slots + 2 * count]
    cos_ref, sin_ref = refs[2 * slots + 2 * count : 2 * slots + 2 * count + 2]
    other_ref, own_ref, normed_ref, full_ref, gains_ref, column = refs[2 * slots + 2 * count + 2 :]
    step = pl.program_id(0)
    target, kind = step // 3, step % 3
    core = place[1]
    half = jnp.where(target == 0, 1 - core, core)
    depth = normed_ref.shape[1]
    wide = own_ref.shape[1]

    @pl.when(step == 0)
    def _():
        for number in range(count):
            at = pl.ds(pl.multiple_of(place[2 + number] * rows, rows), rows)
            for which in range(3):
                columns = slice(which * wide, (which + 1) * wide)
                full_ref[core, which, at, :] = own[number][:, columns]
                full_ref[1 - core, which, at, :] = other[number][:, columns]
            column[at, :] = own[number][:, 3 * wide :]
        gains_ref[...] = column[...].T[:8].astype(F32)
        gain = gains_ref[0:1, :]
        for slot in range(slots):
            values = xs[slot][...].reshape(tok, depth).astype(F32)
            scale = lax.rsqrt(jnp.mean(values * values, axis=1, keepdims=True) + epsilon)
            normed_ref[slot * tok : (slot + 1) * tok, :] = (values * scale * gain).astype(BF16)

    weight = full_ref[half, kind]
    raw = nt(weight.T, normed_ref[...])

    def store(value):
        @pl.when(target == 0)
        def _():
            other_ref[0] = value

        @pl.when(target == 1)
        def _():
            own_ref[0] = value

    @pl.when(kind < 2)
    def _():
        parts = raw.reshape(wide // HEAD_DIM, 2, HALF, raw.shape[1])
        first, second = parts[:, 0], parts[:, 1]
        cosine, sine = cos_ref[...][None], sin_ref[...][None]
        turned = jnp.stack(
            [first * cosine - second * sine, first * sine + second * cosine], axis=1
        )
        store(turned.reshape(raw.shape).astype(BF16))

    @pl.when(kind == 2)
    def _():
        first = jnp.concatenate(
            [ref[...].reshape(tok, wide).T.astype(F32) for ref in firsts], axis=1
        )
        store((0.5 * raw + 0.5 * first).astype(BF16))


def project(inputs, received, firsts, firsts_received, own, other, cosine, sine, place):
    slots, tok, depth = inputs.shape
    count, rows = len(own), own[0].shape[0]
    wide = depth // 2
    span = slots * tok

    def half(s, p):
        return jnp.where(s < 3, 1 - p[1], p[1])

    x_specs = [pl.BlockSpec((1, tok, depth), lambda s, p: (p[0], 0, 0))]
    x_specs += [whole_block((tok, depth))] * (slots - 1)
    first_specs = [pl.BlockSpec((1, tok, wide), lambda s, p: (p[0], 0, half(s, p)))]
    first_specs += [pl.BlockSpec((tok, wide), lambda s, p: (0, half(s, p)))] * (slots - 1)
    grid_spec = pltpu.PrefetchScalarGridSpec(
        num_scalar_prefetch=1,
        grid=(6,),
        in_specs=x_specs
        + first_specs
        + [whole_block(own[0].shape)] * (2 * count)
        + [whole_block((HALF, span))] * 2,
        out_specs=[
            pl.BlockSpec((1, wide, span), lambda s, p: (jnp.minimum(s, 2), 0, 0)),
            pl.BlockSpec((1, wide, span), lambda s, p: (jnp.maximum(s - 3, 0), 0, 0)),
            whole_block((span, depth)),
            whole_block((2, 3, depth, wide)),
            whole_block((8, depth)),
        ],
        scratch_shapes=[pltpu.VMEM((depth, 128), BF16)],
    )
    return pl.pallas_call(
        functools.partial(project_kernel, slots, tok, count, rows),
        out_shape=[
            jax.ShapeDtypeStruct((3, wide, span), BF16),
            jax.ShapeDtypeStruct((3, wide, span), BF16),
            jax.ShapeDtypeStruct((span, depth), BF16),
            jax.ShapeDtypeStruct((2, 3, depth, wide), BF16),
            jax.ShapeDtypeStruct((8, depth), F32),
        ],
        grid_spec=grid_spec,
        compiler_params=parameters(56),
        cost_estimate=pl.CostEstimate(
            flops=6 * span * depth * depth,
            bytes_accessed=2 * (8 * span * depth + 6 * depth * depth),
            transcendentals=0,
        ),
        name="project",
    )(place, inputs, *received, firsts, *firsts_received, *own, *other, cosine, sine)


def output_kernel(slots, tok, count, rows, place, *refs):
    xs = refs[:slots]
    own = refs[slots : slots + count]
    other = refs[slots + count : slots + 2 * count]
    att_other, att_own, gains_ref = refs[slots + 2 * count : slots + 2 * count + 3]
    middle_ref, normed_ref, full_ref = refs[slots + 2 * count + 3 :]
    step = pl.program_id(0)
    core = place[1]
    wide = att_own.shape[0]
    depth = 2 * wide
    mine = pl.ds(pl.multiple_of(core * wide, wide), wide)
    others = pl.ds(pl.multiple_of((1 - core) * wide, wide), wide)

    @pl.when(step == 0)
    def _():
        for number in range(count):
            at = pl.ds(pl.multiple_of(place[2 + number] * rows, rows), rows)
            full_ref[at, mine] = own[number][...]
            full_ref[at, others] = other[number][...]

    total = dot(att_own[...].T, full_ref[mine, :]) + dot(att_other[...].T, full_ref[others, :])
    for slot in range(slots):

        @pl.when(step == slot)
        def _(slot=slot):
            middle_ref[...] = xs[slot][...].reshape(tok, depth).astype(F32) + total

    middle = middle_ref[...]
    scale = lax.rsqrt(jnp.mean(middle * middle, axis=1, keepdims=True) + epsilon)
    normed_ref[...] = (middle * scale * gains_ref[1:2, :]).astype(BF16)


def output_projection(inputs, received, own, other, att_other, att_own, gains, place):
    slots, tok, depth = inputs.shape
    count, rows = len(own), own[0].shape[0]
    wide = depth // 2
    span = slots * tok
    x_specs = [pl.BlockSpec((1, tok, depth), lambda s, p: (p[0], 0, 0))]
    x_specs += [whole_block((tok, depth))] * (slots - 1)
    grid_spec = pltpu.PrefetchScalarGridSpec(
        num_scalar_prefetch=1,
        grid=(slots,),
        in_specs=x_specs
        + [whole_block(own[0].shape)] * (2 * count)
        + [pl.BlockSpec((wide, tok), lambda s, p: (0, s))] * 2
        + [whole_block((8, depth))],
        out_specs=[
            pl.BlockSpec((tok, depth), lambda s, p: (s, 0)),
            pl.BlockSpec((tok, depth), lambda s, p: (s, 0)),
            whole_block((depth, depth)),
        ],
    )
    return pl.pallas_call(
        functools.partial(output_kernel, slots, tok, count, rows),
        out_shape=[
            jax.ShapeDtypeStruct((span, depth), F32),
            jax.ShapeDtypeStruct((span, depth), BF16),
            jax.ShapeDtypeStruct((depth, depth), BF16),
        ],
        grid_spec=grid_spec,
        compiler_params=parameters(56),
        cost_estimate=pl.CostEstimate(
            flops=2 * span * depth * depth,
            bytes_accessed=12 * span * depth + 4 * depth * depth,
            transcendentals=0,
        ),
        name="output_projection",
    )(place, inputs, *received, *own, *other, att_other, att_own, gains)


def mlp_kernel(slots, tok, count, rows, down_rows, blocks, place, *refs):
    grads = refs[:slots]
    middle_ref, normed_ref, gains_ref = refs[slots : slots + 3]
    base = slots + 3
    own_g, other_g, own_u, other_u, own_d, other_d = (
        refs[base + number * count : base + (number + 1) * count] for number in range(6)
    )
    (
        out_ref,
        send_ref,
        grad_ref,
        low_ref,
        gain_ref,
        gu_send,
        gu_keep,
        d_send,
        d_keep,
        wgu,
        wd,
        og,
        normed_t,
        acc,
        back,
        sems,
    ) = refs[base + 6 * count :]
    step = pl.program_id(0)
    core = place[1]
    depth = og.shape[1]
    wide = depth // 2
    strip = 128
    half_width = blocks * strip
    mine = pl.ds(pl.multiple_of(core * wide, wide), wide)
    others = pl.ds(pl.multiple_of((1 - core) * wide, wide), wide)

    def loads():
        copies = []
        for number in range(count):
            at = pl.ds(pl.multiple_of(place[2 + number] * rows, rows), rows)
            for which, (gate, up) in enumerate(((own_g, own_u), (other_g, other_u))):
                copies.append((gate[number], wgu.at[which, at, pl.ds(0, half_width)]))
                copies.append((up[number], wgu.at[which, at, pl.ds(half_width, half_width)]))
        for number in range(count):
            at = pl.ds(pl.multiple_of(place[2 + number] * down_rows, down_rows), down_rows)
            copies.append((own_d[number], wd.at[at, mine]))
            copies.append((other_d[number], wd.at[at, others]))
        return [
            pltpu.make_async_copy(source, target, sems.at[number])
            for number, (source, target) in enumerate(copies)
        ]

    @pl.when(step == 0)
    def _():
        copies = loads()
        for copy in copies:
            copy.start()
        for slot in range(slots):
            og[slot * tok : (slot + 1) * tok, :] = grads[slot][...].reshape(tok, depth)
        normed_t[...] = normed_ref[...].T
        acc[...] = jnp.zeros_like(acc)
        back[...] = jnp.zeros_like(back)
        for copy in copies:
            copy.wait()

    at = pl.ds(pl.multiple_of(step * strip, strip), strip)
    up_at = pl.ds(pl.multiple_of(half_width + step * strip, strip), strip)
    gate_w = jnp.concatenate([wgu[0, :, at], wgu[1, :, at]], axis=1)
    up_w = jnp.concatenate([wgu[0, :, up_at], wgu[1, :, up_at]], axis=1)
    own_rows = pl.ds(pl.multiple_of(core * half_width + step * strip, strip), strip)
    other_rows = pl.ds(pl.multiple_of((1 - core) * half_width + step * strip, strip), strip)
    down_w = jnp.concatenate([wd[own_rows, :], wd[other_rows, :]], axis=0)
    normed = normed_ref[...]
    gate = dot(normed, gate_w)
    up = dot(normed, up_w)
    grad_active = nt(og[...], down_w)
    sigma = jax.nn.sigmoid(gate)
    silu = gate * sigma
    active = (silu * up).astype(BF16)
    grad_up = (grad_active * silu).astype(BF16)
    grad_gate = (grad_active * up * sigma * (1.0 + gate * (1.0 - sigma))).astype(BF16)
    acc[...] += dot(active, down_w)
    back[...] += nt(grad_gate, gate_w) + nt(grad_up, up_w)
    grad_gate_w = dot(normed_t[...], grad_gate).astype(BF16)
    gu_keep[0] = grad_gate_w[:, :strip]
    gu_send[0] = grad_gate_w[:, strip:]
    grad_up_w = dot(normed_t[...], grad_up).astype(BF16)
    gu_keep[1] = grad_up_w[:, :strip]
    gu_send[1] = grad_up_w[:, strip:]
    active_t = active.T
    kept = dot(active_t, og[:, mine]).astype(BF16)
    sent = dot(active_t, og[:, others]).astype(BF16)
    d_keep[core] = kept[:strip]
    d_keep[1 - core] = kept[strip:]
    d_send[core] = sent[:strip]
    d_send[1 - core] = sent[strip:]

    @pl.when(step == blocks - 1)
    def _():
        gain = gains_ref[1:2, :]
        chunk = min(128, tok)
        gain_ref[...] = jnp.zeros_like(gain_ref)
        for slot in range(slots):

            def finish(number, _, slot=slot):
                local = pl.ds(pl.multiple_of(number * chunk, chunk), chunk)
                some = pl.ds(pl.multiple_of(slot * tok + number * chunk, chunk), chunk)
                middle = middle_ref[some, :]
                scale = lax.rsqrt(jnp.mean(middle * middle, axis=1, keepdims=True) + epsilon)
                result = middle + acc[some, :]
                if slot == 0:
                    out_ref[0, local, :] = result
                else:
                    send_ref[pl.ds(pl.multiple_of((slot - 1) * tok + number * chunk, chunk), chunk), :] = (
                        result.astype(BF16)
                    )
                grad = back[some, :]
                gain_ref[0:1, :] += jnp.sum(grad * middle * scale, axis=0, keepdims=True)
                weighted = grad * gain
                inner = jnp.mean(weighted * middle, axis=1, keepdims=True)
                grad_middle = (
                    scale * weighted
                    - middle * (scale * scale * scale) * inner
                    + og[some, :].astype(F32)
                )
                grad_ref[some, :] = grad_middle
                low_ref[some, :] = grad_middle.astype(BF16)
                return 0

            lax.fori_loop(0, tok // chunk, finish, 0)


def mlp(grads, grads_received, middle, normed, gains, gate, up, down, place):
    slots, tok, depth = grads.shape
    own_d, other_d = down
    count, rows = len(own_d), gate[0][0].shape[0]
    down_rows = own_d[0].shape[0]
    half_width = gate[0][0].shape[1]
    wide = depth // 2
    span = slots * tok
    blocks = half_width // 128
    once = pl.Buffered(1)
    g_specs = [pl.BlockSpec((1, tok, depth), lambda s, p: (p[0], 0, 0), pipeline_mode=once)]
    g_specs += [pl.BlockSpec((tok, depth), lambda s, p: (0, 0), pipeline_mode=once)] * (slots - 1)
    gu_spec = pl.BlockSpec((2, depth, 128), lambda s, p: (0, 0, s))
    d_spec = pl.BlockSpec((2, 128, wide), lambda s, p: (0, s, 0))
    grid_spec = pltpu.PrefetchScalarGridSpec(
        num_scalar_prefetch=1,
        grid=(blocks,),
        in_specs=g_specs
        + [
            pl.BlockSpec((span, depth), lambda s, p: (0, 0), pipeline_mode=once),
            pl.BlockSpec((span, depth), lambda s, p: (0, 0), pipeline_mode=once),
            whole_block((8, depth)),
        ]
        + [pl.BlockSpec(memory_space=pl.ANY)] * (6 * count),
        out_specs=[
            pl.BlockSpec((1, tok, depth), lambda s, p: (p[0], 0, 0), pipeline_mode=once),
            pl.BlockSpec(((slots - 1) * tok, depth), lambda s, p: (0, 0), pipeline_mode=once),
            pl.BlockSpec((span, depth), lambda s, p: (0, 0), pipeline_mode=once),
            pl.BlockSpec((span, depth), lambda s, p: (0, 0), pipeline_mode=once),
            whole_block((8, depth)),
            gu_spec,
            gu_spec,
            d_spec,
            d_spec,
        ],
        scratch_shapes=[
            pltpu.VMEM((2, depth, 2 * half_width), BF16),
            pltpu.VMEM((2 * half_width, depth), BF16),
            pltpu.VMEM((span, depth), BF16),
            pltpu.VMEM((depth, span), BF16),
            pltpu.VMEM((span, depth), F32),
            pltpu.VMEM((span, depth), F32),
            pltpu.SemaphoreType.DMA((6 * count,)),
        ],
    )
    return pl.pallas_call(
        functools.partial(mlp_kernel, slots, tok, count, rows, down_rows, blocks),
        out_shape=[
            jax.ShapeDtypeStruct((slots, tok, depth), F32),
            jax.ShapeDtypeStruct(((slots - 1) * tok, depth), BF16),
            jax.ShapeDtypeStruct((span, depth), F32),
            jax.ShapeDtypeStruct((span, depth), BF16),
            jax.ShapeDtypeStruct((8, depth), F32),
            jax.ShapeDtypeStruct((2, depth, half_width), BF16),
            jax.ShapeDtypeStruct((2, depth, half_width), BF16),
            jax.ShapeDtypeStruct((2, half_width, wide), BF16),
            jax.ShapeDtypeStruct((2, half_width, wide), BF16),
        ],
        grid_spec=grid_spec,
        compiler_params=parameters(63),
        cost_estimate=pl.CostEstimate(
            flops=16 * span * depth * 2 * half_width,
            bytes_accessed=24 * depth * half_width + 20 * span * depth,
            transcendentals=2 * span * half_width,
        ),
        name="mlp",
    )(
        place,
        grads,
        *grads_received,
        middle,
        normed,
        gains,
        *gate[0],
        *gate[1],
        *up[0],
        *up[1],
        *own_d,
        *other_d,
    )


def grad_attended_kernel(place, low_ref, full_ref, att_other, att_own, ga_other, ga_own, sent, kept):
    step = pl.program_id(0)
    core = place[1]
    wide = att_own.shape[0]
    mine = pl.ds(pl.multiple_of(core * wide, wide), wide)
    others = pl.ds(pl.multiple_of((1 - core) * wide, wide), wide)
    for number, (att, result) in enumerate(((att_other, ga_other), (att_own, ga_own))):

        @pl.when(step == number)
        def _(att=att, result=result):
            result[...] = nt(full_ref[...], low_ref[...]).astype(BF16)
            kept[...] = dot(att[...], low_ref[:, mine]).astype(BF16)
            sent[...] = dot(att[...], low_ref[:, others]).astype(BF16)


def grad_attended(low, full, att_other, att_own, place):
    span, depth = low.shape
    wide = depth // 2

    def half(s, p):
        return jnp.where(s == 0, 1 - p[1], p[1])

    row_spec = pl.BlockSpec((wide, wide), lambda s, p: (half(s, p), 0))
    grid_spec = pltpu.PrefetchScalarGridSpec(
        num_scalar_prefetch=1,
        grid=(2,),
        in_specs=[
            whole_block((span, depth)),
            pl.BlockSpec((wide, depth), lambda s, p: (half(s, p), 0)),
            whole_block((wide, span)),
            whole_block((wide, span)),
        ],
        out_specs=[whole_block((wide, span)), whole_block((wide, span)), row_spec, row_spec],
    )
    return pl.pallas_call(
        grad_attended_kernel,
        out_shape=[
            jax.ShapeDtypeStruct((wide, span), BF16),
            jax.ShapeDtypeStruct((wide, span), BF16),
            jax.ShapeDtypeStruct((depth, wide), BF16),
            jax.ShapeDtypeStruct((depth, wide), BF16),
        ],
        grid_spec=grid_spec,
        compiler_params=parameters(48),
        cost_estimate=pl.CostEstimate(
            flops=4 * span * depth * depth,
            bytes_accessed=6 * span * depth + 4 * depth * depth,
            transcendentals=0,
        ),
        name="grad_attended",
    )(place, low, full, att_other, att_own)


def tail_kernel(slots, tok, place, *refs):
    xs = refs[:slots]
    (
        back_other,
        back_own,
        full_ref,
        normed_ref,
        grad_ref,
        gains_ref,
        mlp_gain_ref,
        out_ref,
        send_ref,
        first_ref,
        first_send,
        gain_ref,
        sent,
        kept,
        normed_t,
        acc,
    ) = refs[slots:]
    step = pl.program_id(0)
    target, kind = step // 3, step % 3
    depth = acc.shape[1]

    @pl.when(step == 0)
    def _():
        normed_t[...] = normed_ref[...].T
        acc[...] = jnp.zeros_like(acc)

    def part(back, result):
        grad = back[0]

        @pl.when(kind == 2)
        def _():
            rows = 0.5 * grad.astype(F32).T
            first_ref[0] = rows[:tok]
            first_send[...] = rows[tok:].astype(BF16)

        grad = grad * jnp.where(kind == 2, 0.5, 1.0).astype(BF16)
        acc[...] += nt(grad.T, full_ref[0, 0])
        result[0] = nt(normed_t[...], grad).astype(BF16)

    @pl.when(target == 0)
    def _():
        part(back_other, sent)

    @pl.when(target == 1)
    def _():
        part(back_own, kept)

    @pl.when(step == 5)
    def _():
        gain = gains_ref[0:1, :]
        chunk = min(128, tok)
        gain_ref[...] = jnp.zeros_like(gain_ref)
        gain_ref[1:2, :] = mlp_gain_ref[0:1, :]
        for slot in range(slots):

            def finish(number, _, slot=slot):
                local = pl.ds(pl.multiple_of(number * chunk, chunk), chunk)
                some = pl.ds(pl.multiple_of(slot * tok + number * chunk, chunk), chunk)
                if slot == 0:
                    values = xs[slot][0, local, :].astype(F32)
                else:
                    values = xs[slot][local, :].astype(F32)
                scale = lax.rsqrt(jnp.mean(values * values, axis=1, keepdims=True) + epsilon)
                grad = acc[some, :]
                gain_ref[0:1, :] += jnp.sum(grad * values * scale, axis=0, keepdims=True)
                weighted = grad * gain
                inner = jnp.mean(weighted * values, axis=1, keepdims=True)
                result = (
                    scale * weighted
                    - values * (scale * scale * scale) * inner
                    + grad_ref[some, :]
                )
                if slot == 0:
                    out_ref[0, local, :] = result
                else:
                    send_ref[pl.ds(pl.multiple_of((slot - 1) * tok + number * chunk, chunk), chunk), :] = (
                        result.astype(BF16)
                    )
                return 0

            lax.fori_loop(0, tok // chunk, finish, 0)


def tail(inputs, received, back_other, back_own, full, normed, grad_middle, gains, mlp_gain, place):
    slots, tok, depth = inputs.shape
    wide = depth // 2
    span = slots * tok
    rest = (slots - 1) * tok
    once = pl.Buffered(1)

    def half(s, p):
        return jnp.where(s < 3, 1 - p[1], p[1])

    x_specs = [pl.BlockSpec((1, tok, depth), lambda s, p: (p[0], 0, 0))]
    x_specs += [whole_block((tok, depth))] * (slots - 1)
    grid_spec = pltpu.PrefetchScalarGridSpec(
        num_scalar_prefetch=1,
        grid=(6,),
        in_specs=x_specs
        + [
            pl.BlockSpec((1, wide, span), lambda s, p: (jnp.minimum(s, 2), 0, 0)),
            pl.BlockSpec((1, wide, span), lambda s, p: (jnp.maximum(s - 3, 0), 0, 0)),
            pl.BlockSpec((1, 1, depth, wide), lambda s, p: (half(s, p), s % 3, 0, 0)),
            whole_block((span, depth)),
            pl.BlockSpec((span, depth), lambda s, p: (0, 0), pipeline_mode=once),
            whole_block((8, depth)),
            whole_block((8, depth)),
        ],
        out_specs=[
            pl.BlockSpec((1, tok, depth), lambda s, p: (p[0], 0, 0)),
            whole_block((rest, depth)),
            pl.BlockSpec((1, tok, wide), lambda s, p: (p[0], 0, half(s, p))),
            pl.BlockSpec((rest, wide), lambda s, p: (0, half(s, p))),
            whole_block((8, depth)),
            pl.BlockSpec((1, depth, wide), lambda s, p: (jnp.minimum(s, 2), 0, 0)),
            pl.BlockSpec((1, depth, wide), lambda s, p: (jnp.maximum(s - 3, 0), 0, 0)),
        ],
        scratch_shapes=[pltpu.VMEM((depth, span), BF16), pltpu.VMEM((span, depth), F32)],
    )
    return pl.pallas_call(
        functools.partial(tail_kernel, slots, tok),
        out_shape=[
            jax.ShapeDtypeStruct((slots, tok, depth), F32),
            jax.ShapeDtypeStruct((rest, depth), BF16),
            jax.ShapeDtypeStruct((slots, tok, depth), F32),
            jax.ShapeDtypeStruct((rest, depth), BF16),
            jax.ShapeDtypeStruct((8, depth), F32),
            jax.ShapeDtypeStruct((3, depth, wide), BF16),
            jax.ShapeDtypeStruct((3, depth, wide), BF16),
        ],
        grid_spec=grid_spec,
        compiler_params=parameters(60),
        cost_estimate=pl.CostEstimate(
            flops=12 * span * depth * depth,
            bytes_accessed=24 * span * depth + 12 * depth * depth,
            transcendentals=0,
        ),
        name="tail",
    )(
        place, inputs, *received, back_other, back_own, full, normed, grad_middle, gains, mlp_gain
    )


def land_kernel(place, whole_ref, part_ref, out_ref):
    out_ref[0] = part_ref[...].astype(F32)


def land(whole, part, slot):
    _, tok, depth = whole.shape
    tile = min(256, tok)
    grid_spec = pltpu.PrefetchScalarGridSpec(
        num_scalar_prefetch=1,
        grid=(tok // tile,),
        in_specs=[
            pl.BlockSpec(memory_space=pl.ANY),
            pl.BlockSpec((tile, depth), lambda s, p: (s, 0)),
        ],
        out_specs=pl.BlockSpec((1, tile, depth), lambda s, p: (p[0], s, 0)),
    )
    return pl.pallas_call(
        land_kernel,
        out_shape=jax.ShapeDtypeStruct(whole.shape, F32),
        grid_spec=grid_spec,
        input_output_aliases={1: 0},
        compiler_params=parameters(16),
        cost_estimate=pl.CostEstimate(
            flops=tok * depth, bytes_accessed=6 * tok * depth, transcendentals=0
        ),
        name="land",
    )(slot, whole, part)


MESH = pl.DeviceIdType.MESH


def seats():
    shard = lax.axis_index("fsdp")
    seat = lax.axis_index("seq")
    return (shard // 2, shard % 2, seat // 2, seat % 2)


def meet(line, keys):
    shard = lax.axis_index("fsdp")
    seat = lax.axis_index("seq")
    partners = []
    if "z" in keys:
        partners += [{"fsdp": lax.rem(shard + 2 * jump, 2 * line)} for jump in range(1, line)]
    if "y" in keys:
        partners.append({"fsdp": shard + 1 - 2 * (shard % 2)})
    if "x" in keys:
        partners.append({"seq": lax.rem(seat + 2, 4)})
    if "core" in keys:
        partners.append({"seq": seat + 1 - 2 * (seat % 2)})
    barrier = pltpu.get_barrier_semaphore()
    for partner in partners:
        pl.semaphore_signal(barrier, inc=1, device_id=partner, device_id_type=MESH)
    pl.semaphore_wait(barrier, len(partners))


def send(source, target, sems, number, partner):
    return pltpu.make_async_remote_copy(
        src_ref=source,
        dst_ref=target,
        send_sem=sems.at[0, number],
        recv_sem=sems.at[1, number],
        device_id=partner,
        device_id_type=MESH,
    )


def to_core_partner():
    seat = lax.axis_index("seq")
    return {"seq": seat + 1 - 2 * (seat % 2)}


def to_x_partner():
    return {"seq": lax.rem(lax.axis_index("seq") + 2, 4)}


def to_y_partner():
    shard = lax.axis_index("fsdp")
    return {"fsdp": shard + 1 - 2 * (shard % 2)}


def to_z_partner(line, jump):
    return {"fsdp": lax.rem(lax.axis_index("fsdp") + 2 * jump, 2 * line)}


class Gather:
    def __init__(self, line, shard, own, other, sems, split=False):
        self.line, self.shard, self.own, self.other = line, shard, own, other
        self.sems = sems
        z, y, x, _ = seats()
        self.z, self.y = z, y
        rows = own.shape[2]
        if split:
            self.rows = pl.ds(pl.multiple_of(x * (rows // 2), rows // 2), rows // 2)
        else:
            self.rows = pl.ds(0, rows)

    def here(self):
        return pltpu.make_async_copy(
            self.shard.at[self.rows, :],
            self.own.at[self.z, self.y, self.rows, :],
            self.sems.at[0, self.line + 2],
        )

    def along_z(self):
        return [
            send(
                self.shard.at[self.rows, :],
                self.own.at[self.z, self.y, self.rows, :],
                self.sems,
                jump - 1,
                to_z_partner(self.line, jump),
            )
            for jump in range(1, self.line)
        ]

    def along_y(self):
        part = self.own.at[:, self.y, self.rows, :]
        return send(part, part, self.sems, self.line - 1, to_y_partner())

    def along_x(self):
        part = self.own.at[:, :, self.rows, :]
        return send(part, part, self.sems, self.line, to_x_partner())

    def along_core(self):
        return send(self.own, self.other, self.sems, self.line + 1, to_core_partner())

    def start_z(self):
        self.here().start()
        for copy in self.along_z():
            copy.start()

    def wait_z(self):
        self.here().wait()
        for copy in self.along_z():
            copy.wait()


def gather_sems(line):
    return pltpu.SemaphoreType.DMA((2, line + 3))


def front_kernel(line, tok, *refs):
    (
        inputs,
        firsts,
        q_shard,
        k_shard,
        v_shard,
        o_shard,
        d_shard,
        cos_ref,
        sin_ref,
        x_received,
        f_received,
        heads_own,
        heads_received,
        normed_ref,
        full_ref,
        gains_ref,
        o_own,
        o_other,
        d_own,
        xs,
        fs,
        q_own,
        q_other,
        k_own,
        k_other,
        v_own,
        v_other,
        outgoing,
        q_sems,
        k_sems,
        v_sems,
        o_sems,
        d_sems,
        swap_sems,
        head_sems,
        local_sems,
    ) = refs
    step = pl.program_id(0)
    _, _, side, core = seats()
    wide = outgoing.shape[1]
    depth = 2 * wide
    gathers = [
        Gather(line, q_shard, q_own, q_other, q_sems),
        Gather(line, k_shard, k_own, k_other, k_sems),
        Gather(line, v_shard, v_own, v_other, v_sems),
    ]
    query, key, value = gathers
    out = Gather(line, o_shard, o_own, o_other, o_sems)
    down = Gather(line, d_shard, d_own, d_own, d_sems, split=True)
    swap_x = send(inputs.at[1 - side], x_received, swap_sems, 0, to_x_partner())
    swap_f = send(firsts.at[1 - side], f_received, swap_sems, 1, to_x_partner())
    load_x = pltpu.make_async_copy(inputs.at[side], xs.at[pl.ds(0, tok), :], local_sems.at[0])
    load_f = pltpu.make_async_copy(firsts.at[side], fs.at[pl.ds(0, tok), :], local_sems.at[1])
    more_x = pltpu.make_async_copy(x_received, xs.at[pl.ds(tok, tok), :], local_sems.at[2])
    more_f = pltpu.make_async_copy(f_received, fs.at[pl.ds(tok, tok), :], local_sems.at[3])

    def weight(halves, columns):
        return halves[:, :, :, columns].reshape(depth, wide)

    def heads(number):
        return send(
            outgoing.at[number], heads_received.at[number], head_sems, number, to_core_partner()
        )

    saves = []
    for number, (mine, others) in enumerate(((q_own, q_other), (k_own, k_other), (v_own, v_other))):
        for which, ref in ((0, mine), (1, others)):
            half = core if which == 0 else 1 - core
            saves.append(
                pltpu.make_async_copy(
                    ref.at[:, :, :, pl.ds(0, wide)],
                    full_ref.at[half, number],
                    local_sems.at[4 + 2 * number + which],
                )
            )

    @pl.when(step == 0)
    def _():
        meet(line, ("z", "y", "x", "core"))
        swap_x.start()
        load_x.start()
        load_f.start()
        query.start_z()
        query.wait_z()
        query.along_y().start()
        key.start_z()
        key.wait_z()
        key.along_y().start()
        value.start_z()
        query.along_y().wait()
        query.along_core().start()
        swap_x.wait()
        more_x.start()
        swap_f.start()
        value.wait_z()
        value.along_y().start()
        out.start_z()
        key.along_y().wait()
        key.along_core().start()
        load_x.wait()
        more_x.wait()
        value.along_y().wait()
        value.along_core().start()
        columns = v_own[:, :, :, wide:].reshape(depth, 128)
        gains_ref[...] = columns.astype(F32).T[:8]
        gain = gains_ref[0:1, :]
        chunk = min(256, 2 * tok)

        def norm(number, _):
            at = pl.ds(pl.multiple_of(number * chunk, chunk), chunk)
            values = xs[at, :].astype(F32)
            scale = lax.rsqrt(jnp.mean(values * values, axis=1, keepdims=True) + epsilon)
            normed_ref[at, :] = (values * scale * gain).astype(BF16)
            return 0

        lax.fori_loop(0, 2 * tok // chunk, norm, 0)

    @pl.when(step == 2)
    def _():
        out.wait_z()
        out.along_y().start()
        down.start_z()
        swap_f.wait()
        more_f.start()
        load_f.wait()
        more_f.wait()

    @pl.when(step == 3)
    def _():
        query.along_core().wait()
        key.along_core().wait()
        value.along_core().wait()
        for save in saves:
            save.start()

    @pl.when(step == 5)
    def _():
        out.along_y().wait()
        out.along_core().start()

    def project_one(halves, kind, mine):
        raw = nt(weight(halves, slice(0, wide)).T, normed_ref[...])
        if kind < 2:
            parts = raw.reshape(wide // HEAD_DIM, 2, HALF, raw.shape[1])
            first, second = parts[:, 0], parts[:, 1]
            cosine, sine = cos_ref[...][None], sin_ref[...][None]
            turned = jnp.stack(
                [first * cosine - second * sine, first * sine + second * cosine], axis=1
            )
            result = turned.reshape(raw.shape).astype(BF16)
        else:
            half = core if mine else 1 - core
            first = fs[:, pl.ds(pl.multiple_of(half * wide, wide), wide)]
            result = (0.5 * raw + 0.5 * first.astype(F32).T).astype(BF16)
        if mine:
            heads_own[0] = result
        else:
            outgoing[kind] = result
            heads(kind).start()

    for number, (halves, kind, mine) in enumerate(
        (
            (q_own, 0, True),
            (k_own, 1, True),
            (v_own, 2, True),
            (q_other, 0, False),
            (k_other, 1, False),
            (v_other, 2, False),
        )
    ):

        @pl.when(step == number)
        def _(halves=halves, kind=kind, mine=mine):
            project_one(halves, kind, mine)

    @pl.when(step == 5)
    def _():
        for number in range(3):
            heads(number).wait()
        for save in saves:
            save.wait()
        out.along_core().wait()
        down.wait_z()


def front(inputs, firsts, q, k, v, o, d, cosine, sine, line):
    slots, tok, depth = inputs.shape
    span = slots * tok
    wide = depth // 2
    rows, down_rows = q.shape[0], d.shape[0]
    anywhere = pl.BlockSpec(memory_space=pl.ANY)
    weights = lambda columns: pltpu.VMEM((line, 2, rows, columns), BF16)
    return pl.pallas_call(
        functools.partial(front_kernel, line, tok),
        grid=(6,),
        in_specs=[anywhere] * 7 + [whole_block((HALF, span))] * 2,
        out_specs=[
            anywhere,
            anywhere,
            pl.BlockSpec((1, wide, span), lambda s: (jnp.minimum(s, 2), 0, 0)),
            anywhere,
            whole_block((span, depth)),
            anywhere,
            whole_block((8, depth)),
            anywhere,
            anywhere,
            anywhere,
        ],
        out_shape=[
            jax.ShapeDtypeStruct((tok, depth), BF16),
            jax.ShapeDtypeStruct((tok, depth), BF16),
            jax.ShapeDtypeStruct((3, wide, span), BF16),
            jax.ShapeDtypeStruct((3, wide, span), BF16),
            jax.ShapeDtypeStruct((span, depth), BF16),
            jax.ShapeDtypeStruct((2, 3, line, 2, rows, wide), BF16),
            jax.ShapeDtypeStruct((8, depth), F32),
            jax.ShapeDtypeStruct((line, 2, rows, wide), BF16),
            jax.ShapeDtypeStruct((line, 2, rows, wide), BF16),
            jax.ShapeDtypeStruct((line, 2, down_rows, wide), BF16),
        ],
        scratch_shapes=[
            pltpu.VMEM((span, depth), BF16),
            pltpu.VMEM((span, depth), BF16),
            weights(wide),
            weights(wide),
            weights(wide),
            weights(wide),
            weights(v.shape[1]),
            weights(v.shape[1]),
            pltpu.VMEM((3, wide, span), BF16),
        ]
        + [gather_sems(line)] * 5
        + [
            pltpu.SemaphoreType.DMA((2, 2)),
            pltpu.SemaphoreType.DMA((2, 3)),
            pltpu.SemaphoreType.DMA((10,)),
        ],
        compiler_params=pltpu.CompilerParams(
            dimension_semantics=("arbitrary",),
            vmem_limit_bytes=56 * MIB,
            collective_id=1,
            has_side_effects=True,
        ),
        cost_estimate=pl.CostEstimate(
            flops=6 * span * depth * depth,
            bytes_accessed=2 * (8 * span * depth + 6 * depth * depth),
            transcendentals=0,
        ),
        name="front",
    )(inputs, firsts, q, k, v, o, d, cosine, sine)


def block_of(source, slot, tok):
    _, _, side, core = seats()
    rank = 1 - core if source == 0 else core
    group = lax.rem(side + slot, 2)
    return pl.ds(pl.multiple_of((group * 2 + rank) * tok, tok), tok)


def attend_carry_kernel(line, tok, tile_k, *refs):
    (
        received,
        own,
        grad_in,
        d_in,
        g_shard,
        u_shard,
        mix_received,
        mix_own,
        lse_ref,
        att_other,
        grad_received,
        d_own,
        d_other,
        g_own,
        g_other,
        u_own,
        u_other,
        qz,
        kn,
        vt,
        ot,
        outgoing,
        d_sems,
        g_sems,
        u_sems,
        swap_sems,
        att_sems,
    ) = refs
    step = pl.program_id(0)
    pairs = pl.num_programs(0)
    _, _, side, _ = seats()
    down = Gather(line, d_in, d_own, d_other, d_sems, split=True)
    gate = Gather(line, g_shard, g_own, g_other, g_sems, split=True)
    up = Gather(line, u_shard, u_own, u_other, u_sems)
    swap = send(grad_in.at[1 - side], grad_received, swap_sems, 0, to_x_partner())
    pieces = (received, own)

    def hand_over(number):
        rows = pl.ds(number * PAIR, PAIR)
        return send(
            outgoing.at[rows, :], att_other.at[rows, :], att_sems, number, to_core_partner()
        )

    @pl.when(step == 0)
    def _():
        meet(line, ("z", "y", "x", "core"))
        down.along_y().start()
        gate.start_z()
        swap.start()

    @pl.when(step == 2)
    def _():
        gate.wait_z()
        gate.along_y().start()
        up.start_z()

    @pl.when(step == 3)
    def _():
        down.along_y().wait()
        down.along_x().start()

    for source in range(2):
        for slot in range(2):
            cols = block_of(source, slot, tok)
            take = slice(slot * tok, (slot + 1) * tok)
            query = pieces[source][0, :, take] * jnp.asarray(HEAD_DIM**-0.5, BF16)
            for head in range(2):
                qz[head, :, cols] = head_rows(query, head)
            kn[cols, :] = pieces[source][1, :, take].T
            vt[:, cols] = pieces[source][2, :, take]
    attend_body(4 * tok, tile_k, qz, kn, vt, ot, lse_ref)
    for slot in range(2):
        take = slice(slot * tok, (slot + 1) * tok)
        theirs = ot[:, block_of(0, slot, tok)]
        mix_received[:, take] = theirs
        for number in range(4):

            @pl.when(step == number)
            def _(number=number, theirs=theirs, take=take):
                outgoing[number * PAIR : (number + 1) * PAIR, take] = theirs

        mix_own[:, take] = ot[:, block_of(1, slot, tok)]
    for number in range(4):

        @pl.when(step == number)
        def _(number=number):
            hand_over(number).start()

    @pl.when(step == pairs - 1)
    def _():
        gate.along_y().wait()
        up.wait_z()
        up.along_y().start()
        down.along_x().wait()
        swap.wait()
        gate.along_x().start()
        down.along_core().start()
        up.along_y().wait()
        up.along_core().start()
        gate.along_x().wait()
        gate.along_core().start()
        for number in range(4):
            hand_over(number).wait()
        down.along_core().wait()
        up.along_core().wait()
        gate.along_core().wait()


def attend_carry(received, own, grads, d_own, gate, up, line):
    _, width, span = own.shape
    tok = span // 2
    length = 2 * span
    pairs = width // PAIR
    rows, down_rows = gate.shape[0], d_own.shape[2]
    depth = grads.shape[2]
    anywhere = pl.BlockSpec(memory_space=pl.ANY)
    triple = pl.BlockSpec((3, PAIR, span), lambda p: (0, p, 0))
    single = pl.BlockSpec((PAIR, span), lambda p: (p, 0))
    whole_gate = jax.ShapeDtypeStruct((line, 2, rows, gate.shape[1]), BF16)
    whole_down = jax.ShapeDtypeStruct((line, 2, down_rows, d_own.shape[3]), BF16)
    area = pairs * 2 * length * length // 2
    return pl.pallas_call(
        functools.partial(attend_carry_kernel, line, tok, min(256, length)),
        grid=(pairs,),
        in_specs=[triple, triple] + [anywhere] * 4,
        out_specs=[single, single, pl.BlockSpec((1, 8, length), lambda p: (p, 0, 0))]
        + [anywhere] * 8,
        out_shape=[
            jax.ShapeDtypeStruct((width, span), BF16),
            jax.ShapeDtypeStruct((width, span), BF16),
            jax.ShapeDtypeStruct((pairs, 8, length), F32),
            jax.ShapeDtypeStruct((width, span), BF16),
            jax.ShapeDtypeStruct((tok, depth), BF16),
            whole_down,
            whole_down,
            whole_gate,
            whole_gate,
            whole_gate,
            whole_gate,
        ],
        scratch_shapes=[
            pltpu.VMEM((2, PAIR, length), BF16),
            pltpu.VMEM((length, PAIR), BF16),
            pltpu.VMEM((PAIR, length), BF16),
            pltpu.VMEM((PAIR, length), BF16),
            pltpu.VMEM((width, span), BF16),
        ]
        + [gather_sems(line)] * 3
        + [pltpu.SemaphoreType.DMA((2, 1)), pltpu.SemaphoreType.DMA((2, 4))],
        input_output_aliases={3: 5},
        compiler_params=pltpu.CompilerParams(
            dimension_semantics=("arbitrary",),
            vmem_limit_bytes=48 * MIB,
            collective_id=2,
            has_side_effects=True,
        ),
        cost_estimate=pl.CostEstimate(
            flops=area * 1024, bytes_accessed=8 * width * length, transcendentals=area
        ),
        name="attend_carry",
    )(received, own, grads, d_own, gate, up)


def mlp_carry_kernel(line, tok, blocks, *refs):
    (
        grads,
        grads_received,
        middle_ref,
        normed_ref,
        gains_ref,
        g_own,
        g_other,
        u_own,
        u_other,
        d_own_own,
        d_own_other,
        d_other_own,
        d_other_other,
        out_ref,
        send_ref,
        grad_ref,
        low_ref,
        gain_ref,
        gu_ref,
        d_ref,
        gu_y,
        og,
        normed_t,
        acc,
        back,
        gu_kept,
        d_kept,
        gu_sent,
        d_sent,
        gu_landed,
        d_landed,
        gu_outgoing,
        down_full,
        local_sems,
        gu_sends,
        gu_recvs,
        d_sends,
        d_recvs,
        y_sems,
    ) = refs
    step = pl.program_id(0)
    _, y, side, core = seats()
    depth = og.shape[1]
    wide = depth // 2
    strip = 128
    rows = gu_kept.shape[4]
    mine = pl.ds(pl.multiple_of(core * wide, wide), wide)
    others = pl.ds(pl.multiple_of((1 - core) * wide, wide), wide)

    def core_copies(number):
        slot = lax.rem(number, 2)
        return [
            pltpu.make_async_remote_copy(
                src_ref=source.at[slot],
                dst_ref=target.at[number],
                send_sem=sends.at[slot],
                recv_sem=recvs.at[number],
                device_id=to_core_partner(),
                device_id_type=MESH,
            )
            for source, target, sends, recvs in (
                (gu_sent, gu_landed, gu_sends, gu_recvs),
                (d_sent, d_landed, d_sends, d_recvs),
            )
        ]

    def y_copy(number):
        columns = pl.ds(pl.multiple_of(number * strip, strip), strip)
        return send(
            gu_outgoing.at[number], gu_y.at[:, :, :, columns], y_sems, number, to_y_partner()
        )

    @pl.when(step == 0)
    def _():
        meet(line, ("y", "core"))
        loads = [
            pltpu.make_async_copy(grads.at[side], og.at[pl.ds(0, tok), :], local_sems.at[0]),
            pltpu.make_async_copy(grads_received, og.at[pl.ds(tok, tok), :], local_sems.at[1]),
        ]
        for load in loads:
            load.start()
        normed_t[...] = normed_ref[...].T
        acc[...] = jnp.zeros_like(acc)
        back[...] = jnp.zeros_like(back)
        for load in loads:
            load.wait()

    @pl.when(step < blocks)
    def _():
        slot = lax.rem(step, 2)
        gate_w = jnp.concatenate([g_own[...], g_other[...]], axis=1)
        up_w = jnp.concatenate([u_own[...], u_other[...]], axis=1)
        for number, pair in enumerate(
            ((d_own_own, d_own_other), (d_other_own, d_other_other))
        ):
            at = pl.ds(number * strip, strip)
            down_full[at, mine] = pair[0][...]
            down_full[at, others] = pair[1][...]
        down_w = down_full[...]
        normed = normed_ref[...]
        gate = dot(normed, gate_w)
        up = dot(normed, up_w)
        grad_active = nt(og[...], down_w)
        sigma = jax.nn.sigmoid(gate)
        silu = gate * sigma
        active = (silu * up).astype(BF16)
        grad_up = (grad_active * silu).astype(BF16)
        grad_gate = (grad_active * up * sigma * (1.0 + gate * (1.0 - sigma))).astype(BF16)

        @pl.when(step >= 2)
        def _():
            for copy in core_copies(step - 2):
                copy.wait_send()

        for number, grad in enumerate((grad_gate, grad_up)):
            result = dot(normed_t[...], grad).astype(BF16)
            shaped = result.reshape(line, 2, rows, 2 * strip)
            gu_kept[slot, number] = shaped[..., :strip]
            gu_sent[slot, number] = shaped[..., strip:]
        active_t = active.T
        kept = dot(active_t, og[:, mine]).astype(BF16)
        d_kept[slot, core] = kept[:strip]
        d_kept[slot, 1 - core] = kept[strip:]
        sent = dot(active_t, og[:, others]).astype(BF16)
        d_sent[slot, core] = sent[:strip]
        d_sent[slot, 1 - core] = sent[strip:]
        for copy in core_copies(step):
            copy.start()
        acc[...] += dot(active, down_w)
        back[...] += nt(grad_gate, gate_w) + nt(grad_up, up_w)

    @pl.when(step > 0)
    def _():
        number = step - 1
        slot = lax.rem(number, 2)
        for copy in core_copies(number):
            copy.wait_recv()
        for which in range(2):
            theirs = gu_kept[slot, which, :, 1 - y].astype(F32)
            theirs = theirs + gu_landed[number, which, :, 1 - y].astype(F32)
            gu_outgoing[number, which] = theirs.astype(BF16)
            ours = gu_kept[slot, which, :, y].astype(F32)
            ours = ours + gu_landed[number, which, :, y].astype(F32)
            gu_ref[which] = ours.astype(BF16)
        y_copy(number).start()
        d_ref[...] = (d_kept[slot].astype(F32) + d_landed[number].astype(F32)).astype(BF16)

    @pl.when(step == blocks)
    def _():
        gain = gains_ref[1:2, :]
        chunk = min(128, tok)
        gain_ref[...] = jnp.zeros_like(gain_ref)
        for slot in range(2):

            def finish(number, _, slot=slot):
                local = pl.ds(pl.multiple_of(number * chunk, chunk), chunk)
                some = pl.ds(pl.multiple_of(slot * tok + number * chunk, chunk), chunk)
                middle = middle_ref[some, :]
                scale = lax.rsqrt(jnp.mean(middle * middle, axis=1, keepdims=True) + epsilon)
                result = middle + acc[some, :]
                if slot == 0:
                    out_ref[0, local, :] = result
                else:
                    send_ref[local, :] = result.astype(BF16)
                grad = back[some, :]
                gain_ref[0:1, :] += jnp.sum(grad * middle * scale, axis=0, keepdims=True)
                weighted = grad * gain
                inner = jnp.mean(weighted * middle, axis=1, keepdims=True)
                grad_middle = (
                    scale * weighted
                    - middle * (scale * scale * scale) * inner
                    + og[some, :].astype(F32)
                )
                grad_ref[some, :] = grad_middle
                low_ref[some, :] = grad_middle.astype(BF16)
                return 0

            lax.fori_loop(0, tok // chunk, finish, 0)
        for number in (blocks - 2, blocks - 1):
            for copy in core_copies(number):
                copy.wait_send()
        for number in range(blocks):
            y_copy(number).wait()


def mlp_carry(grads, grads_received, middle, normed, gains, gate, up, down, line):
    slots, tok, depth = grads.shape
    half_width = gate[0].shape[1]
    wide = depth // 2
    span = slots * tok
    blocks = half_width // 128
    rows = depth // (2 * line)
    once = pl.Buffered(1)
    anywhere = pl.BlockSpec(memory_space=pl.ANY)

    def now(s):
        return jnp.minimum(s, blocks - 1)

    def done(s):
        return jnp.maximum(s - 1, 0)

    def core():
        return lax.axis_index("seq") % 2

    column = pl.BlockSpec((depth, 128), lambda s: (0, now(s)))
    own_rows = pl.BlockSpec((128, wide), lambda s: (core() * blocks + now(s), 0))
    other_rows = pl.BlockSpec((128, wide), lambda s: ((1 - core()) * blocks + now(s), 0))
    full = pl.BlockSpec((span, depth), lambda s: (0, 0), pipeline_mode=once)
    return pl.pallas_call(
        functools.partial(mlp_carry_kernel, line, tok, blocks),
        grid=(blocks + 1,),
        in_specs=[anywhere, anywhere, full, full, whole_block((8, depth))]
        + [column] * 4
        + [own_rows, own_rows, other_rows, other_rows],
        out_specs=[
            pl.BlockSpec(
                (1, tok, depth), lambda s: (lax.axis_index("seq") // 2, 0, 0), pipeline_mode=once
            ),
            pl.BlockSpec((tok, depth), lambda s: (0, 0), pipeline_mode=once),
            full,
            full,
            whole_block((8, depth)),
            pl.BlockSpec((2, line, rows, 128), lambda s: (0, 0, 0, done(s))),
            pl.BlockSpec((2, 128, wide), lambda s: (0, done(s), 0)),
            anywhere,
        ],
        out_shape=[
            jax.ShapeDtypeStruct((slots, tok, depth), F32),
            jax.ShapeDtypeStruct((tok, depth), BF16),
            jax.ShapeDtypeStruct((span, depth), F32),
            jax.ShapeDtypeStruct((span, depth), BF16),
            jax.ShapeDtypeStruct((8, depth), F32),
            jax.ShapeDtypeStruct((2, line, rows, half_width), BF16),
            jax.ShapeDtypeStruct((2, half_width, wide), BF16),
            jax.ShapeDtypeStruct((2, line, rows, half_width), BF16),
        ],
        scratch_shapes=[
            pltpu.VMEM((span, depth), BF16),
            pltpu.VMEM((depth, span), BF16),
            pltpu.VMEM((span, depth), F32),
            pltpu.VMEM((span, depth), F32),
            pltpu.VMEM((2, 2, line, 2, rows, 128), BF16),
            pltpu.VMEM((2, 2, 128, wide), BF16),
            pltpu.VMEM((2, 2, line, 2, rows, 128), BF16),
            pltpu.VMEM((2, 2, 128, wide), BF16),
            pltpu.VMEM((blocks, 2, line, 2, rows, 128), BF16),
            pltpu.VMEM((blocks, 2, 128, wide), BF16),
            pltpu.VMEM((blocks, 2, line, rows, 128), BF16),
            pltpu.VMEM((256, depth), BF16),
            pltpu.SemaphoreType.DMA((2,)),
            pltpu.SemaphoreType.DMA((2,)),
            pltpu.SemaphoreType.DMA((blocks,)),
            pltpu.SemaphoreType.DMA((2,)),
            pltpu.SemaphoreType.DMA((blocks,)),
            pltpu.SemaphoreType.DMA((2, blocks)),
        ],
        compiler_params=pltpu.CompilerParams(
            dimension_semantics=("arbitrary",),
            vmem_limit_bytes=63 * MIB,
            collective_id=3,
            has_side_effects=True,
        ),
        cost_estimate=pl.CostEstimate(
            flops=16 * span * depth * 2 * half_width,
            bytes_accessed=24 * depth * half_width + 20 * span * depth,
            transcendentals=2 * span * half_width,
        ),
        name="mlp_carry",
    )(
        grads,
        grads_received,
        middle,
        normed,
        gains,
        *gate,
        *up,
        down[0],
        down[1],
        down[0],
        down[1],
    )


def grad_attended_carry_kernel(
    line,
    low_ref,
    full_ref,
    att_other,
    att_own,
    ga_own,
    ga_received,
    o_ref,
    o_landed,
    outgoing,
    o_sent,
    sems,
):
    step = pl.program_id(0)
    _, _, _, core = seats()
    wide = att_own.shape[0]
    mine = pl.ds(pl.multiple_of(core * wide, wide), wide)
    others = pl.ds(pl.multiple_of((1 - core) * wide, wide), wide)
    heads = send(outgoing, ga_received, sems, 0, to_core_partner())

    def sums(number):
        half = 1 - core if number == 0 else core
        at = pl.ds(pl.multiple_of(half * wide, wide), wide)
        return send(o_sent.at[number], o_landed.at[at, :], sems, 1 + number, to_core_partner())

    @pl.when(step == 0)
    def _():
        meet(line, ("core",))
        outgoing[...] = nt(full_ref[...], low_ref[...]).astype(BF16)
        heads.start()

    @pl.when(step == 1)
    def _():
        ga_own[...] = nt(full_ref[...], low_ref[...]).astype(BF16)

    for number, att in enumerate((att_other, att_own)):

        @pl.when(step == number)
        def _(number=number, att=att):
            o_sent[number] = dot(att[...], low_ref[:, others]).astype(BF16)
            sums(number).start()
            o_ref[...] = dot(att[...], low_ref[:, mine]).astype(BF16)

    @pl.when(step == 1)
    def _():
        heads.wait()
        for number in range(2):
            sums(number).wait()


def grad_attended_carry(low, full, att_other, att_own, line):
    span, depth = low.shape
    wide = depth // 2

    def half(s):
        core = lax.axis_index("seq") % 2
        return jnp.where(s == 0, 1 - core, core)

    anywhere = pl.BlockSpec(memory_space=pl.ANY)
    return pl.pallas_call(
        functools.partial(grad_attended_carry_kernel, line),
        grid=(2,),
        in_specs=[
            whole_block((span, depth)),
            pl.BlockSpec((wide, depth), lambda s: (half(s), 0)),
            whole_block((wide, span)),
            whole_block((wide, span)),
        ],
        out_specs=[
            whole_block((wide, span)),
            anywhere,
            pl.BlockSpec((wide, wide), lambda s: (half(s), 0)),
            anywhere,
        ],
        out_shape=[
            jax.ShapeDtypeStruct((wide, span), BF16),
            jax.ShapeDtypeStruct((wide, span), BF16),
            jax.ShapeDtypeStruct((depth, wide), BF16),
            jax.ShapeDtypeStruct((depth, wide), BF16),
        ],
        scratch_shapes=[
            pltpu.VMEM((wide, span), BF16),
            pltpu.VMEM((2, wide, wide), BF16),
            pltpu.SemaphoreType.DMA((2, 3)),
        ],
        compiler_params=pltpu.CompilerParams(
            dimension_semantics=("arbitrary",),
            vmem_limit_bytes=48 * MIB,
            collective_id=4,
            has_side_effects=True,
        ),
        cost_estimate=pl.CostEstimate(
            flops=4 * span * depth * depth,
            bytes_accessed=6 * span * depth + 4 * depth * depth,
            transcendentals=0,
        ),
        name="grad_attended_carry",
    )(low, full, att_other, att_own)


def attend_back_carry_kernel(line, tok, tile_q, tile_k, *refs):
    (
        received,
        own,
        mix_received,
        mix_own,
        grad_received,
        grad_own,
        lse_ref,
        cos_ref,
        sin_ref,
        outputs_sent,
        gu_in,
        gu_y,
        d_in,
        o_in,
        o_landed,
        back_own,
        back_other,
        outputs_received,
        gu_mine,
        gu_z,
        d_y,
        o_kept,
        o_y,
    ) = refs[:23]
    (
        qz,
        gz,
        qn,
        gn,
        kn,
        vn,
        kt,
        inner,
        dq,
        dk,
        dv,
        outgoing,
        gu_a,
        gu_b,
        o_a,
        o_b,
        local_sems,
        back_sems,
        z_sems,
        other_sems,
    ) = refs[23:]
    step = pl.program_id(0)
    pairs = pl.num_programs(0)
    z, y, _, _ = seats()
    length = 4 * tok
    swap = send(outputs_sent, outputs_received, other_sems, 0, to_x_partner())
    d_send = send(d_in.at[:, 1 - y], d_y, other_sems, 1, to_y_partner())
    o_send = send(o_a.at[:, 1 - y], o_y, other_sems, 2, to_y_partner())

    def z_send(jump):
        target = lax.rem(z + jump, line)
        return send(
            gu_a.at[:, target], gu_z.at[jump - 1], z_sems, jump - 1, to_z_partner(line, jump)
        )

    stays = [
        pltpu.make_async_copy(gu_a.at[:, z], gu_mine, local_sems.at[4]),
        pltpu.make_async_copy(o_a.at[:, y], o_kept, local_sems.at[5]),
    ]

    def hand_over(number):
        rows = pl.ds(number * PAIR, PAIR)
        return send(
            outgoing.at[:, rows, :],
            back_other.at[:, rows, :],
            back_sems,
            number,
            to_core_partner(),
        )

    @pl.when(step == 0)
    def _():
        meet(line, ("z", "y", "x", "core"))
        swap.start()
        loads = [
            pltpu.make_async_copy(source, target, local_sems.at[number])
            for number, (source, target) in enumerate(
                ((o_in, o_a), (o_landed, o_b), (gu_in, gu_a), (gu_y, gu_b))
            )
        ]
        for load in loads:
            load.start()
        loads[0].wait()
        loads[1].wait()
        o_a[...] = (o_a[...].astype(F32) + o_b[...].astype(F32)).astype(BF16)
        o_send.start()
        d_send.start()
        loads[2].wait()
        loads[3].wait()

        def add(number, _):
            which, index = number // line, lax.rem(number, line)
            total = gu_a[which, index].astype(F32) + gu_b[which, index].astype(F32)
            gu_a[which, index] = total.astype(BF16)
            return 0

        lax.fori_loop(0, 2 * line, add, 0)
        for jump in range(1, line):
            z_send(jump).start()
        for copy in stays:
            copy.start()

    attend_back_body(
        (received, own),
        (mix_received, mix_own),
        (grad_received, grad_own),
        lambda source, slot: block_of(source, slot, tok),
        tok,
        length,
        tile_q,
        tile_k,
        lse_ref,
        qz,
        gz,
        qn,
        gn,
        kn,
        vn,
        kt,
        inner,
        dq,
        dk,
        dv,
    )
    for slot in range(2):
        take = slice(slot * tok, (slot + 1) * tok)
        for source in range(2):
            cols = block_of(source, slot, tok)
            results = turn_back(dq, dk, dv, cols, cos_ref[:, cols], sin_ref[:, cols])
            for which, result in enumerate(results):
                if source == 1:
                    back_own[which, :, take] = result
                else:
                    at = pl.ds(pl.multiple_of(step * PAIR, PAIR), PAIR)
                    outgoing[which, at, take] = result

    for number in range(4):

        @pl.when(step == number)
        def _(number=number):
            hand_over(number).start()

    @pl.when(step == pairs - 1)
    def _():
        swap.wait()
        d_send.wait()
        o_send.wait()
        for copy in stays:
            copy.wait()
        for jump in range(1, line):
            z_send(jump).wait()
        for number in range(4):
            hand_over(number).wait()


def attend_back_carry(
    pieces, mixes, grads, lse, cosine, sine, outputs_sent, gu, gu_y, d, o, o_landed, line
):
    _, width, span = pieces[0].shape
    tok = span // 2
    length = 2 * span
    pairs = width // PAIR
    tile_q = min(512, length)
    tile_k = min(256, length)
    anywhere = pl.BlockSpec(memory_space=pl.ANY)
    triple = pl.BlockSpec((3, PAIR, span), lambda p: (0, p, 0))
    single = pl.BlockSpec((PAIR, span), lambda p: (p, 0))
    table = pl.BlockSpec((HALF, length), lambda p: (0, 0))
    rows, half_width = gu.shape[2:]
    down_rows, wide = d.shape[2:]
    area = pairs * 2 * length * length // 2
    return pl.pallas_call(
        functools.partial(attend_back_carry_kernel, line, tok, tile_q, tile_k),
        grid=(pairs,),
        in_specs=[triple] * 2
        + [single] * 4
        + [pl.BlockSpec((1, 8, length), lambda p: (p, 0, 0)), table, table]
        + [anywhere] * 6,
        out_specs=[triple] + [anywhere] * 7,
        out_shape=[
            jax.ShapeDtypeStruct((3, width, span), BF16),
            jax.ShapeDtypeStruct((3, width, span), BF16),
            jax.ShapeDtypeStruct(outputs_sent.shape, BF16),
            jax.ShapeDtypeStruct((2, rows, half_width), BF16),
            jax.ShapeDtypeStruct((line - 1, 2, rows, half_width), BF16),
            jax.ShapeDtypeStruct((line, down_rows, wide), BF16),
            jax.ShapeDtypeStruct((line, rows, wide), BF16),
            jax.ShapeDtypeStruct((line, rows, wide), BF16),
        ],
        scratch_shapes=[
            pltpu.VMEM((2, PAIR, length), BF16),
            pltpu.VMEM((2, PAIR, length), BF16),
            pltpu.VMEM((2, length, PAIR), BF16),
            pltpu.VMEM((2, length, PAIR), BF16),
            pltpu.VMEM((length, PAIR), BF16),
            pltpu.VMEM((length, PAIR), BF16),
            pltpu.VMEM((PAIR, length), BF16),
            pltpu.VMEM((8, length), F32),
            pltpu.VMEM((PAIR, length), F32),
            pltpu.VMEM((length, PAIR), F32),
            pltpu.VMEM((length, PAIR), F32),
            pltpu.VMEM((3, width, span), BF16),
            pltpu.VMEM((2, line, rows, half_width), BF16),
            pltpu.VMEM((2, line, rows, half_width), BF16),
            pltpu.VMEM((line, 2, rows, wide), BF16),
            pltpu.VMEM((line, 2, rows, wide), BF16),
            pltpu.SemaphoreType.DMA((6,)),
            pltpu.SemaphoreType.DMA((2, 4)),
            pltpu.SemaphoreType.DMA((2, line - 1)),
            pltpu.SemaphoreType.DMA((2, 3)),
        ],
        compiler_params=pltpu.CompilerParams(
            dimension_semantics=("arbitrary",),
            vmem_limit_bytes=60 * MIB,
            collective_id=5,
            has_side_effects=True,
        ),
        cost_estimate=pl.CostEstimate(
            flops=area * 2560, bytes_accessed=16 * width * length, transcendentals=area
        ),
        name="attend_back_carry",
    )(
        *pieces, *mixes, *grads, lse, cosine, sine, outputs_sent, gu, gu_y, d, o, o_landed
    )


def shards(
    inputs,
    first_values,
    out_grad,
    attn_gain,
    query_weight,
    key_weight,
    value_weight,
    output_weight,
    mlp_gain,
    gate_weight,
    up_weight,
    down_weight,
):
    slots, tok, _ = inputs.shape
    groups = lax.axis_size("seq")
    parts = lax.axis_size("fsdp")
    line = parts // 2
    count = groups // slots
    length = tok * groups
    span = slots * tok
    seat = lax.axis_index("seq")
    shard = lax.axis_index("fsdp")
    side = seat // count
    rank = seat % count
    core = seat % 2
    z, y = shard // 2, shard % 2
    wide = D // 2
    width = D // count

    def along_seq(value, partner):
        return lax.ppermute(value, "seq", [(i, partner(i)) for i in range(groups)])

    def along_fsdp(value, partner):
        return lax.ppermute(value, "fsdp", [(i, partner(i)) for i in range(parts)])

    def to_core(value):
        return along_seq(value, lambda i: i ^ 1)

    def to_y(value):
        return along_fsdp(value, lambda i: i ^ 1)

    def to_z(value, jump):
        return along_fsdp(value, lambda i: (i + 2 * jump) % parts)

    def after(value, *others):
        return lax.optimization_barrier((value,) + others)[0]

    def to_sequence(values):
        taken = []
        for jump in range(1, slots):
            sent = lax.dynamic_index_in_dim(values, (side + jump) % slots, 0, keepdims=False)
            taken.append(along_seq(sent, lambda i: (i + jump * count) % groups))
        return taken

    def to_home(whole, sent):
        for jump in range(1, slots):
            part = sent[(jump - 1) * tok : jump * tok]
            part = along_seq(part, lambda i: (i - jump * count) % groups)
            whole = land(whole, part, ((side + jump) % slots)[None])
        return whole

    def rank_up(i, jump):
        return (i // count) * count + (i % count + jump) % count

    def rank_down(i, jump):
        return (i // count) * count + (i % count - jump) % count

    def halves_to_ranks(other, own, axis):
        if count == 2:
            return [other, own]
        return [
            lax.dynamic_slice_in_dim(
                join(other, own, axis), ((rank + 1 + number) % count) * width, width, axis
            )
            for number in range(count)
        ]

    def join(other, own, axis):
        first = jnp.where(core == 0, own, other)
        second = jnp.where(core == 0, other, own)
        return jnp.concatenate([first, second], axis=axis)

    def ranks_to_halves(pieces, axis):
        if count == 2:
            return pieces
        shape = list(pieces[0].shape)
        shape[axis] = D
        whole = jnp.zeros(shape, pieces[0].dtype)
        for number in range(count):
            whole = lax.dynamic_update_slice_in_dim(
                whole, pieces[number], ((rank + 1 + number) % count) * width, axis
            )
        return [
            lax.dynamic_slice_in_dim(whole, which * wide, wide, axis)
            for which in (1 - core, core)
        ]

    def exchange(pieces):
        received = [
            along_seq(pieces[jump - 1], lambda i: rank_up(i, jump)) for jump in range(1, count)
        ]
        return received + [pieces[count - 1]]

    def exchange_back(pieces):
        received = [
            along_seq(pieces[jump - 1], lambda i: rank_down(i, jump)) for jump in range(1, count)
        ]
        return received + [pieces[count - 1]]

    def split(*weights):
        results = []
        for which in (core, 1 - core):
            columns = []
            for weight in weights:
                size = weight.shape[1] // 2
                columns.append(lax.dynamic_slice_in_dim(weight, which * size, size, 1))
            results.append(columns)
        return results

    def gather_z(half):
        return [half] + [to_z(half, jump) for jump in range(1, line)]

    def gather_rest(along_z, other):
        along_y = [to_y(piece) for piece in along_z]
        own = [piece for pair in zip(along_z, along_y) for piece in pair]
        return (own, [other] + [to_core(piece) for piece in own[1:]])

    numbers = []
    for jump in range(line):
        for flip in range(2):
            numbers.append(((z - jump) % line) * 2 + (y ^ flip))
    place = jnp.stack([side, core] + numbers).astype(jnp.int32)

    def low(value):
        return value.astype(BF16)

    def add(a, b):
        return low(a.astype(F32) + b.astype(F32))

    def pick(value, index, axis):
        return lax.dynamic_index_in_dim(value, index, axis, keepdims=False)

    def along_x_and_core(total):
        mine = low(total)
        for jump in range(1, groups // 2):
            total = total + along_seq(mine, lambda i: (i + 2 * jump) % groups).astype(F32)
        mine = low(total)
        return (mine, to_core(mine))

    def along_z_and_on(partial):
        total = partial(z)
        for jump in range(1, line):
            total = total + to_z(low(partial((z + jump) % line)), jump).astype(F32)
        return along_x_and_core(total)

    def scatter(sent, kept, rows_axis):
        shape = kept.shape
        rows = shape[rows_axis] // parts
        cut = shape[:rows_axis] + (line, 2, rows) + shape[rows_axis + 1 :]
        received = to_core(sent).reshape(cut)
        kept = kept.reshape(cut)
        axis = rows_axis + 1
        received_y = to_y(add(pick(kept, 1 - y, axis), pick(received, 1 - y, axis)))
        kept_y = pick(kept, y, axis), pick(received, y, axis)

        def partial(index):
            total = pick(kept_y[0], index, rows_axis).astype(F32)
            total = total + pick(kept_y[1], index, rows_axis).astype(F32)
            return total + pick(received_y, index, rows_axis).astype(F32)

        return along_z_and_on(partial)

    def columns(mine, others):
        first = jnp.where(core == 0, mine, others)
        second = jnp.where(core == 0, others, mine)
        return jnp.concatenate([first, second], axis=-1).astype(F32)

    def everywhere(value):
        value = value + to_core(value)
        value = value + to_y(value)
        total = value
        for jump in range(1, line):
            total = total + to_z(value, jump)
        value = total
        for jump in range(1, groups // 2):
            total = total + along_seq(value, lambda i: (i + 2 * jump) % groups)
        return total

    steps = jnp.arange(slots, dtype=jnp.int32)
    starts = ((side - steps) % slots) * (count * tok) + rank * tok
    positions = (starts[:, None] + jnp.arange(tok, dtype=jnp.int32)[None]).reshape(span)
    freqs = rope_base ** (-(jnp.arange(HALF, dtype=F32) * 2.0 / HEAD_DIM))

    def tables(positions):
        angles = freqs[:, None] * positions.astype(F32)[None, :]
        return (jnp.cos(angles), jnp.sin(angles))

    cosine, sine = tables(positions)
    full_cos, full_sin = tables(jnp.arange(length, dtype=jnp.int32))
    sources = jnp.concatenate(
        [(rank - 1 - jnp.arange(count - 1, dtype=jnp.int32)) % count, rank[None]]
    ).astype(jnp.int32)
    order = (((side - steps) % slots)[None, :] * count + sources[:, None]).reshape(-1)
    order = order.astype(jnp.int32)

    gains = jnp.pad(jnp.stack([attn_gain, mlp_gain], axis=1), ((0, 0), (0, 126)))
    gate_halves, up_halves, out_halves, down_halves = (
        [half[0] for half in split(weight)]
        for weight in (gate_weight, up_weight, output_weight, down_weight)
    )

    if (slots, count) == (2, 2):
        parts_of = lambda ref: [ref.reshape(-1, ref.shape[-1])]
        (q_half,), (k_half,), (v_half,) = (
            split(weight)[:1] for weight in (query_weight, key_weight, value_weight)
        )
        (
            tokens,
            firsts,
            heads_own,
            heads_received,
            normed,
            qkv_full,
            gains_full,
            out_own,
            out_other,
            down_own,
        ) = front(
            inputs,
            first_values,
            q_half[0],
            k_half[0],
            jnp.concatenate([v_half[0], gains], axis=1),
            out_halves[0],
            down_halves[0],
            cosine,
            sine,
            line,
        )
        qkv_full = qkv_full.reshape(2, 3, D, wide)
        tokens = [tokens]
        pieces = [heads_received, heads_own]
        (
            mix_received,
            att_own,
            lse,
            att_other,
            grads,
            down_own,
            down_other,
            gate_own,
            gate_other,
            up_own,
            up_other,
        ) = attend_carry(
            heads_received, heads_own, out_grad, down_own, gate_halves[0], up_halves[0], line
        )
        mixes = [mix_received, att_own]
        grads = [grads]
        layout = jnp.stack([side, core, 0 * core]).astype(jnp.int32)
        out_own, out_other = parts_of(out_own), parts_of(out_other)
        gate_pieces = parts_of(gate_own), parts_of(gate_other)
        up_pieces = parts_of(up_own), parts_of(up_other)
        down_pieces = parts_of(down_own), parts_of(down_other)
    else:
        qkv = [
            jnp.concatenate(half + [gains], axis=1)
            for half in split(query_weight, key_weight, value_weight)
        ]
        layout = place
        tokens = to_sequence(inputs)
        firsts = to_sequence(first_values)
        grads = to_sequence(out_grad)
        qkv_own, qkv_other = gather_rest(gather_z(qkv[0]), qkv[1])
        out_own, out_other = gather_rest(gather_z(out_halves[0]), out_halves[1])
        gate_pieces = gather_rest(gather_z(gate_halves[0]), gate_halves[1])
        up_pieces = gather_rest(gather_z(up_halves[0]), up_halves[1])
        down_pieces = gather_rest(gather_z(down_halves[0]), down_halves[1])
        heads_other, heads_own, normed, qkv_full, gains_full = project(
            inputs, tokens, first_values, firsts, qkv_own, qkv_other, cosine, sine, place
        )
        pieces = exchange(halves_to_ranks(heads_other, heads_own, 1))
        mixes, lse = attend(pieces, order, slots)
        att_other, att_own = ranks_to_halves(exchange_back(mixes), 0)

    middle, normed2, out_full = output_projection(
        inputs, tokens, out_own, out_other, att_other, att_own, gains_full, layout
    )
    if (slots, count) == (2, 2):
        (
            outputs,
            outputs_sent,
            grad_middle,
            low_grad,
            mlp_gain_grad,
            gu_reduced,
            down_reduced,
            gu_y,
        ) = mlp_carry(
            out_grad,
            grads[0],
            middle,
            normed2,
            gains_full,
            (gate_pieces[0][0], gate_pieces[1][0]),
            (up_pieces[0][0], up_pieces[1][0]),
            (down_pieces[0][0], down_pieces[1][0]),
            line,
        )
        ga_own, ga_received, out_kept, out_landed = grad_attended_carry(
            low_grad, out_full, att_other, att_own, line
        )
        down_reduced = down_reduced.reshape(line, 2, -1, wide)
        out_kept = out_kept.reshape(line, 2, -1, wide)
        out_landed = out_landed.reshape(line, 2, -1, wide)
        (
            back_own,
            back_other,
            outputs_received,
            gu_mine,
            gu_z,
            down_y,
            out_mine,
            out_y,
        ) = attend_back_carry(
            pieces,
            mixes,
            [ga_received, ga_own],
            lse,
            full_cos,
            full_sin,
            outputs_sent,
            gu_reduced,
            gu_y,
            down_reduced,
            out_kept,
            out_landed,
            line,
        )
        outputs = land(outputs, outputs_received, (1 - side)[None])
        gate_up_grad = gu_mine.astype(F32)
        for jump in range(line - 1):
            gate_up_grad = gate_up_grad + gu_z[jump].astype(F32)
        gate_up_grad = along_x_and_core(gate_up_grad)
        down_grad = along_z_and_on(
            lambda index: pick(pick(down_reduced, y, 1), index, 0).astype(F32)
            + pick(down_y, index, 0).astype(F32)
        )
        output_grad = along_z_and_on(
            lambda index: pick(out_mine, index, 0).astype(F32) + pick(out_y, index, 0).astype(F32)
        )
    else:
        (
            outputs,
            outputs_sent,
            grad_middle,
            low_grad,
            mlp_gain_grad,
            gu_sent,
            gu_kept,
            down_sent,
            down_kept,
        ) = mlp(out_grad, grads, middle, normed2, gains_full, gate_pieces, up_pieces, down_pieces, layout)
        ga_other, ga_own, out_sent, out_kept = grad_attended(
            low_grad, out_full, att_other, att_own, place
        )
        gate_up_grad = scatter(gu_sent, gu_kept, 1)
        down_grad = scatter(down_sent.reshape(-1, wide), down_kept.reshape(-1, wide), 0)
        output_grad = scatter(out_sent, out_kept, 0)
        grad_heads = exchange(halves_to_ranks(ga_other, ga_own, 0))
        back = attend_back(pieces, mixes, grad_heads, lse, full_cos, full_sin, order, slots)
        back_other, back_own = ranks_to_halves(exchange_back(back), 1)
        outputs = to_home(outputs, outputs_sent)
    input_grad, input_sent, first_grad, first_sent, gain_grads, qkv_sent, qkv_kept = tail(
        inputs,
        tokens,
        back_other,
        back_own,
        qkv_full,
        normed,
        grad_middle,
        gains_full,
        mlp_gain_grad,
        place,
    )
    qkv_grad = columns(*scatter(qkv_sent, qkv_kept, 1))
    gate_up_grad = columns(*gate_up_grad)
    gain_grads = everywhere(gain_grads)
    gain_grads = lax.dynamic_slice_in_dim(gain_grads, shard * (D // parts), D // parts, 1)
    return (
        outputs,
        to_home(input_grad, input_sent),
        to_home(first_grad, first_sent),
        gain_grads[0],
        gain_grads[1],
        qkv_grad[0],
        qkv_grad[1],
        qkv_grad[2],
        columns(*output_grad),
        gate_up_grad[0],
        gate_up_grad[1],
        columns(*down_grad),
    )


def solution(mesh):
    token_spec = P("fsdp", "seq", None)
    weight_spec = P("fsdp", None)
    gain_spec = P("fsdp")
    return jax.shard_map(
        shards,
        mesh=mesh,
        in_specs=(token_spec,) * 3
        + (gain_spec,)
        + (weight_spec,) * 4
        + (gain_spec,)
        + (weight_spec,) * 3,
        out_specs=(token_spec,) * 3 + (gain_spec,) * 2 + (weight_spec,) * 7,
        check_vma=False,
    )
```

```python
import functools

import jax
import jax.numpy as jnp
from jax import lax
from jax.experimental import pallas as pl
from jax.experimental.pallas import tpu as pltpu
from jax.sharding import PartitionSpec as P

D = 1024
HEADS = 16
HEAD_DIM = 64
HALF = HEAD_DIM // 2
PAIR = 2 * HEAD_DIM
F32 = jnp.float32
BF16 = jnp.bfloat16
NEG = -1e30
MIB = 1024 * 1024
epsilon = 1e-06
rope_base = 10000.0


def dot(a, b):
    return lax.dot_general(a, b, (((1,), (0,)), ((), ())), preferred_element_type=F32)


def head_rows(value, head):
    row = lax.broadcasted_iota(jnp.int32, value.shape, 0)
    return jnp.where((row // HEAD_DIM) == head, value, jnp.zeros_like(value))


def head_lanes(value, head):
    lane = lax.broadcasted_iota(jnp.int32, value.shape, 1)
    return jnp.where((lane // HEAD_DIM) == head, value, jnp.zeros_like(value))


def causal(scores):
    side = scores.shape[0]
    square = scores[:, :side]
    key = lax.broadcasted_iota(jnp.int32, square.shape, 0)
    query = lax.broadcasted_iota(jnp.int32, square.shape, 1)
    square = jnp.where(key <= query, square, NEG)
    if scores.shape[1] == side:
        return square
    return jnp.concatenate([square, scores[:, side:]], axis=1)


def attend_body(length, tile_k, qz, kn, vt, ot, lse_ref):
    def score(sub, head):
        start = sub * tile_k
        return causal(dot(kn[start : start + tile_k, :], qz[head, :, start:]))

    def absorb(sub, head, carry, scores):
        peak, total, mixed = carry
        start = sub * tile_k
        new_peak = jnp.maximum(peak, jnp.max(scores, axis=0, keepdims=True))
        weights = jnp.exp(scores - new_peak)
        fade = jnp.exp(peak - new_peak)
        total = total * fade + jnp.sum(weights, axis=0, keepdims=True)
        values = vt[head * HEAD_DIM : (head + 1) * HEAD_DIM, start : start + tile_k]
        mixed = mixed * fade + dot(values, weights.astype(BF16))
        return (new_peak, total, mixed)

    tiles = [(sub, head) for sub in range(length // tile_k) for head in range(2)]
    carries = [
        (
            jnp.full((1, length), NEG, F32),
            jnp.zeros((1, length), F32),
            jnp.zeros((HEAD_DIM, length), F32),
        )
        for _ in range(2)
    ]
    ahead = score(*tiles[0])
    for number, (sub, head) in enumerate(tiles):
        scores = ahead
        if number + 1 < len(tiles):
            ahead = score(*tiles[number + 1])
        peak, total, mixed = absorb(sub, head, carries[head], scores)
        done = slice(sub * tile_k, (sub + 1) * tile_k)
        rows = slice(head * HEAD_DIM, (head + 1) * HEAD_DIM)
        ot[rows, done] = (mixed[:, :tile_k] / total[:, :tile_k]).astype(BF16)
        lse_ref[0, head : head + 1, done] = peak[:, :tile_k] + jnp.log(total[:, :tile_k])
        carries[head] = (peak[:, tile_k:], total[:, tile_k:], mixed[:, tile_k:])


def attend_kernel(count, slots, tok, tile_k, order, *refs):
    pieces = refs[:count]
    outs = refs[count : 2 * count]
    lse_ref = refs[2 * count]
    qz, kn, vt, ot = refs[2 * count + 1 :]
    for source in range(count):
        for slot in range(slots):
            cols = pl.ds(pl.multiple_of(order[source * slots + slot] * tok, tok), tok)
            take = slice(slot * tok, (slot + 1) * tok)
            query = pieces[source][0, :, take] * jnp.asarray(HEAD_DIM**-0.5, BF16)
            for head in range(2):
                qz[head, :, cols] = head_rows(query, head)
            kn[cols, :] = pieces[source][1, :, take].T
            vt[:, cols] = pieces[source][2, :, take]
    length = count * slots * tok
    attend_body(length, tile_k, qz, kn, vt, ot, lse_ref)
    for source in range(count):
        for slot in range(slots):
            cols = pl.ds(pl.multiple_of(order[source * slots + slot] * tok, tok), tok)
            outs[source][:, slot * tok : (slot + 1) * tok] = ot[:, cols]


def attend(pieces, order, slots):
    count = len(pieces)
    width, span = pieces[0].shape[1:]
    tok = span // slots
    length = count * span
    pairs = width // PAIR
    tile_k = min(256, length)
    grid_spec = pltpu.PrefetchScalarGridSpec(
        num_scalar_prefetch=1,
        grid=(pairs,),
        in_specs=[pl.BlockSpec((3, PAIR, span), lambda p, o: (0, p, 0))] * count,
        out_specs=[pl.BlockSpec((PAIR, span), lambda p, o: (p, 0))] * count
        + [pl.BlockSpec((1, 8, length), lambda p, o: (p, 0, 0))],
        scratch_shapes=[
            pltpu.VMEM((2, PAIR, length), BF16),
            pltpu.VMEM((length, PAIR), BF16),
            pltpu.VMEM((PAIR, length), BF16),
            pltpu.VMEM((PAIR, length), BF16),
        ],
    )
    area = pairs * 2 * length * length // 2
    results = pl.pallas_call(
        functools.partial(attend_kernel, count, slots, tok, tile_k),
        out_shape=[jax.ShapeDtypeStruct((width, span), BF16)] * count
        + [jax.ShapeDtypeStruct((pairs, 8, length), F32)],
        grid_spec=grid_spec,
        compiler_params=pltpu.CompilerParams(
            dimension_semantics=("arbitrary",), vmem_limit_bytes=48 * MIB
        ),
        cost_estimate=pl.CostEstimate(
            flops=area * 1024, bytes_accessed=8 * width * length, transcendentals=area
        ),
        name="attend",
    )(order, *pieces)
    return (results[:count], results[count])


def attend_back_body(
    pieces,
    mixes,
    grads,
    columns,
    tok,
    length,
    tile_q,
    tile_k,
    lse_ref,
    qz,
    gz,
    qn,
    gn,
    kn,
    vn,
    kt,
    inner,
    dq,
    dk,
    dv,
):
    slots = pieces[0].shape[2] // tok
    for source in range(len(pieces)):
        for slot in range(slots):
            cols = columns(source, slot)
            take = slice(slot * tok, (slot + 1) * tok)
            query = pieces[source][0, :, take] * jnp.asarray(HEAD_DIM**-0.5, BF16)
            grad = grads[source][:, take]
            query_rows = query.T
            grad_rows = grad.T
            for head in range(2):
                qz[head, :, cols] = head_rows(query, head)
                gz[head, :, cols] = head_rows(grad, head)
                qn[head, cols, :] = head_lanes(query_rows, head)
                gn[head, cols, :] = head_lanes(grad_rows, head)
            key = pieces[source][1, :, take]
            kt[:, cols] = key
            kn[cols, :] = key.T
            vn[cols, :] = pieces[source][2, :, take].T
            both = grad.astype(F32) * mixes[source][:, take].astype(F32)
            for head in range(2):
                inner[head : head + 1, cols] = jnp.sum(
                    both[head * HEAD_DIM : (head + 1) * HEAD_DIM], axis=0, keepdims=True
                )
    dq[...] = jnp.zeros_like(dq)
    steps = tile_q // tile_k

    def tile(key_start, query_start, width, masked, carry):
        grad_keys, grad_values = carry
        keys = kn[pl.ds(key_start, tile_k), :]
        values = vn[pl.ds(key_start, tile_k), :]
        cols = pl.ds(query_start, width)
        for head in range(2):
            rows = slice(head * HEAD_DIM, (head + 1) * HEAD_DIM)
            scores = dot(keys, qz[head, :, cols])
            if masked:
                scores = causal(scores)
            probs = jnp.exp(scores - lse_ref[0, head : head + 1, cols])
            grad_probs = dot(values, gz[head, :, cols])
            grad_scores = (probs * (grad_probs - inner[head : head + 1, cols])).astype(BF16)
            grad_values = grad_values + dot(probs.astype(BF16), gn[head, cols, :])
            grad_keys = grad_keys + dot(grad_scores, qn[head, cols, :])
            dq[rows, cols] += dot(kt[rows, pl.ds(key_start, tile_k)], grad_scores)
        return (grad_keys, grad_values)

    def one(number, _):
        base = pl.multiple_of(number * tile_q, tile_q)
        for sub in range(steps):
            skip = sub * tile_k
            key_start = pl.multiple_of(base + skip, tile_k)
            carry = (jnp.zeros((tile_k, PAIR), F32), jnp.zeros((tile_k, PAIR), F32))
            carry = tile(key_start, key_start, tile_q - skip, True, carry)

            def body(step, carry):
                return tile(
                    key_start, pl.multiple_of(step * tile_q, tile_q), tile_q, False, carry
                )

            carry = lax.fori_loop(number + 1, length // tile_q, body, carry)
            dk[pl.ds(key_start, tile_k), :] = carry[0]
            dv[pl.ds(key_start, tile_k), :] = carry[1]
        return 0

    lax.fori_loop(0, length // tile_q, one, 0)


def turn_back(dq, dk, dv, cols, cosine, sine):
    half = HEAD_DIM // 2
    results = []
    for grad in (dq[:, cols] * (HEAD_DIM**-0.5), dk[cols, :].T):
        turned = []
        for head in range(2):
            low = head * HEAD_DIM
            first = grad[low : low + half]
            second = grad[low + half : low + 2 * half]
            turned += [first * cosine + second * sine, second * cosine - first * sine]
        results.append(jnp.concatenate(turned, axis=0).astype(BF16))
    results.append(dv[cols, :].T.astype(BF16))
    return results


def attend_back_kernel(count, slots, tok, tile_q, tile_k, order, *refs):
    pieces = refs[:count]
    mixes = refs[count : 2 * count]
    grads = refs[2 * count : 3 * count]
    lse_ref, cos_ref, sin_ref = refs[3 * count : 3 * count + 3]
    outs = refs[3 * count + 3 : 4 * count + 3]
    scratch = refs[4 * count + 3 :]
    dq, dk, dv = scratch[-3:]

    def columns(source, slot):
        return pl.ds(pl.multiple_of(order[source * slots + slot] * tok, tok), tok)

    attend_back_body(
        pieces,
        mixes,
        grads,
        columns,
        tok,
        count * slots * tok,
        tile_q,
        tile_k,
        lse_ref,
        *scratch,
    )
    for source in range(count):
        for slot in range(slots):
            cols = columns(source, slot)
            results = turn_back(dq, dk, dv, cols, cos_ref[:, cols], sin_ref[:, cols])
            for which, result in enumerate(results):
                outs[source][which, :, slot * tok : (slot + 1) * tok] = result


def attend_back(pieces, mixes, grads, lse, cosine, sine, order, slots):
    count = len(pieces)
    width, span = pieces[0].shape[1:]
    tok = span // slots
    length = count * span
    pairs = width // PAIR
    tile_q = min(512, length)
    tile_k = min(256, length)
    triple = pl.BlockSpec((3, PAIR, span), lambda p, o: (0, p, 0))
    single = pl.BlockSpec((PAIR, span), lambda p, o: (p, 0))
    table = pl.BlockSpec((HEAD_DIM // 2, length), lambda p, o: (0, 0))
    grid_spec = pltpu.PrefetchScalarGridSpec(
        num_scalar_prefetch=1,
        grid=(pairs,),
        in_specs=[triple] * count
        + [single] * (2 * count)
        + [pl.BlockSpec((1, 8, length), lambda p, o: (p, 0, 0)), table, table],
        out_specs=[triple] * count,
        scratch_shapes=[
            pltpu.VMEM((2, PAIR, length), BF16),
            pltpu.VMEM((2, PAIR, length), BF16),
            pltpu.VMEM((2, length, PAIR), BF16),
            pltpu.VMEM((2, length, PAIR), BF16),
            pltpu.VMEM((length, PAIR), BF16),
            pltpu.VMEM((length, PAIR), BF16),
            pltpu.VMEM((PAIR, length), BF16),
            pltpu.VMEM((8, length), F32),
            pltpu.VMEM((PAIR, length), F32),
            pltpu.VMEM((length, PAIR), F32),
            pltpu.VMEM((length, PAIR), F32),
        ],
    )
    area = pairs * 2 * length * length // 2
    return pl.pallas_call(
        functools.partial(attend_back_kernel, count, slots, tok, tile_q, tile_k),
        out_shape=[jax.ShapeDtypeStruct((3, width, span), BF16)] * count,
        grid_spec=grid_spec,
        compiler_params=pltpu.CompilerParams(
            dimension_semantics=("arbitrary",), vmem_limit_bytes=56 * MIB
        ),
        cost_estimate=pl.CostEstimate(
            flops=area * 2560, bytes_accessed=16 * width * length, transcendentals=area
        ),
        name="attend_back",
    )(order, *pieces, *mixes, *grads, lse, cosine, sine)


def nt(a, b):
    return lax.dot_general(a, b, (((1,), (1,)), ((), ())), preferred_element_type=F32)


def whole_block(shape):
    zeros = (0,) * len(shape)
    return pl.BlockSpec(shape, lambda *_: zeros)


def parameters(mib):
    return pltpu.CompilerParams(dimension_semantics=("arbitrary",), vmem_limit_bytes=mib * MIB)


def project_kernel(slots, tok, count, rows, place, *refs):
    xs, firsts = refs[:slots], refs[slots : 2 * slots]
    own = refs[2 * slots : 2 * slots + count]
    other = refs[2 * slots + count : 2 * slots + 2 * count]
    cos_ref, sin_ref = refs[2 * slots + 2 * count : 2 * slots + 2 * count + 2]
    other_ref, own_ref, normed_ref, full_ref, gains_ref, column = refs[2 * slots + 2 * count + 2 :]
    step = pl.program_id(0)
    target, kind = step // 3, step % 3
    core = place[1]
    half = jnp.where(target == 0, 1 - core, core)
    depth = normed_ref.shape[1]
    wide = own_ref.shape[1]

    @pl.when(step == 0)
    def _():
        for number in range(count):
            at = pl.ds(pl.multiple_of(place[2 + number] * rows, rows), rows)
            for which in range(3):
                columns = slice(which * wide, (which + 1) * wide)
                full_ref[core, which, at, :] = own[number][:, columns]
                full_ref[1 - core, which, at, :] = other[number][:, columns]
            column[at, :] = own[number][:, 3 * wide :]
        gains_ref[...] = column[...].T[:8].astype(F32)
        gain = gains_ref[0:1, :]
        for slot in range(slots):
            values = xs[slot][...].reshape(tok, depth).astype(F32)
            scale = lax.rsqrt(jnp.mean(values * values, axis=1, keepdims=True) + epsilon)
            normed_ref[slot * tok : (slot + 1) * tok, :] = (values * scale * gain).astype(BF16)

    weight = full_ref[half, kind]
    raw = nt(weight.T, normed_ref[...])

    def store(value):
        @pl.when(target == 0)
        def _():
            other_ref[0] = value

        @pl.when(target == 1)
        def _():
            own_ref[0] = value

    @pl.when(kind < 2)
    def _():
        parts = raw.reshape(wide // HEAD_DIM, 2, HALF, raw.shape[1])
        first, second = parts[:, 0], parts[:, 1]
        cosine, sine = cos_ref[...][None], sin_ref[...][None]
        turned = jnp.stack(
            [first * cosine - second * sine, first * sine + second * cosine], axis=1
        )
        store(turned.reshape(raw.shape).astype(BF16))

    @pl.when(kind == 2)
    def _():
        first = jnp.concatenate(
            [ref[...].reshape(tok, wide).T.astype(F32) for ref in firsts], axis=1
        )
        store((0.5 * raw + 0.5 * first).astype(BF16))


def project(inputs, received, firsts, firsts_received, own, other, cosine, sine, place):
    slots, tok, depth = inputs.shape
    count, rows = len(own), own[0].shape[0]
    wide = depth // 2
    span = slots * tok

    def half(s, p):
        return jnp.where(s < 3, 1 - p[1], p[1])

    x_specs = [pl.BlockSpec((1, tok, depth), lambda s, p: (p[0], 0, 0))]
    x_specs += [whole_block((tok, depth))] * (slots - 1)
    first_specs = [pl.BlockSpec((1, tok, wide), lambda s, p: (p[0], 0, half(s, p)))]
    first_specs += [pl.BlockSpec((tok, wide), lambda s, p: (0, half(s, p)))] * (slots - 1)
    grid_spec = pltpu.PrefetchScalarGridSpec(
        num_scalar_prefetch=1,
        grid=(6,),
        in_specs=x_specs
        + first_specs
        + [whole_block(own[0].shape)] * (2 * count)
        + [whole_block((HALF, span))] * 2,
        out_specs=[
            pl.BlockSpec((1, wide, span), lambda s, p: (jnp.minimum(s, 2), 0, 0)),
            pl.BlockSpec((1, wide, span), lambda s, p: (jnp.maximum(s - 3, 0), 0, 0)),
            whole_block((span, depth)),
            whole_block((2, 3, depth, wide)),
            whole_block((8, depth)),
        ],
        scratch_shapes=[pltpu.VMEM((depth, 128), BF16)],
    )
    return pl.pallas_call(
        functools.partial(project_kernel, slots, tok, count, rows),
        out_shape=[
            jax.ShapeDtypeStruct((3, wide, span), BF16),
            jax.ShapeDtypeStruct((3, wide, span), BF16),
            jax.ShapeDtypeStruct((span, depth), BF16),
            jax.ShapeDtypeStruct((2, 3, depth, wide), BF16),
            jax.ShapeDtypeStruct((8, depth), F32),
        ],
        grid_spec=grid_spec,
        compiler_params=parameters(56),
        cost_estimate=pl.CostEstimate(
            flops=6 * span * depth * depth,
            bytes_accessed=2 * (8 * span * depth + 6 * depth * depth),
            transcendentals=0,
        ),
        name="project",
    )(place, inputs, *received, firsts, *firsts_received, *own, *other, cosine, sine)


def output_kernel(slots, tok, count, rows, place, *refs):
    xs = refs[:slots]
    own = refs[slots : slots + count]
    other = refs[slots + count : slots + 2 * count]
    att_other, att_own, gains_ref = refs[slots + 2 * count : slots + 2 * count + 3]
    middle_ref, normed_ref, full_ref = refs[slots + 2 * count + 3 :]
    step = pl.program_id(0)
    core = place[1]
    wide = att_own.shape[0]
    depth = 2 * wide
    mine = pl.ds(pl.multiple_of(core * wide, wide), wide)
    others = pl.ds(pl.multiple_of((1 - core) * wide, wide), wide)

    @pl.when(step == 0)
    def _():
        for number in range(count):
            at = pl.ds(pl.multiple_of(place[2 + number] * rows, rows), rows)
            full_ref[at, mine] = own[number][...]
            full_ref[at, others] = other[number][...]

    total = dot(att_own[...].T, full_ref[mine, :]) + dot(att_other[...].T, full_ref[others, :])
    for slot in range(slots):

        @pl.when(step == slot)
        def _(slot=slot):
            middle_ref[...] = xs[slot][...].reshape(tok, depth).astype(F32) + total

    middle = middle_ref[...]
    scale = lax.rsqrt(jnp.mean(middle * middle, axis=1, keepdims=True) + epsilon)
    normed_ref[...] = (middle * scale * gains_ref[1:2, :]).astype(BF16)


def output_projection(inputs, received, own, other, att_other, att_own, gains, place):
    slots, tok, depth = inputs.shape
    count, rows = len(own), own[0].shape[0]
    wide = depth // 2
    span = slots * tok
    x_specs = [pl.BlockSpec((1, tok, depth), lambda s, p: (p[0], 0, 0))]
    x_specs += [whole_block((tok, depth))] * (slots - 1)
    grid_spec = pltpu.PrefetchScalarGridSpec(
        num_scalar_prefetch=1,
        grid=(slots,),
        in_specs=x_specs
        + [whole_block(own[0].shape)] * (2 * count)
        + [pl.BlockSpec((wide, tok), lambda s, p: (0, s))] * 2
        + [whole_block((8, depth))],
        out_specs=[
            pl.BlockSpec((tok, depth), lambda s, p: (s, 0)),
            pl.BlockSpec((tok, depth), lambda s, p: (s, 0)),
            whole_block((depth, depth)),
        ],
    )
    return pl.pallas_call(
        functools.partial(output_kernel, slots, tok, count, rows),
        out_shape=[
            jax.ShapeDtypeStruct((span, depth), F32),
            jax.ShapeDtypeStruct((span, depth), BF16),
            jax.ShapeDtypeStruct((depth, depth), BF16),
        ],
        grid_spec=grid_spec,
        compiler_params=parameters(56),
        cost_estimate=pl.CostEstimate(
            flops=2 * span * depth * depth,
            bytes_accessed=12 * span * depth + 4 * depth * depth,
            transcendentals=0,
        ),
        name="output_projection",
    )(place, inputs, *received, *own, *other, att_other, att_own, gains)


def mlp_kernel(slots, tok, count, rows, down_rows, blocks, place, *refs):
    grads = refs[:slots]
    middle_ref, normed_ref, gains_ref = refs[slots : slots + 3]
    base = slots + 3
    own_g, other_g, own_u, other_u, own_d, other_d = (
        refs[base + number * count : base + (number + 1) * count] for number in range(6)
    )
    (
        out_ref,
        send_ref,
        grad_ref,
        low_ref,
        gain_ref,
        gu_send,
        gu_keep,
        d_send,
        d_keep,
        wgu,
        wd,
        og,
        normed_t,
        acc,
        back,
        sems,
    ) = refs[base + 6 * count :]
    step = pl.program_id(0)
    core = place[1]
    depth = og.shape[1]
    wide = depth // 2
    strip = 128
    half_width = blocks * strip
    mine = pl.ds(pl.multiple_of(core * wide, wide), wide)
    others = pl.ds(pl.multiple_of((1 - core) * wide, wide), wide)

    def loads():
        copies = []
        for number in range(count):
            at = pl.ds(pl.multiple_of(place[2 + number] * rows, rows), rows)
            for which, (gate, up) in enumerate(((own_g, own_u), (other_g, other_u))):
                copies.append((gate[number], wgu.at[which, at, pl.ds(0, half_width)]))
                copies.append((up[number], wgu.at[which, at, pl.ds(half_width, half_width)]))
        for number in range(count):
            at = pl.ds(pl.multiple_of(place[2 + number] * down_rows, down_rows), down_rows)
            copies.append((own_d[number], wd.at[at, mine]))
            copies.append((other_d[number], wd.at[at, others]))
        return [
            pltpu.make_async_copy(source, target, sems.at[number])
            for number, (source, target) in enumerate(copies)
        ]

    @pl.when(step == 0)
    def _():
        copies = loads()
        for copy in copies:
            copy.start()
        for slot in range(slots):
            og[slot * tok : (slot + 1) * tok, :] = grads[slot][...].reshape(tok, depth)
        normed_t[...] = normed_ref[...].T
        acc[...] = jnp.zeros_like(acc)
        back[...] = jnp.zeros_like(back)
        for copy in copies:
            copy.wait()

    at = pl.ds(pl.multiple_of(step * strip, strip), strip)
    up_at = pl.ds(pl.multiple_of(half_width + step * strip, strip), strip)
    gate_w = jnp.concatenate([wgu[0, :, at], wgu[1, :, at]], axis=1)
    up_w = jnp.concatenate([wgu[0, :, up_at], wgu[1, :, up_at]], axis=1)
    own_rows = pl.ds(pl.multiple_of(core * half_width + step * strip, strip), strip)
    other_rows = pl.ds(pl.multiple_of((1 - core) * half_width + step * strip, strip), strip)
    down_w = jnp.concatenate([wd[own_rows, :], wd[other_rows, :]], axis=0)
    normed = normed_ref[...]
    gate = dot(normed, gate_w)
    up = dot(normed, up_w)
    grad_active = nt(og[...], down_w)
    sigma = jax.nn.sigmoid(gate)
    silu = gate * sigma
    active = (silu * up).astype(BF16)
    grad_up = (grad_active * silu).astype(BF16)
    grad_gate = (grad_active * up * sigma * (1.0 + gate * (1.0 - sigma))).astype(BF16)
    acc[...] += dot(active, down_w)
    back[...] += nt(grad_gate, gate_w) + nt(grad_up, up_w)
    grad_gate_w = dot(normed_t[...], grad_gate).astype(BF16)
    gu_keep[0] = grad_gate_w[:, :strip]
    gu_send[0] = grad_gate_w[:, strip:]
    grad_up_w = dot(normed_t[...], grad_up).astype(BF16)
    gu_keep[1] = grad_up_w[:, :strip]
    gu_send[1] = grad_up_w[:, strip:]
    active_t = active.T
    kept = dot(active_t, og[:, mine]).astype(BF16)
    sent = dot(active_t, og[:, others]).astype(BF16)
    d_keep[core] = kept[:strip]
    d_keep[1 - core] = kept[strip:]
    d_send[core] = sent[:strip]
    d_send[1 - core] = sent[strip:]

    @pl.when(step == blocks - 1)
    def _():
        gain = gains_ref[1:2, :]
        chunk = min(128, tok)
        gain_ref[...] = jnp.zeros_like(gain_ref)
        for slot in range(slots):

            def finish(number, _, slot=slot):
                local = pl.ds(pl.multiple_of(number * chunk, chunk), chunk)
                some = pl.ds(pl.multiple_of(slot * tok + number * chunk, chunk), chunk)
                middle = middle_ref[some, :]
                scale = lax.rsqrt(jnp.mean(middle * middle, axis=1, keepdims=True) + epsilon)
                result = middle + acc[some, :]
                if slot == 0:
                    out_ref[0, local, :] = result
                else:
                    send_ref[pl.ds(pl.multiple_of((slot - 1) * tok + number * chunk, chunk), chunk), :] = (
                        result.astype(BF16)
                    )
                grad = back[some, :]
                gain_ref[0:1, :] += jnp.sum(grad * middle * scale, axis=0, keepdims=True)
                weighted = grad * gain
                inner = jnp.mean(weighted * middle, axis=1, keepdims=True)
                grad_middle = (
                    scale * weighted
                    - middle * (scale * scale * scale) * inner
                    + og[some, :].astype(F32)
                )
                grad_ref[some, :] = grad_middle
                low_ref[some, :] = grad_middle.astype(BF16)
                return 0

            lax.fori_loop(0, tok // chunk, finish, 0)


def mlp(grads, grads_received, middle, normed, gains, gate, up, down, place):
    slots, tok, depth = grads.shape
    own_d, other_d = down
    count, rows = len(own_d), gate[0][0].shape[0]
    down_rows = own_d[0].shape[0]
    half_width = gate[0][0].shape[1]
    wide = depth // 2
    span = slots * tok
    blocks = half_width // 128
    once = pl.Buffered(1)
    g_specs = [pl.BlockSpec((1, tok, depth), lambda s, p: (p[0], 0, 0), pipeline_mode=once)]
    g_specs += [pl.BlockSpec((tok, depth), lambda s, p: (0, 0), pipeline_mode=once)] * (slots - 1)
    gu_spec = pl.BlockSpec((2, depth, 128), lambda s, p: (0, 0, s))
    d_spec = pl.BlockSpec((2, 128, wide), lambda s, p: (0, s, 0))
    grid_spec = pltpu.PrefetchScalarGridSpec(
        num_scalar_prefetch=1,
        grid=(blocks,),
        in_specs=g_specs
        + [
            pl.BlockSpec((span, depth), lambda s, p: (0, 0), pipeline_mode=once),
            pl.BlockSpec((span, depth), lambda s, p: (0, 0), pipeline_mode=once),
            whole_block((8, depth)),
        ]
        + [pl.BlockSpec(memory_space=pl.ANY)] * (6 * count),
        out_specs=[
            pl.BlockSpec((1, tok, depth), lambda s, p: (p[0], 0, 0), pipeline_mode=once),
            pl.BlockSpec(((slots - 1) * tok, depth), lambda s, p: (0, 0), pipeline_mode=once),
            pl.BlockSpec((span, depth), lambda s, p: (0, 0), pipeline_mode=once),
            pl.BlockSpec((span, depth), lambda s, p: (0, 0), pipeline_mode=once),
            whole_block((8, depth)),
            gu_spec,
            gu_spec,
            d_spec,
            d_spec,
        ],
        scratch_shapes=[
            pltpu.VMEM((2, depth, 2 * half_width), BF16),
            pltpu.VMEM((2 * half_width, depth), BF16),
            pltpu.VMEM((span, depth), BF16),
            pltpu.VMEM((depth, span), BF16),
            pltpu.VMEM((span, depth), F32),
            pltpu.VMEM((span, depth), F32),
            pltpu.SemaphoreType.DMA((6 * count,)),
        ],
    )
    return pl.pallas_call(
        functools.partial(mlp_kernel, slots, tok, count, rows, down_rows, blocks),
        out_shape=[
            jax.ShapeDtypeStruct((slots, tok, depth), F32),
            jax.ShapeDtypeStruct(((slots - 1) * tok, depth), BF16),
            jax.ShapeDtypeStruct((span, depth), F32),
            jax.ShapeDtypeStruct((span, depth), BF16),
            jax.ShapeDtypeStruct((8, depth), F32),
            jax.ShapeDtypeStruct((2, depth, half_width), BF16),
            jax.ShapeDtypeStruct((2, depth, half_width), BF16),
            jax.ShapeDtypeStruct((2, half_width, wide), BF16),
            jax.ShapeDtypeStruct((2, half_width, wide), BF16),
        ],
        grid_spec=grid_spec,
        compiler_params=parameters(63),
        cost_estimate=pl.CostEstimate(
            flops=16 * span * depth * 2 * half_width,
            bytes_accessed=24 * depth * half_width + 20 * span * depth,
            transcendentals=2 * span * half_width,
        ),
        name="mlp",
    )(
        place,
        grads,
        *grads_received,
        middle,
        normed,
        gains,
        *gate[0],
        *gate[1],
        *up[0],
        *up[1],
        *own_d,
        *other_d,
    )


def grad_attended_kernel(place, low_ref, full_ref, att_other, att_own, ga_other, ga_own, sent, kept):
    step = pl.program_id(0)
    core = place[1]
    wide = att_own.shape[0]
    mine = pl.ds(pl.multiple_of(core * wide, wide), wide)
    others = pl.ds(pl.multiple_of((1 - core) * wide, wide), wide)
    for number, (att, result) in enumerate(((att_other, ga_other), (att_own, ga_own))):

        @pl.when(step == number)
        def _(att=att, result=result):
            result[...] = nt(full_ref[...], low_ref[...]).astype(BF16)
            kept[...] = dot(att[...], low_ref[:, mine]).astype(BF16)
            sent[...] = dot(att[...], low_ref[:, others]).astype(BF16)


def grad_attended(low, full, att_other, att_own, place):
    span, depth = low.shape
    wide = depth // 2

    def half(s, p):
        return jnp.where(s == 0, 1 - p[1], p[1])

    row_spec = pl.BlockSpec((wide, wide), lambda s, p: (half(s, p), 0))
    grid_spec = pltpu.PrefetchScalarGridSpec(
        num_scalar_prefetch=1,
        grid=(2,),
        in_specs=[
            whole_block((span, depth)),
            pl.BlockSpec((wide, depth), lambda s, p: (half(s, p), 0)),
            whole_block((wide, span)),
            whole_block((wide, span)),
        ],
        out_specs=[whole_block((wide, span)), whole_block((wide, span)), row_spec, row_spec],
    )
    return pl.pallas_call(
        grad_attended_kernel,
        out_shape=[
            jax.ShapeDtypeStruct((wide, span), BF16),
            jax.ShapeDtypeStruct((wide, span), BF16),
            jax.ShapeDtypeStruct((depth, wide), BF16),
            jax.ShapeDtypeStruct((depth, wide), BF16),
        ],
        grid_spec=grid_spec,
        compiler_params=parameters(48),
        cost_estimate=pl.CostEstimate(
            flops=4 * span * depth * depth,
            bytes_accessed=6 * span * depth + 4 * depth * depth,
            transcendentals=0,
        ),
        name="grad_attended",
    )(place, low, full, att_other, att_own)


def tail_kernel(slots, tok, place, *refs):
    xs = refs[:slots]
    (
        back_other,
        back_own,
        full_ref,
        normed_ref,
        grad_ref,
        gains_ref,
        mlp_gain_ref,
        out_ref,
        send_ref,
        first_ref,
        first_send,
        gain_ref,
        sent,
        kept,
        normed_t,
        acc,
    ) = refs[slots:]
    step = pl.program_id(0)
    target, kind = step // 3, step % 3
    depth = acc.shape[1]

    @pl.when(step == 0)
    def _():
        normed_t[...] = normed_ref[...].T
        acc[...] = jnp.zeros_like(acc)

    def part(back, result):
        grad = back[0]

        @pl.when(kind == 2)
        def _():
            rows = 0.5 * grad.astype(F32).T
            first_ref[0] = rows[:tok]
            first_send[...] = rows[tok:].astype(BF16)

        grad = grad * jnp.where(kind == 2, 0.5, 1.0).astype(BF16)
        acc[...] += nt(grad.T, full_ref[0, 0])
        result[0] = nt(normed_t[...], grad).astype(BF16)

    @pl.when(target == 0)
    def _():
        part(back_other, sent)

    @pl.when(target == 1)
    def _():
        part(back_own, kept)

    @pl.when(step == 5)
    def _():
        gain = gains_ref[0:1, :]
        chunk = min(128, tok)
        gain_ref[...] = jnp.zeros_like(gain_ref)
        gain_ref[1:2, :] = mlp_gain_ref[0:1, :]
        for slot in range(slots):

            def finish(number, _, slot=slot):
                local = pl.ds(pl.multiple_of(number * chunk, chunk), chunk)
                some = pl.ds(pl.multiple_of(slot * tok + number * chunk, chunk), chunk)
                if slot == 0:
                    values = xs[slot][0, local, :].astype(F32)
                else:
                    values = xs[slot][local, :].astype(F32)
                scale = lax.rsqrt(jnp.mean(values * values, axis=1, keepdims=True) + epsilon)
                grad = acc[some, :]
                gain_ref[0:1, :] += jnp.sum(grad * values * scale, axis=0, keepdims=True)
                weighted = grad * gain
                inner = jnp.mean(weighted * values, axis=1, keepdims=True)
                result = (
                    scale * weighted
                    - values * (scale * scale * scale) * inner
                    + grad_ref[some, :]
                )
                if slot == 0:
                    out_ref[0, local, :] = result
                else:
                    send_ref[pl.ds(pl.multiple_of((slot - 1) * tok + number * chunk, chunk), chunk), :] = (
                        result.astype(BF16)
                    )
                return 0

            lax.fori_loop(0, tok // chunk, finish, 0)


def tail(inputs, received, back_other, back_own, full, normed, grad_middle, gains, mlp_gain, place):
    slots, tok, depth = inputs.shape
    wide = depth // 2
    span = slots * tok
    rest = (slots - 1) * tok
    once = pl.Buffered(1)

    def half(s, p):
        return jnp.where(s < 3, 1 - p[1], p[1])

    x_specs = [pl.BlockSpec((1, tok, depth), lambda s, p: (p[0], 0, 0))]
    x_specs += [whole_block((tok, depth))] * (slots - 1)
    grid_spec = pltpu.PrefetchScalarGridSpec(
        num_scalar_prefetch=1,
        grid=(6,),
        in_specs=x_specs
        + [
            pl.BlockSpec((1, wide, span), lambda s, p: (jnp.minimum(s, 2), 0, 0)),
            pl.BlockSpec((1, wide, span), lambda s, p: (jnp.maximum(s - 3, 0), 0, 0)),
            pl.BlockSpec((1, 1, depth, wide), lambda s, p: (half(s, p), s % 3, 0, 0)),
            whole_block((span, depth)),
            pl.BlockSpec((span, depth), lambda s, p: (0, 0), pipeline_mode=once),
            whole_block((8, depth)),
            whole_block((8, depth)),
        ],
        out_specs=[
            pl.BlockSpec((1, tok, depth), lambda s, p: (p[0], 0, 0)),
            whole_block((rest, depth)),
            pl.BlockSpec((1, tok, wide), lambda s, p: (p[0], 0, half(s, p))),
            pl.BlockSpec((rest, wide), lambda s, p: (0, half(s, p))),
            whole_block((8, depth)),
            pl.BlockSpec((1, depth, wide), lambda s, p: (jnp.minimum(s, 2), 0, 0)),
            pl.BlockSpec((1, depth, wide), lambda s, p: (jnp.maximum(s - 3, 0), 0, 0)),
        ],
        scratch_shapes=[pltpu.VMEM((depth, span), BF16), pltpu.VMEM((span, depth), F32)],
    )
    return pl.pallas_call(
        functools.partial(tail_kernel, slots, tok),
        out_shape=[
            jax.ShapeDtypeStruct((slots, tok, depth), F32),
            jax.ShapeDtypeStruct((rest, depth), BF16),
            jax.ShapeDtypeStruct((slots, tok, depth), F32),
            jax.ShapeDtypeStruct((rest, depth), BF16),
            jax.ShapeDtypeStruct((8, depth), F32),
            jax.ShapeDtypeStruct((3, depth, wide), BF16),
            jax.ShapeDtypeStruct((3, depth, wide), BF16),
        ],
        grid_spec=grid_spec,
        compiler_params=parameters(60),
        cost_estimate=pl.CostEstimate(
            flops=12 * span * depth * depth,
            bytes_accessed=24 * span * depth + 12 * depth * depth,
            transcendentals=0,
        ),
        name="tail",
    )(
        place, inputs, *received, back_other, back_own, full, normed, grad_middle, gains, mlp_gain
    )


def land_kernel(place, whole_ref, part_ref, out_ref):
    out_ref[0] = part_ref[...].astype(F32)


def land(whole, part, slot):
    _, tok, depth = whole.shape
    tile = min(256, tok)
    grid_spec = pltpu.PrefetchScalarGridSpec(
        num_scalar_prefetch=1,
        grid=(tok // tile,),
        in_specs=[
            pl.BlockSpec(memory_space=pl.ANY),
            pl.BlockSpec((tile, depth), lambda s, p: (s, 0)),
        ],
        out_specs=pl.BlockSpec((1, tile, depth), lambda s, p: (p[0], s, 0)),
    )
    return pl.pallas_call(
        land_kernel,
        out_shape=jax.ShapeDtypeStruct(whole.shape, F32),
        grid_spec=grid_spec,
        input_output_aliases={1: 0},
        compiler_params=parameters(16),
        cost_estimate=pl.CostEstimate(
            flops=tok * depth, bytes_accessed=6 * tok * depth, transcendentals=0
        ),
        name="land",
    )(slot, whole, part)


MESH = pl.DeviceIdType.MESH


def seats():
    shard = lax.axis_index("fsdp")
    seat = lax.axis_index("seq")
    return (shard // 2, shard % 2, seat // 2, seat % 2)


def meet(line, keys):
    shard = lax.axis_index("fsdp")
    seat = lax.axis_index("seq")
    partners = []
    if "z" in keys:
        partners += [{"fsdp": lax.rem(shard + 2 * jump, 2 * line)} for jump in range(1, line)]
    if "y" in keys:
        partners.append({"fsdp": shard + 1 - 2 * (shard % 2)})
    if "x" in keys:
        partners.append({"seq": lax.rem(seat + 2, 4)})
    if "core" in keys:
        partners.append({"seq": seat + 1 - 2 * (seat % 2)})
    barrier = pltpu.get_barrier_semaphore()
    for partner in partners:
        pl.semaphore_signal(barrier, inc=1, device_id=partner, device_id_type=MESH)
    pl.semaphore_wait(barrier, len(partners))


def send(source, target, sems, number, partner):
    return pltpu.make_async_remote_copy(
        src_ref=source,
        dst_ref=target,
        send_sem=sems.at[0, number],
        recv_sem=sems.at[1, number],
        device_id=partner,
        device_id_type=MESH,
    )


def to_core_partner():
    seat = lax.axis_index("seq")
    return {"seq": seat + 1 - 2 * (seat % 2)}


def to_x_partner():
    return {"seq": lax.rem(lax.axis_index("seq") + 2, 4)}


def to_y_partner():
    shard = lax.axis_index("fsdp")
    return {"fsdp": shard + 1 - 2 * (shard % 2)}


def to_z_partner(line, jump):
    return {"fsdp": lax.rem(lax.axis_index("fsdp") + 2 * jump, 2 * line)}


class Gather:
    def __init__(self, line, shard, own, other, sems, split=False):
        self.line, self.shard, self.own, self.other = line, shard, own, other
        self.sems = sems
        z, y, x, _ = seats()
        self.z, self.y = z, y
        rows = own.shape[2]
        if split:
            self.rows = pl.ds(pl.multiple_of(x * (rows // 2), rows // 2), rows // 2)
        else:
            self.rows = pl.ds(0, rows)

    def here(self):
        return pltpu.make_async_copy(
            self.shard.at[self.rows, :],
            self.own.at[self.z, self.y, self.rows, :],
            self.sems.at[0, self.line + 2],
        )

    def along_z(self):
        return [
            send(
                self.shard.at[self.rows, :],
                self.own.at[self.z, self.y, self.rows, :],
                self.sems,
                jump - 1,
                to_z_partner(self.line, jump),
            )
            for jump in range(1, self.line)
        ]

    def along_y(self):
        part = self.own.at[:, self.y, self.rows, :]
        return send(part, part, self.sems, self.line - 1, to_y_partner())

    def along_x(self):
        part = self.own.at[:, :, self.rows, :]
        return send(part, part, self.sems, self.line, to_x_partner())

    def along_core(self):
        return send(self.own, self.other, self.sems, self.line + 1, to_core_partner())

    def start_z(self):
        self.here().start()
        for copy in self.along_z():
            copy.start()

    def wait_z(self):
        self.here().wait()
        for copy in self.along_z():
            copy.wait()


def gather_sems(line):
    return pltpu.SemaphoreType.DMA((2, line + 3))


def front_kernel(line, tok, *refs):
    (
        inputs,
        firsts,
        q_shard,
        k_shard,
        v_shard,
        o_shard,
        d_shard,
        cos_ref,
        sin_ref,
        x_received,
        f_received,
        heads_own,
        heads_received,
        normed_ref,
        full_ref,
        gains_ref,
        o_own,
        o_other,
        d_own,
        xs,
        fs,
        q_own,
        q_other,
        k_own,
        k_other,
        v_own,
        v_other,
        outgoing,
        q_sems,
        k_sems,
        v_sems,
        o_sems,
        d_sems,
        swap_sems,
        head_sems,
        local_sems,
    ) = refs
    step = pl.program_id(0)
    _, _, side, core = seats()
    wide = outgoing.shape[1]
    depth = 2 * wide
    gathers = [
        Gather(line, q_shard, q_own, q_other, q_sems),
        Gather(line, k_shard, k_own, k_other, k_sems),
        Gather(line, v_shard, v_own, v_other, v_sems),
    ]
    query, key, value = gathers
    out = Gather(line, o_shard, o_own, o_other, o_sems)
    down = Gather(line, d_shard, d_own, d_own, d_sems, split=True)
    swap_x = send(inputs.at[1 - side], x_received, swap_sems, 0, to_x_partner())
    swap_f = send(firsts.at[1 - side], f_received, swap_sems, 1, to_x_partner())
    load_x = pltpu.make_async_copy(inputs.at[side], xs.at[pl.ds(0, tok), :], local_sems.at[0])
    load_f = pltpu.make_async_copy(firsts.at[side], fs.at[pl.ds(0, tok), :], local_sems.at[1])
    more_x = pltpu.make_async_copy(x_received, xs.at[pl.ds(tok, tok), :], local_sems.at[2])
    more_f = pltpu.make_async_copy(f_received, fs.at[pl.ds(tok, tok), :], local_sems.at[3])

    def weight(halves, columns):
        return halves[:, :, :, columns].reshape(depth, wide)

    def heads(number):
        return send(
            outgoing.at[number], heads_received.at[number], head_sems, number, to_core_partner()
        )

    saves = []
    for number, (mine, others) in enumerate(((q_own, q_other), (k_own, k_other), (v_own, v_other))):
        for which, ref in ((0, mine), (1, others)):
            half = core if which == 0 else 1 - core
            saves.append(
                pltpu.make_async_copy(
                    ref.at[:, :, :, pl.ds(0, wide)],
                    full_ref.at[half, number],
                    local_sems.at[4 + 2 * number + which],
                )
            )

    @pl.when(step == 0)
    def _():
        meet(line, ("z", "y", "x", "core"))
        swap_x.start()
        load_x.start()
        load_f.start()
        query.start_z()
        query.wait_z()
        query.along_y().start()
        key.start_z()
        key.wait_z()
        key.along_y().start()
        value.start_z()
        query.along_y().wait()
        query.along_core().start()
        swap_x.wait()
        more_x.start()
        swap_f.start()
        value.wait_z()
        value.along_y().start()
        out.start_z()
        key.along_y().wait()
        key.along_core().start()
        load_x.wait()
        more_x.wait()
        value.along_y().wait()
        value.along_core().start()
        columns = v_own[:, :, :, wide:].reshape(depth, 128)
        gains_ref[...] = columns.astype(F32).T[:8]
        gain = gains_ref[0:1, :]
        chunk = min(256, 2 * tok)

        def norm(number, _):
            at = pl.ds(pl.multiple_of(number * chunk, chunk), chunk)
            values = xs[at, :].astype(F32)
            scale = lax.rsqrt(jnp.mean(values * values, axis=1, keepdims=True) + epsilon)
            normed_ref[at, :] = (values * scale * gain).astype(BF16)
            return 0

        lax.fori_loop(0, 2 * tok // chunk, norm, 0)

    @pl.when(step == 2)
    def _():
        out.wait_z()
        out.along_y().start()
        down.start_z()
        swap_f.wait()
        more_f.start()
        load_f.wait()
        more_f.wait()

    @pl.when(step == 3)
    def _():
        query.along_core().wait()
        key.along_core().wait()
        value.along_core().wait()
        for save in saves:
            save.start()

    @pl.when(step == 5)
    def _():
        out.along_y().wait()
        out.along_core().start()

    def project_one(halves, kind, mine):
        raw = nt(weight(halves, slice(0, wide)).T, normed_ref[...])
        if kind < 2:
            parts = raw.reshape(wide // HEAD_DIM, 2, HALF, raw.shape[1])
            first, second = parts[:, 0], parts[:, 1]
            cosine, sine = cos_ref[...][None], sin_ref[...][None]
            turned = jnp.stack(
                [first * cosine - second * sine, first * sine + second * cosine], axis=1
            )
            result = turned.reshape(raw.shape).astype(BF16)
        else:
            half = core if mine else 1 - core
            first = fs[:, pl.ds(pl.multiple_of(half * wide, wide), wide)]
            result = (0.5 * raw + 0.5 * first.astype(F32).T).astype(BF16)
        if mine:
            heads_own[0] = result
        else:
            outgoing[kind] = result
            heads(kind).start()

    for number, (halves, kind, mine) in enumerate(
        (
            (q_own, 0, True),
            (k_own, 1, True),
            (v_own, 2, True),
            (q_other, 0, False),
            (k_other, 1, False),
            (v_other, 2, False),
        )
    ):

        @pl.when(step == number)
        def _(halves=halves, kind=kind, mine=mine):
            project_one(halves, kind, mine)

    @pl.when(step == 5)
    def _():
        for number in range(3):
            heads(number).wait()
        for save in saves:
            save.wait()
        out.along_core().wait()
        down.wait_z()


def front(inputs, firsts, q, k, v, o, d, cosine, sine, line):
    slots, tok, depth = inputs.shape
    span = slots * tok
    wide = depth // 2
    rows, down_rows = q.shape[0], d.shape[0]
    anywhere = pl.BlockSpec(memory_space=pl.ANY)
    weights = lambda columns: pltpu.VMEM((line, 2, rows, columns), BF16)
    return pl.pallas_call(
        functools.partial(front_kernel, line, tok),
        grid=(6,),
        in_specs=[anywhere] * 7 + [whole_block((HALF, span))] * 2,
        out_specs=[
            anywhere,
            anywhere,
            pl.BlockSpec((1, wide, span), lambda s: (jnp.minimum(s, 2), 0, 0)),
            anywhere,
            whole_block((span, depth)),
            anywhere,
            whole_block((8, depth)),
            anywhere,
            anywhere,
            anywhere,
        ],
        out_shape=[
            jax.ShapeDtypeStruct((tok, depth), BF16),
            jax.ShapeDtypeStruct((tok, depth), BF16),
            jax.ShapeDtypeStruct((3, wide, span), BF16),
            jax.ShapeDtypeStruct((3, wide, span), BF16),
            jax.ShapeDtypeStruct((span, depth), BF16),
            jax.ShapeDtypeStruct((2, 3, line, 2, rows, wide), BF16),
            jax.ShapeDtypeStruct((8, depth), F32),
            jax.ShapeDtypeStruct((line, 2, rows, wide), BF16),
            jax.ShapeDtypeStruct((line, 2, rows, wide), BF16),
            jax.ShapeDtypeStruct((line, 2, down_rows, wide), BF16),
        ],
        scratch_shapes=[
            pltpu.VMEM((span, depth), BF16),
            pltpu.VMEM((span, depth), BF16),
            weights(wide),
            weights(wide),
            weights(wide),
            weights(wide),
            weights(v.shape[1]),
            weights(v.shape[1]),
            pltpu.VMEM((3, wide, span), BF16),
        ]
        + [gather_sems(line)] * 5
        + [
            pltpu.SemaphoreType.DMA((2, 2)),
            pltpu.SemaphoreType.DMA((2, 3)),
            pltpu.SemaphoreType.DMA((10,)),
        ],
        compiler_params=pltpu.CompilerParams(
            dimension_semantics=("arbitrary",),
            vmem_limit_bytes=56 * MIB,
            collective_id=1,
            has_side_effects=True,
        ),
        cost_estimate=pl.CostEstimate(
            flops=6 * span * depth * depth,
            bytes_accessed=2 * (8 * span * depth + 6 * depth * depth),
            transcendentals=0,
        ),
        name="front",
    )(inputs, firsts, q, k, v, o, d, cosine, sine)


def block_of(source, slot, tok):
    _, _, side, core = seats()
    rank = 1 - core if source == 0 else core
    group = lax.rem(side + slot, 2)
    return pl.ds(pl.multiple_of((group * 2 + rank) * tok, tok), tok)


def attend_carry_kernel(line, tok, tile_k, *refs):
    (
        received,
        own,
        grad_in,
        d_in,
        g_shard,
        u_shard,
        mix_received,
        mix_own,
        lse_ref,
        att_other,
        grad_received,
        d_own,
        d_other,
        g_own,
        g_other,
        u_own,
        u_other,
        qz,
        kn,
        vt,
        ot,
        outgoing,
        d_sems,
        g_sems,
        u_sems,
        swap_sems,
        att_sems,
    ) = refs
    step = pl.program_id(0)
    pairs = pl.num_programs(0)
    _, _, side, _ = seats()
    down = Gather(line, d_in, d_own, d_other, d_sems, split=True)
    gate = Gather(line, g_shard, g_own, g_other, g_sems, split=True)
    up = Gather(line, u_shard, u_own, u_other, u_sems)
    swap = send(grad_in.at[1 - side], grad_received, swap_sems, 0, to_x_partner())
    pieces = (received, own)

    def hand_over(number):
        rows = pl.ds(number * PAIR, PAIR)
        return send(
            outgoing.at[rows, :], att_other.at[rows, :], att_sems, number, to_core_partner()
        )

    @pl.when(step == 0)
    def _():
        meet(line, ("z", "y", "x", "core"))
        down.along_y().start()
        gate.start_z()
        swap.start()

    @pl.when(step == 2)
    def _():
        gate.wait_z()
        gate.along_y().start()
        up.start_z()

    @pl.when(step == 3)
    def _():
        down.along_y().wait()
        down.along_x().start()

    for source in range(2):
        for slot in range(2):
            cols = block_of(source, slot, tok)
            take = slice(slot * tok, (slot + 1) * tok)
            query = pieces[source][0, :, take] * jnp.asarray(HEAD_DIM**-0.5, BF16)
            for head in range(2):
                qz[head, :, cols] = head_rows(query, head)
            kn[cols, :] = pieces[source][1, :, take].T
            vt[:, cols] = pieces[source][2, :, take]
    attend_body(4 * tok, tile_k, qz, kn, vt, ot, lse_ref)
    for slot in range(2):
        take = slice(slot * tok, (slot + 1) * tok)
        theirs = ot[:, block_of(0, slot, tok)]
        mix_received[:, take] = theirs
        for number in range(4):

            @pl.when(step == number)
            def _(number=number, theirs=theirs, take=take):
                outgoing[number * PAIR : (number + 1) * PAIR, take] = theirs

        mix_own[:, take] = ot[:, block_of(1, slot, tok)]
    for number in range(4):

        @pl.when(step == number)
        def _(number=number):
            hand_over(number).start()

    @pl.when(step == pairs - 1)
    def _():
        gate.along_y().wait()
        up.wait_z()
        up.along_y().start()
        down.along_x().wait()
        swap.wait()
        gate.along_x().start()
        down.along_core().start()
        up.along_y().wait()
        up.along_core().start()
        gate.along_x().wait()
        gate.along_core().start()
        for number in range(4):
            hand_over(number).wait()
        down.along_core().wait()
        up.along_core().wait()
        gate.along_core().wait()


def attend_carry(received, own, grads, d_own, gate, up, line):
    _, width, span = own.shape
    tok = span // 2
    length = 2 * span
    pairs = width // PAIR
    rows, down_rows = gate.shape[0], d_own.shape[2]
    depth = grads.shape[2]
    anywhere = pl.BlockSpec(memory_space=pl.ANY)
    triple = pl.BlockSpec((3, PAIR, span), lambda p: (0, p, 0))
    single = pl.BlockSpec((PAIR, span), lambda p: (p, 0))
    whole_gate = jax.ShapeDtypeStruct((line, 2, rows, gate.shape[1]), BF16)
    whole_down = jax.ShapeDtypeStruct((line, 2, down_rows, d_own.shape[3]), BF16)
    area = pairs * 2 * length * length // 2
    return pl.pallas_call(
        functools.partial(attend_carry_kernel, line, tok, min(256, length)),
        grid=(pairs,),
        in_specs=[triple, triple] + [anywhere] * 4,
        out_specs=[single, single, pl.BlockSpec((1, 8, length), lambda p: (p, 0, 0))]
        + [anywhere] * 8,
        out_shape=[
            jax.ShapeDtypeStruct((width, span), BF16),
            jax.ShapeDtypeStruct((width, span), BF16),
            jax.ShapeDtypeStruct((pairs, 8, length), F32),
            jax.ShapeDtypeStruct((width, span), BF16),
            jax.ShapeDtypeStruct((tok, depth), BF16),
            whole_down,
            whole_down,
            whole_gate,
            whole_gate,
            whole_gate,
            whole_gate,
        ],
        scratch_shapes=[
            pltpu.VMEM((2, PAIR, length), BF16),
            pltpu.VMEM((length, PAIR), BF16),
            pltpu.VMEM((PAIR, length), BF16),
            pltpu.VMEM((PAIR, length), BF16),
            pltpu.VMEM((width, span), BF16),
        ]
        + [gather_sems(line)] * 3
        + [pltpu.SemaphoreType.DMA((2, 1)), pltpu.SemaphoreType.DMA((2, 4))],
        input_output_aliases={3: 5},
        compiler_params=pltpu.CompilerParams(
            dimension_semantics=("arbitrary",),
            vmem_limit_bytes=48 * MIB,
            collective_id=2,
            has_side_effects=True,
        ),
        cost_estimate=pl.CostEstimate(
            flops=area * 1024, bytes_accessed=8 * width * length, transcendentals=area
        ),
        name="attend_carry",
    )(received, own, grads, d_own, gate, up)


def mlp_carry_kernel(line, tok, blocks, *refs):
    (
        grads,
        grads_received,
        middle_ref,
        normed_ref,
        gains_ref,
        g_own,
        g_other,
        u_own,
        u_other,
        d_own_own,
        d_own_other,
        d_other_own,
        d_other_other,
        out_ref,
        send_ref,
        grad_ref,
        low_ref,
        gain_ref,
        gu_ref,
        d_ref,
        gu_y,
        og,
        normed_t,
        acc,
        back,
        gu_kept,
        d_kept,
        gu_sent,
        d_sent,
        gu_landed,
        d_landed,
        gu_outgoing,
        down_full,
        local_sems,
        gu_sends,
        gu_recvs,
        d_sends,
        d_recvs,
        y_sems,
    ) = refs
    step = pl.program_id(0)
    _, y, side, core = seats()
    depth = og.shape[1]
    wide = depth // 2
    strip = 128
    rows = gu_kept.shape[4]
    mine = pl.ds(pl.multiple_of(core * wide, wide), wide)
    others = pl.ds(pl.multiple_of((1 - core) * wide, wide), wide)

    def core_copies(number):
        slot = lax.rem(number, 2)
        return [
            pltpu.make_async_remote_copy(
                src_ref=source.at[slot],
                dst_ref=target.at[number],
                send_sem=sends.at[slot],
                recv_sem=recvs.at[number],
                device_id=to_core_partner(),
                device_id_type=MESH,
            )
            for source, target, sends, recvs in (
                (gu_sent, gu_landed, gu_sends, gu_recvs),
                (d_sent, d_landed, d_sends, d_recvs),
            )
        ]

    def y_copy(number):
        return send(gu_outgoing.at[number], gu_y.at[number], y_sems, number, to_y_partner())

    @pl.when(step == 0)
    def _():
        meet(line, ("y", "core"))
        loads = [
            pltpu.make_async_copy(grads.at[side], og.at[pl.ds(0, tok), :], local_sems.at[0]),
            pltpu.make_async_copy(grads_received, og.at[pl.ds(tok, tok), :], local_sems.at[1]),
        ]
        for load in loads:
            load.start()
        normed_t[...] = normed_ref[...].T
        acc[...] = jnp.zeros_like(acc)
        back[...] = jnp.zeros_like(back)
        for load in loads:
            load.wait()

    @pl.when(step < blocks)
    def _():
        slot = lax.rem(step, 2)
        gate_w = jnp.concatenate([g_own[...], g_other[...]], axis=1)
        up_w = jnp.concatenate([u_own[...], u_other[...]], axis=1)
        for number, pair in enumerate(
            ((d_own_own, d_own_other), (d_other_own, d_other_other))
        ):
            at = pl.ds(number * strip, strip)
            down_full[at, mine] = pair[0][...]
            down_full[at, others] = pair[1][...]
        down_w = down_full[...]
        normed = normed_ref[...]
        gate = dot(normed, gate_w)
        up = dot(normed, up_w)
        grad_active = nt(og[...], down_w)
        sigma = jax.nn.sigmoid(gate)
        silu = gate * sigma
        active = (silu * up).astype(BF16)
        grad_up = (grad_active * silu).astype(BF16)
        grad_gate = (grad_active * up * sigma * (1.0 + gate * (1.0 - sigma))).astype(BF16)

        @pl.when(step >= 2)
        def _():
            for copy in core_copies(step - 2):
                copy.wait_send()

        for number, grad in enumerate((grad_gate, grad_up)):
            result = dot(normed_t[...], grad).astype(BF16)
            shaped = result.reshape(line, 2, rows, 2 * strip)
            gu_kept[slot, number] = shaped[..., :strip]
            gu_sent[slot, number] = shaped[..., strip:]
        active_t = active.T
        kept = dot(active_t, og[:, mine]).astype(BF16)
        d_kept[slot, core] = kept[:strip]
        d_kept[slot, 1 - core] = kept[strip:]
        sent = dot(active_t, og[:, others]).astype(BF16)
        d_sent[slot, core] = sent[:strip]
        d_sent[slot, 1 - core] = sent[strip:]
        for copy in core_copies(step):
            copy.start()
        acc[...] += dot(active, down_w)
        back[...] += nt(grad_gate, gate_w) + nt(grad_up, up_w)

    @pl.when(step > 0)
    def _():
        number = step - 1
        slot = lax.rem(number, 2)
        for copy in core_copies(number):
            copy.wait_recv()
        for which in range(2):
            theirs = gu_kept[slot, which, :, 1 - y].astype(F32)
            theirs = theirs + gu_landed[number, which, :, 1 - y].astype(F32)
            gu_outgoing[number, which] = theirs.astype(BF16)
            ours = gu_kept[slot, which, :, y].astype(F32)
            ours = ours + gu_landed[number, which, :, y].astype(F32)
            gu_ref[0, which] = ours.astype(BF16)
        y_copy(number).start()
        d_ref[...] = (d_kept[slot].astype(F32) + d_landed[number].astype(F32)).astype(BF16)

    @pl.when(step == blocks)
    def _():
        gain = gains_ref[1:2, :]
        chunk = min(128, tok)
        gain_ref[...] = jnp.zeros_like(gain_ref)
        for slot in range(2):

            def finish(number, _, slot=slot):
                local = pl.ds(pl.multiple_of(number * chunk, chunk), chunk)
                some = pl.ds(pl.multiple_of(slot * tok + number * chunk, chunk), chunk)
                middle = middle_ref[some, :]
                scale = lax.rsqrt(jnp.mean(middle * middle, axis=1, keepdims=True) + epsilon)
                result = middle + acc[some, :]
                if slot == 0:
                    out_ref[0, local, :] = result
                else:
                    send_ref[local, :] = result.astype(BF16)
                grad = back[some, :]
                gain_ref[0:1, :] += jnp.sum(grad * middle * scale, axis=0, keepdims=True)
                weighted = grad * gain
                inner = jnp.mean(weighted * middle, axis=1, keepdims=True)
                grad_middle = (
                    scale * weighted
                    - middle * (scale * scale * scale) * inner
                    + og[some, :].astype(F32)
                )
                grad_ref[some, :] = grad_middle
                low_ref[some, :] = grad_middle.astype(BF16)
                return 0

            lax.fori_loop(0, tok // chunk, finish, 0)
        for number in (blocks - 2, blocks - 1):
            for copy in core_copies(number):
                copy.wait_send()
        for number in range(blocks):
            y_copy(number).wait()


def mlp_carry(grads, grads_received, middle, normed, gains, gate, up, down, line):
    slots, tok, depth = grads.shape
    half_width = gate[0].shape[1]
    wide = depth // 2
    span = slots * tok
    blocks = half_width // 128
    rows = depth // (2 * line)
    once = pl.Buffered(1)
    anywhere = pl.BlockSpec(memory_space=pl.ANY)

    def now(s):
        return jnp.minimum(s, blocks - 1)

    def done(s):
        return jnp.maximum(s - 1, 0)

    def core():
        return lax.axis_index("seq") % 2

    column = pl.BlockSpec((depth, 128), lambda s: (0, now(s)))
    own_rows = pl.BlockSpec((128, wide), lambda s: (core() * blocks + now(s), 0))
    other_rows = pl.BlockSpec((128, wide), lambda s: ((1 - core()) * blocks + now(s), 0))
    full = pl.BlockSpec((span, depth), lambda s: (0, 0), pipeline_mode=once)
    return pl.pallas_call(
        functools.partial(mlp_carry_kernel, line, tok, blocks),
        grid=(blocks + 1,),
        in_specs=[anywhere, anywhere, full, full, whole_block((8, depth))]
        + [column] * 4
        + [own_rows, own_rows, other_rows, other_rows],
        out_specs=[
            pl.BlockSpec(
                (1, tok, depth), lambda s: (lax.axis_index("seq") // 2, 0, 0), pipeline_mode=once
            ),
            pl.BlockSpec((tok, depth), lambda s: (0, 0), pipeline_mode=once),
            full,
            full,
            whole_block((8, depth)),
            pl.BlockSpec((1, 2, line, rows, 128), lambda s: (done(s), 0, 0, 0, 0)),
            pl.BlockSpec((2, 128, wide), lambda s: (0, done(s), 0)),
            anywhere,
        ],
        out_shape=[
            jax.ShapeDtypeStruct((slots, tok, depth), F32),
            jax.ShapeDtypeStruct((tok, depth), BF16),
            jax.ShapeDtypeStruct((span, depth), F32),
            jax.ShapeDtypeStruct((span, depth), BF16),
            jax.ShapeDtypeStruct((8, depth), F32),
            jax.ShapeDtypeStruct((blocks, 2, line, rows, 128), BF16),
            jax.ShapeDtypeStruct((2, half_width, wide), BF16),
            jax.ShapeDtypeStruct((blocks, 2, line, rows, 128), BF16),
        ],
        scratch_shapes=[
            pltpu.VMEM((span, depth), BF16),
            pltpu.VMEM((depth, span), BF16),
            pltpu.VMEM((span, depth), F32),
            pltpu.VMEM((span, depth), F32),
            pltpu.VMEM((2, 2, line, 2, rows, 128), BF16),
            pltpu.VMEM((2, 2, 128, wide), BF16),
            pltpu.VMEM((2, 2, line, 2, rows, 128), BF16),
            pltpu.VMEM((2, 2, 128, wide), BF16),
            pltpu.VMEM((blocks, 2, line, 2, rows, 128), BF16),
            pltpu.VMEM((blocks, 2, 128, wide), BF16),
            pltpu.VMEM((blocks, 2, line, rows, 128), BF16),
            pltpu.VMEM((256, depth), BF16),
            pltpu.SemaphoreType.DMA((2,)),
            pltpu.SemaphoreType.DMA((2,)),
            pltpu.SemaphoreType.DMA((blocks,)),
            pltpu.SemaphoreType.DMA((2,)),
            pltpu.SemaphoreType.DMA((blocks,)),
            pltpu.SemaphoreType.DMA((2, blocks)),
        ],
        compiler_params=pltpu.CompilerParams(
            dimension_semantics=("arbitrary",),
            vmem_limit_bytes=63 * MIB,
            collective_id=3,
            has_side_effects=True,
        ),
        cost_estimate=pl.CostEstimate(
            flops=16 * span * depth * 2 * half_width,
            bytes_accessed=24 * depth * half_width + 20 * span * depth,
            transcendentals=2 * span * half_width,
        ),
        name="mlp_carry",
    )(
        grads,
        grads_received,
        middle,
        normed,
        gains,
        *gate,
        *up,
        down[0],
        down[1],
        down[0],
        down[1],
    )


def grad_attended_carry_kernel(
    line,
    low_ref,
    full_ref,
    att_other,
    att_own,
    ga_own,
    ga_received,
    o_ref,
    o_landed,
    outgoing,
    o_sent,
    sems,
):
    step = pl.program_id(0)
    _, _, _, core = seats()
    wide = att_own.shape[0]
    mine = pl.ds(pl.multiple_of(core * wide, wide), wide)
    others = pl.ds(pl.multiple_of((1 - core) * wide, wide), wide)
    heads = send(outgoing, ga_received, sems, 0, to_core_partner())

    def sums(number):
        half = 1 - core if number == 0 else core
        at = pl.ds(pl.multiple_of(half * wide, wide), wide)
        return send(o_sent.at[number], o_landed.at[at, :], sems, 1 + number, to_core_partner())

    @pl.when(step == 0)
    def _():
        meet(line, ("core",))
        outgoing[...] = nt(full_ref[...], low_ref[...]).astype(BF16)
        heads.start()

    @pl.when(step == 1)
    def _():
        ga_own[...] = nt(full_ref[...], low_ref[...]).astype(BF16)

    for number, att in enumerate((att_other, att_own)):

        @pl.when(step == number)
        def _(number=number, att=att):
            o_sent[number] = dot(att[...], low_ref[:, others]).astype(BF16)
            sums(number).start()
            o_ref[...] = dot(att[...], low_ref[:, mine]).astype(BF16)

    @pl.when(step == 1)
    def _():
        heads.wait()
        for number in range(2):
            sums(number).wait()


def grad_attended_carry(low, full, att_other, att_own, line):
    span, depth = low.shape
    wide = depth // 2

    def half(s):
        core = lax.axis_index("seq") % 2
        return jnp.where(s == 0, 1 - core, core)

    anywhere = pl.BlockSpec(memory_space=pl.ANY)
    return pl.pallas_call(
        functools.partial(grad_attended_carry_kernel, line),
        grid=(2,),
        in_specs=[
            whole_block((span, depth)),
            pl.BlockSpec((wide, depth), lambda s: (half(s), 0)),
            whole_block((wide, span)),
            whole_block((wide, span)),
        ],
        out_specs=[
            whole_block((wide, span)),
            anywhere,
            pl.BlockSpec((wide, wide), lambda s: (half(s), 0)),
            anywhere,
        ],
        out_shape=[
            jax.ShapeDtypeStruct((wide, span), BF16),
            jax.ShapeDtypeStruct((wide, span), BF16),
            jax.ShapeDtypeStruct((depth, wide), BF16),
            jax.ShapeDtypeStruct((depth, wide), BF16),
        ],
        scratch_shapes=[
            pltpu.VMEM((wide, span), BF16),
            pltpu.VMEM((2, wide, wide), BF16),
            pltpu.SemaphoreType.DMA((2, 3)),
        ],
        compiler_params=pltpu.CompilerParams(
            dimension_semantics=("arbitrary",),
            vmem_limit_bytes=48 * MIB,
            collective_id=4,
            has_side_effects=True,
        ),
        cost_estimate=pl.CostEstimate(
            flops=4 * span * depth * depth,
            bytes_accessed=6 * span * depth + 4 * depth * depth,
            transcendentals=0,
        ),
        name="grad_attended_carry",
    )(low, full, att_other, att_own)


def attend_back_carry_kernel(line, tok, tile_q, tile_k, *refs):
    (
        received,
        own,
        mix_received,
        mix_own,
        grad_received,
        grad_own,
        lse_ref,
        cos_ref,
        sin_ref,
        outputs_sent,
        gu_in,
        gu_y,
        d_in,
        o_in,
        o_landed,
        back_own,
        back_other,
        outputs_received,
        gu_mine,
        gu_z,
        d_y,
        o_kept,
        o_y,
    ) = refs[:23]
    (
        qz,
        gz,
        qn,
        gn,
        kn,
        vn,
        kt,
        inner,
        dq,
        dk,
        dv,
        outgoing,
        gu_a,
        gu_b,
        o_a,
        o_b,
        local_sems,
        back_sems,
        z_sems,
        other_sems,
    ) = refs[23:]
    step = pl.program_id(0)
    pairs = pl.num_programs(0)
    z, y, _, _ = seats()
    length = 4 * tok
    swap = send(outputs_sent, outputs_received, other_sems, 0, to_x_partner())
    d_send = send(d_in.at[:, 1 - y], d_y, other_sems, 1, to_y_partner())
    o_send = send(o_a.at[:, 1 - y], o_y, other_sems, 2, to_y_partner())

    def z_send(jump):
        target = lax.rem(z + jump, line)
        return send(
            gu_a.at[:, :, target], gu_z.at[jump - 1], z_sems, jump - 1, to_z_partner(line, jump)
        )

    stays = [
        pltpu.make_async_copy(gu_a.at[:, :, z], gu_mine, local_sems.at[4]),
        pltpu.make_async_copy(o_a.at[:, y], o_kept, local_sems.at[5]),
    ]

    def hand_over(number):
        rows = pl.ds(number * PAIR, PAIR)
        return send(
            outgoing.at[:, rows, :],
            back_other.at[:, rows, :],
            back_sems,
            number,
            to_core_partner(),
        )

    @pl.when(step == 0)
    def _():
        meet(line, ("z", "y", "x", "core"))
        swap.start()
        loads = [
            pltpu.make_async_copy(source, target, local_sems.at[number])
            for number, (source, target) in enumerate(
                ((o_in, o_a), (o_landed, o_b), (gu_in, gu_a), (gu_y, gu_b))
            )
        ]
        for load in loads:
            load.start()
        loads[0].wait()
        loads[1].wait()
        o_a[...] = (o_a[...].astype(F32) + o_b[...].astype(F32)).astype(BF16)
        o_send.start()
        d_send.start()
        loads[2].wait()
        loads[3].wait()

        def add(number, _):
            total = gu_a[number].astype(F32) + gu_b[number].astype(F32)
            gu_a[number] = total.astype(BF16)
            return 0

        lax.fori_loop(0, gu_a.shape[0], add, 0)
        for jump in range(1, line):
            z_send(jump).start()
        for copy in stays:
            copy.start()

    attend_back_body(
        (received, own),
        (mix_received, mix_own),
        (grad_received, grad_own),
        lambda source, slot: block_of(source, slot, tok),
        tok,
        length,
        tile_q,
        tile_k,
        lse_ref,
        qz,
        gz,
        qn,
        gn,
        kn,
        vn,
        kt,
        inner,
        dq,
        dk,
        dv,
    )
    for slot in range(2):
        take = slice(slot * tok, (slot + 1) * tok)
        for source in range(2):
            cols = block_of(source, slot, tok)
            results = turn_back(dq, dk, dv, cols, cos_ref[:, cols], sin_ref[:, cols])
            for which, result in enumerate(results):
                if source == 1:
                    back_own[which, :, take] = result
                else:
                    at = pl.ds(pl.multiple_of(step * PAIR, PAIR), PAIR)
                    outgoing[which, at, take] = result

    for number in range(4):

        @pl.when(step == number)
        def _(number=number):
            hand_over(number).start()

    @pl.when(step == pairs - 1)
    def _():
        swap.wait()
        d_send.wait()
        o_send.wait()
        for copy in stays:
            copy.wait()
        for jump in range(1, line):
            z_send(jump).wait()
        for number in range(4):
            hand_over(number).wait()


def attend_back_carry(
    pieces, mixes, grads, lse, cosine, sine, outputs_sent, gu, gu_y, d, o, o_landed, line
):
    _, width, span = pieces[0].shape
    tok = span // 2
    length = 2 * span
    pairs = width // PAIR
    tile_q = min(512, length)
    tile_k = min(256, length)
    anywhere = pl.BlockSpec(memory_space=pl.ANY)
    triple = pl.BlockSpec((3, PAIR, span), lambda p: (0, p, 0))
    single = pl.BlockSpec((PAIR, span), lambda p: (p, 0))
    table = pl.BlockSpec((HALF, length), lambda p: (0, 0))
    blocks, _, _, rows, _ = gu.shape
    down_rows, wide = d.shape[2:]
    area = pairs * 2 * length * length // 2
    return pl.pallas_call(
        functools.partial(attend_back_carry_kernel, line, tok, tile_q, tile_k),
        grid=(pairs,),
        in_specs=[triple] * 2
        + [single] * 4
        + [pl.BlockSpec((1, 8, length), lambda p: (p, 0, 0)), table, table]
        + [anywhere] * 6,
        out_specs=[triple] + [anywhere] * 7,
        out_shape=[
            jax.ShapeDtypeStruct((3, width, span), BF16),
            jax.ShapeDtypeStruct((3, width, span), BF16),
            jax.ShapeDtypeStruct(outputs_sent.shape, BF16),
            jax.ShapeDtypeStruct((blocks, 2, rows, 128), BF16),
            jax.ShapeDtypeStruct((line - 1, blocks, 2, rows, 128), BF16),
            jax.ShapeDtypeStruct((line, down_rows, wide), BF16),
            jax.ShapeDtypeStruct((line, rows, wide), BF16),
            jax.ShapeDtypeStruct((line, rows, wide), BF16),
        ],
        scratch_shapes=[
            pltpu.VMEM((2, PAIR, length), BF16),
            pltpu.VMEM((2, PAIR, length), BF16),
            pltpu.VMEM((2, length, PAIR), BF16),
            pltpu.VMEM((2, length, PAIR), BF16),
            pltpu.VMEM((length, PAIR), BF16),
            pltpu.VMEM((length, PAIR), BF16),
            pltpu.VMEM((PAIR, length), BF16),
            pltpu.VMEM((8, length), F32),
            pltpu.VMEM((PAIR, length), F32),
            pltpu.VMEM((length, PAIR), F32),
            pltpu.VMEM((length, PAIR), F32),
            pltpu.VMEM((3, width, span), BF16),
            pltpu.VMEM((blocks, 2, line, rows, 128), BF16),
            pltpu.VMEM((blocks, 2, line, rows, 128), BF16),
            pltpu.VMEM((line, 2, rows, wide), BF16),
            pltpu.VMEM((line, 2, rows, wide), BF16),
            pltpu.SemaphoreType.DMA((6,)),
            pltpu.SemaphoreType.DMA((2, 4)),
            pltpu.SemaphoreType.DMA((2, line - 1)),
            pltpu.SemaphoreType.DMA((2, 3)),
        ],
        compiler_params=pltpu.CompilerParams(
            dimension_semantics=("arbitrary",),
            vmem_limit_bytes=60 * MIB,
            collective_id=5,
            has_side_effects=True,
        ),
        cost_estimate=pl.CostEstimate(
            flops=area * 2560, bytes_accessed=16 * width * length, transcendentals=area
        ),
        name="attend_back_carry",
    )(
        *pieces, *mixes, *grads, lse, cosine, sine, outputs_sent, gu, gu_y, d, o, o_landed
    )


def tail_carry_kernel(line, tok, blocks, *refs):
    (
        inputs,
        x_received,
        back_other,
        back_own,
        full_ref,
        normed_ref,
        grad_in,
        gains_ref,
        mlp_gain_ref,
        gu_mine,
        gu_z,
        d_in,
        d_y,
        o_in,
        o_y,
        input_grad,
        first_grad,
        gain_out,
        q_out,
        k_out,
        v_out,
        o_out,
        g_out,
        u_out,
        d_out,
        xs,
        grad_middle,
        normed_t,
        acc,
        grad,
        sent,
        landed,
        y_landed,
        z_landed,
        d_a,
        d_b,
        d_landed,
        o_a,
        o_b,
        o_landed,
        gu_a,
        gu_b,
        gu_x,
        gu_c,
        d_low,
        d_x,
        d_c,
        s_low,
        s_x,
        s_c,
        first_stage,
        first_send,
        first_landed,
        input_send,
        input_landed,
        gain,
        gain_landed,
        local_sems,
        core_sems,
        y_sems,
        z_sems,
        dz_sems,
        oz_sems,
        x_sems,
        c_sems,
        token_sems,
        gain_sems,
    ) = refs
    step = pl.program_id(0)
    target, turn = step // 3, lax.rem(step, 3)
    z, y, side, core = seats()
    wide, span = grad.shape
    depth = 2 * wide
    half = jnp.where(target == 0, 1 - core, core)
    columns = pl.ds(pl.multiple_of(half * wide, wide), wide)
    mine = pl.ds(pl.multiple_of(core * wide, wide), wide)
    others = pl.ds(pl.multiple_of((1 - core) * wide, wide), wide)

    def load(source, place, number):
        return pltpu.make_async_copy(source, place, local_sems.at[number])

    load_tokens = [
        load(inputs.at[side], xs.at[pl.ds(0, tok), :], 0),
        load(x_received, xs.at[pl.ds(tok, tok), :], 1),
        load(grad_in, grad_middle, 2),
    ]
    store_input = load(acc.at[pl.ds(0, tok), :], input_grad.at[side], 3)
    store_input_other = load(acc.at[pl.ds(tok, tok), :], input_grad.at[1 - side], 4)
    store_first = load(first_stage, first_grad.at[side], 5)
    store_first_other = load(first_stage, first_grad.at[1 - side], 6)

    def along_z(source, place, sems, base=0):
        return [
            send(
                source(lax.rem(z + jump, line)),
                place(jump - 1),
                sems,
                base + jump - 1,
                to_z_partner(line, jump),
            )
            for jump in range(1, line)
        ]

    d_sends = along_z(lambda at: d_a.at[at], lambda jump: d_landed.at[jump], dz_sems)
    o_sends = along_z(lambda at: o_a.at[at], lambda jump: o_landed.at[jump], oz_sems)

    def core_send(number):
        return send(sent.at[number], landed.at[number], core_sems, number, to_core_partner())

    def y_send(number):
        return send(
            landed.at[number, :, 1 - y], y_landed.at[number], y_sems, number, to_y_partner()
        )

    def z_sends(number):
        return along_z(
            lambda at: landed.at[number, at, y],
            lambda jump: z_landed.at[number, jump],
            z_sems,
            number * (line - 1),
        )

    def first_part(number):
        which = 1 - core if number == 0 else core
        at = pl.ds(pl.multiple_of(which * wide, wide), wide)
        return send(
            first_send.at[:, at], first_landed.at[:, at], token_sems, number, to_x_partner()
        )

    input_part = send(input_send, input_landed, token_sems, 2, to_x_partner())
    gu_sides = (
        send(gu_a, gu_x, x_sems, 0, to_x_partner()),
        send(gu_a, gu_c, c_sems, 0, to_core_partner()),
    )
    d_sides = (
        send(d_low, d_x, x_sems, 1, to_x_partner()),
        send(d_low, d_c, c_sems, 1, to_core_partner()),
    )

    def square_x(number):
        return send(s_low.at[number], s_x.at[number], x_sems, 2 + number, to_x_partner())

    def square_core(number):
        return send(s_low.at[number], s_c.at[number], c_sems, 2 + number, to_core_partner())

    squares = (o_out, v_out, q_out, k_out)

    def gain_send(number, partner):
        return send(gain.at[number], gain_landed.at[number], gain_sems, number, partner)

    @pl.when(step == 0)
    def _():
        meet(line, ("z", "y", "x", "core"))
        sources = ((d_in.at[:, y], d_a), (d_y, d_b), (o_in, o_a), (o_y, o_b), (gu_mine, gu_a), (gu_z, gu_b))
        loads = [load(source, place, 7 + n) for n, (source, place) in enumerate(sources)]
        for copy in loads:
            copy.start()
        for copy in load_tokens:
            copy.start()
        for copy in loads[:4]:
            copy.wait()
        for at in range(line):
            d_a[at] = (d_a[at].astype(F32) + d_b[at].astype(F32)).astype(BF16)
            o_a[at] = (o_a[at].astype(F32) + o_b[at].astype(F32)).astype(BF16)
        for copy in d_sends + o_sends:
            copy.start()
        for copy in loads[4:]:
            copy.wait()

        def total(number, _):
            for which, out in enumerate((g_out, u_out)):
                value = gu_a[number, which].astype(F32)
                for jump in range(line - 1):
                    value = value + gu_b[jump, number, which].astype(F32)
                at = pl.ds(pl.multiple_of((core * blocks + number) * 128, 128), 128)
                out[:, at] = value
                gu_a[number, which] = value.astype(BF16)
            return 0

        lax.fori_loop(0, blocks, total, 0)
        gu_sides[0].start()
        normed_t[...] = normed_ref[...].T
        acc[...] = jnp.zeros_like(acc)

    def own_part(back):
        @pl.when(turn == 0)
        def _():
            value = 0.5 * back[0].astype(F32)
            rows = value.T
            first_stage[:, columns] = rows[:tok]
            first_send[:, columns] = rows[tok:].astype(BF16)
            grad[...] = value.astype(BF16)

        @pl.when(turn > 0)
        def _():
            grad[...] = back[0]

    @pl.when(target == 0)
    def _():
        own_part(back_other)

    @pl.when(target == 1)
    def _():
        own_part(back_own)

    @pl.when(step == 0)
    def _():
        first_part(0).start()

    @pl.when(step == 3)
    def _():
        first_part(1).start()
        store_first.start()

    @pl.when(target < 2)
    def _():
        value = grad[...]
        result = nt(normed_t[...], value)

        @pl.when(target == 0)
        def _():
            sent[turn] = result.astype(BF16).reshape(sent.shape[1:])
            core_send(turn).start()

        @pl.when(target == 1)
        def _():
            core_send(turn).wait()
            theirs = landed[turn].reshape(result.shape).astype(F32)
            landed[turn] = (result + theirs).astype(BF16).reshape(landed.shape[1:])
            y_send(turn).start()

        acc[...] += nt(value.T, full_ref[0, 0])

    @pl.when(step == 6)
    def _():
        for copy in load_tokens:
            copy.wait()
        weight = gains_ref[0:1, :]
        chunk = min(128, tok)
        gain[...] = jnp.zeros_like(gain)
        gain[0, 1:2, :] = mlp_gain_ref[0:1, :]
        for slot in (1, 0):

            def finish(number, _, slot=slot):
                local = pl.ds(pl.multiple_of(number * chunk, chunk), chunk)
                some = pl.ds(pl.multiple_of(slot * tok + number * chunk, chunk), chunk)
                values = xs[some, :].astype(F32)
                scale = lax.rsqrt(jnp.mean(values * values, axis=1, keepdims=True) + epsilon)
                value = acc[some, :]
                gain[0, 0:1, :] += jnp.sum(value * values * scale, axis=0, keepdims=True)
                weighted = value * weight
                inner = jnp.mean(weighted * values, axis=1, keepdims=True)
                result = (
                    scale * weighted
                    - values * (scale * scale * scale) * inner
                    + grad_middle[some, :]
                )
                if slot == 0:
                    acc[some, :] = result
                else:
                    input_send[local, :] = result.astype(BF16)
                return 0

            lax.fori_loop(0, tok // chunk, finish, 0)
            if slot == 1:
                input_part.start()
        gain_send(0, to_core_partner()).start()
        store_input.start()
        gu_sides[0].wait()

        def gather_x(number, _):
            for which, out in enumerate((g_out, u_out)):
                at = pl.ds(pl.multiple_of((core * blocks + number) * 128, 128), 128)
                value = out[:, at] + gu_x[number, which].astype(F32)
                out[:, at] = value
                gu_a[number, which] = value.astype(BF16)
            return 0

        lax.fori_loop(0, blocks, gather_x, 0)
        gu_sides[1].start()
        gain_send(0, to_core_partner()).wait()
        gain[1] = gain[0] + gain_landed[0]
        gain_send(1, to_y_partner()).start()
        for number in range(3):
            y_send(number).wait()

            def add(at, _, number=number):
                value = landed[number, at, y].astype(F32) + y_landed[number, at].astype(F32)
                landed[number, at, y] = value.astype(BF16)
                return 0

            lax.fori_loop(0, line, add, 0)
            for copy in z_sends(number):
                copy.start()
            if number == 0:
                gain_send(1, to_y_partner()).wait()
                gain[2] = gain[1] + gain_landed[1]
                for jump in range(1, line):
                    gain_z(jump, line, gain, gain_landed, gain_sems).start()
        for copy in d_sends + o_sends:
            copy.wait()

        def sum_z(own, places):
            value = own.astype(F32)
            for place in places:
                value = value + place.astype(F32)
            return value

        value = sum_z(d_a[z], [d_landed[jump] for jump in range(line - 1)])
        d_out[:, mine] = value
        d_low[...] = value.astype(BF16)
        d_sides[0].start()
        value = sum_z(o_a[z], [o_landed[jump] for jump in range(line - 1)])
        o_out[:, mine] = value
        s_low[0] = value.astype(BF16)
        square_x(0).start()
        for jump in range(1, line):
            gain_z(jump, line, gain, gain_landed, gain_sems).wait()
        value = gain[2]
        for jump in range(1, line):
            value = value + gain_landed[1 + jump]
        gain[3] = value
        last_gain = send(gain.at[3], gain_landed.at[line + 1], gain_sems, line + 1, to_x_partner())
        last_gain.start()
        for number in range(3):
            for copy in z_sends(number):
                copy.wait()
            value = sum_z(
                landed[number, z, y], [z_landed[number, jump] for jump in range(line - 1)]
            )
            squares[1 + number][:, mine] = value
            s_low[1 + number] = value.astype(BF16)
            square_x(1 + number).start()
        last_gain.wait()
        gain[4] = gain[3] + gain_landed[line + 1]
        gain_out[...] = gain[4, :, pl.ds(pl.multiple_of((2 * z + y) * 128, 128), 128)]
        store_first.wait()
        for number in range(2):
            first_part(number).wait()
        first_stage[...] = first_landed[...].astype(F32)
        store_first_other.start()
        d_sides[0].wait()
        value = d_out[:, mine] + d_x[...].astype(F32)
        d_out[:, mine] = value
        d_low[...] = value.astype(BF16)
        d_sides[1].start()
        input_part.wait()
        acc[pl.ds(tok, tok), :] = input_landed[...].astype(F32)
        store_input_other.start()
        for number in range(4):
            square_x(number).wait()
            value = squares[number][:, mine] + s_x[number].astype(F32)
            squares[number][:, mine] = value
            s_low[number] = value.astype(BF16)
            square_core(number).start()
        gu_sides[1].wait()

        def gather_core(number, _):
            for which, out in enumerate((g_out, u_out)):
                at = pl.ds(pl.multiple_of(((1 - core) * blocks + number) * 128, 128), 128)
                out[:, at] = gu_c[number, which].astype(F32)
            return 0

        lax.fori_loop(0, blocks, gather_core, 0)
        d_sides[1].wait()
        d_out[:, others] = d_c[...].astype(F32)
        for number in range(4):
            square_core(number).wait()
            squares[number][:, others] = s_c[number].astype(F32)
        store_input.wait()
        store_input_other.wait()
        store_first_other.wait()


def gain_z(jump, line, gain, gain_landed, gain_sems):
    return send(
        gain.at[2], gain_landed.at[1 + jump], gain_sems, 1 + jump, to_z_partner(line, jump)
    )


def tail_carry(
    inputs,
    x_received,
    back_other,
    back_own,
    full,
    normed,
    grad_middle,
    gains,
    mlp_gain,
    gu_mine,
    gu_z,
    d,
    d_y,
    o,
    o_y,
    line,
):
    slots, tok, depth = inputs.shape
    span = slots * tok
    wide = depth // 2
    blocks, _, rows, _ = gu_mine.shape
    down_rows = d.shape[2]
    once = pl.Buffered(1)
    anywhere = pl.BlockSpec(memory_space=pl.ANY)

    def half(s):
        core = lax.axis_index("seq") % 2
        return jnp.where(s < 3, 1 - core, core)

    def kind(s):
        return (s + 2) % 3

    def clear(shape):
        zeros = (0,) * len(shape)
        return pl.BlockSpec(shape, lambda s: zeros, pipeline_mode=once)

    square = jax.ShapeDtypeStruct((rows, depth), F32)
    broad = jax.ShapeDtypeStruct((rows, 2 * blocks * 128), F32)
    tall = jax.ShapeDtypeStruct((down_rows, depth), F32)
    tokens = jax.ShapeDtypeStruct((slots, tok, depth), F32)
    finals = [square] * 4 + [broad] * 2 + [tall]
    vmem = pltpu.VMEM
    dma = pltpu.SemaphoreType.DMA
    return pl.pallas_call(
        functools.partial(tail_carry_kernel, line, tok, blocks),
        grid=(7,),
        in_specs=[
            anywhere,
            anywhere,
            pl.BlockSpec((1, wide, span), lambda s: (kind(jnp.minimum(s, 2)), 0, 0)),
            pl.BlockSpec((1, wide, span), lambda s: (kind(jnp.clip(s, 3, 5)), 0, 0)),
            pl.BlockSpec(
                (1, 1, depth, wide),
                lambda s: (half(jnp.minimum(s, 5)), kind(jnp.minimum(s, 5)), 0, 0),
            ),
            clear((span, depth)),
            anywhere,
            clear((8, depth)),
            clear((8, depth)),
        ]
        + [anywhere] * 6,
        out_specs=[anywhere, anywhere, clear((8, 128))] + [clear(final.shape) for final in finals],
        out_shape=[tokens, tokens, jax.ShapeDtypeStruct((8, 128), F32)] + finals,
        scratch_shapes=[
            vmem((span, depth), BF16),
            vmem((span, depth), F32),
            vmem((depth, span), BF16),
            vmem((span, depth), F32),
            vmem((wide, span), BF16),
            vmem((3, line, 2, rows, wide), BF16),
            vmem((3, line, 2, rows, wide), BF16),
            vmem((3, line, rows, wide), BF16),
            vmem((3, line - 1, rows, wide), BF16),
            vmem((line, down_rows, wide), BF16),
            vmem((line, down_rows, wide), BF16),
            vmem((line - 1, down_rows, wide), BF16),
            vmem((line, rows, wide), BF16),
            vmem((line, rows, wide), BF16),
            vmem((line - 1, rows, wide), BF16),
            vmem((blocks, 2, rows, 128), BF16),
            vmem((line - 1, blocks, 2, rows, 128), BF16),
            vmem((blocks, 2, rows, 128), BF16),
            vmem((blocks, 2, rows, 128), BF16),
            vmem((down_rows, wide), BF16),
            vmem((down_rows, wide), BF16),
            vmem((down_rows, wide), BF16),
            vmem((4, rows, wide), BF16),
            vmem((4, rows, wide), BF16),
            vmem((4, rows, wide), BF16),
            vmem((tok, depth), F32),
            vmem((tok, depth), BF16),
            vmem((tok, depth), BF16),
            vmem((tok, depth), BF16),
            vmem((tok, depth), BF16),
            vmem((5, 8, depth), F32),
            vmem((line + 2, 8, depth), F32),
            dma((13,)),
            dma((2, 3)),
            dma((2, 3)),
            dma((2, 3 * (line - 1))),
            dma((2, line - 1)),
            dma((2, line - 1)),
            dma((2, 6)),
            dma((2, 6)),
            dma((2, 3)),
            dma((2, line + 2)),
        ],
        compiler_params=pltpu.CompilerParams(
            dimension_semantics=("arbitrary",),
            vmem_limit_bytes=63 * MIB,
            collective_id=6,
            has_side_effects=True,
        ),
        cost_estimate=pl.CostEstimate(
            flops=12 * span * depth * depth,
            bytes_accessed=24 * span * depth + 12 * depth * depth,
            transcendentals=0,
        ),
        name="tail_carry",
    )(
        inputs,
        x_received,
        back_other,
        back_own,
        full,
        normed,
        grad_middle,
        gains,
        mlp_gain,
        gu_mine,
        gu_z,
        d,
        d_y,
        o,
        o_y,
    )


def shards(
    inputs,
    first_values,
    out_grad,
    attn_gain,
    query_weight,
    key_weight,
    value_weight,
    output_weight,
    mlp_gain,
    gate_weight,
    up_weight,
    down_weight,
):
    slots, tok, _ = inputs.shape
    groups = lax.axis_size("seq")
    parts = lax.axis_size("fsdp")
    line = parts // 2
    count = groups // slots
    length = tok * groups
    span = slots * tok
    seat = lax.axis_index("seq")
    shard = lax.axis_index("fsdp")
    side = seat // count
    rank = seat % count
    core = seat % 2
    z, y = shard // 2, shard % 2
    wide = D // 2
    width = D // count

    def along_seq(value, partner):
        return lax.ppermute(value, "seq", [(i, partner(i)) for i in range(groups)])

    def along_fsdp(value, partner):
        return lax.ppermute(value, "fsdp", [(i, partner(i)) for i in range(parts)])

    def to_core(value):
        return along_seq(value, lambda i: i ^ 1)

    def to_y(value):
        return along_fsdp(value, lambda i: i ^ 1)

    def to_z(value, jump):
        return along_fsdp(value, lambda i: (i + 2 * jump) % parts)

    def after(value, *others):
        return lax.optimization_barrier((value,) + others)[0]

    def to_sequence(values):
        taken = []
        for jump in range(1, slots):
            sent = lax.dynamic_index_in_dim(values, (side + jump) % slots, 0, keepdims=False)
            taken.append(along_seq(sent, lambda i: (i + jump * count) % groups))
        return taken

    def to_home(whole, sent):
        for jump in range(1, slots):
            part = sent[(jump - 1) * tok : jump * tok]
            part = along_seq(part, lambda i: (i - jump * count) % groups)
            whole = land(whole, part, ((side + jump) % slots)[None])
        return whole

    def rank_up(i, jump):
        return (i // count) * count + (i % count + jump) % count

    def rank_down(i, jump):
        return (i // count) * count + (i % count - jump) % count

    def halves_to_ranks(other, own, axis):
        if count == 2:
            return [other, own]
        return [
            lax.dynamic_slice_in_dim(
                join(other, own, axis), ((rank + 1 + number) % count) * width, width, axis
            )
            for number in range(count)
        ]

    def join(other, own, axis):
        first = jnp.where(core == 0, own, other)
        second = jnp.where(core == 0, other, own)
        return jnp.concatenate([first, second], axis=axis)

    def ranks_to_halves(pieces, axis):
        if count == 2:
            return pieces
        shape = list(pieces[0].shape)
        shape[axis] = D
        whole = jnp.zeros(shape, pieces[0].dtype)
        for number in range(count):
            whole = lax.dynamic_update_slice_in_dim(
                whole, pieces[number], ((rank + 1 + number) % count) * width, axis
            )
        return [
            lax.dynamic_slice_in_dim(whole, which * wide, wide, axis)
            for which in (1 - core, core)
        ]

    def exchange(pieces):
        received = [
            along_seq(pieces[jump - 1], lambda i: rank_up(i, jump)) for jump in range(1, count)
        ]
        return received + [pieces[count - 1]]

    def exchange_back(pieces):
        received = [
            along_seq(pieces[jump - 1], lambda i: rank_down(i, jump)) for jump in range(1, count)
        ]
        return received + [pieces[count - 1]]

    def split(*weights):
        results = []
        for which in (core, 1 - core):
            columns = []
            for weight in weights:
                size = weight.shape[1] // 2
                columns.append(lax.dynamic_slice_in_dim(weight, which * size, size, 1))
            results.append(columns)
        return results

    def gather_z(half):
        return [half] + [to_z(half, jump) for jump in range(1, line)]

    def gather_rest(along_z, other):
        along_y = [to_y(piece) for piece in along_z]
        own = [piece for pair in zip(along_z, along_y) for piece in pair]
        return (own, [other] + [to_core(piece) for piece in own[1:]])

    numbers = []
    for jump in range(line):
        for flip in range(2):
            numbers.append(((z - jump) % line) * 2 + (y ^ flip))
    place = jnp.stack([side, core] + numbers).astype(jnp.int32)

    def low(value):
        return value.astype(BF16)

    def add(a, b):
        return low(a.astype(F32) + b.astype(F32))

    def pick(value, index, axis):
        return lax.dynamic_index_in_dim(value, index, axis, keepdims=False)

    def along_x_and_core(total):
        mine = low(total)
        for jump in range(1, groups // 2):
            total = total + along_seq(mine, lambda i: (i + 2 * jump) % groups).astype(F32)
        mine = low(total)
        return (mine, to_core(mine))

    def along_z_and_on(partial):
        total = partial(z)
        for jump in range(1, line):
            total = total + to_z(low(partial((z + jump) % line)), jump).astype(F32)
        return along_x_and_core(total)

    def scatter(sent, kept, rows_axis):
        shape = kept.shape
        rows = shape[rows_axis] // parts
        cut = shape[:rows_axis] + (line, 2, rows) + shape[rows_axis + 1 :]
        received = to_core(sent).reshape(cut)
        kept = kept.reshape(cut)
        axis = rows_axis + 1
        received_y = to_y(add(pick(kept, 1 - y, axis), pick(received, 1 - y, axis)))
        kept_y = pick(kept, y, axis), pick(received, y, axis)

        def partial(index):
            total = pick(kept_y[0], index, rows_axis).astype(F32)
            total = total + pick(kept_y[1], index, rows_axis).astype(F32)
            return total + pick(received_y, index, rows_axis).astype(F32)

        return along_z_and_on(partial)

    def columns(mine, others):
        first = jnp.where(core == 0, mine, others)
        second = jnp.where(core == 0, others, mine)
        return jnp.concatenate([first, second], axis=-1).astype(F32)

    def everywhere(value):
        value = value + to_core(value)
        value = value + to_y(value)
        total = value
        for jump in range(1, line):
            total = total + to_z(value, jump)
        value = total
        for jump in range(1, groups // 2):
            total = total + along_seq(value, lambda i: (i + 2 * jump) % groups)
        return total

    steps = jnp.arange(slots, dtype=jnp.int32)
    starts = ((side - steps) % slots) * (count * tok) + rank * tok
    positions = (starts[:, None] + jnp.arange(tok, dtype=jnp.int32)[None]).reshape(span)
    freqs = rope_base ** (-(jnp.arange(HALF, dtype=F32) * 2.0 / HEAD_DIM))

    def tables(positions):
        angles = freqs[:, None] * positions.astype(F32)[None, :]
        return (jnp.cos(angles), jnp.sin(angles))

    cosine, sine = tables(positions)
    full_cos, full_sin = tables(jnp.arange(length, dtype=jnp.int32))
    sources = jnp.concatenate(
        [(rank - 1 - jnp.arange(count - 1, dtype=jnp.int32)) % count, rank[None]]
    ).astype(jnp.int32)
    order = (((side - steps) % slots)[None, :] * count + sources[:, None]).reshape(-1)
    order = order.astype(jnp.int32)

    gains = jnp.pad(jnp.stack([attn_gain, mlp_gain], axis=1), ((0, 0), (0, 126)))
    gate_halves, up_halves, out_halves, down_halves = (
        [half[0] for half in split(weight)]
        for weight in (gate_weight, up_weight, output_weight, down_weight)
    )

    whole_lanes = (slots, count) == (2, 2) and (D // parts) % 128 == 0
    if whole_lanes:
        parts_of = lambda ref: [ref.reshape(-1, ref.shape[-1])]
        (q_half,), (k_half,), (v_half,) = (
            split(weight)[:1] for weight in (query_weight, key_weight, value_weight)
        )
        (
            tokens,
            firsts,
            heads_own,
            heads_received,
            normed,
            qkv_full,
            gains_full,
            out_own,
            out_other,
            down_own,
        ) = front(
            inputs,
            first_values,
            q_half[0],
            k_half[0],
            jnp.concatenate([v_half[0], gains], axis=1),
            out_halves[0],
            down_halves[0],
            cosine,
            sine,
            line,
        )
        qkv_full = qkv_full.reshape(2, 3, D, wide)
        tokens = [tokens]
        pieces = [heads_received, heads_own]
        (
            mix_received,
            att_own,
            lse,
            att_other,
            grads,
            down_own,
            down_other,
            gate_own,
            gate_other,
            up_own,
            up_other,
        ) = attend_carry(
            heads_received, heads_own, out_grad, down_own, gate_halves[0], up_halves[0], line
        )
        mixes = [mix_received, att_own]
        grads = [grads]
        layout = jnp.stack([side, core, 0 * core]).astype(jnp.int32)
        out_own, out_other = parts_of(out_own), parts_of(out_other)
        gate_pieces = parts_of(gate_own), parts_of(gate_other)
        up_pieces = parts_of(up_own), parts_of(up_other)
        down_pieces = parts_of(down_own), parts_of(down_other)
    else:
        qkv = [
            jnp.concatenate(half + [gains], axis=1)
            for half in split(query_weight, key_weight, value_weight)
        ]
        layout = place
        tokens = to_sequence(inputs)
        firsts = to_sequence(first_values)
        grads = to_sequence(out_grad)
        qkv_own, qkv_other = gather_rest(gather_z(qkv[0]), qkv[1])
        out_own, out_other = gather_rest(gather_z(out_halves[0]), out_halves[1])
        gate_pieces = gather_rest(gather_z(gate_halves[0]), gate_halves[1])
        up_pieces = gather_rest(gather_z(up_halves[0]), up_halves[1])
        down_pieces = gather_rest(gather_z(down_halves[0]), down_halves[1])
        heads_other, heads_own, normed, qkv_full, gains_full = project(
            inputs, tokens, first_values, firsts, qkv_own, qkv_other, cosine, sine, place
        )
        pieces = exchange(halves_to_ranks(heads_other, heads_own, 1))
        mixes, lse = attend(pieces, order, slots)
        att_other, att_own = ranks_to_halves(exchange_back(mixes), 0)

    middle, normed2, out_full = output_projection(
        inputs, tokens, out_own, out_other, att_other, att_own, gains_full, layout
    )
    if whole_lanes:
        (
            outputs,
            outputs_sent,
            grad_middle,
            low_grad,
            mlp_gain_grad,
            gu_reduced,
            down_reduced,
            gu_y,
        ) = mlp_carry(
            out_grad,
            grads[0],
            middle,
            normed2,
            gains_full,
            (gate_pieces[0][0], gate_pieces[1][0]),
            (up_pieces[0][0], up_pieces[1][0]),
            (down_pieces[0][0], down_pieces[1][0]),
            line,
        )
        ga_own, ga_received, out_kept, out_landed = grad_attended_carry(
            low_grad, out_full, att_other, att_own, line
        )
        down_reduced = down_reduced.reshape(line, 2, -1, wide)
        out_kept = out_kept.reshape(line, 2, -1, wide)
        out_landed = out_landed.reshape(line, 2, -1, wide)
        (
            back_own,
            back_other,
            outputs_received,
            gu_mine,
            gu_z,
            down_y,
            out_mine,
            out_y,
        ) = attend_back_carry(
            pieces,
            mixes,
            [ga_received, ga_own],
            lse,
            full_cos,
            full_sin,
            outputs_sent,
            gu_reduced,
            gu_y,
            down_reduced,
            out_kept,
            out_landed,
            line,
        )
        outputs = land(outputs, outputs_received, (1 - side)[None])
        (
            input_grad,
            first_grad,
            gain_grads,
            query_grad,
            key_grad,
            value_grad,
            output_grad,
            gate_grad,
            up_grad,
            down_grad,
        ) = tail_carry(
            inputs,
            tokens[0],
            back_other,
            back_own,
            qkv_full,
            normed,
            grad_middle,
            gains_full,
            mlp_gain_grad,
            gu_mine,
            gu_z,
            down_reduced,
            down_y,
            out_mine,
            out_y,
            line,
        )
    else:
        (
            outputs,
            outputs_sent,
            grad_middle,
            low_grad,
            mlp_gain_grad,
            gu_sent,
            gu_kept,
            down_sent,
            down_kept,
        ) = mlp(out_grad, grads, middle, normed2, gains_full, gate_pieces, up_pieces, down_pieces, layout)
        ga_other, ga_own, out_sent, out_kept = grad_attended(
            low_grad, out_full, att_other, att_own, place
        )
        gate_up_grad = scatter(gu_sent, gu_kept, 1)
        down_grad = scatter(down_sent.reshape(-1, wide), down_kept.reshape(-1, wide), 0)
        output_grad = scatter(out_sent, out_kept, 0)
        grad_heads = exchange(halves_to_ranks(ga_other, ga_own, 0))
        back = attend_back(pieces, mixes, grad_heads, lse, full_cos, full_sin, order, slots)
        back_other, back_own = ranks_to_halves(exchange_back(back), 1)
        outputs = to_home(outputs, outputs_sent)
        input_grad, input_sent, first_grad, first_sent, gain_grads, qkv_sent, qkv_kept = tail(
            inputs,
            tokens,
            back_other,
            back_own,
            qkv_full,
            normed,
            grad_middle,
            gains_full,
            mlp_gain_grad,
            place,
        )
        query_grad, key_grad, value_grad = columns(*scatter(qkv_sent, qkv_kept, 1))
        gate_grad, up_grad = columns(*gate_up_grad)
        output_grad = columns(*output_grad)
        down_grad = columns(*down_grad)
        gain_grads = everywhere(gain_grads)
        gain_grads = lax.dynamic_slice_in_dim(gain_grads, shard * (D // parts), D // parts, 1)
        input_grad = to_home(input_grad, input_sent)
        first_grad = to_home(first_grad, first_sent)

    return (
        outputs,
        input_grad,
        first_grad,
        gain_grads[0],
        gain_grads[1],
        query_grad,
        key_grad,
        value_grad,
        output_grad,
        gate_grad,
        up_grad,
        down_grad,
    )


def solution(mesh):
    token_spec = P("fsdp", "seq", None)
    weight_spec = P("fsdp", None)
    gain_spec = P("fsdp")
    return jax.shard_map(
        shards,
        mesh=mesh,
        in_specs=(token_spec,) * 3
        + (gain_spec,)
        + (weight_spec,) * 4
        + (gain_spec,)
        + (weight_spec,) * 3,
        out_specs=(token_spec,) * 3 + (gain_spec,) * 2 + (weight_spec,) * 7,
        check_vma=False,
    )
```

```python
import functools
import math

import jax
import jax.numpy as jnp
from jax import lax
from jax.experimental import pallas as pl
from jax.experimental.pallas import tpu as pltpu
from jax.sharding import PartitionSpec as P

D = 1024
HEADS = 16
HEAD_DIM = 64
HALF = HEAD_DIM // 2
PAIR = 2 * HEAD_DIM
F32 = jnp.float32
BF16 = jnp.bfloat16
NEG = -1e30
MIB = 1024 * 1024
epsilon = 1e-06
rope_base = 10000.0


def dot(a, b):
    return lax.dot_general(a, b, (((1,), (0,)), ((), ())), preferred_element_type=F32)


def head_rows(value, head):
    row = lax.broadcasted_iota(jnp.int32, value.shape, 0)
    return jnp.where((row // HEAD_DIM) == head, value, jnp.zeros_like(value))


def head_lanes(value, head):
    lane = lax.broadcasted_iota(jnp.int32, value.shape, 1)
    return jnp.where((lane // HEAD_DIM) == head, value, jnp.zeros_like(value))


def causal(scores):
    side = scores.shape[0]
    square = scores[:, :side]
    key = lax.broadcasted_iota(jnp.int32, square.shape, 0)
    query = lax.broadcasted_iota(jnp.int32, square.shape, 1)
    square = jnp.where(key <= query, square, NEG)
    if scores.shape[1] == side:
        return square
    return jnp.concatenate([square, scores[:, side:]], axis=1)


def attend_body(length, tile_k, qz, kn, vt, ot, lse_ref):
    def score(sub, head):
        start = sub * tile_k
        return causal(dot(kn[start : start + tile_k, :], qz[head, :, start:]))

    def absorb(sub, head, carry, scores):
        peak, total, mixed = carry
        start = sub * tile_k
        new_peak = jnp.maximum(peak, jnp.max(scores, axis=0, keepdims=True))
        weights = jnp.exp(scores - new_peak)
        fade = jnp.exp(peak - new_peak)
        total = total * fade + jnp.sum(weights, axis=0, keepdims=True)
        values = vt[head * HEAD_DIM : (head + 1) * HEAD_DIM, start : start + tile_k]
        mixed = mixed * fade + dot(values, weights.astype(BF16))
        return (new_peak, total, mixed)

    tiles = [(sub, head) for sub in range(length // tile_k) for head in range(2)]
    carries = [
        (
            jnp.full((1, length), NEG, F32),
            jnp.zeros((1, length), F32),
            jnp.zeros((HEAD_DIM, length), F32),
        )
        for _ in range(2)
    ]
    ahead = score(*tiles[0])
    for number, (sub, head) in enumerate(tiles):
        scores = ahead
        if number + 1 < len(tiles):
            ahead = score(*tiles[number + 1])
        peak, total, mixed = absorb(sub, head, carries[head], scores)
        done = slice(sub * tile_k, (sub + 1) * tile_k)
        rows = slice(head * HEAD_DIM, (head + 1) * HEAD_DIM)
        ot[rows, done] = (mixed[:, :tile_k] / total[:, :tile_k]).astype(BF16)
        lse_ref[0, head : head + 1, done] = peak[:, :tile_k] + jnp.log(total[:, :tile_k])
        carries[head] = (peak[:, tile_k:], total[:, tile_k:], mixed[:, tile_k:])


def attend_kernel(count, slots, tok, tile_k, order, *refs):
    pieces = refs[:count]
    outs = refs[count : 2 * count]
    lse_ref = refs[2 * count]
    qz, kn, vt, ot = refs[2 * count + 1 :]
    for source in range(count):
        for slot in range(slots):
            cols = pl.ds(pl.multiple_of(order[source * slots + slot] * tok, tok), tok)
            take = slice(slot * tok, (slot + 1) * tok)
            query = pieces[source][0, :, take] * jnp.asarray(HEAD_DIM**-0.5, BF16)
            for head in range(2):
                qz[head, :, cols] = head_rows(query, head)
            kn[cols, :] = pieces[source][1, :, take].T
            vt[:, cols] = pieces[source][2, :, take]
    length = count * slots * tok
    attend_body(length, tile_k, qz, kn, vt, ot, lse_ref)
    for source in range(count):
        for slot in range(slots):
            cols = pl.ds(pl.multiple_of(order[source * slots + slot] * tok, tok), tok)
            outs[source][:, slot * tok : (slot + 1) * tok] = ot[:, cols]


def attend(pieces, order, slots):
    count = len(pieces)
    width, span = pieces[0].shape[1:]
    tok = span // slots
    length = count * span
    pairs = width // PAIR
    tile_k = min(256, length)
    grid_spec = pltpu.PrefetchScalarGridSpec(
        num_scalar_prefetch=1,
        grid=(pairs,),
        in_specs=[pl.BlockSpec((3, PAIR, span), lambda p, o: (0, p, 0))] * count,
        out_specs=[pl.BlockSpec((PAIR, span), lambda p, o: (p, 0))] * count
        + [pl.BlockSpec((1, 8, length), lambda p, o: (p, 0, 0))],
        scratch_shapes=[
            pltpu.VMEM((2, PAIR, length), BF16),
            pltpu.VMEM((length, PAIR), BF16),
            pltpu.VMEM((PAIR, length), BF16),
            pltpu.VMEM((PAIR, length), BF16),
        ],
    )
    area = pairs * 2 * length * length // 2
    results = pl.pallas_call(
        functools.partial(attend_kernel, count, slots, tok, tile_k),
        out_shape=[jax.ShapeDtypeStruct((width, span), BF16)] * count
        + [jax.ShapeDtypeStruct((pairs, 8, length), F32)],
        grid_spec=grid_spec,
        compiler_params=pltpu.CompilerParams(
            dimension_semantics=("arbitrary",), vmem_limit_bytes=48 * MIB
        ),
        cost_estimate=pl.CostEstimate(
            flops=area * 1024, bytes_accessed=8 * width * length, transcendentals=area
        ),
        name="attend",
    )(order, *pieces)
    return (results[:count], results[count])


def attend_back_body(
    pieces,
    mixes,
    grads,
    columns,
    tok,
    length,
    tile_q,
    tile_k,
    lse_ref,
    qz,
    gz,
    qn,
    gn,
    kn,
    vn,
    kt,
    inner,
    dq,
    dk,
    dv,
):
    slots = pieces[0].shape[2] // tok
    for source in range(len(pieces)):
        for slot in range(slots):
            cols = columns(source, slot)
            take = slice(slot * tok, (slot + 1) * tok)
            query = pieces[source][0, :, take] * jnp.asarray(HEAD_DIM**-0.5, BF16)
            grad = grads[source][:, take]
            query_rows = query.T
            grad_rows = grad.T
            for head in range(2):
                qz[head, :, cols] = head_rows(query, head)
                gz[head, :, cols] = head_rows(grad, head)
                qn[head, cols, :] = head_lanes(query_rows, head)
                gn[head, cols, :] = head_lanes(grad_rows, head)
            key = pieces[source][1, :, take]
            kt[:, cols] = key
            kn[cols, :] = key.T
            vn[cols, :] = pieces[source][2, :, take].T
            both = grad.astype(F32) * mixes[source][:, take].astype(F32)
            for head in range(2):
                inner[head : head + 1, cols] = jnp.sum(
                    both[head * HEAD_DIM : (head + 1) * HEAD_DIM], axis=0, keepdims=True
                )
    dq[...] = jnp.zeros_like(dq)
    steps = tile_q // tile_k

    def tile(key_start, query_start, width, masked, carry):
        grad_keys, grad_values = carry
        keys = kn[pl.ds(key_start, tile_k), :]
        values = vn[pl.ds(key_start, tile_k), :]
        cols = pl.ds(query_start, width)
        for head in range(2):
            rows = slice(head * HEAD_DIM, (head + 1) * HEAD_DIM)
            scores = dot(keys, qz[head, :, cols])
            if masked:
                scores = causal(scores)
            probs = jnp.exp(scores - lse_ref[0, head : head + 1, cols])
            grad_probs = dot(values, gz[head, :, cols])
            grad_scores = (probs * (grad_probs - inner[head : head + 1, cols])).astype(BF16)
            grad_values = grad_values + dot(probs.astype(BF16), gn[head, cols, :])
            grad_keys = grad_keys + dot(grad_scores, qn[head, cols, :])
            dq[rows, cols] += dot(kt[rows, pl.ds(key_start, tile_k)], grad_scores)
        return (grad_keys, grad_values)

    def one(number, _):
        base = pl.multiple_of(number * tile_q, tile_q)
        for sub in range(steps):
            skip = sub * tile_k
            key_start = pl.multiple_of(base + skip, tile_k)
            carry = (jnp.zeros((tile_k, PAIR), F32), jnp.zeros((tile_k, PAIR), F32))
            carry = tile(key_start, key_start, tile_q - skip, True, carry)

            def body(step, carry):
                return tile(
                    key_start, pl.multiple_of(step * tile_q, tile_q), tile_q, False, carry
                )

            carry = lax.fori_loop(number + 1, length // tile_q, body, carry)
            dk[pl.ds(key_start, tile_k), :] = carry[0]
            dv[pl.ds(key_start, tile_k), :] = carry[1]
        return 0

    lax.fori_loop(0, length // tile_q, one, 0)


def turn_back(dq, dk, dv, cols, cosine, sine):
    half = HEAD_DIM // 2
    results = []
    for grad in (dq[:, cols] * (HEAD_DIM**-0.5), dk[cols, :].T):
        turned = []
        for head in range(2):
            low = head * HEAD_DIM
            first = grad[low : low + half]
            second = grad[low + half : low + 2 * half]
            turned += [first * cosine + second * sine, second * cosine - first * sine]
        results.append(jnp.concatenate(turned, axis=0).astype(BF16))
    results.append(dv[cols, :].T.astype(BF16))
    return results


def attend_back_kernel(count, slots, tok, tile_q, tile_k, order, *refs):
    pieces = refs[:count]
    mixes = refs[count : 2 * count]
    grads = refs[2 * count : 3 * count]
    lse_ref, cos_ref, sin_ref = refs[3 * count : 3 * count + 3]
    outs = refs[3 * count + 3 : 4 * count + 3]
    scratch = refs[4 * count + 3 :]
    dq, dk, dv = scratch[-3:]

    def columns(source, slot):
        return pl.ds(pl.multiple_of(order[source * slots + slot] * tok, tok), tok)

    attend_back_body(
        pieces,
        mixes,
        grads,
        columns,
        tok,
        count * slots * tok,
        tile_q,
        tile_k,
        lse_ref,
        *scratch,
    )
    for source in range(count):
        for slot in range(slots):
            cols = columns(source, slot)
            results = turn_back(dq, dk, dv, cols, cos_ref[:, cols], sin_ref[:, cols])
            for which, result in enumerate(results):
                outs[source][which, :, slot * tok : (slot + 1) * tok] = result


def attend_back(pieces, mixes, grads, lse, cosine, sine, order, slots):
    count = len(pieces)
    width, span = pieces[0].shape[1:]
    tok = span // slots
    length = count * span
    pairs = width // PAIR
    tile_q = min(512, length)
    tile_k = min(256, length)
    triple = pl.BlockSpec((3, PAIR, span), lambda p, o: (0, p, 0))
    single = pl.BlockSpec((PAIR, span), lambda p, o: (p, 0))
    table = pl.BlockSpec((HEAD_DIM // 2, length), lambda p, o: (0, 0))
    grid_spec = pltpu.PrefetchScalarGridSpec(
        num_scalar_prefetch=1,
        grid=(pairs,),
        in_specs=[triple] * count
        + [single] * (2 * count)
        + [pl.BlockSpec((1, 8, length), lambda p, o: (p, 0, 0)), table, table],
        out_specs=[triple] * count,
        scratch_shapes=[
            pltpu.VMEM((2, PAIR, length), BF16),
            pltpu.VMEM((2, PAIR, length), BF16),
            pltpu.VMEM((2, length, PAIR), BF16),
            pltpu.VMEM((2, length, PAIR), BF16),
            pltpu.VMEM((length, PAIR), BF16),
            pltpu.VMEM((length, PAIR), BF16),
            pltpu.VMEM((PAIR, length), BF16),
            pltpu.VMEM((8, length), F32),
            pltpu.VMEM((PAIR, length), F32),
            pltpu.VMEM((length, PAIR), F32),
            pltpu.VMEM((length, PAIR), F32),
        ],
    )
    area = pairs * 2 * length * length // 2
    return pl.pallas_call(
        functools.partial(attend_back_kernel, count, slots, tok, tile_q, tile_k),
        out_shape=[jax.ShapeDtypeStruct((3, width, span), BF16)] * count,
        grid_spec=grid_spec,
        compiler_params=pltpu.CompilerParams(
            dimension_semantics=("arbitrary",), vmem_limit_bytes=56 * MIB
        ),
        cost_estimate=pl.CostEstimate(
            flops=area * 2560, bytes_accessed=16 * width * length, transcendentals=area
        ),
        name="attend_back",
    )(order, *pieces, *mixes, *grads, lse, cosine, sine)


def nt(a, b):
    return lax.dot_general(a, b, (((1,), (1,)), ((), ())), preferred_element_type=F32)


def whole_block(shape):
    zeros = (0,) * len(shape)
    return pl.BlockSpec(shape, lambda *_: zeros)


def parameters(mib):
    return pltpu.CompilerParams(dimension_semantics=("arbitrary",), vmem_limit_bytes=mib * MIB)


def project_kernel(slots, tok, count, rows, place, *refs):
    xs, firsts = refs[:slots], refs[slots : 2 * slots]
    own = refs[2 * slots : 2 * slots + count]
    other = refs[2 * slots + count : 2 * slots + 2 * count]
    cos_ref, sin_ref = refs[2 * slots + 2 * count : 2 * slots + 2 * count + 2]
    other_ref, own_ref, normed_ref, full_ref, gains_ref, column = refs[2 * slots + 2 * count + 2 :]
    step = pl.program_id(0)
    target, kind = step // 3, step % 3
    core = place[1]
    half = jnp.where(target == 0, 1 - core, core)
    depth = normed_ref.shape[1]
    wide = own_ref.shape[1]

    @pl.when(step == 0)
    def _():
        for number in range(count):
            at = pl.ds(pl.multiple_of(place[2 + number] * rows, rows), rows)
            for which in range(3):
                columns = slice(which * wide, (which + 1) * wide)
                full_ref[core, which, at, :] = own[number][:, columns]
                full_ref[1 - core, which, at, :] = other[number][:, columns]
            column[at, :] = own[number][:, 3 * wide :]
        gains_ref[...] = column[...].T[:8].astype(F32)
        gain = gains_ref[0:1, :]
        for slot in range(slots):
            values = xs[slot][...].reshape(tok, depth).astype(F32)
            scale = lax.rsqrt(jnp.mean(values * values, axis=1, keepdims=True) + epsilon)
            normed_ref[slot * tok : (slot + 1) * tok, :] = (values * scale * gain).astype(BF16)

    weight = full_ref[half, kind]
    raw = nt(weight.T, normed_ref[...])

    def store(value):
        @pl.when(target == 0)
        def _():
            other_ref[0] = value

        @pl.when(target == 1)
        def _():
            own_ref[0] = value

    @pl.when(kind < 2)
    def _():
        parts = raw.reshape(wide // HEAD_DIM, 2, HALF, raw.shape[1])
        first, second = parts[:, 0], parts[:, 1]
        cosine, sine = cos_ref[...][None], sin_ref[...][None]
        turned = jnp.stack(
            [first * cosine - second * sine, first * sine + second * cosine], axis=1
        )
        store(turned.reshape(raw.shape).astype(BF16))

    @pl.when(kind == 2)
    def _():
        first = jnp.concatenate(
            [ref[...].reshape(tok, wide).T.astype(F32) for ref in firsts], axis=1
        )
        store((0.5 * raw + 0.5 * first).astype(BF16))


def project(inputs, received, firsts, firsts_received, own, other, cosine, sine, place):
    slots, tok, depth = inputs.shape
    count, rows = len(own), own[0].shape[0]
    wide = depth // 2
    span = slots * tok

    def half(s, p):
        return jnp.where(s < 3, 1 - p[1], p[1])

    x_specs = [pl.BlockSpec((1, tok, depth), lambda s, p: (p[0], 0, 0))]
    x_specs += [whole_block((tok, depth))] * (slots - 1)
    first_specs = [pl.BlockSpec((1, tok, wide), lambda s, p: (p[0], 0, half(s, p)))]
    first_specs += [pl.BlockSpec((tok, wide), lambda s, p: (0, half(s, p)))] * (slots - 1)
    grid_spec = pltpu.PrefetchScalarGridSpec(
        num_scalar_prefetch=1,
        grid=(6,),
        in_specs=x_specs
        + first_specs
        + [whole_block(own[0].shape)] * (2 * count)
        + [whole_block((HALF, span))] * 2,
        out_specs=[
            pl.BlockSpec((1, wide, span), lambda s, p: (jnp.minimum(s, 2), 0, 0)),
            pl.BlockSpec((1, wide, span), lambda s, p: (jnp.maximum(s - 3, 0), 0, 0)),
            whole_block((span, depth)),
            whole_block((2, 3, depth, wide)),
            whole_block((8, depth)),
        ],
        scratch_shapes=[pltpu.VMEM((depth, 128), BF16)],
    )
    return pl.pallas_call(
        functools.partial(project_kernel, slots, tok, count, rows),
        out_shape=[
            jax.ShapeDtypeStruct((3, wide, span), BF16),
            jax.ShapeDtypeStruct((3, wide, span), BF16),
            jax.ShapeDtypeStruct((span, depth), BF16),
            jax.ShapeDtypeStruct((2, 3, depth, wide), BF16),
            jax.ShapeDtypeStruct((8, depth), F32),
        ],
        grid_spec=grid_spec,
        compiler_params=parameters(56),
        cost_estimate=pl.CostEstimate(
            flops=6 * span * depth * depth,
            bytes_accessed=2 * (8 * span * depth + 6 * depth * depth),
            transcendentals=0,
        ),
        name="project",
    )(place, inputs, *received, firsts, *firsts_received, *own, *other, cosine, sine)


def output_kernel(slots, tok, count, rows, place, *refs):
    xs = refs[:slots]
    own = refs[slots : slots + count]
    other = refs[slots + count : slots + 2 * count]
    att_other, att_own, gains_ref = refs[slots + 2 * count : slots + 2 * count + 3]
    middle_ref, normed_ref, full_ref = refs[slots + 2 * count + 3 :]
    step = pl.program_id(0)
    core = place[1]
    wide = att_own.shape[0]
    depth = 2 * wide
    mine = pl.ds(pl.multiple_of(core * wide, wide), wide)
    others = pl.ds(pl.multiple_of((1 - core) * wide, wide), wide)

    @pl.when(step == 0)
    def _():
        for number in range(count):
            at = pl.ds(pl.multiple_of(place[2 + number] * rows, rows), rows)
            full_ref[at, mine] = own[number][...]
            full_ref[at, others] = other[number][...]

    total = dot(att_own[...].T, full_ref[mine, :]) + dot(att_other[...].T, full_ref[others, :])
    for slot in range(slots):

        @pl.when(step == slot)
        def _(slot=slot):
            middle_ref[...] = xs[slot][...].reshape(tok, depth).astype(F32) + total

    middle = middle_ref[...]
    scale = lax.rsqrt(jnp.mean(middle * middle, axis=1, keepdims=True) + epsilon)
    normed_ref[...] = (middle * scale * gains_ref[1:2, :]).astype(BF16)


def output_projection(inputs, received, own, other, att_other, att_own, gains, place):
    slots, tok, depth = inputs.shape
    count, rows = len(own), own[0].shape[0]
    wide = depth // 2
    span = slots * tok
    x_specs = [pl.BlockSpec((1, tok, depth), lambda s, p: (p[0], 0, 0))]
    x_specs += [whole_block((tok, depth))] * (slots - 1)
    grid_spec = pltpu.PrefetchScalarGridSpec(
        num_scalar_prefetch=1,
        grid=(slots,),
        in_specs=x_specs
        + [whole_block(own[0].shape)] * (2 * count)
        + [pl.BlockSpec((wide, tok), lambda s, p: (0, s))] * 2
        + [whole_block((8, depth))],
        out_specs=[
            pl.BlockSpec((tok, depth), lambda s, p: (s, 0)),
            pl.BlockSpec((tok, depth), lambda s, p: (s, 0)),
            whole_block((depth, depth)),
        ],
    )
    return pl.pallas_call(
        functools.partial(output_kernel, slots, tok, count, rows),
        out_shape=[
            jax.ShapeDtypeStruct((span, depth), F32),
            jax.ShapeDtypeStruct((span, depth), BF16),
            jax.ShapeDtypeStruct((depth, depth), BF16),
        ],
        grid_spec=grid_spec,
        compiler_params=parameters(56),
        cost_estimate=pl.CostEstimate(
            flops=2 * span * depth * depth,
            bytes_accessed=12 * span * depth + 4 * depth * depth,
            transcendentals=0,
        ),
        name="output_projection",
    )(place, inputs, *received, *own, *other, att_other, att_own, gains)


def mlp_kernel(slots, tok, count, rows, down_rows, blocks, place, *refs):
    grads = refs[:slots]
    middle_ref, normed_ref, gains_ref = refs[slots : slots + 3]
    base = slots + 3
    own_g, other_g, own_u, other_u, own_d, other_d = (
        refs[base + number * count : base + (number + 1) * count] for number in range(6)
    )
    (
        out_ref,
        send_ref,
        grad_ref,
        low_ref,
        gain_ref,
        gu_send,
        gu_keep,
        d_send,
        d_keep,
        wgu,
        wd,
        og,
        normed_t,
        acc,
        back,
        sems,
    ) = refs[base + 6 * count :]
    step = pl.program_id(0)
    core = place[1]
    depth = og.shape[1]
    wide = depth // 2
    strip = 128
    half_width = blocks * strip
    mine = pl.ds(pl.multiple_of(core * wide, wide), wide)
    others = pl.ds(pl.multiple_of((1 - core) * wide, wide), wide)

    def loads():
        copies = []
        for number in range(count):
            at = pl.ds(pl.multiple_of(place[2 + number] * rows, rows), rows)
            for which, (gate, up) in enumerate(((own_g, own_u), (other_g, other_u))):
                copies.append((gate[number], wgu.at[which, at, pl.ds(0, half_width)]))
                copies.append((up[number], wgu.at[which, at, pl.ds(half_width, half_width)]))
        for number in range(count):
            at = pl.ds(pl.multiple_of(place[2 + number] * down_rows, down_rows), down_rows)
            copies.append((own_d[number], wd.at[at, mine]))
            copies.append((other_d[number], wd.at[at, others]))
        return [
            pltpu.make_async_copy(source, target, sems.at[number])
            for number, (source, target) in enumerate(copies)
        ]

    @pl.when(step == 0)
    def _():
        copies = loads()
        for copy in copies:
            copy.start()
        for slot in range(slots):
            og[slot * tok : (slot + 1) * tok, :] = grads[slot][...].reshape(tok, depth)
        normed_t[...] = normed_ref[...].T
        acc[...] = jnp.zeros_like(acc)
        back[...] = jnp.zeros_like(back)
        for copy in copies:
            copy.wait()

    at = pl.ds(pl.multiple_of(step * strip, strip), strip)
    up_at = pl.ds(pl.multiple_of(half_width + step * strip, strip), strip)
    gate_w = jnp.concatenate([wgu[0, :, at], wgu[1, :, at]], axis=1)
    up_w = jnp.concatenate([wgu[0, :, up_at], wgu[1, :, up_at]], axis=1)
    own_rows = pl.ds(pl.multiple_of(core * half_width + step * strip, strip), strip)
    other_rows = pl.ds(pl.multiple_of((1 - core) * half_width + step * strip, strip), strip)
    down_w = jnp.concatenate([wd[own_rows, :], wd[other_rows, :]], axis=0)
    normed = normed_ref[...]
    gate = dot(normed, gate_w)
    up = dot(normed, up_w)
    grad_active = nt(og[...], down_w)
    sigma = jax.nn.sigmoid(gate)
    silu = gate * sigma
    active = (silu * up).astype(BF16)
    grad_up = (grad_active * silu).astype(BF16)
    grad_gate = (grad_active * up * sigma * (1.0 + gate * (1.0 - sigma))).astype(BF16)
    acc[...] += dot(active, down_w)
    back[...] += nt(grad_gate, gate_w) + nt(grad_up, up_w)
    grad_gate_w = dot(normed_t[...], grad_gate).astype(BF16)
    gu_keep[0] = grad_gate_w[:, :strip]
    gu_send[0] = grad_gate_w[:, strip:]
    grad_up_w = dot(normed_t[...], grad_up).astype(BF16)
    gu_keep[1] = grad_up_w[:, :strip]
    gu_send[1] = grad_up_w[:, strip:]
    active_t = active.T
    kept = dot(active_t, og[:, mine]).astype(BF16)
    sent = dot(active_t, og[:, others]).astype(BF16)
    d_keep[core] = kept[:strip]
    d_keep[1 - core] = kept[strip:]
    d_send[core] = sent[:strip]
    d_send[1 - core] = sent[strip:]

    @pl.when(step == blocks - 1)
    def _():
        gain = gains_ref[1:2, :]
        chunk = min(128, tok)
        gain_ref[...] = jnp.zeros_like(gain_ref)
        for slot in range(slots):

            def finish(number, _, slot=slot):
                local = pl.ds(pl.multiple_of(number * chunk, chunk), chunk)
                some = pl.ds(pl.multiple_of(slot * tok + number * chunk, chunk), chunk)
                middle = middle_ref[some, :]
                scale = lax.rsqrt(jnp.mean(middle * middle, axis=1, keepdims=True) + epsilon)
                result = middle + acc[some, :]
                if slot == 0:
                    out_ref[0, local, :] = result
                else:
                    send_ref[pl.ds(pl.multiple_of((slot - 1) * tok + number * chunk, chunk), chunk), :] = (
                        result.astype(BF16)
                    )
                grad = back[some, :]
                gain_ref[0:1, :] += jnp.sum(grad * middle * scale, axis=0, keepdims=True)
                weighted = grad * gain
                inner = jnp.mean(weighted * middle, axis=1, keepdims=True)
                grad_middle = (
                    scale * weighted
                    - middle * (scale * scale * scale) * inner
                    + og[some, :].astype(F32)
                )
                grad_ref[some, :] = grad_middle
                low_ref[some, :] = grad_middle.astype(BF16)
                return 0

            lax.fori_loop(0, tok // chunk, finish, 0)


def mlp(grads, grads_received, middle, normed, gains, gate, up, down, place):
    slots, tok, depth = grads.shape
    own_d, other_d = down
    count, rows = len(own_d), gate[0][0].shape[0]
    down_rows = own_d[0].shape[0]
    half_width = gate[0][0].shape[1]
    wide = depth // 2
    span = slots * tok
    blocks = half_width // 128
    once = pl.Buffered(1)
    g_specs = [pl.BlockSpec((1, tok, depth), lambda s, p: (p[0], 0, 0), pipeline_mode=once)]
    g_specs += [pl.BlockSpec((tok, depth), lambda s, p: (0, 0), pipeline_mode=once)] * (slots - 1)
    gu_spec = pl.BlockSpec((2, depth, 128), lambda s, p: (0, 0, s))
    d_spec = pl.BlockSpec((2, 128, wide), lambda s, p: (0, s, 0))
    grid_spec = pltpu.PrefetchScalarGridSpec(
        num_scalar_prefetch=1,
        grid=(blocks,),
        in_specs=g_specs
        + [
            pl.BlockSpec((span, depth), lambda s, p: (0, 0), pipeline_mode=once),
            pl.BlockSpec((span, depth), lambda s, p: (0, 0), pipeline_mode=once),
            whole_block((8, depth)),
        ]
        + [pl.BlockSpec(memory_space=pl.ANY)] * (6 * count),
        out_specs=[
            pl.BlockSpec((1, tok, depth), lambda s, p: (p[0], 0, 0), pipeline_mode=once),
            pl.BlockSpec(((slots - 1) * tok, depth), lambda s, p: (0, 0), pipeline_mode=once),
            pl.BlockSpec((span, depth), lambda s, p: (0, 0), pipeline_mode=once),
            pl.BlockSpec((span, depth), lambda s, p: (0, 0), pipeline_mode=once),
            whole_block((8, depth)),
            gu_spec,
            gu_spec,
            d_spec,
            d_spec,
        ],
        scratch_shapes=[
            pltpu.VMEM((2, depth, 2 * half_width), BF16),
            pltpu.VMEM((2 * half_width, depth), BF16),
            pltpu.VMEM((span, depth), BF16),
            pltpu.VMEM((depth, span), BF16),
            pltpu.VMEM((span, depth), F32),
            pltpu.VMEM((span, depth), F32),
            pltpu.SemaphoreType.DMA((6 * count,)),
        ],
    )
    return pl.pallas_call(
        functools.partial(mlp_kernel, slots, tok, count, rows, down_rows, blocks),
        out_shape=[
            jax.ShapeDtypeStruct((slots, tok, depth), F32),
            jax.ShapeDtypeStruct(((slots - 1) * tok, depth), BF16),
            jax.ShapeDtypeStruct((span, depth), F32),
            jax.ShapeDtypeStruct((span, depth), BF16),
            jax.ShapeDtypeStruct((8, depth), F32),
            jax.ShapeDtypeStruct((2, depth, half_width), BF16),
            jax.ShapeDtypeStruct((2, depth, half_width), BF16),
            jax.ShapeDtypeStruct((2, half_width, wide), BF16),
            jax.ShapeDtypeStruct((2, half_width, wide), BF16),
        ],
        grid_spec=grid_spec,
        compiler_params=parameters(63),
        cost_estimate=pl.CostEstimate(
            flops=16 * span * depth * 2 * half_width,
            bytes_accessed=24 * depth * half_width + 20 * span * depth,
            transcendentals=2 * span * half_width,
        ),
        name="mlp",
    )(
        place,
        grads,
        *grads_received,
        middle,
        normed,
        gains,
        *gate[0],
        *gate[1],
        *up[0],
        *up[1],
        *own_d,
        *other_d,
    )


def grad_attended_kernel(place, low_ref, full_ref, att_other, att_own, ga_other, ga_own, sent, kept):
    step = pl.program_id(0)
    core = place[1]
    wide = att_own.shape[0]
    mine = pl.ds(pl.multiple_of(core * wide, wide), wide)
    others = pl.ds(pl.multiple_of((1 - core) * wide, wide), wide)
    for number, (att, result) in enumerate(((att_other, ga_other), (att_own, ga_own))):

        @pl.when(step == number)
        def _(att=att, result=result):
            result[...] = nt(full_ref[...], low_ref[...]).astype(BF16)
            kept[...] = dot(att[...], low_ref[:, mine]).astype(BF16)
            sent[...] = dot(att[...], low_ref[:, others]).astype(BF16)


def grad_attended(low, full, att_other, att_own, place):
    span, depth = low.shape
    wide = depth // 2

    def half(s, p):
        return jnp.where(s == 0, 1 - p[1], p[1])

    row_spec = pl.BlockSpec((wide, wide), lambda s, p: (half(s, p), 0))
    grid_spec = pltpu.PrefetchScalarGridSpec(
        num_scalar_prefetch=1,
        grid=(2,),
        in_specs=[
            whole_block((span, depth)),
            pl.BlockSpec((wide, depth), lambda s, p: (half(s, p), 0)),
            whole_block((wide, span)),
            whole_block((wide, span)),
        ],
        out_specs=[whole_block((wide, span)), whole_block((wide, span)), row_spec, row_spec],
    )
    return pl.pallas_call(
        grad_attended_kernel,
        out_shape=[
            jax.ShapeDtypeStruct((wide, span), BF16),
            jax.ShapeDtypeStruct((wide, span), BF16),
            jax.ShapeDtypeStruct((depth, wide), BF16),
            jax.ShapeDtypeStruct((depth, wide), BF16),
        ],
        grid_spec=grid_spec,
        compiler_params=parameters(48),
        cost_estimate=pl.CostEstimate(
            flops=4 * span * depth * depth,
            bytes_accessed=6 * span * depth + 4 * depth * depth,
            transcendentals=0,
        ),
        name="grad_attended",
    )(place, low, full, att_other, att_own)


def tail_kernel(slots, tok, place, *refs):
    xs = refs[:slots]
    (
        back_other,
        back_own,
        full_ref,
        normed_ref,
        grad_ref,
        gains_ref,
        mlp_gain_ref,
        out_ref,
        send_ref,
        first_ref,
        first_send,
        gain_ref,
        sent,
        kept,
        normed_t,
        acc,
    ) = refs[slots:]
    step = pl.program_id(0)
    target, kind = step // 3, step % 3
    depth = acc.shape[1]

    @pl.when(step == 0)
    def _():
        normed_t[...] = normed_ref[...].T
        acc[...] = jnp.zeros_like(acc)

    def part(back, result):
        grad = back[0]

        @pl.when(kind == 2)
        def _():
            rows = 0.5 * grad.astype(F32).T
            first_ref[0] = rows[:tok]
            first_send[...] = rows[tok:].astype(BF16)

        grad = grad * jnp.where(kind == 2, 0.5, 1.0).astype(BF16)
        acc[...] += nt(grad.T, full_ref[0, 0])
        result[0] = nt(normed_t[...], grad).astype(BF16)

    @pl.when(target == 0)
    def _():
        part(back_other, sent)

    @pl.when(target == 1)
    def _():
        part(back_own, kept)

    @pl.when(step == 5)
    def _():
        gain = gains_ref[0:1, :]
        chunk = min(128, tok)
        gain_ref[...] = jnp.zeros_like(gain_ref)
        gain_ref[1:2, :] = mlp_gain_ref[0:1, :]
        for slot in range(slots):

            def finish(number, _, slot=slot):
                local = pl.ds(pl.multiple_of(number * chunk, chunk), chunk)
                some = pl.ds(pl.multiple_of(slot * tok + number * chunk, chunk), chunk)
                if slot == 0:
                    values = xs[slot][0, local, :].astype(F32)
                else:
                    values = xs[slot][local, :].astype(F32)
                scale = lax.rsqrt(jnp.mean(values * values, axis=1, keepdims=True) + epsilon)
                grad = acc[some, :]
                gain_ref[0:1, :] += jnp.sum(grad * values * scale, axis=0, keepdims=True)
                weighted = grad * gain
                inner = jnp.mean(weighted * values, axis=1, keepdims=True)
                result = (
                    scale * weighted
                    - values * (scale * scale * scale) * inner
                    + grad_ref[some, :]
                )
                if slot == 0:
                    out_ref[0, local, :] = result
                else:
                    send_ref[pl.ds(pl.multiple_of((slot - 1) * tok + number * chunk, chunk), chunk), :] = (
                        result.astype(BF16)
                    )
                return 0

            lax.fori_loop(0, tok // chunk, finish, 0)


def tail(inputs, received, back_other, back_own, full, normed, grad_middle, gains, mlp_gain, place):
    slots, tok, depth = inputs.shape
    wide = depth // 2
    span = slots * tok
    rest = (slots - 1) * tok
    once = pl.Buffered(1)

    def half(s, p):
        return jnp.where(s < 3, 1 - p[1], p[1])

    x_specs = [pl.BlockSpec((1, tok, depth), lambda s, p: (p[0], 0, 0))]
    x_specs += [whole_block((tok, depth))] * (slots - 1)
    grid_spec = pltpu.PrefetchScalarGridSpec(
        num_scalar_prefetch=1,
        grid=(6,),
        in_specs=x_specs
        + [
            pl.BlockSpec((1, wide, span), lambda s, p: (jnp.minimum(s, 2), 0, 0)),
            pl.BlockSpec((1, wide, span), lambda s, p: (jnp.maximum(s - 3, 0), 0, 0)),
            pl.BlockSpec((1, 1, depth, wide), lambda s, p: (half(s, p), s % 3, 0, 0)),
            whole_block((span, depth)),
            pl.BlockSpec((span, depth), lambda s, p: (0, 0), pipeline_mode=once),
            whole_block((8, depth)),
            whole_block((8, depth)),
        ],
        out_specs=[
            pl.BlockSpec((1, tok, depth), lambda s, p: (p[0], 0, 0)),
            whole_block((rest, depth)),
            pl.BlockSpec((1, tok, wide), lambda s, p: (p[0], 0, half(s, p))),
            pl.BlockSpec((rest, wide), lambda s, p: (0, half(s, p))),
            whole_block((8, depth)),
            pl.BlockSpec((1, depth, wide), lambda s, p: (jnp.minimum(s, 2), 0, 0)),
            pl.BlockSpec((1, depth, wide), lambda s, p: (jnp.maximum(s - 3, 0), 0, 0)),
        ],
        scratch_shapes=[pltpu.VMEM((depth, span), BF16), pltpu.VMEM((span, depth), F32)],
    )
    return pl.pallas_call(
        functools.partial(tail_kernel, slots, tok),
        out_shape=[
            jax.ShapeDtypeStruct((slots, tok, depth), F32),
            jax.ShapeDtypeStruct((rest, depth), BF16),
            jax.ShapeDtypeStruct((slots, tok, depth), F32),
            jax.ShapeDtypeStruct((rest, depth), BF16),
            jax.ShapeDtypeStruct((8, depth), F32),
            jax.ShapeDtypeStruct((3, depth, wide), BF16),
            jax.ShapeDtypeStruct((3, depth, wide), BF16),
        ],
        grid_spec=grid_spec,
        compiler_params=parameters(60),
        cost_estimate=pl.CostEstimate(
            flops=12 * span * depth * depth,
            bytes_accessed=24 * span * depth + 12 * depth * depth,
            transcendentals=0,
        ),
        name="tail",
    )(
        place, inputs, *received, back_other, back_own, full, normed, grad_middle, gains, mlp_gain
    )


def land_kernel(place, whole_ref, part_ref, out_ref):
    out_ref[0] = part_ref[...].astype(F32)


def land(whole, part, slot):
    _, tok, depth = whole.shape
    tile = min(256, tok)
    grid_spec = pltpu.PrefetchScalarGridSpec(
        num_scalar_prefetch=1,
        grid=(tok // tile,),
        in_specs=[
            pl.BlockSpec(memory_space=pl.ANY),
            pl.BlockSpec((tile, depth), lambda s, p: (s, 0)),
        ],
        out_specs=pl.BlockSpec((1, tile, depth), lambda s, p: (p[0], s, 0)),
    )
    return pl.pallas_call(
        land_kernel,
        out_shape=jax.ShapeDtypeStruct(whole.shape, F32),
        grid_spec=grid_spec,
        input_output_aliases={1: 0},
        compiler_params=parameters(16),
        cost_estimate=pl.CostEstimate(
            flops=tok * depth, bytes_accessed=6 * tok * depth, transcendentals=0
        ),
        name="land",
    )(slot, whole, part)


MESH = pl.DeviceIdType.MESH


def seats():
    shard = lax.axis_index("fsdp")
    seat = lax.axis_index("seq")
    return (shard // 2, shard % 2, seat // 2, seat % 2)


def meet(line, keys):
    shard = lax.axis_index("fsdp")
    seat = lax.axis_index("seq")
    partners = []
    if "z" in keys:
        partners += [{"fsdp": lax.rem(shard + 2 * jump, 2 * line)} for jump in range(1, line)]
    if "y" in keys:
        partners.append({"fsdp": shard + 1 - 2 * (shard % 2)})
    if "x" in keys:
        partners.append({"seq": lax.rem(seat + 2, 4)})
    if "core" in keys:
        partners.append({"seq": seat + 1 - 2 * (seat % 2)})
    barrier = pltpu.get_barrier_semaphore()
    for partner in partners:
        pl.semaphore_signal(barrier, inc=1, device_id=partner, device_id_type=MESH)
    pl.semaphore_wait(barrier, len(partners))


def send(source, target, sems, number, partner):
    return pltpu.make_async_remote_copy(
        src_ref=source,
        dst_ref=target,
        send_sem=sems.at[0, number],
        recv_sem=sems.at[1, number],
        device_id=partner,
        device_id_type=MESH,
    )


def to_core_partner():
    seat = lax.axis_index("seq")
    return {"seq": seat + 1 - 2 * (seat % 2)}


def to_x_partner():
    return {"seq": lax.rem(lax.axis_index("seq") + 2, 4)}


def to_y_partner():
    shard = lax.axis_index("fsdp")
    return {"fsdp": shard + 1 - 2 * (shard % 2)}


def to_z_partner(line, jump):
    return {"fsdp": lax.rem(lax.axis_index("fsdp") + 2 * jump, 2 * line)}


class Gather:
    def __init__(self, line, shard, own, other, sems, share=0, columns=None):
        self.line, self.shard, self.own, self.other = line, shard, own, other
        self.sems = sems
        z, y, x, _ = seats()
        self.z, self.y, self.share = z, y, share
        rows = own.shape[2]
        self.columns = slice(None) if columns is None else pl.ds(*columns)
        if share:
            step = math.gcd(share, rows)
            self.rows = pl.ds(pl.multiple_of(x * share, step), rows - share)
            self.given = pl.ds(pl.multiple_of(x * (rows - share), step), share)
            self.taken = pl.ds(pl.multiple_of((1 - x) * (rows - share), step), share)
        else:
            self.rows = slice(None)

    def here(self):
        return pltpu.make_async_copy(
            self.shard.at[self.rows, self.columns],
            self.own.at[self.z, self.y, self.rows, self.columns],
            self.sems.at[0, self.line + 3],
        )

    def along_z(self):
        return [
            send(
                self.shard.at[self.rows, self.columns],
                self.own.at[self.z, self.y, self.rows, self.columns],
                self.sems,
                jump - 1,
                to_z_partner(self.line, jump),
            )
            for jump in range(1, self.line)
        ]

    def along_y(self):
        part = self.own.at[:, self.y, self.rows, self.columns]
        return send(part, part, self.sems, self.line - 1, to_y_partner())

    def along_x(self):
        part = self.own.at[:, :, self.given, self.columns]
        return send(part, part, self.sems, self.line, to_x_partner())

    def to_core(self, late):
        if self.share:
            at = (slice(None), slice(None), self.taken if late else self.rows, self.columns)
        else:
            at = (slice(None), 1 - self.y if late else self.y, slice(None), self.columns)
        return send(
            self.own.at[at],
            self.other.at[at],
            self.sems,
            self.line + 1 + late,
            to_core_partner(),
        )

    def start_z(self):
        self.here().start()
        for copy in self.along_z():
            copy.start()

    def wait_z(self):
        self.here().wait()
        for copy in self.along_z():
            copy.wait()

    def wait_core(self):
        self.to_core(0).wait()
        self.to_core(1).wait()


def gather_sems(line):
    return pltpu.SemaphoreType.DMA((2, line + 4))


def front_kernel(line, tok, *refs):
    (
        inputs,
        firsts,
        grads,
        q_shard,
        k_shard,
        v_shard,
        o_shard,
        d_shard,
        cos_ref,
        sin_ref,
        x_received,
        f_received,
        g_received,
        heads_own,
        heads_received,
        normed_ref,
        full_ref,
        gains_ref,
        o_own,
        o_other,
        d_own,
        xs,
        fs,
        q_own,
        q_other,
        k_own,
        k_other,
        v_own,
        v_other,
        outgoing,
        q_sems,
        k_sems,
        v_sems,
        o_sems,
        d_sems,
        swap_sems,
        head_sems,
        local_sems,
    ) = refs
    step = pl.program_id(0)
    _, _, side, core = seats()
    wide = outgoing.shape[1]
    depth = 2 * wide
    gathers = [
        Gather(line, q_shard, q_own, q_other, q_sems),
        Gather(line, k_shard, k_own, k_other, k_sems),
        Gather(line, v_shard, v_own, v_other, v_sems),
    ]
    query, key, value = gathers
    out = Gather(line, o_shard, o_own, o_other, o_sems)
    down = Gather(line, d_shard, d_own, d_own, d_sems, d_own.shape[2] // 2)
    swap_x = send(inputs.at[1 - side], x_received, swap_sems, 0, to_x_partner())
    swap_f = send(firsts.at[1 - side], f_received, swap_sems, 1, to_x_partner())
    early = pl.ds(0, tok // 2)
    swap_g = send(
        grads.at[1 - side, early], g_received.at[early], swap_sems, 2, to_x_partner()
    )
    load_x = pltpu.make_async_copy(inputs.at[side], xs.at[pl.ds(0, tok), :], local_sems.at[0])
    load_f = pltpu.make_async_copy(firsts.at[side], fs.at[pl.ds(0, tok), :], local_sems.at[1])
    more_x = pltpu.make_async_copy(x_received, xs.at[pl.ds(tok, tok), :], local_sems.at[2])
    more_f = pltpu.make_async_copy(f_received, fs.at[pl.ds(tok, tok), :], local_sems.at[3])

    def weight(halves, columns):
        return halves[:, :, :, columns].reshape(depth, wide)

    def heads(number):
        return send(
            outgoing.at[number], heads_received.at[number], head_sems, number, to_core_partner()
        )

    saves = []
    for number, (mine, others) in enumerate(((q_own, q_other), (k_own, k_other), (v_own, v_other))):
        for which, ref in ((0, mine), (1, others)):
            half = core if which == 0 else 1 - core
            saves.append(
                pltpu.make_async_copy(
                    ref.at[:, :, :, pl.ds(0, wide)],
                    full_ref.at[half, number],
                    local_sems.at[4 + 2 * number + which],
                )
            )

    @pl.when(step == 0)
    def _():
        meet(line, ("z", "y", "x", "core"))
        swap_x.start()
        load_x.start()
        load_f.start()
        query.start_z()
        query.wait_z()
        query.along_y().start()
        query.to_core(0).start()
        key.start_z()
        key.wait_z()
        key.along_y().start()
        key.to_core(0).start()
        value.start_z()
        swap_x.wait()
        more_x.start()
        swap_f.start()
        query.along_y().wait()
        query.to_core(1).start()
        columns = q_own[:, :, :, wide:].reshape(depth, 128)
        gains_ref[...] = columns.astype(F32).T[:8]
        gain = gains_ref[0:1, :]
        chunk = min(256, 2 * tok)
        load_x.wait()
        more_x.wait()

        def norm(number, _):
            at = pl.ds(pl.multiple_of(number * chunk, chunk), chunk)
            values = xs[at, :].astype(F32)
            scale = lax.rsqrt(jnp.mean(values * values, axis=1, keepdims=True) + epsilon)
            normed_ref[at, :] = (values * scale * gain).astype(BF16)
            return 0

        lax.fori_loop(0, 2 * tok // chunk, norm, 0)

    @pl.when(step == 1)
    def _():
        value.wait_z()
        value.along_y().start()
        value.to_core(0).start()
        out.start_z()
        key.along_y().wait()
        key.to_core(1).start()

    @pl.when(step == 2)
    def _():
        swap_f.wait()
        more_f.start()
        swap_g.start()
        out.wait_z()
        out.along_y().start()
        out.to_core(0).start()
        down.start_z()
        value.along_y().wait()
        value.to_core(1).start()
        load_f.wait()
        more_f.wait()

    @pl.when(step == 3)
    def _():
        query.wait_core()
        key.wait_core()
        for save in saves[:4]:
            save.start()

    @pl.when(step == 5)
    def _():
        value.wait_core()
        for save in saves[4:]:
            save.start()
        out.along_y().wait()
        out.to_core(1).start()

    def project_one(halves, kind, mine):
        raw = nt(weight(halves, slice(0, wide)).T, normed_ref[...])
        if kind < 2:
            parts = raw.reshape(wide // HEAD_DIM, 2, HALF, raw.shape[1])
            first, second = parts[:, 0], parts[:, 1]
            cosine, sine = cos_ref[...][None], sin_ref[...][None]
            turned = jnp.stack(
                [first * cosine - second * sine, first * sine + second * cosine], axis=1
            )
            result = turned.reshape(raw.shape).astype(BF16)
        else:
            half = core if mine else 1 - core
            first = fs[:, pl.ds(pl.multiple_of(half * wide, wide), wide)]
            result = (0.5 * raw + 0.5 * first.astype(F32).T).astype(BF16)
        if mine:
            heads_own[0] = result
        else:
            outgoing[kind] = result
            heads(kind).start()

    for number, (halves, kind, mine) in enumerate(
        (
            (q_own, 0, True),
            (k_own, 1, True),
            (v_own, 2, True),
            (q_other, 0, False),
            (k_other, 1, False),
            (v_other, 2, False),
        )
    ):

        @pl.when(step == number)
        def _(halves=halves, kind=kind, mine=mine):
            project_one(halves, kind, mine)

    @pl.when(step == 5)
    def _():
        for number in range(3):
            heads(number).wait()
        for save in saves:
            save.wait()
        out.wait_core()
        down.wait_z()
        swap_g.wait()


def front(inputs, firsts, grads, q, k, v, o, d, cosine, sine, line):
    slots, tok, depth = inputs.shape
    span = slots * tok
    wide = depth // 2
    rows, down_rows = q.shape[0], d.shape[0]
    anywhere = pl.BlockSpec(memory_space=pl.ANY)
    weights = lambda columns: pltpu.VMEM((line, 2, rows, columns), BF16)
    return pl.pallas_call(
        functools.partial(front_kernel, line, tok),
        grid=(6,),
        in_specs=[anywhere] * 8 + [whole_block((HALF, span))] * 2,
        out_specs=[
            anywhere,
            anywhere,
            anywhere,
            pl.BlockSpec((1, wide, span), lambda s: (jnp.minimum(s, 2), 0, 0)),
            anywhere,
            whole_block((span, depth)),
            anywhere,
            whole_block((8, depth)),
            anywhere,
            anywhere,
            anywhere,
        ],
        out_shape=[
            jax.ShapeDtypeStruct((tok, depth), BF16),
            jax.ShapeDtypeStruct((tok, depth), BF16),
            jax.ShapeDtypeStruct((tok, depth), BF16),
            jax.ShapeDtypeStruct((3, wide, span), BF16),
            jax.ShapeDtypeStruct((3, wide, span), BF16),
            jax.ShapeDtypeStruct((span, depth), BF16),
            jax.ShapeDtypeStruct((2, 3, line, 2, rows, wide), BF16),
            jax.ShapeDtypeStruct((8, depth), F32),
            jax.ShapeDtypeStruct((line, 2, rows, wide), BF16),
            jax.ShapeDtypeStruct((line, 2, rows, wide), BF16),
            jax.ShapeDtypeStruct((line, 2, down_rows, wide), BF16),
        ],
        scratch_shapes=[
            pltpu.VMEM((span, depth), BF16),
            pltpu.VMEM((span, depth), BF16),
            weights(q.shape[1]),
            weights(q.shape[1]),
            weights(wide),
            weights(wide),
            weights(wide),
            weights(wide),
            pltpu.VMEM((3, wide, span), BF16),
        ]
        + [gather_sems(line)] * 5
        + [
            pltpu.SemaphoreType.DMA((2, 3)),
            pltpu.SemaphoreType.DMA((2, 3)),
            pltpu.SemaphoreType.DMA((10,)),
        ],
        compiler_params=pltpu.CompilerParams(
            dimension_semantics=("arbitrary",),
            vmem_limit_bytes=63 * MIB,
            collective_id=1,
            has_side_effects=True,
        ),
        cost_estimate=pl.CostEstimate(
            flops=6 * span * depth * depth,
            bytes_accessed=2 * (8 * span * depth + 6 * depth * depth),
            transcendentals=0,
        ),
        name="front",
    )(inputs, firsts, grads, q, k, v, o, d, cosine, sine)


def block_of(source, slot, tok):
    _, _, side, core = seats()
    rank = 1 - core if source == 0 else core
    group = lax.rem(side + slot, 2)
    return pl.ds(pl.multiple_of((group * 2 + rank) * tok, tok), tok)


def attend_carry_kernel(line, tok, tile_k, *refs):
    (
        received,
        own,
        inputs,
        x_received,
        gains_ref,
        o_own,
        o_other,
        grad_in,
        _,
        d_in,
        g_shard,
        u_shard,
        mix_received,
        mix_own,
        lse_ref,
        middle_ref,
        normed_ref,
        full_ref,
        att_other,
        grad_received,
        d_own,
        d_other,
        g_own,
        g_other,
        u_own,
        u_other,
        qz,
        kn,
        vt,
        ot,
        outgoing,
        att_mine,
        att_theirs,
        xs,
        d_sems,
        g_sems,
        u_sems,
        v_sems,
        swap_sems,
        att_sems,
        local_sems,
    ) = refs
    step = pl.program_id(0)
    pairs = pl.num_programs(0)
    _, _, side, core = seats()
    rows, columns = g_own.shape[2:]
    first = columns // 256 * 128
    down = Gather(line, d_in, d_own, d_other, d_sems, d_own.shape[2] // 2)
    gate = Gather(line, g_shard, g_own, g_other, g_sems, rows * 3 // 8)
    up = Gather(line, u_shard, u_own, u_other, u_sems, columns=(0, first))
    up_more = Gather(line, u_shard, u_own, u_other, v_sems, columns=(first, columns - first))
    late = pl.ds(tok // 2, tok - tok // 2)
    swap = send(grad_in.at[1 - side, late], grad_received.at[late], swap_sems, 0, to_x_partner())
    depth = xs.shape[1]
    wide = depth // 2
    mine = pl.ds(pl.multiple_of(core * wide, wide), wide)
    others = pl.ds(pl.multiple_of((1 - core) * wide, wide), wide)
    loads = [
        pltpu.make_async_copy(source, place, local_sems.at[number])
        for number, (source, place) in enumerate(
            (
                (inputs.at[side], xs.at[pl.ds(0, tok), :]),
                (x_received, xs.at[pl.ds(tok, tok), :]),
                (o_own, full_ref.at[:, mine]),
                (o_other, full_ref.at[:, others]),
            )
        )
    ]
    save_att = pltpu.make_async_copy(att_theirs, att_other, local_sems.at[4])
    pieces = (received, own)

    def hand_over(number):
        rows = pl.ds(number * PAIR, PAIR)
        return send(
            outgoing.at[rows, :], att_theirs.at[rows, :], att_sems, number, to_core_partner()
        )

    @pl.when(step == 0)
    def _():
        meet(line, ("z", "y", "x", "core"))
        down.along_y().start()
        gate.start_z()
        swap.start()

    @pl.when(step == 2)
    def _():
        down.along_y().wait()
        down.along_x().start()
        down.to_core(0).start()
        gate.wait_z()
        gate.along_y().start()
        up.start_z()
        for load in loads:
            load.start()

    for source in range(2):
        for slot in range(2):
            cols = block_of(source, slot, tok)
            take = slice(slot * tok, (slot + 1) * tok)
            query = pieces[source][0, :, take] * jnp.asarray(HEAD_DIM**-0.5, BF16)
            for head in range(2):
                qz[head, :, cols] = head_rows(query, head)
            kn[cols, :] = pieces[source][1, :, take].T
            vt[:, cols] = pieces[source][2, :, take]
    attend_body(4 * tok, tile_k, qz, kn, vt, ot, lse_ref)
    for slot in range(2):
        take = slice(slot * tok, (slot + 1) * tok)
        theirs = ot[:, block_of(0, slot, tok)]
        mix_received[:, take] = theirs
        for number in range(4):

            @pl.when(step == number)
            def _(number=number, theirs=theirs, take=take):
                outgoing[number * PAIR : (number + 1) * PAIR, take] = theirs

        ours = ot[:, block_of(1, slot, tok)]
        mix_own[:, take] = ours
        for number in range(4):

            @pl.when(step == number)
            def _(number=number, ours=ours, take=take):
                att_mine[number * PAIR : (number + 1) * PAIR, take] = ours

    for number in range(4):

        @pl.when(step == number)
        def _(number=number):
            hand_over(number).start()

    @pl.when(step == pairs - 1)
    def _():
        up.wait_z()
        up.along_y().start()
        up.to_core(0).start()
        up_more.start_z()
        gate.along_y().wait()
        gate.to_core(0).start()
        down.along_x().wait()
        gate.along_x().start()
        down.to_core(1).start()
        up_more.wait_z()
        up_more.along_y().start()
        up_more.to_core(0).start()
        for number in range(4):
            hand_over(number).wait()
        save_att.start()
        for load in loads:
            load.wait()
        for slot in range(2):
            take = slice(slot * tok, (slot + 1) * tok)
            total = dot(att_mine[:, take].T, full_ref[mine, :])
            total = total + dot(att_theirs[:, take].T, full_ref[others, :])
            middle = xs[take, :].astype(F32) + total
            middle_ref[take, :] = middle
            scale = lax.rsqrt(jnp.mean(middle * middle, axis=1, keepdims=True) + epsilon)
            normed_ref[take, :] = (middle * scale * gains_ref[1:2, :]).astype(BF16)
        up.along_y().wait()
        up.to_core(1).start()
        up_more.along_y().wait()
        up_more.to_core(1).start()
        gate.along_x().wait()
        gate.to_core(1).start()
        swap.wait()
        for gather in (down, up, up_more, gate):
            gather.wait_core()
        save_att.wait()


def attend_carry(
    received, own, inputs, x_received, gains, o_own, o_other, grads, g_received, d_own, gate, up, line
):
    _, width, span = own.shape
    tok = span // 2
    length = 2 * span
    pairs = width // PAIR
    rows, down_rows = gate.shape[0], d_own.shape[2]
    depth = grads.shape[2]
    anywhere = pl.BlockSpec(memory_space=pl.ANY)
    triple = pl.BlockSpec((3, PAIR, span), lambda p: (0, p, 0))
    single = pl.BlockSpec((PAIR, span), lambda p: (p, 0))
    whole_gate = jax.ShapeDtypeStruct((line, 2, rows, gate.shape[1]), BF16)
    whole_down = jax.ShapeDtypeStruct((line, 2, down_rows, d_own.shape[3]), BF16)
    area = pairs * 2 * length * length // 2
    return pl.pallas_call(
        functools.partial(attend_carry_kernel, line, tok, min(256, length)),
        grid=(pairs,),
        in_specs=[triple, triple]
        + [anywhere] * 2
        + [whole_block((8, depth))]
        + [anywhere] * 7,
        out_specs=[single, single, pl.BlockSpec((1, 8, length), lambda p: (p, 0, 0))]
        + [
            pl.BlockSpec(shape, lambda p: (0, 0), pipeline_mode=pl.Buffered(1))
            for shape in ((span, depth), (span, depth), (depth, depth))
        ]
        + [anywhere] * 8,
        out_shape=[
            jax.ShapeDtypeStruct((width, span), BF16),
            jax.ShapeDtypeStruct((width, span), BF16),
            jax.ShapeDtypeStruct((pairs, 8, length), F32),
            jax.ShapeDtypeStruct((span, depth), F32),
            jax.ShapeDtypeStruct((span, depth), BF16),
            jax.ShapeDtypeStruct((depth, depth), BF16),
            jax.ShapeDtypeStruct((width, span), BF16),
            jax.ShapeDtypeStruct((tok, depth), BF16),
            whole_down,
            whole_down,
            whole_gate,
            whole_gate,
            whole_gate,
            whole_gate,
        ],
        scratch_shapes=[
            pltpu.VMEM((2, PAIR, length), BF16),
            pltpu.VMEM((length, PAIR), BF16),
            pltpu.VMEM((PAIR, length), BF16),
            pltpu.VMEM((PAIR, length), BF16),
            pltpu.VMEM((width, span), BF16),
            pltpu.VMEM((width, span), BF16),
            pltpu.VMEM((width, span), BF16),
            pltpu.VMEM((span, depth), BF16),
        ]
        + [gather_sems(line)] * 4
        + [
            pltpu.SemaphoreType.DMA((2, 1)),
            pltpu.SemaphoreType.DMA((2, 4)),
            pltpu.SemaphoreType.DMA((5,)),
        ],
        input_output_aliases={8: 7, 9: 8},
        compiler_params=pltpu.CompilerParams(
            dimension_semantics=("arbitrary",),
            vmem_limit_bytes=63 * MIB,
            collective_id=2,
            has_side_effects=True,
        ),
        cost_estimate=pl.CostEstimate(
            flops=area * 1024, bytes_accessed=8 * width * length, transcendentals=area
        ),
        name="attend_carry",
    )(
        received,
        own,
        inputs,
        x_received,
        gains,
        o_own,
        o_other,
        grads,
        g_received,
        d_own,
        gate,
        up,
    )


def mlp_carry_kernel(line, tok, blocks, *refs):
    (
        grads,
        grads_received,
        middle_ref,
        normed_ref,
        gains_ref,
        g_own,
        g_other,
        u_own,
        u_other,
        d_own_own,
        d_own_other,
        d_other_own,
        d_other_other,
        out_ref,
        send_ref,
        grad_ref,
        low_ref,
        gain_ref,
        gu_ref,
        d_ref,
        gu_y,
        og,
        normed_t,
        acc,
        back,
        gu_kept,
        d_kept,
        gu_sent,
        d_sent,
        gu_landed,
        d_landed,
        gu_outgoing,
        down_full,
        local_sems,
        gu_sends,
        gu_recvs,
        d_sends,
        d_recvs,
        y_sems,
    ) = refs
    step = pl.program_id(0)
    _, y, side, core = seats()
    depth = og.shape[1]
    wide = depth // 2
    strip = 128
    rows = gu_kept.shape[4]
    mine = pl.ds(pl.multiple_of(core * wide, wide), wide)
    others = pl.ds(pl.multiple_of((1 - core) * wide, wide), wide)

    def core_copies(number):
        slot = lax.rem(number, 2)
        return [
            pltpu.make_async_remote_copy(
                src_ref=source.at[slot],
                dst_ref=target.at[number],
                send_sem=sends.at[slot],
                recv_sem=recvs.at[number],
                device_id=to_core_partner(),
                device_id_type=MESH,
            )
            for source, target, sends, recvs in (
                (gu_sent, gu_landed, gu_sends, gu_recvs),
                (d_sent, d_landed, d_sends, d_recvs),
            )
        ]

    def y_copy(number):
        return send(gu_outgoing.at[number], gu_y.at[number], y_sems, number, to_y_partner())

    @pl.when(step == 0)
    def _():
        meet(line, ("y", "core"))
        loads = [
            pltpu.make_async_copy(grads.at[side], og.at[pl.ds(0, tok), :], local_sems.at[0]),
            pltpu.make_async_copy(grads_received, og.at[pl.ds(tok, tok), :], local_sems.at[1]),
        ]
        for load in loads:
            load.start()
        normed_t[...] = normed_ref[...].T
        acc[...] = jnp.zeros_like(acc)
        back[...] = jnp.zeros_like(back)
        for load in loads:
            load.wait()

    @pl.when(step < blocks)
    def _():
        slot = lax.rem(step, 2)
        gate_w = jnp.concatenate([g_own[...], g_other[...]], axis=1)
        up_w = jnp.concatenate([u_own[...], u_other[...]], axis=1)
        for number, pair in enumerate(
            ((d_own_own, d_own_other), (d_other_own, d_other_other))
        ):
            at = pl.ds(number * strip, strip)
            down_full[at, mine] = pair[0][...]
            down_full[at, others] = pair[1][...]
        down_w = down_full[...]
        normed = normed_ref[...]
        gate = dot(normed, gate_w)
        up = dot(normed, up_w)
        grad_active = nt(og[...], down_w)
        sigma = jax.nn.sigmoid(gate)
        silu = gate * sigma
        active = (silu * up).astype(BF16)
        grad_up = (grad_active * silu).astype(BF16)
        grad_gate = (grad_active * up * sigma * (1.0 + gate * (1.0 - sigma))).astype(BF16)

        @pl.when(step >= 2)
        def _():
            for copy in core_copies(step - 2):
                copy.wait_send()

        for number, grad in enumerate((grad_gate, grad_up)):
            result = dot(normed_t[...], grad).astype(BF16)
            shaped = result.reshape(line, 2, rows, 2 * strip)
            gu_kept[slot, number] = shaped[..., :strip]
            gu_sent[slot, number] = shaped[..., strip:]
        active_t = active.T
        kept = dot(active_t, og[:, mine]).astype(BF16)
        d_kept[slot, core] = kept[:strip]
        d_kept[slot, 1 - core] = kept[strip:]
        sent = dot(active_t, og[:, others]).astype(BF16)
        d_sent[slot, core] = sent[:strip]
        d_sent[slot, 1 - core] = sent[strip:]
        for copy in core_copies(step):
            copy.start()
        acc[...] += dot(active, down_w)
        back[...] += nt(grad_gate, gate_w) + nt(grad_up, up_w)

    @pl.when(step > 0)
    def _():
        number = step - 1
        slot = lax.rem(number, 2)
        for copy in core_copies(number):
            copy.wait_recv()
        for which in range(2):
            theirs = gu_kept[slot, which, :, 1 - y].astype(F32)
            theirs = theirs + gu_landed[number, which, :, 1 - y].astype(F32)
            gu_outgoing[number, which] = theirs.astype(BF16)
            ours = gu_kept[slot, which, :, y].astype(F32)
            ours = ours + gu_landed[number, which, :, y].astype(F32)
            gu_ref[0, which] = ours.astype(BF16)
        y_copy(number).start()
        d_ref[...] = (d_kept[slot].astype(F32) + d_landed[number].astype(F32)).astype(BF16)

    @pl.when(step == blocks)
    def _():
        gain = gains_ref[1:2, :]
        chunk = min(128, tok)
        gain_ref[...] = jnp.zeros_like(gain_ref)
        for slot in range(2):

            def finish(number, _, slot=slot):
                local = pl.ds(pl.multiple_of(number * chunk, chunk), chunk)
                some = pl.ds(pl.multiple_of(slot * tok + number * chunk, chunk), chunk)
                middle = middle_ref[some, :]
                scale = lax.rsqrt(jnp.mean(middle * middle, axis=1, keepdims=True) + epsilon)
                result = middle + acc[some, :]
                if slot == 0:
                    out_ref[0, local, :] = result
                else:
                    send_ref[local, :] = result.astype(BF16)
                grad = back[some, :]
                gain_ref[0:1, :] += jnp.sum(grad * middle * scale, axis=0, keepdims=True)
                weighted = grad * gain
                inner = jnp.mean(weighted * middle, axis=1, keepdims=True)
                grad_middle = (
                    scale * weighted
                    - middle * (scale * scale * scale) * inner
                    + og[some, :].astype(F32)
                )
                grad_ref[some, :] = grad_middle
                low_ref[some, :] = grad_middle.astype(BF16)
                return 0

            lax.fori_loop(0, tok // chunk, finish, 0)
        for number in (blocks - 2, blocks - 1):
            for copy in core_copies(number):
                copy.wait_send()
        for number in range(blocks):
            y_copy(number).wait()


def mlp_carry(grads, grads_received, middle, normed, gains, gate, up, down, line):
    slots, tok, depth = grads.shape
    half_width = gate[0].shape[1]
    wide = depth // 2
    span = slots * tok
    blocks = half_width // 128
    rows = depth // (2 * line)
    once = pl.Buffered(1)
    anywhere = pl.BlockSpec(memory_space=pl.ANY)

    def now(s):
        return jnp.minimum(s, blocks - 1)

    def done(s):
        return jnp.maximum(s - 1, 0)

    def core():
        return lax.axis_index("seq") % 2

    column = pl.BlockSpec((depth, 128), lambda s: (0, now(s)))
    own_rows = pl.BlockSpec((128, wide), lambda s: (core() * blocks + now(s), 0))
    other_rows = pl.BlockSpec((128, wide), lambda s: ((1 - core()) * blocks + now(s), 0))
    full = pl.BlockSpec((span, depth), lambda s: (0, 0), pipeline_mode=once)
    return pl.pallas_call(
        functools.partial(mlp_carry_kernel, line, tok, blocks),
        grid=(blocks + 1,),
        in_specs=[anywhere, anywhere, full, full, whole_block((8, depth))]
        + [column] * 4
        + [own_rows, own_rows, other_rows, other_rows],
        out_specs=[
            pl.BlockSpec(
                (1, tok, depth), lambda s: (lax.axis_index("seq") // 2, 0, 0), pipeline_mode=once
            ),
            pl.BlockSpec((tok, depth), lambda s: (0, 0), pipeline_mode=once),
            full,
            full,
            whole_block((8, depth)),
            pl.BlockSpec((1, 2, line, rows, 128), lambda s: (done(s), 0, 0, 0, 0)),
            pl.BlockSpec((2, 128, wide), lambda s: (0, done(s), 0)),
            anywhere,
        ],
        out_shape=[
            jax.ShapeDtypeStruct((slots, tok, depth), F32),
            jax.ShapeDtypeStruct((tok, depth), BF16),
            jax.ShapeDtypeStruct((span, depth), F32),
            jax.ShapeDtypeStruct((span, depth), BF16),
            jax.ShapeDtypeStruct((8, depth), F32),
            jax.ShapeDtypeStruct((blocks, 2, line, rows, 128), BF16),
            jax.ShapeDtypeStruct((2, half_width, wide), BF16),
            jax.ShapeDtypeStruct((blocks, 2, line, rows, 128), BF16),
        ],
        scratch_shapes=[
            pltpu.VMEM((span, depth), BF16),
            pltpu.VMEM((depth, span), BF16),
            pltpu.VMEM((span, depth), F32),
            pltpu.VMEM((span, depth), F32),
            pltpu.VMEM((2, 2, line, 2, rows, 128), BF16),
            pltpu.VMEM((2, 2, 128, wide), BF16),
            pltpu.VMEM((2, 2, line, 2, rows, 128), BF16),
            pltpu.VMEM((2, 2, 128, wide), BF16),
            pltpu.VMEM((blocks, 2, line, 2, rows, 128), BF16),
            pltpu.VMEM((blocks, 2, 128, wide), BF16),
            pltpu.VMEM((blocks, 2, line, rows, 128), BF16),
            pltpu.VMEM((256, depth), BF16),
            pltpu.SemaphoreType.DMA((2,)),
            pltpu.SemaphoreType.DMA((2,)),
            pltpu.SemaphoreType.DMA((blocks,)),
            pltpu.SemaphoreType.DMA((2,)),
            pltpu.SemaphoreType.DMA((blocks,)),
            pltpu.SemaphoreType.DMA((2, blocks)),
        ],
        compiler_params=pltpu.CompilerParams(
            dimension_semantics=("arbitrary",),
            vmem_limit_bytes=63 * MIB,
            collective_id=3,
            has_side_effects=True,
        ),
        cost_estimate=pl.CostEstimate(
            flops=16 * span * depth * 2 * half_width,
            bytes_accessed=24 * depth * half_width + 20 * span * depth,
            transcendentals=2 * span * half_width,
        ),
        name="mlp_carry",
    )(
        grads,
        grads_received,
        middle,
        normed,
        gains,
        *gate,
        *up,
        down[0],
        down[1],
        down[0],
        down[1],
    )


def grad_attended_carry_kernel(
    line,
    low_ref,
    full_ref,
    att_other,
    att_own,
    ga_own,
    ga_received,
    o_ref,
    o_landed,
    outgoing,
    o_sent,
    sems,
):
    step = pl.program_id(0)
    _, _, _, core = seats()
    wide = att_own.shape[0]
    mine = pl.ds(pl.multiple_of(core * wide, wide), wide)
    others = pl.ds(pl.multiple_of((1 - core) * wide, wide), wide)
    heads = send(outgoing, ga_received, sems, 0, to_core_partner())

    def sums(number):
        half = 1 - core if number == 0 else core
        at = pl.ds(pl.multiple_of(half * wide, wide), wide)
        return send(o_sent.at[number], o_landed.at[at, :], sems, 1 + number, to_core_partner())

    @pl.when(step == 0)
    def _():
        meet(line, ("core",))
        outgoing[...] = nt(full_ref[...], low_ref[...]).astype(BF16)
        heads.start()

    @pl.when(step == 1)
    def _():
        ga_own[...] = nt(full_ref[...], low_ref[...]).astype(BF16)

    for number, att in enumerate((att_other, att_own)):

        @pl.when(step == number)
        def _(number=number, att=att):
            o_sent[number] = dot(att[...], low_ref[:, others]).astype(BF16)
            sums(number).start()
            o_ref[...] = dot(att[...], low_ref[:, mine]).astype(BF16)

    @pl.when(step == 1)
    def _():
        heads.wait()
        for number in range(2):
            sums(number).wait()


def grad_attended_carry(low, full, att_other, att_own, line):
    span, depth = low.shape
    wide = depth // 2

    def half(s):
        core = lax.axis_index("seq") % 2
        return jnp.where(s == 0, 1 - core, core)

    anywhere = pl.BlockSpec(memory_space=pl.ANY)
    return pl.pallas_call(
        functools.partial(grad_attended_carry_kernel, line),
        grid=(2,),
        in_specs=[
            whole_block((span, depth)),
            pl.BlockSpec((wide, depth), lambda s: (half(s), 0)),
            whole_block((wide, span)),
            whole_block((wide, span)),
        ],
        out_specs=[
            whole_block((wide, span)),
            anywhere,
            pl.BlockSpec((wide, wide), lambda s: (half(s), 0)),
            anywhere,
        ],
        out_shape=[
            jax.ShapeDtypeStruct((wide, span), BF16),
            jax.ShapeDtypeStruct((wide, span), BF16),
            jax.ShapeDtypeStruct((depth, wide), BF16),
            jax.ShapeDtypeStruct((depth, wide), BF16),
        ],
        scratch_shapes=[
            pltpu.VMEM((wide, span), BF16),
            pltpu.VMEM((2, wide, wide), BF16),
            pltpu.SemaphoreType.DMA((2, 3)),
        ],
        compiler_params=pltpu.CompilerParams(
            dimension_semantics=("arbitrary",),
            vmem_limit_bytes=63 * MIB,
            collective_id=4,
            has_side_effects=True,
        ),
        cost_estimate=pl.CostEstimate(
            flops=4 * span * depth * depth,
            bytes_accessed=6 * span * depth + 4 * depth * depth,
            transcendentals=0,
        ),
        name="grad_attended_carry",
    )(low, full, att_other, att_own)


def attend_back_carry_kernel(line, tok, tile_q, tile_k, *refs):
    (
        received,
        own,
        mix_received,
        mix_own,
        grad_received,
        grad_own,
        lse_ref,
        cos_ref,
        sin_ref,
        outputs_sent,
        gu_in,
        gu_y,
        d_in,
        o_in,
        o_landed,
        back_own,
        back_other,
        outputs_received,
        gu_mine,
        gu_z,
        d_y,
        o_kept,
        o_y,
    ) = refs[:23]
    (
        qz,
        gz,
        qn,
        gn,
        kn,
        vn,
        kt,
        inner,
        dq,
        dk,
        dv,
        outgoing,
        gu_a,
        gu_b,
        o_a,
        o_b,
        local_sems,
        back_sems,
        z_sems,
        other_sems,
    ) = refs[23:]
    step = pl.program_id(0)
    pairs = pl.num_programs(0)
    z, y, _, _ = seats()
    length = 4 * tok
    swap = send(outputs_sent, outputs_received, other_sems, 0, to_x_partner())
    d_send = send(d_in.at[:, 1 - y], d_y, other_sems, 1, to_y_partner())
    o_send = send(o_a.at[:, 1 - y], o_y, other_sems, 2, to_y_partner())

    def z_send(jump):
        target = lax.rem(z + jump, line)
        return send(
            gu_a.at[:, :, target], gu_z.at[jump - 1], z_sems, jump - 1, to_z_partner(line, jump)
        )

    stays = [
        pltpu.make_async_copy(gu_a.at[:, :, z], gu_mine, local_sems.at[4]),
        pltpu.make_async_copy(o_a.at[:, y], o_kept, local_sems.at[5]),
    ]

    def hand_over(number):
        rows = pl.ds(number * PAIR, PAIR)
        return send(
            outgoing.at[:, rows, :],
            back_other.at[:, rows, :],
            back_sems,
            number,
            to_core_partner(),
        )

    @pl.when(step == 0)
    def _():
        meet(line, ("z", "y", "x", "core"))
        swap.start()
        loads = [
            pltpu.make_async_copy(source, target, local_sems.at[number])
            for number, (source, target) in enumerate(
                ((o_in, o_a), (o_landed, o_b), (gu_in, gu_a), (gu_y, gu_b))
            )
        ]
        for load in loads:
            load.start()
        loads[0].wait()
        loads[1].wait()
        o_a[...] = (o_a[...].astype(F32) + o_b[...].astype(F32)).astype(BF16)
        o_send.start()
        d_send.start()
        loads[2].wait()
        loads[3].wait()

        def add(number, _):
            total = gu_a[number].astype(F32) + gu_b[number].astype(F32)
            gu_a[number] = total.astype(BF16)
            return 0

        lax.fori_loop(0, gu_a.shape[0], add, 0)
        for jump in range(1, line):
            z_send(jump).start()
        for copy in stays:
            copy.start()

    attend_back_body(
        (received, own),
        (mix_received, mix_own),
        (grad_received, grad_own),
        lambda source, slot: block_of(source, slot, tok),
        tok,
        length,
        tile_q,
        tile_k,
        lse_ref,
        qz,
        gz,
        qn,
        gn,
        kn,
        vn,
        kt,
        inner,
        dq,
        dk,
        dv,
    )
    for slot in range(2):
        take = slice(slot * tok, (slot + 1) * tok)
        for source in range(2):
            cols = block_of(source, slot, tok)
            results = turn_back(dq, dk, dv, cols, cos_ref[:, cols], sin_ref[:, cols])
            for which, result in enumerate(results):
                if source == 1:
                    back_own[which, :, take] = result
                else:
                    at = pl.ds(pl.multiple_of(step * PAIR, PAIR), PAIR)
                    outgoing[which, at, take] = result

    for number in range(4):

        @pl.when(step == number)
        def _(number=number):
            hand_over(number).start()

    @pl.when(step == pairs - 1)
    def _():
        swap.wait()
        d_send.wait()
        o_send.wait()
        for copy in stays:
            copy.wait()
        for jump in range(1, line):
            z_send(jump).wait()
        for number in range(4):
            hand_over(number).wait()


def attend_back_carry(
    pieces, mixes, grads, lse, cosine, sine, outputs_sent, gu, gu_y, d, o, o_landed, line
):
    _, width, span = pieces[0].shape
    tok = span // 2
    length = 2 * span
    pairs = width // PAIR
    tile_q = min(512, length)
    tile_k = min(256, length)
    anywhere = pl.BlockSpec(memory_space=pl.ANY)
    triple = pl.BlockSpec((3, PAIR, span), lambda p: (0, p, 0))
    single = pl.BlockSpec((PAIR, span), lambda p: (p, 0))
    table = pl.BlockSpec((HALF, length), lambda p: (0, 0))
    blocks, _, _, rows, _ = gu.shape
    down_rows, wide = d.shape[2:]
    area = pairs * 2 * length * length // 2
    return pl.pallas_call(
        functools.partial(attend_back_carry_kernel, line, tok, tile_q, tile_k),
        grid=(pairs,),
        in_specs=[triple] * 2
        + [single] * 4
        + [pl.BlockSpec((1, 8, length), lambda p: (p, 0, 0)), table, table]
        + [anywhere] * 6,
        out_specs=[triple] + [anywhere] * 7,
        out_shape=[
            jax.ShapeDtypeStruct((3, width, span), BF16),
            jax.ShapeDtypeStruct((3, width, span), BF16),
            jax.ShapeDtypeStruct(outputs_sent.shape, BF16),
            jax.ShapeDtypeStruct((blocks, 2, rows, 128), BF16),
            jax.ShapeDtypeStruct((line - 1, blocks, 2, rows, 128), BF16),
            jax.ShapeDtypeStruct((line, down_rows, wide), BF16),
            jax.ShapeDtypeStruct((line, rows, wide), BF16),
            jax.ShapeDtypeStruct((line, rows, wide), BF16),
        ],
        scratch_shapes=[
            pltpu.VMEM((2, PAIR, length), BF16),
            pltpu.VMEM((2, PAIR, length), BF16),
            pltpu.VMEM((2, length, PAIR), BF16),
            pltpu.VMEM((2, length, PAIR), BF16),
            pltpu.VMEM((length, PAIR), BF16),
            pltpu.VMEM((length, PAIR), BF16),
            pltpu.VMEM((PAIR, length), BF16),
            pltpu.VMEM((8, length), F32),
            pltpu.VMEM((PAIR, length), F32),
            pltpu.VMEM((length, PAIR), F32),
            pltpu.VMEM((length, PAIR), F32),
            pltpu.VMEM((3, width, span), BF16),
            pltpu.VMEM((blocks, 2, line, rows, 128), BF16),
            pltpu.VMEM((blocks, 2, line, rows, 128), BF16),
            pltpu.VMEM((line, 2, rows, wide), BF16),
            pltpu.VMEM((line, 2, rows, wide), BF16),
            pltpu.SemaphoreType.DMA((6,)),
            pltpu.SemaphoreType.DMA((2, 4)),
            pltpu.SemaphoreType.DMA((2, line - 1)),
            pltpu.SemaphoreType.DMA((2, 3)),
        ],
        compiler_params=pltpu.CompilerParams(
            dimension_semantics=("arbitrary",),
            vmem_limit_bytes=63 * MIB,
            collective_id=5,
            has_side_effects=True,
        ),
        cost_estimate=pl.CostEstimate(
            flops=area * 2560, bytes_accessed=16 * width * length, transcendentals=area
        ),
        name="attend_back_carry",
    )(
        *pieces, *mixes, *grads, lse, cosine, sine, outputs_sent, gu, gu_y, d, o, o_landed
    )


def tail_carry_kernel(line, tok, blocks, *refs):
    (
        inputs,
        x_received,
        back_other,
        back_own,
        full_ref,
        normed_ref,
        grad_in,
        gains_ref,
        mlp_gain_ref,
        gu_mine,
        gu_z,
        d_in,
        d_y,
        o_in,
        o_y,
        input_grad,
        input_landed,
        first_grad,
        first_landed,
        gain_out,
        q_out,
        k_out,
        v_out,
        o_out,
        g_out,
        u_out,
        d_out,
        xs,
        grad_middle,
        normed_t,
        acc,
        grad,
        sent,
        landed,
        y_landed,
        z_landed,
        d_a,
        d_b,
        d_landed,
        o_a,
        o_b,
        o_landed,
        gu_a,
        gu_b,
        gu_x,
        gu_c,
        d_low,
        d_x,
        d_c,
        s_low,
        s_x,
        s_c,
        first_stage,
        first_send,
        input_send,
        gain,
        gain_landed,
        local_sems,
        core_sems,
        y_sems,
        z_sems,
        dz_sems,
        oz_sems,
        x_sems,
        c_sems,
        token_sems,
        gain_sems,
    ) = refs
    step = pl.program_id(0)
    target, turn = step // 3, lax.rem(step, 3)
    z, y, side, core = seats()
    wide, span = grad.shape
    depth = 2 * wide
    half = jnp.where(target == 0, 1 - core, core)
    columns = pl.ds(pl.multiple_of(half * wide, wide), wide)
    mine = pl.ds(pl.multiple_of(core * wide, wide), wide)
    others = pl.ds(pl.multiple_of((1 - core) * wide, wide), wide)

    def load(source, place, number):
        return pltpu.make_async_copy(source, place, local_sems.at[number])

    load_tokens = [
        load(inputs.at[side], xs.at[pl.ds(0, tok), :], 0),
        load(x_received, xs.at[pl.ds(tok, tok), :], 1),
        load(grad_in, grad_middle, 2),
    ]
    store_input = load(acc.at[pl.ds(0, tok), :], input_grad, 3)
    store_first = load(first_stage, first_grad, 4)

    def along_z(source, place, sems, base=0):
        return [
            send(
                source(lax.rem(z + jump, line)),
                place(jump - 1),
                sems,
                base + jump - 1,
                to_z_partner(line, jump),
            )
            for jump in range(1, line)
        ]

    d_sends = along_z(lambda at: d_a.at[at], lambda jump: d_landed.at[jump], dz_sems)
    o_sends = along_z(lambda at: o_a.at[at], lambda jump: o_landed.at[jump], oz_sems)

    def core_send(number):
        return send(sent.at[number], landed.at[number], core_sems, number, to_core_partner())

    def y_send(number):
        return send(
            landed.at[number, :, 1 - y], y_landed.at[number], y_sems, number, to_y_partner()
        )

    def z_sends(number):
        return along_z(
            lambda at: landed.at[number, at, y],
            lambda jump: z_landed.at[number, jump],
            z_sems,
            number * (line - 1),
        )

    def first_part(number):
        which = 1 - core if number == 0 else core
        at = pl.ds(pl.multiple_of(which * wide, wide), wide)
        return send(
            first_send.at[:, at], first_landed.at[:, at], token_sems, number, to_x_partner()
        )

    input_part = send(input_send, input_landed, token_sems, 2, to_x_partner())
    gu_sides = (
        send(gu_a, gu_x, x_sems, 0, to_x_partner()),
        send(gu_a, gu_c, c_sems, 0, to_core_partner()),
    )
    d_sides = (
        send(d_low, d_x, x_sems, 1, to_x_partner()),
        send(d_low, d_c, c_sems, 1, to_core_partner()),
    )

    def square_x(number):
        return send(s_low.at[number], s_x.at[number], x_sems, 2 + number, to_x_partner())

    def square_core(number):
        return send(s_low.at[number], s_c.at[number], c_sems, 2 + number, to_core_partner())

    squares = (o_out, v_out, q_out, k_out)

    def gain_send(number, partner):
        return send(gain.at[number], gain_landed.at[number], gain_sems, number, partner)

    @pl.when(step == 0)
    def _():
        meet(line, ("z", "y", "x", "core"))
        sources = ((d_in.at[:, y], d_a), (d_y, d_b), (o_in, o_a), (o_y, o_b), (gu_mine, gu_a), (gu_z, gu_b))
        loads = [load(source, place, 7 + n) for n, (source, place) in enumerate(sources)]
        for copy in loads:
            copy.start()
        for copy in load_tokens:
            copy.start()
        for copy in loads[:4]:
            copy.wait()
        for at in range(line):
            d_a[at] = (d_a[at].astype(F32) + d_b[at].astype(F32)).astype(BF16)
            o_a[at] = (o_a[at].astype(F32) + o_b[at].astype(F32)).astype(BF16)
        for copy in d_sends + o_sends:
            copy.start()
        for copy in loads[4:]:
            copy.wait()

        def total(number, _):
            for which, out in enumerate((g_out, u_out)):
                value = gu_a[number, which].astype(F32)
                for jump in range(line - 1):
                    value = value + gu_b[jump, number, which].astype(F32)
                at = pl.ds(pl.multiple_of((core * blocks + number) * 128, 128), 128)
                out[:, at] = value
                gu_a[number, which] = value.astype(BF16)
            return 0

        lax.fori_loop(0, blocks, total, 0)
        gu_sides[0].start()
        normed_t[...] = normed_ref[...].T
        acc[...] = jnp.zeros_like(acc)

    def own_part(back):
        @pl.when(turn == 0)
        def _():
            value = 0.5 * back[0].astype(F32)
            rows = value.T
            first_stage[:, columns] = rows[:tok]
            first_send[:, columns] = rows[tok:].astype(BF16)
            grad[...] = value.astype(BF16)

        @pl.when(turn > 0)
        def _():
            grad[...] = back[0]

    @pl.when(target == 0)
    def _():
        own_part(back_other)

    @pl.when(target == 1)
    def _():
        own_part(back_own)

    @pl.when(step == 0)
    def _():
        first_part(0).start()

    @pl.when(step == 3)
    def _():
        first_part(1).start()
        store_first.start()

    @pl.when(target < 2)
    def _():
        value = grad[...]
        result = nt(normed_t[...], value)

        @pl.when(target == 0)
        def _():
            sent[turn] = result.astype(BF16).reshape(sent.shape[1:])
            core_send(turn).start()

        @pl.when(target == 1)
        def _():
            core_send(turn).wait()
            theirs = landed[turn].reshape(result.shape).astype(F32)
            landed[turn] = (result + theirs).astype(BF16).reshape(landed.shape[1:])
            y_send(turn).start()

        acc[...] += nt(value.T, full_ref[0, 0])

    @pl.when(step == 6)
    def _():
        for copy in load_tokens:
            copy.wait()
        weight = gains_ref[0:1, :]
        chunk = min(128, tok)
        gain[...] = jnp.zeros_like(gain)
        gain[0, 1:2, :] = mlp_gain_ref[0:1, :]
        for slot in (1, 0):

            def finish(number, _, slot=slot):
                local = pl.ds(pl.multiple_of(number * chunk, chunk), chunk)
                some = pl.ds(pl.multiple_of(slot * tok + number * chunk, chunk), chunk)
                values = xs[some, :].astype(F32)
                scale = lax.rsqrt(jnp.mean(values * values, axis=1, keepdims=True) + epsilon)
                value = acc[some, :]
                gain[0, 0:1, :] += jnp.sum(value * values * scale, axis=0, keepdims=True)
                weighted = value * weight
                inner = jnp.mean(weighted * values, axis=1, keepdims=True)
                result = (
                    scale * weighted
                    - values * (scale * scale * scale) * inner
                    + grad_middle[some, :]
                )
                if slot == 0:
                    acc[some, :] = result
                else:
                    input_send[local, :] = result.astype(BF16)
                return 0

            lax.fori_loop(0, tok // chunk, finish, 0)
            if slot == 1:
                input_part.start()
        gain_send(0, to_core_partner()).start()
        store_input.start()
        gu_sides[0].wait()

        def gather_x(number, _):
            for which, out in enumerate((g_out, u_out)):
                at = pl.ds(pl.multiple_of((core * blocks + number) * 128, 128), 128)
                value = out[:, at] + gu_x[number, which].astype(F32)
                out[:, at] = value
                gu_a[number, which] = value.astype(BF16)
            return 0

        lax.fori_loop(0, blocks, gather_x, 0)
        gu_sides[1].start()
        gain_send(0, to_core_partner()).wait()
        gain[1] = gain[0] + gain_landed[0]
        gain_send(1, to_y_partner()).start()
        for number in range(3):
            y_send(number).wait()

            def add(at, _, number=number):
                value = landed[number, at, y].astype(F32) + y_landed[number, at].astype(F32)
                landed[number, at, y] = value.astype(BF16)
                return 0

            lax.fori_loop(0, line, add, 0)
            for copy in z_sends(number):
                copy.start()
            if number == 0:
                gain_send(1, to_y_partner()).wait()
                gain[2] = gain[1] + gain_landed[1]
                for jump in range(1, line):
                    gain_z(jump, line, gain, gain_landed, gain_sems).start()
        for copy in d_sends + o_sends:
            copy.wait()

        def sum_z(own, places):
            value = own.astype(F32)
            for place in places:
                value = value + place.astype(F32)
            return value

        value = sum_z(d_a[z], [d_landed[jump] for jump in range(line - 1)])
        d_out[:, mine] = value
        d_low[...] = value.astype(BF16)
        d_sides[0].start()
        value = sum_z(o_a[z], [o_landed[jump] for jump in range(line - 1)])
        o_out[:, mine] = value
        s_low[0] = value.astype(BF16)
        square_x(0).start()
        for jump in range(1, line):
            gain_z(jump, line, gain, gain_landed, gain_sems).wait()
        value = gain[2]
        for jump in range(1, line):
            value = value + gain_landed[1 + jump]
        gain[3] = value
        last_gain = send(gain.at[3], gain_landed.at[line + 1], gain_sems, line + 1, to_x_partner())
        last_gain.start()
        for number in range(3):
            for copy in z_sends(number):
                copy.wait()
            value = sum_z(
                landed[number, z, y], [z_landed[number, jump] for jump in range(line - 1)]
            )
            squares[1 + number][:, mine] = value
            s_low[1 + number] = value.astype(BF16)
            square_x(1 + number).start()
        last_gain.wait()
        gain[4] = gain[3] + gain_landed[line + 1]
        gain_out[...] = gain[4, :, pl.ds(pl.multiple_of((2 * z + y) * 128, 128), 128)]
        store_first.wait()
        for number in range(2):
            first_part(number).wait()
        d_sides[0].wait()
        value = d_out[:, mine] + d_x[...].astype(F32)
        d_out[:, mine] = value
        d_low[...] = value.astype(BF16)
        d_sides[1].start()
        input_part.wait()
        for number in range(4):
            square_x(number).wait()
            value = squares[number][:, mine] + s_x[number].astype(F32)
            squares[number][:, mine] = value
            s_low[number] = value.astype(BF16)
            square_core(number).start()
        gu_sides[1].wait()

        def gather_core(number, _):
            for which, out in enumerate((g_out, u_out)):
                at = pl.ds(pl.multiple_of(((1 - core) * blocks + number) * 128, 128), 128)
                out[:, at] = gu_c[number, which].astype(F32)
            return 0

        lax.fori_loop(0, blocks, gather_core, 0)
        d_sides[1].wait()
        d_out[:, others] = d_c[...].astype(F32)
        for number in range(4):
            square_core(number).wait()
            squares[number][:, others] = s_c[number].astype(F32)
        store_input.wait()


def gain_z(jump, line, gain, gain_landed, gain_sems):
    return send(
        gain.at[2], gain_landed.at[1 + jump], gain_sems, 1 + jump, to_z_partner(line, jump)
    )


def tail_carry(
    inputs,
    x_received,
    back_other,
    back_own,
    full,
    normed,
    grad_middle,
    gains,
    mlp_gain,
    gu_mine,
    gu_z,
    d,
    d_y,
    o,
    o_y,
    line,
):
    slots, tok, depth = inputs.shape
    span = slots * tok
    wide = depth // 2
    blocks, _, rows, _ = gu_mine.shape
    down_rows = d.shape[2]
    once = pl.Buffered(1)
    anywhere = pl.BlockSpec(memory_space=pl.ANY)

    def half(s):
        core = lax.axis_index("seq") % 2
        return jnp.where(s < 3, 1 - core, core)

    def kind(s):
        return (s + 2) % 3

    def clear(shape):
        zeros = (0,) * len(shape)
        return pl.BlockSpec(shape, lambda s: zeros, pipeline_mode=once)

    square = jax.ShapeDtypeStruct((rows, depth), F32)
    broad = jax.ShapeDtypeStruct((rows, 2 * blocks * 128), F32)
    tall = jax.ShapeDtypeStruct((down_rows, depth), F32)
    tokens = [jax.ShapeDtypeStruct((tok, depth), dtype) for dtype in (F32, BF16)] * 2
    finals = [square] * 4 + [broad] * 2 + [tall]
    vmem = pltpu.VMEM
    dma = pltpu.SemaphoreType.DMA
    return pl.pallas_call(
        functools.partial(tail_carry_kernel, line, tok, blocks),
        grid=(7,),
        in_specs=[
            anywhere,
            anywhere,
            pl.BlockSpec((1, wide, span), lambda s: (kind(jnp.minimum(s, 2)), 0, 0)),
            pl.BlockSpec((1, wide, span), lambda s: (kind(jnp.clip(s, 3, 5)), 0, 0)),
            pl.BlockSpec(
                (1, 1, depth, wide),
                lambda s: (half(jnp.minimum(s, 5)), kind(jnp.minimum(s, 5)), 0, 0),
            ),
            clear((span, depth)),
            anywhere,
            clear((8, depth)),
            clear((8, depth)),
        ]
        + [anywhere] * 6,
        out_specs=[anywhere] * 4 + [clear((8, 128))] + [clear(final.shape) for final in finals],
        out_shape=tokens + [jax.ShapeDtypeStruct((8, 128), F32)] + finals,
        scratch_shapes=[
            vmem((span, depth), BF16),
            vmem((span, depth), F32),
            vmem((depth, span), BF16),
            vmem((span, depth), F32),
            vmem((wide, span), BF16),
            vmem((3, line, 2, rows, wide), BF16),
            vmem((3, line, 2, rows, wide), BF16),
            vmem((3, line, rows, wide), BF16),
            vmem((3, line - 1, rows, wide), BF16),
            vmem((line, down_rows, wide), BF16),
            vmem((line, down_rows, wide), BF16),
            vmem((line - 1, down_rows, wide), BF16),
            vmem((line, rows, wide), BF16),
            vmem((line, rows, wide), BF16),
            vmem((line - 1, rows, wide), BF16),
            vmem((blocks, 2, rows, 128), BF16),
            vmem((line - 1, blocks, 2, rows, 128), BF16),
            vmem((blocks, 2, rows, 128), BF16),
            vmem((blocks, 2, rows, 128), BF16),
            vmem((down_rows, wide), BF16),
            vmem((down_rows, wide), BF16),
            vmem((down_rows, wide), BF16),
            vmem((4, rows, wide), BF16),
            vmem((4, rows, wide), BF16),
            vmem((4, rows, wide), BF16),
            vmem((tok, depth), F32),
            vmem((tok, depth), BF16),
            vmem((tok, depth), BF16),
            vmem((5, 8, depth), F32),
            vmem((line + 2, 8, depth), F32),
            dma((13,)),
            dma((2, 3)),
            dma((2, 3)),
            dma((2, 3 * (line - 1))),
            dma((2, line - 1)),
            dma((2, line - 1)),
            dma((2, 6)),
            dma((2, 6)),
            dma((2, 3)),
            dma((2, line + 2)),
        ],
        compiler_params=pltpu.CompilerParams(
            dimension_semantics=("arbitrary",),
            vmem_limit_bytes=63 * MIB,
            collective_id=6,
            has_side_effects=True,
        ),
        cost_estimate=pl.CostEstimate(
            flops=12 * span * depth * depth,
            bytes_accessed=24 * span * depth + 12 * depth * depth,
            transcendentals=0,
        ),
        name="tail_carry",
    )(
        inputs,
        x_received,
        back_other,
        back_own,
        full,
        normed,
        grad_middle,
        gains,
        mlp_gain,
        gu_mine,
        gu_z,
        d,
        d_y,
        o,
        o_y,
    )


def finish_kernel(place, *refs):
    count = (len(refs) - 2 * 3 - 3) // 2
    tokens, plain = refs[:6], refs[6 : 6 + count]
    outs = refs[6 + count :]
    side = place[0]
    for number in range(3):
        outs[number][side] = tokens[2 * number][...].reshape(tokens[2 * number + 1].shape)
        outs[number][1 - side] = tokens[2 * number + 1][...].astype(F32)
    for number in range(count):
        outs[3 + number][...] = plain[number][...]


def finish(outputs, tokens, plain, side):
    _, tok, depth = outputs[0].shape
    steps = 4
    tile = tok // steps
    row = pl.BlockSpec((tile, depth), lambda s, p: (s, 0))
    tiles = [
        pl.BlockSpec((value.shape[0] // steps, value.shape[1]), lambda s, p: (s, 0))
        for value in plain
    ]
    grid_spec = pltpu.PrefetchScalarGridSpec(
        num_scalar_prefetch=1,
        grid=(steps,),
        in_specs=[pl.BlockSpec((1, tile, depth), lambda s, p: (p[0], s, 0))] + [row] * 5 + tiles,
        out_specs=[pl.BlockSpec((2, tile, depth), lambda s, p: (0, s, 0))] * 3 + tiles,
    )
    return pl.pallas_call(
        finish_kernel,
        out_shape=[jax.ShapeDtypeStruct((2, tok, depth), F32)] * 3
        + [jax.ShapeDtypeStruct(value.shape, value.dtype) for value in plain],
        grid_spec=grid_spec,
        compiler_params=parameters(60),
        cost_estimate=pl.CostEstimate(
            flops=tok * depth, bytes_accessed=60 * tok * depth, transcendentals=0
        ),
        name="finish",
    )(side, *outputs, *tokens, *plain)


def shards(
    inputs,
    first_values,
    out_grad,
    attn_gain,
    query_weight,
    key_weight,
    value_weight,
    output_weight,
    mlp_gain,
    gate_weight,
    up_weight,
    down_weight,
):
    slots, tok, _ = inputs.shape
    groups = lax.axis_size("seq")
    parts = lax.axis_size("fsdp")
    line = parts // 2
    count = groups // slots
    length = tok * groups
    span = slots * tok
    seat = lax.axis_index("seq")
    shard = lax.axis_index("fsdp")
    side = seat // count
    rank = seat % count
    core = seat % 2
    z, y = shard // 2, shard % 2
    wide = D // 2
    width = D // count

    def along_seq(value, partner):
        return lax.ppermute(value, "seq", [(i, partner(i)) for i in range(groups)])

    def along_fsdp(value, partner):
        return lax.ppermute(value, "fsdp", [(i, partner(i)) for i in range(parts)])

    def to_core(value):
        return along_seq(value, lambda i: i ^ 1)

    def to_y(value):
        return along_fsdp(value, lambda i: i ^ 1)

    def to_z(value, jump):
        return along_fsdp(value, lambda i: (i + 2 * jump) % parts)

    def after(value, *others):
        return lax.optimization_barrier((value,) + others)[0]

    def to_sequence(values):
        taken = []
        for jump in range(1, slots):
            sent = lax.dynamic_index_in_dim(values, (side + jump) % slots, 0, keepdims=False)
            taken.append(along_seq(sent, lambda i: (i + jump * count) % groups))
        return taken

    def to_home(whole, sent):
        for jump in range(1, slots):
            part = sent[(jump - 1) * tok : jump * tok]
            part = along_seq(part, lambda i: (i - jump * count) % groups)
            whole = land(whole, part, ((side + jump) % slots)[None])
        return whole

    def rank_up(i, jump):
        return (i // count) * count + (i % count + jump) % count

    def rank_down(i, jump):
        return (i // count) * count + (i % count - jump) % count

    def halves_to_ranks(other, own, axis):
        if count == 2:
            return [other, own]
        return [
            lax.dynamic_slice_in_dim(
                join(other, own, axis), ((rank + 1 + number) % count) * width, width, axis
            )
            for number in range(count)
        ]

    def join(other, own, axis):
        first = jnp.where(core == 0, own, other)
        second = jnp.where(core == 0, other, own)
        return jnp.concatenate([first, second], axis=axis)

    def ranks_to_halves(pieces, axis):
        if count == 2:
            return pieces
        shape = list(pieces[0].shape)
        shape[axis] = D
        whole = jnp.zeros(shape, pieces[0].dtype)
        for number in range(count):
            whole = lax.dynamic_update_slice_in_dim(
                whole, pieces[number], ((rank + 1 + number) % count) * width, axis
            )
        return [
            lax.dynamic_slice_in_dim(whole, which * wide, wide, axis)
            for which in (1 - core, core)
        ]

    def exchange(pieces):
        received = [
            along_seq(pieces[jump - 1], lambda i: rank_up(i, jump)) for jump in range(1, count)
        ]
        return received + [pieces[count - 1]]

    def exchange_back(pieces):
        received = [
            along_seq(pieces[jump - 1], lambda i: rank_down(i, jump)) for jump in range(1, count)
        ]
        return received + [pieces[count - 1]]

    def split(*weights):
        results = []
        for which in (core, 1 - core):
            columns = []
            for weight in weights:
                size = weight.shape[1] // 2
                columns.append(lax.dynamic_slice_in_dim(weight, which * size, size, 1))
            results.append(columns)
        return results

    def gather_z(half):
        return [half] + [to_z(half, jump) for jump in range(1, line)]

    def gather_rest(along_z, other):
        along_y = [to_y(piece) for piece in along_z]
        own = [piece for pair in zip(along_z, along_y) for piece in pair]
        return (own, [other] + [to_core(piece) for piece in own[1:]])

    numbers = []
    for jump in range(line):
        for flip in range(2):
            numbers.append(((z - jump) % line) * 2 + (y ^ flip))
    place = jnp.stack([side, core] + numbers).astype(jnp.int32)

    def low(value):
        return value.astype(BF16)

    def add(a, b):
        return low(a.astype(F32) + b.astype(F32))

    def pick(value, index, axis):
        return lax.dynamic_index_in_dim(value, index, axis, keepdims=False)

    def along_x_and_core(total):
        mine = low(total)
        for jump in range(1, groups // 2):
            total = total + along_seq(mine, lambda i: (i + 2 * jump) % groups).astype(F32)
        mine = low(total)
        return (mine, to_core(mine))

    def along_z_and_on(partial):
        total = partial(z)
        for jump in range(1, line):
            total = total + to_z(low(partial((z + jump) % line)), jump).astype(F32)
        return along_x_and_core(total)

    def scatter(sent, kept, rows_axis):
        shape = kept.shape
        rows = shape[rows_axis] // parts
        cut = shape[:rows_axis] + (line, 2, rows) + shape[rows_axis + 1 :]
        received = to_core(sent).reshape(cut)
        kept = kept.reshape(cut)
        axis = rows_axis + 1
        received_y = to_y(add(pick(kept, 1 - y, axis), pick(received, 1 - y, axis)))
        kept_y = pick(kept, y, axis), pick(received, y, axis)

        def partial(index):
            total = pick(kept_y[0], index, rows_axis).astype(F32)
            total = total + pick(kept_y[1], index, rows_axis).astype(F32)
            return total + pick(received_y, index, rows_axis).astype(F32)

        return along_z_and_on(partial)

    def columns(mine, others):
        first = jnp.where(core == 0, mine, others)
        second = jnp.where(core == 0, others, mine)
        return jnp.concatenate([first, second], axis=-1).astype(F32)

    def everywhere(value):
        value = value + to_core(value)
        value = value + to_y(value)
        total = value
        for jump in range(1, line):
            total = total + to_z(value, jump)
        value = total
        for jump in range(1, groups // 2):
            total = total + along_seq(value, lambda i: (i + 2 * jump) % groups)
        return total

    steps = jnp.arange(slots, dtype=jnp.int32)
    starts = ((side - steps) % slots) * (count * tok) + rank * tok
    positions = (starts[:, None] + jnp.arange(tok, dtype=jnp.int32)[None]).reshape(span)
    freqs = rope_base ** (-(jnp.arange(HALF, dtype=F32) * 2.0 / HEAD_DIM))

    def tables(positions):
        angles = freqs[:, None] * positions.astype(F32)[None, :]
        return (jnp.cos(angles), jnp.sin(angles))

    cosine, sine = tables(positions)
    full_cos, full_sin = tables(jnp.arange(length, dtype=jnp.int32))
    sources = jnp.concatenate(
        [(rank - 1 - jnp.arange(count - 1, dtype=jnp.int32)) % count, rank[None]]
    ).astype(jnp.int32)
    order = (((side - steps) % slots)[None, :] * count + sources[:, None]).reshape(-1)
    order = order.astype(jnp.int32)

    gains = jnp.pad(jnp.stack([attn_gain, mlp_gain], axis=1), ((0, 0), (0, 126)))
    gate_halves, up_halves, out_halves, down_halves = (
        [half[0] for half in split(weight)]
        for weight in (gate_weight, up_weight, output_weight, down_weight)
    )

    whole_lanes = (slots, count) == (2, 2) and (D // parts) % 128 == 0
    if whole_lanes:
        parts_of = lambda ref: [ref.reshape(-1, ref.shape[-1])]
        (q_half,), (k_half,), (v_half,) = (
            split(weight)[:1] for weight in (query_weight, key_weight, value_weight)
        )
        (
            tokens,
            _,
            grads_early,
            heads_own,
            heads_received,
            normed,
            qkv_full,
            gains_full,
            out_own,
            out_other,
            down_own,
        ) = front(
            inputs,
            first_values,
            out_grad,
            jnp.concatenate([q_half[0], gains], axis=1),
            k_half[0],
            v_half[0],
            out_halves[0],
            down_halves[0],
            cosine,
            sine,
            line,
        )
        qkv_full = qkv_full.reshape(2, 3, D, wide)
        tokens = [tokens]
        pieces = [heads_received, heads_own]
        (
            mix_received,
            att_own,
            lse,
            middle,
            normed2,
            out_full,
            att_other,
            grads,
            down_own,
            down_other,
            gate_own,
            gate_other,
            up_own,
            up_other,
        ) = attend_carry(
            heads_received,
            heads_own,
            inputs,
            tokens[0],
            gains_full,
            out_own.reshape(D, wide),
            out_other.reshape(D, wide),
            out_grad,
            grads_early,
            down_own,
            gate_halves[0],
            up_halves[0],
            line,
        )
        mixes = [mix_received, att_own]
        grads = [grads]
        gate_pieces = parts_of(gate_own), parts_of(gate_other)
        up_pieces = parts_of(up_own), parts_of(up_other)
        down_pieces = parts_of(down_own), parts_of(down_other)
    else:
        qkv = [
            jnp.concatenate(half + [gains], axis=1)
            for half in split(query_weight, key_weight, value_weight)
        ]
        tokens = to_sequence(inputs)
        firsts = to_sequence(first_values)
        grads = to_sequence(out_grad)
        qkv_own, qkv_other = gather_rest(gather_z(qkv[0]), qkv[1])
        out_own, out_other = gather_rest(gather_z(out_halves[0]), out_halves[1])
        gate_pieces = gather_rest(gather_z(gate_halves[0]), gate_halves[1])
        up_pieces = gather_rest(gather_z(up_halves[0]), up_halves[1])
        down_pieces = gather_rest(gather_z(down_halves[0]), down_halves[1])
        heads_other, heads_own, normed, qkv_full, gains_full = project(
            inputs, tokens, first_values, firsts, qkv_own, qkv_other, cosine, sine, place
        )
        pieces = exchange(halves_to_ranks(heads_other, heads_own, 1))
        mixes, lse = attend(pieces, order, slots)
        att_other, att_own = ranks_to_halves(exchange_back(mixes), 0)
        middle, normed2, out_full = output_projection(
            inputs, tokens, out_own, out_other, att_other, att_own, gains_full, place
        )

    if whole_lanes:
        (
            outputs,
            outputs_sent,
            grad_middle,
            low_grad,
            mlp_gain_grad,
            gu_reduced,
            down_reduced,
            gu_y,
        ) = mlp_carry(
            out_grad,
            grads[0],
            middle,
            normed2,
            gains_full,
            (gate_pieces[0][0], gate_pieces[1][0]),
            (up_pieces[0][0], up_pieces[1][0]),
            (down_pieces[0][0], down_pieces[1][0]),
            line,
        )
        ga_own, ga_received, out_kept, out_landed = grad_attended_carry(
            low_grad, out_full, att_other, att_own, line
        )
        down_reduced = down_reduced.reshape(line, 2, -1, wide)
        out_kept = out_kept.reshape(line, 2, -1, wide)
        out_landed = out_landed.reshape(line, 2, -1, wide)
        (
            back_own,
            back_other,
            outputs_received,
            gu_mine,
            gu_z,
            down_y,
            out_mine,
            out_y,
        ) = attend_back_carry(
            pieces,
            mixes,
            [ga_received, ga_own],
            lse,
            full_cos,
            full_sin,
            outputs_sent,
            gu_reduced,
            gu_y,
            down_reduced,
            out_kept,
            out_landed,
            line,
        )
        input_own, input_received, first_own, first_received, *rest = tail_carry(
            inputs,
            tokens[0],
            back_other,
            back_own,
            qkv_full,
            normed,
            grad_middle,
            gains_full,
            mlp_gain_grad,
            gu_mine,
            gu_z,
            down_reduced,
            down_y,
            out_mine,
            out_y,
            line,
        )
        gain_grads = rest[0]
        outputs, input_grad, first_grad, *rest = finish(
            (outputs,),
            (outputs_received, input_own, input_received, first_own, first_received),
            rest[1:],
            side[None],
        )
        query_grad, key_grad, value_grad, output_grad, gate_grad, up_grad, down_grad = rest
    else:
        (
            outputs,
            outputs_sent,
            grad_middle,
            low_grad,
            mlp_gain_grad,
            gu_sent,
            gu_kept,
            down_sent,
            down_kept,
        ) = mlp(out_grad, grads, middle, normed2, gains_full, gate_pieces, up_pieces, down_pieces, place)
        ga_other, ga_own, out_sent, out_kept = grad_attended(
            low_grad, out_full, att_other, att_own, place
        )
        gate_up_grad = scatter(gu_sent, gu_kept, 1)
        down_grad = scatter(down_sent.reshape(-1, wide), down_kept.reshape(-1, wide), 0)
        output_grad = scatter(out_sent, out_kept, 0)
        grad_heads = exchange(halves_to_ranks(ga_other, ga_own, 0))
        back = attend_back(pieces, mixes, grad_heads, lse, full_cos, full_sin, order, slots)
        back_other, back_own = ranks_to_halves(exchange_back(back), 1)
        outputs = to_home(outputs, outputs_sent)
        input_grad, input_sent, first_grad, first_sent, gain_grads, qkv_sent, qkv_kept = tail(
            inputs,
            tokens,
            back_other,
            back_own,
            qkv_full,
            normed,
            grad_middle,
            gains_full,
            mlp_gain_grad,
            place,
        )
        query_grad, key_grad, value_grad = columns(*scatter(qkv_sent, qkv_kept, 1))
        gate_grad, up_grad = columns(*gate_up_grad)
        output_grad = columns(*output_grad)
        down_grad = columns(*down_grad)
        gain_grads = everywhere(gain_grads)
        gain_grads = lax.dynamic_slice_in_dim(gain_grads, shard * (D // parts), D // parts, 1)
        input_grad = to_home(input_grad, input_sent)
        first_grad = to_home(first_grad, first_sent)

    return (
        outputs,
        input_grad,
        first_grad,
        gain_grads[0],
        gain_grads[1],
        query_grad,
        key_grad,
        value_grad,
        output_grad,
        gate_grad,
        up_grad,
        down_grad,
    )


def solution(mesh):
    token_spec = P("fsdp", "seq", None)
    weight_spec = P("fsdp", None)
    gain_spec = P("fsdp")
    return jax.shard_map(
        shards,
        mesh=mesh,
        in_specs=(token_spec,) * 3
        + (gain_spec,)
        + (weight_spec,) * 4
        + (gain_spec,)
        + (weight_spec,) * 3,
        out_specs=(token_spec,) * 3 + (gain_spec,) * 2 + (weight_spec,) * 7,
        check_vma=False,
    )
```

```python
import functools
import math

import jax
import jax.numpy as jnp
from jax import lax
from jax.experimental import pallas as pl
from jax.experimental.pallas import tpu as pltpu
from jax.sharding import PartitionSpec as P

D = 1024
HEADS = 16
HEAD_DIM = 64
HALF = HEAD_DIM // 2
PAIR = 2 * HEAD_DIM
F32 = jnp.float32
BF16 = jnp.bfloat16
NEG = -1e30
MIB = 1024 * 1024
epsilon = 1e-06
rope_base = 10000.0


def dot(a, b):
    return lax.dot_general(a, b, (((1,), (0,)), ((), ())), preferred_element_type=F32)


def head_rows(value, head):
    row = lax.broadcasted_iota(jnp.int32, value.shape, 0)
    return jnp.where((row // HEAD_DIM) == head, value, jnp.zeros_like(value))


def head_lanes(value, head):
    lane = lax.broadcasted_iota(jnp.int32, value.shape, 1)
    return jnp.where((lane // HEAD_DIM) == head, value, jnp.zeros_like(value))


def causal(scores):
    side = scores.shape[0]
    square = scores[:, :side]
    key = lax.broadcasted_iota(jnp.int32, square.shape, 0)
    query = lax.broadcasted_iota(jnp.int32, square.shape, 1)
    square = jnp.where(key <= query, square, NEG)
    if scores.shape[1] == side:
        return square
    return jnp.concatenate([square, scores[:, side:]], axis=1)


def attend_body(length, tile_k, qz, kn, vt, ot, lse_ref):
    def score(sub, head):
        start = sub * tile_k
        return causal(dot(kn[start : start + tile_k, :], qz[head, :, start:]))

    def absorb(sub, head, carry, scores):
        peak, total, mixed = carry
        start = sub * tile_k
        new_peak = jnp.maximum(peak, jnp.max(scores, axis=0, keepdims=True))
        weights = jnp.exp(scores - new_peak)
        fade = jnp.exp(peak - new_peak)
        total = total * fade + jnp.sum(weights, axis=0, keepdims=True)
        values = vt[head * HEAD_DIM : (head + 1) * HEAD_DIM, start : start + tile_k]
        mixed = mixed * fade + dot(values, weights.astype(BF16))
        return (new_peak, total, mixed)

    tiles = [(sub, head) for sub in range(length // tile_k) for head in range(2)]
    carries = [
        (
            jnp.full((1, length), NEG, F32),
            jnp.zeros((1, length), F32),
            jnp.zeros((HEAD_DIM, length), F32),
        )
        for _ in range(2)
    ]
    ahead = score(*tiles[0])
    for number, (sub, head) in enumerate(tiles):
        scores = ahead
        if number + 1 < len(tiles):
            ahead = score(*tiles[number + 1])
        peak, total, mixed = absorb(sub, head, carries[head], scores)
        done = slice(sub * tile_k, (sub + 1) * tile_k)
        rows = slice(head * HEAD_DIM, (head + 1) * HEAD_DIM)
        ot[rows, done] = (mixed[:, :tile_k] / total[:, :tile_k]).astype(BF16)
        lse_ref[0, head : head + 1, done] = peak[:, :tile_k] + jnp.log(total[:, :tile_k])
        carries[head] = (peak[:, tile_k:], total[:, tile_k:], mixed[:, tile_k:])


def attend_kernel(count, slots, tok, tile_k, order, *refs):
    pieces = refs[:count]
    outs = refs[count : 2 * count]
    lse_ref = refs[2 * count]
    qz, kn, vt, ot = refs[2 * count + 1 :]
    for source in range(count):
        for slot in range(slots):
            cols = pl.ds(pl.multiple_of(order[source * slots + slot] * tok, tok), tok)
            take = slice(slot * tok, (slot + 1) * tok)
            query = pieces[source][0, :, take] * jnp.asarray(HEAD_DIM**-0.5, BF16)
            for head in range(2):
                qz[head, :, cols] = head_rows(query, head)
            kn[cols, :] = pieces[source][1, :, take].T
            vt[:, cols] = pieces[source][2, :, take]
    length = count * slots * tok
    attend_body(length, tile_k, qz, kn, vt, ot, lse_ref)
    for source in range(count):
        for slot in range(slots):
            cols = pl.ds(pl.multiple_of(order[source * slots + slot] * tok, tok), tok)
            outs[source][:, slot * tok : (slot + 1) * tok] = ot[:, cols]


def attend(pieces, order, slots):
    count = len(pieces)
    width, span = pieces[0].shape[1:]
    tok = span // slots
    length = count * span
    pairs = width // PAIR
    tile_k = min(256, length)
    grid_spec = pltpu.PrefetchScalarGridSpec(
        num_scalar_prefetch=1,
        grid=(pairs,),
        in_specs=[pl.BlockSpec((3, PAIR, span), lambda p, o: (0, p, 0))] * count,
        out_specs=[pl.BlockSpec((PAIR, span), lambda p, o: (p, 0))] * count
        + [pl.BlockSpec((1, 8, length), lambda p, o: (p, 0, 0))],
        scratch_shapes=[
            pltpu.VMEM((2, PAIR, length), BF16),
            pltpu.VMEM((length, PAIR), BF16),
            pltpu.VMEM((PAIR, length), BF16),
            pltpu.VMEM((PAIR, length), BF16),
        ],
    )
    area = pairs * 2 * length * length // 2
    results = pl.pallas_call(
        functools.partial(attend_kernel, count, slots, tok, tile_k),
        out_shape=[jax.ShapeDtypeStruct((width, span), BF16)] * count
        + [jax.ShapeDtypeStruct((pairs, 8, length), F32)],
        grid_spec=grid_spec,
        compiler_params=pltpu.CompilerParams(
            dimension_semantics=("arbitrary",), vmem_limit_bytes=48 * MIB
        ),
        cost_estimate=pl.CostEstimate(
            flops=area * 1024, bytes_accessed=8 * width * length, transcendentals=area
        ),
        name="attend",
    )(order, *pieces)
    return (results[:count], results[count])


def attend_back_body(
    pieces,
    mixes,
    grads,
    columns,
    tok,
    length,
    tile_q,
    tile_k,
    lse_ref,
    qz,
    gz,
    qn,
    gn,
    kn,
    vn,
    kt,
    inner,
    dq,
    dk,
    dv,
):
    slots = pieces[0].shape[2] // tok
    for source in range(len(pieces)):
        for slot in range(slots):
            cols = columns(source, slot)
            take = slice(slot * tok, (slot + 1) * tok)
            query = pieces[source][0, :, take] * jnp.asarray(HEAD_DIM**-0.5, BF16)
            grad = grads[source][:, take]
            query_rows = query.T
            grad_rows = grad.T
            for head in range(2):
                qz[head, :, cols] = head_rows(query, head)
                gz[head, :, cols] = head_rows(grad, head)
                qn[head, cols, :] = head_lanes(query_rows, head)
                gn[head, cols, :] = head_lanes(grad_rows, head)
            key = pieces[source][1, :, take]
            kt[:, cols] = key
            kn[cols, :] = key.T
            vn[cols, :] = pieces[source][2, :, take].T
            both = grad.astype(F32) * mixes[source][:, take].astype(F32)
            for head in range(2):
                inner[head : head + 1, cols] = jnp.sum(
                    both[head * HEAD_DIM : (head + 1) * HEAD_DIM], axis=0, keepdims=True
                )
    dq[...] = jnp.zeros_like(dq)
    steps = tile_q // tile_k

    def tile(key_start, query_start, width, masked, carry):
        grad_keys, grad_values = carry
        keys = kn[pl.ds(key_start, tile_k), :]
        values = vn[pl.ds(key_start, tile_k), :]
        cols = pl.ds(query_start, width)
        for head in range(2):
            rows = slice(head * HEAD_DIM, (head + 1) * HEAD_DIM)
            scores = dot(keys, qz[head, :, cols])
            if masked:
                scores = causal(scores)
            probs = jnp.exp(scores - lse_ref[0, head : head + 1, cols])
            grad_probs = dot(values, gz[head, :, cols])
            grad_scores = (probs * (grad_probs - inner[head : head + 1, cols])).astype(BF16)
            grad_values = grad_values + dot(probs.astype(BF16), gn[head, cols, :])
            grad_keys = grad_keys + dot(grad_scores, qn[head, cols, :])
            dq[rows, cols] += dot(kt[rows, pl.ds(key_start, tile_k)], grad_scores)
        return (grad_keys, grad_values)

    def one(number, _):
        base = pl.multiple_of(number * tile_q, tile_q)
        for sub in range(steps):
            skip = sub * tile_k
            key_start = pl.multiple_of(base + skip, tile_k)
            carry = (jnp.zeros((tile_k, PAIR), F32), jnp.zeros((tile_k, PAIR), F32))
            carry = tile(key_start, key_start, tile_q - skip, True, carry)

            def body(step, carry):
                return tile(
                    key_start, pl.multiple_of(step * tile_q, tile_q), tile_q, False, carry
                )

            carry = lax.fori_loop(number + 1, length // tile_q, body, carry)
            dk[pl.ds(key_start, tile_k), :] = carry[0]
            dv[pl.ds(key_start, tile_k), :] = carry[1]
        return 0

    lax.fori_loop(0, length // tile_q, one, 0)


def turn_back(dq, dk, dv, cols, cosine, sine):
    half = HEAD_DIM // 2
    results = []
    for grad in (dq[:, cols] * (HEAD_DIM**-0.5), dk[cols, :].T):
        turned = []
        for head in range(2):
            low = head * HEAD_DIM
            first = grad[low : low + half]
            second = grad[low + half : low + 2 * half]
            turned += [first * cosine + second * sine, second * cosine - first * sine]
        results.append(jnp.concatenate(turned, axis=0).astype(BF16))
    results.append(dv[cols, :].T.astype(BF16))
    return results


def attend_back_kernel(count, slots, tok, tile_q, tile_k, order, *refs):
    pieces = refs[:count]
    mixes = refs[count : 2 * count]
    grads = refs[2 * count : 3 * count]
    lse_ref, cos_ref, sin_ref = refs[3 * count : 3 * count + 3]
    outs = refs[3 * count + 3 : 4 * count + 3]
    scratch = refs[4 * count + 3 :]
    dq, dk, dv = scratch[-3:]

    def columns(source, slot):
        return pl.ds(pl.multiple_of(order[source * slots + slot] * tok, tok), tok)

    attend_back_body(
        pieces,
        mixes,
        grads,
        columns,
        tok,
        count * slots * tok,
        tile_q,
        tile_k,
        lse_ref,
        *scratch,
    )
    for source in range(count):
        for slot in range(slots):
            cols = columns(source, slot)
            results = turn_back(dq, dk, dv, cols, cos_ref[:, cols], sin_ref[:, cols])
            for which, result in enumerate(results):
                outs[source][which, :, slot * tok : (slot + 1) * tok] = result


def attend_back(pieces, mixes, grads, lse, cosine, sine, order, slots):
    count = len(pieces)
    width, span = pieces[0].shape[1:]
    tok = span // slots
    length = count * span
    pairs = width // PAIR
    tile_q = min(512, length)
    tile_k = min(256, length)
    triple = pl.BlockSpec((3, PAIR, span), lambda p, o: (0, p, 0))
    single = pl.BlockSpec((PAIR, span), lambda p, o: (p, 0))
    table = pl.BlockSpec((HEAD_DIM // 2, length), lambda p, o: (0, 0))
    grid_spec = pltpu.PrefetchScalarGridSpec(
        num_scalar_prefetch=1,
        grid=(pairs,),
        in_specs=[triple] * count
        + [single] * (2 * count)
        + [pl.BlockSpec((1, 8, length), lambda p, o: (p, 0, 0)), table, table],
        out_specs=[triple] * count,
        scratch_shapes=[
            pltpu.VMEM((2, PAIR, length), BF16),
            pltpu.VMEM((2, PAIR, length), BF16),
            pltpu.VMEM((2, length, PAIR), BF16),
            pltpu.VMEM((2, length, PAIR), BF16),
            pltpu.VMEM((length, PAIR), BF16),
            pltpu.VMEM((length, PAIR), BF16),
            pltpu.VMEM((PAIR, length), BF16),
            pltpu.VMEM((8, length), F32),
            pltpu.VMEM((PAIR, length), F32),
            pltpu.VMEM((length, PAIR), F32),
            pltpu.VMEM((length, PAIR), F32),
        ],
    )
    area = pairs * 2 * length * length // 2
    return pl.pallas_call(
        functools.partial(attend_back_kernel, count, slots, tok, tile_q, tile_k),
        out_shape=[jax.ShapeDtypeStruct((3, width, span), BF16)] * count,
        grid_spec=grid_spec,
        compiler_params=pltpu.CompilerParams(
            dimension_semantics=("arbitrary",), vmem_limit_bytes=56 * MIB
        ),
        cost_estimate=pl.CostEstimate(
            flops=area * 2560, bytes_accessed=16 * width * length, transcendentals=area
        ),
        name="attend_back",
    )(order, *pieces, *mixes, *grads, lse, cosine, sine)


def nt(a, b):
    return lax.dot_general(a, b, (((1,), (1,)), ((), ())), preferred_element_type=F32)


def whole_block(shape):
    zeros = (0,) * len(shape)
    return pl.BlockSpec(shape, lambda *_: zeros)


def parameters(mib):
    return pltpu.CompilerParams(dimension_semantics=("arbitrary",), vmem_limit_bytes=mib * MIB)


def project_kernel(slots, tok, count, rows, place, *refs):
    xs, firsts = refs[:slots], refs[slots : 2 * slots]
    own = refs[2 * slots : 2 * slots + count]
    other = refs[2 * slots + count : 2 * slots + 2 * count]
    cos_ref, sin_ref = refs[2 * slots + 2 * count : 2 * slots + 2 * count + 2]
    other_ref, own_ref, normed_ref, full_ref, gains_ref, column = refs[2 * slots + 2 * count + 2 :]
    step = pl.program_id(0)
    target, kind = step // 3, step % 3
    core = place[1]
    half = jnp.where(target == 0, 1 - core, core)
    depth = normed_ref.shape[1]
    wide = own_ref.shape[1]

    @pl.when(step == 0)
    def _():
        for number in range(count):
            at = pl.ds(pl.multiple_of(place[2 + number] * rows, rows), rows)
            for which in range(3):
                columns = slice(which * wide, (which + 1) * wide)
                full_ref[core, which, at, :] = own[number][:, columns]
                full_ref[1 - core, which, at, :] = other[number][:, columns]
            column[at, :] = own[number][:, 3 * wide :]
        gains_ref[...] = column[...].T[:8].astype(F32)
        gain = gains_ref[0:1, :]
        for slot in range(slots):
            values = xs[slot][...].reshape(tok, depth).astype(F32)
            scale = lax.rsqrt(jnp.mean(values * values, axis=1, keepdims=True) + epsilon)
            normed_ref[slot * tok : (slot + 1) * tok, :] = (values * scale * gain).astype(BF16)

    weight = full_ref[half, kind]
    raw = nt(weight.T, normed_ref[...])

    def store(value):
        @pl.when(target == 0)
        def _():
            other_ref[0] = value

        @pl.when(target == 1)
        def _():
            own_ref[0] = value

    @pl.when(kind < 2)
    def _():
        parts = raw.reshape(wide // HEAD_DIM, 2, HALF, raw.shape[1])
        first, second = parts[:, 0], parts[:, 1]
        cosine, sine = cos_ref[...][None], sin_ref[...][None]
        turned = jnp.stack(
            [first * cosine - second * sine, first * sine + second * cosine], axis=1
        )
        store(turned.reshape(raw.shape).astype(BF16))

    @pl.when(kind == 2)
    def _():
        first = jnp.concatenate(
            [ref[...].reshape(tok, wide).T.astype(F32) for ref in firsts], axis=1
        )
        store((0.5 * raw + 0.5 * first).astype(BF16))


def project(inputs, received, firsts, firsts_received, own, other, cosine, sine, place):
    slots, tok, depth = inputs.shape
    count, rows = len(own), own[0].shape[0]
    wide = depth // 2
    span = slots * tok

    def half(s, p):
        return jnp.where(s < 3, 1 - p[1], p[1])

    x_specs = [pl.BlockSpec((1, tok, depth), lambda s, p: (p[0], 0, 0))]
    x_specs += [whole_block((tok, depth))] * (slots - 1)
    first_specs = [pl.BlockSpec((1, tok, wide), lambda s, p: (p[0], 0, half(s, p)))]
    first_specs += [pl.BlockSpec((tok, wide), lambda s, p: (0, half(s, p)))] * (slots - 1)
    grid_spec = pltpu.PrefetchScalarGridSpec(
        num_scalar_prefetch=1,
        grid=(6,),
        in_specs=x_specs
        + first_specs
        + [whole_block(own[0].shape)] * (2 * count)
        + [whole_block((HALF, span))] * 2,
        out_specs=[
            pl.BlockSpec((1, wide, span), lambda s, p: (jnp.minimum(s, 2), 0, 0)),
            pl.BlockSpec((1, wide, span), lambda s, p: (jnp.maximum(s - 3, 0), 0, 0)),
            whole_block((span, depth)),
            whole_block((2, 3, depth, wide)),
            whole_block((8, depth)),
        ],
        scratch_shapes=[pltpu.VMEM((depth, 128), BF16)],
    )
    return pl.pallas_call(
        functools.partial(project_kernel, slots, tok, count, rows),
        out_shape=[
            jax.ShapeDtypeStruct((3, wide, span), BF16),
            jax.ShapeDtypeStruct((3, wide, span), BF16),
            jax.ShapeDtypeStruct((span, depth), BF16),
            jax.ShapeDtypeStruct((2, 3, depth, wide), BF16),
            jax.ShapeDtypeStruct((8, depth), F32),
        ],
        grid_spec=grid_spec,
        compiler_params=parameters(56),
        cost_estimate=pl.CostEstimate(
            flops=6 * span * depth * depth,
            bytes_accessed=2 * (8 * span * depth + 6 * depth * depth),
            transcendentals=0,
        ),
        name="project",
    )(place, inputs, *received, firsts, *firsts_received, *own, *other, cosine, sine)


def output_kernel(slots, tok, count, rows, place, *refs):
    xs = refs[:slots]
    own = refs[slots : slots + count]
    other = refs[slots + count : slots + 2 * count]
    att_other, att_own, gains_ref = refs[slots + 2 * count : slots + 2 * count + 3]
    middle_ref, normed_ref, full_ref = refs[slots + 2 * count + 3 :]
    step = pl.program_id(0)
    core = place[1]
    wide = att_own.shape[0]
    depth = 2 * wide
    mine = pl.ds(pl.multiple_of(core * wide, wide), wide)
    others = pl.ds(pl.multiple_of((1 - core) * wide, wide), wide)

    @pl.when(step == 0)
    def _():
        for number in range(count):
            at = pl.ds(pl.multiple_of(place[2 + number] * rows, rows), rows)
            full_ref[at, mine] = own[number][...]
            full_ref[at, others] = other[number][...]

    total = dot(att_own[...].T, full_ref[mine, :]) + dot(att_other[...].T, full_ref[others, :])
    for slot in range(slots):

        @pl.when(step == slot)
        def _(slot=slot):
            middle_ref[...] = xs[slot][...].reshape(tok, depth).astype(F32) + total

    middle = middle_ref[...]
    scale = lax.rsqrt(jnp.mean(middle * middle, axis=1, keepdims=True) + epsilon)
    normed_ref[...] = (middle * scale * gains_ref[1:2, :]).astype(BF16)


def output_projection(inputs, received, own, other, att_other, att_own, gains, place):
    slots, tok, depth = inputs.shape
    count, rows = len(own), own[0].shape[0]
    wide = depth // 2
    span = slots * tok
    x_specs = [pl.BlockSpec((1, tok, depth), lambda s, p: (p[0], 0, 0))]
    x_specs += [whole_block((tok, depth))] * (slots - 1)
    grid_spec = pltpu.PrefetchScalarGridSpec(
        num_scalar_prefetch=1,
        grid=(slots,),
        in_specs=x_specs
        + [whole_block(own[0].shape)] * (2 * count)
        + [pl.BlockSpec((wide, tok), lambda s, p: (0, s))] * 2
        + [whole_block((8, depth))],
        out_specs=[
            pl.BlockSpec((tok, depth), lambda s, p: (s, 0)),
            pl.BlockSpec((tok, depth), lambda s, p: (s, 0)),
            whole_block((depth, depth)),
        ],
    )
    return pl.pallas_call(
        functools.partial(output_kernel, slots, tok, count, rows),
        out_shape=[
            jax.ShapeDtypeStruct((span, depth), F32),
            jax.ShapeDtypeStruct((span, depth), BF16),
            jax.ShapeDtypeStruct((depth, depth), BF16),
        ],
        grid_spec=grid_spec,
        compiler_params=parameters(56),
        cost_estimate=pl.CostEstimate(
            flops=2 * span * depth * depth,
            bytes_accessed=12 * span * depth + 4 * depth * depth,
            transcendentals=0,
        ),
        name="output_projection",
    )(place, inputs, *received, *own, *other, att_other, att_own, gains)


def mlp_kernel(slots, tok, count, rows, down_rows, blocks, place, *refs):
    grads = refs[:slots]
    middle_ref, normed_ref, gains_ref = refs[slots : slots + 3]
    base = slots + 3
    own_g, other_g, own_u, other_u, own_d, other_d = (
        refs[base + number * count : base + (number + 1) * count] for number in range(6)
    )
    (
        out_ref,
        send_ref,
        grad_ref,
        low_ref,
        gain_ref,
        gu_send,
        gu_keep,
        d_send,
        d_keep,
        wgu,
        wd,
        og,
        normed_t,
        acc,
        back,
        sems,
    ) = refs[base + 6 * count :]
    step = pl.program_id(0)
    core = place[1]
    depth = og.shape[1]
    wide = depth // 2
    strip = 128
    half_width = blocks * strip
    mine = pl.ds(pl.multiple_of(core * wide, wide), wide)
    others = pl.ds(pl.multiple_of((1 - core) * wide, wide), wide)

    def loads():
        copies = []
        for number in range(count):
            at = pl.ds(pl.multiple_of(place[2 + number] * rows, rows), rows)
            for which, (gate, up) in enumerate(((own_g, own_u), (other_g, other_u))):
                copies.append((gate[number], wgu.at[which, at, pl.ds(0, half_width)]))
                copies.append((up[number], wgu.at[which, at, pl.ds(half_width, half_width)]))
        for number in range(count):
            at = pl.ds(pl.multiple_of(place[2 + number] * down_rows, down_rows), down_rows)
            copies.append((own_d[number], wd.at[at, mine]))
            copies.append((other_d[number], wd.at[at, others]))
        return [
            pltpu.make_async_copy(source, target, sems.at[number])
            for number, (source, target) in enumerate(copies)
        ]

    @pl.when(step == 0)
    def _():
        copies = loads()
        for copy in copies:
            copy.start()
        for slot in range(slots):
            og[slot * tok : (slot + 1) * tok, :] = grads[slot][...].reshape(tok, depth)
        normed_t[...] = normed_ref[...].T
        acc[...] = jnp.zeros_like(acc)
        back[...] = jnp.zeros_like(back)
        for copy in copies:
            copy.wait()

    at = pl.ds(pl.multiple_of(step * strip, strip), strip)
    up_at = pl.ds(pl.multiple_of(half_width + step * strip, strip), strip)
    gate_w = jnp.concatenate([wgu[0, :, at], wgu[1, :, at]], axis=1)
    up_w = jnp.concatenate([wgu[0, :, up_at], wgu[1, :, up_at]], axis=1)
    own_rows = pl.ds(pl.multiple_of(core * half_width + step * strip, strip), strip)
    other_rows = pl.ds(pl.multiple_of((1 - core) * half_width + step * strip, strip), strip)
    down_w = jnp.concatenate([wd[own_rows, :], wd[other_rows, :]], axis=0)
    normed = normed_ref[...]
    gate = dot(normed, gate_w)
    up = dot(normed, up_w)
    grad_active = nt(og[...], down_w)
    sigma = jax.nn.sigmoid(gate)
    silu = gate * sigma
    active = (silu * up).astype(BF16)
    grad_up = (grad_active * silu).astype(BF16)
    grad_gate = (grad_active * up * sigma * (1.0 + gate * (1.0 - sigma))).astype(BF16)
    acc[...] += dot(active, down_w)
    back[...] += nt(grad_gate, gate_w) + nt(grad_up, up_w)
    grad_gate_w = dot(normed_t[...], grad_gate).astype(BF16)
    gu_keep[0] = grad_gate_w[:, :strip]
    gu_send[0] = grad_gate_w[:, strip:]
    grad_up_w = dot(normed_t[...], grad_up).astype(BF16)
    gu_keep[1] = grad_up_w[:, :strip]
    gu_send[1] = grad_up_w[:, strip:]
    active_t = active.T
    kept = dot(active_t, og[:, mine]).astype(BF16)
    sent = dot(active_t, og[:, others]).astype(BF16)
    d_keep[core] = kept[:strip]
    d_keep[1 - core] = kept[strip:]
    d_send[core] = sent[:strip]
    d_send[1 - core] = sent[strip:]

    @pl.when(step == blocks - 1)
    def _():
        gain = gains_ref[1:2, :]
        chunk = min(128, tok)
        gain_ref[...] = jnp.zeros_like(gain_ref)
        for slot in range(slots):

            def finish(number, _, slot=slot):
                local = pl.ds(pl.multiple_of(number * chunk, chunk), chunk)
                some = pl.ds(pl.multiple_of(slot * tok + number * chunk, chunk), chunk)
                middle = middle_ref[some, :]
                scale = lax.rsqrt(jnp.mean(middle * middle, axis=1, keepdims=True) + epsilon)
                result = middle + acc[some, :]
                if slot == 0:
                    out_ref[0, local, :] = result
                else:
                    send_ref[pl.ds(pl.multiple_of((slot - 1) * tok + number * chunk, chunk), chunk), :] = (
                        result.astype(BF16)
                    )
                grad = back[some, :]
                gain_ref[0:1, :] += jnp.sum(grad * middle * scale, axis=0, keepdims=True)
                weighted = grad * gain
                inner = jnp.mean(weighted * middle, axis=1, keepdims=True)
                grad_middle = (
                    scale * weighted
                    - middle * (scale * scale * scale) * inner
                    + og[some, :].astype(F32)
                )
                grad_ref[some, :] = grad_middle
                low_ref[some, :] = grad_middle.astype(BF16)
                return 0

            lax.fori_loop(0, tok // chunk, finish, 0)


def mlp(grads, grads_received, middle, normed, gains, gate, up, down, place):
    slots, tok, depth = grads.shape
    own_d, other_d = down
    count, rows = len(own_d), gate[0][0].shape[0]
    down_rows = own_d[0].shape[0]
    half_width = gate[0][0].shape[1]
    wide = depth // 2
    span = slots * tok
    blocks = half_width // 128
    once = pl.Buffered(1)
    g_specs = [pl.BlockSpec((1, tok, depth), lambda s, p: (p[0], 0, 0), pipeline_mode=once)]
    g_specs += [pl.BlockSpec((tok, depth), lambda s, p: (0, 0), pipeline_mode=once)] * (slots - 1)
    gu_spec = pl.BlockSpec((2, depth, 128), lambda s, p: (0, 0, s))
    d_spec = pl.BlockSpec((2, 128, wide), lambda s, p: (0, s, 0))
    grid_spec = pltpu.PrefetchScalarGridSpec(
        num_scalar_prefetch=1,
        grid=(blocks,),
        in_specs=g_specs
        + [
            pl.BlockSpec((span, depth), lambda s, p: (0, 0), pipeline_mode=once),
            pl.BlockSpec((span, depth), lambda s, p: (0, 0), pipeline_mode=once),
            whole_block((8, depth)),
        ]
        + [pl.BlockSpec(memory_space=pl.ANY)] * (6 * count),
        out_specs=[
            pl.BlockSpec((1, tok, depth), lambda s, p: (p[0], 0, 0), pipeline_mode=once),
            pl.BlockSpec(((slots - 1) * tok, depth), lambda s, p: (0, 0), pipeline_mode=once),
            pl.BlockSpec((span, depth), lambda s, p: (0, 0), pipeline_mode=once),
            pl.BlockSpec((span, depth), lambda s, p: (0, 0), pipeline_mode=once),
            whole_block((8, depth)),
            gu_spec,
            gu_spec,
            d_spec,
            d_spec,
        ],
        scratch_shapes=[
            pltpu.VMEM((2, depth, 2 * half_width), BF16),
            pltpu.VMEM((2 * half_width, depth), BF16),
            pltpu.VMEM((span, depth), BF16),
            pltpu.VMEM((depth, span), BF16),
            pltpu.VMEM((span, depth), F32),
            pltpu.VMEM((span, depth), F32),
            pltpu.SemaphoreType.DMA((6 * count,)),
        ],
    )
    return pl.pallas_call(
        functools.partial(mlp_kernel, slots, tok, count, rows, down_rows, blocks),
        out_shape=[
            jax.ShapeDtypeStruct((slots, tok, depth), F32),
            jax.ShapeDtypeStruct(((slots - 1) * tok, depth), BF16),
            jax.ShapeDtypeStruct((span, depth), F32),
            jax.ShapeDtypeStruct((span, depth), BF16),
            jax.ShapeDtypeStruct((8, depth), F32),
            jax.ShapeDtypeStruct((2, depth, half_width), BF16),
            jax.ShapeDtypeStruct((2, depth, half_width), BF16),
            jax.ShapeDtypeStruct((2, half_width, wide), BF16),
            jax.ShapeDtypeStruct((2, half_width, wide), BF16),
        ],
        grid_spec=grid_spec,
        compiler_params=parameters(63),
        cost_estimate=pl.CostEstimate(
            flops=16 * span * depth * 2 * half_width,
            bytes_accessed=24 * depth * half_width + 20 * span * depth,
            transcendentals=2 * span * half_width,
        ),
        name="mlp",
    )(
        place,
        grads,
        *grads_received,
        middle,
        normed,
        gains,
        *gate[0],
        *gate[1],
        *up[0],
        *up[1],
        *own_d,
        *other_d,
    )


def grad_attended_kernel(place, low_ref, full_ref, att_other, att_own, ga_other, ga_own, sent, kept):
    step = pl.program_id(0)
    core = place[1]
    wide = att_own.shape[0]
    mine = pl.ds(pl.multiple_of(core * wide, wide), wide)
    others = pl.ds(pl.multiple_of((1 - core) * wide, wide), wide)
    for number, (att, result) in enumerate(((att_other, ga_other), (att_own, ga_own))):

        @pl.when(step == number)
        def _(att=att, result=result):
            result[...] = nt(full_ref[...], low_ref[...]).astype(BF16)
            kept[...] = dot(att[...], low_ref[:, mine]).astype(BF16)
            sent[...] = dot(att[...], low_ref[:, others]).astype(BF16)


def grad_attended(low, full, att_other, att_own, place):
    span, depth = low.shape
    wide = depth // 2

    def half(s, p):
        return jnp.where(s == 0, 1 - p[1], p[1])

    row_spec = pl.BlockSpec((wide, wide), lambda s, p: (half(s, p), 0))
    grid_spec = pltpu.PrefetchScalarGridSpec(
        num_scalar_prefetch=1,
        grid=(2,),
        in_specs=[
            whole_block((span, depth)),
            pl.BlockSpec((wide, depth), lambda s, p: (half(s, p), 0)),
            whole_block((wide, span)),
            whole_block((wide, span)),
        ],
        out_specs=[whole_block((wide, span)), whole_block((wide, span)), row_spec, row_spec],
    )
    return pl.pallas_call(
        grad_attended_kernel,
        out_shape=[
            jax.ShapeDtypeStruct((wide, span), BF16),
            jax.ShapeDtypeStruct((wide, span), BF16),
            jax.ShapeDtypeStruct((depth, wide), BF16),
            jax.ShapeDtypeStruct((depth, wide), BF16),
        ],
        grid_spec=grid_spec,
        compiler_params=parameters(48),
        cost_estimate=pl.CostEstimate(
            flops=4 * span * depth * depth,
            bytes_accessed=6 * span * depth + 4 * depth * depth,
            transcendentals=0,
        ),
        name="grad_attended",
    )(place, low, full, att_other, att_own)


def tail_kernel(slots, tok, place, *refs):
    xs = refs[:slots]
    (
        back_other,
        back_own,
        full_ref,
        normed_ref,
        grad_ref,
        gains_ref,
        mlp_gain_ref,
        out_ref,
        send_ref,
        first_ref,
        first_send,
        gain_ref,
        sent,
        kept,
        normed_t,
        acc,
    ) = refs[slots:]
    step = pl.program_id(0)
    target, kind = step // 3, step % 3
    depth = acc.shape[1]

    @pl.when(step == 0)
    def _():
        normed_t[...] = normed_ref[...].T
        acc[...] = jnp.zeros_like(acc)

    def part(back, result):
        grad = back[0]

        @pl.when(kind == 2)
        def _():
            rows = 0.5 * grad.astype(F32).T
            first_ref[0] = rows[:tok]
            first_send[...] = rows[tok:].astype(BF16)

        grad = grad * jnp.where(kind == 2, 0.5, 1.0).astype(BF16)
        acc[...] += nt(grad.T, full_ref[0, 0])
        result[0] = nt(normed_t[...], grad).astype(BF16)

    @pl.when(target == 0)
    def _():
        part(back_other, sent)

    @pl.when(target == 1)
    def _():
        part(back_own, kept)

    @pl.when(step == 5)
    def _():
        gain = gains_ref[0:1, :]
        chunk = min(128, tok)
        gain_ref[...] = jnp.zeros_like(gain_ref)
        gain_ref[1:2, :] = mlp_gain_ref[0:1, :]
        for slot in range(slots):

            def finish(number, _, slot=slot):
                local = pl.ds(pl.multiple_of(number * chunk, chunk), chunk)
                some = pl.ds(pl.multiple_of(slot * tok + number * chunk, chunk), chunk)
                if slot == 0:
                    values = xs[slot][0, local, :].astype(F32)
                else:
                    values = xs[slot][local, :].astype(F32)
                scale = lax.rsqrt(jnp.mean(values * values, axis=1, keepdims=True) + epsilon)
                grad = acc[some, :]
                gain_ref[0:1, :] += jnp.sum(grad * values * scale, axis=0, keepdims=True)
                weighted = grad * gain
                inner = jnp.mean(weighted * values, axis=1, keepdims=True)
                result = (
                    scale * weighted
                    - values * (scale * scale * scale) * inner
                    + grad_ref[some, :]
                )
                if slot == 0:
                    out_ref[0, local, :] = result
                else:
                    send_ref[pl.ds(pl.multiple_of((slot - 1) * tok + number * chunk, chunk), chunk), :] = (
                        result.astype(BF16)
                    )
                return 0

            lax.fori_loop(0, tok // chunk, finish, 0)


def tail(inputs, received, back_other, back_own, full, normed, grad_middle, gains, mlp_gain, place):
    slots, tok, depth = inputs.shape
    wide = depth // 2
    span = slots * tok
    rest = (slots - 1) * tok
    once = pl.Buffered(1)

    def half(s, p):
        return jnp.where(s < 3, 1 - p[1], p[1])

    x_specs = [pl.BlockSpec((1, tok, depth), lambda s, p: (p[0], 0, 0))]
    x_specs += [whole_block((tok, depth))] * (slots - 1)
    grid_spec = pltpu.PrefetchScalarGridSpec(
        num_scalar_prefetch=1,
        grid=(6,),
        in_specs=x_specs
        + [
            pl.BlockSpec((1, wide, span), lambda s, p: (jnp.minimum(s, 2), 0, 0)),
            pl.BlockSpec((1, wide, span), lambda s, p: (jnp.maximum(s - 3, 0), 0, 0)),
            pl.BlockSpec((1, 1, depth, wide), lambda s, p: (half(s, p), s % 3, 0, 0)),
            whole_block((span, depth)),
            pl.BlockSpec((span, depth), lambda s, p: (0, 0), pipeline_mode=once),
            whole_block((8, depth)),
            whole_block((8, depth)),
        ],
        out_specs=[
            pl.BlockSpec((1, tok, depth), lambda s, p: (p[0], 0, 0)),
            whole_block((rest, depth)),
            pl.BlockSpec((1, tok, wide), lambda s, p: (p[0], 0, half(s, p))),
            pl.BlockSpec((rest, wide), lambda s, p: (0, half(s, p))),
            whole_block((8, depth)),
            pl.BlockSpec((1, depth, wide), lambda s, p: (jnp.minimum(s, 2), 0, 0)),
            pl.BlockSpec((1, depth, wide), lambda s, p: (jnp.maximum(s - 3, 0), 0, 0)),
        ],
        scratch_shapes=[pltpu.VMEM((depth, span), BF16), pltpu.VMEM((span, depth), F32)],
    )
    return pl.pallas_call(
        functools.partial(tail_kernel, slots, tok),
        out_shape=[
            jax.ShapeDtypeStruct((slots, tok, depth), F32),
            jax.ShapeDtypeStruct((rest, depth), BF16),
            jax.ShapeDtypeStruct((slots, tok, depth), F32),
            jax.ShapeDtypeStruct((rest, depth), BF16),
            jax.ShapeDtypeStruct((8, depth), F32),
            jax.ShapeDtypeStruct((3, depth, wide), BF16),
            jax.ShapeDtypeStruct((3, depth, wide), BF16),
        ],
        grid_spec=grid_spec,
        compiler_params=parameters(60),
        cost_estimate=pl.CostEstimate(
            flops=12 * span * depth * depth,
            bytes_accessed=24 * span * depth + 12 * depth * depth,
            transcendentals=0,
        ),
        name="tail",
    )(
        place, inputs, *received, back_other, back_own, full, normed, grad_middle, gains, mlp_gain
    )


def land_kernel(place, whole_ref, part_ref, out_ref):
    out_ref[0] = part_ref[...].astype(F32)


def land(whole, part, slot):
    _, tok, depth = whole.shape
    tile = min(256, tok)
    grid_spec = pltpu.PrefetchScalarGridSpec(
        num_scalar_prefetch=1,
        grid=(tok // tile,),
        in_specs=[
            pl.BlockSpec(memory_space=pl.ANY),
            pl.BlockSpec((tile, depth), lambda s, p: (s, 0)),
        ],
        out_specs=pl.BlockSpec((1, tile, depth), lambda s, p: (p[0], s, 0)),
    )
    return pl.pallas_call(
        land_kernel,
        out_shape=jax.ShapeDtypeStruct(whole.shape, F32),
        grid_spec=grid_spec,
        input_output_aliases={1: 0},
        compiler_params=parameters(16),
        cost_estimate=pl.CostEstimate(
            flops=tok * depth, bytes_accessed=6 * tok * depth, transcendentals=0
        ),
        name="land",
    )(slot, whole, part)


MESH = pl.DeviceIdType.MESH


def seats():
    shard = lax.axis_index("fsdp")
    seat = lax.axis_index("seq")
    return (shard // 2, shard % 2, seat // 2, seat % 2)


def meet(line, keys):
    shard = lax.axis_index("fsdp")
    seat = lax.axis_index("seq")
    partners = []
    if "z" in keys:
        partners += [{"fsdp": lax.rem(shard + 2 * jump, 2 * line)} for jump in range(1, line)]
    if "y" in keys:
        partners.append({"fsdp": shard + 1 - 2 * (shard % 2)})
    if "x" in keys:
        partners.append({"seq": lax.rem(seat + 2, 4)})
    if "core" in keys:
        partners.append({"seq": seat + 1 - 2 * (seat % 2)})
    barrier = pltpu.get_barrier_semaphore()
    for partner in partners:
        pl.semaphore_signal(barrier, inc=1, device_id=partner, device_id_type=MESH)
    pl.semaphore_wait(barrier, len(partners))


def send(source, target, sems, number, partner):
    return pltpu.make_async_remote_copy(
        src_ref=source,
        dst_ref=target,
        send_sem=sems.at[0, number],
        recv_sem=sems.at[1, number],
        device_id=partner,
        device_id_type=MESH,
    )


def to_core_partner():
    seat = lax.axis_index("seq")
    return {"seq": seat + 1 - 2 * (seat % 2)}


def to_x_partner():
    return {"seq": lax.rem(lax.axis_index("seq") + 2, 4)}


def to_y_partner():
    shard = lax.axis_index("fsdp")
    return {"fsdp": shard + 1 - 2 * (shard % 2)}


def to_z_partner(line, jump):
    return {"fsdp": lax.rem(lax.axis_index("fsdp") + 2 * jump, 2 * line)}


class Gather:
    def __init__(self, line, shard, own, other, sems, share=0, columns=None):
        self.line, self.shard, self.own, self.other = line, shard, own, other
        self.sems = sems
        z, y, x, core = seats()
        self.z, self.y, self.share = z, y, share
        rows, width = own.shape[2:]
        first, size = columns or (0, width)
        self.columns = pl.ds(first, size)
        if shard.shape[1] == width:
            self.source = self.columns
        else:
            self.source = pl.ds(pl.multiple_of(core * width + first, 128), size)
        if share:
            step = math.gcd(share, rows)
            self.rows = pl.ds(pl.multiple_of(x * share, step), rows - share)
            self.given = pl.ds(pl.multiple_of(x * (rows - share), step), share)
            self.taken = pl.ds(pl.multiple_of((1 - x) * (rows - share), step), share)
        else:
            self.rows = slice(None)

    def here(self):
        return pltpu.make_async_copy(
            self.shard.at[self.rows, self.source],
            self.own.at[self.z, self.y, self.rows, self.columns],
            self.sems.at[0, self.line + 3],
        )

    def along_z(self):
        return [
            send(
                self.shard.at[self.rows, self.source],
                self.own.at[self.z, self.y, self.rows, self.columns],
                self.sems,
                jump - 1,
                to_z_partner(self.line, jump),
            )
            for jump in range(1, self.line)
        ]

    def along_y(self):
        part = self.own.at[:, self.y, self.rows, self.columns]
        return send(part, part, self.sems, self.line - 1, to_y_partner())

    def along_x(self):
        part = self.own.at[:, :, self.given, self.columns]
        return send(part, part, self.sems, self.line, to_x_partner())

    def to_core(self, late):
        if self.share:
            at = (slice(None), slice(None), self.taken if late else self.rows, self.columns)
        else:
            at = (slice(None), 1 - self.y if late else self.y, slice(None), self.columns)
        return send(
            self.own.at[at],
            self.other.at[at],
            self.sems,
            self.line + 1 + late,
            to_core_partner(),
        )

    def start_z(self):
        self.here().start()
        for copy in self.along_z():
            copy.start()

    def wait_z(self):
        self.here().wait()
        for copy in self.along_z():
            copy.wait()

    def wait_core(self):
        self.to_core(0).wait()
        self.to_core(1).wait()


def gather_sems(line):
    return pltpu.SemaphoreType.DMA((2, line + 4))


def front_kernel(line, tok, *refs):
    (
        inputs,
        firsts,
        grads,
        q_shard,
        k_shard,
        v_shard,
        o_shard,
        d_shard,
        gains_shard,
        cos_ref,
        sin_ref,
        x_received,
        f_received,
        g_received,
        heads_own,
        heads_received,
        normed_ref,
        full_ref,
        gains_ref,
        o_own,
        o_other,
        d_own,
        xs,
        fs,
        q_own,
        q_other,
        k_own,
        k_other,
        v_own,
        v_other,
        outgoing,
        all_gains,
        q_sems,
        k_sems,
        v_sems,
        w_sems,
        o_sems,
        d_sems,
        gain_sems,
        swap_sems,
        head_sems,
        local_sems,
    ) = refs
    step = pl.program_id(0)
    _, _, side, core = seats()
    wide = outgoing.shape[1]
    depth = 2 * wide
    gathers = [
        Gather(line, q_shard, q_own, q_other, q_sems),
        Gather(line, k_shard, k_own, k_other, k_sems),
        Gather(line, v_shard, v_own, v_other, v_sems, columns=(0, wide // 2)),
        Gather(line, v_shard, v_own, v_other, w_sems, columns=(wide // 2, wide // 2)),
    ]
    query, key, value, value_more = gathers
    gains = Gather(line, gains_shard, all_gains, all_gains, gain_sems)
    out = Gather(line, o_shard, o_own, o_other, o_sems)
    down = Gather(line, d_shard, d_own, d_own, d_sems, d_own.shape[2] // 2)
    swap_x = send(inputs.at[1 - side], x_received, swap_sems, 0, to_x_partner())
    swap_f = send(firsts.at[1 - side], f_received, swap_sems, 1, to_x_partner())
    early = pl.ds(0, tok // 2)
    swap_g = send(
        grads.at[1 - side, early], g_received.at[early], swap_sems, 2, to_x_partner()
    )
    load_x = pltpu.make_async_copy(inputs.at[side], xs.at[pl.ds(0, tok), :], local_sems.at[0])
    load_f = pltpu.make_async_copy(firsts.at[side], fs.at[pl.ds(0, tok), :], local_sems.at[1])
    more_x = pltpu.make_async_copy(x_received, xs.at[pl.ds(tok, tok), :], local_sems.at[2])
    more_f = pltpu.make_async_copy(f_received, fs.at[pl.ds(tok, tok), :], local_sems.at[3])

    def weight(halves, columns):
        return halves[:, :, :, columns].reshape(depth, wide)

    def heads(number):
        return send(
            outgoing.at[number], heads_received.at[number], head_sems, number, to_core_partner()
        )

    saves = []
    for number, (mine, others) in enumerate(((q_own, q_other), (k_own, k_other), (v_own, v_other))):
        for which, ref in ((0, mine), (1, others)):
            half = core if which == 0 else 1 - core
            saves.append(
                pltpu.make_async_copy(
                    ref.at[:, :, :, pl.ds(0, wide)],
                    full_ref.at[half, number],
                    local_sems.at[4 + 2 * number + which],
                )
            )

    @pl.when(step == 0)
    def _():
        meet(line, ("z", "y", "x", "core"))
        swap_x.start()
        load_x.start()
        load_f.start()
        gains.start_z()
        query.start_z()
        gains.wait_z()
        gains.along_y().start()
        query.wait_z()
        query.along_y().start()
        query.to_core(0).start()
        key.start_z()
        key.wait_z()
        key.along_y().start()
        key.to_core(0).start()
        value.start_z()
        swap_x.wait()
        more_x.start()
        swap_f.start()
        gains.along_y().wait()
        query.along_y().wait()
        query.to_core(1).start()
        for number in range(2 * line):
            columns = slice(number * 128, (number + 1) * 128)
            gains_ref[:, columns] = all_gains[number // 2, number % 2]
        gain = gains_ref[0:1, :]
        chunk = min(256, 2 * tok)
        load_x.wait()
        more_x.wait()

        def norm(number, _):
            at = pl.ds(pl.multiple_of(number * chunk, chunk), chunk)
            values = xs[at, :].astype(F32)
            scale = lax.rsqrt(jnp.mean(values * values, axis=1, keepdims=True) + epsilon)
            normed_ref[at, :] = (values * scale * gain).astype(BF16)
            return 0

        lax.fori_loop(0, 2 * tok // chunk, norm, 0)
        value.wait_z()
        value.along_y().start()
        value.to_core(0).start()
        value_more.start_z()

    @pl.when(step == 1)
    def _():
        key.along_y().wait()
        key.to_core(1).start()
        value_more.wait_z()
        value_more.along_y().start()
        value_more.to_core(0).start()
        out.start_z()

    @pl.when(step == 2)
    def _():
        swap_f.wait()
        more_f.start()
        swap_g.start()
        value.along_y().wait()
        value.to_core(1).start()
        value_more.along_y().wait()
        value_more.to_core(1).start()
        out.wait_z()
        out.along_y().start()
        out.to_core(0).start()
        down.start_z()
        load_f.wait()
        more_f.wait()

    @pl.when(step == 3)
    def _():
        query.wait_core()
        key.wait_core()
        for save in saves[:4]:
            save.start()

    @pl.when(step == 5)
    def _():
        value.wait_core()
        value_more.wait_core()
        for save in saves[4:]:
            save.start()
        out.along_y().wait()
        out.to_core(1).start()

    def project_one(halves, kind, mine):
        raw = nt(weight(halves, slice(0, wide)).T, normed_ref[...])
        if kind < 2:
            parts = raw.reshape(wide // HEAD_DIM, 2, HALF, raw.shape[1])
            first, second = parts[:, 0], parts[:, 1]
            cosine, sine = (
                jnp.concatenate([ref[:, block_of(1, slot, tok)] for slot in range(2)], axis=1)[None]
                for ref in (cos_ref, sin_ref)
            )
            turned = jnp.stack(
                [first * cosine - second * sine, first * sine + second * cosine], axis=1
            )
            result = turned.reshape(raw.shape).astype(BF16)
        else:
            half = core if mine else 1 - core
            first = fs[:, pl.ds(pl.multiple_of(half * wide, wide), wide)]
            result = (0.5 * raw + 0.5 * first.astype(F32).T).astype(BF16)
        if mine:
            heads_own[0] = result
        else:
            outgoing[kind] = result
            heads(kind).start()

    for number, (halves, kind, mine) in enumerate(
        (
            (q_own, 0, True),
            (k_own, 1, True),
            (v_own, 2, True),
            (q_other, 0, False),
            (k_other, 1, False),
            (v_other, 2, False),
        )
    ):

        @pl.when(step == number)
        def _(halves=halves, kind=kind, mine=mine):
            project_one(halves, kind, mine)

    @pl.when(step == 5)
    def _():
        for number in range(3):
            heads(number).wait()
        for save in saves:
            save.wait()
        out.wait_core()
        down.wait_z()
        swap_g.wait()


def front(inputs, firsts, grads, q, k, v, o, d, gains, cosine, sine, line):
    slots, tok, depth = inputs.shape
    span = slots * tok
    wide = depth // 2
    rows, down_rows = q.shape[0], d.shape[0]
    anywhere = pl.BlockSpec(memory_space=pl.ANY)
    weights = lambda columns: pltpu.VMEM((line, 2, rows, columns), BF16)
    return pl.pallas_call(
        functools.partial(front_kernel, line, tok),
        grid=(6,),
        in_specs=[anywhere] * 9 + [whole_block(cosine.shape)] * 2,
        out_specs=[
            anywhere,
            anywhere,
            anywhere,
            pl.BlockSpec((1, wide, span), lambda s: (jnp.minimum(s, 2), 0, 0)),
            anywhere,
            whole_block((span, depth)),
            anywhere,
            whole_block((8, depth)),
            anywhere,
            anywhere,
            anywhere,
        ],
        out_shape=[
            jax.ShapeDtypeStruct((tok, depth), BF16),
            jax.ShapeDtypeStruct((tok, depth), BF16),
            jax.ShapeDtypeStruct((tok, depth), BF16),
            jax.ShapeDtypeStruct((3, wide, span), BF16),
            jax.ShapeDtypeStruct((3, wide, span), BF16),
            jax.ShapeDtypeStruct((span, depth), BF16),
            jax.ShapeDtypeStruct((2, 3, line, 2, rows, wide), BF16),
            jax.ShapeDtypeStruct((8, depth), F32),
            jax.ShapeDtypeStruct((line, 2, rows, wide), BF16),
            jax.ShapeDtypeStruct((line, 2, rows, wide), BF16),
            jax.ShapeDtypeStruct((line, 2, down_rows, wide), BF16),
        ],
        scratch_shapes=[
            pltpu.VMEM((span, depth), BF16),
            pltpu.VMEM((span, depth), BF16),
            weights(wide),
            weights(wide),
            weights(wide),
            weights(wide),
            weights(wide),
            weights(wide),
            pltpu.VMEM((3, wide, span), BF16),
            pltpu.VMEM((line, 2, 8, 128), F32),
        ]
        + [gather_sems(line)] * 7
        + [
            pltpu.SemaphoreType.DMA((2, 3)),
            pltpu.SemaphoreType.DMA((2, 3)),
            pltpu.SemaphoreType.DMA((10,)),
        ],
        compiler_params=pltpu.CompilerParams(
            dimension_semantics=("arbitrary",),
            vmem_limit_bytes=63 * MIB,
            collective_id=1,
            has_side_effects=True,
        ),
        cost_estimate=pl.CostEstimate(
            flops=6 * span * depth * depth,
            bytes_accessed=2 * (8 * span * depth + 6 * depth * depth),
            transcendentals=0,
        ),
        name="front",
    )(inputs, firsts, grads, q, k, v, o, d, gains, cosine, sine)


def block_of(source, slot, tok):
    _, _, side, core = seats()
    rank = 1 - core if source == 0 else core
    group = lax.rem(side + slot, 2)
    return pl.ds(pl.multiple_of((group * 2 + rank) * tok, tok), tok)


def attend_carry_kernel(line, tok, tile_k, *refs):
    (
        received,
        own,
        inputs,
        x_received,
        gains_ref,
        o_own,
        o_other,
        grad_in,
        _,
        d_in,
        g_shard,
        u_shard,
        mix_received,
        mix_own,
        lse_ref,
        middle_ref,
        normed_ref,
        full_ref,
        att_other,
        grad_received,
        d_own,
        d_other,
        g_own,
        g_other,
        u_own,
        u_other,
        qz,
        kn,
        vt,
        ot,
        outgoing,
        att_mine,
        att_theirs,
        xs,
        d_sems,
        g_sems,
        u_sems,
        v_sems,
        swap_sems,
        att_sems,
        local_sems,
    ) = refs
    step = pl.program_id(0)
    pairs = pl.num_programs(0)
    _, _, side, core = seats()
    rows, columns = g_own.shape[2:]
    first = columns // 256 * 128
    down = Gather(line, d_in, d_own, d_other, d_sems, d_own.shape[2] // 2)
    gate = Gather(line, g_shard, g_own, g_other, g_sems, rows * 3 // 8)
    up = Gather(line, u_shard, u_own, u_other, u_sems, columns=(0, first))
    up_more = Gather(line, u_shard, u_own, u_other, v_sems, columns=(first, columns - first))
    late = pl.ds(tok // 2, tok - tok // 2)
    swap = send(grad_in.at[1 - side, late], grad_received.at[late], swap_sems, 0, to_x_partner())
    depth = xs.shape[1]
    wide = depth // 2
    mine = pl.ds(pl.multiple_of(core * wide, wide), wide)
    others = pl.ds(pl.multiple_of((1 - core) * wide, wide), wide)
    loads = [
        pltpu.make_async_copy(source, place, local_sems.at[number])
        for number, (source, place) in enumerate(
            (
                (inputs.at[side], xs.at[pl.ds(0, tok), :]),
                (x_received, xs.at[pl.ds(tok, tok), :]),
                (o_own, full_ref.at[:, mine]),
                (o_other, full_ref.at[:, others]),
            )
        )
    ]
    save_att = pltpu.make_async_copy(att_theirs, att_other, local_sems.at[4])
    pieces = (received, own)

    def hand_over(number):
        rows = pl.ds(number * PAIR, PAIR)
        return send(
            outgoing.at[rows, :], att_theirs.at[rows, :], att_sems, number, to_core_partner()
        )

    @pl.when(step == 0)
    def _():
        meet(line, ("z", "y", "x", "core"))
        down.along_y().start()
        gate.start_z()
        swap.start()

    @pl.when(step == 2)
    def _():
        down.along_y().wait()
        down.along_x().start()
        down.to_core(0).start()
        gate.wait_z()
        gate.along_y().start()
        up.start_z()
        for load in loads:
            load.start()

    for source in range(2):
        for slot in range(2):
            cols = block_of(source, slot, tok)
            take = slice(slot * tok, (slot + 1) * tok)
            query = pieces[source][0, :, take] * jnp.asarray(HEAD_DIM**-0.5, BF16)
            for head in range(2):
                qz[head, :, cols] = head_rows(query, head)
            kn[cols, :] = pieces[source][1, :, take].T
            vt[:, cols] = pieces[source][2, :, take]
    attend_body(4 * tok, tile_k, qz, kn, vt, ot, lse_ref)
    for slot in range(2):
        take = slice(slot * tok, (slot + 1) * tok)
        theirs = ot[:, block_of(0, slot, tok)]
        mix_received[:, take] = theirs
        for number in range(4):

            @pl.when(step == number)
            def _(number=number, theirs=theirs, take=take):
                outgoing[number * PAIR : (number + 1) * PAIR, take] = theirs

        ours = ot[:, block_of(1, slot, tok)]
        mix_own[:, take] = ours
        for number in range(4):

            @pl.when(step == number)
            def _(number=number, ours=ours, take=take):
                att_mine[number * PAIR : (number + 1) * PAIR, take] = ours

    for number in range(4):

        @pl.when(step == number)
        def _(number=number):
            hand_over(number).start()

    @pl.when(step == pairs - 1)
    def _():
        up.wait_z()
        up.along_y().start()
        up.to_core(0).start()
        up_more.start_z()
        gate.along_y().wait()
        gate.to_core(0).start()
        down.along_x().wait()
        gate.along_x().start()
        down.to_core(1).start()
        up_more.wait_z()
        up_more.along_y().start()
        up_more.to_core(0).start()
        for number in range(4):
            hand_over(number).wait()
        save_att.start()
        for load in loads:
            load.wait()
        for slot in range(2):
            take = slice(slot * tok, (slot + 1) * tok)
            total = dot(att_mine[:, take].T, full_ref[mine, :])
            total = total + dot(att_theirs[:, take].T, full_ref[others, :])
            middle = xs[take, :].astype(F32) + total
            middle_ref[take, :] = middle
            scale = lax.rsqrt(jnp.mean(middle * middle, axis=1, keepdims=True) + epsilon)
            normed_ref[take, :] = (middle * scale * gains_ref[1:2, :]).astype(BF16)
        up.along_y().wait()
        up.to_core(1).start()
        up_more.along_y().wait()
        up_more.to_core(1).start()
        gate.along_x().wait()
        gate.to_core(1).start()
        swap.wait()
        for gather in (down, up, up_more, gate):
            gather.wait_core()
        save_att.wait()


def attend_carry(
    received, own, inputs, x_received, gains, o_own, o_other, grads, g_received, d_own, gate, up, line
):
    _, width, span = own.shape
    tok = span // 2
    length = 2 * span
    pairs = width // PAIR
    rows, down_rows = gate.shape[0], d_own.shape[2]
    depth = grads.shape[2]
    anywhere = pl.BlockSpec(memory_space=pl.ANY)
    triple = pl.BlockSpec((3, PAIR, span), lambda p: (0, p, 0))
    single = pl.BlockSpec((PAIR, span), lambda p: (p, 0))
    whole_gate = jax.ShapeDtypeStruct((line, 2, rows, gate.shape[1] // 2), BF16)
    whole_down = jax.ShapeDtypeStruct((line, 2, down_rows, d_own.shape[3]), BF16)
    area = pairs * 2 * length * length // 2
    return pl.pallas_call(
        functools.partial(attend_carry_kernel, line, tok, min(256, length)),
        grid=(pairs,),
        in_specs=[triple, triple]
        + [anywhere] * 2
        + [whole_block((8, depth))]
        + [anywhere] * 7,
        out_specs=[single, single, pl.BlockSpec((1, 8, length), lambda p: (p, 0, 0))]
        + [
            pl.BlockSpec(shape, lambda p: (0, 0), pipeline_mode=pl.Buffered(1))
            for shape in ((span, depth), (span, depth), (depth, depth))
        ]
        + [anywhere] * 8,
        out_shape=[
            jax.ShapeDtypeStruct((width, span), BF16),
            jax.ShapeDtypeStruct((width, span), BF16),
            jax.ShapeDtypeStruct((pairs, 8, length), F32),
            jax.ShapeDtypeStruct((span, depth), F32),
            jax.ShapeDtypeStruct((span, depth), BF16),
            jax.ShapeDtypeStruct((depth, depth), BF16),
            jax.ShapeDtypeStruct((width, span), BF16),
            jax.ShapeDtypeStruct((tok, depth), BF16),
            whole_down,
            whole_down,
            whole_gate,
            whole_gate,
            whole_gate,
            whole_gate,
        ],
        scratch_shapes=[
            pltpu.VMEM((2, PAIR, length), BF16),
            pltpu.VMEM((length, PAIR), BF16),
            pltpu.VMEM((PAIR, length), BF16),
            pltpu.VMEM((PAIR, length), BF16),
            pltpu.VMEM((width, span), BF16),
            pltpu.VMEM((width, span), BF16),
            pltpu.VMEM((width, span), BF16),
            pltpu.VMEM((span, depth), BF16),
        ]
        + [gather_sems(line)] * 4
        + [
            pltpu.SemaphoreType.DMA((2, 1)),
            pltpu.SemaphoreType.DMA((2, 4)),
            pltpu.SemaphoreType.DMA((5,)),
        ],
        input_output_aliases={8: 7, 9: 8},
        compiler_params=pltpu.CompilerParams(
            dimension_semantics=("arbitrary",),
            vmem_limit_bytes=63 * MIB,
            collective_id=2,
            has_side_effects=True,
        ),
        cost_estimate=pl.CostEstimate(
            flops=area * 1024, bytes_accessed=8 * width * length, transcendentals=area
        ),
        name="attend_carry",
    )(
        received,
        own,
        inputs,
        x_received,
        gains,
        o_own,
        o_other,
        grads,
        g_received,
        d_own,
        gate,
        up,
    )


LATE = 2


def mlp_carry_kernel(line, tok, blocks, *refs):
    (
        grads,
        grads_received,
        middle_ref,
        normed_ref,
        gains_ref,
        g_own,
        g_other,
        u_own,
        u_other,
        d_own_own,
        d_own_other,
        d_other_own,
        d_other_other,
        out_ref,
        send_ref,
        grad_ref,
        low_ref,
        gain_ref,
        gu_ref,
        d_ref,
        gu_y,
        gu_late,
        og,
        normed_t,
        acc,
        back,
        gu_kept,
        d_kept,
        gu_sent,
        d_sent,
        gu_landed,
        d_landed,
        gu_outgoing,
        down_full,
        local_sems,
        gu_sends,
        gu_recvs,
        d_sends,
        d_recvs,
        y_sems,
    ) = refs
    step = pl.program_id(0)
    _, y, side, core = seats()
    depth = og.shape[1]
    wide = depth // 2
    strip = 128
    rows = gu_kept.shape[4]
    mine = pl.ds(pl.multiple_of(core * wide, wide), wide)
    others = pl.ds(pl.multiple_of((1 - core) * wide, wide), wide)

    def core_copies(number):
        slot = lax.rem(number, 2)
        return [
            pltpu.make_async_remote_copy(
                src_ref=source.at[slot],
                dst_ref=target.at[number],
                send_sem=sends.at[slot],
                recv_sem=recvs.at[number],
                device_id=to_core_partner(),
                device_id_type=MESH,
            )
            for source, target, sends, recvs in (
                (gu_sent, gu_landed, gu_sends, gu_recvs),
                (d_sent, d_landed, d_sends, d_recvs),
            )
        ]

    def y_copy(number):
        return send(gu_outgoing.at[number], gu_y.at[number], y_sems, number, to_y_partner())

    def leave(late):
        return pltpu.make_async_copy(
            gu_outgoing.at[blocks - LATE + late], gu_late.at[late], local_sems.at[2 + late]
        )

    @pl.when(step == 0)
    def _():
        meet(line, ("y", "core"))
        loads = [
            pltpu.make_async_copy(grads.at[side], og.at[pl.ds(0, tok), :], local_sems.at[0]),
            pltpu.make_async_copy(grads_received, og.at[pl.ds(tok, tok), :], local_sems.at[1]),
        ]
        for load in loads:
            load.start()
        normed_t[...] = normed_ref[...].T
        acc[...] = jnp.zeros_like(acc)
        back[...] = jnp.zeros_like(back)
        for load in loads:
            load.wait()

    @pl.when(step < blocks)
    def _():
        slot = lax.rem(step, 2)
        gate_w = jnp.concatenate([g_own[...], g_other[...]], axis=1)
        up_w = jnp.concatenate([u_own[...], u_other[...]], axis=1)
        for number, pair in enumerate(
            ((d_own_own, d_own_other), (d_other_own, d_other_other))
        ):
            at = pl.ds(number * strip, strip)
            down_full[at, mine] = pair[0][...]
            down_full[at, others] = pair[1][...]
        down_w = down_full[...]
        both_w = jnp.concatenate([gate_w, up_w], axis=1)
        span = og.shape[0]
        size = span // 2

        def products(at):
            both = dot(normed_ref[at, :], both_w)
            return (both[:, : 2 * strip], both[:, 2 * strip :], nt(og[at, :], down_w))

        def bend(gate, up, grad_active):
            sigma = jax.nn.sigmoid(gate)
            silu = gate * sigma
            turned = grad_active * up * sigma * (1.0 + gate * (1.0 - sigma))
            grad_both = jnp.concatenate([turned.astype(BF16), (grad_active * silu).astype(BF16)], axis=1)
            return ((silu * up).astype(BF16), grad_both)

        def spread(at, active, grad_both):
            acc[at, :] += dot(active, down_w)
            back[at, :] += nt(grad_both, both_w)

        pieces = [slice(n * size, (n + 1) * size) for n in range(2)]
        bent = []
        ahead = products(pieces[0])
        for number, at in enumerate(pieces):
            now = ahead
            if number + 1 < len(pieces):
                ahead = products(pieces[number + 1])
            bent.append(bend(*now))
            if number:
                spread(pieces[number - 1], *bent[number - 1])
        spread(pieces[-1], *bent[-1])
        active = jnp.concatenate([one for one, _ in bent], axis=0)
        grad_both = jnp.concatenate([one for _, one in bent], axis=0)

        @pl.when(step >= 2)
        def _():
            for copy in core_copies(step - 2):
                copy.wait_send()

        shaped = dot(normed_t[...], grad_both).astype(BF16).reshape(line, 2, rows, 4 * strip)
        for number in range(2):
            base = 2 * number * strip
            gu_kept[slot, number] = shaped[..., base : base + strip]
            gu_sent[slot, number] = shaped[..., base + strip : base + 2 * strip]
        active_t = active.T
        kept = dot(active_t, og[:, mine]).astype(BF16)
        d_kept[slot, core] = kept[:strip]
        d_kept[slot, 1 - core] = kept[strip:]
        sent = dot(active_t, og[:, others]).astype(BF16)
        d_sent[slot, core] = sent[:strip]
        d_sent[slot, 1 - core] = sent[strip:]
        for copy in core_copies(step):
            copy.start()

    @pl.when(step > 0)
    def _():
        number = step - 1
        slot = lax.rem(number, 2)
        for copy in core_copies(number):
            copy.wait_recv()
        for which in range(2):
            theirs = gu_kept[slot, which, :, 1 - y].astype(F32)
            theirs = theirs + gu_landed[number, which, :, 1 - y].astype(F32)
            gu_outgoing[number, which] = theirs.astype(BF16)
            ours = gu_kept[slot, which, :, y].astype(F32)
            ours = ours + gu_landed[number, which, :, y].astype(F32)
            gu_ref[0, which] = ours.astype(BF16)
        @pl.when(number < blocks - LATE)
        def _():
            y_copy(number).start()

        for late in range(LATE):

            @pl.when(number == blocks - LATE + late)
            def _(late=late):
                leave(late).start()

        d_ref[...] = (d_kept[slot].astype(F32) + d_landed[number].astype(F32)).astype(BF16)

    @pl.when(step == blocks)
    def _():
        gain = gains_ref[1:2, :]
        chunk = min(128, tok)
        gain_ref[...] = jnp.zeros_like(gain_ref)
        for slot in range(2):

            def finish(number, _, slot=slot):
                local = pl.ds(pl.multiple_of(number * chunk, chunk), chunk)
                some = pl.ds(pl.multiple_of(slot * tok + number * chunk, chunk), chunk)
                middle = middle_ref[some, :]
                scale = lax.rsqrt(jnp.mean(middle * middle, axis=1, keepdims=True) + epsilon)
                result = middle + acc[some, :]
                if slot == 0:
                    out_ref[0, local, :] = result
                else:
                    send_ref[local, :] = result.astype(BF16)
                grad = back[some, :]
                gain_ref[0:1, :] += jnp.sum(grad * middle * scale, axis=0, keepdims=True)
                weighted = grad * gain
                inner = jnp.mean(weighted * middle, axis=1, keepdims=True)
                grad_middle = (
                    scale * weighted
                    - middle * (scale * scale * scale) * inner
                    + og[some, :].astype(F32)
                )
                grad_ref[some, :] = grad_middle
                low_ref[some, :] = grad_middle.astype(BF16)
                return 0

            lax.fori_loop(0, tok // chunk, finish, 0)
        for number in (blocks - 2, blocks - 1):
            for copy in core_copies(number):
                copy.wait_send()
        for late in range(LATE):
            leave(late).wait()
        for number in range(blocks - LATE):
            y_copy(number).wait()


def mlp_carry(grads, grads_received, middle, normed, gains, gate, up, down, line):
    slots, tok, depth = grads.shape
    half_width = gate[0].shape[1]
    wide = depth // 2
    span = slots * tok
    blocks = half_width // 128
    rows = depth // (2 * line)
    once = pl.Buffered(1)
    anywhere = pl.BlockSpec(memory_space=pl.ANY)

    def now(s):
        return jnp.minimum(s, blocks - 1)

    def done(s):
        return jnp.maximum(s - 1, 0)

    def core():
        return lax.axis_index("seq") % 2

    column = pl.BlockSpec((depth, 128), lambda s: (0, now(s)))
    own_rows = pl.BlockSpec((128, wide), lambda s: (core() * blocks + now(s), 0))
    other_rows = pl.BlockSpec((128, wide), lambda s: ((1 - core()) * blocks + now(s), 0))
    full = pl.BlockSpec((span, depth), lambda s: (0, 0), pipeline_mode=once)
    return pl.pallas_call(
        functools.partial(mlp_carry_kernel, line, tok, blocks),
        grid=(blocks + 1,),
        in_specs=[anywhere, anywhere, full, full, whole_block((8, depth))]
        + [column] * 4
        + [own_rows, own_rows, other_rows, other_rows],
        out_specs=[
            pl.BlockSpec(
                (1, tok, depth), lambda s: (lax.axis_index("seq") // 2, 0, 0), pipeline_mode=once
            ),
            pl.BlockSpec((tok, depth), lambda s: (0, 0), pipeline_mode=once),
            full,
            full,
            whole_block((8, depth)),
            pl.BlockSpec((1, 2, line, rows, 128), lambda s: (done(s), 0, 0, 0, 0)),
            pl.BlockSpec((2, 128, wide), lambda s: (0, done(s), 0)),
            anywhere,
            anywhere,
        ],
        out_shape=[
            jax.ShapeDtypeStruct((slots, tok, depth), F32),
            jax.ShapeDtypeStruct((tok, depth), BF16),
            jax.ShapeDtypeStruct((span, depth), F32),
            jax.ShapeDtypeStruct((span, depth), BF16),
            jax.ShapeDtypeStruct((8, depth), F32),
            jax.ShapeDtypeStruct((blocks, 2, line, rows, 128), BF16),
            jax.ShapeDtypeStruct((2, half_width, wide), BF16),
            jax.ShapeDtypeStruct((blocks - LATE, 2, line, rows, 128), BF16),
            jax.ShapeDtypeStruct((LATE, 2, line, rows, 128), BF16),
        ],
        scratch_shapes=[
            pltpu.VMEM((span, depth), BF16),
            pltpu.VMEM((depth, span), BF16),
            pltpu.VMEM((span, depth), F32),
            pltpu.VMEM((span, depth), F32),
            pltpu.VMEM((2, 2, line, 2, rows, 128), BF16),
            pltpu.VMEM((2, 2, 128, wide), BF16),
            pltpu.VMEM((2, 2, line, 2, rows, 128), BF16),
            pltpu.VMEM((2, 2, 128, wide), BF16),
            pltpu.VMEM((blocks, 2, line, 2, rows, 128), BF16),
            pltpu.VMEM((blocks, 2, 128, wide), BF16),
            pltpu.VMEM((blocks, 2, line, rows, 128), BF16),
            pltpu.VMEM((256, depth), BF16),
            pltpu.SemaphoreType.DMA((2 + LATE,)),
            pltpu.SemaphoreType.DMA((2,)),
            pltpu.SemaphoreType.DMA((blocks,)),
            pltpu.SemaphoreType.DMA((2,)),
            pltpu.SemaphoreType.DMA((blocks,)),
            pltpu.SemaphoreType.DMA((2, blocks - LATE)),
        ],
        compiler_params=pltpu.CompilerParams(
            dimension_semantics=("arbitrary",),
            vmem_limit_bytes=63 * MIB,
            collective_id=3,
            has_side_effects=True,
        ),
        cost_estimate=pl.CostEstimate(
            flops=16 * span * depth * 2 * half_width,
            bytes_accessed=24 * depth * half_width + 20 * span * depth,
            transcendentals=2 * span * half_width,
        ),
        name="mlp_carry",
    )(
        grads,
        grads_received,
        middle,
        normed,
        gains,
        *gate,
        *up,
        down[0],
        down[1],
        down[0],
        down[1],
    )


def grad_attended_carry_kernel(
    line,
    low_ref,
    full_ref,
    att_other,
    att_own,
    ga_own,
    ga_received,
    o_ref,
    o_landed,
    outgoing,
    o_sent,
    sems,
):
    step = pl.program_id(0)
    _, _, _, core = seats()
    wide = att_own.shape[0]
    mine = pl.ds(pl.multiple_of(core * wide, wide), wide)
    others = pl.ds(pl.multiple_of((1 - core) * wide, wide), wide)
    heads = send(outgoing, ga_received, sems, 0, to_core_partner())

    def sums(number):
        half = 1 - core if number == 0 else core
        at = pl.ds(pl.multiple_of(half * wide, wide), wide)
        return send(o_sent.at[number], o_landed.at[at, :], sems, 1 + number, to_core_partner())

    @pl.when(step == 0)
    def _():
        meet(line, ("core",))
        outgoing[...] = nt(full_ref[...], low_ref[...]).astype(BF16)
        heads.start()

    @pl.when(step == 1)
    def _():
        ga_own[...] = nt(full_ref[...], low_ref[...]).astype(BF16)

    for number, att in enumerate((att_other, att_own)):

        @pl.when(step == number)
        def _(number=number, att=att):
            o_sent[number] = dot(att[...], low_ref[:, others]).astype(BF16)
            sums(number).start()
            o_ref[...] = dot(att[...], low_ref[:, mine]).astype(BF16)

    @pl.when(step == 1)
    def _():
        heads.wait()
        for number in range(2):
            sums(number).wait()


def grad_attended_carry(low, full, att_other, att_own, line):
    span, depth = low.shape
    wide = depth // 2

    def half(s):
        core = lax.axis_index("seq") % 2
        return jnp.where(s == 0, 1 - core, core)

    anywhere = pl.BlockSpec(memory_space=pl.ANY)
    return pl.pallas_call(
        functools.partial(grad_attended_carry_kernel, line),
        grid=(2,),
        in_specs=[
            whole_block((span, depth)),
            pl.BlockSpec((wide, depth), lambda s: (half(s), 0)),
            whole_block((wide, span)),
            whole_block((wide, span)),
        ],
        out_specs=[
            whole_block((wide, span)),
            anywhere,
            pl.BlockSpec((wide, wide), lambda s: (half(s), 0)),
            anywhere,
        ],
        out_shape=[
            jax.ShapeDtypeStruct((wide, span), BF16),
            jax.ShapeDtypeStruct((wide, span), BF16),
            jax.ShapeDtypeStruct((depth, wide), BF16),
            jax.ShapeDtypeStruct((depth, wide), BF16),
        ],
        scratch_shapes=[
            pltpu.VMEM((wide, span), BF16),
            pltpu.VMEM((2, wide, wide), BF16),
            pltpu.SemaphoreType.DMA((2, 3)),
        ],
        compiler_params=pltpu.CompilerParams(
            dimension_semantics=("arbitrary",),
            vmem_limit_bytes=48 * MIB,
            collective_id=4,
            has_side_effects=True,
        ),
        cost_estimate=pl.CostEstimate(
            flops=4 * span * depth * depth,
            bytes_accessed=6 * span * depth + 4 * depth * depth,
            transcendentals=0,
        ),
        name="grad_attended_carry",
    )(low, full, att_other, att_own)


def attend_back_carry_kernel(line, tok, tile_q, tile_k, *refs):
    (
        received,
        own,
        mix_received,
        mix_own,
        grad_received,
        grad_own,
        lse_ref,
        cos_ref,
        sin_ref,
        outputs_sent,
        gu_in,
        gu_y,
        gu_late,
        d_in,
        o_in,
        o_landed,
        back_own,
        back_other,
        outputs_received,
        gu_mine,
        gu_z,
        d_kept,
        d_y,
        o_kept,
        o_y,
    ) = refs[:25]
    (
        qz,
        gz,
        qn,
        gn,
        kn,
        vn,
        kt,
        inner,
        dq,
        dk,
        dv,
        outgoing,
        gu_a,
        gu_b,
        o_a,
        o_b,
        o_x,
        d_a,
        d_x,
        local_sems,
        back_sems,
        z_sems,
        other_sems,
    ) = refs[25:]
    step = pl.program_id(0)
    pairs = pl.num_programs(0)
    z, y, x, _ = seats()
    length = 4 * tok
    blocks = gu_a.shape[0]
    o_half, d_half = o_x.shape[2], d_x.shape[2]
    o_mine = pl.ds(pl.multiple_of(x * o_half, o_half), o_half)
    o_theirs = pl.ds(pl.multiple_of((1 - x) * o_half, o_half), o_half)
    d_mine = pl.ds(pl.multiple_of(x * d_half, d_half), d_half)
    d_theirs = pl.ds(pl.multiple_of((1 - x) * d_half, d_half), d_half)
    swap = send(outputs_sent, outputs_received, other_sems, 0, to_x_partner())
    o_over = send(o_a.at[:, :, o_theirs, :], o_x, other_sems, 1, to_x_partner())
    d_over = send(d_in.at[:, :, d_theirs, :], d_x, other_sems, 2, to_x_partner())
    o_send = send(o_a.at[:, 1 - y, o_mine, :], o_y, other_sems, 3, to_y_partner())
    d_send = send(d_a.at[:, 1 - y], d_y, other_sems, 4, to_y_partner())
    late = pl.ds(blocks - LATE, LATE)
    late_send = send(gu_late, gu_b.at[late], other_sems, 5, to_y_partner())

    def z_send(jump, number):
        target = lax.rem(z + jump, line)
        at = late if number else pl.ds(0, blocks - LATE)
        return send(
            gu_a.at[at, :, target],
            gu_z.at[jump - 1, at],
            z_sems,
            number * (line - 1) + jump - 1,
            to_z_partner(line, jump),
        )

    def add(number, _):
        total = gu_a[number].astype(F32) + gu_b[number].astype(F32)
        gu_a[number] = total.astype(BF16)
        return 0

    gu_stays = pltpu.make_async_copy(gu_a.at[:, :, z], gu_mine, local_sems.at[5])
    o_stays = pltpu.make_async_copy(o_a.at[:, y, o_mine, :], o_kept, local_sems.at[6])
    d_stays = pltpu.make_async_copy(d_a.at[:, y], d_kept, local_sems.at[7])
    load_d = pltpu.make_async_copy(d_in.at[:, :, d_mine, :], d_a, local_sems.at[4])

    def hand_over(number):
        rows = pl.ds(number * PAIR, PAIR)
        return send(
            outgoing.at[:, rows, :],
            back_other.at[:, rows, :],
            back_sems,
            number,
            to_core_partner(),
        )

    @pl.when(step == 0)
    def _():
        meet(line, ("z", "y", "x", "core"))
        late_send.start()
        loads = [
            pltpu.make_async_copy(source, target, local_sems.at[number])
            for number, (source, target) in enumerate(
                (
                    (o_in, o_a),
                    (o_landed, o_b),
                    (gu_in, gu_a),
                    (gu_y, gu_b.at[pl.ds(0, blocks - LATE)]),
                )
            )
        ]
        for load in loads:
            load.start()
        load_d.start()
        loads[0].wait()
        loads[1].wait()
        o_a[...] = (o_a[...].astype(F32) + o_b[...].astype(F32)).astype(BF16)
        o_over.start()
        d_over.start()
        loads[2].wait()
        loads[3].wait()
        lax.fori_loop(0, blocks - LATE, add, 0)
        for jump in range(1, line):
            z_send(jump, 0).start()

    @pl.when(step == 1)
    def _():
        late_send.wait()
        lax.fori_loop(blocks - LATE, blocks, add, 0)
        for jump in range(1, line):
            z_send(jump, 1).start()
        gu_stays.start()
        o_over.wait()
        summed = o_a[:, :, o_mine, :].astype(F32) + o_x[...].astype(F32)
        o_a[:, :, o_mine, :] = summed.astype(BF16)
        o_send.start()
        o_stays.start()

    @pl.when(step == 2)
    def _():
        swap.start()

    @pl.when(step == 3)
    def _():
        load_d.wait()
        d_over.wait()
        for at in range(line):
            d_a[at] = (d_a[at].astype(F32) + d_x[at].astype(F32)).astype(BF16)
        d_send.start()
        d_stays.start()

    attend_back_body(
        (received, own),
        (mix_received, mix_own),
        (grad_received, grad_own),
        lambda source, slot: block_of(source, slot, tok),
        tok,
        length,
        tile_q,
        tile_k,
        lse_ref,
        qz,
        gz,
        qn,
        gn,
        kn,
        vn,
        kt,
        inner,
        dq,
        dk,
        dv,
    )
    for slot in range(2):
        take = slice(slot * tok, (slot + 1) * tok)
        for source in range(2):
            cols = block_of(source, slot, tok)
            results = turn_back(dq, dk, dv, cols, cos_ref[:, cols], sin_ref[:, cols])
            for which, result in enumerate(results):
                if source == 1:
                    back_own[which, :, take] = result
                else:
                    at = pl.ds(pl.multiple_of(step * PAIR, PAIR), PAIR)
                    outgoing[which, at, take] = result

    for number in range(4):

        @pl.when(step == number)
        def _(number=number):
            hand_over(number).start()

    @pl.when(step == pairs - 1)
    def _():
        swap.wait()
        d_send.wait()
        o_send.wait()
        for copy in (gu_stays, o_stays, d_stays):
            copy.wait()
        for number in range(2):
            for jump in range(1, line):
                z_send(jump, number).wait()
        for number in range(4):
            hand_over(number).wait()


def attend_back_carry(
    pieces, mixes, grads, lse, cosine, sine, outputs_sent, gu, gu_y, gu_late, d, o, o_landed, line
):
    _, width, span = pieces[0].shape
    tok = span // 2
    length = 2 * span
    pairs = width // PAIR
    tile_q = min(512, length)
    tile_k = min(256, length)
    anywhere = pl.BlockSpec(memory_space=pl.ANY)
    triple = pl.BlockSpec((3, PAIR, span), lambda p: (0, p, 0))
    single = pl.BlockSpec((PAIR, span), lambda p: (p, 0))
    table = pl.BlockSpec((HALF, length), lambda p: (0, 0))
    blocks, _, _, rows, _ = gu.shape
    down_rows, wide = d.shape[2:]
    area = pairs * 2 * length * length // 2
    return pl.pallas_call(
        functools.partial(attend_back_carry_kernel, line, tok, tile_q, tile_k),
        grid=(pairs,),
        in_specs=[triple] * 2
        + [single] * 4
        + [pl.BlockSpec((1, 8, length), lambda p: (p, 0, 0)), table, table]
        + [anywhere] * 7,
        out_specs=[triple] + [anywhere] * 8,
        out_shape=[
            jax.ShapeDtypeStruct((3, width, span), BF16),
            jax.ShapeDtypeStruct((3, width, span), BF16),
            jax.ShapeDtypeStruct(outputs_sent.shape, BF16),
            jax.ShapeDtypeStruct((blocks, 2, rows, 128), BF16),
            jax.ShapeDtypeStruct((line - 1, blocks, 2, rows, 128), BF16),
            jax.ShapeDtypeStruct((line, down_rows // 2, wide), BF16),
            jax.ShapeDtypeStruct((line, down_rows // 2, wide), BF16),
            jax.ShapeDtypeStruct((line, rows // 2, wide), BF16),
            jax.ShapeDtypeStruct((line, rows // 2, wide), BF16),
        ],
        scratch_shapes=[
            pltpu.VMEM((2, PAIR, length), BF16),
            pltpu.VMEM((2, PAIR, length), BF16),
            pltpu.VMEM((2, length, PAIR), BF16),
            pltpu.VMEM((2, length, PAIR), BF16),
            pltpu.VMEM((length, PAIR), BF16),
            pltpu.VMEM((length, PAIR), BF16),
            pltpu.VMEM((PAIR, length), BF16),
            pltpu.VMEM((8, length), F32),
            pltpu.VMEM((PAIR, length), F32),
            pltpu.VMEM((length, PAIR), F32),
            pltpu.VMEM((length, PAIR), F32),
            pltpu.VMEM((3, width, span), BF16),
            pltpu.VMEM((blocks, 2, line, rows, 128), BF16),
            pltpu.VMEM((blocks, 2, line, rows, 128), BF16),
            pltpu.VMEM((line, 2, rows, wide), BF16),
            pltpu.VMEM((line, 2, rows, wide), BF16),
            pltpu.VMEM((line, 2, rows // 2, wide), BF16),
            pltpu.VMEM((line, 2, down_rows // 2, wide), BF16),
            pltpu.VMEM((line, 2, down_rows // 2, wide), BF16),
            pltpu.SemaphoreType.DMA((8,)),
            pltpu.SemaphoreType.DMA((2, 4)),
            pltpu.SemaphoreType.DMA((2, 2 * (line - 1))),
            pltpu.SemaphoreType.DMA((2, 6)),
        ],
        compiler_params=pltpu.CompilerParams(
            dimension_semantics=("arbitrary",),
            vmem_limit_bytes=60 * MIB,
            collective_id=5,
            has_side_effects=True,
        ),
        cost_estimate=pl.CostEstimate(
            flops=area * 2560, bytes_accessed=16 * width * length, transcendentals=area
        ),
        name="attend_back_carry",
    )(
        *pieces, *mixes, *grads, lse, cosine, sine, outputs_sent, gu, gu_y, gu_late, d, o, o_landed
    )


def tail_carry_kernel(line, tok, blocks, *refs):
    (
        inputs,
        x_received,
        back_other,
        back_own,
        full_ref,
        normed_ref,
        grad_in,
        gains_ref,
        mlp_gain_ref,
        gu_mine,
        gu_z,
        d_in,
        d_y,
        o_in,
        o_y,
        input_grad,
        input_landed,
        first_grad,
        first_landed,
        gain_out,
        q_out,
        k_out,
        v_out,
        o_out,
        g_out,
        u_out,
        d_out,
        xs,
        grad_middle,
        normed_t,
        acc,
        grad,
        sent,
        landed,
        y_landed,
        z_landed,
        d_a,
        d_b,
        d_landed,
        o_a,
        o_b,
        o_landed,
        gu_a,
        gu_b,
        gu_x,
        gu_c,
        d_low,
        d_c,
        s_low,
        s_x,
        s_c,
        first_stage,
        first_send,
        input_send,
        gain,
        gain_landed,
        local_sems,
        core_sems,
        y_sems,
        z_sems,
        dz_sems,
        oz_sems,
        x_sems,
        c_sems,
        token_sems,
        gain_sems,
    ) = refs
    step = pl.program_id(0)
    target, turn = step // 3, lax.rem(step, 3)
    z, y, x, core = seats()
    side = x
    wide, span = grad.shape
    depth = 2 * wide
    half = jnp.where(target == 0, 1 - core, core)
    columns = pl.ds(pl.multiple_of(half * wide, wide), wide)
    mine = pl.ds(pl.multiple_of(core * wide, wide), wide)
    others = pl.ds(pl.multiple_of((1 - core) * wide, wide), wide)

    def load(source, place, number):
        return pltpu.make_async_copy(source, place, local_sems.at[number])

    load_tokens = [
        load(inputs.at[side], xs.at[pl.ds(0, tok), :], 0),
        load(x_received, xs.at[pl.ds(tok, tok), :], 1),
        load(grad_in, grad_middle, 2),
    ]
    store_input = load(acc.at[pl.ds(0, tok), :], input_grad, 3)
    store_first = load(first_stage, first_grad, 4)

    def along_z(source, place, sems, base=0):
        return [
            send(
                source(lax.rem(z + jump, line)),
                place(jump - 1),
                sems,
                base + jump - 1,
                to_z_partner(line, jump),
            )
            for jump in range(1, line)
        ]

    d_sends = along_z(lambda at: d_a.at[at], lambda jump: d_landed.at[jump], dz_sems)
    o_sends = along_z(lambda at: o_a.at[at], lambda jump: o_landed.at[jump], oz_sems)

    def core_send(number):
        return send(sent.at[number], landed.at[number], core_sems, number, to_core_partner())

    def y_send(number):
        return send(
            landed.at[number, :, 1 - y], y_landed.at[number], y_sems, number, to_y_partner()
        )

    def z_sends(number):
        return along_z(
            lambda at: landed.at[number, at, y],
            lambda jump: z_landed.at[number, jump],
            z_sems,
            number * (line - 1),
        )

    def first_part(number):
        which = 1 - core if number == 0 else core
        at = pl.ds(pl.multiple_of(which * wide, wide), wide)
        return send(
            first_send.at[:, at], first_landed.at[:, at], token_sems, number, to_x_partner()
        )

    input_part = send(input_send, input_landed, token_sems, 2, to_x_partner())
    gu_sides = (
        send(gu_a, gu_x, x_sems, 0, to_x_partner()),
        send(gu_a, gu_c, c_sems, 0, to_core_partner()),
    )
    d_half, o_half = d_a.shape[1], o_a.shape[1]
    d_mine = pl.ds(pl.multiple_of(x * d_half, d_half), d_half)
    d_theirs = pl.ds(pl.multiple_of((1 - x) * d_half, d_half), d_half)
    o_mine = pl.ds(pl.multiple_of(x * o_half, o_half), o_half)
    o_theirs = pl.ds(pl.multiple_of((1 - x) * o_half, o_half), o_half)
    d_sides = (
        send(d_low.at[d_mine, :], d_low.at[d_mine, :], x_sems, 1, to_x_partner()),
        send(d_low, d_c, c_sems, 1, to_core_partner()),
    )
    o_side = send(s_low.at[0, o_mine, :], s_low.at[0, o_mine, :], x_sems, 2, to_x_partner())

    def square_x(number):
        return send(s_low.at[number], s_x.at[number], x_sems, 2 + number, to_x_partner())

    def square_core(number):
        return send(s_low.at[number], s_c.at[number], c_sems, 2 + number, to_core_partner())

    squares = (o_out, v_out, q_out, k_out)

    def gain_send(number, partner):
        return send(gain.at[number], gain_landed.at[number], gain_sems, number, partner)

    @pl.when(step == 0)
    def _():
        meet(line, ("z", "y", "x", "core"))
        sources = ((d_in, d_a), (d_y, d_b), (o_in, o_a), (o_y, o_b), (gu_mine, gu_a), (gu_z, gu_b))
        loads = [load(source, place, 7 + n) for n, (source, place) in enumerate(sources)]
        for copy in loads:
            copy.start()
        for copy in load_tokens:
            copy.start()
        for copy in loads[:4]:
            copy.wait()
        for at in range(line):
            d_a[at] = (d_a[at].astype(F32) + d_b[at].astype(F32)).astype(BF16)
            o_a[at] = (o_a[at].astype(F32) + o_b[at].astype(F32)).astype(BF16)
        for copy in d_sends + o_sends:
            copy.start()
        for copy in loads[4:]:
            copy.wait()

        def total(number, _):
            for which, out in enumerate((g_out, u_out)):
                value = gu_a[number, which].astype(F32)
                for jump in range(line - 1):
                    value = value + gu_b[jump, number, which].astype(F32)
                at = pl.ds(pl.multiple_of((core * blocks + number) * 128, 128), 128)
                out[:, at] = value
                gu_a[number, which] = value.astype(BF16)
            return 0

        lax.fori_loop(0, blocks, total, 0)
        gu_sides[0].start()
        normed_t[...] = normed_ref[...].T
        acc[...] = jnp.zeros_like(acc)

    def own_part(back):
        @pl.when(turn == 0)
        def _():
            value = 0.5 * back[0].astype(F32)
            rows = value.T
            first_stage[:, columns] = rows[:tok]
            first_send[:, columns] = rows[tok:].astype(BF16)
            grad[...] = value.astype(BF16)

        @pl.when(turn > 0)
        def _():
            grad[...] = back[0]

    @pl.when(target == 0)
    def _():
        own_part(back_other)

    @pl.when(target == 1)
    def _():
        own_part(back_own)

    @pl.when(step == 0)
    def _():
        first_part(0).start()

    @pl.when(step == 3)
    def _():
        first_part(1).start()
        store_first.start()

    @pl.when(target < 2)
    def _():
        value = grad[...]
        result = nt(normed_t[...], value)

        @pl.when(target == 0)
        def _():
            sent[turn] = result.astype(BF16).reshape(sent.shape[1:])
            core_send(turn).start()

        @pl.when(target == 1)
        def _():
            core_send(turn).wait()
            theirs = landed[turn].reshape(result.shape).astype(F32)
            landed[turn] = (result + theirs).astype(BF16).reshape(landed.shape[1:])
            y_send(turn).start()

        acc[...] += nt(value.T, full_ref[0, 0])

    @pl.when(step == 6)
    def _():
        for copy in load_tokens:
            copy.wait()
        weight = gains_ref[0:1, :]
        chunk = min(128, tok)
        gain[...] = jnp.zeros_like(gain)
        gain[0, 1:2, :] = mlp_gain_ref[0:1, :]
        for slot in (1, 0):

            def finish(number, _, slot=slot):
                local = pl.ds(pl.multiple_of(number * chunk, chunk), chunk)
                some = pl.ds(pl.multiple_of(slot * tok + number * chunk, chunk), chunk)
                values = xs[some, :].astype(F32)
                scale = lax.rsqrt(jnp.mean(values * values, axis=1, keepdims=True) + epsilon)
                value = acc[some, :]
                gain[0, 0:1, :] += jnp.sum(value * values * scale, axis=0, keepdims=True)
                weighted = value * weight
                inner = jnp.mean(weighted * values, axis=1, keepdims=True)
                result = (
                    scale * weighted
                    - values * (scale * scale * scale) * inner
                    + grad_middle[some, :]
                )
                if slot == 0:
                    acc[some, :] = result
                else:
                    input_send[local, :] = result.astype(BF16)
                return 0

            lax.fori_loop(0, tok // chunk, finish, 0)
            if slot == 1:
                input_part.start()
        gain_send(0, to_core_partner()).start()
        store_input.start()
        gu_sides[0].wait()

        def gather_x(number, _):
            for which, out in enumerate((g_out, u_out)):
                at = pl.ds(pl.multiple_of((core * blocks + number) * 128, 128), 128)
                value = out[:, at] + gu_x[number, which].astype(F32)
                out[:, at] = value
                gu_a[number, which] = value.astype(BF16)
            return 0

        lax.fori_loop(0, blocks, gather_x, 0)
        gu_sides[1].start()
        gain_send(0, to_core_partner()).wait()
        gain[1] = gain[0] + gain_landed[0]
        gain_send(1, to_y_partner()).start()
        for number in range(3):
            y_send(number).wait()

            def add(at, _, number=number):
                value = landed[number, at, y].astype(F32) + y_landed[number, at].astype(F32)
                landed[number, at, y] = value.astype(BF16)
                return 0

            lax.fori_loop(0, line, add, 0)
            for copy in z_sends(number):
                copy.start()
            if number == 0:
                gain_send(1, to_y_partner()).wait()
                gain[2] = gain[1] + gain_landed[1]
                for jump in range(1, line):
                    gain_z(jump, line, gain, gain_landed, gain_sems).start()
        for copy in d_sends + o_sends:
            copy.wait()

        def sum_z(own, places):
            value = own.astype(F32)
            for place in places:
                value = value + place.astype(F32)
            return value

        value = sum_z(d_a[z], [d_landed[jump] for jump in range(line - 1)])
        d_out[d_mine, mine] = value
        d_low[d_mine, :] = value.astype(BF16)
        d_sides[0].start()
        value = sum_z(o_a[z], [o_landed[jump] for jump in range(line - 1)])
        o_out[o_mine, mine] = value
        s_low[0, o_mine, :] = value.astype(BF16)
        o_side.start()
        for jump in range(1, line):
            gain_z(jump, line, gain, gain_landed, gain_sems).wait()
        value = gain[2]
        for jump in range(1, line):
            value = value + gain_landed[1 + jump]
        gain[3] = value
        last_gain = send(gain.at[3], gain_landed.at[line + 1], gain_sems, line + 1, to_x_partner())
        last_gain.start()
        for number in range(3):
            for copy in z_sends(number):
                copy.wait()
            value = sum_z(
                landed[number, z, y], [z_landed[number, jump] for jump in range(line - 1)]
            )
            squares[1 + number][:, mine] = value
            s_low[1 + number] = value.astype(BF16)
            square_x(1 + number).start()
        last_gain.wait()
        gain[4] = gain[3] + gain_landed[line + 1]
        gain_out[...] = gain[4, :, pl.ds(pl.multiple_of((2 * z + y) * 128, 128), 128)]
        store_first.wait()
        for number in range(2):
            first_part(number).wait()
        d_sides[0].wait()
        d_out[d_theirs, mine] = d_low[d_theirs, :].astype(F32)
        d_sides[1].start()
        o_side.wait()
        o_out[o_theirs, mine] = s_low[0, o_theirs, :].astype(F32)
        square_core(0).start()
        input_part.wait()
        for number in range(1, 4):
            square_x(number).wait()
            value = squares[number][:, mine] + s_x[number].astype(F32)
            squares[number][:, mine] = value
            s_low[number] = value.astype(BF16)
            square_core(number).start()
        gu_sides[1].wait()

        def gather_core(number, _):
            for which, out in enumerate((g_out, u_out)):
                at = pl.ds(pl.multiple_of(((1 - core) * blocks + number) * 128, 128), 128)
                out[:, at] = gu_c[number, which].astype(F32)
            return 0

        lax.fori_loop(0, blocks, gather_core, 0)
        d_sides[1].wait()
        d_out[:, others] = d_c[...].astype(F32)
        for number in range(4):
            square_core(number).wait()
            squares[number][:, others] = s_c[number].astype(F32)
        store_input.wait()


def gain_z(jump, line, gain, gain_landed, gain_sems):
    return send(
        gain.at[2], gain_landed.at[1 + jump], gain_sems, 1 + jump, to_z_partner(line, jump)
    )


def tail_carry(
    inputs,
    x_received,
    back_other,
    back_own,
    full,
    normed,
    grad_middle,
    gains,
    mlp_gain,
    gu_mine,
    gu_z,
    d,
    d_y,
    o,
    o_y,
    line,
):
    slots, tok, depth = inputs.shape
    span = slots * tok
    wide = depth // 2
    blocks, _, rows, _ = gu_mine.shape
    down_rows = 2 * d.shape[1]
    once = pl.Buffered(1)
    anywhere = pl.BlockSpec(memory_space=pl.ANY)

    def half(s):
        core = lax.axis_index("seq") % 2
        return jnp.where(s < 3, 1 - core, core)

    def kind(s):
        return (s + 2) % 3

    def clear(shape):
        zeros = (0,) * len(shape)
        return pl.BlockSpec(shape, lambda s: zeros, pipeline_mode=once)

    square = jax.ShapeDtypeStruct((rows, depth), F32)
    broad = jax.ShapeDtypeStruct((rows, 2 * blocks * 128), F32)
    tall = jax.ShapeDtypeStruct((down_rows, depth), F32)
    tokens = [jax.ShapeDtypeStruct((tok, depth), dtype) for dtype in (F32, BF16)] * 2
    finals = [square] * 4 + [broad] * 2 + [tall]
    vmem = pltpu.VMEM
    dma = pltpu.SemaphoreType.DMA
    return pl.pallas_call(
        functools.partial(tail_carry_kernel, line, tok, blocks),
        grid=(7,),
        in_specs=[
            anywhere,
            anywhere,
            pl.BlockSpec((1, wide, span), lambda s: (kind(jnp.minimum(s, 2)), 0, 0)),
            pl.BlockSpec((1, wide, span), lambda s: (kind(jnp.clip(s, 3, 5)), 0, 0)),
            pl.BlockSpec(
                (1, 1, depth, wide),
                lambda s: (half(jnp.minimum(s, 5)), kind(jnp.minimum(s, 5)), 0, 0),
            ),
            clear((span, depth)),
            anywhere,
            clear((8, depth)),
            clear((8, depth)),
        ]
        + [anywhere] * 6,
        out_specs=[anywhere] * 4 + [clear((8, 128))] + [clear(final.shape) for final in finals],
        out_shape=tokens + [jax.ShapeDtypeStruct((8, 128), F32)] + finals,
        scratch_shapes=[
            vmem((span, depth), BF16),
            vmem((span, depth), F32),
            vmem((depth, span), BF16),
            vmem((span, depth), F32),
            vmem((wide, span), BF16),
            vmem((3, line, 2, rows, wide), BF16),
            vmem((3, line, 2, rows, wide), BF16),
            vmem((3, line, rows, wide), BF16),
            vmem((3, line - 1, rows, wide), BF16),
            vmem((line, down_rows // 2, wide), BF16),
            vmem((line, down_rows // 2, wide), BF16),
            vmem((line - 1, down_rows // 2, wide), BF16),
            vmem((line, rows // 2, wide), BF16),
            vmem((line, rows // 2, wide), BF16),
            vmem((line - 1, rows // 2, wide), BF16),
            vmem((blocks, 2, rows, 128), BF16),
            vmem((line - 1, blocks, 2, rows, 128), BF16),
            vmem((blocks, 2, rows, 128), BF16),
            vmem((blocks, 2, rows, 128), BF16),
            vmem((down_rows, wide), BF16),
            vmem((down_rows, wide), BF16),
            vmem((4, rows, wide), BF16),
            vmem((4, rows, wide), BF16),
            vmem((4, rows, wide), BF16),
            vmem((tok, depth), F32),
            vmem((tok, depth), BF16),
            vmem((tok, depth), BF16),
            vmem((5, 8, depth), F32),
            vmem((line + 2, 8, depth), F32),
            dma((13,)),
            dma((2, 3)),
            dma((2, 3)),
            dma((2, 3 * (line - 1))),
            dma((2, line - 1)),
            dma((2, line - 1)),
            dma((2, 6)),
            dma((2, 6)),
            dma((2, 3)),
            dma((2, line + 2)),
        ],
        compiler_params=pltpu.CompilerParams(
            dimension_semantics=("arbitrary",),
            vmem_limit_bytes=63 * MIB,
            collective_id=6,
            has_side_effects=True,
        ),
        cost_estimate=pl.CostEstimate(
            flops=12 * span * depth * depth,
            bytes_accessed=24 * span * depth + 12 * depth * depth,
            transcendentals=0,
        ),
        name="tail_carry",
    )(
        inputs,
        x_received,
        back_other,
        back_own,
        full,
        normed,
        grad_middle,
        gains,
        mlp_gain,
        gu_mine,
        gu_z,
        d,
        d_y,
        o,
        o_y,
    )


def finish_kernel(place, *refs):
    count = (len(refs) - 2 * 3 - 3) // 2
    tokens, plain = refs[:6], refs[6 : 6 + count]
    outs = refs[6 + count :]
    side = place[0]
    for number in range(3):
        outs[number][side] = tokens[2 * number][...].reshape(tokens[2 * number + 1].shape)
        outs[number][1 - side] = tokens[2 * number + 1][...].astype(F32)
    for number in range(count):
        outs[3 + number][...] = plain[number][...]


def finish(outputs, tokens, plain, side):
    _, tok, depth = outputs[0].shape
    steps = 4
    tile = tok // steps
    row = pl.BlockSpec((tile, depth), lambda s, p: (s, 0))
    tiles = [
        pl.BlockSpec((value.shape[0] // steps, value.shape[1]), lambda s, p: (s, 0))
        for value in plain
    ]
    grid_spec = pltpu.PrefetchScalarGridSpec(
        num_scalar_prefetch=1,
        grid=(steps,),
        in_specs=[pl.BlockSpec((1, tile, depth), lambda s, p: (p[0], s, 0))] + [row] * 5 + tiles,
        out_specs=[pl.BlockSpec((2, tile, depth), lambda s, p: (0, s, 0))] * 3 + tiles,
    )
    return pl.pallas_call(
        finish_kernel,
        out_shape=[jax.ShapeDtypeStruct((2, tok, depth), F32)] * 3
        + [jax.ShapeDtypeStruct(value.shape, value.dtype) for value in plain],
        grid_spec=grid_spec,
        compiler_params=parameters(60),
        cost_estimate=pl.CostEstimate(
            flops=tok * depth, bytes_accessed=60 * tok * depth, transcendentals=0
        ),
        name="finish",
    )(side, *outputs, *tokens, *plain)


def shards(
    inputs,
    first_values,
    out_grad,
    attn_gain,
    query_weight,
    key_weight,
    value_weight,
    output_weight,
    mlp_gain,
    gate_weight,
    up_weight,
    down_weight,
):
    slots, tok, _ = inputs.shape
    groups = lax.axis_size("seq")
    parts = lax.axis_size("fsdp")
    line = parts // 2
    count = groups // slots
    length = tok * groups
    span = slots * tok
    seat = lax.axis_index("seq")
    shard = lax.axis_index("fsdp")
    side = seat // count
    rank = seat % count
    core = seat % 2
    z, y = shard // 2, shard % 2
    wide = D // 2
    width = D // count

    def along_seq(value, partner):
        return lax.ppermute(value, "seq", [(i, partner(i)) for i in range(groups)])

    def along_fsdp(value, partner):
        return lax.ppermute(value, "fsdp", [(i, partner(i)) for i in range(parts)])

    def to_core(value):
        return along_seq(value, lambda i: i ^ 1)

    def to_y(value):
        return along_fsdp(value, lambda i: i ^ 1)

    def to_z(value, jump):
        return along_fsdp(value, lambda i: (i + 2 * jump) % parts)

    def after(value, *others):
        return lax.optimization_barrier((value,) + others)[0]

    def to_sequence(values):
        taken = []
        for jump in range(1, slots):
            sent = lax.dynamic_index_in_dim(values, (side + jump) % slots, 0, keepdims=False)
            taken.append(along_seq(sent, lambda i: (i + jump * count) % groups))
        return taken

    def to_home(whole, sent):
        for jump in range(1, slots):
            part = sent[(jump - 1) * tok : jump * tok]
            part = along_seq(part, lambda i: (i - jump * count) % groups)
            whole = land(whole, part, ((side + jump) % slots)[None])
        return whole

    def rank_up(i, jump):
        return (i // count) * count + (i % count + jump) % count

    def rank_down(i, jump):
        return (i // count) * count + (i % count - jump) % count

    def halves_to_ranks(other, own, axis):
        if count == 2:
            return [other, own]
        return [
            lax.dynamic_slice_in_dim(
                join(other, own, axis), ((rank + 1 + number) % count) * width, width, axis
            )
            for number in range(count)
        ]

    def join(other, own, axis):
        first = jnp.where(core == 0, own, other)
        second = jnp.where(core == 0, other, own)
        return jnp.concatenate([first, second], axis=axis)

    def ranks_to_halves(pieces, axis):
        if count == 2:
            return pieces
        shape = list(pieces[0].shape)
        shape[axis] = D
        whole = jnp.zeros(shape, pieces[0].dtype)
        for number in range(count):
            whole = lax.dynamic_update_slice_in_dim(
                whole, pieces[number], ((rank + 1 + number) % count) * width, axis
            )
        return [
            lax.dynamic_slice_in_dim(whole, which * wide, wide, axis)
            for which in (1 - core, core)
        ]

    def exchange(pieces):
        received = [
            along_seq(pieces[jump - 1], lambda i: rank_up(i, jump)) for jump in range(1, count)
        ]
        return received + [pieces[count - 1]]

    def exchange_back(pieces):
        received = [
            along_seq(pieces[jump - 1], lambda i: rank_down(i, jump)) for jump in range(1, count)
        ]
        return received + [pieces[count - 1]]

    def split(*weights):
        results = []
        for which in (core, 1 - core):
            columns = []
            for weight in weights:
                size = weight.shape[1] // 2
                columns.append(lax.dynamic_slice_in_dim(weight, which * size, size, 1))
            results.append(columns)
        return results

    def gather_z(half):
        return [half] + [to_z(half, jump) for jump in range(1, line)]

    def gather_rest(along_z, other):
        along_y = [to_y(piece) for piece in along_z]
        own = [piece for pair in zip(along_z, along_y) for piece in pair]
        return (own, [other] + [to_core(piece) for piece in own[1:]])

    numbers = []
    for jump in range(line):
        for flip in range(2):
            numbers.append(((z - jump) % line) * 2 + (y ^ flip))
    place = jnp.stack([side, core] + numbers).astype(jnp.int32)

    def low(value):
        return value.astype(BF16)

    def add(a, b):
        return low(a.astype(F32) + b.astype(F32))

    def pick(value, index, axis):
        return lax.dynamic_index_in_dim(value, index, axis, keepdims=False)

    def along_x_and_core(total):
        mine = low(total)
        for jump in range(1, groups // 2):
            total = total + along_seq(mine, lambda i: (i + 2 * jump) % groups).astype(F32)
        mine = low(total)
        return (mine, to_core(mine))

    def along_z_and_on(partial):
        total = partial(z)
        for jump in range(1, line):
            total = total + to_z(low(partial((z + jump) % line)), jump).astype(F32)
        return along_x_and_core(total)

    def scatter(sent, kept, rows_axis):
        shape = kept.shape
        rows = shape[rows_axis] // parts
        cut = shape[:rows_axis] + (line, 2, rows) + shape[rows_axis + 1 :]
        received = to_core(sent).reshape(cut)
        kept = kept.reshape(cut)
        axis = rows_axis + 1
        received_y = to_y(add(pick(kept, 1 - y, axis), pick(received, 1 - y, axis)))
        kept_y = pick(kept, y, axis), pick(received, y, axis)

        def partial(index):
            total = pick(kept_y[0], index, rows_axis).astype(F32)
            total = total + pick(kept_y[1], index, rows_axis).astype(F32)
            return total + pick(received_y, index, rows_axis).astype(F32)

        return along_z_and_on(partial)

    def columns(mine, others):
        first = jnp.where(core == 0, mine, others)
        second = jnp.where(core == 0, others, mine)
        return jnp.concatenate([first, second], axis=-1).astype(F32)

    def everywhere(value):
        value = value + to_core(value)
        value = value + to_y(value)
        total = value
        for jump in range(1, line):
            total = total + to_z(value, jump)
        value = total
        for jump in range(1, groups // 2):
            total = total + along_seq(value, lambda i: (i + 2 * jump) % groups)
        return total

    steps = jnp.arange(slots, dtype=jnp.int32)
    starts = ((side - steps) % slots) * (count * tok) + rank * tok
    positions = (starts[:, None] + jnp.arange(tok, dtype=jnp.int32)[None]).reshape(span)
    freqs = rope_base ** (-(jnp.arange(HALF, dtype=F32) * 2.0 / HEAD_DIM))

    def tables(positions):
        angles = freqs[:, None] * positions.astype(F32)[None, :]
        return (jnp.cos(angles), jnp.sin(angles))

    full_cos, full_sin = tables(jnp.arange(length, dtype=jnp.int32))
    sources = jnp.concatenate(
        [(rank - 1 - jnp.arange(count - 1, dtype=jnp.int32)) % count, rank[None]]
    ).astype(jnp.int32)
    order = (((side - steps) % slots)[None, :] * count + sources[:, None]).reshape(-1)
    order = order.astype(jnp.int32)

    whole_lanes = (slots, count) == (2, 2) and (D // parts) % 128 == 0
    if whole_lanes:
        gains = jnp.pad(jnp.stack([attn_gain, mlp_gain]).astype(F32), ((0, 6), (0, 0)))
        parts_of = lambda ref: [ref.reshape(-1, ref.shape[-1])]
        (
            tokens,
            _,
            grads_early,
            heads_own,
            heads_received,
            normed,
            qkv_full,
            gains_full,
            out_own,
            out_other,
            down_own,
        ) = front(
            inputs,
            first_values,
            out_grad,
            query_weight,
            key_weight,
            value_weight,
            output_weight,
            down_weight,
            gains,
            full_cos,
            full_sin,
            line,
        )
        qkv_full = qkv_full.reshape(2, 3, D, wide)
        tokens = [tokens]
        pieces = [heads_received, heads_own]
        (
            mix_received,
            att_own,
            lse,
            middle,
            normed2,
            out_full,
            att_other,
            grads,
            down_own,
            down_other,
            gate_own,
            gate_other,
            up_own,
            up_other,
        ) = attend_carry(
            heads_received,
            heads_own,
            inputs,
            tokens[0],
            gains_full,
            out_own.reshape(D, wide),
            out_other.reshape(D, wide),
            out_grad,
            grads_early,
            down_own,
            gate_weight,
            up_weight,
            line,
        )
        mixes = [mix_received, att_own]
        grads = [grads]
        gate_pieces = parts_of(gate_own), parts_of(gate_other)
        up_pieces = parts_of(up_own), parts_of(up_other)
        down_pieces = parts_of(down_own), parts_of(down_other)
    else:
        gains = jnp.pad(jnp.stack([attn_gain, mlp_gain], axis=1), ((0, 0), (0, 126)))
        gate_halves, up_halves, out_halves, down_halves = (
            [half[0] for half in split(weight)]
            for weight in (gate_weight, up_weight, output_weight, down_weight)
        )
        cosine, sine = tables(positions)
        qkv = [
            jnp.concatenate(half + [gains], axis=1)
            for half in split(query_weight, key_weight, value_weight)
        ]
        tokens = to_sequence(inputs)
        firsts = to_sequence(first_values)
        grads = to_sequence(out_grad)
        qkv_own, qkv_other = gather_rest(gather_z(qkv[0]), qkv[1])
        out_own, out_other = gather_rest(gather_z(out_halves[0]), out_halves[1])
        gate_pieces = gather_rest(gather_z(gate_halves[0]), gate_halves[1])
        up_pieces = gather_rest(gather_z(up_halves[0]), up_halves[1])
        down_pieces = gather_rest(gather_z(down_halves[0]), down_halves[1])
        heads_other, heads_own, normed, qkv_full, gains_full = project(
            inputs, tokens, first_values, firsts, qkv_own, qkv_other, cosine, sine, place
        )
        pieces = exchange(halves_to_ranks(heads_other, heads_own, 1))
        mixes, lse = attend(pieces, order, slots)
        att_other, att_own = ranks_to_halves(exchange_back(mixes), 0)
        middle, normed2, out_full = output_projection(
            inputs, tokens, out_own, out_other, att_other, att_own, gains_full, place
        )

    if whole_lanes:
        (
            outputs,
            outputs_sent,
            grad_middle,
            low_grad,
            mlp_gain_grad,
            gu_reduced,
            down_reduced,
            gu_y,
            gu_late,
        ) = mlp_carry(
            out_grad,
            grads[0],
            middle,
            normed2,
            gains_full,
            (gate_pieces[0][0], gate_pieces[1][0]),
            (up_pieces[0][0], up_pieces[1][0]),
            (down_pieces[0][0], down_pieces[1][0]),
            line,
        )
        ga_own, ga_received, out_kept, out_landed = grad_attended_carry(
            low_grad, out_full, att_other, att_own, line
        )
        down_reduced = down_reduced.reshape(line, 2, -1, wide)
        out_kept = out_kept.reshape(line, 2, -1, wide)
        out_landed = out_landed.reshape(line, 2, -1, wide)
        (
            back_own,
            back_other,
            outputs_received,
            gu_mine,
            gu_z,
            down_mine,
            down_y,
            out_mine,
            out_y,
        ) = attend_back_carry(
            pieces,
            mixes,
            [ga_received, ga_own],
            lse,
            full_cos,
            full_sin,
            outputs_sent,
            gu_reduced,
            gu_y,
            gu_late,
            down_reduced,
            out_kept,
            out_landed,
            line,
        )
        input_own, input_received, first_own, first_received, *rest = tail_carry(
            inputs,
            tokens[0],
            back_other,
            back_own,
            qkv_full,
            normed,
            grad_middle,
            gains_full,
            mlp_gain_grad,
            gu_mine,
            gu_z,
            down_mine,
            down_y,
            out_mine,
            out_y,
            line,
        )
        gain_grads = rest[0]
        outputs, input_grad, first_grad, *rest = finish(
            (outputs,),
            (outputs_received, input_own, input_received, first_own, first_received),
            rest[1:],
            side[None],
        )
        query_grad, key_grad, value_grad, output_grad, gate_grad, up_grad, down_grad = rest
    else:
        (
            outputs,
            outputs_sent,
            grad_middle,
            low_grad,
            mlp_gain_grad,
            gu_sent,
            gu_kept,
            down_sent,
            down_kept,
        ) = mlp(out_grad, grads, middle, normed2, gains_full, gate_pieces, up_pieces, down_pieces, place)
        ga_other, ga_own, out_sent, out_kept = grad_attended(
            low_grad, out_full, att_other, att_own, place
        )
        gate_up_grad = scatter(gu_sent, gu_kept, 1)
        down_grad = scatter(down_sent.reshape(-1, wide), down_kept.reshape(-1, wide), 0)
        output_grad = scatter(out_sent, out_kept, 0)
        grad_heads = exchange(halves_to_ranks(ga_other, ga_own, 0))
        back = attend_back(pieces, mixes, grad_heads, lse, full_cos, full_sin, order, slots)
        back_other, back_own = ranks_to_halves(exchange_back(back), 1)
        outputs = to_home(outputs, outputs_sent)
        input_grad, input_sent, first_grad, first_sent, gain_grads, qkv_sent, qkv_kept = tail(
            inputs,
            tokens,
            back_other,
            back_own,
            qkv_full,
            normed,
            grad_middle,
            gains_full,
            mlp_gain_grad,
            place,
        )
        query_grad, key_grad, value_grad = columns(*scatter(qkv_sent, qkv_kept, 1))
        gate_grad, up_grad = columns(*gate_up_grad)
        output_grad = columns(*output_grad)
        down_grad = columns(*down_grad)
        gain_grads = everywhere(gain_grads)
        gain_grads = lax.dynamic_slice_in_dim(gain_grads, shard * (D // parts), D // parts, 1)
        input_grad = to_home(input_grad, input_sent)
        first_grad = to_home(first_grad, first_sent)

    return (
        outputs,
        input_grad,
        first_grad,
        gain_grads[0],
        gain_grads[1],
        query_grad,
        key_grad,
        value_grad,
        output_grad,
        gate_grad,
        up_grad,
        down_grad,
    )


def solution(mesh):
    token_spec = P("fsdp", "seq", None)
    weight_spec = P("fsdp", None)
    gain_spec = P("fsdp")
    return jax.shard_map(
        shards,
        mesh=mesh,
        in_specs=(token_spec,) * 3
        + (gain_spec,)
        + (weight_spec,) * 4
        + (gain_spec,)
        + (weight_spec,) * 3,
        out_specs=(token_spec,) * 3 + (gain_spec,) * 2 + (weight_spec,) * 7,
        check_vma=False,
    )
```

```python
import functools
import math

import jax
import jax.numpy as jnp
from jax import lax
from jax.experimental import pallas as pl
from jax.experimental.pallas import tpu as pltpu
from jax.sharding import PartitionSpec as P

D = 1024
HEADS = 16
HEAD_DIM = 64
HALF = HEAD_DIM // 2
PAIR = 2 * HEAD_DIM
F32 = jnp.float32
BF16 = jnp.bfloat16
NEG = -1e30
MIB = 1024 * 1024
epsilon = 1e-06
rope_base = 10000.0


def dot(a, b):
    return lax.dot_general(a, b, (((1,), (0,)), ((), ())), preferred_element_type=F32)


def head_rows(value, head):
    row = lax.broadcasted_iota(jnp.int32, value.shape, 0)
    return jnp.where((row // HEAD_DIM) == head, value, jnp.zeros_like(value))


def head_lanes(value, head):
    lane = lax.broadcasted_iota(jnp.int32, value.shape, 1)
    return jnp.where((lane // HEAD_DIM) == head, value, jnp.zeros_like(value))


def causal(scores):
    side = scores.shape[0]
    square = scores[:, :side]
    key = lax.broadcasted_iota(jnp.int32, square.shape, 0)
    query = lax.broadcasted_iota(jnp.int32, square.shape, 1)
    square = jnp.where(key <= query, square, NEG)
    if scores.shape[1] == side:
        return square
    return jnp.concatenate([square, scores[:, side:]], axis=1)


def attend_body(length, tile_k, qz, kn, vt, ot, lse_ref):
    def score(sub, head):
        start = sub * tile_k
        return causal(dot(kn[start : start + tile_k, :], qz[head, :, start:]))

    def absorb(sub, head, carry, scores):
        peak, total, mixed = carry
        start = sub * tile_k
        new_peak = jnp.maximum(peak, jnp.max(scores, axis=0, keepdims=True))
        weights = jnp.exp(scores - new_peak)
        fade = jnp.exp(peak - new_peak)
        total = total * fade + jnp.sum(weights, axis=0, keepdims=True)
        values = vt[head * HEAD_DIM : (head + 1) * HEAD_DIM, start : start + tile_k]
        mixed = mixed * fade + dot(values, weights.astype(BF16))
        return (new_peak, total, mixed)

    tiles = [(sub, head) for sub in range(length // tile_k) for head in range(2)]
    carries = [
        (
            jnp.full((1, length), NEG, F32),
            jnp.zeros((1, length), F32),
            jnp.zeros((HEAD_DIM, length), F32),
        )
        for _ in range(2)
    ]
    ahead = score(*tiles[0])
    for number, (sub, head) in enumerate(tiles):
        scores = ahead
        if number + 1 < len(tiles):
            ahead = score(*tiles[number + 1])
        peak, total, mixed = absorb(sub, head, carries[head], scores)
        done = slice(sub * tile_k, (sub + 1) * tile_k)
        rows = slice(head * HEAD_DIM, (head + 1) * HEAD_DIM)
        ot[rows, done] = (mixed[:, :tile_k] / total[:, :tile_k]).astype(BF16)
        lse_ref[0, head : head + 1, done] = peak[:, :tile_k] + jnp.log(total[:, :tile_k])
        carries[head] = (peak[:, tile_k:], total[:, tile_k:], mixed[:, tile_k:])


def attend_kernel(count, slots, tok, tile_k, order, *refs):
    pieces = refs[:count]
    outs = refs[count : 2 * count]
    lse_ref = refs[2 * count]
    qz, kn, vt, ot = refs[2 * count + 1 :]
    for source in range(count):
        for slot in range(slots):
            cols = pl.ds(pl.multiple_of(order[source * slots + slot] * tok, tok), tok)
            take = slice(slot * tok, (slot + 1) * tok)
            query = pieces[source][0, :, take] * jnp.asarray(HEAD_DIM**-0.5, BF16)
            for head in range(2):
                qz[head, :, cols] = head_rows(query, head)
            kn[cols, :] = pieces[source][1, :, take].T
            vt[:, cols] = pieces[source][2, :, take]
    length = count * slots * tok
    attend_body(length, tile_k, qz, kn, vt, ot, lse_ref)
    for source in range(count):
        for slot in range(slots):
            cols = pl.ds(pl.multiple_of(order[source * slots + slot] * tok, tok), tok)
            outs[source][:, slot * tok : (slot + 1) * tok] = ot[:, cols]


def attend(pieces, order, slots):
    count = len(pieces)
    width, span = pieces[0].shape[1:]
    tok = span // slots
    length = count * span
    pairs = width // PAIR
    tile_k = min(256, length)
    grid_spec = pltpu.PrefetchScalarGridSpec(
        num_scalar_prefetch=1,
        grid=(pairs,),
        in_specs=[pl.BlockSpec((3, PAIR, span), lambda p, o: (0, p, 0))] * count,
        out_specs=[pl.BlockSpec((PAIR, span), lambda p, o: (p, 0))] * count
        + [pl.BlockSpec((1, 8, length), lambda p, o: (p, 0, 0))],
        scratch_shapes=[
            pltpu.VMEM((2, PAIR, length), BF16),
            pltpu.VMEM((length, PAIR), BF16),
            pltpu.VMEM((PAIR, length), BF16),
            pltpu.VMEM((PAIR, length), BF16),
        ],
    )
    area = pairs * 2 * length * length // 2
    results = pl.pallas_call(
        functools.partial(attend_kernel, count, slots, tok, tile_k),
        out_shape=[jax.ShapeDtypeStruct((width, span), BF16)] * count
        + [jax.ShapeDtypeStruct((pairs, 8, length), F32)],
        grid_spec=grid_spec,
        compiler_params=pltpu.CompilerParams(
            dimension_semantics=("arbitrary",), vmem_limit_bytes=48 * MIB
        ),
        cost_estimate=pl.CostEstimate(
            flops=area * 1024, bytes_accessed=8 * width * length, transcendentals=area
        ),
        name="attend",
    )(order, *pieces)
    return (results[:count], results[count])


def attend_back_body(
    pieces,
    mixes,
    grads,
    columns,
    tok,
    length,
    tile_q,
    tile_k,
    lse_ref,
    qz,
    gz,
    qn,
    gn,
    kn,
    vn,
    kt,
    inner,
    dq,
    dk,
    dv,
):
    slots = pieces[0].shape[2] // tok
    for source in range(len(pieces)):
        for slot in range(slots):
            cols = columns(source, slot)
            take = slice(slot * tok, (slot + 1) * tok)
            query = pieces[source][0, :, take] * jnp.asarray(HEAD_DIM**-0.5, BF16)
            grad = grads[source][:, take]
            query_rows = query.T
            grad_rows = grad.T
            for head in range(2):
                qz[head, :, cols] = head_rows(query, head)
                gz[head, :, cols] = head_rows(grad, head)
                qn[head, cols, :] = head_lanes(query_rows, head)
                gn[head, cols, :] = head_lanes(grad_rows, head)
            key = pieces[source][1, :, take]
            kt[:, cols] = key
            kn[cols, :] = key.T
            vn[cols, :] = pieces[source][2, :, take].T
            both = grad.astype(F32) * mixes[source][:, take].astype(F32)
            for head in range(2):
                inner[head : head + 1, cols] = jnp.sum(
                    both[head * HEAD_DIM : (head + 1) * HEAD_DIM], axis=0, keepdims=True
                )
    dq[...] = jnp.zeros_like(dq)
    steps = tile_q // tile_k

    def tile(key_start, query_start, width, masked, carry):
        grad_keys, grad_values = carry
        keys = kn[pl.ds(key_start, tile_k), :]
        values = vn[pl.ds(key_start, tile_k), :]
        cols = pl.ds(query_start, width)
        for head in range(2):
            rows = slice(head * HEAD_DIM, (head + 1) * HEAD_DIM)
            scores = dot(keys, qz[head, :, cols])
            if masked:
                scores = causal(scores)
            probs = jnp.exp(scores - lse_ref[0, head : head + 1, cols])
            grad_probs = dot(values, gz[head, :, cols])
            grad_scores = (probs * (grad_probs - inner[head : head + 1, cols])).astype(BF16)
            grad_values = grad_values + dot(probs.astype(BF16), gn[head, cols, :])
            grad_keys = grad_keys + dot(grad_scores, qn[head, cols, :])
            dq[rows, cols] += dot(kt[rows, pl.ds(key_start, tile_k)], grad_scores)
        return (grad_keys, grad_values)

    def one(number, _):
        base = pl.multiple_of(number * tile_q, tile_q)
        for sub in range(steps):
            skip = sub * tile_k
            key_start = pl.multiple_of(base + skip, tile_k)
            carry = (jnp.zeros((tile_k, PAIR), F32), jnp.zeros((tile_k, PAIR), F32))
            carry = tile(key_start, key_start, tile_q - skip, True, carry)

            def body(step, carry):
                return tile(
                    key_start, pl.multiple_of(step * tile_q, tile_q), tile_q, False, carry
                )

            carry = lax.fori_loop(number + 1, length // tile_q, body, carry)
            dk[pl.ds(key_start, tile_k), :] = carry[0]
            dv[pl.ds(key_start, tile_k), :] = carry[1]
        return 0

    lax.fori_loop(0, length // tile_q, one, 0)


def turn_back(dq, dk, dv, cols, cosine, sine):
    half = HEAD_DIM // 2
    results = []
    for grad in (dq[:, cols] * (HEAD_DIM**-0.5), dk[cols, :].T):
        turned = []
        for head in range(2):
            low = head * HEAD_DIM
            first = grad[low : low + half]
            second = grad[low + half : low + 2 * half]
            turned += [first * cosine + second * sine, second * cosine - first * sine]
        results.append(jnp.concatenate(turned, axis=0).astype(BF16))
    results.append(dv[cols, :].T.astype(BF16))
    return results


def attend_back_kernel(count, slots, tok, tile_q, tile_k, order, *refs):
    pieces = refs[:count]
    mixes = refs[count : 2 * count]
    grads = refs[2 * count : 3 * count]
    lse_ref, cos_ref, sin_ref = refs[3 * count : 3 * count + 3]
    outs = refs[3 * count + 3 : 4 * count + 3]
    scratch = refs[4 * count + 3 :]
    dq, dk, dv = scratch[-3:]

    def columns(source, slot):
        return pl.ds(pl.multiple_of(order[source * slots + slot] * tok, tok), tok)

    attend_back_body(
        pieces,
        mixes,
        grads,
        columns,
        tok,
        count * slots * tok,
        tile_q,
        tile_k,
        lse_ref,
        *scratch,
    )
    for source in range(count):
        for slot in range(slots):
            cols = columns(source, slot)
            results = turn_back(dq, dk, dv, cols, cos_ref[:, cols], sin_ref[:, cols])
            for which, result in enumerate(results):
                outs[source][which, :, slot * tok : (slot + 1) * tok] = result


def attend_back(pieces, mixes, grads, lse, cosine, sine, order, slots):
    count = len(pieces)
    width, span = pieces[0].shape[1:]
    tok = span // slots
    length = count * span
    pairs = width // PAIR
    tile_q = min(512, length)
    tile_k = min(256, length)
    triple = pl.BlockSpec((3, PAIR, span), lambda p, o: (0, p, 0))
    single = pl.BlockSpec((PAIR, span), lambda p, o: (p, 0))
    table = pl.BlockSpec((HEAD_DIM // 2, length), lambda p, o: (0, 0))
    grid_spec = pltpu.PrefetchScalarGridSpec(
        num_scalar_prefetch=1,
        grid=(pairs,),
        in_specs=[triple] * count
        + [single] * (2 * count)
        + [pl.BlockSpec((1, 8, length), lambda p, o: (p, 0, 0)), table, table],
        out_specs=[triple] * count,
        scratch_shapes=[
            pltpu.VMEM((2, PAIR, length), BF16),
            pltpu.VMEM((2, PAIR, length), BF16),
            pltpu.VMEM((2, length, PAIR), BF16),
            pltpu.VMEM((2, length, PAIR), BF16),
            pltpu.VMEM((length, PAIR), BF16),
            pltpu.VMEM((length, PAIR), BF16),
            pltpu.VMEM((PAIR, length), BF16),
            pltpu.VMEM((8, length), F32),
            pltpu.VMEM((PAIR, length), F32),
            pltpu.VMEM((length, PAIR), F32),
            pltpu.VMEM((length, PAIR), F32),
        ],
    )
    area = pairs * 2 * length * length // 2
    return pl.pallas_call(
        functools.partial(attend_back_kernel, count, slots, tok, tile_q, tile_k),
        out_shape=[jax.ShapeDtypeStruct((3, width, span), BF16)] * count,
        grid_spec=grid_spec,
        compiler_params=pltpu.CompilerParams(
            dimension_semantics=("arbitrary",), vmem_limit_bytes=56 * MIB
        ),
        cost_estimate=pl.CostEstimate(
            flops=area * 2560, bytes_accessed=16 * width * length, transcendentals=area
        ),
        name="attend_back",
    )(order, *pieces, *mixes, *grads, lse, cosine, sine)


def nt(a, b):
    return lax.dot_general(a, b, (((1,), (1,)), ((), ())), preferred_element_type=F32)


def whole_block(shape):
    zeros = (0,) * len(shape)
    return pl.BlockSpec(shape, lambda *_: zeros)


def parameters(mib):
    return pltpu.CompilerParams(dimension_semantics=("arbitrary",), vmem_limit_bytes=mib * MIB)


def project_kernel(slots, tok, count, rows, place, *refs):
    xs, firsts = refs[:slots], refs[slots : 2 * slots]
    own = refs[2 * slots : 2 * slots + count]
    other = refs[2 * slots + count : 2 * slots + 2 * count]
    cos_ref, sin_ref = refs[2 * slots + 2 * count : 2 * slots + 2 * count + 2]
    other_ref, own_ref, normed_ref, full_ref, gains_ref, column = refs[2 * slots + 2 * count + 2 :]
    step = pl.program_id(0)
    target, kind = step // 3, step % 3
    core = place[1]
    half = jnp.where(target == 0, 1 - core, core)
    depth = normed_ref.shape[1]
    wide = own_ref.shape[1]

    @pl.when(step == 0)
    def _():
        for number in range(count):
            at = pl.ds(pl.multiple_of(place[2 + number] * rows, rows), rows)
            for which in range(3):
                columns = slice(which * wide, (which + 1) * wide)
                full_ref[core, which, at, :] = own[number][:, columns]
                full_ref[1 - core, which, at, :] = other[number][:, columns]
            column[at, :] = own[number][:, 3 * wide :]
        gains_ref[...] = column[...].T[:8].astype(F32)
        gain = gains_ref[0:1, :]
        for slot in range(slots):
            values = xs[slot][...].reshape(tok, depth).astype(F32)
            scale = lax.rsqrt(jnp.mean(values * values, axis=1, keepdims=True) + epsilon)
            normed_ref[slot * tok : (slot + 1) * tok, :] = (values * scale * gain).astype(BF16)

    weight = full_ref[half, kind]
    raw = nt(weight.T, normed_ref[...])

    def store(value):
        @pl.when(target == 0)
        def _():
            other_ref[0] = value

        @pl.when(target == 1)
        def _():
            own_ref[0] = value

    @pl.when(kind < 2)
    def _():
        parts = raw.reshape(wide // HEAD_DIM, 2, HALF, raw.shape[1])
        first, second = parts[:, 0], parts[:, 1]
        cosine, sine = cos_ref[...][None], sin_ref[...][None]
        turned = jnp.stack(
            [first * cosine - second * sine, first * sine + second * cosine], axis=1
        )
        store(turned.reshape(raw.shape).astype(BF16))

    @pl.when(kind == 2)
    def _():
        first = jnp.concatenate(
            [ref[...].reshape(tok, wide).T.astype(F32) for ref in firsts], axis=1
        )
        store((0.5 * raw + 0.5 * first).astype(BF16))


def project(inputs, received, firsts, firsts_received, own, other, cosine, sine, place):
    slots, tok, depth = inputs.shape
    count, rows = len(own), own[0].shape[0]
    wide = depth // 2
    span = slots * tok

    def half(s, p):
        return jnp.where(s < 3, 1 - p[1], p[1])

    x_specs = [pl.BlockSpec((1, tok, depth), lambda s, p: (p[0], 0, 0))]
    x_specs += [whole_block((tok, depth))] * (slots - 1)
    first_specs = [pl.BlockSpec((1, tok, wide), lambda s, p: (p[0], 0, half(s, p)))]
    first_specs += [pl.BlockSpec((tok, wide), lambda s, p: (0, half(s, p)))] * (slots - 1)
    grid_spec = pltpu.PrefetchScalarGridSpec(
        num_scalar_prefetch=1,
        grid=(6,),
        in_specs=x_specs
        + first_specs
        + [whole_block(own[0].shape)] * (2 * count)
        + [whole_block((HALF, span))] * 2,
        out_specs=[
            pl.BlockSpec((1, wide, span), lambda s, p: (jnp.minimum(s, 2), 0, 0)),
            pl.BlockSpec((1, wide, span), lambda s, p: (jnp.maximum(s - 3, 0), 0, 0)),
            whole_block((span, depth)),
            whole_block((2, 3, depth, wide)),
            whole_block((8, depth)),
        ],
        scratch_shapes=[pltpu.VMEM((depth, 128), BF16)],
    )
    return pl.pallas_call(
        functools.partial(project_kernel, slots, tok, count, rows),
        out_shape=[
            jax.ShapeDtypeStruct((3, wide, span), BF16),
            jax.ShapeDtypeStruct((3, wide, span), BF16),
            jax.ShapeDtypeStruct((span, depth), BF16),
            jax.ShapeDtypeStruct((2, 3, depth, wide), BF16),
            jax.ShapeDtypeStruct((8, depth), F32),
        ],
        grid_spec=grid_spec,
        compiler_params=parameters(56),
        cost_estimate=pl.CostEstimate(
            flops=6 * span * depth * depth,
            bytes_accessed=2 * (8 * span * depth + 6 * depth * depth),
            transcendentals=0,
        ),
        name="project",
    )(place, inputs, *received, firsts, *firsts_received, *own, *other, cosine, sine)


def output_kernel(slots, tok, count, rows, place, *refs):
    xs = refs[:slots]
    own = refs[slots : slots + count]
    other = refs[slots + count : slots + 2 * count]
    att_other, att_own, gains_ref = refs[slots + 2 * count : slots + 2 * count + 3]
    middle_ref, normed_ref, full_ref = refs[slots + 2 * count + 3 :]
    step = pl.program_id(0)
    core = place[1]
    wide = att_own.shape[0]
    depth = 2 * wide
    mine = pl.ds(pl.multiple_of(core * wide, wide), wide)
    others = pl.ds(pl.multiple_of((1 - core) * wide, wide), wide)

    @pl.when(step == 0)
    def _():
        for number in range(count):
            at = pl.ds(pl.multiple_of(place[2 + number] * rows, rows), rows)
            full_ref[at, mine] = own[number][...]
            full_ref[at, others] = other[number][...]

    total = dot(att_own[...].T, full_ref[mine, :]) + dot(att_other[...].T, full_ref[others, :])
    for slot in range(slots):

        @pl.when(step == slot)
        def _(slot=slot):
            middle_ref[...] = xs[slot][...].reshape(tok, depth).astype(F32) + total

    middle = middle_ref[...]
    scale = lax.rsqrt(jnp.mean(middle * middle, axis=1, keepdims=True) + epsilon)
    normed_ref[...] = (middle * scale * gains_ref[1:2, :]).astype(BF16)


def output_projection(inputs, received, own, other, att_other, att_own, gains, place):
    slots, tok, depth = inputs.shape
    count, rows = len(own), own[0].shape[0]
    wide = depth // 2
    span = slots * tok
    x_specs = [pl.BlockSpec((1, tok, depth), lambda s, p: (p[0], 0, 0))]
    x_specs += [whole_block((tok, depth))] * (slots - 1)
    grid_spec = pltpu.PrefetchScalarGridSpec(
        num_scalar_prefetch=1,
        grid=(slots,),
        in_specs=x_specs
        + [whole_block(own[0].shape)] * (2 * count)
        + [pl.BlockSpec((wide, tok), lambda s, p: (0, s))] * 2
        + [whole_block((8, depth))],
        out_specs=[
            pl.BlockSpec((tok, depth), lambda s, p: (s, 0)),
            pl.BlockSpec((tok, depth), lambda s, p: (s, 0)),
            whole_block((depth, depth)),
        ],
    )
    return pl.pallas_call(
        functools.partial(output_kernel, slots, tok, count, rows),
        out_shape=[
            jax.ShapeDtypeStruct((span, depth), F32),
            jax.ShapeDtypeStruct((span, depth), BF16),
            jax.ShapeDtypeStruct((depth, depth), BF16),
        ],
        grid_spec=grid_spec,
        compiler_params=parameters(56),
        cost_estimate=pl.CostEstimate(
            flops=2 * span * depth * depth,
            bytes_accessed=12 * span * depth + 4 * depth * depth,
            transcendentals=0,
        ),
        name="output_projection",
    )(place, inputs, *received, *own, *other, att_other, att_own, gains)


def mlp_kernel(slots, tok, count, rows, down_rows, blocks, place, *refs):
    grads = refs[:slots]
    middle_ref, normed_ref, gains_ref = refs[slots : slots + 3]
    base = slots + 3
    own_g, other_g, own_u, other_u, own_d, other_d = (
        refs[base + number * count : base + (number + 1) * count] for number in range(6)
    )
    (
        out_ref,
        send_ref,
        grad_ref,
        low_ref,
        gain_ref,
        gu_send,
        gu_keep,
        d_send,
        d_keep,
        wgu,
        wd,
        og,
        normed_t,
        acc,
        back,
        sems,
    ) = refs[base + 6 * count :]
    step = pl.program_id(0)
    core = place[1]
    depth = og.shape[1]
    wide = depth // 2
    strip = 128
    half_width = blocks * strip
    mine = pl.ds(pl.multiple_of(core * wide, wide), wide)
    others = pl.ds(pl.multiple_of((1 - core) * wide, wide), wide)

    def loads():
        copies = []
        for number in range(count):
            at = pl.ds(pl.multiple_of(place[2 + number] * rows, rows), rows)
            for which, (gate, up) in enumerate(((own_g, own_u), (other_g, other_u))):
                copies.append((gate[number], wgu.at[which, at, pl.ds(0, half_width)]))
                copies.append((up[number], wgu.at[which, at, pl.ds(half_width, half_width)]))
        for number in range(count):
            at = pl.ds(pl.multiple_of(place[2 + number] * down_rows, down_rows), down_rows)
            copies.append((own_d[number], wd.at[at, mine]))
            copies.append((other_d[number], wd.at[at, others]))
        return [
            pltpu.make_async_copy(source, target, sems.at[number])
            for number, (source, target) in enumerate(copies)
        ]

    @pl.when(step == 0)
    def _():
        copies = loads()
        for copy in copies:
            copy.start()
        for slot in range(slots):
            og[slot * tok : (slot + 1) * tok, :] = grads[slot][...].reshape(tok, depth)
        normed_t[...] = normed_ref[...].T
        acc[...] = jnp.zeros_like(acc)
        back[...] = jnp.zeros_like(back)
        for copy in copies:
            copy.wait()

    at = pl.ds(pl.multiple_of(step * strip, strip), strip)
    up_at = pl.ds(pl.multiple_of(half_width + step * strip, strip), strip)
    gate_w = jnp.concatenate([wgu[0, :, at], wgu[1, :, at]], axis=1)
    up_w = jnp.concatenate([wgu[0, :, up_at], wgu[1, :, up_at]], axis=1)
    own_rows = pl.ds(pl.multiple_of(core * half_width + step * strip, strip), strip)
    other_rows = pl.ds(pl.multiple_of((1 - core) * half_width + step * strip, strip), strip)
    down_w = jnp.concatenate([wd[own_rows, :], wd[other_rows, :]], axis=0)
    normed = normed_ref[...]
    gate = dot(normed, gate_w)
    up = dot(normed, up_w)
    grad_active = nt(og[...], down_w)
    sigma = jax.nn.sigmoid(gate)
    silu = gate * sigma
    active = (silu * up).astype(BF16)
    grad_up = (grad_active * silu).astype(BF16)
    grad_gate = (grad_active * up * sigma * (1.0 + gate * (1.0 - sigma))).astype(BF16)
    acc[...] += dot(active, down_w)
    back[...] += nt(grad_gate, gate_w) + nt(grad_up, up_w)
    grad_gate_w = dot(normed_t[...], grad_gate).astype(BF16)
    gu_keep[0] = grad_gate_w[:, :strip]
    gu_send[0] = grad_gate_w[:, strip:]
    grad_up_w = dot(normed_t[...], grad_up).astype(BF16)
    gu_keep[1] = grad_up_w[:, :strip]
    gu_send[1] = grad_up_w[:, strip:]
    active_t = active.T
    kept = dot(active_t, og[:, mine]).astype(BF16)
    sent = dot(active_t, og[:, others]).astype(BF16)
    d_keep[core] = kept[:strip]
    d_keep[1 - core] = kept[strip:]
    d_send[core] = sent[:strip]
    d_send[1 - core] = sent[strip:]

    @pl.when(step == blocks - 1)
    def _():
        gain = gains_ref[1:2, :]
        chunk = min(128, tok)
        gain_ref[...] = jnp.zeros_like(gain_ref)
        for slot in range(slots):

            def finish(number, _, slot=slot):
                local = pl.ds(pl.multiple_of(number * chunk, chunk), chunk)
                some = pl.ds(pl.multiple_of(slot * tok + number * chunk, chunk), chunk)
                middle = middle_ref[some, :]
                scale = lax.rsqrt(jnp.mean(middle * middle, axis=1, keepdims=True) + epsilon)
                result = middle + acc[some, :]
                if slot == 0:
                    out_ref[0, local, :] = result
                else:
                    send_ref[pl.ds(pl.multiple_of((slot - 1) * tok + number * chunk, chunk), chunk), :] = (
                        result.astype(BF16)
                    )
                grad = back[some, :]
                gain_ref[0:1, :] += jnp.sum(grad * middle * scale, axis=0, keepdims=True)
                weighted = grad * gain
                inner = jnp.mean(weighted * middle, axis=1, keepdims=True)
                grad_middle = (
                    scale * weighted
                    - middle * (scale * scale * scale) * inner
                    + og[some, :].astype(F32)
                )
                grad_ref[some, :] = grad_middle
                low_ref[some, :] = grad_middle.astype(BF16)
                return 0

            lax.fori_loop(0, tok // chunk, finish, 0)


def mlp(grads, grads_received, middle, normed, gains, gate, up, down, place):
    slots, tok, depth = grads.shape
    own_d, other_d = down
    count, rows = len(own_d), gate[0][0].shape[0]
    down_rows = own_d[0].shape[0]
    half_width = gate[0][0].shape[1]
    wide = depth // 2
    span = slots * tok
    blocks = half_width // 128
    once = pl.Buffered(1)
    g_specs = [pl.BlockSpec((1, tok, depth), lambda s, p: (p[0], 0, 0), pipeline_mode=once)]
    g_specs += [pl.BlockSpec((tok, depth), lambda s, p: (0, 0), pipeline_mode=once)] * (slots - 1)
    gu_spec = pl.BlockSpec((2, depth, 128), lambda s, p: (0, 0, s))
    d_spec = pl.BlockSpec((2, 128, wide), lambda s, p: (0, s, 0))
    grid_spec = pltpu.PrefetchScalarGridSpec(
        num_scalar_prefetch=1,
        grid=(blocks,),
        in_specs=g_specs
        + [
            pl.BlockSpec((span, depth), lambda s, p: (0, 0), pipeline_mode=once),
            pl.BlockSpec((span, depth), lambda s, p: (0, 0), pipeline_mode=once),
            whole_block((8, depth)),
        ]
        + [pl.BlockSpec(memory_space=pl.ANY)] * (6 * count),
        out_specs=[
            pl.BlockSpec((1, tok, depth), lambda s, p: (p[0], 0, 0), pipeline_mode=once),
            pl.BlockSpec(((slots - 1) * tok, depth), lambda s, p: (0, 0), pipeline_mode=once),
            pl.BlockSpec((span, depth), lambda s, p: (0, 0), pipeline_mode=once),
            pl.BlockSpec((span, depth), lambda s, p: (0, 0), pipeline_mode=once),
            whole_block((8, depth)),
            gu_spec,
            gu_spec,
            d_spec,
            d_spec,
        ],
        scratch_shapes=[
            pltpu.VMEM((2, depth, 2 * half_width), BF16),
            pltpu.VMEM((2 * half_width, depth), BF16),
            pltpu.VMEM((span, depth), BF16),
            pltpu.VMEM((depth, span), BF16),
            pltpu.VMEM((span, depth), F32),
            pltpu.VMEM((span, depth), F32),
            pltpu.SemaphoreType.DMA((6 * count,)),
        ],
    )
    return pl.pallas_call(
        functools.partial(mlp_kernel, slots, tok, count, rows, down_rows, blocks),
        out_shape=[
            jax.ShapeDtypeStruct((slots, tok, depth), F32),
            jax.ShapeDtypeStruct(((slots - 1) * tok, depth), BF16),
            jax.ShapeDtypeStruct((span, depth), F32),
            jax.ShapeDtypeStruct((span, depth), BF16),
            jax.ShapeDtypeStruct((8, depth), F32),
            jax.ShapeDtypeStruct((2, depth, half_width), BF16),
            jax.ShapeDtypeStruct((2, depth, half_width), BF16),
            jax.ShapeDtypeStruct((2, half_width, wide), BF16),
            jax.ShapeDtypeStruct((2, half_width, wide), BF16),
        ],
        grid_spec=grid_spec,
        compiler_params=parameters(63),
        cost_estimate=pl.CostEstimate(
            flops=16 * span * depth * 2 * half_width,
            bytes_accessed=24 * depth * half_width + 20 * span * depth,
            transcendentals=2 * span * half_width,
        ),
        name="mlp",
    )(
        place,
        grads,
        *grads_received,
        middle,
        normed,
        gains,
        *gate[0],
        *gate[1],
        *up[0],
        *up[1],
        *own_d,
        *other_d,
    )


def grad_attended_kernel(place, low_ref, full_ref, att_other, att_own, ga_other, ga_own, sent, kept):
    step = pl.program_id(0)
    core = place[1]
    wide = att_own.shape[0]
    mine = pl.ds(pl.multiple_of(core * wide, wide), wide)
    others = pl.ds(pl.multiple_of((1 - core) * wide, wide), wide)
    for number, (att, result) in enumerate(((att_other, ga_other), (att_own, ga_own))):

        @pl.when(step == number)
        def _(att=att, result=result):
            result[...] = nt(full_ref[...], low_ref[...]).astype(BF16)
            kept[...] = dot(att[...], low_ref[:, mine]).astype(BF16)
            sent[...] = dot(att[...], low_ref[:, others]).astype(BF16)


def grad_attended(low, full, att_other, att_own, place):
    span, depth = low.shape
    wide = depth // 2

    def half(s, p):
        return jnp.where(s == 0, 1 - p[1], p[1])

    row_spec = pl.BlockSpec((wide, wide), lambda s, p: (half(s, p), 0))
    grid_spec = pltpu.PrefetchScalarGridSpec(
        num_scalar_prefetch=1,
        grid=(2,),
        in_specs=[
            whole_block((span, depth)),
            pl.BlockSpec((wide, depth), lambda s, p: (half(s, p), 0)),
            whole_block((wide, span)),
            whole_block((wide, span)),
        ],
        out_specs=[whole_block((wide, span)), whole_block((wide, span)), row_spec, row_spec],
    )
    return pl.pallas_call(
        grad_attended_kernel,
        out_shape=[
            jax.ShapeDtypeStruct((wide, span), BF16),
            jax.ShapeDtypeStruct((wide, span), BF16),
            jax.ShapeDtypeStruct((depth, wide), BF16),
            jax.ShapeDtypeStruct((depth, wide), BF16),
        ],
        grid_spec=grid_spec,
        compiler_params=parameters(48),
        cost_estimate=pl.CostEstimate(
            flops=4 * span * depth * depth,
            bytes_accessed=6 * span * depth + 4 * depth * depth,
            transcendentals=0,
        ),
        name="grad_attended",
    )(place, low, full, att_other, att_own)


def tail_kernel(slots, tok, place, *refs):
    xs = refs[:slots]
    (
        back_other,
        back_own,
        full_ref,
        normed_ref,
        grad_ref,
        gains_ref,
        mlp_gain_ref,
        out_ref,
        send_ref,
        first_ref,
        first_send,
        gain_ref,
        sent,
        kept,
        normed_t,
        acc,
    ) = refs[slots:]
    step = pl.program_id(0)
    target, kind = step // 3, step % 3
    depth = acc.shape[1]

    @pl.when(step == 0)
    def _():
        normed_t[...] = normed_ref[...].T
        acc[...] = jnp.zeros_like(acc)

    def part(back, result):
        grad = back[0]

        @pl.when(kind == 2)
        def _():
            rows = 0.5 * grad.astype(F32).T
            first_ref[0] = rows[:tok]
            first_send[...] = rows[tok:].astype(BF16)

        grad = grad * jnp.where(kind == 2, 0.5, 1.0).astype(BF16)
        acc[...] += nt(grad.T, full_ref[0, 0])
        result[0] = nt(normed_t[...], grad).astype(BF16)

    @pl.when(target == 0)
    def _():
        part(back_other, sent)

    @pl.when(target == 1)
    def _():
        part(back_own, kept)

    @pl.when(step == 5)
    def _():
        gain = gains_ref[0:1, :]
        chunk = min(128, tok)
        gain_ref[...] = jnp.zeros_like(gain_ref)
        gain_ref[1:2, :] = mlp_gain_ref[0:1, :]
        for slot in range(slots):

            def finish(number, _, slot=slot):
                local = pl.ds(pl.multiple_of(number * chunk, chunk), chunk)
                some = pl.ds(pl.multiple_of(slot * tok + number * chunk, chunk), chunk)
                if slot == 0:
                    values = xs[slot][0, local, :].astype(F32)
                else:
                    values = xs[slot][local, :].astype(F32)
                scale = lax.rsqrt(jnp.mean(values * values, axis=1, keepdims=True) + epsilon)
                grad = acc[some, :]
                gain_ref[0:1, :] += jnp.sum(grad * values * scale, axis=0, keepdims=True)
                weighted = grad * gain
                inner = jnp.mean(weighted * values, axis=1, keepdims=True)
                result = (
                    scale * weighted
                    - values * (scale * scale * scale) * inner
                    + grad_ref[some, :]
                )
                if slot == 0:
                    out_ref[0, local, :] = result
                else:
                    send_ref[pl.ds(pl.multiple_of((slot - 1) * tok + number * chunk, chunk), chunk), :] = (
                        result.astype(BF16)
                    )
                return 0

            lax.fori_loop(0, tok // chunk, finish, 0)


def tail(inputs, received, back_other, back_own, full, normed, grad_middle, gains, mlp_gain, place):
    slots, tok, depth = inputs.shape
    wide = depth // 2
    span = slots * tok
    rest = (slots - 1) * tok
    once = pl.Buffered(1)

    def half(s, p):
        return jnp.where(s < 3, 1 - p[1], p[1])

    x_specs = [pl.BlockSpec((1, tok, depth), lambda s, p: (p[0], 0, 0))]
    x_specs += [whole_block((tok, depth))] * (slots - 1)
    grid_spec = pltpu.PrefetchScalarGridSpec(
        num_scalar_prefetch=1,
        grid=(6,),
        in_specs=x_specs
        + [
            pl.BlockSpec((1, wide, span), lambda s, p: (jnp.minimum(s, 2), 0, 0)),
            pl.BlockSpec((1, wide, span), lambda s, p: (jnp.maximum(s - 3, 0), 0, 0)),
            pl.BlockSpec((1, 1, depth, wide), lambda s, p: (half(s, p), s % 3, 0, 0)),
            whole_block((span, depth)),
            pl.BlockSpec((span, depth), lambda s, p: (0, 0), pipeline_mode=once),
            whole_block((8, depth)),
            whole_block((8, depth)),
        ],
        out_specs=[
            pl.BlockSpec((1, tok, depth), lambda s, p: (p[0], 0, 0)),
            whole_block((rest, depth)),
            pl.BlockSpec((1, tok, wide), lambda s, p: (p[0], 0, half(s, p))),
            pl.BlockSpec((rest, wide), lambda s, p: (0, half(s, p))),
            whole_block((8, depth)),
            pl.BlockSpec((1, depth, wide), lambda s, p: (jnp.minimum(s, 2), 0, 0)),
            pl.BlockSpec((1, depth, wide), lambda s, p: (jnp.maximum(s - 3, 0), 0, 0)),
        ],
        scratch_shapes=[pltpu.VMEM((depth, span), BF16), pltpu.VMEM((span, depth), F32)],
    )
    return pl.pallas_call(
        functools.partial(tail_kernel, slots, tok),
        out_shape=[
            jax.ShapeDtypeStruct((slots, tok, depth), F32),
            jax.ShapeDtypeStruct((rest, depth), BF16),
            jax.ShapeDtypeStruct((slots, tok, depth), F32),
            jax.ShapeDtypeStruct((rest, depth), BF16),
            jax.ShapeDtypeStruct((8, depth), F32),
            jax.ShapeDtypeStruct((3, depth, wide), BF16),
            jax.ShapeDtypeStruct((3, depth, wide), BF16),
        ],
        grid_spec=grid_spec,
        compiler_params=parameters(60),
        cost_estimate=pl.CostEstimate(
            flops=12 * span * depth * depth,
            bytes_accessed=24 * span * depth + 12 * depth * depth,
            transcendentals=0,
        ),
        name="tail",
    )(
        place, inputs, *received, back_other, back_own, full, normed, grad_middle, gains, mlp_gain
    )


def land_kernel(place, whole_ref, part_ref, out_ref):
    out_ref[0] = part_ref[...].astype(F32)


def land(whole, part, slot):
    _, tok, depth = whole.shape
    tile = min(256, tok)
    grid_spec = pltpu.PrefetchScalarGridSpec(
        num_scalar_prefetch=1,
        grid=(tok // tile,),
        in_specs=[
            pl.BlockSpec(memory_space=pl.ANY),
            pl.BlockSpec((tile, depth), lambda s, p: (s, 0)),
        ],
        out_specs=pl.BlockSpec((1, tile, depth), lambda s, p: (p[0], s, 0)),
    )
    return pl.pallas_call(
        land_kernel,
        out_shape=jax.ShapeDtypeStruct(whole.shape, F32),
        grid_spec=grid_spec,
        input_output_aliases={1: 0},
        compiler_params=parameters(16),
        cost_estimate=pl.CostEstimate(
            flops=tok * depth, bytes_accessed=6 * tok * depth, transcendentals=0
        ),
        name="land",
    )(slot, whole, part)


MESH = pl.DeviceIdType.MESH


def seats():
    shard = lax.axis_index("fsdp")
    seat = lax.axis_index("seq")
    return (shard // 2, shard % 2, seat // 2, seat % 2)


def meet(line, keys):
    shard = lax.axis_index("fsdp")
    seat = lax.axis_index("seq")
    partners = []
    if "z" in keys:
        partners += [{"fsdp": lax.rem(shard + 2 * jump, 2 * line)} for jump in range(1, line)]
    if "y" in keys:
        partners.append({"fsdp": shard + 1 - 2 * (shard % 2)})
    if "x" in keys:
        partners.append({"seq": lax.rem(seat + 2, 4)})
    if "diagonal" in keys:
        partners.append({"seq": 3 - seat})
    if "core" in keys:
        partners.append({"seq": seat + 1 - 2 * (seat % 2)})
    barrier = pltpu.get_barrier_semaphore()
    for partner in partners:
        pl.semaphore_signal(barrier, inc=1, device_id=partner, device_id_type=MESH)
    pl.semaphore_wait(barrier, len(partners))


def send(source, target, sems, number, partner):
    return pltpu.make_async_remote_copy(
        src_ref=source,
        dst_ref=target,
        send_sem=sems.at[0, number],
        recv_sem=sems.at[1, number],
        device_id=partner,
        device_id_type=MESH,
    )


def to_core_partner():
    seat = lax.axis_index("seq")
    return {"seq": seat + 1 - 2 * (seat % 2)}


def to_x_partner():
    return {"seq": lax.rem(lax.axis_index("seq") + 2, 4)}


def to_y_partner():
    shard = lax.axis_index("fsdp")
    return {"fsdp": shard + 1 - 2 * (shard % 2)}


def to_z_partner(line, jump):
    return {"fsdp": lax.rem(lax.axis_index("fsdp") + 2 * jump, 2 * line)}


class Gather:
    def __init__(self, line, shard, own, other, sems, share=0, columns=None):
        self.line, self.shard, self.own, self.other = line, shard, own, other
        self.sems = sems
        z, y, x, core = seats()
        self.z, self.y, self.share = z, y, share
        rows, width = own.shape[2:]
        first, size = columns or (0, width)
        self.columns = pl.ds(first, size)
        if shard.shape[1] == width:
            self.source = self.columns
        else:
            self.source = pl.ds(pl.multiple_of(core * width + first, 128), size)
        if share:
            step = math.gcd(share, rows)
            self.rows = pl.ds(pl.multiple_of(x * share, step), rows - share)
            self.given = pl.ds(pl.multiple_of(x * (rows - share), step), share)
            self.taken = pl.ds(pl.multiple_of((1 - x) * (rows - share), step), share)
        else:
            self.rows = slice(None)

    def here(self):
        return pltpu.make_async_copy(
            self.shard.at[self.rows, self.source],
            self.own.at[self.z, self.y, self.rows, self.columns],
            self.sems.at[0, self.line + 3],
        )

    def along_z(self):
        return [
            send(
                self.shard.at[self.rows, self.source],
                self.own.at[self.z, self.y, self.rows, self.columns],
                self.sems,
                jump - 1,
                to_z_partner(self.line, jump),
            )
            for jump in range(1, self.line)
        ]

    def along_y(self):
        part = self.own.at[:, self.y, self.rows, self.columns]
        return send(part, part, self.sems, self.line - 1, to_y_partner())

    def along_x(self):
        part = self.own.at[:, :, self.given, self.columns]
        return send(part, part, self.sems, self.line, to_x_partner())

    def to_core(self, late):
        if self.share:
            at = (slice(None), slice(None), self.taken if late else self.rows, self.columns)
        else:
            at = (slice(None), 1 - self.y if late else self.y, slice(None), self.columns)
        return send(
            self.own.at[at],
            self.other.at[at],
            self.sems,
            self.line + 1 + late,
            to_core_partner(),
        )

    def start_z(self):
        self.here().start()
        for copy in self.along_z():
            copy.start()

    def wait_z(self):
        self.here().wait()
        for copy in self.along_z():
            copy.wait()

    def wait_core(self):
        self.to_core(0).wait()
        self.to_core(1).wait()


def gather_sems(line):
    return pltpu.SemaphoreType.DMA((2, line + 4))


def front_kernel(line, tok, *refs):
    (
        inputs,
        firsts,
        grads,
        q_shard,
        k_shard,
        v_shard,
        o_shard,
        d_shard,
        gains_shard,
        cos_ref,
        sin_ref,
        x_received,
        f_received,
        g_received,
        heads_own,
        heads_received,
        normed_ref,
        full_ref,
        gains_ref,
        o_own,
        o_other,
        d_own,
        xs,
        fs,
        q_own,
        q_other,
        k_own,
        k_other,
        v_own,
        v_other,
        outgoing,
        all_gains,
        q_sems,
        k_sems,
        v_sems,
        w_sems,
        o_sems,
        d_sems,
        gain_sems,
        swap_sems,
        head_sems,
        local_sems,
    ) = refs
    step = pl.program_id(0)
    _, _, side, core = seats()
    wide = outgoing.shape[1]
    depth = 2 * wide
    gathers = [
        Gather(line, q_shard, q_own, q_other, q_sems),
        Gather(line, k_shard, k_own, k_other, k_sems),
        Gather(line, v_shard, v_own, v_other, v_sems, columns=(0, wide // 2)),
        Gather(line, v_shard, v_own, v_other, w_sems, columns=(wide // 2, wide // 2)),
    ]
    query, key, value, value_more = gathers
    gains = Gather(line, gains_shard, all_gains, all_gains, gain_sems)
    out = Gather(line, o_shard, o_own, o_other, o_sems)
    down = Gather(line, d_shard, d_own, d_own, d_sems, d_own.shape[2] // 2)
    swap_x = send(inputs.at[1 - side], x_received, swap_sems, 0, to_x_partner())
    swap_f = send(firsts.at[1 - side], f_received, swap_sems, 1, to_x_partner())
    early = pl.ds(0, tok // 2)
    swap_g = send(
        grads.at[1 - side, early], g_received.at[early], swap_sems, 2, to_x_partner()
    )
    load_x = pltpu.make_async_copy(inputs.at[side], xs.at[pl.ds(0, tok), :], local_sems.at[0])
    load_f = pltpu.make_async_copy(firsts.at[side], fs.at[pl.ds(0, tok), :], local_sems.at[1])
    more_x = pltpu.make_async_copy(x_received, xs.at[pl.ds(tok, tok), :], local_sems.at[2])
    more_f = pltpu.make_async_copy(f_received, fs.at[pl.ds(tok, tok), :], local_sems.at[3])

    def weight(halves, columns):
        return halves[:, :, :, columns].reshape(depth, wide)

    def heads(number):
        return send(
            outgoing.at[number], heads_received.at[number], head_sems, number, to_core_partner()
        )

    saves = []
    for number, (mine, others) in enumerate(((q_own, q_other), (k_own, k_other), (v_own, v_other))):
        for which, ref in ((0, mine), (1, others)):
            half = core if which == 0 else 1 - core
            saves.append(
                pltpu.make_async_copy(
                    ref.at[:, :, :, pl.ds(0, wide)],
                    full_ref.at[half, number],
                    local_sems.at[4 + 2 * number + which],
                )
            )

    @pl.when(step == 0)
    def _():
        meet(line, ("z", "y", "x", "core"))
        swap_x.start()
        load_x.start()
        load_f.start()
        gains.start_z()
        query.start_z()
        gains.wait_z()
        gains.along_y().start()
        query.wait_z()
        query.along_y().start()
        query.to_core(0).start()
        key.start_z()
        key.wait_z()
        key.along_y().start()
        key.to_core(0).start()
        value.start_z()
        swap_x.wait()
        more_x.start()
        swap_f.start()
        gains.along_y().wait()
        query.along_y().wait()
        query.to_core(1).start()
        for number in range(2 * line):
            columns = slice(number * 128, (number + 1) * 128)
            gains_ref[:, columns] = all_gains[number // 2, number % 2]
        gain = gains_ref[0:1, :]
        chunk = min(256, 2 * tok)
        load_x.wait()
        more_x.wait()

        def norm(number, _):
            at = pl.ds(pl.multiple_of(number * chunk, chunk), chunk)
            values = xs[at, :].astype(F32)
            scale = lax.rsqrt(jnp.mean(values * values, axis=1, keepdims=True) + epsilon)
            normed_ref[at, :] = (values * scale * gain).astype(BF16)
            return 0

        lax.fori_loop(0, 2 * tok // chunk, norm, 0)
        value.wait_z()
        value.along_y().start()
        value.to_core(0).start()
        value_more.start_z()

    @pl.when(step == 1)
    def _():
        key.along_y().wait()
        key.to_core(1).start()
        value_more.wait_z()
        value_more.along_y().start()
        value_more.to_core(0).start()
        out.start_z()

    @pl.when(step == 2)
    def _():
        swap_f.wait()
        more_f.start()
        swap_g.start()
        value.along_y().wait()
        value.to_core(1).start()
        value_more.along_y().wait()
        value_more.to_core(1).start()
        out.wait_z()
        out.along_y().start()
        out.to_core(0).start()
        down.start_z()
        load_f.wait()
        more_f.wait()

    @pl.when(step == 3)
    def _():
        query.wait_core()
        key.wait_core()
        for save in saves[:4]:
            save.start()

    @pl.when(step == 5)
    def _():
        value.wait_core()
        value_more.wait_core()
        for save in saves[4:]:
            save.start()
        out.along_y().wait()
        out.to_core(1).start()

    def project_one(halves, kind, mine):
        raw = nt(weight(halves, slice(0, wide)).T, normed_ref[...])
        if kind < 2:
            parts = raw.reshape(wide // HEAD_DIM, 2, HALF, raw.shape[1])
            first, second = parts[:, 0], parts[:, 1]
            cosine, sine = (
                jnp.concatenate([ref[:, block_of(1, slot, tok)] for slot in range(2)], axis=1)[None]
                for ref in (cos_ref, sin_ref)
            )
            turned = jnp.stack(
                [first * cosine - second * sine, first * sine + second * cosine], axis=1
            )
            result = turned.reshape(raw.shape).astype(BF16)
        else:
            half = core if mine else 1 - core
            first = fs[:, pl.ds(pl.multiple_of(half * wide, wide), wide)]
            result = (0.5 * raw + 0.5 * first.astype(F32).T).astype(BF16)
        if mine:
            heads_own[0] = result
        else:
            outgoing[kind] = result
            heads(kind).start()

    for number, (halves, kind, mine) in enumerate(
        (
            (q_own, 0, True),
            (k_own, 1, True),
            (v_own, 2, True),
            (q_other, 0, False),
            (k_other, 1, False),
            (v_other, 2, False),
        )
    ):

        @pl.when(step == number)
        def _(halves=halves, kind=kind, mine=mine):
            project_one(halves, kind, mine)

    @pl.when(step == 5)
    def _():
        for number in range(3):
            heads(number).wait()
        for save in saves:
            save.wait()
        out.wait_core()
        down.wait_z()
        swap_g.wait()


def front(inputs, firsts, grads, q, k, v, o, d, gains, cosine, sine, line):
    slots, tok, depth = inputs.shape
    span = slots * tok
    wide = depth // 2
    rows, down_rows = q.shape[0], d.shape[0]
    anywhere = pl.BlockSpec(memory_space=pl.ANY)
    weights = lambda columns: pltpu.VMEM((line, 2, rows, columns), BF16)
    return pl.pallas_call(
        functools.partial(front_kernel, line, tok),
        grid=(6,),
        in_specs=[anywhere] * 9 + [whole_block(cosine.shape)] * 2,
        out_specs=[
            anywhere,
            anywhere,
            anywhere,
            pl.BlockSpec((1, wide, span), lambda s: (jnp.minimum(s, 2), 0, 0)),
            anywhere,
            whole_block((span, depth)),
            anywhere,
            whole_block((8, depth)),
            anywhere,
            anywhere,
            anywhere,
        ],
        out_shape=[
            jax.ShapeDtypeStruct((tok, depth), BF16),
            jax.ShapeDtypeStruct((tok, depth), BF16),
            jax.ShapeDtypeStruct((tok, depth), BF16),
            jax.ShapeDtypeStruct((3, wide, span), BF16),
            jax.ShapeDtypeStruct((3, wide, span), BF16),
            jax.ShapeDtypeStruct((span, depth), BF16),
            jax.ShapeDtypeStruct((2, 3, line, 2, rows, wide), BF16),
            jax.ShapeDtypeStruct((8, depth), F32),
            jax.ShapeDtypeStruct((line, 2, rows, wide), BF16),
            jax.ShapeDtypeStruct((line, 2, rows, wide), BF16),
            jax.ShapeDtypeStruct((line, 2, down_rows, wide), BF16),
        ],
        scratch_shapes=[
            pltpu.VMEM((span, depth), BF16),
            pltpu.VMEM((span, depth), BF16),
            weights(wide),
            weights(wide),
            weights(wide),
            weights(wide),
            weights(wide),
            weights(wide),
            pltpu.VMEM((3, wide, span), BF16),
            pltpu.VMEM((line, 2, 8, 128), F32),
        ]
        + [gather_sems(line)] * 7
        + [
            pltpu.SemaphoreType.DMA((2, 3)),
            pltpu.SemaphoreType.DMA((2, 3)),
            pltpu.SemaphoreType.DMA((10,)),
        ],
        compiler_params=pltpu.CompilerParams(
            dimension_semantics=("arbitrary",),
            vmem_limit_bytes=63 * MIB,
            collective_id=1,
            has_side_effects=True,
        ),
        cost_estimate=pl.CostEstimate(
            flops=6 * span * depth * depth,
            bytes_accessed=2 * (8 * span * depth + 6 * depth * depth),
            transcendentals=0,
        ),
        name="front",
    )(inputs, firsts, grads, q, k, v, o, d, gains, cosine, sine)


def block_of(source, slot, tok):
    _, _, side, core = seats()
    rank = 1 - core if source == 0 else core
    group = lax.rem(side + slot, 2)
    return pl.ds(pl.multiple_of((group * 2 + rank) * tok, tok), tok)


def attend_carry_kernel(line, tok, tile_k, *refs):
    (
        received,
        own,
        inputs,
        x_received,
        gains_ref,
        o_own,
        o_other,
        grad_in,
        _,
        d_in,
        g_shard,
        u_shard,
        mix_received,
        mix_own,
        lse_ref,
        middle_ref,
        normed_ref,
        full_ref,
        att_other,
        grad_received,
        d_own,
        d_other,
        g_own,
        g_other,
        u_own,
        u_other,
        qz,
        kn,
        vt,
        ot,
        outgoing,
        att_mine,
        att_theirs,
        xs,
        d_sems,
        g_sems,
        u_sems,
        v_sems,
        swap_sems,
        att_sems,
        local_sems,
    ) = refs
    step = pl.program_id(0)
    pairs = pl.num_programs(0)
    _, _, side, core = seats()
    rows, columns = g_own.shape[2:]
    first = columns // 256 * 128
    down = Gather(line, d_in, d_own, d_other, d_sems, d_own.shape[2] // 2)
    gate = Gather(line, g_shard, g_own, g_other, g_sems, rows * 3 // 8)
    up = Gather(line, u_shard, u_own, u_other, u_sems, columns=(0, first))
    up_more = Gather(line, u_shard, u_own, u_other, v_sems, columns=(first, columns - first))
    late = pl.ds(tok // 2, tok - tok // 2)
    swap = send(grad_in.at[1 - side, late], grad_received.at[late], swap_sems, 0, to_x_partner())
    depth = xs.shape[1]
    wide = depth // 2
    mine = pl.ds(pl.multiple_of(core * wide, wide), wide)
    others = pl.ds(pl.multiple_of((1 - core) * wide, wide), wide)
    loads = [
        pltpu.make_async_copy(source, place, local_sems.at[number])
        for number, (source, place) in enumerate(
            (
                (inputs.at[side], xs.at[pl.ds(0, tok), :]),
                (x_received, xs.at[pl.ds(tok, tok), :]),
                (o_own, full_ref.at[:, mine]),
                (o_other, full_ref.at[:, others]),
            )
        )
    ]
    save_att = pltpu.make_async_copy(att_theirs, att_other, local_sems.at[4])
    pieces = (received, own)

    def hand_over(number):
        rows = pl.ds(number * PAIR, PAIR)
        return send(
            outgoing.at[rows, :], att_theirs.at[rows, :], att_sems, number, to_core_partner()
        )

    @pl.when(step == 0)
    def _():
        meet(line, ("z", "y", "x", "core"))
        down.along_y().start()
        gate.start_z()
        swap.start()

    @pl.when(step == 2)
    def _():
        down.along_y().wait()
        down.along_x().start()
        down.to_core(0).start()
        gate.wait_z()
        gate.along_y().start()
        up.start_z()
        for load in loads:
            load.start()

    for source in range(2):
        for slot in range(2):
            cols = block_of(source, slot, tok)
            take = slice(slot * tok, (slot + 1) * tok)
            query = pieces[source][0, :, take] * jnp.asarray(HEAD_DIM**-0.5, BF16)
            for head in range(2):
                qz[head, :, cols] = head_rows(query, head)
            kn[cols, :] = pieces[source][1, :, take].T
            vt[:, cols] = pieces[source][2, :, take]
    attend_body(4 * tok, tile_k, qz, kn, vt, ot, lse_ref)
    for slot in range(2):
        take = slice(slot * tok, (slot + 1) * tok)
        theirs = ot[:, block_of(0, slot, tok)]
        mix_received[:, take] = theirs
        for number in range(4):

            @pl.when(step == number)
            def _(number=number, theirs=theirs, take=take):
                outgoing[number * PAIR : (number + 1) * PAIR, take] = theirs

        ours = ot[:, block_of(1, slot, tok)]
        mix_own[:, take] = ours
        for number in range(4):

            @pl.when(step == number)
            def _(number=number, ours=ours, take=take):
                att_mine[number * PAIR : (number + 1) * PAIR, take] = ours

    for number in range(4):

        @pl.when(step == number)
        def _(number=number):
            hand_over(number).start()

    @pl.when(step == pairs - 1)
    def _():
        up.wait_z()
        up.along_y().start()
        up.to_core(0).start()
        up_more.start_z()
        gate.along_y().wait()
        gate.to_core(0).start()
        down.along_x().wait()
        gate.along_x().start()
        down.to_core(1).start()
        up_more.wait_z()
        up_more.along_y().start()
        up_more.to_core(0).start()
        for number in range(4):
            hand_over(number).wait()
        save_att.start()
        for load in loads:
            load.wait()
        for slot in range(2):
            take = slice(slot * tok, (slot + 1) * tok)
            total = dot(att_mine[:, take].T, full_ref[mine, :])
            total = total + dot(att_theirs[:, take].T, full_ref[others, :])
            middle = xs[take, :].astype(F32) + total
            middle_ref[take, :] = middle
            scale = lax.rsqrt(jnp.mean(middle * middle, axis=1, keepdims=True) + epsilon)
            normed_ref[take, :] = (middle * scale * gains_ref[1:2, :]).astype(BF16)
        up.along_y().wait()
        up.to_core(1).start()
        up_more.along_y().wait()
        up_more.to_core(1).start()
        gate.along_x().wait()
        gate.to_core(1).start()
        swap.wait()
        for gather in (down, up, up_more, gate):
            gather.wait_core()
        save_att.wait()


def attend_carry(
    received, own, inputs, x_received, gains, o_own, o_other, grads, g_received, d_own, gate, up, line
):
    _, width, span = own.shape
    tok = span // 2
    length = 2 * span
    pairs = width // PAIR
    rows, down_rows = gate.shape[0], d_own.shape[2]
    depth = grads.shape[2]
    anywhere = pl.BlockSpec(memory_space=pl.ANY)
    triple = pl.BlockSpec((3, PAIR, span), lambda p: (0, p, 0))
    single = pl.BlockSpec((PAIR, span), lambda p: (p, 0))
    whole_gate = jax.ShapeDtypeStruct((line, 2, rows, gate.shape[1] // 2), BF16)
    whole_down = jax.ShapeDtypeStruct((line, 2, down_rows, d_own.shape[3]), BF16)
    area = pairs * 2 * length * length // 2
    return pl.pallas_call(
        functools.partial(attend_carry_kernel, line, tok, min(256, length)),
        grid=(pairs,),
        in_specs=[triple, triple]
        + [anywhere] * 2
        + [whole_block((8, depth))]
        + [anywhere] * 7,
        out_specs=[single, single, pl.BlockSpec((1, 8, length), lambda p: (p, 0, 0))]
        + [
            pl.BlockSpec(shape, lambda p: (0, 0), pipeline_mode=pl.Buffered(1))
            for shape in ((span, depth), (span, depth), (depth, depth))
        ]
        + [anywhere] * 8,
        out_shape=[
            jax.ShapeDtypeStruct((width, span), BF16),
            jax.ShapeDtypeStruct((width, span), BF16),
            jax.ShapeDtypeStruct((pairs, 8, length), F32),
            jax.ShapeDtypeStruct((span, depth), F32),
            jax.ShapeDtypeStruct((span, depth), BF16),
            jax.ShapeDtypeStruct((depth, depth), BF16),
            jax.ShapeDtypeStruct((width, span), BF16),
            jax.ShapeDtypeStruct((tok, depth), BF16),
            whole_down,
            whole_down,
            whole_gate,
            whole_gate,
            whole_gate,
            whole_gate,
        ],
        scratch_shapes=[
            pltpu.VMEM((2, PAIR, length), BF16),
            pltpu.VMEM((length, PAIR), BF16),
            pltpu.VMEM((PAIR, length), BF16),
            pltpu.VMEM((PAIR, length), BF16),
            pltpu.VMEM((width, span), BF16),
            pltpu.VMEM((width, span), BF16),
            pltpu.VMEM((width, span), BF16),
            pltpu.VMEM((span, depth), BF16),
        ]
        + [gather_sems(line)] * 4
        + [
            pltpu.SemaphoreType.DMA((2, 1)),
            pltpu.SemaphoreType.DMA((2, 4)),
            pltpu.SemaphoreType.DMA((5,)),
        ],
        input_output_aliases={8: 7, 9: 8},
        compiler_params=pltpu.CompilerParams(
            dimension_semantics=("arbitrary",),
            vmem_limit_bytes=63 * MIB,
            collective_id=2,
            has_side_effects=True,
        ),
        cost_estimate=pl.CostEstimate(
            flops=area * 1024, bytes_accessed=8 * width * length, transcendentals=area
        ),
        name="attend_carry",
    )(
        received,
        own,
        inputs,
        x_received,
        gains,
        o_own,
        o_other,
        grads,
        g_received,
        d_own,
        gate,
        up,
    )


LATE = 2


def mlp_carry_kernel(line, tok, blocks, *refs):
    (
        grads,
        grads_received,
        middle_ref,
        normed_ref,
        gains_ref,
        g_own,
        g_other,
        u_own,
        u_other,
        d_own_own,
        d_own_other,
        d_other_own,
        d_other_other,
        out_ref,
        send_ref,
        grad_ref,
        low_ref,
        gain_ref,
        gu_ref,
        d_ref,
        gu_y,
        gu_late,
        og,
        normed_t,
        acc,
        back,
        gu_kept,
        d_kept,
        gu_sent,
        d_sent,
        gu_landed,
        d_landed,
        gu_outgoing,
        down_full,
        local_sems,
        gu_sends,
        gu_recvs,
        d_sends,
        d_recvs,
        y_sems,
    ) = refs
    step = pl.program_id(0)
    _, y, side, core = seats()
    depth = og.shape[1]
    wide = depth // 2
    strip = 128
    rows = gu_kept.shape[4]
    mine = pl.ds(pl.multiple_of(core * wide, wide), wide)
    others = pl.ds(pl.multiple_of((1 - core) * wide, wide), wide)

    def core_copies(number):
        slot = lax.rem(number, 2)
        return [
            pltpu.make_async_remote_copy(
                src_ref=source.at[slot],
                dst_ref=target.at[number],
                send_sem=sends.at[slot],
                recv_sem=recvs.at[number],
                device_id=to_core_partner(),
                device_id_type=MESH,
            )
            for source, target, sends, recvs in (
                (gu_sent, gu_landed, gu_sends, gu_recvs),
                (d_sent, d_landed, d_sends, d_recvs),
            )
        ]

    def y_copy(number):
        return send(gu_outgoing.at[number], gu_y.at[number], y_sems, number, to_y_partner())

    def leave(late):
        return pltpu.make_async_copy(
            gu_outgoing.at[blocks - LATE + late], gu_late.at[late], local_sems.at[2 + late]
        )

    @pl.when(step == 0)
    def _():
        meet(line, ("y", "core"))
        loads = [
            pltpu.make_async_copy(grads.at[side], og.at[pl.ds(0, tok), :], local_sems.at[0]),
            pltpu.make_async_copy(grads_received, og.at[pl.ds(tok, tok), :], local_sems.at[1]),
        ]
        for load in loads:
            load.start()
        normed_t[...] = normed_ref[...].T
        acc[...] = jnp.zeros_like(acc)
        back[...] = jnp.zeros_like(back)
        for load in loads:
            load.wait()

    @pl.when(step < blocks)
    def _():
        slot = lax.rem(step, 2)
        gate_w = jnp.concatenate([g_own[...], g_other[...]], axis=1)
        up_w = jnp.concatenate([u_own[...], u_other[...]], axis=1)
        for number, pair in enumerate(
            ((d_own_own, d_own_other), (d_other_own, d_other_other))
        ):
            at = pl.ds(number * strip, strip)
            down_full[at, mine] = pair[0][...]
            down_full[at, others] = pair[1][...]
        down_w = down_full[...]
        both_w = jnp.concatenate([gate_w, up_w], axis=1)
        span = og.shape[0]
        size = span // 2

        def products(at):
            both = dot(normed_ref[at, :], both_w)
            return (both[:, : 2 * strip], both[:, 2 * strip :], nt(og[at, :], down_w))

        def bend(gate, up, grad_active):
            sigma = jax.nn.sigmoid(gate)
            silu = gate * sigma
            turned = grad_active * up * sigma * (1.0 + gate * (1.0 - sigma))
            grad_both = jnp.concatenate([turned.astype(BF16), (grad_active * silu).astype(BF16)], axis=1)
            return ((silu * up).astype(BF16), grad_both)

        def spread(at, active, grad_both):
            acc[at, :] += dot(active, down_w)
            back[at, :] += nt(grad_both, both_w)

        pieces = [slice(n * size, (n + 1) * size) for n in range(2)]
        bent = []
        ahead = products(pieces[0])
        for number, at in enumerate(pieces):
            now = ahead
            if number + 1 < len(pieces):
                ahead = products(pieces[number + 1])
            bent.append(bend(*now))
            if number:
                spread(pieces[number - 1], *bent[number - 1])
        spread(pieces[-1], *bent[-1])
        active = jnp.concatenate([one for one, _ in bent], axis=0)
        grad_both = jnp.concatenate([one for _, one in bent], axis=0)

        @pl.when(step >= 2)
        def _():
            for copy in core_copies(step - 2):
                copy.wait_send()

        shaped = dot(normed_t[...], grad_both).astype(BF16).reshape(line, 2, rows, 4 * strip)
        for number in range(2):
            base = 2 * number * strip
            gu_kept[slot, number] = shaped[..., base : base + strip]
            gu_sent[slot, number] = shaped[..., base + strip : base + 2 * strip]
        active_t = active.T
        kept = dot(active_t, og[:, mine]).astype(BF16)
        d_kept[slot, core] = kept[:strip]
        d_kept[slot, 1 - core] = kept[strip:]
        sent = dot(active_t, og[:, others]).astype(BF16)
        d_sent[slot, core] = sent[:strip]
        d_sent[slot, 1 - core] = sent[strip:]
        for copy in core_copies(step):
            copy.start()

    @pl.when(step > 0)
    def _():
        number = step - 1
        slot = lax.rem(number, 2)
        for copy in core_copies(number):
            copy.wait_recv()
        for which in range(2):
            theirs = gu_kept[slot, which, :, 1 - y].astype(F32)
            theirs = theirs + gu_landed[number, which, :, 1 - y].astype(F32)
            gu_outgoing[number, which] = theirs.astype(BF16)
            ours = gu_kept[slot, which, :, y].astype(F32)
            ours = ours + gu_landed[number, which, :, y].astype(F32)
            gu_ref[0, which] = ours.astype(BF16)
        @pl.when(number < blocks - LATE)
        def _():
            y_copy(number).start()

        for late in range(LATE):

            @pl.when(number == blocks - LATE + late)
            def _(late=late):
                leave(late).start()

        d_ref[...] = (d_kept[slot].astype(F32) + d_landed[number].astype(F32)).astype(BF16)

    @pl.when(step == blocks)
    def _():
        gain = gains_ref[1:2, :]
        chunk = min(128, tok)
        gain_ref[...] = jnp.zeros_like(gain_ref)
        for slot in range(2):

            def finish(number, _, slot=slot):
                local = pl.ds(pl.multiple_of(number * chunk, chunk), chunk)
                some = pl.ds(pl.multiple_of(slot * tok + number * chunk, chunk), chunk)
                middle = middle_ref[some, :]
                scale = lax.rsqrt(jnp.mean(middle * middle, axis=1, keepdims=True) + epsilon)
                result = middle + acc[some, :]
                if slot == 0:
                    out_ref[0, local, :] = result
                else:
                    send_ref[local, :] = result.astype(BF16)
                grad = back[some, :]
                gain_ref[0:1, :] += jnp.sum(grad * middle * scale, axis=0, keepdims=True)
                weighted = grad * gain
                inner = jnp.mean(weighted * middle, axis=1, keepdims=True)
                grad_middle = (
                    scale * weighted
                    - middle * (scale * scale * scale) * inner
                    + og[some, :].astype(F32)
                )
                grad_ref[some, :] = grad_middle
                low_ref[some, :] = grad_middle.astype(BF16)
                return 0

            lax.fori_loop(0, tok // chunk, finish, 0)
        for number in (blocks - 2, blocks - 1):
            for copy in core_copies(number):
                copy.wait_send()
        for late in range(LATE):
            leave(late).wait()
        for number in range(blocks - LATE):
            y_copy(number).wait()


def mlp_carry(grads, grads_received, middle, normed, gains, gate, up, down, line):
    slots, tok, depth = grads.shape
    half_width = gate[0].shape[1]
    wide = depth // 2
    span = slots * tok
    blocks = half_width // 128
    rows = depth // (2 * line)
    once = pl.Buffered(1)
    anywhere = pl.BlockSpec(memory_space=pl.ANY)

    def now(s):
        return jnp.minimum(s, blocks - 1)

    def done(s):
        return jnp.maximum(s - 1, 0)

    def core():
        return lax.axis_index("seq") % 2

    column = pl.BlockSpec((depth, 128), lambda s: (0, now(s)))
    own_rows = pl.BlockSpec((128, wide), lambda s: (core() * blocks + now(s), 0))
    other_rows = pl.BlockSpec((128, wide), lambda s: ((1 - core()) * blocks + now(s), 0))
    full = pl.BlockSpec((span, depth), lambda s: (0, 0), pipeline_mode=once)
    return pl.pallas_call(
        functools.partial(mlp_carry_kernel, line, tok, blocks),
        grid=(blocks + 1,),
        in_specs=[anywhere, anywhere, full, full, whole_block((8, depth))]
        + [column] * 4
        + [own_rows, own_rows, other_rows, other_rows],
        out_specs=[
            pl.BlockSpec(
                (1, tok, depth), lambda s: (lax.axis_index("seq") // 2, 0, 0), pipeline_mode=once
            ),
            pl.BlockSpec((tok, depth), lambda s: (0, 0), pipeline_mode=once),
            full,
            full,
            whole_block((8, depth)),
            pl.BlockSpec((1, 2, line, rows, 128), lambda s: (done(s), 0, 0, 0, 0)),
            pl.BlockSpec((2, 128, wide), lambda s: (0, done(s), 0)),
            anywhere,
            anywhere,
        ],
        out_shape=[
            jax.ShapeDtypeStruct((slots, tok, depth), F32),
            jax.ShapeDtypeStruct((tok, depth), BF16),
            jax.ShapeDtypeStruct((span, depth), F32),
            jax.ShapeDtypeStruct((span, depth), BF16),
            jax.ShapeDtypeStruct((8, depth), F32),
            jax.ShapeDtypeStruct((blocks, 2, line, rows, 128), BF16),
            jax.ShapeDtypeStruct((2, half_width, wide), BF16),
            jax.ShapeDtypeStruct((blocks - LATE, 2, line, rows, 128), BF16),
            jax.ShapeDtypeStruct((LATE, 2, line, rows, 128), BF16),
        ],
        scratch_shapes=[
            pltpu.VMEM((span, depth), BF16),
            pltpu.VMEM((depth, span), BF16),
            pltpu.VMEM((span, depth), F32),
            pltpu.VMEM((span, depth), F32),
            pltpu.VMEM((2, 2, line, 2, rows, 128), BF16),
            pltpu.VMEM((2, 2, 128, wide), BF16),
            pltpu.VMEM((2, 2, line, 2, rows, 128), BF16),
            pltpu.VMEM((2, 2, 128, wide), BF16),
            pltpu.VMEM((blocks, 2, line, 2, rows, 128), BF16),
            pltpu.VMEM((blocks, 2, 128, wide), BF16),
            pltpu.VMEM((blocks, 2, line, rows, 128), BF16),
            pltpu.VMEM((256, depth), BF16),
            pltpu.SemaphoreType.DMA((2 + LATE,)),
            pltpu.SemaphoreType.DMA((2,)),
            pltpu.SemaphoreType.DMA((blocks,)),
            pltpu.SemaphoreType.DMA((2,)),
            pltpu.SemaphoreType.DMA((blocks,)),
            pltpu.SemaphoreType.DMA((2, blocks - LATE)),
        ],
        compiler_params=pltpu.CompilerParams(
            dimension_semantics=("arbitrary",),
            vmem_limit_bytes=63 * MIB,
            collective_id=3,
            has_side_effects=True,
        ),
        cost_estimate=pl.CostEstimate(
            flops=16 * span * depth * 2 * half_width,
            bytes_accessed=24 * depth * half_width + 20 * span * depth,
            transcendentals=2 * span * half_width,
        ),
        name="mlp_carry",
    )(
        grads,
        grads_received,
        middle,
        normed,
        gains,
        *gate,
        *up,
        down[0],
        down[1],
        down[0],
        down[1],
    )


def early_rows(rows):
    return pl.ds(0, rows // 8)


def late_rows(rows):
    return pl.ds(rows // 8, rows - rows // 8)


def grad_attended_carry_kernel(
    line,
    low_ref,
    full_ref,
    att_other,
    att_own,
    outputs_sent,
    ga_own,
    ga_received,
    o_ref,
    o_landed,
    outputs_received,
    outgoing,
    o_sent,
    sems,
):
    step = pl.program_id(0)
    _, _, _, core = seats()
    wide = att_own.shape[0]
    mine = pl.ds(pl.multiple_of(core * wide, wide), wide)
    others = pl.ds(pl.multiple_of((1 - core) * wide, wide), wide)
    heads = send(outgoing, ga_received, sems, 0, to_core_partner())
    early = early_rows(outputs_sent.shape[0])
    swap = send(
        outputs_sent.at[early], outputs_received.at[early], sems, 3, to_x_partner()
    )

    def sums(number):
        half = 1 - core if number == 0 else core
        at = pl.ds(pl.multiple_of(half * wide, wide), wide)
        return send(o_sent.at[number], o_landed.at[at, :], sems, 1 + number, to_core_partner())

    @pl.when(step == 0)
    def _():
        meet(line, ("x", "core"))
        swap.start()
        outgoing[...] = nt(full_ref[...], low_ref[...]).astype(BF16)
        heads.start()

    @pl.when(step == 1)
    def _():
        ga_own[...] = nt(full_ref[...], low_ref[...]).astype(BF16)

    for number, att in enumerate((att_other, att_own)):

        @pl.when(step == number)
        def _(number=number, att=att):
            o_sent[number] = dot(att[...], low_ref[:, others]).astype(BF16)
            sums(number).start()
            o_ref[...] = dot(att[...], low_ref[:, mine]).astype(BF16)

    @pl.when(step == 1)
    def _():
        swap.wait()
        heads.wait()
        for number in range(2):
            sums(number).wait()


def grad_attended_carry(low, full, att_other, att_own, outputs_sent, line):
    span, depth = low.shape
    wide = depth // 2

    def half(s):
        core = lax.axis_index("seq") % 2
        return jnp.where(s == 0, 1 - core, core)

    anywhere = pl.BlockSpec(memory_space=pl.ANY)
    return pl.pallas_call(
        functools.partial(grad_attended_carry_kernel, line),
        grid=(2,),
        in_specs=[
            whole_block((span, depth)),
            pl.BlockSpec((wide, depth), lambda s: (half(s), 0)),
            whole_block((wide, span)),
            whole_block((wide, span)),
            anywhere,
        ],
        out_specs=[
            whole_block((wide, span)),
            anywhere,
            pl.BlockSpec((wide, wide), lambda s: (half(s), 0)),
            anywhere,
            anywhere,
        ],
        out_shape=[
            jax.ShapeDtypeStruct((wide, span), BF16),
            jax.ShapeDtypeStruct((wide, span), BF16),
            jax.ShapeDtypeStruct((depth, wide), BF16),
            jax.ShapeDtypeStruct((depth, wide), BF16),
            jax.ShapeDtypeStruct(outputs_sent.shape, BF16),
        ],
        scratch_shapes=[
            pltpu.VMEM((wide, span), BF16),
            pltpu.VMEM((2, wide, wide), BF16),
            pltpu.SemaphoreType.DMA((2, 4)),
        ],
        compiler_params=pltpu.CompilerParams(
            dimension_semantics=("arbitrary",),
            vmem_limit_bytes=48 * MIB,
            collective_id=4,
            has_side_effects=True,
        ),
        cost_estimate=pl.CostEstimate(
            flops=4 * span * depth * depth,
            bytes_accessed=6 * span * depth + 4 * depth * depth,
            transcendentals=0,
        ),
        name="grad_attended_carry",
    )(low, full, att_other, att_own, outputs_sent)


def attend_back_carry_kernel(line, tok, tile_q, tile_k, *refs):
    (
        received,
        own,
        mix_received,
        mix_own,
        grad_received,
        grad_own,
        lse_ref,
        cos_ref,
        sin_ref,
        outputs_sent,
        _,
        gu_in,
        gu_y,
        gu_late,
        d_in,
        o_in,
        o_landed,
        back_own,
        back_other,
        outputs_received,
        gu_mine,
        gu_z,
        d_kept,
        d_y,
        o_kept,
        o_y,
        first_received,
    ) = refs[:27]
    (
        qz,
        gz,
        qn,
        gn,
        kn,
        vn,
        kt,
        inner,
        dq,
        dk,
        dv,
        outgoing,
        gu_a,
        gu_b,
        o_a,
        o_b,
        o_x,
        d_a,
        d_x,
        first_out,
        local_sems,
        back_sems,
        z_sems,
        other_sems,
        first_sems,
    ) = refs[27:]
    step = pl.program_id(0)
    pairs = pl.num_programs(0)
    z, y, x, core = seats()
    wide = d_a.shape[3]
    late_part = late_rows(tok)
    length = 4 * tok
    blocks = gu_a.shape[0]
    o_half, d_half = o_x.shape[2], d_x.shape[2]
    o_mine = pl.ds(pl.multiple_of(x * o_half, o_half), o_half)
    o_theirs = pl.ds(pl.multiple_of((1 - x) * o_half, o_half), o_half)
    d_mine = pl.ds(pl.multiple_of(x * d_half, d_half), d_half)
    d_theirs = pl.ds(pl.multiple_of((1 - x) * d_half, d_half), d_half)
    swap = send(
        outputs_sent.at[late_part],
        outputs_received.at[late_part],
        other_sems,
        0,
        to_x_partner(),
    )
    o_over = send(o_a.at[:, :, o_theirs, :], o_x, other_sems, 1, to_x_partner())
    d_over = send(d_in.at[:, :, d_theirs, :], d_x, other_sems, 2, to_x_partner())
    o_send = send(o_a.at[:, 1 - y, o_mine, :], o_y, other_sems, 3, to_y_partner())
    d_send = send(d_a.at[:, 1 - y], d_y, other_sems, 4, to_y_partner())
    late = pl.ds(blocks - LATE, LATE)
    late_send = send(gu_late, gu_b.at[late], other_sems, 5, to_y_partner())

    def z_send(jump, number):
        target = lax.rem(z + jump, line)
        at = late if number else pl.ds(0, blocks - LATE)
        return send(
            gu_a.at[at, :, target],
            gu_z.at[jump - 1, at],
            z_sems,
            number * (line - 1) + jump - 1,
            to_z_partner(line, jump),
        )

    def add(number, _):
        total = gu_a[number].astype(F32) + gu_b[number].astype(F32)
        gu_a[number] = total.astype(BF16)
        return 0

    gu_stays = pltpu.make_async_copy(gu_a.at[:, :, z], gu_mine, local_sems.at[5])
    o_stays = pltpu.make_async_copy(o_a.at[:, y, o_mine, :], o_kept, local_sems.at[6])
    d_stays = pltpu.make_async_copy(d_a.at[:, y], d_kept, local_sems.at[7])
    load_d = pltpu.make_async_copy(d_in.at[:, :, d_mine, :], d_a, local_sems.at[4])

    def first_send(source):
        columns = pl.ds(pl.multiple_of(core * wide, wide), PAIR)
        partner = to_x_partner() if source else {"seq": 3 - lax.axis_index("seq")}
        return send(
            first_out.at[source], first_received.at[:, columns], first_sems, source, partner
        )

    def hand_over(number):
        rows = pl.ds(number * PAIR, PAIR)
        return send(
            outgoing.at[:, rows, :],
            back_other.at[:, rows, :],
            back_sems,
            number,
            to_core_partner(),
        )

    @pl.when(step == 0)
    def _():
        meet(line, ("z", "y", "x", "core", "diagonal"))
        late_send.start()
        loads = [
            pltpu.make_async_copy(source, target, local_sems.at[number])
            for number, (source, target) in enumerate(
                (
                    (o_in, o_a),
                    (o_landed, o_b),
                    (gu_in, gu_a),
                    (gu_y, gu_b.at[pl.ds(0, blocks - LATE)]),
                )
            )
        ]
        for load in loads:
            load.start()
        load_d.start()
        loads[0].wait()
        loads[1].wait()
        o_a[...] = (o_a[...].astype(F32) + o_b[...].astype(F32)).astype(BF16)
        o_over.start()
        d_over.start()
        loads[2].wait()
        loads[3].wait()
        lax.fori_loop(0, blocks - LATE, add, 0)
        for jump in range(1, line):
            z_send(jump, 0).start()

    @pl.when(step == 1)
    def _():
        late_send.wait()
        lax.fori_loop(blocks - LATE, blocks, add, 0)
        for jump in range(1, line):
            z_send(jump, 1).start()
        gu_stays.start()
        o_over.wait()
        summed = o_a[:, :, o_mine, :].astype(F32) + o_x[...].astype(F32)
        o_a[:, :, o_mine, :] = summed.astype(BF16)
        o_send.start()
        o_stays.start()

    @pl.when(step == 2)
    def _():
        swap.start()

    @pl.when(step == 3)
    def _():
        load_d.wait()
        d_over.wait()
        for at in range(line):
            d_a[at] = (d_a[at].astype(F32) + d_x[at].astype(F32)).astype(BF16)
        d_send.start()
        d_stays.start()

    attend_back_body(
        (received, own),
        (mix_received, mix_own),
        (grad_received, grad_own),
        lambda source, slot: block_of(source, slot, tok),
        tok,
        length,
        tile_q,
        tile_k,
        lse_ref,
        qz,
        gz,
        qn,
        gn,
        kn,
        vn,
        kt,
        inner,
        dq,
        dk,
        dv,
    )
    for slot in range(2):
        take = slice(slot * tok, (slot + 1) * tok)
        for source in range(2):
            cols = block_of(source, slot, tok)
            results = turn_back(dq, dk, dv, cols, cos_ref[:, cols], sin_ref[:, cols])
            for which, result in enumerate(results):
                if source == 1:
                    back_own[which, :, take] = result
                else:
                    at = pl.ds(pl.multiple_of(step * PAIR, PAIR), PAIR)
                    outgoing[which, at, take] = result

    @pl.when(step == 0)
    def _():
        for source in range(2):
            rows = dv[block_of(source, 1, tok), :]
            first_out[source] = (0.5 * rows).astype(BF16)
            first_send(source).start()

    for number in range(4):

        @pl.when(step == number)
        def _(number=number):
            hand_over(number).start()

    @pl.when(step == pairs - 1)
    def _():
        swap.wait()
        for source in range(2):
            first_send(source).wait()
        d_send.wait()
        o_send.wait()
        for copy in (gu_stays, o_stays, d_stays):
            copy.wait()
        for number in range(2):
            for jump in range(1, line):
                z_send(jump, number).wait()
        for number in range(4):
            hand_over(number).wait()


def attend_back_carry(
    pieces,
    mixes,
    grads,
    lse,
    cosine,
    sine,
    outputs_sent,
    outputs_received,
    gu,
    gu_y,
    gu_late,
    d,
    o,
    o_landed,
    line,
):
    _, width, span = pieces[0].shape
    tok = span // 2
    length = 2 * span
    pairs = width // PAIR
    tile_q = min(512, length)
    tile_k = min(256, length)
    anywhere = pl.BlockSpec(memory_space=pl.ANY)
    triple = pl.BlockSpec((3, PAIR, span), lambda p: (0, p, 0))
    single = pl.BlockSpec((PAIR, span), lambda p: (p, 0))
    table = pl.BlockSpec((HALF, length), lambda p: (0, 0))
    blocks, _, _, rows, _ = gu.shape
    down_rows, wide = d.shape[2:]
    area = pairs * 2 * length * length // 2
    return pl.pallas_call(
        functools.partial(attend_back_carry_kernel, line, tok, tile_q, tile_k),
        grid=(pairs,),
        in_specs=[triple] * 2
        + [single] * 4
        + [pl.BlockSpec((1, 8, length), lambda p: (p, 0, 0)), table, table]
        + [anywhere] * 8,
        out_specs=[triple] + [anywhere] * 9,
        out_shape=[
            jax.ShapeDtypeStruct((3, width, span), BF16),
            jax.ShapeDtypeStruct((3, width, span), BF16),
            jax.ShapeDtypeStruct(outputs_sent.shape, BF16),
            jax.ShapeDtypeStruct((blocks, 2, rows, 128), BF16),
            jax.ShapeDtypeStruct((line - 1, blocks, 2, rows, 128), BF16),
            jax.ShapeDtypeStruct((line, down_rows // 2, wide), BF16),
            jax.ShapeDtypeStruct((line, down_rows // 2, wide), BF16),
            jax.ShapeDtypeStruct((line, rows // 2, wide), BF16),
            jax.ShapeDtypeStruct((line, rows // 2, wide), BF16),
            jax.ShapeDtypeStruct(outputs_sent.shape, BF16),
        ],
        input_output_aliases={10: 2},
        scratch_shapes=[
            pltpu.VMEM((2, PAIR, length), BF16),
            pltpu.VMEM((2, PAIR, length), BF16),
            pltpu.VMEM((2, length, PAIR), BF16),
            pltpu.VMEM((2, length, PAIR), BF16),
            pltpu.VMEM((length, PAIR), BF16),
            pltpu.VMEM((length, PAIR), BF16),
            pltpu.VMEM((PAIR, length), BF16),
            pltpu.VMEM((8, length), F32),
            pltpu.VMEM((PAIR, length), F32),
            pltpu.VMEM((length, PAIR), F32),
            pltpu.VMEM((length, PAIR), F32),
            pltpu.VMEM((3, width, span), BF16),
            pltpu.VMEM((blocks, 2, line, rows, 128), BF16),
            pltpu.VMEM((blocks, 2, line, rows, 128), BF16),
            pltpu.VMEM((line, 2, rows, wide), BF16),
            pltpu.VMEM((line, 2, rows, wide), BF16),
            pltpu.VMEM((line, 2, rows // 2, wide), BF16),
            pltpu.VMEM((line, 2, down_rows // 2, wide), BF16),
            pltpu.VMEM((line, 2, down_rows // 2, wide), BF16),
            pltpu.VMEM((2, tok, PAIR), BF16),
            pltpu.SemaphoreType.DMA((8,)),
            pltpu.SemaphoreType.DMA((2, 4)),
            pltpu.SemaphoreType.DMA((2, 2 * (line - 1))),
            pltpu.SemaphoreType.DMA((2, 6)),
            pltpu.SemaphoreType.DMA((2, 2)),
        ],
        compiler_params=pltpu.CompilerParams(
            dimension_semantics=("arbitrary",),
            vmem_limit_bytes=60 * MIB,
            collective_id=5,
            has_side_effects=True,
        ),
        cost_estimate=pl.CostEstimate(
            flops=area * 2560, bytes_accessed=16 * width * length, transcendentals=area
        ),
        name="attend_back_carry",
    )(
        *pieces,
        *mixes,
        *grads,
        lse,
        cosine,
        sine,
        outputs_sent,
        outputs_received,
        gu,
        gu_y,
        gu_late,
        d,
        o,
        o_landed,
    )


def tail_carry_kernel(line, tok, blocks, *refs):
    (
        inputs,
        x_received,
        back_other,
        back_own,
        full_ref,
        normed_ref,
        grad_in,
        gains_ref,
        mlp_gain_ref,
        gu_mine,
        gu_z,
        d_in,
        d_y,
        o_in,
        o_y,
        _,
        input_grad,
        input_landed,
        first_grad,
        first_landed,
        gain_out,
        q_out,
        k_out,
        v_out,
        o_out,
        g_out,
        u_out,
        d_out,
        xs,
        grad_middle,
        normed_t,
        acc,
        grad,
        sent,
        landed,
        y_landed,
        z_landed,
        d_a,
        d_b,
        d_landed,
        o_a,
        o_b,
        o_landed,
        gu_a,
        gu_b,
        gu_x,
        gu_c,
        d_low,
        d_c,
        s_low,
        s_x,
        s_c,
        first_stage,
        first_send,
        input_send,
        gain,
        gain_landed,
        local_sems,
        core_sems,
        y_sems,
        z_sems,
        dz_sems,
        oz_sems,
        x_sems,
        c_sems,
        token_sems,
        gain_sems,
    ) = refs
    step = pl.program_id(0)
    target = jnp.where(step < 6, lax.rem(step, 2), 2)
    turn = lax.rem(step // 2, 3)
    z, y, x, core = seats()
    side = x
    wide, span = grad.shape
    depth = 2 * wide
    half = jnp.where(target == 0, 1 - core, core)
    columns = pl.ds(pl.multiple_of(half * wide, wide), wide)
    mine = pl.ds(pl.multiple_of(core * wide, wide), wide)
    others = pl.ds(pl.multiple_of((1 - core) * wide, wide), wide)

    def load(source, place, number):
        return pltpu.make_async_copy(source, place, local_sems.at[number])

    load_tokens = [
        load(inputs.at[side], xs.at[pl.ds(0, tok), :], 0),
        load(x_received, xs.at[pl.ds(tok, tok), :], 1),
        load(grad_in, grad_middle, 2),
    ]
    store_input = load(acc.at[pl.ds(0, tok), :], input_grad, 3)
    store_first = load(first_stage, first_grad, 4)

    def along_z(source, place, sems, base=0):
        return [
            send(
                source(lax.rem(z + jump, line)),
                place(jump - 1),
                sems,
                base + jump - 1,
                to_z_partner(line, jump),
            )
            for jump in range(1, line)
        ]

    d_sends = along_z(lambda at: d_a.at[at], lambda jump: d_landed.at[jump], dz_sems)
    o_sends = along_z(lambda at: o_a.at[at], lambda jump: o_landed.at[jump], oz_sems)

    def core_send(number):
        return send(sent.at[number], landed.at[number], core_sems, number, to_core_partner())

    def y_send(number):
        return send(
            landed.at[number, :, 1 - y], y_landed.at[number], y_sems, number, to_y_partner()
        )

    def z_sends(number):
        return along_z(
            lambda at: landed.at[number, at, y],
            lambda jump: z_landed.at[number, jump],
            z_sems,
            number * (line - 1),
        )

    def first_part(number):
        which = 1 - core if number == 0 else core
        at = pl.ds(pl.multiple_of(which * wide + PAIR, PAIR), wide - PAIR)
        return send(
            first_send.at[:, at], first_landed.at[:, at], token_sems, number, to_x_partner()
        )

    input_part = send(input_send, input_landed, token_sems, 2, to_x_partner())
    gu_sides = (
        send(gu_a, gu_x, x_sems, 0, to_x_partner()),
        send(gu_a, gu_c, c_sems, 0, to_core_partner()),
    )
    d_half, o_half = d_a.shape[1], o_a.shape[1]
    d_mine = pl.ds(pl.multiple_of(x * d_half, d_half), d_half)
    d_theirs = pl.ds(pl.multiple_of((1 - x) * d_half, d_half), d_half)
    o_mine = pl.ds(pl.multiple_of(x * o_half, o_half), o_half)
    o_theirs = pl.ds(pl.multiple_of((1 - x) * o_half, o_half), o_half)
    d_sides = (
        send(d_low.at[d_mine, :], d_low.at[d_mine, :], x_sems, 1, to_x_partner()),
        send(d_low, d_c, c_sems, 1, to_core_partner()),
    )
    o_side = send(s_low.at[0, o_mine, :], s_low.at[0, o_mine, :], x_sems, 2, to_x_partner())

    def square_x(number):
        return send(s_low.at[number], s_x.at[number], x_sems, 2 + number, to_x_partner())

    def square_core(number):
        return send(s_low.at[number], s_c.at[number], c_sems, 2 + number, to_core_partner())

    squares = (o_out, v_out, q_out, k_out)

    def gain_send(number, partner):
        return send(gain.at[number], gain_landed.at[number], gain_sems, number, partner)

    @pl.when(step == 0)
    def _():
        meet(line, ("z", "y", "x", "core"))
        sources = ((d_in, d_a), (d_y, d_b), (o_in, o_a), (o_y, o_b), (gu_mine, gu_a), (gu_z, gu_b))
        loads = [load(source, place, 7 + n) for n, (source, place) in enumerate(sources)]
        for copy in loads:
            copy.start()
        for copy in load_tokens:
            copy.start()
        for copy in loads[:4]:
            copy.wait()
        for at in range(line):
            d_a[at] = (d_a[at].astype(F32) + d_b[at].astype(F32)).astype(BF16)
            o_a[at] = (o_a[at].astype(F32) + o_b[at].astype(F32)).astype(BF16)
        for copy in d_sends + o_sends:
            copy.start()
        for copy in loads[4:]:
            copy.wait()

        def total(number, _):
            for which, out in enumerate((g_out, u_out)):
                value = gu_a[number, which].astype(F32)
                for jump in range(line - 1):
                    value = value + gu_b[jump, number, which].astype(F32)
                at = pl.ds(pl.multiple_of((core * blocks + number) * 128, 128), 128)
                out[:, at] = value
                gu_a[number, which] = value.astype(BF16)
            return 0

        lax.fori_loop(0, blocks, total, 0)
        gu_sides[0].start()
        normed_t[...] = normed_ref[...].T
        acc[...] = jnp.zeros_like(acc)

    def own_part(back):
        @pl.when(turn == 0)
        def _():
            value = 0.5 * back[0].astype(F32)
            rows = value.T
            first_stage[:, columns] = rows[:tok]
            first_send[:, columns] = rows[tok:].astype(BF16)
            grad[...] = value.astype(BF16)

        @pl.when(turn > 0)
        def _():
            grad[...] = back[0]

    @pl.when(target == 0)
    def _():
        own_part(back_other)

    @pl.when(target == 1)
    def _():
        own_part(back_own)

    @pl.when(step == 0)
    def _():
        first_part(0).start()

    @pl.when(step == 1)
    def _():
        first_part(1).start()
        store_first.start()

    @pl.when(target < 2)
    def _():
        value = grad[...]
        result = nt(normed_t[...], value)

        @pl.when(target == 0)
        def _():
            sent[turn] = result.astype(BF16).reshape(sent.shape[1:])
            core_send(turn).start()

        @pl.when(target == 1)
        def _():
            core_send(turn).wait()
            theirs = landed[turn].reshape(result.shape).astype(F32)
            landed[turn] = (result + theirs).astype(BF16).reshape(landed.shape[1:])
            y_send(turn).start()

        acc[...] += nt(value.T, full_ref[0, 0])

    @pl.when(step == 6)
    def _():
        for copy in load_tokens:
            copy.wait()
        weight = gains_ref[0:1, :]
        chunk = min(128, tok)
        gain[...] = jnp.zeros_like(gain)
        gain[0, 1:2, :] = mlp_gain_ref[0:1, :]
        for slot in (1, 0):

            def finish(number, _, slot=slot):
                local = pl.ds(pl.multiple_of(number * chunk, chunk), chunk)
                some = pl.ds(pl.multiple_of(slot * tok + number * chunk, chunk), chunk)
                values = xs[some, :].astype(F32)
                scale = lax.rsqrt(jnp.mean(values * values, axis=1, keepdims=True) + epsilon)
                value = acc[some, :]
                gain[0, 0:1, :] += jnp.sum(value * values * scale, axis=0, keepdims=True)
                weighted = value * weight
                inner = jnp.mean(weighted * values, axis=1, keepdims=True)
                result = (
                    scale * weighted
                    - values * (scale * scale * scale) * inner
                    + grad_middle[some, :]
                )
                if slot == 0:
                    acc[some, :] = result
                else:
                    input_send[local, :] = result.astype(BF16)
                return 0

            lax.fori_loop(0, tok // chunk, finish, 0)
            if slot == 1:
                input_part.start()
        gain_send(0, to_core_partner()).start()
        store_input.start()
        gu_sides[0].wait()

        def gather_x(number, _):
            for which, out in enumerate((g_out, u_out)):
                at = pl.ds(pl.multiple_of((core * blocks + number) * 128, 128), 128)
                value = out[:, at] + gu_x[number, which].astype(F32)
                out[:, at] = value
                gu_a[number, which] = value.astype(BF16)
            return 0

        lax.fori_loop(0, blocks, gather_x, 0)
        gu_sides[1].start()
        gain_send(0, to_core_partner()).wait()
        gain[1] = gain[0] + gain_landed[0]
        gain_send(1, to_y_partner()).start()
        for number in range(3):
            y_send(number).wait()

            def add(at, _, number=number):
                value = landed[number, at, y].astype(F32) + y_landed[number, at].astype(F32)
                landed[number, at, y] = value.astype(BF16)
                return 0

            lax.fori_loop(0, line, add, 0)
            for copy in z_sends(number):
                copy.start()
            if number == 0:
                gain_send(1, to_y_partner()).wait()
                gain[2] = gain[1] + gain_landed[1]
                for jump in range(1, line):
                    gain_z(jump, line, gain, gain_landed, gain_sems).start()
        for copy in d_sends + o_sends:
            copy.wait()

        def sum_z(own, places):
            value = own.astype(F32)
            for place in places:
                value = value + place.astype(F32)
            return value

        value = sum_z(d_a[z], [d_landed[jump] for jump in range(line - 1)])
        d_out[d_mine, mine] = value
        d_low[d_mine, :] = value.astype(BF16)
        d_sides[0].start()
        value = sum_z(o_a[z], [o_landed[jump] for jump in range(line - 1)])
        o_out[o_mine, mine] = value
        s_low[0, o_mine, :] = value.astype(BF16)
        o_side.start()
        for jump in range(1, line):
            gain_z(jump, line, gain, gain_landed, gain_sems).wait()
        value = gain[2]
        for jump in range(1, line):
            value = value + gain_landed[1 + jump]
        gain[3] = value
        last_gain = send(gain.at[3], gain_landed.at[line + 1], gain_sems, line + 1, to_x_partner())
        last_gain.start()
        for number in range(3):
            for copy in z_sends(number):
                copy.wait()
            value = sum_z(
                landed[number, z, y], [z_landed[number, jump] for jump in range(line - 1)]
            )
            squares[1 + number][:, mine] = value
            s_low[1 + number] = value.astype(BF16)
            square_x(1 + number).start()
        last_gain.wait()
        gain[4] = gain[3] + gain_landed[line + 1]
        gain_out[...] = gain[4, :, pl.ds(pl.multiple_of((2 * z + y) * 128, 128), 128)]
        store_first.wait()
        for number in range(2):
            first_part(number).wait()
        d_sides[0].wait()
        d_out[d_theirs, mine] = d_low[d_theirs, :].astype(F32)
        d_sides[1].start()
        o_side.wait()
        o_out[o_theirs, mine] = s_low[0, o_theirs, :].astype(F32)
        square_core(0).start()
        input_part.wait()
        for number in range(1, 4):
            square_x(number).wait()
            value = squares[number][:, mine] + s_x[number].astype(F32)
            squares[number][:, mine] = value
            s_low[number] = value.astype(BF16)
            square_core(number).start()
        gu_sides[1].wait()

        def gather_core(number, _):
            for which, out in enumerate((g_out, u_out)):
                at = pl.ds(pl.multiple_of(((1 - core) * blocks + number) * 128, 128), 128)
                out[:, at] = gu_c[number, which].astype(F32)
            return 0

        lax.fori_loop(0, blocks, gather_core, 0)
        d_sides[1].wait()
        d_out[:, others] = d_c[...].astype(F32)
        for number in range(4):
            square_core(number).wait()
            squares[number][:, others] = s_c[number].astype(F32)
        store_input.wait()


def gain_z(jump, line, gain, gain_landed, gain_sems):
    return send(
        gain.at[2], gain_landed.at[1 + jump], gain_sems, 1 + jump, to_z_partner(line, jump)
    )


def tail_carry(
    inputs,
    x_received,
    back_other,
    back_own,
    full,
    normed,
    grad_middle,
    gains,
    mlp_gain,
    gu_mine,
    gu_z,
    d,
    d_y,
    o,
    o_y,
    first_received,
    line,
):
    slots, tok, depth = inputs.shape
    span = slots * tok
    wide = depth // 2
    blocks, _, rows, _ = gu_mine.shape
    down_rows = 2 * d.shape[1]
    once = pl.Buffered(1)
    anywhere = pl.BlockSpec(memory_space=pl.ANY)

    def half(s):
        core = lax.axis_index("seq") % 2
        return jnp.where(s % 2 == 0, 1 - core, core)

    def kind(s):
        return (jnp.minimum(s // 2, 2) + 2) % 3

    def clear(shape):
        zeros = (0,) * len(shape)
        return pl.BlockSpec(shape, lambda s: zeros, pipeline_mode=once)

    square = jax.ShapeDtypeStruct((rows, depth), F32)
    broad = jax.ShapeDtypeStruct((rows, 2 * blocks * 128), F32)
    tall = jax.ShapeDtypeStruct((down_rows, depth), F32)
    tokens = [jax.ShapeDtypeStruct((tok, depth), dtype) for dtype in (F32, BF16)] * 2
    finals = [square] * 4 + [broad] * 2 + [tall]
    vmem = pltpu.VMEM
    dma = pltpu.SemaphoreType.DMA
    return pl.pallas_call(
        functools.partial(tail_carry_kernel, line, tok, blocks),
        grid=(7,),
        in_specs=[
            anywhere,
            anywhere,
            pl.BlockSpec((1, wide, span), lambda s: (kind(s), 0, 0)),
            pl.BlockSpec((1, wide, span), lambda s: (kind(s), 0, 0)),
            pl.BlockSpec(
                (1, 1, depth, wide),
                lambda s: (half(jnp.minimum(s, 5)), kind(s), 0, 0),
            ),
            clear((span, depth)),
            anywhere,
            clear((8, depth)),
            clear((8, depth)),
        ]
        + [anywhere] * 7,
        input_output_aliases={15: 3},
        out_specs=[anywhere] * 4 + [clear((8, 128))] + [clear(final.shape) for final in finals],
        out_shape=tokens + [jax.ShapeDtypeStruct((8, 128), F32)] + finals,
        scratch_shapes=[
            vmem((span, depth), BF16),
            vmem((span, depth), F32),
            vmem((depth, span), BF16),
            vmem((span, depth), F32),
            vmem((wide, span), BF16),
            vmem((3, line, 2, rows, wide), BF16),
            vmem((3, line, 2, rows, wide), BF16),
            vmem((3, line, rows, wide), BF16),
            vmem((3, line - 1, rows, wide), BF16),
            vmem((line, down_rows // 2, wide), BF16),
            vmem((line, down_rows // 2, wide), BF16),
            vmem((line - 1, down_rows // 2, wide), BF16),
            vmem((line, rows // 2, wide), BF16),
            vmem((line, rows // 2, wide), BF16),
            vmem((line - 1, rows // 2, wide), BF16),
            vmem((blocks, 2, rows, 128), BF16),
            vmem((line - 1, blocks, 2, rows, 128), BF16),
            vmem((blocks, 2, rows, 128), BF16),
            vmem((blocks, 2, rows, 128), BF16),
            vmem((down_rows, wide), BF16),
            vmem((down_rows, wide), BF16),
            vmem((4, rows, wide), BF16),
            vmem((4, rows, wide), BF16),
            vmem((4, rows, wide), BF16),
            vmem((tok, depth), F32),
            vmem((tok, depth), BF16),
            vmem((tok, depth), BF16),
            vmem((5, 8, depth), F32),
            vmem((line + 2, 8, depth), F32),
            dma((13,)),
            dma((2, 3)),
            dma((2, 3)),
            dma((2, 3 * (line - 1))),
            dma((2, line - 1)),
            dma((2, line - 1)),
            dma((2, 6)),
            dma((2, 6)),
            dma((2, 3)),
            dma((2, line + 2)),
        ],
        compiler_params=pltpu.CompilerParams(
            dimension_semantics=("arbitrary",),
            vmem_limit_bytes=63 * MIB,
            collective_id=6,
            has_side_effects=True,
        ),
        cost_estimate=pl.CostEstimate(
            flops=12 * span * depth * depth,
            bytes_accessed=24 * span * depth + 12 * depth * depth,
            transcendentals=0,
        ),
        name="tail_carry",
    )(
        inputs,
        x_received,
        back_other,
        back_own,
        full,
        normed,
        grad_middle,
        gains,
        mlp_gain,
        gu_mine,
        gu_z,
        d,
        d_y,
        o,
        o_y,
        first_received,
    )


def finish_kernel(place, *refs):
    count = (len(refs) - 2 * 3 - 3) // 2
    tokens, plain = refs[:6], refs[6 : 6 + count]
    outs = refs[6 + count :]
    side = place[0]
    for number in range(3):
        outs[number][side] = tokens[2 * number][...].reshape(tokens[2 * number + 1].shape)
        outs[number][1 - side] = tokens[2 * number + 1][...].astype(F32)
    for number in range(count):
        outs[3 + number][...] = plain[number][...]


def finish(outputs, tokens, plain, side):
    _, tok, depth = outputs[0].shape
    steps = 4
    tile = tok // steps
    row = pl.BlockSpec((tile, depth), lambda s, p: (s, 0))
    tiles = [
        pl.BlockSpec((value.shape[0] // steps, value.shape[1]), lambda s, p: (s, 0))
        for value in plain
    ]
    grid_spec = pltpu.PrefetchScalarGridSpec(
        num_scalar_prefetch=1,
        grid=(steps,),
        in_specs=[pl.BlockSpec((1, tile, depth), lambda s, p: (p[0], s, 0))] + [row] * 5 + tiles,
        out_specs=[pl.BlockSpec((2, tile, depth), lambda s, p: (0, s, 0))] * 3 + tiles,
    )
    return pl.pallas_call(
        finish_kernel,
        out_shape=[jax.ShapeDtypeStruct((2, tok, depth), F32)] * 3
        + [jax.ShapeDtypeStruct(value.shape, value.dtype) for value in plain],
        grid_spec=grid_spec,
        compiler_params=parameters(60),
        cost_estimate=pl.CostEstimate(
            flops=tok * depth, bytes_accessed=60 * tok * depth, transcendentals=0
        ),
        name="finish",
    )(side, *outputs, *tokens, *plain)


def shards(
    inputs,
    first_values,
    out_grad,
    attn_gain,
    query_weight,
    key_weight,
    value_weight,
    output_weight,
    mlp_gain,
    gate_weight,
    up_weight,
    down_weight,
):
    slots, tok, _ = inputs.shape
    groups = lax.axis_size("seq")
    parts = lax.axis_size("fsdp")
    line = parts // 2
    count = groups // slots
    length = tok * groups
    span = slots * tok
    seat = lax.axis_index("seq")
    shard = lax.axis_index("fsdp")
    side = seat // count
    rank = seat % count
    core = seat % 2
    z, y = shard // 2, shard % 2
    wide = D // 2
    width = D // count

    def along_seq(value, partner):
        return lax.ppermute(value, "seq", [(i, partner(i)) for i in range(groups)])

    def along_fsdp(value, partner):
        return lax.ppermute(value, "fsdp", [(i, partner(i)) for i in range(parts)])

    def to_core(value):
        return along_seq(value, lambda i: i ^ 1)

    def to_y(value):
        return along_fsdp(value, lambda i: i ^ 1)

    def to_z(value, jump):
        return along_fsdp(value, lambda i: (i + 2 * jump) % parts)

    def after(value, *others):
        return lax.optimization_barrier((value,) + others)[0]

    def to_sequence(values):
        taken = []
        for jump in range(1, slots):
            sent = lax.dynamic_index_in_dim(values, (side + jump) % slots, 0, keepdims=False)
            taken.append(along_seq(sent, lambda i: (i + jump * count) % groups))
        return taken

    def to_home(whole, sent):
        for jump in range(1, slots):
            part = sent[(jump - 1) * tok : jump * tok]
            part = along_seq(part, lambda i: (i - jump * count) % groups)
            whole = land(whole, part, ((side + jump) % slots)[None])
        return whole

    def rank_up(i, jump):
        return (i // count) * count + (i % count + jump) % count

    def rank_down(i, jump):
        return (i // count) * count + (i % count - jump) % count

    def halves_to_ranks(other, own, axis):
        if count == 2:
            return [other, own]
        return [
            lax.dynamic_slice_in_dim(
                join(other, own, axis), ((rank + 1 + number) % count) * width, width, axis
            )
            for number in range(count)
        ]

    def join(other, own, axis):
        first = jnp.where(core == 0, own, other)
        second = jnp.where(core == 0, other, own)
        return jnp.concatenate([first, second], axis=axis)

    def ranks_to_halves(pieces, axis):
        if count == 2:
            return pieces
        shape = list(pieces[0].shape)
        shape[axis] = D
        whole = jnp.zeros(shape, pieces[0].dtype)
        for number in range(count):
            whole = lax.dynamic_update_slice_in_dim(
                whole, pieces[number], ((rank + 1 + number) % count) * width, axis
            )
        return [
            lax.dynamic_slice_in_dim(whole, which * wide, wide, axis)
            for which in (1 - core, core)
        ]

    def exchange(pieces):
        received = [
            along_seq(pieces[jump - 1], lambda i: rank_up(i, jump)) for jump in range(1, count)
        ]
        return received + [pieces[count - 1]]

    def exchange_back(pieces):
        received = [
            along_seq(pieces[jump - 1], lambda i: rank_down(i, jump)) for jump in range(1, count)
        ]
        return received + [pieces[count - 1]]

    def split(*weights):
        results = []
        for which in (core, 1 - core):
            columns = []
            for weight in weights:
                size = weight.shape[1] // 2
                columns.append(lax.dynamic_slice_in_dim(weight, which * size, size, 1))
            results.append(columns)
        return results

    def gather_z(half):
        return [half] + [to_z(half, jump) for jump in range(1, line)]

    def gather_rest(along_z, other):
        along_y = [to_y(piece) for piece in along_z]
        own = [piece for pair in zip(along_z, along_y) for piece in pair]
        return (own, [other] + [to_core(piece) for piece in own[1:]])

    numbers = []
    for jump in range(line):
        for flip in range(2):
            numbers.append(((z - jump) % line) * 2 + (y ^ flip))
    place = jnp.stack([side, core] + numbers).astype(jnp.int32)

    def low(value):
        return value.astype(BF16)

    def add(a, b):
        return low(a.astype(F32) + b.astype(F32))

    def pick(value, index, axis):
        return lax.dynamic_index_in_dim(value, index, axis, keepdims=False)

    def along_x_and_core(total):
        mine = low(total)
        for jump in range(1, groups // 2):
            total = total + along_seq(mine, lambda i: (i + 2 * jump) % groups).astype(F32)
        mine = low(total)
        return (mine, to_core(mine))

    def along_z_and_on(partial):
        total = partial(z)
        for jump in range(1, line):
            total = total + to_z(low(partial((z + jump) % line)), jump).astype(F32)
        return along_x_and_core(total)

    def scatter(sent, kept, rows_axis):
        shape = kept.shape
        rows = shape[rows_axis] // parts
        cut = shape[:rows_axis] + (line, 2, rows) + shape[rows_axis + 1 :]
        received = to_core(sent).reshape(cut)
        kept = kept.reshape(cut)
        axis = rows_axis + 1
        received_y = to_y(add(pick(kept, 1 - y, axis), pick(received, 1 - y, axis)))
        kept_y = pick(kept, y, axis), pick(received, y, axis)

        def partial(index):
            total = pick(kept_y[0], index, rows_axis).astype(F32)
            total = total + pick(kept_y[1], index, rows_axis).astype(F32)
            return total + pick(received_y, index, rows_axis).astype(F32)

        return along_z_and_on(partial)

    def columns(mine, others):
        first = jnp.where(core == 0, mine, others)
        second = jnp.where(core == 0, others, mine)
        return jnp.concatenate([first, second], axis=-1).astype(F32)

    def everywhere(value):
        value = value + to_core(value)
        value = value + to_y(value)
        total = value
        for jump in range(1, line):
            total = total + to_z(value, jump)
        value = total
        for jump in range(1, groups // 2):
            total = total + along_seq(value, lambda i: (i + 2 * jump) % groups)
        return total

    steps = jnp.arange(slots, dtype=jnp.int32)
    starts = ((side - steps) % slots) * (count * tok) + rank * tok
    positions = (starts[:, None] + jnp.arange(tok, dtype=jnp.int32)[None]).reshape(span)
    freqs = rope_base ** (-(jnp.arange(HALF, dtype=F32) * 2.0 / HEAD_DIM))

    def tables(positions):
        angles = freqs[:, None] * positions.astype(F32)[None, :]
        return (jnp.cos(angles), jnp.sin(angles))

    full_cos, full_sin = tables(jnp.arange(length, dtype=jnp.int32))
    sources = jnp.concatenate(
        [(rank - 1 - jnp.arange(count - 1, dtype=jnp.int32)) % count, rank[None]]
    ).astype(jnp.int32)
    order = (((side - steps) % slots)[None, :] * count + sources[:, None]).reshape(-1)
    order = order.astype(jnp.int32)

    whole_lanes = (slots, count) == (2, 2) and (D // parts) % 128 == 0
    if whole_lanes:
        gains = jnp.pad(jnp.stack([attn_gain, mlp_gain]).astype(F32), ((0, 6), (0, 0)))
        parts_of = lambda ref: [ref.reshape(-1, ref.shape[-1])]
        (
            tokens,
            _,
            grads_early,
            heads_own,
            heads_received,
            normed,
            qkv_full,
            gains_full,
            out_own,
            out_other,
            down_own,
        ) = front(
            inputs,
            first_values,
            out_grad,
            query_weight,
            key_weight,
            value_weight,
            output_weight,
            down_weight,
            gains,
            full_cos,
            full_sin,
            line,
        )
        qkv_full = qkv_full.reshape(2, 3, D, wide)
        tokens = [tokens]
        pieces = [heads_received, heads_own]
        (
            mix_received,
            att_own,
            lse,
            middle,
            normed2,
            out_full,
            att_other,
            grads,
            down_own,
            down_other,
            gate_own,
            gate_other,
            up_own,
            up_other,
        ) = attend_carry(
            heads_received,
            heads_own,
            inputs,
            tokens[0],
            gains_full,
            out_own.reshape(D, wide),
            out_other.reshape(D, wide),
            out_grad,
            grads_early,
            down_own,
            gate_weight,
            up_weight,
            line,
        )
        mixes = [mix_received, att_own]
        grads = [grads]
        gate_pieces = parts_of(gate_own), parts_of(gate_other)
        up_pieces = parts_of(up_own), parts_of(up_other)
        down_pieces = parts_of(down_own), parts_of(down_other)
    else:
        gains = jnp.pad(jnp.stack([attn_gain, mlp_gain], axis=1), ((0, 0), (0, 126)))
        gate_halves, up_halves, out_halves, down_halves = (
            [half[0] for half in split(weight)]
            for weight in (gate_weight, up_weight, output_weight, down_weight)
        )
        cosine, sine = tables(positions)
        qkv = [
            jnp.concatenate(half + [gains], axis=1)
            for half in split(query_weight, key_weight, value_weight)
        ]
        tokens = to_sequence(inputs)
        firsts = to_sequence(first_values)
        grads = to_sequence(out_grad)
        qkv_own, qkv_other = gather_rest(gather_z(qkv[0]), qkv[1])
        out_own, out_other = gather_rest(gather_z(out_halves[0]), out_halves[1])
        gate_pieces = gather_rest(gather_z(gate_halves[0]), gate_halves[1])
        up_pieces = gather_rest(gather_z(up_halves[0]), up_halves[1])
        down_pieces = gather_rest(gather_z(down_halves[0]), down_halves[1])
        heads_other, heads_own, normed, qkv_full, gains_full = project(
            inputs, tokens, first_values, firsts, qkv_own, qkv_other, cosine, sine, place
        )
        pieces = exchange(halves_to_ranks(heads_other, heads_own, 1))
        mixes, lse = attend(pieces, order, slots)
        att_other, att_own = ranks_to_halves(exchange_back(mixes), 0)
        middle, normed2, out_full = output_projection(
            inputs, tokens, out_own, out_other, att_other, att_own, gains_full, place
        )

    if whole_lanes:
        (
            outputs,
            outputs_sent,
            grad_middle,
            low_grad,
            mlp_gain_grad,
            gu_reduced,
            down_reduced,
            gu_y,
            gu_late,
        ) = mlp_carry(
            out_grad,
            grads[0],
            middle,
            normed2,
            gains_full,
            (gate_pieces[0][0], gate_pieces[1][0]),
            (up_pieces[0][0], up_pieces[1][0]),
            (down_pieces[0][0], down_pieces[1][0]),
            line,
        )
        ga_own, ga_received, out_kept, out_landed, outputs_received = grad_attended_carry(
            low_grad, out_full, att_other, att_own, outputs_sent, line
        )
        down_reduced = down_reduced.reshape(line, 2, -1, wide)
        out_kept = out_kept.reshape(line, 2, -1, wide)
        out_landed = out_landed.reshape(line, 2, -1, wide)
        (
            back_own,
            back_other,
            outputs_received,
            gu_mine,
            gu_z,
            down_mine,
            down_y,
            out_mine,
            out_y,
            first_received,
        ) = attend_back_carry(
            pieces,
            mixes,
            [ga_received, ga_own],
            lse,
            full_cos,
            full_sin,
            outputs_sent,
            outputs_received,
            gu_reduced,
            gu_y,
            gu_late,
            down_reduced,
            out_kept,
            out_landed,
            line,
        )
        input_own, input_received, first_own, first_received, *rest = tail_carry(
            inputs,
            tokens[0],
            back_other,
            back_own,
            qkv_full,
            normed,
            grad_middle,
            gains_full,
            mlp_gain_grad,
            gu_mine,
            gu_z,
            down_mine,
            down_y,
            out_mine,
            out_y,
            first_received,
            line,
        )
        gain_grads = rest[0]
        outputs, input_grad, first_grad, *rest = finish(
            (outputs,),
            (outputs_received, input_own, input_received, first_own, first_received),
            rest[1:],
            side[None],
        )
        query_grad, key_grad, value_grad, output_grad, gate_grad, up_grad, down_grad = rest
    else:
        (
            outputs,
            outputs_sent,
            grad_middle,
            low_grad,
            mlp_gain_grad,
            gu_sent,
            gu_kept,
            down_sent,
            down_kept,
        ) = mlp(out_grad, grads, middle, normed2, gains_full, gate_pieces, up_pieces, down_pieces, place)
        ga_other, ga_own, out_sent, out_kept = grad_attended(
            low_grad, out_full, att_other, att_own, place
        )
        gate_up_grad = scatter(gu_sent, gu_kept, 1)
        down_grad = scatter(down_sent.reshape(-1, wide), down_kept.reshape(-1, wide), 0)
        output_grad = scatter(out_sent, out_kept, 0)
        grad_heads = exchange(halves_to_ranks(ga_other, ga_own, 0))
        back = attend_back(pieces, mixes, grad_heads, lse, full_cos, full_sin, order, slots)
        back_other, back_own = ranks_to_halves(exchange_back(back), 1)
        outputs = to_home(outputs, outputs_sent)
        input_grad, input_sent, first_grad, first_sent, gain_grads, qkv_sent, qkv_kept = tail(
            inputs,
            tokens,
            back_other,
            back_own,
            qkv_full,
            normed,
            grad_middle,
            gains_full,
            mlp_gain_grad,
            place,
        )
        query_grad, key_grad, value_grad = columns(*scatter(qkv_sent, qkv_kept, 1))
        gate_grad, up_grad = columns(*gate_up_grad)
        output_grad = columns(*output_grad)
        down_grad = columns(*down_grad)
        gain_grads = everywhere(gain_grads)
        gain_grads = lax.dynamic_slice_in_dim(gain_grads, shard * (D // parts), D // parts, 1)
        input_grad = to_home(input_grad, input_sent)
        first_grad = to_home(first_grad, first_sent)

    return (
        outputs,
        input_grad,
        first_grad,
        gain_grads[0],
        gain_grads[1],
        query_grad,
        key_grad,
        value_grad,
        output_grad,
        gate_grad,
        up_grad,
        down_grad,
    )


def solution(mesh):
    token_spec = P("fsdp", "seq", None)
    weight_spec = P("fsdp", None)
    gain_spec = P("fsdp")
    return jax.shard_map(
        shards,
        mesh=mesh,
        in_specs=(token_spec,) * 3
        + (gain_spec,)
        + (weight_spec,) * 4
        + (gain_spec,)
        + (weight_spec,) * 3,
        out_specs=(token_spec,) * 3 + (gain_spec,) * 2 + (weight_spec,) * 7,
        check_vma=False,
    )
```

```python
import functools
import math

import jax
import jax.numpy as jnp
from jax import lax
from jax.experimental import pallas as pl
from jax.experimental.pallas import tpu as pltpu
from jax.sharding import PartitionSpec as P

D = 1024
HEADS = 16
HEAD_DIM = 64
HALF = HEAD_DIM // 2
PAIR = 2 * HEAD_DIM
F32 = jnp.float32
BF16 = jnp.bfloat16
NEG = -1e30
MIB = 1024 * 1024
epsilon = 1e-06
rope_base = 10000.0


def dot(a, b):
    return lax.dot_general(a, b, (((1,), (0,)), ((), ())), preferred_element_type=F32)


def head_rows(value, head):
    row = lax.broadcasted_iota(jnp.int32, value.shape, 0)
    return jnp.where((row // HEAD_DIM) == head, value, jnp.zeros_like(value))


def head_lanes(value, head):
    lane = lax.broadcasted_iota(jnp.int32, value.shape, 1)
    return jnp.where((lane // HEAD_DIM) == head, value, jnp.zeros_like(value))


def causal(scores):
    side = scores.shape[0]
    square = scores[:, :side]
    key = lax.broadcasted_iota(jnp.int32, square.shape, 0)
    query = lax.broadcasted_iota(jnp.int32, square.shape, 1)
    square = jnp.where(key <= query, square, NEG)
    if scores.shape[1] == side:
        return square
    return jnp.concatenate([square, scores[:, side:]], axis=1)


def attend_body(length, tile_k, qz, kn, vt, ot, lse_ref):
    def score(sub, head):
        start = sub * tile_k
        return causal(dot(kn[start : start + tile_k, :], qz[head, :, start:]))

    def absorb(sub, head, carry, scores):
        peak, total, mixed = carry
        start = sub * tile_k
        new_peak = jnp.maximum(peak, jnp.max(scores, axis=0, keepdims=True))
        weights = jnp.exp(scores - new_peak)
        fade = jnp.exp(peak - new_peak)
        total = total * fade + jnp.sum(weights, axis=0, keepdims=True)
        values = vt[head * HEAD_DIM : (head + 1) * HEAD_DIM, start : start + tile_k]
        mixed = mixed * fade + dot(values, weights.astype(BF16))
        return (new_peak, total, mixed)

    tiles = [(sub, head) for sub in range(length // tile_k) for head in range(2)]
    carries = [
        (
            jnp.full((1, length), NEG, F32),
            jnp.zeros((1, length), F32),
            jnp.zeros((HEAD_DIM, length), F32),
        )
        for _ in range(2)
    ]
    ahead = score(*tiles[0])
    for number, (sub, head) in enumerate(tiles):
        scores = ahead
        if number + 1 < len(tiles):
            ahead = score(*tiles[number + 1])
        peak, total, mixed = absorb(sub, head, carries[head], scores)
        done = slice(sub * tile_k, (sub + 1) * tile_k)
        rows = slice(head * HEAD_DIM, (head + 1) * HEAD_DIM)
        ot[rows, done] = (mixed[:, :tile_k] / total[:, :tile_k]).astype(BF16)
        lse_ref[0, head : head + 1, done] = peak[:, :tile_k] + jnp.log(total[:, :tile_k])
        carries[head] = (peak[:, tile_k:], total[:, tile_k:], mixed[:, tile_k:])


def attend_kernel(count, slots, tok, tile_k, order, *refs):
    pieces = refs[:count]
    outs = refs[count : 2 * count]
    lse_ref = refs[2 * count]
    qz, kn, vt, ot = refs[2 * count + 1 :]
    for source in range(count):
        for slot in range(slots):
            cols = pl.ds(pl.multiple_of(order[source * slots + slot] * tok, tok), tok)
            take = slice(slot * tok, (slot + 1) * tok)
            query = pieces[source][0, :, take] * jnp.asarray(HEAD_DIM**-0.5, BF16)
            for head in range(2):
                qz[head, :, cols] = head_rows(query, head)
            kn[cols, :] = pieces[source][1, :, take].T
            vt[:, cols] = pieces[source][2, :, take]
    length = count * slots * tok
    attend_body(length, tile_k, qz, kn, vt, ot, lse_ref)
    for source in range(count):
        for slot in range(slots):
            cols = pl.ds(pl.multiple_of(order[source * slots + slot] * tok, tok), tok)
            outs[source][:, slot * tok : (slot + 1) * tok] = ot[:, cols]


def attend(pieces, order, slots):
    count = len(pieces)
    width, span = pieces[0].shape[1:]
    tok = span // slots
    length = count * span
    pairs = width // PAIR
    tile_k = min(256, length)
    grid_spec = pltpu.PrefetchScalarGridSpec(
        num_scalar_prefetch=1,
        grid=(pairs,),
        in_specs=[pl.BlockSpec((3, PAIR, span), lambda p, o: (0, p, 0))] * count,
        out_specs=[pl.BlockSpec((PAIR, span), lambda p, o: (p, 0))] * count
        + [pl.BlockSpec((1, 8, length), lambda p, o: (p, 0, 0))],
        scratch_shapes=[
            pltpu.VMEM((2, PAIR, length), BF16),
            pltpu.VMEM((length, PAIR), BF16),
            pltpu.VMEM((PAIR, length), BF16),
            pltpu.VMEM((PAIR, length), BF16),
        ],
    )
    area = pairs * 2 * length * length // 2
    results = pl.pallas_call(
        functools.partial(attend_kernel, count, slots, tok, tile_k),
        out_shape=[jax.ShapeDtypeStruct((width, span), BF16)] * count
        + [jax.ShapeDtypeStruct((pairs, 8, length), F32)],
        grid_spec=grid_spec,
        compiler_params=pltpu.CompilerParams(
            dimension_semantics=("arbitrary",), vmem_limit_bytes=48 * MIB
        ),
        cost_estimate=pl.CostEstimate(
            flops=area * 1024, bytes_accessed=8 * width * length, transcendentals=area
        ),
        name="attend",
    )(order, *pieces)
    return (results[:count], results[count])


def attend_back_body(
    pieces,
    mixes,
    grads,
    columns,
    tok,
    length,
    tile_q,
    tile_k,
    lse_ref,
    qz,
    gz,
    qn,
    gn,
    kn,
    vn,
    kt,
    inner,
    dq,
    dk,
    dv,
):
    slots = pieces[0].shape[2] // tok
    for source in range(len(pieces)):
        for slot in range(slots):
            cols = columns(source, slot)
            take = slice(slot * tok, (slot + 1) * tok)
            query = pieces[source][0, :, take] * jnp.asarray(HEAD_DIM**-0.5, BF16)
            grad = grads[source][:, take]
            query_rows = query.T
            grad_rows = grad.T
            for head in range(2):
                qz[head, :, cols] = head_rows(query, head)
                gz[head, :, cols] = head_rows(grad, head)
                qn[head, cols, :] = head_lanes(query_rows, head)
                gn[head, cols, :] = head_lanes(grad_rows, head)
            key = pieces[source][1, :, take]
            kt[:, cols] = key
            kn[cols, :] = key.T
            vn[cols, :] = pieces[source][2, :, take].T
            both = grad.astype(F32) * mixes[source][:, take].astype(F32)
            for head in range(2):
                inner[head : head + 1, cols] = jnp.sum(
                    both[head * HEAD_DIM : (head + 1) * HEAD_DIM], axis=0, keepdims=True
                )
    dq[...] = jnp.zeros_like(dq)
    steps = tile_q // tile_k

    def tile(key_start, query_start, width, masked, carry):
        grad_keys, grad_values = carry
        keys = kn[pl.ds(key_start, tile_k), :]
        values = vn[pl.ds(key_start, tile_k), :]
        cols = pl.ds(query_start, width)
        for head in range(2):
            rows = slice(head * HEAD_DIM, (head + 1) * HEAD_DIM)
            scores = dot(keys, qz[head, :, cols])
            if masked:
                scores = causal(scores)
            probs = jnp.exp(scores - lse_ref[0, head : head + 1, cols])
            grad_probs = dot(values, gz[head, :, cols])
            grad_scores = (probs * (grad_probs - inner[head : head + 1, cols])).astype(BF16)
            grad_values = grad_values + dot(probs.astype(BF16), gn[head, cols, :])
            grad_keys = grad_keys + dot(grad_scores, qn[head, cols, :])
            dq[rows, cols] += dot(kt[rows, pl.ds(key_start, tile_k)], grad_scores)
        return (grad_keys, grad_values)

    def one(number, _):
        base = pl.multiple_of(number * tile_q, tile_q)
        for sub in range(steps):
            skip = sub * tile_k
            key_start = pl.multiple_of(base + skip, tile_k)
            carry = (jnp.zeros((tile_k, PAIR), F32), jnp.zeros((tile_k, PAIR), F32))
            carry = tile(key_start, key_start, tile_q - skip, True, carry)

            def body(step, carry):
                return tile(
                    key_start, pl.multiple_of(step * tile_q, tile_q), tile_q, False, carry
                )

            carry = lax.fori_loop(number + 1, length // tile_q, body, carry)
            dk[pl.ds(key_start, tile_k), :] = carry[0]
            dv[pl.ds(key_start, tile_k), :] = carry[1]
        return 0

    lax.fori_loop(0, length // tile_q, one, 0)


def turn_back(dq, dk, dv, cols, cosine, sine):
    half = HEAD_DIM // 2
    results = []
    for grad in (dq[:, cols] * (HEAD_DIM**-0.5), dk[cols, :].T):
        turned = []
        for head in range(2):
            low = head * HEAD_DIM
            first = grad[low : low + half]
            second = grad[low + half : low + 2 * half]
            turned += [first * cosine + second * sine, second * cosine - first * sine]
        results.append(jnp.concatenate(turned, axis=0).astype(BF16))
    results.append(dv[cols, :].T.astype(BF16))
    return results


def attend_back_kernel(count, slots, tok, tile_q, tile_k, order, *refs):
    pieces = refs[:count]
    mixes = refs[count : 2 * count]
    grads = refs[2 * count : 3 * count]
    lse_ref, cos_ref, sin_ref = refs[3 * count : 3 * count + 3]
    outs = refs[3 * count + 3 : 4 * count + 3]
    scratch = refs[4 * count + 3 :]
    dq, dk, dv = scratch[-3:]

    def columns(source, slot):
        return pl.ds(pl.multiple_of(order[source * slots + slot] * tok, tok), tok)

    attend_back_body(
        pieces,
        mixes,
        grads,
        columns,
        tok,
        count * slots * tok,
        tile_q,
        tile_k,
        lse_ref,
        *scratch,
    )
    for source in range(count):
        for slot in range(slots):
            cols = columns(source, slot)
            results = turn_back(dq, dk, dv, cols, cos_ref[:, cols], sin_ref[:, cols])
            for which, result in enumerate(results):
                outs[source][which, :, slot * tok : (slot + 1) * tok] = result


def attend_back(pieces, mixes, grads, lse, cosine, sine, order, slots):
    count = len(pieces)
    width, span = pieces[0].shape[1:]
    tok = span // slots
    length = count * span
    pairs = width // PAIR
    tile_q = min(512, length)
    tile_k = min(256, length)
    triple = pl.BlockSpec((3, PAIR, span), lambda p, o: (0, p, 0))
    single = pl.BlockSpec((PAIR, span), lambda p, o: (p, 0))
    table = pl.BlockSpec((HEAD_DIM // 2, length), lambda p, o: (0, 0))
    grid_spec = pltpu.PrefetchScalarGridSpec(
        num_scalar_prefetch=1,
        grid=(pairs,),
        in_specs=[triple] * count
        + [single] * (2 * count)
        + [pl.BlockSpec((1, 8, length), lambda p, o: (p, 0, 0)), table, table],
        out_specs=[triple] * count,
        scratch_shapes=[
            pltpu.VMEM((2, PAIR, length), BF16),
            pltpu.VMEM((2, PAIR, length), BF16),
            pltpu.VMEM((2, length, PAIR), BF16),
            pltpu.VMEM((2, length, PAIR), BF16),
            pltpu.VMEM((length, PAIR), BF16),
            pltpu.VMEM((length, PAIR), BF16),
            pltpu.VMEM((PAIR, length), BF16),
            pltpu.VMEM((8, length), F32),
            pltpu.VMEM((PAIR, length), F32),
            pltpu.VMEM((length, PAIR), F32),
            pltpu.VMEM((length, PAIR), F32),
        ],
    )
    area = pairs * 2 * length * length // 2
    return pl.pallas_call(
        functools.partial(attend_back_kernel, count, slots, tok, tile_q, tile_k),
        out_shape=[jax.ShapeDtypeStruct((3, width, span), BF16)] * count,
        grid_spec=grid_spec,
        compiler_params=pltpu.CompilerParams(
            dimension_semantics=("arbitrary",), vmem_limit_bytes=56 * MIB
        ),
        cost_estimate=pl.CostEstimate(
            flops=area * 2560, bytes_accessed=16 * width * length, transcendentals=area
        ),
        name="attend_back",
    )(order, *pieces, *mixes, *grads, lse, cosine, sine)


def nt(a, b):
    return lax.dot_general(a, b, (((1,), (1,)), ((), ())), preferred_element_type=F32)


def whole_block(shape):
    zeros = (0,) * len(shape)
    return pl.BlockSpec(shape, lambda *_: zeros)


def parameters(mib):
    return pltpu.CompilerParams(dimension_semantics=("arbitrary",), vmem_limit_bytes=mib * MIB)


def project_kernel(slots, tok, count, rows, place, *refs):
    xs, firsts = refs[:slots], refs[slots : 2 * slots]
    own = refs[2 * slots : 2 * slots + count]
    other = refs[2 * slots + count : 2 * slots + 2 * count]
    cos_ref, sin_ref = refs[2 * slots + 2 * count : 2 * slots + 2 * count + 2]
    other_ref, own_ref, normed_ref, full_ref, gains_ref, column = refs[2 * slots + 2 * count + 2 :]
    step = pl.program_id(0)
    target, kind = step // 3, step % 3
    core = place[1]
    half = jnp.where(target == 0, 1 - core, core)
    depth = normed_ref.shape[1]
    wide = own_ref.shape[1]

    @pl.when(step == 0)
    def _():
        for number in range(count):
            at = pl.ds(pl.multiple_of(place[2 + number] * rows, rows), rows)
            for which in range(3):
                columns = slice(which * wide, (which + 1) * wide)
                full_ref[core, which, at, :] = own[number][:, columns]
                full_ref[1 - core, which, at, :] = other[number][:, columns]
            column[at, :] = own[number][:, 3 * wide :]
        gains_ref[...] = column[...].T[:8].astype(F32)
        gain = gains_ref[0:1, :]
        for slot in range(slots):
            values = xs[slot][...].reshape(tok, depth).astype(F32)
            scale = lax.rsqrt(jnp.mean(values * values, axis=1, keepdims=True) + epsilon)
            normed_ref[slot * tok : (slot + 1) * tok, :] = (values * scale * gain).astype(BF16)

    weight = full_ref[half, kind]
    raw = nt(weight.T, normed_ref[...])

    def store(value):
        @pl.when(target == 0)
        def _():
            other_ref[0] = value

        @pl.when(target == 1)
        def _():
            own_ref[0] = value

    @pl.when(kind < 2)
    def _():
        parts = raw.reshape(wide // HEAD_DIM, 2, HALF, raw.shape[1])
        first, second = parts[:, 0], parts[:, 1]
        cosine, sine = cos_ref[...][None], sin_ref[...][None]
        turned = jnp.stack(
            [first * cosine - second * sine, first * sine + second * cosine], axis=1
        )
        store(turned.reshape(raw.shape).astype(BF16))

    @pl.when(kind == 2)
    def _():
        first = jnp.concatenate(
            [ref[...].reshape(tok, wide).T.astype(F32) for ref in firsts], axis=1
        )
        store((0.5 * raw + 0.5 * first).astype(BF16))


def project(inputs, received, firsts, firsts_received, own, other, cosine, sine, place):
    slots, tok, depth = inputs.shape
    count, rows = len(own), own[0].shape[0]
    wide = depth // 2
    span = slots * tok

    def half(s, p):
        return jnp.where(s < 3, 1 - p[1], p[1])

    x_specs = [pl.BlockSpec((1, tok, depth), lambda s, p: (p[0], 0, 0))]
    x_specs += [whole_block((tok, depth))] * (slots - 1)
    first_specs = [pl.BlockSpec((1, tok, wide), lambda s, p: (p[0], 0, half(s, p)))]
    first_specs += [pl.BlockSpec((tok, wide), lambda s, p: (0, half(s, p)))] * (slots - 1)
    grid_spec = pltpu.PrefetchScalarGridSpec(
        num_scalar_prefetch=1,
        grid=(6,),
        in_specs=x_specs
        + first_specs
        + [whole_block(own[0].shape)] * (2 * count)
        + [whole_block((HALF, span))] * 2,
        out_specs=[
            pl.BlockSpec((1, wide, span), lambda s, p: (jnp.minimum(s, 2), 0, 0)),
            pl.BlockSpec((1, wide, span), lambda s, p: (jnp.maximum(s - 3, 0), 0, 0)),
            whole_block((span, depth)),
            whole_block((2, 3, depth, wide)),
            whole_block((8, depth)),
        ],
        scratch_shapes=[pltpu.VMEM((depth, 128), BF16)],
    )
    return pl.pallas_call(
        functools.partial(project_kernel, slots, tok, count, rows),
        out_shape=[
            jax.ShapeDtypeStruct((3, wide, span), BF16),
            jax.ShapeDtypeStruct((3, wide, span), BF16),
            jax.ShapeDtypeStruct((span, depth), BF16),
            jax.ShapeDtypeStruct((2, 3, depth, wide), BF16),
            jax.ShapeDtypeStruct((8, depth), F32),
        ],
        grid_spec=grid_spec,
        compiler_params=parameters(56),
        cost_estimate=pl.CostEstimate(
            flops=6 * span * depth * depth,
            bytes_accessed=2 * (8 * span * depth + 6 * depth * depth),
            transcendentals=0,
        ),
        name="project",
    )(place, inputs, *received, firsts, *firsts_received, *own, *other, cosine, sine)


def output_kernel(slots, tok, count, rows, place, *refs):
    xs = refs[:slots]
    own = refs[slots : slots + count]
    other = refs[slots + count : slots + 2 * count]
    att_other, att_own, gains_ref = refs[slots + 2 * count : slots + 2 * count + 3]
    middle_ref, normed_ref, full_ref = refs[slots + 2 * count + 3 :]
    step = pl.program_id(0)
    core = place[1]
    wide = att_own.shape[0]
    depth = 2 * wide
    mine = pl.ds(pl.multiple_of(core * wide, wide), wide)
    others = pl.ds(pl.multiple_of((1 - core) * wide, wide), wide)

    @pl.when(step == 0)
    def _():
        for number in range(count):
            at = pl.ds(pl.multiple_of(place[2 + number] * rows, rows), rows)
            full_ref[at, mine] = own[number][...]
            full_ref[at, others] = other[number][...]

    total = dot(att_own[...].T, full_ref[mine, :]) + dot(att_other[...].T, full_ref[others, :])
    for slot in range(slots):

        @pl.when(step == slot)
        def _(slot=slot):
            middle_ref[...] = xs[slot][...].reshape(tok, depth).astype(F32) + total

    middle = middle_ref[...]
    scale = lax.rsqrt(jnp.mean(middle * middle, axis=1, keepdims=True) + epsilon)
    normed_ref[...] = (middle * scale * gains_ref[1:2, :]).astype(BF16)


def output_projection(inputs, received, own, other, att_other, att_own, gains, place):
    slots, tok, depth = inputs.shape
    count, rows = len(own), own[0].shape[0]
    wide = depth // 2
    span = slots * tok
    x_specs = [pl.BlockSpec((1, tok, depth), lambda s, p: (p[0], 0, 0))]
    x_specs += [whole_block((tok, depth))] * (slots - 1)
    grid_spec = pltpu.PrefetchScalarGridSpec(
        num_scalar_prefetch=1,
        grid=(slots,),
        in_specs=x_specs
        + [whole_block(own[0].shape)] * (2 * count)
        + [pl.BlockSpec((wide, tok), lambda s, p: (0, s))] * 2
        + [whole_block((8, depth))],
        out_specs=[
            pl.BlockSpec((tok, depth), lambda s, p: (s, 0)),
            pl.BlockSpec((tok, depth), lambda s, p: (s, 0)),
            whole_block((depth, depth)),
        ],
    )
    return pl.pallas_call(
        functools.partial(output_kernel, slots, tok, count, rows),
        out_shape=[
            jax.ShapeDtypeStruct((span, depth), F32),
            jax.ShapeDtypeStruct((span, depth), BF16),
            jax.ShapeDtypeStruct((depth, depth), BF16),
        ],
        grid_spec=grid_spec,
        compiler_params=parameters(56),
        cost_estimate=pl.CostEstimate(
            flops=2 * span * depth * depth,
            bytes_accessed=12 * span * depth + 4 * depth * depth,
            transcendentals=0,
        ),
        name="output_projection",
    )(place, inputs, *received, *own, *other, att_other, att_own, gains)


def mlp_kernel(slots, tok, count, rows, down_rows, blocks, place, *refs):
    grads = refs[:slots]
    middle_ref, normed_ref, gains_ref = refs[slots : slots + 3]
    base = slots + 3
    own_g, other_g, own_u, other_u, own_d, other_d = (
        refs[base + number * count : base + (number + 1) * count] for number in range(6)
    )
    (
        out_ref,
        send_ref,
        grad_ref,
        low_ref,
        gain_ref,
        gu_send,
        gu_keep,
        d_send,
        d_keep,
        wgu,
        wd,
        og,
        normed_t,
        acc,
        back,
        sems,
    ) = refs[base + 6 * count :]
    step = pl.program_id(0)
    core = place[1]
    depth = og.shape[1]
    wide = depth // 2
    strip = 128
    half_width = blocks * strip
    mine = pl.ds(pl.multiple_of(core * wide, wide), wide)
    others = pl.ds(pl.multiple_of((1 - core) * wide, wide), wide)

    def loads():
        copies = []
        for number in range(count):
            at = pl.ds(pl.multiple_of(place[2 + number] * rows, rows), rows)
            for which, (gate, up) in enumerate(((own_g, own_u), (other_g, other_u))):
                copies.append((gate[number], wgu.at[which, at, pl.ds(0, half_width)]))
                copies.append((up[number], wgu.at[which, at, pl.ds(half_width, half_width)]))
        for number in range(count):
            at = pl.ds(pl.multiple_of(place[2 + number] * down_rows, down_rows), down_rows)
            copies.append((own_d[number], wd.at[at, mine]))
            copies.append((other_d[number], wd.at[at, others]))
        return [
            pltpu.make_async_copy(source, target, sems.at[number])
            for number, (source, target) in enumerate(copies)
        ]

    @pl.when(step == 0)
    def _():
        copies = loads()
        for copy in copies:
            copy.start()
        for slot in range(slots):
            og[slot * tok : (slot + 1) * tok, :] = grads[slot][...].reshape(tok, depth)
        normed_t[...] = normed_ref[...].T
        acc[...] = jnp.zeros_like(acc)
        back[...] = jnp.zeros_like(back)
        for copy in copies:
            copy.wait()

    at = pl.ds(pl.multiple_of(step * strip, strip), strip)
    up_at = pl.ds(pl.multiple_of(half_width + step * strip, strip), strip)
    gate_w = jnp.concatenate([wgu[0, :, at], wgu[1, :, at]], axis=1)
    up_w = jnp.concatenate([wgu[0, :, up_at], wgu[1, :, up_at]], axis=1)
    own_rows = pl.ds(pl.multiple_of(core * half_width + step * strip, strip), strip)
    other_rows = pl.ds(pl.multiple_of((1 - core) * half_width + step * strip, strip), strip)
    down_w = jnp.concatenate([wd[own_rows, :], wd[other_rows, :]], axis=0)
    normed = normed_ref[...]
    gate = dot(normed, gate_w)
    up = dot(normed, up_w)
    grad_active = nt(og[...], down_w)
    sigma = jax.nn.sigmoid(gate)
    silu = gate * sigma
    active = (silu * up).astype(BF16)
    grad_up = (grad_active * silu).astype(BF16)
    grad_gate = (grad_active * up * sigma * (1.0 + gate * (1.0 - sigma))).astype(BF16)
    acc[...] += dot(active, down_w)
    back[...] += nt(grad_gate, gate_w) + nt(grad_up, up_w)
    grad_gate_w = dot(normed_t[...], grad_gate).astype(BF16)
    gu_keep[0] = grad_gate_w[:, :strip]
    gu_send[0] = grad_gate_w[:, strip:]
    grad_up_w = dot(normed_t[...], grad_up).astype(BF16)
    gu_keep[1] = grad_up_w[:, :strip]
    gu_send[1] = grad_up_w[:, strip:]
    active_t = active.T
    kept = dot(active_t, og[:, mine]).astype(BF16)
    sent = dot(active_t, og[:, others]).astype(BF16)
    d_keep[core] = kept[:strip]
    d_keep[1 - core] = kept[strip:]
    d_send[core] = sent[:strip]
    d_send[1 - core] = sent[strip:]

    @pl.when(step == blocks - 1)
    def _():
        gain = gains_ref[1:2, :]
        chunk = min(128, tok)
        gain_ref[...] = jnp.zeros_like(gain_ref)
        for slot in range(slots):

            def finish(number, _, slot=slot):
                local = pl.ds(pl.multiple_of(number * chunk, chunk), chunk)
                some = pl.ds(pl.multiple_of(slot * tok + number * chunk, chunk), chunk)
                middle = middle_ref[some, :]
                scale = lax.rsqrt(jnp.mean(middle * middle, axis=1, keepdims=True) + epsilon)
                result = middle + acc[some, :]
                if slot == 0:
                    out_ref[0, local, :] = result
                else:
                    send_ref[pl.ds(pl.multiple_of((slot - 1) * tok + number * chunk, chunk), chunk), :] = (
                        result.astype(BF16)
                    )
                grad = back[some, :]
                gain_ref[0:1, :] += jnp.sum(grad * middle * scale, axis=0, keepdims=True)
                weighted = grad * gain
                inner = jnp.mean(weighted * middle, axis=1, keepdims=True)
                grad_middle = (
                    scale * weighted
                    - middle * (scale * scale * scale) * inner
                    + og[some, :].astype(F32)
                )
                grad_ref[some, :] = grad_middle
                low_ref[some, :] = grad_middle.astype(BF16)
                return 0

            lax.fori_loop(0, tok // chunk, finish, 0)


def mlp(grads, grads_received, middle, normed, gains, gate, up, down, place):
    slots, tok, depth = grads.shape
    own_d, other_d = down
    count, rows = len(own_d), gate[0][0].shape[0]
    down_rows = own_d[0].shape[0]
    half_width = gate[0][0].shape[1]
    wide = depth // 2
    span = slots * tok
    blocks = half_width // 128
    once = pl.Buffered(1)
    g_specs = [pl.BlockSpec((1, tok, depth), lambda s, p: (p[0], 0, 0), pipeline_mode=once)]
    g_specs += [pl.BlockSpec((tok, depth), lambda s, p: (0, 0), pipeline_mode=once)] * (slots - 1)
    gu_spec = pl.BlockSpec((2, depth, 128), lambda s, p: (0, 0, s))
    d_spec = pl.BlockSpec((2, 128, wide), lambda s, p: (0, s, 0))
    grid_spec = pltpu.PrefetchScalarGridSpec(
        num_scalar_prefetch=1,
        grid=(blocks,),
        in_specs=g_specs
        + [
            pl.BlockSpec((span, depth), lambda s, p: (0, 0), pipeline_mode=once),
            pl.BlockSpec((span, depth), lambda s, p: (0, 0), pipeline_mode=once),
            whole_block((8, depth)),
        ]
        + [pl.BlockSpec(memory_space=pl.ANY)] * (6 * count),
        out_specs=[
            pl.BlockSpec((1, tok, depth), lambda s, p: (p[0], 0, 0), pipeline_mode=once),
            pl.BlockSpec(((slots - 1) * tok, depth), lambda s, p: (0, 0), pipeline_mode=once),
            pl.BlockSpec((span, depth), lambda s, p: (0, 0), pipeline_mode=once),
            pl.BlockSpec((span, depth), lambda s, p: (0, 0), pipeline_mode=once),
            whole_block((8, depth)),
            gu_spec,
            gu_spec,
            d_spec,
            d_spec,
        ],
        scratch_shapes=[
            pltpu.VMEM((2, depth, 2 * half_width), BF16),
            pltpu.VMEM((2 * half_width, depth), BF16),
            pltpu.VMEM((span, depth), BF16),
            pltpu.VMEM((depth, span), BF16),
            pltpu.VMEM((span, depth), F32),
            pltpu.VMEM((span, depth), F32),
            pltpu.SemaphoreType.DMA((6 * count,)),
        ],
    )
    return pl.pallas_call(
        functools.partial(mlp_kernel, slots, tok, count, rows, down_rows, blocks),
        out_shape=[
            jax.ShapeDtypeStruct((slots, tok, depth), F32),
            jax.ShapeDtypeStruct(((slots - 1) * tok, depth), BF16),
            jax.ShapeDtypeStruct((span, depth), F32),
            jax.ShapeDtypeStruct((span, depth), BF16),
            jax.ShapeDtypeStruct((8, depth), F32),
            jax.ShapeDtypeStruct((2, depth, half_width), BF16),
            jax.ShapeDtypeStruct((2, depth, half_width), BF16),
            jax.ShapeDtypeStruct((2, half_width, wide), BF16),
            jax.ShapeDtypeStruct((2, half_width, wide), BF16),
        ],
        grid_spec=grid_spec,
        compiler_params=parameters(63),
        cost_estimate=pl.CostEstimate(
            flops=16 * span * depth * 2 * half_width,
            bytes_accessed=24 * depth * half_width + 20 * span * depth,
            transcendentals=2 * span * half_width,
        ),
        name="mlp",
    )(
        place,
        grads,
        *grads_received,
        middle,
        normed,
        gains,
        *gate[0],
        *gate[1],
        *up[0],
        *up[1],
        *own_d,
        *other_d,
    )


def grad_attended_kernel(place, low_ref, full_ref, att_other, att_own, ga_other, ga_own, sent, kept):
    step = pl.program_id(0)
    core = place[1]
    wide = att_own.shape[0]
    mine = pl.ds(pl.multiple_of(core * wide, wide), wide)
    others = pl.ds(pl.multiple_of((1 - core) * wide, wide), wide)
    for number, (att, result) in enumerate(((att_other, ga_other), (att_own, ga_own))):

        @pl.when(step == number)
        def _(att=att, result=result):
            result[...] = nt(full_ref[...], low_ref[...]).astype(BF16)
            kept[...] = dot(att[...], low_ref[:, mine]).astype(BF16)
            sent[...] = dot(att[...], low_ref[:, others]).astype(BF16)


def grad_attended(low, full, att_other, att_own, place):
    span, depth = low.shape
    wide = depth // 2

    def half(s, p):
        return jnp.where(s == 0, 1 - p[1], p[1])

    row_spec = pl.BlockSpec((wide, wide), lambda s, p: (half(s, p), 0))
    grid_spec = pltpu.PrefetchScalarGridSpec(
        num_scalar_prefetch=1,
        grid=(2,),
        in_specs=[
            whole_block((span, depth)),
            pl.BlockSpec((wide, depth), lambda s, p: (half(s, p), 0)),
            whole_block((wide, span)),
            whole_block((wide, span)),
        ],
        out_specs=[whole_block((wide, span)), whole_block((wide, span)), row_spec, row_spec],
    )
    return pl.pallas_call(
        grad_attended_kernel,
        out_shape=[
            jax.ShapeDtypeStruct((wide, span), BF16),
            jax.ShapeDtypeStruct((wide, span), BF16),
            jax.ShapeDtypeStruct((depth, wide), BF16),
            jax.ShapeDtypeStruct((depth, wide), BF16),
        ],
        grid_spec=grid_spec,
        compiler_params=parameters(48),
        cost_estimate=pl.CostEstimate(
            flops=4 * span * depth * depth,
            bytes_accessed=6 * span * depth + 4 * depth * depth,
            transcendentals=0,
        ),
        name="grad_attended",
    )(place, low, full, att_other, att_own)


def tail_kernel(slots, tok, place, *refs):
    xs = refs[:slots]
    (
        back_other,
        back_own,
        full_ref,
        normed_ref,
        grad_ref,
        gains_ref,
        mlp_gain_ref,
        out_ref,
        send_ref,
        first_ref,
        first_send,
        gain_ref,
        sent,
        kept,
        normed_t,
        acc,
    ) = refs[slots:]
    step = pl.program_id(0)
    target, kind = step // 3, step % 3
    depth = acc.shape[1]

    @pl.when(step == 0)
    def _():
        normed_t[...] = normed_ref[...].T
        acc[...] = jnp.zeros_like(acc)

    def part(back, result):
        grad = back[0]

        @pl.when(kind == 2)
        def _():
            rows = 0.5 * grad.astype(F32).T
            first_ref[0] = rows[:tok]
            first_send[...] = rows[tok:].astype(BF16)

        grad = grad * jnp.where(kind == 2, 0.5, 1.0).astype(BF16)
        acc[...] += nt(grad.T, full_ref[0, 0])
        result[0] = nt(normed_t[...], grad).astype(BF16)

    @pl.when(target == 0)
    def _():
        part(back_other, sent)

    @pl.when(target == 1)
    def _():
        part(back_own, kept)

    @pl.when(step == 5)
    def _():
        gain = gains_ref[0:1, :]
        chunk = min(128, tok)
        gain_ref[...] = jnp.zeros_like(gain_ref)
        gain_ref[1:2, :] = mlp_gain_ref[0:1, :]
        for slot in range(slots):

            def finish(number, _, slot=slot):
                local = pl.ds(pl.multiple_of(number * chunk, chunk), chunk)
                some = pl.ds(pl.multiple_of(slot * tok + number * chunk, chunk), chunk)
                if slot == 0:
                    values = xs[slot][0, local, :].astype(F32)
                else:
                    values = xs[slot][local, :].astype(F32)
                scale = lax.rsqrt(jnp.mean(values * values, axis=1, keepdims=True) + epsilon)
                grad = acc[some, :]
                gain_ref[0:1, :] += jnp.sum(grad * values * scale, axis=0, keepdims=True)
                weighted = grad * gain
                inner = jnp.mean(weighted * values, axis=1, keepdims=True)
                result = (
                    scale * weighted
                    - values * (scale * scale * scale) * inner
                    + grad_ref[some, :]
                )
                if slot == 0:
                    out_ref[0, local, :] = result
                else:
                    send_ref[pl.ds(pl.multiple_of((slot - 1) * tok + number * chunk, chunk), chunk), :] = (
                        result.astype(BF16)
                    )
                return 0

            lax.fori_loop(0, tok // chunk, finish, 0)


def tail(inputs, received, back_other, back_own, full, normed, grad_middle, gains, mlp_gain, place):
    slots, tok, depth = inputs.shape
    wide = depth // 2
    span = slots * tok
    rest = (slots - 1) * tok
    once = pl.Buffered(1)

    def half(s, p):
        return jnp.where(s < 3, 1 - p[1], p[1])

    x_specs = [pl.BlockSpec((1, tok, depth), lambda s, p: (p[0], 0, 0))]
    x_specs += [whole_block((tok, depth))] * (slots - 1)
    grid_spec = pltpu.PrefetchScalarGridSpec(
        num_scalar_prefetch=1,
        grid=(6,),
        in_specs=x_specs
        + [
            pl.BlockSpec((1, wide, span), lambda s, p: (jnp.minimum(s, 2), 0, 0)),
            pl.BlockSpec((1, wide, span), lambda s, p: (jnp.maximum(s - 3, 0), 0, 0)),
            pl.BlockSpec((1, 1, depth, wide), lambda s, p: (half(s, p), s % 3, 0, 0)),
            whole_block((span, depth)),
            pl.BlockSpec((span, depth), lambda s, p: (0, 0), pipeline_mode=once),
            whole_block((8, depth)),
            whole_block((8, depth)),
        ],
        out_specs=[
            pl.BlockSpec((1, tok, depth), lambda s, p: (p[0], 0, 0)),
            whole_block((rest, depth)),
            pl.BlockSpec((1, tok, wide), lambda s, p: (p[0], 0, half(s, p))),
            pl.BlockSpec((rest, wide), lambda s, p: (0, half(s, p))),
            whole_block((8, depth)),
            pl.BlockSpec((1, depth, wide), lambda s, p: (jnp.minimum(s, 2), 0, 0)),
            pl.BlockSpec((1, depth, wide), lambda s, p: (jnp.maximum(s - 3, 0), 0, 0)),
        ],
        scratch_shapes=[pltpu.VMEM((depth, span), BF16), pltpu.VMEM((span, depth), F32)],
    )
    return pl.pallas_call(
        functools.partial(tail_kernel, slots, tok),
        out_shape=[
            jax.ShapeDtypeStruct((slots, tok, depth), F32),
            jax.ShapeDtypeStruct((rest, depth), BF16),
            jax.ShapeDtypeStruct((slots, tok, depth), F32),
            jax.ShapeDtypeStruct((rest, depth), BF16),
            jax.ShapeDtypeStruct((8, depth), F32),
            jax.ShapeDtypeStruct((3, depth, wide), BF16),
            jax.ShapeDtypeStruct((3, depth, wide), BF16),
        ],
        grid_spec=grid_spec,
        compiler_params=parameters(60),
        cost_estimate=pl.CostEstimate(
            flops=12 * span * depth * depth,
            bytes_accessed=24 * span * depth + 12 * depth * depth,
            transcendentals=0,
        ),
        name="tail",
    )(
        place, inputs, *received, back_other, back_own, full, normed, grad_middle, gains, mlp_gain
    )


def land_kernel(place, whole_ref, part_ref, out_ref):
    out_ref[0] = part_ref[...].astype(F32)


def land(whole, part, slot):
    _, tok, depth = whole.shape
    tile = min(256, tok)
    grid_spec = pltpu.PrefetchScalarGridSpec(
        num_scalar_prefetch=1,
        grid=(tok // tile,),
        in_specs=[
            pl.BlockSpec(memory_space=pl.ANY),
            pl.BlockSpec((tile, depth), lambda s, p: (s, 0)),
        ],
        out_specs=pl.BlockSpec((1, tile, depth), lambda s, p: (p[0], s, 0)),
    )
    return pl.pallas_call(
        land_kernel,
        out_shape=jax.ShapeDtypeStruct(whole.shape, F32),
        grid_spec=grid_spec,
        input_output_aliases={1: 0},
        compiler_params=parameters(16),
        cost_estimate=pl.CostEstimate(
            flops=tok * depth, bytes_accessed=6 * tok * depth, transcendentals=0
        ),
        name="land",
    )(slot, whole, part)


MESH = pl.DeviceIdType.MESH


def seats():
    shard = lax.axis_index("fsdp")
    seat = lax.axis_index("seq")
    return (shard // 2, shard % 2, seat // 2, seat % 2)


def meet(line, keys):
    shard = lax.axis_index("fsdp")
    seat = lax.axis_index("seq")
    partners = []
    if "z" in keys:
        partners += [{"fsdp": lax.rem(shard + 2 * jump, 2 * line)} for jump in range(1, line)]
    if "y" in keys:
        partners.append({"fsdp": shard + 1 - 2 * (shard % 2)})
    if "x" in keys:
        partners.append({"seq": lax.rem(seat + 2, 4)})
    if "diagonal" in keys:
        partners.append({"seq": 3 - seat})
    if "core" in keys:
        partners.append({"seq": seat + 1 - 2 * (seat % 2)})
    barrier = pltpu.get_barrier_semaphore()
    for partner in partners:
        pl.semaphore_signal(barrier, inc=1, device_id=partner, device_id_type=MESH)
    pl.semaphore_wait(barrier, len(partners))


def send(source, target, sems, number, partner):
    return pltpu.make_async_remote_copy(
        src_ref=source,
        dst_ref=target,
        send_sem=sems.at[0, number],
        recv_sem=sems.at[1, number],
        device_id=partner,
        device_id_type=MESH,
    )


def to_core_partner():
    seat = lax.axis_index("seq")
    return {"seq": seat + 1 - 2 * (seat % 2)}


def to_x_partner():
    return {"seq": lax.rem(lax.axis_index("seq") + 2, 4)}


def to_y_partner():
    shard = lax.axis_index("fsdp")
    return {"fsdp": shard + 1 - 2 * (shard % 2)}


def to_z_partner(line, jump):
    return {"fsdp": lax.rem(lax.axis_index("fsdp") + 2 * jump, 2 * line)}


class Gather:
    def __init__(self, line, shard, own, other, sems, share=0, columns=None):
        self.line, self.shard, self.own, self.other = line, shard, own, other
        self.sems = sems
        z, y, x, core = seats()
        self.z, self.y, self.share = z, y, share
        rows, width = own.shape[2:]
        first, size = columns or (0, width)
        self.columns = pl.ds(first, size)
        if shard.shape[1] == width:
            self.source = self.columns
        else:
            self.source = pl.ds(pl.multiple_of(core * width + first, 128), size)
        if share:
            step = math.gcd(share, rows)
            self.rows = pl.ds(pl.multiple_of(x * share, step), rows - share)
            self.given = pl.ds(pl.multiple_of(x * (rows - share), step), share)
            self.taken = pl.ds(pl.multiple_of((1 - x) * (rows - share), step), share)
        else:
            self.rows = slice(None)

    def here(self):
        return pltpu.make_async_copy(
            self.shard.at[self.rows, self.source],
            self.own.at[self.z, self.y, self.rows, self.columns],
            self.sems.at[0, self.line + 3],
        )

    def along_z(self):
        return [
            send(
                self.shard.at[self.rows, self.source],
                self.own.at[self.z, self.y, self.rows, self.columns],
                self.sems,
                jump - 1,
                to_z_partner(self.line, jump),
            )
            for jump in range(1, self.line)
        ]

    def along_y(self):
        part = self.own.at[:, self.y, self.rows, self.columns]
        return send(part, part, self.sems, self.line - 1, to_y_partner())

    def along_x(self):
        part = self.own.at[:, :, self.given, self.columns]
        return send(part, part, self.sems, self.line, to_x_partner())

    def to_core(self, late):
        if self.share:
            at = (slice(None), slice(None), self.taken if late else self.rows, self.columns)
        else:
            at = (slice(None), 1 - self.y if late else self.y, slice(None), self.columns)
        return send(
            self.own.at[at],
            self.other.at[at],
            self.sems,
            self.line + 1 + late,
            to_core_partner(),
        )

    def start_z(self):
        self.here().start()
        for copy in self.along_z():
            copy.start()

    def wait_z(self):
        self.here().wait()
        for copy in self.along_z():
            copy.wait()

    def wait_core(self):
        self.to_core(0).wait()
        self.to_core(1).wait()


def gather_sems(line):
    return pltpu.SemaphoreType.DMA((2, line + 4))


def front_kernel(line, tok, *refs):
    (
        inputs,
        firsts,
        grads,
        q_shard,
        k_shard,
        v_shard,
        o_shard,
        d_shard,
        gains_shard,
        cos_ref,
        sin_ref,
        x_received,
        f_received,
        g_received,
        heads_own,
        heads_received,
        normed_ref,
        full_ref,
        gains_ref,
        o_own,
        o_other,
        d_own,
        xs,
        fs,
        q_own,
        q_other,
        k_own,
        k_other,
        v_own,
        v_other,
        outgoing,
        all_gains,
        q_sems,
        k_sems,
        v_sems,
        w_sems,
        o_sems,
        d_sems,
        gain_sems,
        swap_sems,
        head_sems,
        local_sems,
    ) = refs
    step = pl.program_id(0)
    _, _, side, core = seats()
    wide = outgoing.shape[1]
    depth = 2 * wide
    gathers = [
        Gather(line, q_shard, q_own, q_other, q_sems),
        Gather(line, k_shard, k_own, k_other, k_sems),
        Gather(line, v_shard, v_own, v_other, v_sems, columns=(0, wide // 2)),
        Gather(line, v_shard, v_own, v_other, w_sems, columns=(wide // 2, wide // 2)),
    ]
    query, key, value, value_more = gathers
    gains = Gather(line, gains_shard, all_gains, all_gains, gain_sems)
    out = Gather(line, o_shard, o_own, o_other, o_sems)
    down = Gather(line, d_shard, d_own, d_own, d_sems, d_own.shape[2] // 2)
    swap_x = send(inputs.at[1 - side], x_received, swap_sems, 0, to_x_partner())
    swap_f = send(firsts.at[1 - side], f_received, swap_sems, 1, to_x_partner())
    early = pl.ds(0, tok // 2)
    swap_g = send(
        grads.at[1 - side, early], g_received.at[early], swap_sems, 2, to_x_partner()
    )
    load_x = pltpu.make_async_copy(inputs.at[side], xs.at[pl.ds(0, tok), :], local_sems.at[0])
    load_f = pltpu.make_async_copy(firsts.at[side], fs.at[pl.ds(0, tok), :], local_sems.at[1])
    more_x = pltpu.make_async_copy(x_received, xs.at[pl.ds(tok, tok), :], local_sems.at[2])
    more_f = pltpu.make_async_copy(f_received, fs.at[pl.ds(tok, tok), :], local_sems.at[3])

    def weight(halves, columns):
        return halves[:, :, :, columns].reshape(depth, wide)

    def heads(number):
        return send(
            outgoing.at[number], heads_received.at[number], head_sems, number, to_core_partner()
        )

    saves = []
    for number, (mine, others) in enumerate(((q_own, q_other), (k_own, k_other), (v_own, v_other))):
        for which, ref in ((0, mine), (1, others)):
            half = core if which == 0 else 1 - core
            saves.append(
                pltpu.make_async_copy(
                    ref.at[:, :, :, pl.ds(0, wide)],
                    full_ref.at[half, number],
                    local_sems.at[4 + 2 * number + which],
                )
            )

    @pl.when(step == 0)
    def _():
        meet(line, ("z", "y", "x", "core"))
        swap_x.start()
        load_x.start()
        load_f.start()
        gains.start_z()
        query.start_z()
        gains.wait_z()
        gains.along_y().start()
        query.wait_z()
        query.along_y().start()
        query.to_core(0).start()
        key.start_z()
        key.wait_z()
        key.along_y().start()
        key.to_core(0).start()
        value.start_z()
        swap_x.wait()
        more_x.start()
        swap_f.start()
        gains.along_y().wait()
        query.along_y().wait()
        query.to_core(1).start()
        for number in range(2 * line):
            columns = slice(number * 128, (number + 1) * 128)
            gains_ref[:, columns] = all_gains[number // 2, number % 2]
        gain = gains_ref[0:1, :]
        chunk = min(256, 2 * tok)
        load_x.wait()
        more_x.wait()

        def norm(number, _):
            at = pl.ds(pl.multiple_of(number * chunk, chunk), chunk)
            values = xs[at, :].astype(F32)
            scale = lax.rsqrt(jnp.mean(values * values, axis=1, keepdims=True) + epsilon)
            normed_ref[at, :] = (values * scale * gain).astype(BF16)
            return 0

        lax.fori_loop(0, 2 * tok // chunk, norm, 0)
        value.wait_z()
        value.along_y().start()
        value.to_core(0).start()
        value_more.start_z()

    @pl.when(step == 1)
    def _():
        key.along_y().wait()
        key.to_core(1).start()
        value_more.wait_z()
        value_more.along_y().start()
        value_more.to_core(0).start()
        out.start_z()

    @pl.when(step == 2)
    def _():
        swap_f.wait()
        more_f.start()
        swap_g.start()
        value.along_y().wait()
        value.to_core(1).start()
        value_more.along_y().wait()
        value_more.to_core(1).start()
        out.wait_z()
        out.along_y().start()
        out.to_core(0).start()
        down.start_z()
        load_f.wait()
        more_f.wait()

    @pl.when(step == 3)
    def _():
        query.wait_core()
        key.wait_core()
        for save in saves[:4]:
            save.start()

    @pl.when(step == 5)
    def _():
        value.wait_core()
        value_more.wait_core()
        for save in saves[4:]:
            save.start()
        out.along_y().wait()
        out.to_core(1).start()

    def project_one(halves, kind, mine):
        raw = nt(weight(halves, slice(0, wide)).T, normed_ref[...])
        if kind < 2:
            parts = raw.reshape(wide // HEAD_DIM, 2, HALF, raw.shape[1])
            first, second = parts[:, 0], parts[:, 1]
            cosine, sine = (
                jnp.concatenate([ref[:, block_of(1, slot, tok)] for slot in range(2)], axis=1)[None]
                for ref in (cos_ref, sin_ref)
            )
            turned = jnp.stack(
                [first * cosine - second * sine, first * sine + second * cosine], axis=1
            )
            result = turned.reshape(raw.shape).astype(BF16)
        else:
            half = core if mine else 1 - core
            first = fs[:, pl.ds(pl.multiple_of(half * wide, wide), wide)]
            result = (0.5 * raw + 0.5 * first.astype(F32).T).astype(BF16)
        if mine:
            heads_own[0] = result
        else:
            outgoing[kind] = result
            heads(kind).start()

    for number, (halves, kind, mine) in enumerate(
        (
            (q_own, 0, True),
            (k_own, 1, True),
            (v_own, 2, True),
            (q_other, 0, False),
            (k_other, 1, False),
            (v_other, 2, False),
        )
    ):

        @pl.when(step == number)
        def _(halves=halves, kind=kind, mine=mine):
            project_one(halves, kind, mine)

    @pl.when(step == 5)
    def _():
        for number in range(3):
            heads(number).wait()
        for save in saves:
            save.wait()
        out.wait_core()
        down.wait_z()
        swap_g.wait()


def front(inputs, firsts, grads, q, k, v, o, d, gains, cosine, sine, line):
    slots, tok, depth = inputs.shape
    span = slots * tok
    wide = depth // 2
    rows, down_rows = q.shape[0], d.shape[0]
    anywhere = pl.BlockSpec(memory_space=pl.ANY)
    weights = lambda columns: pltpu.VMEM((line, 2, rows, columns), BF16)
    return pl.pallas_call(
        functools.partial(front_kernel, line, tok),
        grid=(6,),
        in_specs=[anywhere] * 9 + [whole_block(cosine.shape)] * 2,
        out_specs=[
            anywhere,
            anywhere,
            anywhere,
            pl.BlockSpec((1, wide, span), lambda s: (jnp.minimum(s, 2), 0, 0)),
            anywhere,
            whole_block((span, depth)),
            anywhere,
            whole_block((8, depth)),
            anywhere,
            anywhere,
            anywhere,
        ],
        out_shape=[
            jax.ShapeDtypeStruct((tok, depth), BF16),
            jax.ShapeDtypeStruct((tok, depth), BF16),
            jax.ShapeDtypeStruct((tok, depth), BF16),
            jax.ShapeDtypeStruct((3, wide, span), BF16),
            jax.ShapeDtypeStruct((3, wide, span), BF16),
            jax.ShapeDtypeStruct((span, depth), BF16),
            jax.ShapeDtypeStruct((2, 3, line, 2, rows, wide), BF16),
            jax.ShapeDtypeStruct((8, depth), F32),
            jax.ShapeDtypeStruct((line, 2, rows, wide), BF16),
            jax.ShapeDtypeStruct((line, 2, rows, wide), BF16),
            jax.ShapeDtypeStruct((line, 2, down_rows, wide), BF16),
        ],
        scratch_shapes=[
            pltpu.VMEM((span, depth), BF16),
            pltpu.VMEM((span, depth), BF16),
            weights(wide),
            weights(wide),
            weights(wide),
            weights(wide),
            weights(wide),
            weights(wide),
            pltpu.VMEM((3, wide, span), BF16),
            pltpu.VMEM((line, 2, 8, 128), F32),
        ]
        + [gather_sems(line)] * 7
        + [
            pltpu.SemaphoreType.DMA((2, 3)),
            pltpu.SemaphoreType.DMA((2, 3)),
            pltpu.SemaphoreType.DMA((10,)),
        ],
        compiler_params=pltpu.CompilerParams(
            dimension_semantics=("arbitrary",),
            vmem_limit_bytes=63 * MIB,
            collective_id=1,
            has_side_effects=True,
        ),
        cost_estimate=pl.CostEstimate(
            flops=6 * span * depth * depth,
            bytes_accessed=2 * (8 * span * depth + 6 * depth * depth),
            transcendentals=0,
        ),
        name="front",
    )(inputs, firsts, grads, q, k, v, o, d, gains, cosine, sine)


def block_of(source, slot, tok):
    _, _, side, core = seats()
    rank = 1 - core if source == 0 else core
    group = lax.rem(side + slot, 2)
    return pl.ds(pl.multiple_of((group * 2 + rank) * tok, tok), tok)


def attend_carry_kernel(line, tok, tile_k, *refs):
    (
        received,
        own,
        inputs,
        x_received,
        gains_ref,
        o_own,
        o_other,
        grad_in,
        _,
        d_in,
        g_shard,
        u_shard,
        mix_received,
        mix_own,
        lse_ref,
        middle_ref,
        normed_ref,
        full_ref,
        att_other,
        grad_received,
        d_own,
        d_other,
        g_own,
        g_other,
        u_own,
        u_other,
        qz,
        kn,
        vt,
        ot,
        outgoing,
        att_mine,
        att_theirs,
        xs,
        d_sems,
        g_sems,
        u_sems,
        v_sems,
        swap_sems,
        att_sems,
        local_sems,
    ) = refs
    step = pl.program_id(0)
    pairs = pl.num_programs(0)
    _, _, side, core = seats()
    rows, columns = g_own.shape[2:]
    first = columns // 256 * 128
    down = Gather(line, d_in, d_own, d_other, d_sems, d_own.shape[2] // 2)
    gate = Gather(line, g_shard, g_own, g_other, g_sems, rows * 3 // 8)
    up = Gather(line, u_shard, u_own, u_other, u_sems, columns=(0, first))
    up_more = Gather(line, u_shard, u_own, u_other, v_sems, columns=(first, columns - first))
    late = pl.ds(tok // 2, tok - tok // 2)
    swap = send(grad_in.at[1 - side, late], grad_received.at[late], swap_sems, 0, to_x_partner())
    depth = xs.shape[1]
    wide = depth // 2
    mine = pl.ds(pl.multiple_of(core * wide, wide), wide)
    others = pl.ds(pl.multiple_of((1 - core) * wide, wide), wide)
    loads = [
        pltpu.make_async_copy(source, place, local_sems.at[number])
        for number, (source, place) in enumerate(
            (
                (inputs.at[side], xs.at[pl.ds(0, tok), :]),
                (x_received, xs.at[pl.ds(tok, tok), :]),
                (o_own, full_ref.at[:, mine]),
                (o_other, full_ref.at[:, others]),
            )
        )
    ]
    save_att = pltpu.make_async_copy(att_theirs, att_other, local_sems.at[4])
    pieces = (received, own)

    def hand_over(number):
        rows = pl.ds(number * PAIR, PAIR)
        return send(
            outgoing.at[rows, :], att_theirs.at[rows, :], att_sems, number, to_core_partner()
        )

    @pl.when(step == 0)
    def _():
        meet(line, ("z", "y", "x", "core"))
        down.along_y().start()
        gate.start_z()
        swap.start()

    @pl.when(step == 2)
    def _():
        down.along_y().wait()
        down.along_x().start()
        down.to_core(0).start()
        gate.wait_z()
        gate.along_y().start()
        up.start_z()
        for load in loads:
            load.start()

    for source in range(2):
        for slot in range(2):
            cols = block_of(source, slot, tok)
            take = slice(slot * tok, (slot + 1) * tok)
            query = pieces[source][0, :, take] * jnp.asarray(HEAD_DIM**-0.5, BF16)
            for head in range(2):
                qz[head, :, cols] = head_rows(query, head)
            kn[cols, :] = pieces[source][1, :, take].T
            vt[:, cols] = pieces[source][2, :, take]
    attend_body(4 * tok, tile_k, qz, kn, vt, ot, lse_ref)
    for slot in range(2):
        take = slice(slot * tok, (slot + 1) * tok)
        theirs = ot[:, block_of(0, slot, tok)]
        mix_received[:, take] = theirs
        for number in range(4):

            @pl.when(step == number)
            def _(number=number, theirs=theirs, take=take):
                outgoing[number * PAIR : (number + 1) * PAIR, take] = theirs

        ours = ot[:, block_of(1, slot, tok)]
        mix_own[:, take] = ours
        for number in range(4):

            @pl.when(step == number)
            def _(number=number, ours=ours, take=take):
                att_mine[number * PAIR : (number + 1) * PAIR, take] = ours

    for number in range(4):

        @pl.when(step == number)
        def _(number=number):
            hand_over(number).start()

    @pl.when(step == pairs - 1)
    def _():
        up.wait_z()
        up.along_y().start()
        up.to_core(0).start()
        up_more.start_z()
        gate.along_y().wait()
        gate.to_core(0).start()
        down.along_x().wait()
        gate.along_x().start()
        down.to_core(1).start()
        up_more.wait_z()
        up_more.along_y().start()
        up_more.to_core(0).start()
        for number in range(4):
            hand_over(number).wait()
        save_att.start()
        for load in loads:
            load.wait()
        for slot in range(2):
            take = slice(slot * tok, (slot + 1) * tok)
            total = dot(att_mine[:, take].T, full_ref[mine, :])
            total = total + dot(att_theirs[:, take].T, full_ref[others, :])
            middle = xs[take, :].astype(F32) + total
            middle_ref[take, :] = middle
            scale = lax.rsqrt(jnp.mean(middle * middle, axis=1, keepdims=True) + epsilon)
            normed_ref[take, :] = (middle * scale * gains_ref[1:2, :]).astype(BF16)
        up.along_y().wait()
        up.to_core(1).start()
        up_more.along_y().wait()
        up_more.to_core(1).start()
        gate.along_x().wait()
        gate.to_core(1).start()
        swap.wait()
        for gather in (down, up, up_more, gate):
            gather.wait_core()
        save_att.wait()


def attend_carry(
    received, own, inputs, x_received, gains, o_own, o_other, grads, g_received, d_own, gate, up, line
):
    _, width, span = own.shape
    tok = span // 2
    length = 2 * span
    pairs = width // PAIR
    rows, down_rows = gate.shape[0], d_own.shape[2]
    depth = grads.shape[2]
    anywhere = pl.BlockSpec(memory_space=pl.ANY)
    triple = pl.BlockSpec((3, PAIR, span), lambda p: (0, p, 0))
    single = pl.BlockSpec((PAIR, span), lambda p: (p, 0))
    whole_gate = jax.ShapeDtypeStruct((line, 2, rows, gate.shape[1] // 2), BF16)
    whole_down = jax.ShapeDtypeStruct((line, 2, down_rows, d_own.shape[3]), BF16)
    area = pairs * 2 * length * length // 2
    return pl.pallas_call(
        functools.partial(attend_carry_kernel, line, tok, min(256, length)),
        grid=(pairs,),
        in_specs=[triple, triple]
        + [anywhere] * 2
        + [whole_block((8, depth))]
        + [anywhere] * 7,
        out_specs=[single, single, pl.BlockSpec((1, 8, length), lambda p: (p, 0, 0))]
        + [
            pl.BlockSpec(shape, lambda p: (0, 0), pipeline_mode=pl.Buffered(1))
            for shape in ((span, depth), (span, depth), (depth, depth))
        ]
        + [anywhere] * 8,
        out_shape=[
            jax.ShapeDtypeStruct((width, span), BF16),
            jax.ShapeDtypeStruct((width, span), BF16),
            jax.ShapeDtypeStruct((pairs, 8, length), F32),
            jax.ShapeDtypeStruct((span, depth), F32),
            jax.ShapeDtypeStruct((span, depth), BF16),
            jax.ShapeDtypeStruct((depth, depth), BF16),
            jax.ShapeDtypeStruct((width, span), BF16),
            jax.ShapeDtypeStruct((tok, depth), BF16),
            whole_down,
            whole_down,
            whole_gate,
            whole_gate,
            whole_gate,
            whole_gate,
        ],
        scratch_shapes=[
            pltpu.VMEM((2, PAIR, length), BF16),
            pltpu.VMEM((length, PAIR), BF16),
            pltpu.VMEM((PAIR, length), BF16),
            pltpu.VMEM((PAIR, length), BF16),
            pltpu.VMEM((width, span), BF16),
            pltpu.VMEM((width, span), BF16),
            pltpu.VMEM((width, span), BF16),
            pltpu.VMEM((span, depth), BF16),
        ]
        + [gather_sems(line)] * 4
        + [
            pltpu.SemaphoreType.DMA((2, 1)),
            pltpu.SemaphoreType.DMA((2, 4)),
            pltpu.SemaphoreType.DMA((5,)),
        ],
        input_output_aliases={8: 7, 9: 8},
        compiler_params=pltpu.CompilerParams(
            dimension_semantics=("arbitrary",),
            vmem_limit_bytes=63 * MIB,
            collective_id=2,
            has_side_effects=True,
        ),
        cost_estimate=pl.CostEstimate(
            flops=area * 1024, bytes_accessed=8 * width * length, transcendentals=area
        ),
        name="attend_carry",
    )(
        received,
        own,
        inputs,
        x_received,
        gains,
        o_own,
        o_other,
        grads,
        g_received,
        d_own,
        gate,
        up,
    )


LATE = 2


def mlp_carry_kernel(line, tok, blocks, *refs):
    (
        grads,
        grads_received,
        middle_ref,
        normed_ref,
        gains_ref,
        g_own,
        g_other,
        u_own,
        u_other,
        d_own_own,
        d_own_other,
        d_other_own,
        d_other_other,
        out_ref,
        send_ref,
        grad_ref,
        low_ref,
        gain_ref,
        gu_ref,
        d_ref,
        gu_y,
        gu_late,
        og,
        normed_t,
        acc,
        back,
        gu_kept,
        d_kept,
        gu_sent,
        d_sent,
        gu_landed,
        d_landed,
        gu_outgoing,
        down_full,
        local_sems,
        gu_sends,
        gu_recvs,
        d_sends,
        d_recvs,
        y_sems,
    ) = refs
    step = pl.program_id(0)
    _, y, side, core = seats()
    depth = og.shape[1]
    wide = depth // 2
    strip = 128
    rows = gu_kept.shape[4]
    mine = pl.ds(pl.multiple_of(core * wide, wide), wide)
    others = pl.ds(pl.multiple_of((1 - core) * wide, wide), wide)

    def core_copies(number):
        slot = lax.rem(number, 2)
        return [
            pltpu.make_async_remote_copy(
                src_ref=source.at[slot],
                dst_ref=target.at[number],
                send_sem=sends.at[slot],
                recv_sem=recvs.at[number],
                device_id=to_core_partner(),
                device_id_type=MESH,
            )
            for source, target, sends, recvs in (
                (gu_sent, gu_landed, gu_sends, gu_recvs),
                (d_sent, d_landed, d_sends, d_recvs),
            )
        ]

    def y_copy(number):
        return send(gu_outgoing.at[number], gu_y.at[number], y_sems, number, to_y_partner())

    def leave(late):
        return pltpu.make_async_copy(
            gu_outgoing.at[blocks - LATE + late], gu_late.at[late], local_sems.at[2 + late]
        )

    @pl.when(step == 0)
    def _():
        meet(line, ("y", "core"))
        loads = [
            pltpu.make_async_copy(grads.at[side], og.at[pl.ds(0, tok), :], local_sems.at[0]),
            pltpu.make_async_copy(grads_received, og.at[pl.ds(tok, tok), :], local_sems.at[1]),
        ]
        for load in loads:
            load.start()
        normed_t[...] = normed_ref[...].T
        acc[...] = jnp.zeros_like(acc)
        back[...] = jnp.zeros_like(back)
        for load in loads:
            load.wait()

    @pl.when(step < blocks)
    def _():
        slot = lax.rem(step, 2)
        gate_w = jnp.concatenate([g_own[...], g_other[...]], axis=1)
        up_w = jnp.concatenate([u_own[...], u_other[...]], axis=1)
        for number, pair in enumerate(
            ((d_own_own, d_own_other), (d_other_own, d_other_other))
        ):
            at = pl.ds(number * strip, strip)
            down_full[at, mine] = pair[0][...]
            down_full[at, others] = pair[1][...]
        down_w = down_full[...]
        both_w = jnp.concatenate([gate_w, up_w], axis=1)
        span = og.shape[0]
        size = span // 2

        def products(at):
            both = dot(normed_ref[at, :], both_w)
            return (both[:, : 2 * strip], both[:, 2 * strip :], nt(og[at, :], down_w))

        def bend(gate, up, grad_active):
            sigma = jax.nn.sigmoid(gate)
            silu = gate * sigma
            turned = grad_active * up * sigma * (1.0 + gate * (1.0 - sigma))
            grad_both = jnp.concatenate([turned.astype(BF16), (grad_active * silu).astype(BF16)], axis=1)
            return ((silu * up).astype(BF16), grad_both)

        def spread(at, active, grad_both):
            acc[at, :] += dot(active, down_w)
            back[at, :] += nt(grad_both, both_w)

        pieces = [slice(n * size, (n + 1) * size) for n in range(2)]
        bent = []
        ahead = products(pieces[0])
        for number, at in enumerate(pieces):
            now = ahead
            if number + 1 < len(pieces):
                ahead = products(pieces[number + 1])
            bent.append(bend(*now))
            if number:
                spread(pieces[number - 1], *bent[number - 1])
        spread(pieces[-1], *bent[-1])
        active = jnp.concatenate([one for one, _ in bent], axis=0)
        grad_both = jnp.concatenate([one for _, one in bent], axis=0)

        @pl.when(step >= 2)
        def _():
            for copy in core_copies(step - 2):
                copy.wait_send()

        shaped = dot(normed_t[...], grad_both).astype(BF16).reshape(line, 2, rows, 4 * strip)
        for number in range(2):
            base = 2 * number * strip
            gu_kept[slot, number] = shaped[..., base : base + strip]
            gu_sent[slot, number] = shaped[..., base + strip : base + 2 * strip]
        active_t = active.T
        kept = dot(active_t, og[:, mine]).astype(BF16)
        d_kept[slot, core] = kept[:strip]
        d_kept[slot, 1 - core] = kept[strip:]
        sent = dot(active_t, og[:, others]).astype(BF16)
        d_sent[slot, core] = sent[:strip]
        d_sent[slot, 1 - core] = sent[strip:]
        for copy in core_copies(step):
            copy.start()

    @pl.when(step > 0)
    def _():
        number = step - 1
        slot = lax.rem(number, 2)
        for copy in core_copies(number):
            copy.wait_recv()
        for which in range(2):
            theirs = gu_kept[slot, which, :, 1 - y].astype(F32)
            theirs = theirs + gu_landed[number, which, :, 1 - y].astype(F32)
            gu_outgoing[number, which] = theirs.astype(BF16)
            ours = gu_kept[slot, which, :, y].astype(F32)
            ours = ours + gu_landed[number, which, :, y].astype(F32)
            gu_ref[0, which] = ours.astype(BF16)
        @pl.when(number < blocks - LATE)
        def _():
            y_copy(number).start()

        for late in range(LATE):

            @pl.when(number == blocks - LATE + late)
            def _(late=late):
                leave(late).start()

        d_ref[...] = (d_kept[slot].astype(F32) + d_landed[number].astype(F32)).astype(BF16)

    @pl.when(step == blocks)
    def _():
        gain = gains_ref[1:2, :]
        chunk = min(128, tok)
        gain_ref[...] = jnp.zeros_like(gain_ref)
        for slot in range(2):

            def finish(number, _, slot=slot):
                local = pl.ds(pl.multiple_of(number * chunk, chunk), chunk)
                some = pl.ds(pl.multiple_of(slot * tok + number * chunk, chunk), chunk)
                middle = middle_ref[some, :]
                scale = lax.rsqrt(jnp.mean(middle * middle, axis=1, keepdims=True) + epsilon)
                result = middle + acc[some, :]
                if slot == 0:
                    out_ref[0, local, :] = result
                else:
                    send_ref[local, :] = result.astype(BF16)
                grad = back[some, :]
                gain_ref[0:1, :] += jnp.sum(grad * middle * scale, axis=0, keepdims=True)
                weighted = grad * gain
                inner = jnp.mean(weighted * middle, axis=1, keepdims=True)
                grad_middle = (
                    scale * weighted
                    - middle * (scale * scale * scale) * inner
                    + og[some, :].astype(F32)
                )
                grad_ref[some, :] = grad_middle
                low_ref[some, :] = grad_middle.astype(BF16)
                return 0

            lax.fori_loop(0, tok // chunk, finish, 0)
        for number in (blocks - 2, blocks - 1):
            for copy in core_copies(number):
                copy.wait_send()
        for late in range(LATE):
            leave(late).wait()
        for number in range(blocks - LATE):
            y_copy(number).wait()


def mlp_carry(grads, grads_received, middle, normed, gains, gate, up, down, line):
    slots, tok, depth = grads.shape
    half_width = gate[0].shape[1]
    wide = depth // 2
    span = slots * tok
    blocks = half_width // 128
    rows = depth // (2 * line)
    once = pl.Buffered(1)
    anywhere = pl.BlockSpec(memory_space=pl.ANY)

    def now(s):
        return jnp.minimum(s, blocks - 1)

    def done(s):
        return jnp.maximum(s - 1, 0)

    def core():
        return lax.axis_index("seq") % 2

    column = pl.BlockSpec((depth, 128), lambda s: (0, now(s)))
    own_rows = pl.BlockSpec((128, wide), lambda s: (core() * blocks + now(s), 0))
    other_rows = pl.BlockSpec((128, wide), lambda s: ((1 - core()) * blocks + now(s), 0))
    full = pl.BlockSpec((span, depth), lambda s: (0, 0), pipeline_mode=once)
    return pl.pallas_call(
        functools.partial(mlp_carry_kernel, line, tok, blocks),
        grid=(blocks + 1,),
        in_specs=[anywhere, anywhere, full, full, whole_block((8, depth))]
        + [column] * 4
        + [own_rows, own_rows, other_rows, other_rows],
        out_specs=[
            pl.BlockSpec(
                (1, tok, depth), lambda s: (lax.axis_index("seq") // 2, 0, 0), pipeline_mode=once
            ),
            pl.BlockSpec((tok, depth), lambda s: (0, 0), pipeline_mode=once),
            full,
            full,
            whole_block((8, depth)),
            pl.BlockSpec((1, 2, line, rows, 128), lambda s: (done(s), 0, 0, 0, 0)),
            pl.BlockSpec((2, 128, wide), lambda s: (0, done(s), 0)),
            anywhere,
            anywhere,
        ],
        out_shape=[
            jax.ShapeDtypeStruct((slots, tok, depth), F32),
            jax.ShapeDtypeStruct((tok, depth), BF16),
            jax.ShapeDtypeStruct((span, depth), F32),
            jax.ShapeDtypeStruct((span, depth), BF16),
            jax.ShapeDtypeStruct((8, depth), F32),
            jax.ShapeDtypeStruct((blocks, 2, line, rows, 128), BF16),
            jax.ShapeDtypeStruct((2, half_width, wide), BF16),
            jax.ShapeDtypeStruct((blocks - LATE, 2, line, rows, 128), BF16),
            jax.ShapeDtypeStruct((LATE, 2, line, rows, 128), BF16),
        ],
        scratch_shapes=[
            pltpu.VMEM((span, depth), BF16),
            pltpu.VMEM((depth, span), BF16),
            pltpu.VMEM((span, depth), F32),
            pltpu.VMEM((span, depth), F32),
            pltpu.VMEM((2, 2, line, 2, rows, 128), BF16),
            pltpu.VMEM((2, 2, 128, wide), BF16),
            pltpu.VMEM((2, 2, line, 2, rows, 128), BF16),
            pltpu.VMEM((2, 2, 128, wide), BF16),
            pltpu.VMEM((blocks, 2, line, 2, rows, 128), BF16),
            pltpu.VMEM((blocks, 2, 128, wide), BF16),
            pltpu.VMEM((blocks, 2, line, rows, 128), BF16),
            pltpu.VMEM((256, depth), BF16),
            pltpu.SemaphoreType.DMA((2 + LATE,)),
            pltpu.SemaphoreType.DMA((2,)),
            pltpu.SemaphoreType.DMA((blocks,)),
            pltpu.SemaphoreType.DMA((2,)),
            pltpu.SemaphoreType.DMA((blocks,)),
            pltpu.SemaphoreType.DMA((2, blocks - LATE)),
        ],
        compiler_params=pltpu.CompilerParams(
            dimension_semantics=("arbitrary",),
            vmem_limit_bytes=63 * MIB,
            collective_id=3,
            has_side_effects=True,
        ),
        cost_estimate=pl.CostEstimate(
            flops=16 * span * depth * 2 * half_width,
            bytes_accessed=24 * depth * half_width + 20 * span * depth,
            transcendentals=2 * span * half_width,
        ),
        name="mlp_carry",
    )(
        grads,
        grads_received,
        middle,
        normed,
        gains,
        *gate,
        *up,
        down[0],
        down[1],
        down[0],
        down[1],
    )


def early_rows(rows):
    return pl.ds(0, rows // 8)


def late_rows(rows):
    return pl.ds(rows // 8, rows - rows // 8)


def grad_attended_carry_kernel(
    line,
    low_ref,
    full_ref,
    att_other,
    att_own,
    outputs_sent,
    ga_own,
    ga_received,
    o_ref,
    o_landed,
    outputs_received,
    outgoing,
    o_sent,
    sems,
):
    step = pl.program_id(0)
    _, _, _, core = seats()
    wide = att_own.shape[0]
    mine = pl.ds(pl.multiple_of(core * wide, wide), wide)
    others = pl.ds(pl.multiple_of((1 - core) * wide, wide), wide)
    heads = send(outgoing, ga_received, sems, 0, to_core_partner())
    early = early_rows(outputs_sent.shape[0])
    swap = send(
        outputs_sent.at[early], outputs_received.at[early], sems, 3, to_x_partner()
    )

    def sums(number):
        half = 1 - core if number == 0 else core
        at = pl.ds(pl.multiple_of(half * wide, wide), wide)
        return send(o_sent.at[number], o_landed.at[at, :], sems, 1 + number, to_core_partner())

    @pl.when(step == 0)
    def _():
        meet(line, ("x", "core"))
        swap.start()
        outgoing[...] = nt(full_ref[...], low_ref[...]).astype(BF16)
        heads.start()

    @pl.when(step == 1)
    def _():
        ga_own[...] = nt(full_ref[...], low_ref[...]).astype(BF16)

    for number, att in enumerate((att_other, att_own)):

        @pl.when(step == number)
        def _(number=number, att=att):
            o_sent[number] = dot(att[...], low_ref[:, others]).astype(BF16)
            sums(number).start()
            o_ref[...] = dot(att[...], low_ref[:, mine]).astype(BF16)

    @pl.when(step == 1)
    def _():
        swap.wait()
        heads.wait()
        for number in range(2):
            sums(number).wait()


def grad_attended_carry(low, full, att_other, att_own, outputs_sent, line):
    span, depth = low.shape
    wide = depth // 2

    def half(s):
        core = lax.axis_index("seq") % 2
        return jnp.where(s == 0, 1 - core, core)

    anywhere = pl.BlockSpec(memory_space=pl.ANY)
    return pl.pallas_call(
        functools.partial(grad_attended_carry_kernel, line),
        grid=(2,),
        in_specs=[
            whole_block((span, depth)),
            pl.BlockSpec((wide, depth), lambda s: (half(s), 0)),
            whole_block((wide, span)),
            whole_block((wide, span)),
            anywhere,
        ],
        out_specs=[
            whole_block((wide, span)),
            anywhere,
            pl.BlockSpec((wide, wide), lambda s: (half(s), 0)),
            anywhere,
            anywhere,
        ],
        out_shape=[
            jax.ShapeDtypeStruct((wide, span), BF16),
            jax.ShapeDtypeStruct((wide, span), BF16),
            jax.ShapeDtypeStruct((depth, wide), BF16),
            jax.ShapeDtypeStruct((depth, wide), BF16),
            jax.ShapeDtypeStruct(outputs_sent.shape, BF16),
        ],
        scratch_shapes=[
            pltpu.VMEM((wide, span), BF16),
            pltpu.VMEM((2, wide, wide), BF16),
            pltpu.SemaphoreType.DMA((2, 4)),
        ],
        compiler_params=pltpu.CompilerParams(
            dimension_semantics=("arbitrary",),
            vmem_limit_bytes=48 * MIB,
            collective_id=4,
            has_side_effects=True,
        ),
        cost_estimate=pl.CostEstimate(
            flops=4 * span * depth * depth,
            bytes_accessed=6 * span * depth + 4 * depth * depth,
            transcendentals=0,
        ),
        name="grad_attended_carry",
    )(low, full, att_other, att_own, outputs_sent)


def attend_back_carry_kernel(line, tok, tile_q, tile_k, *refs):
    (
        received,
        own,
        mix_received,
        mix_own,
        grad_received,
        grad_own,
        lse_ref,
        cos_ref,
        sin_ref,
        outputs_sent,
        _,
        gu_in,
        gu_y,
        gu_late,
        d_in,
        o_in,
        o_landed,
        back_own,
        back_other,
        outputs_received,
        gu_mine,
        gu_z,
        d_kept,
        d_y,
        o_kept,
        o_y,
        first_received,
    ) = refs[:27]
    (
        qz,
        gz,
        qn,
        gn,
        kn,
        vn,
        kt,
        inner,
        dq,
        dk,
        dv,
        outgoing,
        gu_a,
        gu_b,
        o_a,
        o_b,
        o_x,
        d_a,
        d_x,
        first_out,
        local_sems,
        back_sems,
        z_sems,
        other_sems,
        first_sems,
    ) = refs[27:]
    step = pl.program_id(0)
    pairs = pl.num_programs(0)
    z, y, x, core = seats()
    wide = d_a.shape[3]
    late_part = late_rows(tok)
    length = 4 * tok
    blocks = gu_a.shape[0]
    o_half, d_half = o_x.shape[2], d_x.shape[2]
    o_mine = pl.ds(pl.multiple_of(x * o_half, o_half), o_half)
    o_theirs = pl.ds(pl.multiple_of((1 - x) * o_half, o_half), o_half)
    d_mine = pl.ds(pl.multiple_of(x * d_half, d_half), d_half)
    d_theirs = pl.ds(pl.multiple_of((1 - x) * d_half, d_half), d_half)
    swap = send(
        outputs_sent.at[late_part],
        outputs_received.at[late_part],
        other_sems,
        0,
        to_x_partner(),
    )
    o_over = send(o_a.at[:, :, o_theirs, :], o_x, other_sems, 1, to_x_partner())
    d_over = send(d_in.at[:, :, d_theirs, :], d_x, other_sems, 2, to_x_partner())
    o_send = send(o_a.at[:, 1 - y, o_mine, :], o_y, other_sems, 3, to_y_partner())
    d_send = send(d_a.at[:, 1 - y], d_y, other_sems, 4, to_y_partner())
    late = pl.ds(blocks - LATE, LATE)
    late_send = send(gu_late, gu_b.at[late], other_sems, 5, to_y_partner())

    def z_send(jump, number):
        target = lax.rem(z + jump, line)
        at = late if number else pl.ds(0, blocks - LATE)
        return send(
            gu_a.at[at, :, target],
            gu_z.at[jump - 1, at],
            z_sems,
            number * (line - 1) + jump - 1,
            to_z_partner(line, jump),
        )

    def add(number, _):
        total = gu_a[number].astype(F32) + gu_b[number].astype(F32)
        gu_a[number] = total.astype(BF16)
        return 0

    gu_stays = pltpu.make_async_copy(gu_a.at[:, :, z], gu_mine, local_sems.at[5])
    o_stays = pltpu.make_async_copy(o_a.at[:, y, o_mine, :], o_kept, local_sems.at[6])
    d_stays = pltpu.make_async_copy(d_a.at[:, y], d_kept, local_sems.at[7])
    load_d = pltpu.make_async_copy(d_in.at[:, :, d_mine, :], d_a, local_sems.at[4])

    def first_send(source):
        columns = pl.ds(pl.multiple_of(core * wide, wide), PAIR)
        partner = to_x_partner() if source else {"seq": 3 - lax.axis_index("seq")}
        return send(
            first_out.at[source], first_received.at[:, columns], first_sems, source, partner
        )

    def hand_over(number):
        rows = pl.ds(number * PAIR, PAIR)
        return send(
            outgoing.at[:, rows, :],
            back_other.at[:, rows, :],
            back_sems,
            number,
            to_core_partner(),
        )

    @pl.when(step == 0)
    def _():
        meet(line, ("z", "y", "x", "core", "diagonal"))
        late_send.start()
        loads = [
            pltpu.make_async_copy(source, target, local_sems.at[number])
            for number, (source, target) in enumerate(
                (
                    (o_in, o_a),
                    (o_landed, o_b),
                    (gu_in, gu_a),
                    (gu_y, gu_b.at[pl.ds(0, blocks - LATE)]),
                )
            )
        ]
        for load in loads:
            load.start()
        load_d.start()
        loads[0].wait()
        loads[1].wait()
        o_a[...] = (o_a[...].astype(F32) + o_b[...].astype(F32)).astype(BF16)
        o_over.start()
        d_over.start()
        loads[2].wait()
        loads[3].wait()
        lax.fori_loop(0, blocks - LATE, add, 0)
        for jump in range(1, line):
            z_send(jump, 0).start()

    @pl.when(step == 1)
    def _():
        late_send.wait()
        lax.fori_loop(blocks - LATE, blocks, add, 0)
        for jump in range(1, line):
            z_send(jump, 1).start()
        gu_stays.start()
        o_over.wait()
        summed = o_a[:, :, o_mine, :].astype(F32) + o_x[...].astype(F32)
        o_a[:, :, o_mine, :] = summed.astype(BF16)
        o_send.start()
        o_stays.start()

    @pl.when(step == 2)
    def _():
        swap.start()

    @pl.when(step == 3)
    def _():
        load_d.wait()
        d_over.wait()
        for at in range(line):
            d_a[at] = (d_a[at].astype(F32) + d_x[at].astype(F32)).astype(BF16)
        d_send.start()
        d_stays.start()

    attend_back_body(
        (received, own),
        (mix_received, mix_own),
        (grad_received, grad_own),
        lambda source, slot: block_of(source, slot, tok),
        tok,
        length,
        tile_q,
        tile_k,
        lse_ref,
        qz,
        gz,
        qn,
        gn,
        kn,
        vn,
        kt,
        inner,
        dq,
        dk,
        dv,
    )
    for slot in range(2):
        take = slice(slot * tok, (slot + 1) * tok)
        for source in range(2):
            cols = block_of(source, slot, tok)
            results = turn_back(dq, dk, dv, cols, cos_ref[:, cols], sin_ref[:, cols])
            for which, result in enumerate(results):
                if source == 1:
                    back_own[which, :, take] = result
                else:
                    at = pl.ds(pl.multiple_of(step * PAIR, PAIR), PAIR)
                    outgoing[which, at, take] = result

    @pl.when(step == 0)
    def _():
        for source in range(2):
            rows = dv[block_of(source, 1, tok), :]
            first_out[source] = (0.5 * rows).astype(BF16)
            first_send(source).start()

    for number in range(4):

        @pl.when(step == number)
        def _(number=number):
            hand_over(number).start()

    @pl.when(step == pairs - 1)
    def _():
        swap.wait()
        for source in range(2):
            first_send(source).wait()
        d_send.wait()
        o_send.wait()
        for copy in (gu_stays, o_stays, d_stays):
            copy.wait()
        for number in range(2):
            for jump in range(1, line):
                z_send(jump, number).wait()
        for number in range(4):
            hand_over(number).wait()


def attend_back_carry(
    pieces,
    mixes,
    grads,
    lse,
    cosine,
    sine,
    outputs_sent,
    outputs_received,
    gu,
    gu_y,
    gu_late,
    d,
    o,
    o_landed,
    line,
):
    _, width, span = pieces[0].shape
    tok = span // 2
    length = 2 * span
    pairs = width // PAIR
    tile_q = min(1024, length)
    tile_k = min(256, length)
    anywhere = pl.BlockSpec(memory_space=pl.ANY)
    triple = pl.BlockSpec((3, PAIR, span), lambda p: (0, p, 0))
    single = pl.BlockSpec((PAIR, span), lambda p: (p, 0))
    table = pl.BlockSpec((HALF, length), lambda p: (0, 0))
    blocks, _, _, rows, _ = gu.shape
    down_rows, wide = d.shape[2:]
    area = pairs * 2 * length * length // 2
    return pl.pallas_call(
        functools.partial(attend_back_carry_kernel, line, tok, tile_q, tile_k),
        grid=(pairs,),
        in_specs=[triple] * 2
        + [single] * 4
        + [pl.BlockSpec((1, 8, length), lambda p: (p, 0, 0)), table, table]
        + [anywhere] * 8,
        out_specs=[triple] + [anywhere] * 9,
        out_shape=[
            jax.ShapeDtypeStruct((3, width, span), BF16),
            jax.ShapeDtypeStruct((3, width, span), BF16),
            jax.ShapeDtypeStruct(outputs_sent.shape, BF16),
            jax.ShapeDtypeStruct((blocks, 2, rows, 128), BF16),
            jax.ShapeDtypeStruct((line - 1, blocks, 2, rows, 128), BF16),
            jax.ShapeDtypeStruct((line, down_rows // 2, wide), BF16),
            jax.ShapeDtypeStruct((line, down_rows // 2, wide), BF16),
            jax.ShapeDtypeStruct((line, rows // 2, wide), BF16),
            jax.ShapeDtypeStruct((line, rows // 2, wide), BF16),
            jax.ShapeDtypeStruct(outputs_sent.shape, BF16),
        ],
        input_output_aliases={10: 2},
        scratch_shapes=[
            pltpu.VMEM((2, PAIR, length), BF16),
            pltpu.VMEM((2, PAIR, length), BF16),
            pltpu.VMEM((2, length, PAIR), BF16),
            pltpu.VMEM((2, length, PAIR), BF16),
            pltpu.VMEM((length, PAIR), BF16),
            pltpu.VMEM((length, PAIR), BF16),
            pltpu.VMEM((PAIR, length), BF16),
            pltpu.VMEM((8, length), F32),
            pltpu.VMEM((PAIR, length), F32),
            pltpu.VMEM((length, PAIR), F32),
            pltpu.VMEM((length, PAIR), F32),
            pltpu.VMEM((3, width, span), BF16),
            pltpu.VMEM((blocks, 2, line, rows, 128), BF16),
            pltpu.VMEM((blocks, 2, line, rows, 128), BF16),
            pltpu.VMEM((line, 2, rows, wide), BF16),
            pltpu.VMEM((line, 2, rows, wide), BF16),
            pltpu.VMEM((line, 2, rows // 2, wide), BF16),
            pltpu.VMEM((line, 2, down_rows // 2, wide), BF16),
            pltpu.VMEM((line, 2, down_rows // 2, wide), BF16),
            pltpu.VMEM((2, tok, PAIR), BF16),
            pltpu.SemaphoreType.DMA((8,)),
            pltpu.SemaphoreType.DMA((2, 4)),
            pltpu.SemaphoreType.DMA((2, 2 * (line - 1))),
            pltpu.SemaphoreType.DMA((2, 6)),
            pltpu.SemaphoreType.DMA((2, 2)),
        ],
        compiler_params=pltpu.CompilerParams(
            dimension_semantics=("arbitrary",),
            vmem_limit_bytes=60 * MIB,
            collective_id=5,
            has_side_effects=True,
        ),
        cost_estimate=pl.CostEstimate(
            flops=area * 2560, bytes_accessed=16 * width * length, transcendentals=area
        ),
        name="attend_back_carry",
    )(
        *pieces,
        *mixes,
        *grads,
        lse,
        cosine,
        sine,
        outputs_sent,
        outputs_received,
        gu,
        gu_y,
        gu_late,
        d,
        o,
        o_landed,
    )


def tail_carry_kernel(line, tok, blocks, *refs):
    (
        inputs,
        x_received,
        back_other,
        back_own,
        full_ref,
        normed_ref,
        grad_in,
        gains_ref,
        mlp_gain_ref,
        gu_mine,
        gu_z,
        d_in,
        d_y,
        o_in,
        o_y,
        _,
        input_grad,
        input_landed,
        first_grad,
        first_landed,
        gain_out,
        q_out,
        k_out,
        v_out,
        o_out,
        g_out,
        u_out,
        d_out,
        xs,
        grad_middle,
        normed_t,
        acc,
        grad,
        sent,
        landed,
        y_landed,
        z_landed,
        d_a,
        d_b,
        d_landed,
        o_a,
        o_b,
        o_landed,
        gu_a,
        gu_b,
        gu_x,
        gu_c,
        d_low,
        d_c,
        s_low,
        s_x,
        s_c,
        first_stage,
        first_send,
        input_send,
        gain,
        gain_landed,
        local_sems,
        core_sems,
        y_sems,
        z_sems,
        dz_sems,
        oz_sems,
        x_sems,
        c_sems,
        token_sems,
        gain_sems,
    ) = refs
    step = pl.program_id(0)
    target = jnp.where(step < 6, lax.rem(step, 2), 2)
    turn = lax.rem(step // 2, 3)
    z, y, x, core = seats()
    side = x
    wide, span = grad.shape
    depth = 2 * wide
    half = jnp.where(target == 0, 1 - core, core)
    columns = pl.ds(pl.multiple_of(half * wide, wide), wide)
    mine = pl.ds(pl.multiple_of(core * wide, wide), wide)
    others = pl.ds(pl.multiple_of((1 - core) * wide, wide), wide)

    def load(source, place, number):
        return pltpu.make_async_copy(source, place, local_sems.at[number])

    load_tokens = [
        load(inputs.at[side], xs.at[pl.ds(0, tok), :], 0),
        load(x_received, xs.at[pl.ds(tok, tok), :], 1),
        load(grad_in, grad_middle, 2),
    ]
    store_input = load(acc.at[pl.ds(0, tok), :], input_grad, 3)
    store_first = load(first_stage, first_grad, 4)

    def along_z(source, place, sems, base=0):
        return [
            send(
                source(lax.rem(z + jump, line)),
                place(jump - 1),
                sems,
                base + jump - 1,
                to_z_partner(line, jump),
            )
            for jump in range(1, line)
        ]

    d_sends = along_z(lambda at: d_a.at[at], lambda jump: d_landed.at[jump], dz_sems)
    o_sends = along_z(lambda at: o_a.at[at], lambda jump: o_landed.at[jump], oz_sems)

    def core_send(number):
        return send(sent.at[number], landed.at[number], core_sems, number, to_core_partner())

    def y_send(number):
        return send(
            landed.at[number, :, 1 - y], y_landed.at[number], y_sems, number, to_y_partner()
        )

    def z_sends(number):
        return along_z(
            lambda at: landed.at[number, at, y],
            lambda jump: z_landed.at[number, jump],
            z_sems,
            number * (line - 1),
        )

    def first_part(number):
        which = 1 - core if number == 0 else core
        at = pl.ds(pl.multiple_of(which * wide + PAIR, PAIR), wide - PAIR)
        return send(
            first_send.at[:, at], first_landed.at[:, at], token_sems, number, to_x_partner()
        )

    input_part = send(input_send, input_landed, token_sems, 2, to_x_partner())
    gu_sides = (
        send(gu_a, gu_x, x_sems, 0, to_x_partner()),
        send(gu_a, gu_c, c_sems, 0, to_core_partner()),
    )
    d_half, o_half = d_a.shape[1], o_a.shape[1]
    d_mine = pl.ds(pl.multiple_of(x * d_half, d_half), d_half)
    d_theirs = pl.ds(pl.multiple_of((1 - x) * d_half, d_half), d_half)
    o_mine = pl.ds(pl.multiple_of(x * o_half, o_half), o_half)
    o_theirs = pl.ds(pl.multiple_of((1 - x) * o_half, o_half), o_half)
    d_sides = (
        send(d_low.at[d_mine, :], d_low.at[d_mine, :], x_sems, 1, to_x_partner()),
        send(d_low, d_c, c_sems, 1, to_core_partner()),
    )
    o_side = send(s_low.at[0, o_mine, :], s_low.at[0, o_mine, :], x_sems, 2, to_x_partner())

    def square_x(number):
        return send(s_low.at[number], s_x.at[number], x_sems, 2 + number, to_x_partner())

    def square_core(number):
        return send(s_low.at[number], s_c.at[number], c_sems, 2 + number, to_core_partner())

    squares = (o_out, v_out, q_out, k_out)

    def gain_send(number, partner):
        return send(gain.at[number], gain_landed.at[number], gain_sems, number, partner)

    @pl.when(step == 0)
    def _():
        meet(line, ("z", "y", "x", "core"))
        sources = ((d_in, d_a), (d_y, d_b), (o_in, o_a), (o_y, o_b), (gu_mine, gu_a), (gu_z, gu_b))
        loads = [load(source, place, 7 + n) for n, (source, place) in enumerate(sources)]
        for copy in loads:
            copy.start()
        for copy in load_tokens:
            copy.start()
        for copy in loads[:4]:
            copy.wait()
        for at in range(line):
            d_a[at] = (d_a[at].astype(F32) + d_b[at].astype(F32)).astype(BF16)
            o_a[at] = (o_a[at].astype(F32) + o_b[at].astype(F32)).astype(BF16)
        for copy in d_sends + o_sends:
            copy.start()
        for copy in loads[4:]:
            copy.wait()

        def total(number, _):
            for which, out in enumerate((g_out, u_out)):
                value = gu_a[number, which].astype(F32)
                for jump in range(line - 1):
                    value = value + gu_b[jump, number, which].astype(F32)
                at = pl.ds(pl.multiple_of((core * blocks + number) * 128, 128), 128)
                out[:, at] = value
                gu_a[number, which] = value.astype(BF16)
            return 0

        lax.fori_loop(0, blocks, total, 0)
        gu_sides[0].start()
        normed_t[...] = normed_ref[...].T
        acc[...] = jnp.zeros_like(acc)

    def own_part(back):
        @pl.when(turn == 0)
        def _():
            value = 0.5 * back[0].astype(F32)
            rows = value.T
            first_stage[:, columns] = rows[:tok]
            first_send[:, columns] = rows[tok:].astype(BF16)
            grad[...] = value.astype(BF16)

        @pl.when(turn > 0)
        def _():
            grad[...] = back[0]

    @pl.when(target == 0)
    def _():
        own_part(back_other)

    @pl.when(target == 1)
    def _():
        own_part(back_own)

    @pl.when(step == 0)
    def _():
        first_part(0).start()

    @pl.when(step == 1)
    def _():
        first_part(1).start()
        store_first.start()

    @pl.when(target < 2)
    def _():
        value = grad[...]
        result = nt(normed_t[...], value)

        @pl.when(target == 0)
        def _():
            sent[turn] = result.astype(BF16).reshape(sent.shape[1:])
            core_send(turn).start()

        @pl.when(target == 1)
        def _():
            core_send(turn).wait()
            theirs = landed[turn].reshape(result.shape).astype(F32)
            landed[turn] = (result + theirs).astype(BF16).reshape(landed.shape[1:])
            y_send(turn).start()

        acc[...] += nt(value.T, full_ref[0, 0])

    @pl.when(step == 6)
    def _():
        for copy in load_tokens:
            copy.wait()
        weight = gains_ref[0:1, :]
        chunk = min(128, tok)
        gain[...] = jnp.zeros_like(gain)
        gain[0, 1:2, :] = mlp_gain_ref[0:1, :]
        for slot in (1, 0):

            def finish(number, _, slot=slot):
                local = pl.ds(pl.multiple_of(number * chunk, chunk), chunk)
                some = pl.ds(pl.multiple_of(slot * tok + number * chunk, chunk), chunk)
                values = xs[some, :].astype(F32)
                scale = lax.rsqrt(jnp.mean(values * values, axis=1, keepdims=True) + epsilon)
                value = acc[some, :]
                gain[0, 0:1, :] += jnp.sum(value * values * scale, axis=0, keepdims=True)
                weighted = value * weight
                inner = jnp.mean(weighted * values, axis=1, keepdims=True)
                result = (
                    scale * weighted
                    - values * (scale * scale * scale) * inner
                    + grad_middle[some, :]
                )
                if slot == 0:
                    acc[some, :] = result
                else:
                    input_send[local, :] = result.astype(BF16)
                return 0

            lax.fori_loop(0, tok // chunk, finish, 0)
            if slot == 1:
                input_part.start()
        gain_send(0, to_core_partner()).start()
        store_input.start()
        gu_sides[0].wait()

        def gather_x(number, _):
            for which, out in enumerate((g_out, u_out)):
                at = pl.ds(pl.multiple_of((core * blocks + number) * 128, 128), 128)
                value = out[:, at] + gu_x[number, which].astype(F32)
                out[:, at] = value
                gu_a[number, which] = value.astype(BF16)
            return 0

        lax.fori_loop(0, blocks, gather_x, 0)
        gu_sides[1].start()
        gain_send(0, to_core_partner()).wait()
        gain[1] = gain[0] + gain_landed[0]
        gain_send(1, to_y_partner()).start()
        for number in range(3):
            y_send(number).wait()

            def add(at, _, number=number):
                value = landed[number, at, y].astype(F32) + y_landed[number, at].astype(F32)
                landed[number, at, y] = value.astype(BF16)
                return 0

            lax.fori_loop(0, line, add, 0)
            for copy in z_sends(number):
                copy.start()
            if number == 0:
                gain_send(1, to_y_partner()).wait()
                gain[2] = gain[1] + gain_landed[1]
                for jump in range(1, line):
                    gain_z(jump, line, gain, gain_landed, gain_sems).start()
        for copy in d_sends + o_sends:
            copy.wait()

        def sum_z(own, places):
            value = own.astype(F32)
            for place in places:
                value = value + place.astype(F32)
            return value

        value = sum_z(d_a[z], [d_landed[jump] for jump in range(line - 1)])
        d_out[d_mine, mine] = value
        d_low[d_mine, :] = value.astype(BF16)
        d_sides[0].start()
        value = sum_z(o_a[z], [o_landed[jump] for jump in range(line - 1)])
        o_out[o_mine, mine] = value
        s_low[0, o_mine, :] = value.astype(BF16)
        o_side.start()
        for jump in range(1, line):
            gain_z(jump, line, gain, gain_landed, gain_sems).wait()
        value = gain[2]
        for jump in range(1, line):
            value = value + gain_landed[1 + jump]
        gain[3] = value
        last_gain = send(gain.at[3], gain_landed.at[line + 1], gain_sems, line + 1, to_x_partner())
        last_gain.start()
        for number in range(3):
            for copy in z_sends(number):
                copy.wait()
            value = sum_z(
                landed[number, z, y], [z_landed[number, jump] for jump in range(line - 1)]
            )
            squares[1 + number][:, mine] = value
            s_low[1 + number] = value.astype(BF16)
            square_x(1 + number).start()
        last_gain.wait()
        gain[4] = gain[3] + gain_landed[line + 1]
        gain_out[...] = gain[4, :, pl.ds(pl.multiple_of((2 * z + y) * 128, 128), 128)]
        store_first.wait()
        for number in range(2):
            first_part(number).wait()
        d_sides[0].wait()
        d_out[d_theirs, mine] = d_low[d_theirs, :].astype(F32)
        d_sides[1].start()
        o_side.wait()
        o_out[o_theirs, mine] = s_low[0, o_theirs, :].astype(F32)
        square_core(0).start()
        input_part.wait()
        for number in range(1, 4):
            square_x(number).wait()
            value = squares[number][:, mine] + s_x[number].astype(F32)
            squares[number][:, mine] = value
            s_low[number] = value.astype(BF16)
            square_core(number).start()
        gu_sides[1].wait()

        def gather_core(number, _):
            for which, out in enumerate((g_out, u_out)):
                at = pl.ds(pl.multiple_of(((1 - core) * blocks + number) * 128, 128), 128)
                out[:, at] = gu_c[number, which].astype(F32)
            return 0

        lax.fori_loop(0, blocks, gather_core, 0)
        d_sides[1].wait()
        d_out[:, others] = d_c[...].astype(F32)
        for number in range(4):
            square_core(number).wait()
            squares[number][:, others] = s_c[number].astype(F32)
        store_input.wait()


def gain_z(jump, line, gain, gain_landed, gain_sems):
    return send(
        gain.at[2], gain_landed.at[1 + jump], gain_sems, 1 + jump, to_z_partner(line, jump)
    )


def tail_carry(
    inputs,
    x_received,
    back_other,
    back_own,
    full,
    normed,
    grad_middle,
    gains,
    mlp_gain,
    gu_mine,
    gu_z,
    d,
    d_y,
    o,
    o_y,
    first_received,
    line,
):
    slots, tok, depth = inputs.shape
    span = slots * tok
    wide = depth // 2
    blocks, _, rows, _ = gu_mine.shape
    down_rows = 2 * d.shape[1]
    once = pl.Buffered(1)
    anywhere = pl.BlockSpec(memory_space=pl.ANY)

    def half(s):
        core = lax.axis_index("seq") % 2
        return jnp.where(s % 2 == 0, 1 - core, core)

    def kind(s):
        return (jnp.minimum(s // 2, 2) + 2) % 3

    def clear(shape):
        zeros = (0,) * len(shape)
        return pl.BlockSpec(shape, lambda s: zeros, pipeline_mode=once)

    square = jax.ShapeDtypeStruct((rows, depth), F32)
    broad = jax.ShapeDtypeStruct((rows, 2 * blocks * 128), F32)
    tall = jax.ShapeDtypeStruct((down_rows, depth), F32)
    tokens = [jax.ShapeDtypeStruct((tok, depth), dtype) for dtype in (F32, BF16)] * 2
    finals = [square] * 4 + [broad] * 2 + [tall]
    vmem = pltpu.VMEM
    dma = pltpu.SemaphoreType.DMA
    return pl.pallas_call(
        functools.partial(tail_carry_kernel, line, tok, blocks),
        grid=(7,),
        in_specs=[
            anywhere,
            anywhere,
            pl.BlockSpec((1, wide, span), lambda s: (kind(s), 0, 0)),
            pl.BlockSpec((1, wide, span), lambda s: (kind(s), 0, 0)),
            pl.BlockSpec(
                (1, 1, depth, wide),
                lambda s: (half(jnp.minimum(s, 5)), kind(s), 0, 0),
            ),
            clear((span, depth)),
            anywhere,
            clear((8, depth)),
            clear((8, depth)),
        ]
        + [anywhere] * 7,
        input_output_aliases={15: 3},
        out_specs=[anywhere] * 4 + [clear((8, 128))] + [clear(final.shape) for final in finals],
        out_shape=tokens + [jax.ShapeDtypeStruct((8, 128), F32)] + finals,
        scratch_shapes=[
            vmem((span, depth), BF16),
            vmem((span, depth), F32),
            vmem((depth, span), BF16),
            vmem((span, depth), F32),
            vmem((wide, span), BF16),
            vmem((3, line, 2, rows, wide), BF16),
            vmem((3, line, 2, rows, wide), BF16),
            vmem((3, line, rows, wide), BF16),
            vmem((3, line - 1, rows, wide), BF16),
            vmem((line, down_rows // 2, wide), BF16),
            vmem((line, down_rows // 2, wide), BF16),
            vmem((line - 1, down_rows // 2, wide), BF16),
            vmem((line, rows // 2, wide), BF16),
            vmem((line, rows // 2, wide), BF16),
            vmem((line - 1, rows // 2, wide), BF16),
            vmem((blocks, 2, rows, 128), BF16),
            vmem((line - 1, blocks, 2, rows, 128), BF16),
            vmem((blocks, 2, rows, 128), BF16),
            vmem((blocks, 2, rows, 128), BF16),
            vmem((down_rows, wide), BF16),
            vmem((down_rows, wide), BF16),
            vmem((4, rows, wide), BF16),
            vmem((4, rows, wide), BF16),
            vmem((4, rows, wide), BF16),
            vmem((tok, depth), F32),
            vmem((tok, depth), BF16),
            vmem((tok, depth), BF16),
            vmem((5, 8, depth), F32),
            vmem((line + 2, 8, depth), F32),
            dma((13,)),
            dma((2, 3)),
            dma((2, 3)),
            dma((2, 3 * (line - 1))),
            dma((2, line - 1)),
            dma((2, line - 1)),
            dma((2, 6)),
            dma((2, 6)),
            dma((2, 3)),
            dma((2, line + 2)),
        ],
        compiler_params=pltpu.CompilerParams(
            dimension_semantics=("arbitrary",),
            vmem_limit_bytes=63 * MIB,
            collective_id=6,
            has_side_effects=True,
        ),
        cost_estimate=pl.CostEstimate(
            flops=12 * span * depth * depth,
            bytes_accessed=24 * span * depth + 12 * depth * depth,
            transcendentals=0,
        ),
        name="tail_carry",
    )(
        inputs,
        x_received,
        back_other,
        back_own,
        full,
        normed,
        grad_middle,
        gains,
        mlp_gain,
        gu_mine,
        gu_z,
        d,
        d_y,
        o,
        o_y,
        first_received,
    )


def finish_kernel(place, *refs):
    count = (len(refs) - 2 * 3 - 3) // 2
    tokens, plain = refs[:6], refs[6 : 6 + count]
    outs = refs[6 + count :]
    side = place[0]
    for number in range(3):
        outs[number][side] = tokens[2 * number][...].reshape(tokens[2 * number + 1].shape)
        outs[number][1 - side] = tokens[2 * number + 1][...].astype(F32)
    for number in range(count):
        outs[3 + number][...] = plain[number][...]


def finish(outputs, tokens, plain, side):
    _, tok, depth = outputs[0].shape
    steps = 4
    tile = tok // steps
    row = pl.BlockSpec((tile, depth), lambda s, p: (s, 0))
    tiles = [
        pl.BlockSpec((value.shape[0] // steps, value.shape[1]), lambda s, p: (s, 0))
        for value in plain
    ]
    grid_spec = pltpu.PrefetchScalarGridSpec(
        num_scalar_prefetch=1,
        grid=(steps,),
        in_specs=[pl.BlockSpec((1, tile, depth), lambda s, p: (p[0], s, 0))] + [row] * 5 + tiles,
        out_specs=[pl.BlockSpec((2, tile, depth), lambda s, p: (0, s, 0))] * 3 + tiles,
    )
    return pl.pallas_call(
        finish_kernel,
        out_shape=[jax.ShapeDtypeStruct((2, tok, depth), F32)] * 3
        + [jax.ShapeDtypeStruct(value.shape, value.dtype) for value in plain],
        grid_spec=grid_spec,
        compiler_params=parameters(60),
        cost_estimate=pl.CostEstimate(
            flops=tok * depth, bytes_accessed=60 * tok * depth, transcendentals=0
        ),
        name="finish",
    )(side, *outputs, *tokens, *plain)


def shards(
    inputs,
    first_values,
    out_grad,
    attn_gain,
    query_weight,
    key_weight,
    value_weight,
    output_weight,
    mlp_gain,
    gate_weight,
    up_weight,
    down_weight,
):
    slots, tok, _ = inputs.shape
    groups = lax.axis_size("seq")
    parts = lax.axis_size("fsdp")
    line = parts // 2
    count = groups // slots
    length = tok * groups
    span = slots * tok
    seat = lax.axis_index("seq")
    shard = lax.axis_index("fsdp")
    side = seat // count
    rank = seat % count
    core = seat % 2
    z, y = shard // 2, shard % 2
    wide = D // 2
    width = D // count

    def along_seq(value, partner):
        return lax.ppermute(value, "seq", [(i, partner(i)) for i in range(groups)])

    def along_fsdp(value, partner):
        return lax.ppermute(value, "fsdp", [(i, partner(i)) for i in range(parts)])

    def to_core(value):
        return along_seq(value, lambda i: i ^ 1)

    def to_y(value):
        return along_fsdp(value, lambda i: i ^ 1)

    def to_z(value, jump):
        return along_fsdp(value, lambda i: (i + 2 * jump) % parts)

    def after(value, *others):
        return lax.optimization_barrier((value,) + others)[0]

    def to_sequence(values):
        taken = []
        for jump in range(1, slots):
            sent = lax.dynamic_index_in_dim(values, (side + jump) % slots, 0, keepdims=False)
            taken.append(along_seq(sent, lambda i: (i + jump * count) % groups))
        return taken

    def to_home(whole, sent):
        for jump in range(1, slots):
            part = sent[(jump - 1) * tok : jump * tok]
            part = along_seq(part, lambda i: (i - jump * count) % groups)
            whole = land(whole, part, ((side + jump) % slots)[None])
        return whole

    def rank_up(i, jump):
        return (i // count) * count + (i % count + jump) % count

    def rank_down(i, jump):
        return (i // count) * count + (i % count - jump) % count

    def halves_to_ranks(other, own, axis):
        if count == 2:
            return [other, own]
        return [
            lax.dynamic_slice_in_dim(
                join(other, own, axis), ((rank + 1 + number) % count) * width, width, axis
            )
            for number in range(count)
        ]

    def join(other, own, axis):
        first = jnp.where(core == 0, own, other)
        second = jnp.where(core == 0, other, own)
        return jnp.concatenate([first, second], axis=axis)

    def ranks_to_halves(pieces, axis):
        if count == 2:
            return pieces
        shape = list(pieces[0].shape)
        shape[axis] = D
        whole = jnp.zeros(shape, pieces[0].dtype)
        for number in range(count):
            whole = lax.dynamic_update_slice_in_dim(
                whole, pieces[number], ((rank + 1 + number) % count) * width, axis
            )
        return [
            lax.dynamic_slice_in_dim(whole, which * wide, wide, axis)
            for which in (1 - core, core)
        ]

    def exchange(pieces):
        received = [
            along_seq(pieces[jump - 1], lambda i: rank_up(i, jump)) for jump in range(1, count)
        ]
        return received + [pieces[count - 1]]

    def exchange_back(pieces):
        received = [
            along_seq(pieces[jump - 1], lambda i: rank_down(i, jump)) for jump in range(1, count)
        ]
        return received + [pieces[count - 1]]

    def split(*weights):
        results = []
        for which in (core, 1 - core):
            columns = []
            for weight in weights:
                size = weight.shape[1] // 2
                columns.append(lax.dynamic_slice_in_dim(weight, which * size, size, 1))
            results.append(columns)
        return results

    def gather_z(half):
        return [half] + [to_z(half, jump) for jump in range(1, line)]

    def gather_rest(along_z, other):
        along_y = [to_y(piece) for piece in along_z]
        own = [piece for pair in zip(along_z, along_y) for piece in pair]
        return (own, [other] + [to_core(piece) for piece in own[1:]])

    numbers = []
    for jump in range(line):
        for flip in range(2):
            numbers.append(((z - jump) % line) * 2 + (y ^ flip))
    place = jnp.stack([side, core] + numbers).astype(jnp.int32)

    def low(value):
        return value.astype(BF16)

    def add(a, b):
        return low(a.astype(F32) + b.astype(F32))

    def pick(value, index, axis):
        return lax.dynamic_index_in_dim(value, index, axis, keepdims=False)

    def along_x_and_core(total):
        mine = low(total)
        for jump in range(1, groups // 2):
            total = total + along_seq(mine, lambda i: (i + 2 * jump) % groups).astype(F32)
        mine = low(total)
        return (mine, to_core(mine))

    def along_z_and_on(partial):
        total = partial(z)
        for jump in range(1, line):
            total = total + to_z(low(partial((z + jump) % line)), jump).astype(F32)
        return along_x_and_core(total)

    def scatter(sent, kept, rows_axis):
        shape = kept.shape
        rows = shape[rows_axis] // parts
        cut = shape[:rows_axis] + (line, 2, rows) + shape[rows_axis + 1 :]
        received = to_core(sent).reshape(cut)
        kept = kept.reshape(cut)
        axis = rows_axis + 1
        received_y = to_y(add(pick(kept, 1 - y, axis), pick(received, 1 - y, axis)))
        kept_y = pick(kept, y, axis), pick(received, y, axis)

        def partial(index):
            total = pick(kept_y[0], index, rows_axis).astype(F32)
            total = total + pick(kept_y[1], index, rows_axis).astype(F32)
            return total + pick(received_y, index, rows_axis).astype(F32)

        return along_z_and_on(partial)

    def columns(mine, others):
        first = jnp.where(core == 0, mine, others)
        second = jnp.where(core == 0, others, mine)
        return jnp.concatenate([first, second], axis=-1).astype(F32)

    def everywhere(value):
        value = value + to_core(value)
        value = value + to_y(value)
        total = value
        for jump in range(1, line):
            total = total + to_z(value, jump)
        value = total
        for jump in range(1, groups // 2):
            total = total + along_seq(value, lambda i: (i + 2 * jump) % groups)
        return total

    steps = jnp.arange(slots, dtype=jnp.int32)
    starts = ((side - steps) % slots) * (count * tok) + rank * tok
    positions = (starts[:, None] + jnp.arange(tok, dtype=jnp.int32)[None]).reshape(span)
    freqs = rope_base ** (-(jnp.arange(HALF, dtype=F32) * 2.0 / HEAD_DIM))

    def tables(positions):
        angles = freqs[:, None] * positions.astype(F32)[None, :]
        return (jnp.cos(angles), jnp.sin(angles))

    full_cos, full_sin = tables(jnp.arange(length, dtype=jnp.int32))
    sources = jnp.concatenate(
        [(rank - 1 - jnp.arange(count - 1, dtype=jnp.int32)) % count, rank[None]]
    ).astype(jnp.int32)
    order = (((side - steps) % slots)[None, :] * count + sources[:, None]).reshape(-1)
    order = order.astype(jnp.int32)

    whole_lanes = (slots, count) == (2, 2) and (D // parts) % 128 == 0
    if whole_lanes:
        gains = jnp.pad(jnp.stack([attn_gain, mlp_gain]).astype(F32), ((0, 6), (0, 0)))
        parts_of = lambda ref: [ref.reshape(-1, ref.shape[-1])]
        (
            tokens,
            _,
            grads_early,
            heads_own,
            heads_received,
            normed,
            qkv_full,
            gains_full,
            out_own,
            out_other,
            down_own,
        ) = front(
            inputs,
            first_values,
            out_grad,
            query_weight,
            key_weight,
            value_weight,
            output_weight,
            down_weight,
            gains,
            full_cos,
            full_sin,
            line,
        )
        qkv_full = qkv_full.reshape(2, 3, D, wide)
        tokens = [tokens]
        pieces = [heads_received, heads_own]
        (
            mix_received,
            att_own,
            lse,
            middle,
            normed2,
            out_full,
            att_other,
            grads,
            down_own,
            down_other,
            gate_own,
            gate_other,
            up_own,
            up_other,
        ) = attend_carry(
            heads_received,
            heads_own,
            inputs,
            tokens[0],
            gains_full,
            out_own.reshape(D, wide),
            out_other.reshape(D, wide),
            out_grad,
            grads_early,
            down_own,
            gate_weight,
            up_weight,
            line,
        )
        mixes = [mix_received, att_own]
        grads = [grads]
        gate_pieces = parts_of(gate_own), parts_of(gate_other)
        up_pieces = parts_of(up_own), parts_of(up_other)
        down_pieces = parts_of(down_own), parts_of(down_other)
    else:
        gains = jnp.pad(jnp.stack([attn_gain, mlp_gain], axis=1), ((0, 0), (0, 126)))
        gate_halves, up_halves, out_halves, down_halves = (
            [half[0] for half in split(weight)]
            for weight in (gate_weight, up_weight, output_weight, down_weight)
        )
        cosine, sine = tables(positions)
        qkv = [
            jnp.concatenate(half + [gains], axis=1)
            for half in split(query_weight, key_weight, value_weight)
        ]
        tokens = to_sequence(inputs)
        firsts = to_sequence(first_values)
        grads = to_sequence(out_grad)
        qkv_own, qkv_other = gather_rest(gather_z(qkv[0]), qkv[1])
        out_own, out_other = gather_rest(gather_z(out_halves[0]), out_halves[1])
        gate_pieces = gather_rest(gather_z(gate_halves[0]), gate_halves[1])
        up_pieces = gather_rest(gather_z(up_halves[0]), up_halves[1])
        down_pieces = gather_rest(gather_z(down_halves[0]), down_halves[1])
        heads_other, heads_own, normed, qkv_full, gains_full = project(
            inputs, tokens, first_values, firsts, qkv_own, qkv_other, cosine, sine, place
        )
        pieces = exchange(halves_to_ranks(heads_other, heads_own, 1))
        mixes, lse = attend(pieces, order, slots)
        att_other, att_own = ranks_to_halves(exchange_back(mixes), 0)
        middle, normed2, out_full = output_projection(
            inputs, tokens, out_own, out_other, att_other, att_own, gains_full, place
        )

    if whole_lanes:
        (
            outputs,
            outputs_sent,
            grad_middle,
            low_grad,
            mlp_gain_grad,
            gu_reduced,
            down_reduced,
            gu_y,
            gu_late,
        ) = mlp_carry(
            out_grad,
            grads[0],
            middle,
            normed2,
            gains_full,
            (gate_pieces[0][0], gate_pieces[1][0]),
            (up_pieces[0][0], up_pieces[1][0]),
            (down_pieces[0][0], down_pieces[1][0]),
            line,
        )
        ga_own, ga_received, out_kept, out_landed, outputs_received = grad_attended_carry(
            low_grad, out_full, att_other, att_own, outputs_sent, line
        )
        down_reduced = down_reduced.reshape(line, 2, -1, wide)
        out_kept = out_kept.reshape(line, 2, -1, wide)
        out_landed = out_landed.reshape(line, 2, -1, wide)
        (
            back_own,
            back_other,
            outputs_received,
            gu_mine,
            gu_z,
            down_mine,
            down_y,
            out_mine,
            out_y,
            first_received,
        ) = attend_back_carry(
            pieces,
            mixes,
            [ga_received, ga_own],
            lse,
            full_cos,
            full_sin,
            outputs_sent,
            outputs_received,
            gu_reduced,
            gu_y,
            gu_late,
            down_reduced,
            out_kept,
            out_landed,
            line,
        )
        input_own, input_received, first_own, first_received, *rest = tail_carry(
            inputs,
            tokens[0],
            back_other,
            back_own,
            qkv_full,
            normed,
            grad_middle,
            gains_full,
            mlp_gain_grad,
            gu_mine,
            gu_z,
            down_mine,
            down_y,
            out_mine,
            out_y,
            first_received,
            line,
        )
        gain_grads = rest[0]
        outputs, input_grad, first_grad, *rest = finish(
            (outputs,),
            (outputs_received, input_own, input_received, first_own, first_received),
            rest[1:],
            side[None],
        )
        query_grad, key_grad, value_grad, output_grad, gate_grad, up_grad, down_grad = rest
    else:
        (
            outputs,
            outputs_sent,
            grad_middle,
            low_grad,
            mlp_gain_grad,
            gu_sent,
            gu_kept,
            down_sent,
            down_kept,
        ) = mlp(out_grad, grads, middle, normed2, gains_full, gate_pieces, up_pieces, down_pieces, place)
        ga_other, ga_own, out_sent, out_kept = grad_attended(
            low_grad, out_full, att_other, att_own, place
        )
        gate_up_grad = scatter(gu_sent, gu_kept, 1)
        down_grad = scatter(down_sent.reshape(-1, wide), down_kept.reshape(-1, wide), 0)
        output_grad = scatter(out_sent, out_kept, 0)
        grad_heads = exchange(halves_to_ranks(ga_other, ga_own, 0))
        back = attend_back(pieces, mixes, grad_heads, lse, full_cos, full_sin, order, slots)
        back_other, back_own = ranks_to_halves(exchange_back(back), 1)
        outputs = to_home(outputs, outputs_sent)
        input_grad, input_sent, first_grad, first_sent, gain_grads, qkv_sent, qkv_kept = tail(
            inputs,
            tokens,
            back_other,
            back_own,
            qkv_full,
            normed,
            grad_middle,
            gains_full,
            mlp_gain_grad,
            place,
        )
        query_grad, key_grad, value_grad = columns(*scatter(qkv_sent, qkv_kept, 1))
        gate_grad, up_grad = columns(*gate_up_grad)
        output_grad = columns(*output_grad)
        down_grad = columns(*down_grad)
        gain_grads = everywhere(gain_grads)
        gain_grads = lax.dynamic_slice_in_dim(gain_grads, shard * (D // parts), D // parts, 1)
        input_grad = to_home(input_grad, input_sent)
        first_grad = to_home(first_grad, first_sent)

    return (
        outputs,
        input_grad,
        first_grad,
        gain_grads[0],
        gain_grads[1],
        query_grad,
        key_grad,
        value_grad,
        output_grad,
        gate_grad,
        up_grad,
        down_grad,
    )


def solution(mesh):
    token_spec = P("fsdp", "seq", None)
    weight_spec = P("fsdp", None)
    gain_spec = P("fsdp")
    return jax.shard_map(
        shards,
        mesh=mesh,
        in_specs=(token_spec,) * 3
        + (gain_spec,)
        + (weight_spec,) * 4
        + (gain_spec,)
        + (weight_spec,) * 3,
        out_specs=(token_spec,) * 3 + (gain_spec,) * 2 + (weight_spec,) * 7,
        check_vma=False,
    )
```

```python
import functools
import math

import jax
import jax.numpy as jnp
from jax import lax
from jax.experimental import pallas as pl
from jax.experimental.pallas import tpu as pltpu
from jax.sharding import PartitionSpec as P

D = 1024
HEADS = 16
HEAD_DIM = 64
HALF = HEAD_DIM // 2
PAIR = 2 * HEAD_DIM
F32 = jnp.float32
BF16 = jnp.bfloat16
NEG = -1e30
MIB = 1024 * 1024
epsilon = 1e-06
rope_base = 10000.0


def dot(a, b):
    return lax.dot_general(a, b, (((1,), (0,)), ((), ())), preferred_element_type=F32)


def head_rows(value, head):
    row = lax.broadcasted_iota(jnp.int32, value.shape, 0)
    return jnp.where((row // HEAD_DIM) == head, value, jnp.zeros_like(value))


def head_lanes(value, head):
    lane = lax.broadcasted_iota(jnp.int32, value.shape, 1)
    return jnp.where((lane // HEAD_DIM) == head, value, jnp.zeros_like(value))


def causal(scores):
    side = scores.shape[0]
    square = scores[:, :side]
    key = lax.broadcasted_iota(jnp.int32, square.shape, 0)
    query = lax.broadcasted_iota(jnp.int32, square.shape, 1)
    square = jnp.where(key <= query, square, NEG)
    if scores.shape[1] == side:
        return square
    return jnp.concatenate([square, scores[:, side:]], axis=1)


def attend_body(length, tile_k, qz, kn, vt, ot, lse_ref):
    def score(sub, head):
        start = sub * tile_k
        return causal(dot(kn[start : start + tile_k, :], qz[head, :, start:]))

    def absorb(sub, head, carry, scores):
        peak, total, mixed = carry
        start = sub * tile_k
        new_peak = jnp.maximum(peak, jnp.max(scores, axis=0, keepdims=True))
        weights = jnp.exp(scores - new_peak)
        fade = jnp.exp(peak - new_peak)
        total = total * fade + jnp.sum(weights, axis=0, keepdims=True)
        values = vt[head * HEAD_DIM : (head + 1) * HEAD_DIM, start : start + tile_k]
        mixed = mixed * fade + dot(values, weights.astype(BF16))
        return (new_peak, total, mixed)

    tiles = [(sub, head) for sub in range(length // tile_k) for head in range(2)]
    carries = [
        (
            jnp.full((1, length), NEG, F32),
            jnp.zeros((1, length), F32),
            jnp.zeros((HEAD_DIM, length), F32),
        )
        for _ in range(2)
    ]
    ahead = score(*tiles[0])
    for number, (sub, head) in enumerate(tiles):
        scores = ahead
        if number + 1 < len(tiles):
            ahead = score(*tiles[number + 1])
        peak, total, mixed = absorb(sub, head, carries[head], scores)
        done = slice(sub * tile_k, (sub + 1) * tile_k)
        rows = slice(head * HEAD_DIM, (head + 1) * HEAD_DIM)
        ot[rows, done] = (mixed[:, :tile_k] / total[:, :tile_k]).astype(BF16)
        lse_ref[0, head : head + 1, done] = peak[:, :tile_k] + jnp.log(total[:, :tile_k])
        carries[head] = (peak[:, tile_k:], total[:, tile_k:], mixed[:, tile_k:])


def attend_kernel(count, slots, tok, tile_k, order, *refs):
    pieces = refs[:count]
    outs = refs[count : 2 * count]
    lse_ref = refs[2 * count]
    qz, kn, vt, ot = refs[2 * count + 1 :]
    for source in range(count):
        for slot in range(slots):
            cols = pl.ds(pl.multiple_of(order[source * slots + slot] * tok, tok), tok)
            take = slice(slot * tok, (slot + 1) * tok)
            query = pieces[source][0, :, take] * jnp.asarray(HEAD_DIM**-0.5, BF16)
            for head in range(2):
                qz[head, :, cols] = head_rows(query, head)
            kn[cols, :] = pieces[source][1, :, take].T
            vt[:, cols] = pieces[source][2, :, take]
    length = count * slots * tok
    attend_body(length, tile_k, qz, kn, vt, ot, lse_ref)
    for source in range(count):
        for slot in range(slots):
            cols = pl.ds(pl.multiple_of(order[source * slots + slot] * tok, tok), tok)
            outs[source][:, slot * tok : (slot + 1) * tok] = ot[:, cols]


def attend(pieces, order, slots):
    count = len(pieces)
    width, span = pieces[0].shape[1:]
    tok = span // slots
    length = count * span
    pairs = width // PAIR
    tile_k = min(256, length)
    grid_spec = pltpu.PrefetchScalarGridSpec(
        num_scalar_prefetch=1,
        grid=(pairs,),
        in_specs=[pl.BlockSpec((3, PAIR, span), lambda p, o: (0, p, 0))] * count,
        out_specs=[pl.BlockSpec((PAIR, span), lambda p, o: (p, 0))] * count
        + [pl.BlockSpec((1, 8, length), lambda p, o: (p, 0, 0))],
        scratch_shapes=[
            pltpu.VMEM((2, PAIR, length), BF16),
            pltpu.VMEM((length, PAIR), BF16),
            pltpu.VMEM((PAIR, length), BF16),
            pltpu.VMEM((PAIR, length), BF16),
        ],
    )
    area = pairs * 2 * length * length // 2
    results = pl.pallas_call(
        functools.partial(attend_kernel, count, slots, tok, tile_k),
        out_shape=[jax.ShapeDtypeStruct((width, span), BF16)] * count
        + [jax.ShapeDtypeStruct((pairs, 8, length), F32)],
        grid_spec=grid_spec,
        compiler_params=pltpu.CompilerParams(
            dimension_semantics=("arbitrary",), vmem_limit_bytes=48 * MIB
        ),
        cost_estimate=pl.CostEstimate(
            flops=area * 1024, bytes_accessed=8 * width * length, transcendentals=area
        ),
        name="attend",
    )(order, *pieces)
    return (results[:count], results[count])


def attend_back_body(
    pieces,
    mixes,
    grads,
    columns,
    tok,
    length,
    tile_q,
    tile_k,
    lse_ref,
    qz,
    gz,
    qn,
    gn,
    kn,
    vn,
    kt,
    inner,
    dq,
    dk,
    dv,
):
    slots = pieces[0].shape[2] // tok
    for source in range(len(pieces)):
        for slot in range(slots):
            cols = columns(source, slot)
            take = slice(slot * tok, (slot + 1) * tok)
            query = pieces[source][0, :, take] * jnp.asarray(HEAD_DIM**-0.5, BF16)
            grad = grads[source][:, take]
            query_rows = query.T
            grad_rows = grad.T
            for head in range(2):
                qz[head, :, cols] = head_rows(query, head)
                gz[head, :, cols] = head_rows(grad, head)
                qn[head, cols, :] = head_lanes(query_rows, head)
                gn[head, cols, :] = head_lanes(grad_rows, head)
            key = pieces[source][1, :, take]
            kt[:, cols] = key
            kn[cols, :] = key.T
            vn[cols, :] = pieces[source][2, :, take].T
            both = grad.astype(F32) * mixes[source][:, take].astype(F32)
            for head in range(2):
                inner[head : head + 1, cols] = jnp.sum(
                    both[head * HEAD_DIM : (head + 1) * HEAD_DIM], axis=0, keepdims=True
                )
    dq[...] = jnp.zeros_like(dq)
    steps = tile_q // tile_k

    def tile(key_start, query_start, width, masked, carry):
        grad_keys, grad_values = carry
        keys = kn[pl.ds(key_start, tile_k), :]
        values = vn[pl.ds(key_start, tile_k), :]
        cols = pl.ds(query_start, width)
        for head in range(2):
            rows = slice(head * HEAD_DIM, (head + 1) * HEAD_DIM)
            scores = dot(keys, qz[head, :, cols])
            if masked:
                scores = causal(scores)
            probs = jnp.exp(scores - lse_ref[0, head : head + 1, cols])
            grad_probs = dot(values, gz[head, :, cols])
            grad_scores = (probs * (grad_probs - inner[head : head + 1, cols])).astype(BF16)
            grad_values = grad_values + dot(probs.astype(BF16), gn[head, cols, :])
            grad_keys = grad_keys + dot(grad_scores, qn[head, cols, :])
            dq[rows, cols] += dot(kt[rows, pl.ds(key_start, tile_k)], grad_scores)
        return (grad_keys, grad_values)

    def one(number, _):
        base = pl.multiple_of(number * tile_q, tile_q)
        for sub in range(steps):
            skip = sub * tile_k
            key_start = pl.multiple_of(base + skip, tile_k)
            carry = (jnp.zeros((tile_k, PAIR), F32), jnp.zeros((tile_k, PAIR), F32))
            carry = tile(key_start, key_start, tile_q - skip, True, carry)

            def body(step, carry):
                return tile(
                    key_start, pl.multiple_of(step * tile_q, tile_q), tile_q, False, carry
                )

            carry = lax.fori_loop(number + 1, length // tile_q, body, carry)
            dk[pl.ds(key_start, tile_k), :] = carry[0]
            dv[pl.ds(key_start, tile_k), :] = carry[1]
        return 0

    lax.fori_loop(0, length // tile_q, one, 0)


def turn_back(dq, dk, dv, cols, cosine, sine):
    half = HEAD_DIM // 2
    results = []
    for grad in (dq[:, cols] * (HEAD_DIM**-0.5), dk[cols, :].T):
        turned = []
        for head in range(2):
            low = head * HEAD_DIM
            first = grad[low : low + half]
            second = grad[low + half : low + 2 * half]
            turned += [first * cosine + second * sine, second * cosine - first * sine]
        results.append(jnp.concatenate(turned, axis=0).astype(BF16))
    results.append(dv[cols, :].T.astype(BF16))
    return results


def attend_back_kernel(count, slots, tok, tile_q, tile_k, order, *refs):
    pieces = refs[:count]
    mixes = refs[count : 2 * count]
    grads = refs[2 * count : 3 * count]
    lse_ref, cos_ref, sin_ref = refs[3 * count : 3 * count + 3]
    outs = refs[3 * count + 3 : 4 * count + 3]
    scratch = refs[4 * count + 3 :]
    dq, dk, dv = scratch[-3:]

    def columns(source, slot):
        return pl.ds(pl.multiple_of(order[source * slots + slot] * tok, tok), tok)

    attend_back_body(
        pieces,
        mixes,
        grads,
        columns,
        tok,
        count * slots * tok,
        tile_q,
        tile_k,
        lse_ref,
        *scratch,
    )
    for source in range(count):
        for slot in range(slots):
            cols = columns(source, slot)
            results = turn_back(dq, dk, dv, cols, cos_ref[:, cols], sin_ref[:, cols])
            for which, result in enumerate(results):
                outs[source][which, :, slot * tok : (slot + 1) * tok] = result


def attend_back(pieces, mixes, grads, lse, cosine, sine, order, slots):
    count = len(pieces)
    width, span = pieces[0].shape[1:]
    tok = span // slots
    length = count * span
    pairs = width // PAIR
    tile_q = min(512, length)
    tile_k = min(256, length)
    triple = pl.BlockSpec((3, PAIR, span), lambda p, o: (0, p, 0))
    single = pl.BlockSpec((PAIR, span), lambda p, o: (p, 0))
    table = pl.BlockSpec((HEAD_DIM // 2, length), lambda p, o: (0, 0))
    grid_spec = pltpu.PrefetchScalarGridSpec(
        num_scalar_prefetch=1,
        grid=(pairs,),
        in_specs=[triple] * count
        + [single] * (2 * count)
        + [pl.BlockSpec((1, 8, length), lambda p, o: (p, 0, 0)), table, table],
        out_specs=[triple] * count,
        scratch_shapes=[
            pltpu.VMEM((2, PAIR, length), BF16),
            pltpu.VMEM((2, PAIR, length), BF16),
            pltpu.VMEM((2, length, PAIR), BF16),
            pltpu.VMEM((2, length, PAIR), BF16),
            pltpu.VMEM((length, PAIR), BF16),
            pltpu.VMEM((length, PAIR), BF16),
            pltpu.VMEM((PAIR, length), BF16),
            pltpu.VMEM((8, length), F32),
            pltpu.VMEM((PAIR, length), F32),
            pltpu.VMEM((length, PAIR), F32),
            pltpu.VMEM((length, PAIR), F32),
        ],
    )
    area = pairs * 2 * length * length // 2
    return pl.pallas_call(
        functools.partial(attend_back_kernel, count, slots, tok, tile_q, tile_k),
        out_shape=[jax.ShapeDtypeStruct((3, width, span), BF16)] * count,
        grid_spec=grid_spec,
        compiler_params=pltpu.CompilerParams(
            dimension_semantics=("arbitrary",), vmem_limit_bytes=56 * MIB
        ),
        cost_estimate=pl.CostEstimate(
            flops=area * 2560, bytes_accessed=16 * width * length, transcendentals=area
        ),
        name="attend_back",
    )(order, *pieces, *mixes, *grads, lse, cosine, sine)


def nt(a, b):
    return lax.dot_general(a, b, (((1,), (1,)), ((), ())), preferred_element_type=F32)


def whole_block(shape):
    zeros = (0,) * len(shape)
    return pl.BlockSpec(shape, lambda *_: zeros)


def parameters(mib):
    return pltpu.CompilerParams(dimension_semantics=("arbitrary",), vmem_limit_bytes=mib * MIB)


def project_kernel(slots, tok, count, rows, place, *refs):
    xs, firsts = refs[:slots], refs[slots : 2 * slots]
    own = refs[2 * slots : 2 * slots + count]
    other = refs[2 * slots + count : 2 * slots + 2 * count]
    cos_ref, sin_ref = refs[2 * slots + 2 * count : 2 * slots + 2 * count + 2]
    other_ref, own_ref, normed_ref, full_ref, gains_ref, column = refs[2 * slots + 2 * count + 2 :]
    step = pl.program_id(0)
    target, kind = step // 3, step % 3
    core = place[1]
    half = jnp.where(target == 0, 1 - core, core)
    depth = normed_ref.shape[1]
    wide = own_ref.shape[1]

    @pl.when(step == 0)
    def _():
        for number in range(count):
            at = pl.ds(pl.multiple_of(place[2 + number] * rows, rows), rows)
            for which in range(3):
                columns = slice(which * wide, (which + 1) * wide)
                full_ref[core, which, at, :] = own[number][:, columns]
                full_ref[1 - core, which, at, :] = other[number][:, columns]
            column[at, :] = own[number][:, 3 * wide :]
        gains_ref[...] = column[...].T[:8].astype(F32)
        gain = gains_ref[0:1, :]
        for slot in range(slots):
            values = xs[slot][...].reshape(tok, depth).astype(F32)
            scale = lax.rsqrt(jnp.mean(values * values, axis=1, keepdims=True) + epsilon)
            normed_ref[slot * tok : (slot + 1) * tok, :] = (values * scale * gain).astype(BF16)

    weight = full_ref[half, kind]
    raw = nt(weight.T, normed_ref[...])

    def store(value):
        @pl.when(target == 0)
        def _():
            other_ref[0] = value

        @pl.when(target == 1)
        def _():
            own_ref[0] = value

    @pl.when(kind < 2)
    def _():
        parts = raw.reshape(wide // HEAD_DIM, 2, HALF, raw.shape[1])
        first, second = parts[:, 0], parts[:, 1]
        cosine, sine = cos_ref[...][None], sin_ref[...][None]
        turned = jnp.stack(
            [first * cosine - second * sine, first * sine + second * cosine], axis=1
        )
        store(turned.reshape(raw.shape).astype(BF16))

    @pl.when(kind == 2)
    def _():
        first = jnp.concatenate(
            [ref[...].reshape(tok, wide).T.astype(F32) for ref in firsts], axis=1
        )
        store((0.5 * raw + 0.5 * first).astype(BF16))


def project(inputs, received, firsts, firsts_received, own, other, cosine, sine, place):
    slots, tok, depth = inputs.shape
    count, rows = len(own), own[0].shape[0]
    wide = depth // 2
    span = slots * tok

    def half(s, p):
        return jnp.where(s < 3, 1 - p[1], p[1])

    x_specs = [pl.BlockSpec((1, tok, depth), lambda s, p: (p[0], 0, 0))]
    x_specs += [whole_block((tok, depth))] * (slots - 1)
    first_specs = [pl.BlockSpec((1, tok, wide), lambda s, p: (p[0], 0, half(s, p)))]
    first_specs += [pl.BlockSpec((tok, wide), lambda s, p: (0, half(s, p)))] * (slots - 1)
    grid_spec = pltpu.PrefetchScalarGridSpec(
        num_scalar_prefetch=1,
        grid=(6,),
        in_specs=x_specs
        + first_specs
        + [whole_block(own[0].shape)] * (2 * count)
        + [whole_block((HALF, span))] * 2,
        out_specs=[
            pl.BlockSpec((1, wide, span), lambda s, p: (jnp.minimum(s, 2), 0, 0)),
            pl.BlockSpec((1, wide, span), lambda s, p: (jnp.maximum(s - 3, 0), 0, 0)),
            whole_block((span, depth)),
            whole_block((2, 3, depth, wide)),
            whole_block((8, depth)),
        ],
        scratch_shapes=[pltpu.VMEM((depth, 128), BF16)],
    )
    return pl.pallas_call(
        functools.partial(project_kernel, slots, tok, count, rows),
        out_shape=[
            jax.ShapeDtypeStruct((3, wide, span), BF16),
            jax.ShapeDtypeStruct((3, wide, span), BF16),
            jax.ShapeDtypeStruct((span, depth), BF16),
            jax.ShapeDtypeStruct((2, 3, depth, wide), BF16),
            jax.ShapeDtypeStruct((8, depth), F32),
        ],
        grid_spec=grid_spec,
        compiler_params=parameters(56),
        cost_estimate=pl.CostEstimate(
            flops=6 * span * depth * depth,
            bytes_accessed=2 * (8 * span * depth + 6 * depth * depth),
            transcendentals=0,
        ),
        name="project",
    )(place, inputs, *received, firsts, *firsts_received, *own, *other, cosine, sine)


def output_kernel(slots, tok, count, rows, place, *refs):
    xs = refs[:slots]
    own = refs[slots : slots + count]
    other = refs[slots + count : slots + 2 * count]
    att_other, att_own, gains_ref = refs[slots + 2 * count : slots + 2 * count + 3]
    middle_ref, normed_ref, full_ref = refs[slots + 2 * count + 3 :]
    step = pl.program_id(0)
    core = place[1]
    wide = att_own.shape[0]
    depth = 2 * wide
    mine = pl.ds(pl.multiple_of(core * wide, wide), wide)
    others = pl.ds(pl.multiple_of((1 - core) * wide, wide), wide)

    @pl.when(step == 0)
    def _():
        for number in range(count):
            at = pl.ds(pl.multiple_of(place[2 + number] * rows, rows), rows)
            full_ref[at, mine] = own[number][...]
            full_ref[at, others] = other[number][...]

    total = dot(att_own[...].T, full_ref[mine, :]) + dot(att_other[...].T, full_ref[others, :])
    for slot in range(slots):

        @pl.when(step == slot)
        def _(slot=slot):
            middle_ref[...] = xs[slot][...].reshape(tok, depth).astype(F32) + total

    middle = middle_ref[...]
    scale = lax.rsqrt(jnp.mean(middle * middle, axis=1, keepdims=True) + epsilon)
    normed_ref[...] = (middle * scale * gains_ref[1:2, :]).astype(BF16)


def output_projection(inputs, received, own, other, att_other, att_own, gains, place):
    slots, tok, depth = inputs.shape
    count, rows = len(own), own[0].shape[0]
    wide = depth // 2
    span = slots * tok
    x_specs = [pl.BlockSpec((1, tok, depth), lambda s, p: (p[0], 0, 0))]
    x_specs += [whole_block((tok, depth))] * (slots - 1)
    grid_spec = pltpu.PrefetchScalarGridSpec(
        num_scalar_prefetch=1,
        grid=(slots,),
        in_specs=x_specs
        + [whole_block(own[0].shape)] * (2 * count)
        + [pl.BlockSpec((wide, tok), lambda s, p: (0, s))] * 2
        + [whole_block((8, depth))],
        out_specs=[
            pl.BlockSpec((tok, depth), lambda s, p: (s, 0)),
            pl.BlockSpec((tok, depth), lambda s, p: (s, 0)),
            whole_block((depth, depth)),
        ],
    )
    return pl.pallas_call(
        functools.partial(output_kernel, slots, tok, count, rows),
        out_shape=[
            jax.ShapeDtypeStruct((span, depth), F32),
            jax.ShapeDtypeStruct((span, depth), BF16),
            jax.ShapeDtypeStruct((depth, depth), BF16),
        ],
        grid_spec=grid_spec,
        compiler_params=parameters(56),
        cost_estimate=pl.CostEstimate(
            flops=2 * span * depth * depth,
            bytes_accessed=12 * span * depth + 4 * depth * depth,
            transcendentals=0,
        ),
        name="output_projection",
    )(place, inputs, *received, *own, *other, att_other, att_own, gains)


def mlp_kernel(slots, tok, count, rows, down_rows, blocks, place, *refs):
    grads = refs[:slots]
    middle_ref, normed_ref, gains_ref = refs[slots : slots + 3]
    base = slots + 3
    own_g, other_g, own_u, other_u, own_d, other_d = (
        refs[base + number * count : base + (number + 1) * count] for number in range(6)
    )
    (
        out_ref,
        send_ref,
        grad_ref,
        low_ref,
        gain_ref,
        gu_send,
        gu_keep,
        d_send,
        d_keep,
        wgu,
        wd,
        og,
        normed_t,
        acc,
        back,
        sems,
    ) = refs[base + 6 * count :]
    step = pl.program_id(0)
    core = place[1]
    depth = og.shape[1]
    wide = depth // 2
    strip = 128
    half_width = blocks * strip
    mine = pl.ds(pl.multiple_of(core * wide, wide), wide)
    others = pl.ds(pl.multiple_of((1 - core) * wide, wide), wide)

    def loads():
        copies = []
        for number in range(count):
            at = pl.ds(pl.multiple_of(place[2 + number] * rows, rows), rows)
            for which, (gate, up) in enumerate(((own_g, own_u), (other_g, other_u))):
                copies.append((gate[number], wgu.at[which, at, pl.ds(0, half_width)]))
                copies.append((up[number], wgu.at[which, at, pl.ds(half_width, half_width)]))
        for number in range(count):
            at = pl.ds(pl.multiple_of(place[2 + number] * down_rows, down_rows), down_rows)
            copies.append((own_d[number], wd.at[at, mine]))
            copies.append((other_d[number], wd.at[at, others]))
        return [
            pltpu.make_async_copy(source, target, sems.at[number])
            for number, (source, target) in enumerate(copies)
        ]

    @pl.when(step == 0)
    def _():
        copies = loads()
        for copy in copies:
            copy.start()
        for slot in range(slots):
            og[slot * tok : (slot + 1) * tok, :] = grads[slot][...].reshape(tok, depth)
        normed_t[...] = normed_ref[...].T
        acc[...] = jnp.zeros_like(acc)
        back[...] = jnp.zeros_like(back)
        for copy in copies:
            copy.wait()

    at = pl.ds(pl.multiple_of(step * strip, strip), strip)
    up_at = pl.ds(pl.multiple_of(half_width + step * strip, strip), strip)
    gate_w = jnp.concatenate([wgu[0, :, at], wgu[1, :, at]], axis=1)
    up_w = jnp.concatenate([wgu[0, :, up_at], wgu[1, :, up_at]], axis=1)
    own_rows = pl.ds(pl.multiple_of(core * half_width + step * strip, strip), strip)
    other_rows = pl.ds(pl.multiple_of((1 - core) * half_width + step * strip, strip), strip)
    down_w = jnp.concatenate([wd[own_rows, :], wd[other_rows, :]], axis=0)
    normed = normed_ref[...]
    gate = dot(normed, gate_w)
    up = dot(normed, up_w)
    grad_active = nt(og[...], down_w)
    sigma = jax.nn.sigmoid(gate)
    silu = gate * sigma
    active = (silu * up).astype(BF16)
    grad_up = (grad_active * silu).astype(BF16)
    grad_gate = (grad_active * up * sigma * (1.0 + gate * (1.0 - sigma))).astype(BF16)
    acc[...] += dot(active, down_w)
    back[...] += nt(grad_gate, gate_w) + nt(grad_up, up_w)
    grad_gate_w = dot(normed_t[...], grad_gate).astype(BF16)
    gu_keep[0] = grad_gate_w[:, :strip]
    gu_send[0] = grad_gate_w[:, strip:]
    grad_up_w = dot(normed_t[...], grad_up).astype(BF16)
    gu_keep[1] = grad_up_w[:, :strip]
    gu_send[1] = grad_up_w[:, strip:]
    active_t = active.T
    kept = dot(active_t, og[:, mine]).astype(BF16)
    sent = dot(active_t, og[:, others]).astype(BF16)
    d_keep[core] = kept[:strip]
    d_keep[1 - core] = kept[strip:]
    d_send[core] = sent[:strip]
    d_send[1 - core] = sent[strip:]

    @pl.when(step == blocks - 1)
    def _():
        gain = gains_ref[1:2, :]
        chunk = min(128, tok)
        gain_ref[...] = jnp.zeros_like(gain_ref)
        for slot in range(slots):

            def finish(number, _, slot=slot):
                local = pl.ds(pl.multiple_of(number * chunk, chunk), chunk)
                some = pl.ds(pl.multiple_of(slot * tok + number * chunk, chunk), chunk)
                middle = middle_ref[some, :]
                scale = lax.rsqrt(jnp.mean(middle * middle, axis=1, keepdims=True) + epsilon)
                result = middle + acc[some, :]
                if slot == 0:
                    out_ref[0, local, :] = result
                else:
                    send_ref[pl.ds(pl.multiple_of((slot - 1) * tok + number * chunk, chunk), chunk), :] = (
                        result.astype(BF16)
                    )
                grad = back[some, :]
                gain_ref[0:1, :] += jnp.sum(grad * middle * scale, axis=0, keepdims=True)
                weighted = grad * gain
                inner = jnp.mean(weighted * middle, axis=1, keepdims=True)
                grad_middle = (
                    scale * weighted
                    - middle * (scale * scale * scale) * inner
                    + og[some, :].astype(F32)
                )
                grad_ref[some, :] = grad_middle
                low_ref[some, :] = grad_middle.astype(BF16)
                return 0

            lax.fori_loop(0, tok // chunk, finish, 0)


def mlp(grads, grads_received, middle, normed, gains, gate, up, down, place):
    slots, tok, depth = grads.shape
    own_d, other_d = down
    count, rows = len(own_d), gate[0][0].shape[0]
    down_rows = own_d[0].shape[0]
    half_width = gate[0][0].shape[1]
    wide = depth // 2
    span = slots * tok
    blocks = half_width // 128
    once = pl.Buffered(1)
    g_specs = [pl.BlockSpec((1, tok, depth), lambda s, p: (p[0], 0, 0), pipeline_mode=once)]
    g_specs += [pl.BlockSpec((tok, depth), lambda s, p: (0, 0), pipeline_mode=once)] * (slots - 1)
    gu_spec = pl.BlockSpec((2, depth, 128), lambda s, p: (0, 0, s))
    d_spec = pl.BlockSpec((2, 128, wide), lambda s, p: (0, s, 0))
    grid_spec = pltpu.PrefetchScalarGridSpec(
        num_scalar_prefetch=1,
        grid=(blocks,),
        in_specs=g_specs
        + [
            pl.BlockSpec((span, depth), lambda s, p: (0, 0), pipeline_mode=once),
            pl.BlockSpec((span, depth), lambda s, p: (0, 0), pipeline_mode=once),
            whole_block((8, depth)),
        ]
        + [pl.BlockSpec(memory_space=pl.ANY)] * (6 * count),
        out_specs=[
            pl.BlockSpec((1, tok, depth), lambda s, p: (p[0], 0, 0), pipeline_mode=once),
            pl.BlockSpec(((slots - 1) * tok, depth), lambda s, p: (0, 0), pipeline_mode=once),
            pl.BlockSpec((span, depth), lambda s, p: (0, 0), pipeline_mode=once),
            pl.BlockSpec((span, depth), lambda s, p: (0, 0), pipeline_mode=once),
            whole_block((8, depth)),
            gu_spec,
            gu_spec,
            d_spec,
            d_spec,
        ],
        scratch_shapes=[
            pltpu.VMEM((2, depth, 2 * half_width), BF16),
            pltpu.VMEM((2 * half_width, depth), BF16),
            pltpu.VMEM((span, depth), BF16),
            pltpu.VMEM((depth, span), BF16),
            pltpu.VMEM((span, depth), F32),
            pltpu.VMEM((span, depth), F32),
            pltpu.SemaphoreType.DMA((6 * count,)),
        ],
    )
    return pl.pallas_call(
        functools.partial(mlp_kernel, slots, tok, count, rows, down_rows, blocks),
        out_shape=[
            jax.ShapeDtypeStruct((slots, tok, depth), F32),
            jax.ShapeDtypeStruct(((slots - 1) * tok, depth), BF16),
            jax.ShapeDtypeStruct((span, depth), F32),
            jax.ShapeDtypeStruct((span, depth), BF16),
            jax.ShapeDtypeStruct((8, depth), F32),
            jax.ShapeDtypeStruct((2, depth, half_width), BF16),
            jax.ShapeDtypeStruct((2, depth, half_width), BF16),
            jax.ShapeDtypeStruct((2, half_width, wide), BF16),
            jax.ShapeDtypeStruct((2, half_width, wide), BF16),
        ],
        grid_spec=grid_spec,
        compiler_params=parameters(63),
        cost_estimate=pl.CostEstimate(
            flops=16 * span * depth * 2 * half_width,
            bytes_accessed=24 * depth * half_width + 20 * span * depth,
            transcendentals=2 * span * half_width,
        ),
        name="mlp",
    )(
        place,
        grads,
        *grads_received,
        middle,
        normed,
        gains,
        *gate[0],
        *gate[1],
        *up[0],
        *up[1],
        *own_d,
        *other_d,
    )


def grad_attended_kernel(place, low_ref, full_ref, att_other, att_own, ga_other, ga_own, sent, kept):
    step = pl.program_id(0)
    core = place[1]
    wide = att_own.shape[0]
    mine = pl.ds(pl.multiple_of(core * wide, wide), wide)
    others = pl.ds(pl.multiple_of((1 - core) * wide, wide), wide)
    for number, (att, result) in enumerate(((att_other, ga_other), (att_own, ga_own))):

        @pl.when(step == number)
        def _(att=att, result=result):
            result[...] = nt(full_ref[...], low_ref[...]).astype(BF16)
            kept[...] = dot(att[...], low_ref[:, mine]).astype(BF16)
            sent[...] = dot(att[...], low_ref[:, others]).astype(BF16)


def grad_attended(low, full, att_other, att_own, place):
    span, depth = low.shape
    wide = depth // 2

    def half(s, p):
        return jnp.where(s == 0, 1 - p[1], p[1])

    row_spec = pl.BlockSpec((wide, wide), lambda s, p: (half(s, p), 0))
    grid_spec = pltpu.PrefetchScalarGridSpec(
        num_scalar_prefetch=1,
        grid=(2,),
        in_specs=[
            whole_block((span, depth)),
            pl.BlockSpec((wide, depth), lambda s, p: (half(s, p), 0)),
            whole_block((wide, span)),
            whole_block((wide, span)),
        ],
        out_specs=[whole_block((wide, span)), whole_block((wide, span)), row_spec, row_spec],
    )
    return pl.pallas_call(
        grad_attended_kernel,
        out_shape=[
            jax.ShapeDtypeStruct((wide, span), BF16),
            jax.ShapeDtypeStruct((wide, span), BF16),
            jax.ShapeDtypeStruct((depth, wide), BF16),
            jax.ShapeDtypeStruct((depth, wide), BF16),
        ],
        grid_spec=grid_spec,
        compiler_params=parameters(48),
        cost_estimate=pl.CostEstimate(
            flops=4 * span * depth * depth,
            bytes_accessed=6 * span * depth + 4 * depth * depth,
            transcendentals=0,
        ),
        name="grad_attended",
    )(place, low, full, att_other, att_own)


def tail_kernel(slots, tok, place, *refs):
    xs = refs[:slots]
    (
        back_other,
        back_own,
        full_ref,
        normed_ref,
        grad_ref,
        gains_ref,
        mlp_gain_ref,
        out_ref,
        send_ref,
        first_ref,
        first_send,
        gain_ref,
        sent,
        kept,
        normed_t,
        acc,
    ) = refs[slots:]
    step = pl.program_id(0)
    target, kind = step // 3, step % 3
    depth = acc.shape[1]

    @pl.when(step == 0)
    def _():
        normed_t[...] = normed_ref[...].T
        acc[...] = jnp.zeros_like(acc)

    def part(back, result):
        grad = back[0]

        @pl.when(kind == 2)
        def _():
            rows = 0.5 * grad.astype(F32).T
            first_ref[0] = rows[:tok]
            first_send[...] = rows[tok:].astype(BF16)

        grad = grad * jnp.where(kind == 2, 0.5, 1.0).astype(BF16)
        acc[...] += nt(grad.T, full_ref[0, 0])
        result[0] = nt(normed_t[...], grad).astype(BF16)

    @pl.when(target == 0)
    def _():
        part(back_other, sent)

    @pl.when(target == 1)
    def _():
        part(back_own, kept)

    @pl.when(step == 5)
    def _():
        gain = gains_ref[0:1, :]
        chunk = min(128, tok)
        gain_ref[...] = jnp.zeros_like(gain_ref)
        gain_ref[1:2, :] = mlp_gain_ref[0:1, :]
        for slot in range(slots):

            def finish(number, _, slot=slot):
                local = pl.ds(pl.multiple_of(number * chunk, chunk), chunk)
                some = pl.ds(pl.multiple_of(slot * tok + number * chunk, chunk), chunk)
                if slot == 0:
                    values = xs[slot][0, local, :].astype(F32)
                else:
                    values = xs[slot][local, :].astype(F32)
                scale = lax.rsqrt(jnp.mean(values * values, axis=1, keepdims=True) + epsilon)
                grad = acc[some, :]
                gain_ref[0:1, :] += jnp.sum(grad * values * scale, axis=0, keepdims=True)
                weighted = grad * gain
                inner = jnp.mean(weighted * values, axis=1, keepdims=True)
                result = (
                    scale * weighted
                    - values * (scale * scale * scale) * inner
                    + grad_ref[some, :]
                )
                if slot == 0:
                    out_ref[0, local, :] = result
                else:
                    send_ref[pl.ds(pl.multiple_of((slot - 1) * tok + number * chunk, chunk), chunk), :] = (
                        result.astype(BF16)
                    )
                return 0

            lax.fori_loop(0, tok // chunk, finish, 0)


def tail(inputs, received, back_other, back_own, full, normed, grad_middle, gains, mlp_gain, place):
    slots, tok, depth = inputs.shape
    wide = depth // 2
    span = slots * tok
    rest = (slots - 1) * tok
    once = pl.Buffered(1)

    def half(s, p):
        return jnp.where(s < 3, 1 - p[1], p[1])

    x_specs = [pl.BlockSpec((1, tok, depth), lambda s, p: (p[0], 0, 0))]
    x_specs += [whole_block((tok, depth))] * (slots - 1)
    grid_spec = pltpu.PrefetchScalarGridSpec(
        num_scalar_prefetch=1,
        grid=(6,),
        in_specs=x_specs
        + [
            pl.BlockSpec((1, wide, span), lambda s, p: (jnp.minimum(s, 2), 0, 0)),
            pl.BlockSpec((1, wide, span), lambda s, p: (jnp.maximum(s - 3, 0), 0, 0)),
            pl.BlockSpec((1, 1, depth, wide), lambda s, p: (half(s, p), s % 3, 0, 0)),
            whole_block((span, depth)),
            pl.BlockSpec((span, depth), lambda s, p: (0, 0), pipeline_mode=once),
            whole_block((8, depth)),
            whole_block((8, depth)),
        ],
        out_specs=[
            pl.BlockSpec((1, tok, depth), lambda s, p: (p[0], 0, 0)),
            whole_block((rest, depth)),
            pl.BlockSpec((1, tok, wide), lambda s, p: (p[0], 0, half(s, p))),
            pl.BlockSpec((rest, wide), lambda s, p: (0, half(s, p))),
            whole_block((8, depth)),
            pl.BlockSpec((1, depth, wide), lambda s, p: (jnp.minimum(s, 2), 0, 0)),
            pl.BlockSpec((1, depth, wide), lambda s, p: (jnp.maximum(s - 3, 0), 0, 0)),
        ],
        scratch_shapes=[pltpu.VMEM((depth, span), BF16), pltpu.VMEM((span, depth), F32)],
    )
    return pl.pallas_call(
        functools.partial(tail_kernel, slots, tok),
        out_shape=[
            jax.ShapeDtypeStruct((slots, tok, depth), F32),
            jax.ShapeDtypeStruct((rest, depth), BF16),
            jax.ShapeDtypeStruct((slots, tok, depth), F32),
            jax.ShapeDtypeStruct((rest, depth), BF16),
            jax.ShapeDtypeStruct((8, depth), F32),
            jax.ShapeDtypeStruct((3, depth, wide), BF16),
            jax.ShapeDtypeStruct((3, depth, wide), BF16),
        ],
        grid_spec=grid_spec,
        compiler_params=parameters(60),
        cost_estimate=pl.CostEstimate(
            flops=12 * span * depth * depth,
            bytes_accessed=24 * span * depth + 12 * depth * depth,
            transcendentals=0,
        ),
        name="tail",
    )(
        place, inputs, *received, back_other, back_own, full, normed, grad_middle, gains, mlp_gain
    )


def land_kernel(place, whole_ref, part_ref, out_ref):
    out_ref[0] = part_ref[...].astype(F32)


def land(whole, part, slot):
    _, tok, depth = whole.shape
    tile = min(256, tok)
    grid_spec = pltpu.PrefetchScalarGridSpec(
        num_scalar_prefetch=1,
        grid=(tok // tile,),
        in_specs=[
            pl.BlockSpec(memory_space=pl.ANY),
            pl.BlockSpec((tile, depth), lambda s, p: (s, 0)),
        ],
        out_specs=pl.BlockSpec((1, tile, depth), lambda s, p: (p[0], s, 0)),
    )
    return pl.pallas_call(
        land_kernel,
        out_shape=jax.ShapeDtypeStruct(whole.shape, F32),
        grid_spec=grid_spec,
        input_output_aliases={1: 0},
        compiler_params=parameters(16),
        cost_estimate=pl.CostEstimate(
            flops=tok * depth, bytes_accessed=6 * tok * depth, transcendentals=0
        ),
        name="land",
    )(slot, whole, part)


MESH = pl.DeviceIdType.MESH


def seats():
    shard = lax.axis_index("fsdp")
    seat = lax.axis_index("seq")
    return (shard // 2, shard % 2, seat // 2, seat % 2)


def meet(line, keys):
    shard = lax.axis_index("fsdp")
    seat = lax.axis_index("seq")
    partners = []
    if "z" in keys:
        partners += [{"fsdp": lax.rem(shard + 2 * jump, 2 * line)} for jump in range(1, line)]
    if "y" in keys:
        partners.append({"fsdp": shard + 1 - 2 * (shard % 2)})
    if "x" in keys:
        partners.append({"seq": lax.rem(seat + 2, 4)})
    if "diagonal" in keys:
        partners.append({"seq": 3 - seat})
    if "core" in keys:
        partners.append({"seq": seat + 1 - 2 * (seat % 2)})
    barrier = pltpu.get_barrier_semaphore()
    for partner in partners:
        pl.semaphore_signal(barrier, inc=1, device_id=partner, device_id_type=MESH)
    pl.semaphore_wait(barrier, len(partners))


def send(source, target, sems, number, partner):
    return pltpu.make_async_remote_copy(
        src_ref=source,
        dst_ref=target,
        send_sem=sems.at[0, number],
        recv_sem=sems.at[1, number],
        device_id=partner,
        device_id_type=MESH,
    )


def to_core_partner():
    seat = lax.axis_index("seq")
    return {"seq": seat + 1 - 2 * (seat % 2)}


def to_x_partner():
    return {"seq": lax.rem(lax.axis_index("seq") + 2, 4)}


def to_y_partner():
    shard = lax.axis_index("fsdp")
    return {"fsdp": shard + 1 - 2 * (shard % 2)}


def to_z_partner(line, jump):
    return {"fsdp": lax.rem(lax.axis_index("fsdp") + 2 * jump, 2 * line)}


class Gather:
    def __init__(self, line, shard, own, other, sems, share=0, columns=None):
        self.line, self.shard, self.own, self.other = line, shard, own, other
        self.sems = sems
        z, y, x, core = seats()
        self.z, self.y, self.share = z, y, share
        rows, width = own.shape[2:]
        first, size = columns or (0, width)
        self.columns = pl.ds(first, size)
        if shard.shape[1] == width:
            self.source = self.columns
        else:
            self.source = pl.ds(pl.multiple_of(core * width + first, 128), size)
        if share:
            step = math.gcd(share, rows)
            self.rows = pl.ds(pl.multiple_of(x * share, step), rows - share)
            self.given = pl.ds(pl.multiple_of(x * (rows - share), step), share)
            self.taken = pl.ds(pl.multiple_of((1 - x) * (rows - share), step), share)
        else:
            self.rows = slice(None)

    def here(self):
        return pltpu.make_async_copy(
            self.shard.at[self.rows, self.source],
            self.own.at[self.z, self.y, self.rows, self.columns],
            self.sems.at[0, self.line + 3],
        )

    def along_z(self):
        return [
            send(
                self.shard.at[self.rows, self.source],
                self.own.at[self.z, self.y, self.rows, self.columns],
                self.sems,
                jump - 1,
                to_z_partner(self.line, jump),
            )
            for jump in range(1, self.line)
        ]

    def along_y(self):
        part = self.own.at[:, self.y, self.rows, self.columns]
        return send(part, part, self.sems, self.line - 1, to_y_partner())

    def along_x(self):
        part = self.own.at[:, :, self.given, self.columns]
        return send(part, part, self.sems, self.line, to_x_partner())

    def to_core(self, late):
        if self.share:
            at = (slice(None), slice(None), self.taken if late else self.rows, self.columns)
        else:
            at = (slice(None), 1 - self.y if late else self.y, slice(None), self.columns)
        return send(
            self.own.at[at],
            self.other.at[at],
            self.sems,
            self.line + 1 + late,
            to_core_partner(),
        )

    def start_z(self):
        self.here().start()
        for copy in self.along_z():
            copy.start()

    def wait_z(self):
        self.here().wait()
        for copy in self.along_z():
            copy.wait()

    def wait_core(self):
        self.to_core(0).wait()
        self.to_core(1).wait()


def gather_sems(line):
    return pltpu.SemaphoreType.DMA((2, line + 4))


def front_kernel(line, tok, *refs):
    (
        inputs,
        firsts,
        grads,
        q_shard,
        k_shard,
        v_shard,
        o_shard,
        d_shard,
        gains_shard,
        cos_ref,
        sin_ref,
        x_received,
        f_received,
        g_received,
        heads_own,
        heads_received,
        normed_ref,
        full_ref,
        gains_ref,
        o_own,
        o_other,
        d_own,
        xs,
        fs,
        q_own,
        q_other,
        k_own,
        k_other,
        v_own,
        v_other,
        outgoing,
        all_gains,
        q_sems,
        k_sems,
        v_sems,
        w_sems,
        o_sems,
        d_sems,
        gain_sems,
        swap_sems,
        head_sems,
        local_sems,
    ) = refs
    step = pl.program_id(0)
    _, _, side, core = seats()
    wide = outgoing.shape[1]
    depth = 2 * wide
    gathers = [
        Gather(line, q_shard, q_own, q_other, q_sems),
        Gather(line, k_shard, k_own, k_other, k_sems),
        Gather(line, v_shard, v_own, v_other, v_sems, columns=(0, wide // 2)),
        Gather(line, v_shard, v_own, v_other, w_sems, columns=(wide // 2, wide // 2)),
    ]
    query, key, value, value_more = gathers
    gains = Gather(line, gains_shard, all_gains, all_gains, gain_sems)
    out = Gather(line, o_shard, o_own, o_other, o_sems)
    down = Gather(line, d_shard, d_own, d_own, d_sems, d_own.shape[2] // 2)
    swap_x = send(inputs.at[1 - side], x_received, swap_sems, 0, to_x_partner())
    swap_f = send(firsts.at[1 - side], f_received, swap_sems, 1, to_x_partner())
    early = pl.ds(0, tok // 2)
    swap_g = send(
        grads.at[1 - side, early], g_received.at[early], swap_sems, 2, to_x_partner()
    )
    load_x = pltpu.make_async_copy(inputs.at[side], xs.at[pl.ds(0, tok), :], local_sems.at[0])
    load_f = pltpu.make_async_copy(firsts.at[side], fs.at[pl.ds(0, tok), :], local_sems.at[1])
    more_x = pltpu.make_async_copy(x_received, xs.at[pl.ds(tok, tok), :], local_sems.at[2])
    more_f = pltpu.make_async_copy(f_received, fs.at[pl.ds(tok, tok), :], local_sems.at[3])

    def weight(halves, columns):
        return halves[:, :, :, columns].reshape(depth, wide)

    def heads(number):
        return send(
            outgoing.at[number], heads_received.at[number], head_sems, number, to_core_partner()
        )

    saves = []
    for number, (mine, others) in enumerate(((q_own, q_other), (k_own, k_other), (v_own, v_other))):
        for which, ref in ((0, mine), (1, others)):
            half = core if which == 0 else 1 - core
            saves.append(
                pltpu.make_async_copy(
                    ref.at[:, :, :, pl.ds(0, wide)],
                    full_ref.at[half, number],
                    local_sems.at[4 + 2 * number + which],
                )
            )

    @pl.when(step == 0)
    def _():
        meet(line, ("z", "y", "x", "core"))
        swap_x.start()
        load_x.start()
        load_f.start()
        gains.start_z()
        query.start_z()
        gains.wait_z()
        gains.along_y().start()
        query.wait_z()
        query.along_y().start()
        query.to_core(0).start()
        key.start_z()
        key.wait_z()
        key.along_y().start()
        key.to_core(0).start()
        value.start_z()
        swap_x.wait()
        more_x.start()
        swap_f.start()
        gains.along_y().wait()
        query.along_y().wait()
        query.to_core(1).start()
        for number in range(2 * line):
            columns = slice(number * 128, (number + 1) * 128)
            gains_ref[:, columns] = all_gains[number // 2, number % 2]
        gain = gains_ref[0:1, :]
        chunk = min(256, 2 * tok)
        load_x.wait()
        more_x.wait()

        def norm(number, _):
            at = pl.ds(pl.multiple_of(number * chunk, chunk), chunk)
            values = xs[at, :].astype(F32)
            scale = lax.rsqrt(jnp.mean(values * values, axis=1, keepdims=True) + epsilon)
            normed_ref[at, :] = (values * scale * gain).astype(BF16)
            return 0

        lax.fori_loop(0, 2 * tok // chunk, norm, 0)
        value.wait_z()
        value.along_y().start()
        value.to_core(0).start()
        value_more.start_z()

    @pl.when(step == 1)
    def _():
        key.along_y().wait()
        key.to_core(1).start()
        value_more.wait_z()
        value_more.along_y().start()
        value_more.to_core(0).start()
        out.start_z()

    @pl.when(step == 2)
    def _():
        swap_f.wait()
        more_f.start()
        swap_g.start()
        value.along_y().wait()
        value.to_core(1).start()
        value_more.along_y().wait()
        value_more.to_core(1).start()
        out.wait_z()
        out.along_y().start()
        out.to_core(0).start()
        down.start_z()
        load_f.wait()
        more_f.wait()

    @pl.when(step == 3)
    def _():
        query.wait_core()
        key.wait_core()
        for save in saves[:4]:
            save.start()

    @pl.when(step == 5)
    def _():
        value.wait_core()
        value_more.wait_core()
        for save in saves[4:]:
            save.start()
        out.along_y().wait()
        out.to_core(1).start()

    def project_one(halves, kind, mine):
        raw = nt(weight(halves, slice(0, wide)).T, normed_ref[...])
        if kind < 2:
            parts = raw.reshape(wide // HEAD_DIM, 2, HALF, raw.shape[1])
            first, second = parts[:, 0], parts[:, 1]
            cosine, sine = (
                jnp.concatenate([ref[:, block_of(1, slot, tok)] for slot in range(2)], axis=1)[None]
                for ref in (cos_ref, sin_ref)
            )
            turned = jnp.stack(
                [first * cosine - second * sine, first * sine + second * cosine], axis=1
            )
            result = turned.reshape(raw.shape).astype(BF16)
        else:
            half = core if mine else 1 - core
            first = fs[:, pl.ds(pl.multiple_of(half * wide, wide), wide)]
            result = (0.5 * raw + 0.5 * first.astype(F32).T).astype(BF16)
        if mine:
            heads_own[0] = result
        else:
            outgoing[kind] = result
            heads(kind).start()

    for number, (halves, kind, mine) in enumerate(
        (
            (q_own, 0, True),
            (k_own, 1, True),
            (v_own, 2, True),
            (q_other, 0, False),
            (k_other, 1, False),
            (v_other, 2, False),
        )
    ):

        @pl.when(step == number)
        def _(halves=halves, kind=kind, mine=mine):
            project_one(halves, kind, mine)

    @pl.when(step == 5)
    def _():
        for number in range(3):
            heads(number).wait()
        for save in saves:
            save.wait()
        out.wait_core()
        down.wait_z()
        swap_g.wait()


def front(inputs, firsts, grads, q, k, v, o, d, gains, cosine, sine, line):
    slots, tok, depth = inputs.shape
    span = slots * tok
    wide = depth // 2
    rows, down_rows = q.shape[0], d.shape[0]
    anywhere = pl.BlockSpec(memory_space=pl.ANY)
    weights = lambda columns: pltpu.VMEM((line, 2, rows, columns), BF16)
    return pl.pallas_call(
        functools.partial(front_kernel, line, tok),
        grid=(6,),
        in_specs=[anywhere] * 9 + [whole_block(cosine.shape)] * 2,
        out_specs=[
            anywhere,
            anywhere,
            anywhere,
            pl.BlockSpec((1, wide, span), lambda s: (jnp.minimum(s, 2), 0, 0)),
            anywhere,
            whole_block((span, depth)),
            anywhere,
            whole_block((8, depth)),
            anywhere,
            anywhere,
            anywhere,
        ],
        out_shape=[
            jax.ShapeDtypeStruct((tok, depth), BF16),
            jax.ShapeDtypeStruct((tok, depth), BF16),
            jax.ShapeDtypeStruct((tok, depth), BF16),
            jax.ShapeDtypeStruct((3, wide, span), BF16),
            jax.ShapeDtypeStruct((3, wide, span), BF16),
            jax.ShapeDtypeStruct((span, depth), BF16),
            jax.ShapeDtypeStruct((2, 3, line, 2, rows, wide), BF16),
            jax.ShapeDtypeStruct((8, depth), F32),
            jax.ShapeDtypeStruct((line, 2, rows, wide), BF16),
            jax.ShapeDtypeStruct((line, 2, rows, wide), BF16),
            jax.ShapeDtypeStruct((line, 2, down_rows, wide), BF16),
        ],
        scratch_shapes=[
            pltpu.VMEM((span, depth), BF16),
            pltpu.VMEM((span, depth), BF16),
            weights(wide),
            weights(wide),
            weights(wide),
            weights(wide),
            weights(wide),
            weights(wide),
            pltpu.VMEM((3, wide, span), BF16),
            pltpu.VMEM((line, 2, 8, 128), F32),
        ]
        + [gather_sems(line)] * 7
        + [
            pltpu.SemaphoreType.DMA((2, 3)),
            pltpu.SemaphoreType.DMA((2, 3)),
            pltpu.SemaphoreType.DMA((10,)),
        ],
        compiler_params=pltpu.CompilerParams(
            dimension_semantics=("arbitrary",),
            vmem_limit_bytes=63 * MIB,
            collective_id=1,
            has_side_effects=True,
        ),
        cost_estimate=pl.CostEstimate(
            flops=6 * span * depth * depth,
            bytes_accessed=2 * (8 * span * depth + 6 * depth * depth),
            transcendentals=0,
        ),
        name="front",
    )(inputs, firsts, grads, q, k, v, o, d, gains, cosine, sine)


def block_of(source, slot, tok):
    _, _, side, core = seats()
    rank = 1 - core if source == 0 else core
    group = lax.rem(side + slot, 2)
    return pl.ds(pl.multiple_of((group * 2 + rank) * tok, tok), tok)


def attend_carry_kernel(line, tok, tile_k, *refs):
    (
        received,
        own,
        inputs,
        x_received,
        gains_ref,
        o_own,
        o_other,
        grad_in,
        _,
        d_in,
        g_shard,
        u_shard,
        mix_received,
        mix_own,
        lse_ref,
        middle_ref,
        normed_ref,
        full_ref,
        att_other,
        grad_received,
        d_own,
        d_other,
        g_own,
        g_other,
        u_own,
        u_other,
        qz,
        kn,
        vt,
        ot,
        outgoing,
        att_mine,
        att_theirs,
        xs,
        d_sems,
        g_sems,
        u_sems,
        v_sems,
        swap_sems,
        att_sems,
        local_sems,
    ) = refs
    step = pl.program_id(0)
    pairs = pl.num_programs(0)
    _, _, side, core = seats()
    rows, columns = g_own.shape[2:]
    first = columns // 256 * 128
    down = Gather(line, d_in, d_own, d_other, d_sems, d_own.shape[2] // 2)
    gate = Gather(line, g_shard, g_own, g_other, g_sems, rows * 3 // 8)
    up = Gather(line, u_shard, u_own, u_other, u_sems, columns=(0, first))
    up_more = Gather(line, u_shard, u_own, u_other, v_sems, columns=(first, columns - first))
    late = pl.ds(tok // 2, tok - tok // 2)
    swap = send(grad_in.at[1 - side, late], grad_received.at[late], swap_sems, 0, to_x_partner())
    depth = xs.shape[1]
    wide = depth // 2
    mine = pl.ds(pl.multiple_of(core * wide, wide), wide)
    others = pl.ds(pl.multiple_of((1 - core) * wide, wide), wide)
    loads = [
        pltpu.make_async_copy(source, place, local_sems.at[number])
        for number, (source, place) in enumerate(
            (
                (inputs.at[side], xs.at[pl.ds(0, tok), :]),
                (x_received, xs.at[pl.ds(tok, tok), :]),
                (o_own, full_ref.at[:, mine]),
                (o_other, full_ref.at[:, others]),
            )
        )
    ]
    save_att = pltpu.make_async_copy(att_theirs, att_other, local_sems.at[4])
    pieces = (received, own)

    def hand_over(number):
        rows = pl.ds(number * PAIR, PAIR)
        return send(
            outgoing.at[rows, :], att_theirs.at[rows, :], att_sems, number, to_core_partner()
        )

    @pl.when(step == 0)
    def _():
        meet(line, ("z", "y", "x", "core"))
        down.along_y().start()
        gate.start_z()
        swap.start()

    @pl.when(step == 2)
    def _():
        down.along_y().wait()
        down.along_x().start()
        down.to_core(0).start()
        gate.wait_z()
        gate.along_y().start()
        up.start_z()
        for load in loads:
            load.start()

    for source in range(2):
        for slot in range(2):
            cols = block_of(source, slot, tok)
            take = slice(slot * tok, (slot + 1) * tok)
            query = pieces[source][0, :, take] * jnp.asarray(HEAD_DIM**-0.5, BF16)
            for head in range(2):
                qz[head, :, cols] = head_rows(query, head)
            kn[cols, :] = pieces[source][1, :, take].T
            vt[:, cols] = pieces[source][2, :, take]
    attend_body(4 * tok, tile_k, qz, kn, vt, ot, lse_ref)
    for slot in range(2):
        take = slice(slot * tok, (slot + 1) * tok)
        theirs = ot[:, block_of(0, slot, tok)]
        mix_received[:, take] = theirs
        for number in range(4):

            @pl.when(step == number)
            def _(number=number, theirs=theirs, take=take):
                outgoing[number * PAIR : (number + 1) * PAIR, take] = theirs

        ours = ot[:, block_of(1, slot, tok)]
        mix_own[:, take] = ours
        for number in range(4):

            @pl.when(step == number)
            def _(number=number, ours=ours, take=take):
                att_mine[number * PAIR : (number + 1) * PAIR, take] = ours

    for number in range(4):

        @pl.when(step == number)
        def _(number=number):
            hand_over(number).start()

    @pl.when(step == pairs - 1)
    def _():
        up.wait_z()
        up.along_y().start()
        up.to_core(0).start()
        up_more.start_z()
        gate.along_y().wait()
        gate.to_core(0).start()
        down.along_x().wait()
        gate.along_x().start()
        down.to_core(1).start()
        up_more.wait_z()
        up_more.along_y().start()
        up_more.to_core(0).start()
        for number in range(4):
            hand_over(number).wait()
        save_att.start()
        for load in loads:
            load.wait()
        for slot in range(2):
            take = slice(slot * tok, (slot + 1) * tok)
            total = dot(att_mine[:, take].T, full_ref[mine, :])
            total = total + dot(att_theirs[:, take].T, full_ref[others, :])
            middle = xs[take, :].astype(F32) + total
            middle_ref[take, :] = middle
            scale = lax.rsqrt(jnp.mean(middle * middle, axis=1, keepdims=True) + epsilon)
            normed_ref[take, :] = (middle * scale * gains_ref[1:2, :]).astype(BF16)
        up.along_y().wait()
        up.to_core(1).start()
        up_more.along_y().wait()
        up_more.to_core(1).start()
        gate.along_x().wait()
        gate.to_core(1).start()
        swap.wait()
        for gather in (down, up, up_more, gate):
            gather.wait_core()
        save_att.wait()


def attend_carry(
    received, own, inputs, x_received, gains, o_own, o_other, grads, g_received, d_own, gate, up, line
):
    _, width, span = own.shape
    tok = span // 2
    length = 2 * span
    pairs = width // PAIR
    rows, down_rows = gate.shape[0], d_own.shape[2]
    depth = grads.shape[2]
    anywhere = pl.BlockSpec(memory_space=pl.ANY)
    triple = pl.BlockSpec((3, PAIR, span), lambda p: (0, p, 0))
    single = pl.BlockSpec((PAIR, span), lambda p: (p, 0))
    whole_gate = jax.ShapeDtypeStruct((line, 2, rows, gate.shape[1] // 2), BF16)
    whole_down = jax.ShapeDtypeStruct((line, 2, down_rows, d_own.shape[3]), BF16)
    area = pairs * 2 * length * length // 2
    return pl.pallas_call(
        functools.partial(attend_carry_kernel, line, tok, min(256, length)),
        grid=(pairs,),
        in_specs=[triple, triple]
        + [anywhere] * 2
        + [whole_block((8, depth))]
        + [anywhere] * 7,
        out_specs=[single, single, pl.BlockSpec((1, 8, length), lambda p: (p, 0, 0))]
        + [
            pl.BlockSpec(shape, lambda p: (0, 0), pipeline_mode=pl.Buffered(1))
            for shape in ((span, depth), (span, depth), (depth, depth))
        ]
        + [anywhere] * 8,
        out_shape=[
            jax.ShapeDtypeStruct((width, span), BF16),
            jax.ShapeDtypeStruct((width, span), BF16),
            jax.ShapeDtypeStruct((pairs, 8, length), F32),
            jax.ShapeDtypeStruct((span, depth), F32),
            jax.ShapeDtypeStruct((span, depth), BF16),
            jax.ShapeDtypeStruct((depth, depth), BF16),
            jax.ShapeDtypeStruct((width, span), BF16),
            jax.ShapeDtypeStruct((tok, depth), BF16),
            whole_down,
            whole_down,
            whole_gate,
            whole_gate,
            whole_gate,
            whole_gate,
        ],
        scratch_shapes=[
            pltpu.VMEM((2, PAIR, length), BF16),
            pltpu.VMEM((length, PAIR), BF16),
            pltpu.VMEM((PAIR, length), BF16),
            pltpu.VMEM((PAIR, length), BF16),
            pltpu.VMEM((width, span), BF16),
            pltpu.VMEM((width, span), BF16),
            pltpu.VMEM((width, span), BF16),
            pltpu.VMEM((span, depth), BF16),
        ]
        + [gather_sems(line)] * 4
        + [
            pltpu.SemaphoreType.DMA((2, 1)),
            pltpu.SemaphoreType.DMA((2, 4)),
            pltpu.SemaphoreType.DMA((5,)),
        ],
        input_output_aliases={8: 7, 9: 8},
        compiler_params=pltpu.CompilerParams(
            dimension_semantics=("arbitrary",),
            vmem_limit_bytes=63 * MIB,
            collective_id=2,
            has_side_effects=True,
        ),
        cost_estimate=pl.CostEstimate(
            flops=area * 1024, bytes_accessed=8 * width * length, transcendentals=area
        ),
        name="attend_carry",
    )(
        received,
        own,
        inputs,
        x_received,
        gains,
        o_own,
        o_other,
        grads,
        g_received,
        d_own,
        gate,
        up,
    )


LATE = 2


def mlp_carry_kernel(line, tok, blocks, *refs):
    (
        grads,
        grads_received,
        middle_ref,
        normed_ref,
        gains_ref,
        g_own,
        g_other,
        u_own,
        u_other,
        d_own_own,
        d_own_other,
        d_other_own,
        d_other_other,
        out_ref,
        send_ref,
        grad_ref,
        low_ref,
        gain_ref,
        gu_ref,
        d_ref,
        gu_y,
        gu_late,
        og,
        normed_t,
        acc,
        back,
        gu_kept,
        d_kept,
        gu_sent,
        d_sent,
        gu_landed,
        d_landed,
        gu_outgoing,
        down_full,
        local_sems,
        gu_sends,
        gu_recvs,
        d_sends,
        d_recvs,
        y_sems,
    ) = refs
    step = pl.program_id(0)
    _, y, side, core = seats()
    depth = og.shape[1]
    wide = depth // 2
    strip = 128
    rows = gu_kept.shape[4]
    mine = pl.ds(pl.multiple_of(core * wide, wide), wide)
    others = pl.ds(pl.multiple_of((1 - core) * wide, wide), wide)

    def core_copies(number):
        slot = lax.rem(number, 2)
        return [
            pltpu.make_async_remote_copy(
                src_ref=source.at[slot],
                dst_ref=target.at[number],
                send_sem=sends.at[slot],
                recv_sem=recvs.at[number],
                device_id=to_core_partner(),
                device_id_type=MESH,
            )
            for source, target, sends, recvs in (
                (gu_sent, gu_landed, gu_sends, gu_recvs),
                (d_sent, d_landed, d_sends, d_recvs),
            )
        ]

    def y_copy(number):
        return send(gu_outgoing.at[number], gu_y.at[number], y_sems, number, to_y_partner())

    def leave(late):
        return pltpu.make_async_copy(
            gu_outgoing.at[blocks - LATE + late], gu_late.at[late], local_sems.at[2 + late]
        )

    @pl.when(step == 0)
    def _():
        meet(line, ("y", "core"))
        loads = [
            pltpu.make_async_copy(grads.at[side], og.at[pl.ds(0, tok), :], local_sems.at[0]),
            pltpu.make_async_copy(grads_received, og.at[pl.ds(tok, tok), :], local_sems.at[1]),
        ]
        for load in loads:
            load.start()
        normed_t[...] = normed_ref[...].T
        acc[...] = jnp.zeros_like(acc)
        back[...] = jnp.zeros_like(back)
        for load in loads:
            load.wait()

    @pl.when(step < blocks)
    def _():
        slot = lax.rem(step, 2)
        gate_w = jnp.concatenate([g_own[...], g_other[...]], axis=1)
        up_w = jnp.concatenate([u_own[...], u_other[...]], axis=1)
        for number, pair in enumerate(
            ((d_own_own, d_own_other), (d_other_own, d_other_other))
        ):
            at = pl.ds(number * strip, strip)
            down_full[at, mine] = pair[0][...]
            down_full[at, others] = pair[1][...]
        down_w = down_full[...]
        both_w = jnp.concatenate([gate_w, up_w], axis=1)
        span = og.shape[0]
        size = span // 4

        def products(at):
            both = dot(normed_ref[at, :], both_w)
            return (both[:, : 2 * strip], both[:, 2 * strip :], nt(og[at, :], down_w))

        def bend(gate, up, grad_active):
            sigma = jax.nn.sigmoid(gate)
            silu = gate * sigma
            turned = grad_active * up * sigma * (1.0 + gate * (1.0 - sigma))
            grad_both = jnp.concatenate([turned.astype(BF16), (grad_active * silu).astype(BF16)], axis=1)
            return ((silu * up).astype(BF16), grad_both)

        def spread(at, active, grad_both):
            acc[at, :] += dot(active, down_w)
            back[at, :] += nt(grad_both, both_w)

        pieces = [slice(n * size, (n + 1) * size) for n in range(4)]
        bent = []
        ahead = products(pieces[0])
        for number, at in enumerate(pieces):
            now = ahead
            if number + 1 < len(pieces):
                ahead = products(pieces[number + 1])
            bent.append(bend(*now))
            if number:
                spread(pieces[number - 1], *bent[number - 1])
        spread(pieces[-1], *bent[-1])
        active = jnp.concatenate([one for one, _ in bent], axis=0)
        grad_both = jnp.concatenate([one for _, one in bent], axis=0)

        @pl.when(step >= 2)
        def _():
            for copy in core_copies(step - 2):
                copy.wait_send()

        shaped = dot(normed_t[...], grad_both).astype(BF16).reshape(line, 2, rows, 4 * strip)
        for number in range(2):
            base = 2 * number * strip
            gu_kept[slot, number] = shaped[..., base : base + strip]
            gu_sent[slot, number] = shaped[..., base + strip : base + 2 * strip]
        active_t = active.T
        kept = dot(active_t, og[:, mine]).astype(BF16)
        d_kept[slot, core] = kept[:strip]
        d_kept[slot, 1 - core] = kept[strip:]
        sent = dot(active_t, og[:, others]).astype(BF16)
        d_sent[slot, core] = sent[:strip]
        d_sent[slot, 1 - core] = sent[strip:]
        for copy in core_copies(step):
            copy.start()

    @pl.when(step > 0)
    def _():
        number = step - 1
        slot = lax.rem(number, 2)
        for copy in core_copies(number):
            copy.wait_recv()
        for which in range(2):
            theirs = gu_kept[slot, which, :, 1 - y].astype(F32)
            theirs = theirs + gu_landed[number, which, :, 1 - y].astype(F32)
            gu_outgoing[number, which] = theirs.astype(BF16)
            ours = gu_kept[slot, which, :, y].astype(F32)
            ours = ours + gu_landed[number, which, :, y].astype(F32)
            gu_ref[0, which] = ours.astype(BF16)
        @pl.when(number < blocks - LATE)
        def _():
            y_copy(number).start()

        for late in range(LATE):

            @pl.when(number == blocks - LATE + late)
            def _(late=late):
                leave(late).start()

        d_ref[...] = (d_kept[slot].astype(F32) + d_landed[number].astype(F32)).astype(BF16)

    @pl.when(step == blocks)
    def _():
        gain = gains_ref[1:2, :]
        chunk = min(128, tok)
        gain_ref[...] = jnp.zeros_like(gain_ref)
        for slot in range(2):

            def finish(number, _, slot=slot):
                local = pl.ds(pl.multiple_of(number * chunk, chunk), chunk)
                some = pl.ds(pl.multiple_of(slot * tok + number * chunk, chunk), chunk)
                middle = middle_ref[some, :]
                scale = lax.rsqrt(jnp.mean(middle * middle, axis=1, keepdims=True) + epsilon)
                result = middle + acc[some, :]
                if slot == 0:
                    out_ref[0, local, :] = result
                else:
                    send_ref[local, :] = result.astype(BF16)
                grad = back[some, :]
                gain_ref[0:1, :] += jnp.sum(grad * middle * scale, axis=0, keepdims=True)
                weighted = grad * gain
                inner = jnp.mean(weighted * middle, axis=1, keepdims=True)
                grad_middle = (
                    scale * weighted
                    - middle * (scale * scale * scale) * inner
                    + og[some, :].astype(F32)
                )
                grad_ref[some, :] = grad_middle
                low_ref[some, :] = grad_middle.astype(BF16)
                return 0

            lax.fori_loop(0, tok // chunk, finish, 0)
        for number in (blocks - 2, blocks - 1):
            for copy in core_copies(number):
                copy.wait_send()
        for late in range(LATE):
            leave(late).wait()
        for number in range(blocks - LATE):
            y_copy(number).wait()


def mlp_carry(grads, grads_received, middle, normed, gains, gate, up, down, line):
    slots, tok, depth = grads.shape
    half_width = gate[0].shape[1]
    wide = depth // 2
    span = slots * tok
    blocks = half_width // 128
    rows = depth // (2 * line)
    once = pl.Buffered(1)
    anywhere = pl.BlockSpec(memory_space=pl.ANY)

    def now(s):
        return jnp.minimum(s, blocks - 1)

    def done(s):
        return jnp.maximum(s - 1, 0)

    def core():
        return lax.axis_index("seq") % 2

    column = pl.BlockSpec((depth, 128), lambda s: (0, now(s)))
    own_rows = pl.BlockSpec((128, wide), lambda s: (core() * blocks + now(s), 0))
    other_rows = pl.BlockSpec((128, wide), lambda s: ((1 - core()) * blocks + now(s), 0))
    full = pl.BlockSpec((span, depth), lambda s: (0, 0), pipeline_mode=once)
    return pl.pallas_call(
        functools.partial(mlp_carry_kernel, line, tok, blocks),
        grid=(blocks + 1,),
        in_specs=[anywhere, anywhere, full, full, whole_block((8, depth))]
        + [column] * 4
        + [own_rows, own_rows, other_rows, other_rows],
        out_specs=[
            pl.BlockSpec(
                (1, tok, depth), lambda s: (lax.axis_index("seq") // 2, 0, 0), pipeline_mode=once
            ),
            pl.BlockSpec((tok, depth), lambda s: (0, 0), pipeline_mode=once),
            full,
            full,
            whole_block((8, depth)),
            pl.BlockSpec((1, 2, line, rows, 128), lambda s: (done(s), 0, 0, 0, 0)),
            pl.BlockSpec((2, 128, wide), lambda s: (0, done(s), 0)),
            anywhere,
            anywhere,
        ],
        out_shape=[
            jax.ShapeDtypeStruct((slots, tok, depth), F32),
            jax.ShapeDtypeStruct((tok, depth), BF16),
            jax.ShapeDtypeStruct((span, depth), F32),
            jax.ShapeDtypeStruct((span, depth), BF16),
            jax.ShapeDtypeStruct((8, depth), F32),
            jax.ShapeDtypeStruct((blocks, 2, line, rows, 128), BF16),
            jax.ShapeDtypeStruct((2, half_width, wide), BF16),
            jax.ShapeDtypeStruct((blocks - LATE, 2, line, rows, 128), BF16),
            jax.ShapeDtypeStruct((LATE, 2, line, rows, 128), BF16),
        ],
        scratch_shapes=[
            pltpu.VMEM((span, depth), BF16),
            pltpu.VMEM((depth, span), BF16),
            pltpu.VMEM((span, depth), F32),
            pltpu.VMEM((span, depth), F32),
            pltpu.VMEM((2, 2, line, 2, rows, 128), BF16),
            pltpu.VMEM((2, 2, 128, wide), BF16),
            pltpu.VMEM((2, 2, line, 2, rows, 128), BF16),
            pltpu.VMEM((2, 2, 128, wide), BF16),
            pltpu.VMEM((blocks, 2, line, 2, rows, 128), BF16),
            pltpu.VMEM((blocks, 2, 128, wide), BF16),
            pltpu.VMEM((blocks, 2, line, rows, 128), BF16),
            pltpu.VMEM((256, depth), BF16),
            pltpu.SemaphoreType.DMA((2 + LATE,)),
            pltpu.SemaphoreType.DMA((2,)),
            pltpu.SemaphoreType.DMA((blocks,)),
            pltpu.SemaphoreType.DMA((2,)),
            pltpu.SemaphoreType.DMA((blocks,)),
            pltpu.SemaphoreType.DMA((2, blocks - LATE)),
        ],
        compiler_params=pltpu.CompilerParams(
            dimension_semantics=("arbitrary",),
            vmem_limit_bytes=63 * MIB,
            collective_id=3,
            has_side_effects=True,
        ),
        cost_estimate=pl.CostEstimate(
            flops=16 * span * depth * 2 * half_width,
            bytes_accessed=24 * depth * half_width + 20 * span * depth,
            transcendentals=2 * span * half_width,
        ),
        name="mlp_carry",
    )(
        grads,
        grads_received,
        middle,
        normed,
        gains,
        *gate,
        *up,
        down[0],
        down[1],
        down[0],
        down[1],
    )


def early_rows(rows):
    return pl.ds(0, rows // 8)


def late_rows(rows):
    return pl.ds(rows // 8, rows - rows // 8)


def grad_attended_carry_kernel(
    line,
    low_ref,
    full_ref,
    att_other,
    att_own,
    outputs_sent,
    ga_own,
    ga_received,
    o_ref,
    o_landed,
    outputs_received,
    outgoing,
    o_sent,
    sems,
):
    step = pl.program_id(0)
    _, _, _, core = seats()
    wide = att_own.shape[0]
    mine = pl.ds(pl.multiple_of(core * wide, wide), wide)
    others = pl.ds(pl.multiple_of((1 - core) * wide, wide), wide)
    heads = send(outgoing, ga_received, sems, 0, to_core_partner())
    early = early_rows(outputs_sent.shape[0])
    swap = send(
        outputs_sent.at[early], outputs_received.at[early], sems, 3, to_x_partner()
    )

    def sums(number):
        half = 1 - core if number == 0 else core
        at = pl.ds(pl.multiple_of(half * wide, wide), wide)
        return send(o_sent.at[number], o_landed.at[at, :], sems, 1 + number, to_core_partner())

    @pl.when(step == 0)
    def _():
        meet(line, ("x", "core"))
        swap.start()
        outgoing[...] = nt(full_ref[...], low_ref[...]).astype(BF16)
        heads.start()

    @pl.when(step == 1)
    def _():
        ga_own[...] = nt(full_ref[...], low_ref[...]).astype(BF16)

    for number, att in enumerate((att_other, att_own)):

        @pl.when(step == number)
        def _(number=number, att=att):
            o_sent[number] = dot(att[...], low_ref[:, others]).astype(BF16)
            sums(number).start()
            o_ref[...] = dot(att[...], low_ref[:, mine]).astype(BF16)

    @pl.when(step == 1)
    def _():
        swap.wait()
        heads.wait()
        for number in range(2):
            sums(number).wait()


def grad_attended_carry(low, full, att_other, att_own, outputs_sent, line):
    span, depth = low.shape
    wide = depth // 2

    def half(s):
        core = lax.axis_index("seq") % 2
        return jnp.where(s == 0, 1 - core, core)

    anywhere = pl.BlockSpec(memory_space=pl.ANY)
    return pl.pallas_call(
        functools.partial(grad_attended_carry_kernel, line),
        grid=(2,),
        in_specs=[
            whole_block((span, depth)),
            pl.BlockSpec((wide, depth), lambda s: (half(s), 0)),
            whole_block((wide, span)),
            whole_block((wide, span)),
            anywhere,
        ],
        out_specs=[
            whole_block((wide, span)),
            anywhere,
            pl.BlockSpec((wide, wide), lambda s: (half(s), 0)),
            anywhere,
            anywhere,
        ],
        out_shape=[
            jax.ShapeDtypeStruct((wide, span), BF16),
            jax.ShapeDtypeStruct((wide, span), BF16),
            jax.ShapeDtypeStruct((depth, wide), BF16),
            jax.ShapeDtypeStruct((depth, wide), BF16),
            jax.ShapeDtypeStruct(outputs_sent.shape, BF16),
        ],
        scratch_shapes=[
            pltpu.VMEM((wide, span), BF16),
            pltpu.VMEM((2, wide, wide), BF16),
            pltpu.SemaphoreType.DMA((2, 4)),
        ],
        compiler_params=pltpu.CompilerParams(
            dimension_semantics=("arbitrary",),
            vmem_limit_bytes=48 * MIB,
            collective_id=4,
            has_side_effects=True,
        ),
        cost_estimate=pl.CostEstimate(
            flops=4 * span * depth * depth,
            bytes_accessed=6 * span * depth + 4 * depth * depth,
            transcendentals=0,
        ),
        name="grad_attended_carry",
    )(low, full, att_other, att_own, outputs_sent)


def attend_back_carry_kernel(line, tok, tile_q, tile_k, *refs):
    (
        received,
        own,
        mix_received,
        mix_own,
        grad_received,
        grad_own,
        lse_ref,
        cos_ref,
        sin_ref,
        outputs_sent,
        _,
        gu_in,
        gu_y,
        gu_late,
        d_in,
        o_in,
        o_landed,
        back_own,
        back_other,
        outputs_received,
        gu_mine,
        gu_z,
        d_kept,
        d_y,
        o_kept,
        o_y,
        first_received,
    ) = refs[:27]
    (
        qz,
        gz,
        qn,
        gn,
        kn,
        vn,
        kt,
        inner,
        dq,
        dk,
        dv,
        outgoing,
        gu_a,
        gu_b,
        o_a,
        o_b,
        o_x,
        d_a,
        d_x,
        first_out,
        local_sems,
        back_sems,
        z_sems,
        other_sems,
        first_sems,
    ) = refs[27:]
    step = pl.program_id(0)
    pairs = pl.num_programs(0)
    z, y, x, core = seats()
    wide = d_a.shape[3]
    late_part = late_rows(tok)
    length = 4 * tok
    blocks = gu_a.shape[0]
    o_half, d_half = o_x.shape[2], d_x.shape[2]
    o_mine = pl.ds(pl.multiple_of(x * o_half, o_half), o_half)
    o_theirs = pl.ds(pl.multiple_of((1 - x) * o_half, o_half), o_half)
    d_mine = pl.ds(pl.multiple_of(x * d_half, d_half), d_half)
    d_theirs = pl.ds(pl.multiple_of((1 - x) * d_half, d_half), d_half)
    swap = send(
        outputs_sent.at[late_part],
        outputs_received.at[late_part],
        other_sems,
        0,
        to_x_partner(),
    )
    o_over = send(o_a.at[:, :, o_theirs, :], o_x, other_sems, 1, to_x_partner())
    d_over = send(d_in.at[:, :, d_theirs, :], d_x, other_sems, 2, to_x_partner())
    o_send = send(o_a.at[:, 1 - y, o_mine, :], o_y, other_sems, 3, to_y_partner())
    d_send = send(d_a.at[:, 1 - y], d_y, other_sems, 4, to_y_partner())
    late = pl.ds(blocks - LATE, LATE)
    late_send = send(gu_late, gu_b.at[late], other_sems, 5, to_y_partner())

    def z_send(jump, number):
        target = lax.rem(z + jump, line)
        at = late if number else pl.ds(0, blocks - LATE)
        return send(
            gu_a.at[at, :, target],
            gu_z.at[jump - 1, at],
            z_sems,
            number * (line - 1) + jump - 1,
            to_z_partner(line, jump),
        )

    def add(number, _):
        total = gu_a[number].astype(F32) + gu_b[number].astype(F32)
        gu_a[number] = total.astype(BF16)
        return 0

    gu_stays = pltpu.make_async_copy(gu_a.at[:, :, z], gu_mine, local_sems.at[5])
    o_stays = pltpu.make_async_copy(o_a.at[:, y, o_mine, :], o_kept, local_sems.at[6])
    d_stays = pltpu.make_async_copy(d_a.at[:, y], d_kept, local_sems.at[7])
    load_d = pltpu.make_async_copy(d_in.at[:, :, d_mine, :], d_a, local_sems.at[4])

    def first_send(source):
        columns = pl.ds(pl.multiple_of(core * wide, wide), PAIR)
        partner = to_x_partner() if source else {"seq": 3 - lax.axis_index("seq")}
        return send(
            first_out.at[source], first_received.at[:, columns], first_sems, source, partner
        )

    def hand_over(number):
        rows = pl.ds(number * PAIR, PAIR)
        return send(
            outgoing.at[:, rows, :],
            back_other.at[:, rows, :],
            back_sems,
            number,
            to_core_partner(),
        )

    @pl.when(step == 0)
    def _():
        meet(line, ("z", "y", "x", "core", "diagonal"))
        late_send.start()
        loads = [
            pltpu.make_async_copy(source, target, local_sems.at[number])
            for number, (source, target) in enumerate(
                (
                    (o_in, o_a),
                    (o_landed, o_b),
                    (gu_in, gu_a),
                    (gu_y, gu_b.at[pl.ds(0, blocks - LATE)]),
                )
            )
        ]
        for load in loads:
            load.start()
        load_d.start()
        loads[0].wait()
        loads[1].wait()
        o_a[...] = (o_a[...].astype(F32) + o_b[...].astype(F32)).astype(BF16)
        o_over.start()
        d_over.start()
        loads[2].wait()
        loads[3].wait()
        lax.fori_loop(0, blocks - LATE, add, 0)
        for jump in range(1, line):
            z_send(jump, 0).start()

    @pl.when(step == 1)
    def _():
        late_send.wait()
        lax.fori_loop(blocks - LATE, blocks, add, 0)
        for jump in range(1, line):
            z_send(jump, 1).start()
        gu_stays.start()
        o_over.wait()
        summed = o_a[:, :, o_mine, :].astype(F32) + o_x[...].astype(F32)
        o_a[:, :, o_mine, :] = summed.astype(BF16)
        o_send.start()
        o_stays.start()

    @pl.when(step == 2)
    def _():
        swap.start()

    @pl.when(step == 3)
    def _():
        load_d.wait()
        d_over.wait()
        for at in range(line):
            d_a[at] = (d_a[at].astype(F32) + d_x[at].astype(F32)).astype(BF16)
        d_send.start()
        d_stays.start()

    attend_back_body(
        (received, own),
        (mix_received, mix_own),
        (grad_received, grad_own),
        lambda source, slot: block_of(source, slot, tok),
        tok,
        length,
        tile_q,
        tile_k,
        lse_ref,
        qz,
        gz,
        qn,
        gn,
        kn,
        vn,
        kt,
        inner,
        dq,
        dk,
        dv,
    )
    for slot in range(2):
        take = slice(slot * tok, (slot + 1) * tok)
        for source in range(2):
            cols = block_of(source, slot, tok)
            results = turn_back(dq, dk, dv, cols, cos_ref[:, cols], sin_ref[:, cols])
            for which, result in enumerate(results):
                if source == 1:
                    back_own[which, :, take] = result
                else:
                    at = pl.ds(pl.multiple_of(step * PAIR, PAIR), PAIR)
                    outgoing[which, at, take] = result

    @pl.when(step == 0)
    def _():
        for source in range(2):
            rows = dv[block_of(source, 1, tok), :]
            first_out[source] = (0.5 * rows).astype(BF16)
            first_send(source).start()

    for number in range(4):

        @pl.when(step == number)
        def _(number=number):
            hand_over(number).start()

    @pl.when(step == pairs - 1)
    def _():
        swap.wait()
        for source in range(2):
            first_send(source).wait()
        d_send.wait()
        o_send.wait()
        for copy in (gu_stays, o_stays, d_stays):
            copy.wait()
        for number in range(2):
            for jump in range(1, line):
                z_send(jump, number).wait()
        for number in range(4):
            hand_over(number).wait()


def attend_back_carry(
    pieces,
    mixes,
    grads,
    lse,
    cosine,
    sine,
    outputs_sent,
    outputs_received,
    gu,
    gu_y,
    gu_late,
    d,
    o,
    o_landed,
    line,
):
    _, width, span = pieces[0].shape
    tok = span // 2
    length = 2 * span
    pairs = width // PAIR
    tile_q = min(1024, length)
    tile_k = min(256, length)
    anywhere = pl.BlockSpec(memory_space=pl.ANY)
    triple = pl.BlockSpec((3, PAIR, span), lambda p: (0, p, 0))
    single = pl.BlockSpec((PAIR, span), lambda p: (p, 0))
    table = pl.BlockSpec((HALF, length), lambda p: (0, 0))
    blocks, _, _, rows, _ = gu.shape
    down_rows, wide = d.shape[2:]
    area = pairs * 2 * length * length // 2
    return pl.pallas_call(
        functools.partial(attend_back_carry_kernel, line, tok, tile_q, tile_k),
        grid=(pairs,),
        in_specs=[triple] * 2
        + [single] * 4
        + [pl.BlockSpec((1, 8, length), lambda p: (p, 0, 0)), table, table]
        + [anywhere] * 8,
        out_specs=[triple] + [anywhere] * 9,
        out_shape=[
            jax.ShapeDtypeStruct((3, width, span), BF16),
            jax.ShapeDtypeStruct((3, width, span), BF16),
            jax.ShapeDtypeStruct(outputs_sent.shape, BF16),
            jax.ShapeDtypeStruct((blocks, 2, rows, 128), BF16),
            jax.ShapeDtypeStruct((line - 1, blocks, 2, rows, 128), BF16),
            jax.ShapeDtypeStruct((line, down_rows // 2, wide), BF16),
            jax.ShapeDtypeStruct((line, down_rows // 2, wide), BF16),
            jax.ShapeDtypeStruct((line, rows // 2, wide), BF16),
            jax.ShapeDtypeStruct((line, rows // 2, wide), BF16),
            jax.ShapeDtypeStruct(outputs_sent.shape, BF16),
        ],
        input_output_aliases={10: 2},
        scratch_shapes=[
            pltpu.VMEM((2, PAIR, length), BF16),
            pltpu.VMEM((2, PAIR, length), BF16),
            pltpu.VMEM((2, length, PAIR), BF16),
            pltpu.VMEM((2, length, PAIR), BF16),
            pltpu.VMEM((length, PAIR), BF16),
            pltpu.VMEM((length, PAIR), BF16),
            pltpu.VMEM((PAIR, length), BF16),
            pltpu.VMEM((8, length), F32),
            pltpu.VMEM((PAIR, length), F32),
            pltpu.VMEM((length, PAIR), F32),
            pltpu.VMEM((length, PAIR), F32),
            pltpu.VMEM((3, width, span), BF16),
            pltpu.VMEM((blocks, 2, line, rows, 128), BF16),
            pltpu.VMEM((blocks, 2, line, rows, 128), BF16),
            pltpu.VMEM((line, 2, rows, wide), BF16),
            pltpu.VMEM((line, 2, rows, wide), BF16),
            pltpu.VMEM((line, 2, rows // 2, wide), BF16),
            pltpu.VMEM((line, 2, down_rows // 2, wide), BF16),
            pltpu.VMEM((line, 2, down_rows // 2, wide), BF16),
            pltpu.VMEM((2, tok, PAIR), BF16),
            pltpu.SemaphoreType.DMA((8,)),
            pltpu.SemaphoreType.DMA((2, 4)),
            pltpu.SemaphoreType.DMA((2, 2 * (line - 1))),
            pltpu.SemaphoreType.DMA((2, 6)),
            pltpu.SemaphoreType.DMA((2, 2)),
        ],
        compiler_params=pltpu.CompilerParams(
            dimension_semantics=("arbitrary",),
            vmem_limit_bytes=60 * MIB,
            collective_id=5,
            has_side_effects=True,
        ),
        cost_estimate=pl.CostEstimate(
            flops=area * 2560, bytes_accessed=16 * width * length, transcendentals=area
        ),
        name="attend_back_carry",
    )(
        *pieces,
        *mixes,
        *grads,
        lse,
        cosine,
        sine,
        outputs_sent,
        outputs_received,
        gu,
        gu_y,
        gu_late,
        d,
        o,
        o_landed,
    )


def tail_carry_kernel(line, tok, blocks, *refs):
    (
        inputs,
        x_received,
        back_other,
        back_own,
        full_ref,
        normed_ref,
        grad_in,
        gains_ref,
        mlp_gain_ref,
        gu_mine,
        gu_z,
        d_in,
        d_y,
        o_in,
        o_y,
        _,
        input_grad,
        input_landed,
        first_grad,
        first_landed,
        gain_out,
        q_out,
        k_out,
        v_out,
        o_out,
        g_out,
        u_out,
        d_out,
        xs,
        grad_middle,
        normed_t,
        acc,
        grad,
        sent,
        landed,
        y_landed,
        z_landed,
        d_a,
        d_b,
        d_landed,
        o_a,
        o_b,
        o_landed,
        gu_a,
        gu_b,
        gu_x,
        gu_c,
        d_low,
        d_c,
        s_low,
        s_x,
        s_c,
        first_stage,
        first_send,
        input_send,
        gain,
        gain_landed,
        local_sems,
        core_sems,
        y_sems,
        z_sems,
        dz_sems,
        oz_sems,
        x_sems,
        c_sems,
        token_sems,
        gain_sems,
    ) = refs
    step = pl.program_id(0)
    target = jnp.where(step < 6, lax.rem(step, 2), 2)
    turn = lax.rem(step // 2, 3)
    z, y, x, core = seats()
    side = x
    wide, span = grad.shape
    depth = 2 * wide
    half = jnp.where(target == 0, 1 - core, core)
    columns = pl.ds(pl.multiple_of(half * wide, wide), wide)
    mine = pl.ds(pl.multiple_of(core * wide, wide), wide)
    others = pl.ds(pl.multiple_of((1 - core) * wide, wide), wide)

    def load(source, place, number):
        return pltpu.make_async_copy(source, place, local_sems.at[number])

    load_tokens = [
        load(inputs.at[side], xs.at[pl.ds(0, tok), :], 0),
        load(x_received, xs.at[pl.ds(tok, tok), :], 1),
        load(grad_in, grad_middle, 2),
    ]
    store_input = load(acc.at[pl.ds(0, tok), :], input_grad, 3)
    store_first = load(first_stage, first_grad, 4)

    def along_z(source, place, sems, base=0):
        return [
            send(
                source(lax.rem(z + jump, line)),
                place(jump - 1),
                sems,
                base + jump - 1,
                to_z_partner(line, jump),
            )
            for jump in range(1, line)
        ]

    d_sends = along_z(lambda at: d_a.at[at], lambda jump: d_landed.at[jump], dz_sems)
    o_sends = along_z(lambda at: o_a.at[at], lambda jump: o_landed.at[jump], oz_sems)

    def core_send(number):
        return send(sent.at[number], landed.at[number], core_sems, number, to_core_partner())

    def y_send(number):
        return send(
            landed.at[number, :, 1 - y], y_landed.at[number], y_sems, number, to_y_partner()
        )

    def z_sends(number):
        return along_z(
            lambda at: landed.at[number, at, y],
            lambda jump: z_landed.at[number, jump],
            z_sems,
            number * (line - 1),
        )

    def first_part(number):
        which = 1 - core if number == 0 else core
        at = pl.ds(pl.multiple_of(which * wide + PAIR, PAIR), wide - PAIR)
        return send(
            first_send.at[:, at], first_landed.at[:, at], token_sems, number, to_x_partner()
        )

    def input_part(number):
        at = pl.ds(number * (tok // 2), tok // 2)
        return send(
            input_send.at[at], input_landed.at[at], token_sems, 2 + number, to_x_partner()
        )

    gu_sides = (
        send(gu_a, gu_x, x_sems, 0, to_x_partner()),
        send(gu_a, gu_c, c_sems, 0, to_core_partner()),
    )
    d_half, o_half = d_a.shape[1], o_a.shape[1]
    d_mine = pl.ds(pl.multiple_of(x * d_half, d_half), d_half)
    d_theirs = pl.ds(pl.multiple_of((1 - x) * d_half, d_half), d_half)
    o_mine = pl.ds(pl.multiple_of(x * o_half, o_half), o_half)
    o_theirs = pl.ds(pl.multiple_of((1 - x) * o_half, o_half), o_half)
    d_sides = (
        send(d_low.at[d_mine, :], d_low.at[d_mine, :], x_sems, 1, to_x_partner()),
        send(d_low, d_c, c_sems, 1, to_core_partner()),
    )
    o_side = send(s_low.at[0, o_mine, :], s_low.at[0, o_mine, :], x_sems, 2, to_x_partner())

    def square_x(number):
        return send(s_low.at[number], s_x.at[number], x_sems, 2 + number, to_x_partner())

    def square_core(number):
        return send(s_low.at[number], s_c.at[number], c_sems, 2 + number, to_core_partner())

    squares = (o_out, v_out, q_out, k_out)

    def gain_send(number, partner):
        return send(gain.at[number], gain_landed.at[number], gain_sems, number, partner)

    @pl.when(step == 0)
    def _():
        meet(line, ("z", "y", "x", "core"))
        sources = ((d_in, d_a), (d_y, d_b), (o_in, o_a), (o_y, o_b), (gu_mine, gu_a), (gu_z, gu_b))
        loads = [load(source, place, 7 + n) for n, (source, place) in enumerate(sources)]
        for copy in loads:
            copy.start()
        for copy in load_tokens:
            copy.start()
        for copy in loads[:4]:
            copy.wait()
        for at in range(line):
            d_a[at] = (d_a[at].astype(F32) + d_b[at].astype(F32)).astype(BF16)
            o_a[at] = (o_a[at].astype(F32) + o_b[at].astype(F32)).astype(BF16)
        for copy in d_sends + o_sends:
            copy.start()
        for copy in loads[4:]:
            copy.wait()

        def total(number, _):
            for which, out in enumerate((g_out, u_out)):
                value = gu_a[number, which].astype(F32)
                for jump in range(line - 1):
                    value = value + gu_b[jump, number, which].astype(F32)
                at = pl.ds(pl.multiple_of((core * blocks + number) * 128, 128), 128)
                out[:, at] = value
                gu_a[number, which] = value.astype(BF16)
            return 0

        lax.fori_loop(0, blocks, total, 0)
        gu_sides[0].start()
        normed_t[...] = normed_ref[...].T
        acc[...] = jnp.zeros_like(acc)

    def own_part(back):
        @pl.when(turn == 0)
        def _():
            value = 0.5 * back[0].astype(F32)
            rows = value.T
            first_stage[:, columns] = rows[:tok]
            first_send[:, columns] = rows[tok:].astype(BF16)
            grad[...] = value.astype(BF16)

        @pl.when(turn > 0)
        def _():
            grad[...] = back[0]

    @pl.when(target == 0)
    def _():
        own_part(back_other)

    @pl.when(target == 1)
    def _():
        own_part(back_own)

    @pl.when(step == 0)
    def _():
        first_part(0).start()

    @pl.when(step == 1)
    def _():
        first_part(1).start()
        store_first.start()

    @pl.when(target < 2)
    def _():
        value = grad[...]
        result = nt(normed_t[...], value)

        @pl.when(target == 0)
        def _():
            sent[turn] = result.astype(BF16).reshape(sent.shape[1:])
            core_send(turn).start()

        @pl.when(target == 1)
        def _():
            core_send(turn).wait()
            theirs = landed[turn].reshape(result.shape).astype(F32)
            landed[turn] = (result + theirs).astype(BF16).reshape(landed.shape[1:])
            y_send(turn).start()

        acc[...] += nt(value.T, full_ref[0, 0])

    @pl.when(step == 6)
    def _():
        for copy in load_tokens:
            copy.wait()
        weight = gains_ref[0:1, :]
        chunk = min(128, tok)
        gain[...] = jnp.zeros_like(gain)
        gain[0, 1:2, :] = mlp_gain_ref[0:1, :]
        for slot in (1, 0):

            def finish(number, _, slot=slot):
                local = pl.ds(pl.multiple_of(number * chunk, chunk), chunk)
                some = pl.ds(pl.multiple_of(slot * tok + number * chunk, chunk), chunk)
                values = xs[some, :].astype(F32)
                scale = lax.rsqrt(jnp.mean(values * values, axis=1, keepdims=True) + epsilon)
                value = acc[some, :]
                gain[0, 0:1, :] += jnp.sum(value * values * scale, axis=0, keepdims=True)
                weighted = value * weight
                inner = jnp.mean(weighted * values, axis=1, keepdims=True)
                result = (
                    scale * weighted
                    - values * (scale * scale * scale) * inner
                    + grad_middle[some, :]
                )
                if slot == 0:
                    acc[some, :] = result
                else:
                    input_send[local, :] = result.astype(BF16)
                return 0

            for number in range(2):
                turns = tok // chunk // 2
                lax.fori_loop(number * turns, (number + 1) * turns, finish, 0)
                if slot == 1:
                    input_part(number).start()
        gain_send(0, to_core_partner()).start()
        store_input.start()
        gu_sides[0].wait()

        def gather_x(number, _):
            for which, out in enumerate((g_out, u_out)):
                at = pl.ds(pl.multiple_of((core * blocks + number) * 128, 128), 128)
                value = out[:, at] + gu_x[number, which].astype(F32)
                out[:, at] = value
                gu_a[number, which] = value.astype(BF16)
            return 0

        lax.fori_loop(0, blocks, gather_x, 0)
        gu_sides[1].start()
        gain_send(0, to_core_partner()).wait()
        gain[1] = gain[0] + gain_landed[0]
        gain_send(1, to_y_partner()).start()
        for number in range(3):
            y_send(number).wait()

            def add(at, _, number=number):
                value = landed[number, at, y].astype(F32) + y_landed[number, at].astype(F32)
                landed[number, at, y] = value.astype(BF16)
                return 0

            lax.fori_loop(0, line, add, 0)
            for copy in z_sends(number):
                copy.start()
            if number == 0:
                gain_send(1, to_y_partner()).wait()
                gain[2] = gain[1] + gain_landed[1]
                for jump in range(1, line):
                    gain_z(jump, line, gain, gain_landed, gain_sems).start()
        for copy in d_sends + o_sends:
            copy.wait()

        def sum_z(own, places):
            value = own.astype(F32)
            for place in places:
                value = value + place.astype(F32)
            return value

        value = sum_z(d_a[z], [d_landed[jump] for jump in range(line - 1)])
        d_out[d_mine, mine] = value
        d_low[d_mine, :] = value.astype(BF16)
        d_sides[0].start()
        value = sum_z(o_a[z], [o_landed[jump] for jump in range(line - 1)])
        o_out[o_mine, mine] = value
        s_low[0, o_mine, :] = value.astype(BF16)
        o_side.start()
        for jump in range(1, line):
            gain_z(jump, line, gain, gain_landed, gain_sems).wait()
        value = gain[2]
        for jump in range(1, line):
            value = value + gain_landed[1 + jump]
        gain[3] = value
        last_gain = send(gain.at[3], gain_landed.at[line + 1], gain_sems, line + 1, to_x_partner())
        last_gain.start()
        for number in range(3):
            for copy in z_sends(number):
                copy.wait()
            value = sum_z(
                landed[number, z, y], [z_landed[number, jump] for jump in range(line - 1)]
            )
            squares[1 + number][:, mine] = value
            s_low[1 + number] = value.astype(BF16)
            square_x(1 + number).start()
        last_gain.wait()
        gain[4] = gain[3] + gain_landed[line + 1]
        gain_out[...] = gain[4, :, pl.ds(pl.multiple_of((2 * z + y) * 128, 128), 128)]
        store_first.wait()
        for number in range(2):
            first_part(number).wait()
        d_sides[0].wait()
        d_out[d_theirs, mine] = d_low[d_theirs, :].astype(F32)
        d_sides[1].start()
        o_side.wait()
        o_out[o_theirs, mine] = s_low[0, o_theirs, :].astype(F32)
        square_core(0).start()
        for number in range(2):
            input_part(number).wait()
        for number in range(1, 4):
            square_x(number).wait()
            value = squares[number][:, mine] + s_x[number].astype(F32)
            squares[number][:, mine] = value
            s_low[number] = value.astype(BF16)
            square_core(number).start()
        gu_sides[1].wait()

        def gather_core(number, _):
            for which, out in enumerate((g_out, u_out)):
                at = pl.ds(pl.multiple_of(((1 - core) * blocks + number) * 128, 128), 128)
                out[:, at] = gu_c[number, which].astype(F32)
            return 0

        lax.fori_loop(0, blocks, gather_core, 0)
        d_sides[1].wait()
        d_out[:, others] = d_c[...].astype(F32)
        for number in range(4):
            square_core(number).wait()
            squares[number][:, others] = s_c[number].astype(F32)
        store_input.wait()


def gain_z(jump, line, gain, gain_landed, gain_sems):
    return send(
        gain.at[2], gain_landed.at[1 + jump], gain_sems, 1 + jump, to_z_partner(line, jump)
    )


def tail_carry(
    inputs,
    x_received,
    back_other,
    back_own,
    full,
    normed,
    grad_middle,
    gains,
    mlp_gain,
    gu_mine,
    gu_z,
    d,
    d_y,
    o,
    o_y,
    first_received,
    line,
):
    slots, tok, depth = inputs.shape
    span = slots * tok
    wide = depth // 2
    blocks, _, rows, _ = gu_mine.shape
    down_rows = 2 * d.shape[1]
    once = pl.Buffered(1)
    anywhere = pl.BlockSpec(memory_space=pl.ANY)

    def half(s):
        core = lax.axis_index("seq") % 2
        return jnp.where(s % 2 == 0, 1 - core, core)

    def kind(s):
        return (jnp.minimum(s // 2, 2) + 2) % 3

    def clear(shape):
        zeros = (0,) * len(shape)
        return pl.BlockSpec(shape, lambda s: zeros, pipeline_mode=once)

    square = jax.ShapeDtypeStruct((rows, depth), F32)
    broad = jax.ShapeDtypeStruct((rows, 2 * blocks * 128), F32)
    tall = jax.ShapeDtypeStruct((down_rows, depth), F32)
    tokens = [jax.ShapeDtypeStruct((tok, depth), dtype) for dtype in (F32, BF16)] * 2
    finals = [square] * 4 + [broad] * 2 + [tall]
    vmem = pltpu.VMEM
    dma = pltpu.SemaphoreType.DMA
    return pl.pallas_call(
        functools.partial(tail_carry_kernel, line, tok, blocks),
        grid=(7,),
        in_specs=[
            anywhere,
            anywhere,
            pl.BlockSpec((1, wide, span), lambda s: (kind(s), 0, 0)),
            pl.BlockSpec((1, wide, span), lambda s: (kind(s), 0, 0)),
            pl.BlockSpec(
                (1, 1, depth, wide),
                lambda s: (half(jnp.minimum(s, 5)), kind(s), 0, 0),
            ),
            clear((span, depth)),
            anywhere,
            clear((8, depth)),
            clear((8, depth)),
        ]
        + [anywhere] * 7,
        input_output_aliases={15: 3},
        out_specs=[anywhere] * 4 + [clear((8, 128))] + [clear(final.shape) for final in finals],
        out_shape=tokens + [jax.ShapeDtypeStruct((8, 128), F32)] + finals,
        scratch_shapes=[
            vmem((span, depth), BF16),
            vmem((span, depth), F32),
            vmem((depth, span), BF16),
            vmem((span, depth), F32),
            vmem((wide, span), BF16),
            vmem((3, line, 2, rows, wide), BF16),
            vmem((3, line, 2, rows, wide), BF16),
            vmem((3, line, rows, wide), BF16),
            vmem((3, line - 1, rows, wide), BF16),
            vmem((line, down_rows // 2, wide), BF16),
            vmem((line, down_rows // 2, wide), BF16),
            vmem((line - 1, down_rows // 2, wide), BF16),
            vmem((line, rows // 2, wide), BF16),
            vmem((line, rows // 2, wide), BF16),
            vmem((line - 1, rows // 2, wide), BF16),
            vmem((blocks, 2, rows, 128), BF16),
            vmem((line - 1, blocks, 2, rows, 128), BF16),
            vmem((blocks, 2, rows, 128), BF16),
            vmem((blocks, 2, rows, 128), BF16),
            vmem((down_rows, wide), BF16),
            vmem((down_rows, wide), BF16),
            vmem((4, rows, wide), BF16),
            vmem((4, rows, wide), BF16),
            vmem((4, rows, wide), BF16),
            vmem((tok, depth), F32),
            vmem((tok, depth), BF16),
            vmem((tok, depth), BF16),
            vmem((5, 8, depth), F32),
            vmem((line + 2, 8, depth), F32),
            dma((13,)),
            dma((2, 3)),
            dma((2, 3)),
            dma((2, 3 * (line - 1))),
            dma((2, line - 1)),
            dma((2, line - 1)),
            dma((2, 6)),
            dma((2, 6)),
            dma((2, 4)),
            dma((2, line + 2)),
        ],
        compiler_params=pltpu.CompilerParams(
            dimension_semantics=("arbitrary",),
            vmem_limit_bytes=63 * MIB,
            collective_id=6,
            has_side_effects=True,
        ),
        cost_estimate=pl.CostEstimate(
            flops=12 * span * depth * depth,
            bytes_accessed=24 * span * depth + 12 * depth * depth,
            transcendentals=0,
        ),
        name="tail_carry",
    )(
        inputs,
        x_received,
        back_other,
        back_own,
        full,
        normed,
        grad_middle,
        gains,
        mlp_gain,
        gu_mine,
        gu_z,
        d,
        d_y,
        o,
        o_y,
        first_received,
    )


def finish_kernel(place, *refs):
    count = (len(refs) - 2 * 3 - 3) // 2
    tokens, plain = refs[:6], refs[6 : 6 + count]
    outs = refs[6 + count :]
    side = place[0]
    for number in range(3):
        outs[number][side] = tokens[2 * number][...].reshape(tokens[2 * number + 1].shape)
        outs[number][1 - side] = tokens[2 * number + 1][...].astype(F32)
    for number in range(count):
        outs[3 + number][...] = plain[number][...]


def finish(outputs, tokens, plain, side):
    _, tok, depth = outputs[0].shape
    steps = 4
    tile = tok // steps
    row = pl.BlockSpec((tile, depth), lambda s, p: (s, 0))
    tiles = [
        pl.BlockSpec((value.shape[0] // steps, value.shape[1]), lambda s, p: (s, 0))
        for value in plain
    ]
    grid_spec = pltpu.PrefetchScalarGridSpec(
        num_scalar_prefetch=1,
        grid=(steps,),
        in_specs=[pl.BlockSpec((1, tile, depth), lambda s, p: (p[0], s, 0))] + [row] * 5 + tiles,
        out_specs=[pl.BlockSpec((2, tile, depth), lambda s, p: (0, s, 0))] * 3 + tiles,
    )
    return pl.pallas_call(
        finish_kernel,
        out_shape=[jax.ShapeDtypeStruct((2, tok, depth), F32)] * 3
        + [jax.ShapeDtypeStruct(value.shape, value.dtype) for value in plain],
        grid_spec=grid_spec,
        compiler_params=parameters(60),
        cost_estimate=pl.CostEstimate(
            flops=tok * depth, bytes_accessed=60 * tok * depth, transcendentals=0
        ),
        name="finish",
    )(side, *outputs, *tokens, *plain)


def shards(
    inputs,
    first_values,
    out_grad,
    attn_gain,
    query_weight,
    key_weight,
    value_weight,
    output_weight,
    mlp_gain,
    gate_weight,
    up_weight,
    down_weight,
):
    slots, tok, _ = inputs.shape
    groups = lax.axis_size("seq")
    parts = lax.axis_size("fsdp")
    line = parts // 2
    count = groups // slots
    length = tok * groups
    span = slots * tok
    seat = lax.axis_index("seq")
    shard = lax.axis_index("fsdp")
    side = seat // count
    rank = seat % count
    core = seat % 2
    z, y = shard // 2, shard % 2
    wide = D // 2
    width = D // count

    def along_seq(value, partner):
        return lax.ppermute(value, "seq", [(i, partner(i)) for i in range(groups)])

    def along_fsdp(value, partner):
        return lax.ppermute(value, "fsdp", [(i, partner(i)) for i in range(parts)])

    def to_core(value):
        return along_seq(value, lambda i: i ^ 1)

    def to_y(value):
        return along_fsdp(value, lambda i: i ^ 1)

    def to_z(value, jump):
        return along_fsdp(value, lambda i: (i + 2 * jump) % parts)

    def after(value, *others):
        return lax.optimization_barrier((value,) + others)[0]

    def to_sequence(values):
        taken = []
        for jump in range(1, slots):
            sent = lax.dynamic_index_in_dim(values, (side + jump) % slots, 0, keepdims=False)
            taken.append(along_seq(sent, lambda i: (i + jump * count) % groups))
        return taken

    def to_home(whole, sent):
        for jump in range(1, slots):
            part = sent[(jump - 1) * tok : jump * tok]
            part = along_seq(part, lambda i: (i - jump * count) % groups)
            whole = land(whole, part, ((side + jump) % slots)[None])
        return whole

    def rank_up(i, jump):
        return (i // count) * count + (i % count + jump) % count

    def rank_down(i, jump):
        return (i // count) * count + (i % count - jump) % count

    def halves_to_ranks(other, own, axis):
        if count == 2:
            return [other, own]
        return [
            lax.dynamic_slice_in_dim(
                join(other, own, axis), ((rank + 1 + number) % count) * width, width, axis
            )
            for number in range(count)
        ]

    def join(other, own, axis):
        first = jnp.where(core == 0, own, other)
        second = jnp.where(core == 0, other, own)
        return jnp.concatenate([first, second], axis=axis)

    def ranks_to_halves(pieces, axis):
        if count == 2:
            return pieces
        shape = list(pieces[0].shape)
        shape[axis] = D
        whole = jnp.zeros(shape, pieces[0].dtype)
        for number in range(count):
            whole = lax.dynamic_update_slice_in_dim(
                whole, pieces[number], ((rank + 1 + number) % count) * width, axis
            )
        return [
            lax.dynamic_slice_in_dim(whole, which * wide, wide, axis)
            for which in (1 - core, core)
        ]

    def exchange(pieces):
        received = [
            along_seq(pieces[jump - 1], lambda i: rank_up(i, jump)) for jump in range(1, count)
        ]
        return received + [pieces[count - 1]]

    def exchange_back(pieces):
        received = [
            along_seq(pieces[jump - 1], lambda i: rank_down(i, jump)) for jump in range(1, count)
        ]
        return received + [pieces[count - 1]]

    def split(*weights):
        results = []
        for which in (core, 1 - core):
            columns = []
            for weight in weights:
                size = weight.shape[1] // 2
                columns.append(lax.dynamic_slice_in_dim(weight, which * size, size, 1))
            results.append(columns)
        return results

    def gather_z(half):
        return [half] + [to_z(half, jump) for jump in range(1, line)]

    def gather_rest(along_z, other):
        along_y = [to_y(piece) for piece in along_z]
        own = [piece for pair in zip(along_z, along_y) for piece in pair]
        return (own, [other] + [to_core(piece) for piece in own[1:]])

    numbers = []
    for jump in range(line):
        for flip in range(2):
            numbers.append(((z - jump) % line) * 2 + (y ^ flip))
    place = jnp.stack([side, core] + numbers).astype(jnp.int32)

    def low(value):
        return value.astype(BF16)

    def add(a, b):
        return low(a.astype(F32) + b.astype(F32))

    def pick(value, index, axis):
        return lax.dynamic_index_in_dim(value, index, axis, keepdims=False)

    def along_x_and_core(total):
        mine = low(total)
        for jump in range(1, groups // 2):
            total = total + along_seq(mine, lambda i: (i + 2 * jump) % groups).astype(F32)
        mine = low(total)
        return (mine, to_core(mine))

    def along_z_and_on(partial):
        total = partial(z)
        for jump in range(1, line):
            total = total + to_z(low(partial((z + jump) % line)), jump).astype(F32)
        return along_x_and_core(total)

    def scatter(sent, kept, rows_axis):
        shape = kept.shape
        rows = shape[rows_axis] // parts
        cut = shape[:rows_axis] + (line, 2, rows) + shape[rows_axis + 1 :]
        received = to_core(sent).reshape(cut)
        kept = kept.reshape(cut)
        axis = rows_axis + 1
        received_y = to_y(add(pick(kept, 1 - y, axis), pick(received, 1 - y, axis)))
        kept_y = pick(kept, y, axis), pick(received, y, axis)

        def partial(index):
            total = pick(kept_y[0], index, rows_axis).astype(F32)
            total = total + pick(kept_y[1], index, rows_axis).astype(F32)
            return total + pick(received_y, index, rows_axis).astype(F32)

        return along_z_and_on(partial)

    def columns(mine, others):
        first = jnp.where(core == 0, mine, others)
        second = jnp.where(core == 0, others, mine)
        return jnp.concatenate([first, second], axis=-1).astype(F32)

    def everywhere(value):
        value = value + to_core(value)
        value = value + to_y(value)
        total = value
        for jump in range(1, line):
            total = total + to_z(value, jump)
        value = total
        for jump in range(1, groups // 2):
            total = total + along_seq(value, lambda i: (i + 2 * jump) % groups)
        return total

    steps = jnp.arange(slots, dtype=jnp.int32)
    starts = ((side - steps) % slots) * (count * tok) + rank * tok
    positions = (starts[:, None] + jnp.arange(tok, dtype=jnp.int32)[None]).reshape(span)
    freqs = rope_base ** (-(jnp.arange(HALF, dtype=F32) * 2.0 / HEAD_DIM))

    def tables(positions):
        angles = freqs[:, None] * positions.astype(F32)[None, :]
        return (jnp.cos(angles), jnp.sin(angles))

    full_cos, full_sin = tables(jnp.arange(length, dtype=jnp.int32))
    sources = jnp.concatenate(
        [(rank - 1 - jnp.arange(count - 1, dtype=jnp.int32)) % count, rank[None]]
    ).astype(jnp.int32)
    order = (((side - steps) % slots)[None, :] * count + sources[:, None]).reshape(-1)
    order = order.astype(jnp.int32)

    whole_lanes = (slots, count) == (2, 2) and (D // parts) % 128 == 0
    if whole_lanes:
        gains = jnp.pad(jnp.stack([attn_gain, mlp_gain]).astype(F32), ((0, 6), (0, 0)))
        parts_of = lambda ref: [ref.reshape(-1, ref.shape[-1])]
        (
            tokens,
            _,
            grads_early,
            heads_own,
            heads_received,
            normed,
            qkv_full,
            gains_full,
            out_own,
            out_other,
            down_own,
        ) = front(
            inputs,
            first_values,
            out_grad,
            query_weight,
            key_weight,
            value_weight,
            output_weight,
            down_weight,
            gains,
            full_cos,
            full_sin,
            line,
        )
        qkv_full = qkv_full.reshape(2, 3, D, wide)
        tokens = [tokens]
        pieces = [heads_received, heads_own]
        (
            mix_received,
            att_own,
            lse,
            middle,
            normed2,
            out_full,
            att_other,
            grads,
            down_own,
            down_other,
            gate_own,
            gate_other,
            up_own,
            up_other,
        ) = attend_carry(
            heads_received,
            heads_own,
            inputs,
            tokens[0],
            gains_full,
            out_own.reshape(D, wide),
            out_other.reshape(D, wide),
            out_grad,
            grads_early,
            down_own,
            gate_weight,
            up_weight,
            line,
        )
        mixes = [mix_received, att_own]
        grads = [grads]
        gate_pieces = parts_of(gate_own), parts_of(gate_other)
        up_pieces = parts_of(up_own), parts_of(up_other)
        down_pieces = parts_of(down_own), parts_of(down_other)
    else:
        gains = jnp.pad(jnp.stack([attn_gain, mlp_gain], axis=1), ((0, 0), (0, 126)))
        gate_halves, up_halves, out_halves, down_halves = (
            [half[0] for half in split(weight)]
            for weight in (gate_weight, up_weight, output_weight, down_weight)
        )
        cosine, sine = tables(positions)
        qkv = [
            jnp.concatenate(half + [gains], axis=1)
            for half in split(query_weight, key_weight, value_weight)
        ]
        tokens = to_sequence(inputs)
        firsts = to_sequence(first_values)
        grads = to_sequence(out_grad)
        qkv_own, qkv_other = gather_rest(gather_z(qkv[0]), qkv[1])
        out_own, out_other = gather_rest(gather_z(out_halves[0]), out_halves[1])
        gate_pieces = gather_rest(gather_z(gate_halves[0]), gate_halves[1])
        up_pieces = gather_rest(gather_z(up_halves[0]), up_halves[1])
        down_pieces = gather_rest(gather_z(down_halves[0]), down_halves[1])
        heads_other, heads_own, normed, qkv_full, gains_full = project(
            inputs, tokens, first_values, firsts, qkv_own, qkv_other, cosine, sine, place
        )
        pieces = exchange(halves_to_ranks(heads_other, heads_own, 1))
        mixes, lse = attend(pieces, order, slots)
        att_other, att_own = ranks_to_halves(exchange_back(mixes), 0)
        middle, normed2, out_full = output_projection(
            inputs, tokens, out_own, out_other, att_other, att_own, gains_full, place
        )

    if whole_lanes:
        (
            outputs,
            outputs_sent,
            grad_middle,
            low_grad,
            mlp_gain_grad,
            gu_reduced,
            down_reduced,
            gu_y,
            gu_late,
        ) = mlp_carry(
            out_grad,
            grads[0],
            middle,
            normed2,
            gains_full,
            (gate_pieces[0][0], gate_pieces[1][0]),
            (up_pieces[0][0], up_pieces[1][0]),
            (down_pieces[0][0], down_pieces[1][0]),
            line,
        )
        ga_own, ga_received, out_kept, out_landed, outputs_received = grad_attended_carry(
            low_grad, out_full, att_other, att_own, outputs_sent, line
        )
        down_reduced = down_reduced.reshape(line, 2, -1, wide)
        out_kept = out_kept.reshape(line, 2, -1, wide)
        out_landed = out_landed.reshape(line, 2, -1, wide)
        (
            back_own,
            back_other,
            outputs_received,
            gu_mine,
            gu_z,
            down_mine,
            down_y,
            out_mine,
            out_y,
            first_received,
        ) = attend_back_carry(
            pieces,
            mixes,
            [ga_received, ga_own],
            lse,
            full_cos,
            full_sin,
            outputs_sent,
            outputs_received,
            gu_reduced,
            gu_y,
            gu_late,
            down_reduced,
            out_kept,
            out_landed,
            line,
        )
        input_own, input_received, first_own, first_received, *rest = tail_carry(
            inputs,
            tokens[0],
            back_other,
            back_own,
            qkv_full,
            normed,
            grad_middle,
            gains_full,
            mlp_gain_grad,
            gu_mine,
            gu_z,
            down_mine,
            down_y,
            out_mine,
            out_y,
            first_received,
            line,
        )
        gain_grads = rest[0]
        outputs, input_grad, first_grad, *rest = finish(
            (outputs,),
            (outputs_received, input_own, input_received, first_own, first_received),
            rest[1:],
            side[None],
        )
        query_grad, key_grad, value_grad, output_grad, gate_grad, up_grad, down_grad = rest
    else:
        (
            outputs,
            outputs_sent,
            grad_middle,
            low_grad,
            mlp_gain_grad,
            gu_sent,
            gu_kept,
            down_sent,
            down_kept,
        ) = mlp(out_grad, grads, middle, normed2, gains_full, gate_pieces, up_pieces, down_pieces, place)
        ga_other, ga_own, out_sent, out_kept = grad_attended(
            low_grad, out_full, att_other, att_own, place
        )
        gate_up_grad = scatter(gu_sent, gu_kept, 1)
        down_grad = scatter(down_sent.reshape(-1, wide), down_kept.reshape(-1, wide), 0)
        output_grad = scatter(out_sent, out_kept, 0)
        grad_heads = exchange(halves_to_ranks(ga_other, ga_own, 0))
        back = attend_back(pieces, mixes, grad_heads, lse, full_cos, full_sin, order, slots)
        back_other, back_own = ranks_to_halves(exchange_back(back), 1)
        outputs = to_home(outputs, outputs_sent)
        input_grad, input_sent, first_grad, first_sent, gain_grads, qkv_sent, qkv_kept = tail(
            inputs,
            tokens,
            back_other,
            back_own,
            qkv_full,
            normed,
            grad_middle,
            gains_full,
            mlp_gain_grad,
            place,
        )
        query_grad, key_grad, value_grad = columns(*scatter(qkv_sent, qkv_kept, 1))
        gate_grad, up_grad = columns(*gate_up_grad)
        output_grad = columns(*output_grad)
        down_grad = columns(*down_grad)
        gain_grads = everywhere(gain_grads)
        gain_grads = lax.dynamic_slice_in_dim(gain_grads, shard * (D // parts), D // parts, 1)
        input_grad = to_home(input_grad, input_sent)
        first_grad = to_home(first_grad, first_sent)

    return (
        outputs,
        input_grad,
        first_grad,
        gain_grads[0],
        gain_grads[1],
        query_grad,
        key_grad,
        value_grad,
        output_grad,
        gate_grad,
        up_grad,
        down_grad,
    )


def solution(mesh):
    token_spec = P("fsdp", "seq", None)
    weight_spec = P("fsdp", None)
    gain_spec = P("fsdp")
    return jax.shard_map(
        shards,
        mesh=mesh,
        in_specs=(token_spec,) * 3
        + (gain_spec,)
        + (weight_spec,) * 4
        + (gain_spec,)
        + (weight_spec,) * 3,
        out_specs=(token_spec,) * 3 + (gain_spec,) * 2 + (weight_spec,) * 7,
        check_vma=False,
    )
```
